32 devices in a mesh: section: 2 (over y), tensor: 2 (over x), dp: 8 (over z, core).
Axes of the slice: x: 2, y: 2, z: 4, core: 2. Of those that a mesh axis runs over, the one named last changes fastest.
Arguments:
- inputs: bfloat16 [32, 512, 1024], P('dp', 'tensor'), may hold values from -6 to 6
- cotangent: bfloat16 [32, 512, 1024], P('dp', 'tensor'), may hold values from -6 to 6
- lengths: int32 [32], P('dp'), may hold values from 256 to 512, as said below
- w_qkv: bfloat16 [2, 1024, 3, 1024], P('section', None, None, 'tensor'), may hold values from -0.1875 to 0.1875
- b_qv: bfloat16 [2, 2, 1024], P('section', None, 'tensor'), may hold values from -4 to 4
- w_out: bfloat16 [2, 1024, 1024], P('section', 'tensor'), may hold values from -0.5 to 0.5
- b_out: bfloat16 [2, 1024], P('section'), may hold values from -3 to 3
- ln_gain: bfloat16 [2, 2, 1024], P('section'), may hold values from 0.5 to 1.5
- ln_bias: bfloat16 [2, 2, 1024], P('section'), may hold values from -3 to 3
- w_up: bfloat16 [2, 2, 1024, 4096], P('section', None, None, 'tensor'), may hold values from -0.1875 to 0.1875
- b_up: bfloat16 [2, 2, 4096], P('section', None, 'tensor'), may hold values from -3 to 3
- w_down: bfloat16 [2, 1024, 4096], P('section', None, 'tensor'), may hold values from -0.125 to 0.125
- b_down: bfloat16 [2, 1024], P('section'), may hold values from -3 to 3
Outputs:
- layer_outputs: bfloat16 [2, 32, 512, 1024], P('section', 'dp', 'tensor')
- input_grads: float32 [2, 32, 512, 1024], P('section', 'dp', 'tensor')
- grad_w_qkv: float32 [2, 1024, 3, 1024], P('section', None, None, 'tensor')
- grad_b_qv: float32 [2, 2, 1024], P('section', None, 'tensor')
- grad_w_out: float32 [2, 1024, 1024], P('section', 'tensor')
- grad_b_out: float32 [2, 1024], P('section')
- grad_ln_gain: float32 [2, 2, 1024], P('section')
- grad_ln_bias: float32 [2, 2, 1024], P('section')
- grad_w_up: float32 [2, 2, 1024, 4096], P('section', None, None, 'tensor')
- grad_b_up: float32 [2, 2, 4096], P('section', None, 'tensor')
- grad_w_down: float32 [2, 1024, 4096], P('section', None, 'tensor')
- grad_b_down: float32 [2, 1024], P('section')
The draws below stay inside these ranges and needn't reach their ends.
Inputs may be any that keep to these rules, and one draw needn't show every extreme that they name: `lengths`: some sequence in every draw has all 512 positions in use.
All inputs are finite; a program needn't handle non-finite values.
Results may differ from the reference program's by a relative error of at most 0.03.
Values may be sent and summed in bfloat16 or wider, within the bound.
A program may use at most 256 MiB of HBM per device.

```python
import math
import jax
import jax.numpy as jnp
from jax import lax

D = 1024
H = 16
F = 4096
S = 512
L = 2
A = 1024
SEQS = 32


def draw_lengths(key, part):
    values = jax.random.randint(key, (SEQS,), S // 2, S + 1)
    chosen = jax.random.randint(jax.random.fold_in(key, 7), (), 0, SEQS)
    return jnp.where(jnp.arange(SEQS) == chosen, S, values).astype(jnp.int32)


def block_levels(rng, dims, shards, least, top_value):
    def one(dim, shards_of):
        heights = jax.random.uniform(jax.random.fold_in(jax.random.fold_in(rng, 6), dim), (shards_of,), jnp.float32, least / len(shards), top_value / len(shards))
        return jnp.repeat(jnp.exp(heights), dims[dim] // shards_of).reshape((-1,) + (1,) * (len(dims) - dim - 1))

    level = one(*shards[0])
    for cut in shards[1:]:
        level = level * one(*cut)
    return level


def bell_draw(stream_key, shape, deviation, bound, split=(), kind=jnp.bfloat16):
    factor_of = block_levels(stream_key, shape, split, -0.22, 0.18) if split else 1.0
    array = jax.random.normal(stream_key, shape, jnp.float32) * deviation * factor_of
    return jnp.minimum(jnp.maximum(array, -bound), bound).astype(kind)


def setup_inputs(seed: int = 0) -> dict:
    key_of = jax.random.split(jax.random.key(seed), 14)
    inputs = bell_draw(key_of[0], (SEQS, S, D), 1.0, 6.0, ((0, 8), (1, 2)))
    cotangent = bell_draw(key_of[1], (SEQS, S, D), 1.0, 6.0, ((0, 8), (1, 2)))
    lengths = draw_lengths(jax.random.fold_in(key_of[13], 71), 0)
    w_qkv = bell_draw(key_of[3], (L, D, 3, A), D ** -0.5, 0.1875, ((0, 2), (3, 2)))
    b_qv = bell_draw(key_of[4], (L, 2, A), 0.3, 4.0, ((0, 2), (2, 2)))
    w_out = bell_draw(key_of[5], (L, A, D), (A // 8) ** -0.5, 0.5, ((0, 2), (1, 2)))
    b_out = bell_draw(key_of[6], (L, D), 0.2, 3.0, ((0, 2),))
    ln_gain = jnp.clip(1.0 + 0.1 * jax.random.normal(key_of[7], (L, 2, D), jnp.float32), 0.5, 1.5).astype(jnp.bfloat16)
    ln_bias = bell_draw(key_of[8], (L, 2, D), 0.2, 3.0, ((0, 2),))
    w_up = bell_draw(key_of[9], (L, 2, D, F), D ** -0.5, 0.1875, ((0, 2), (3, 2)))
    b_up = bell_draw(key_of[10], (L, 2, F), 0.2, 3.0, ((0, 2), (2, 2)))
    w_down = bell_draw(key_of[11], (L, D, F), (F // 2) ** -0.5, 0.125, ((0, 2), (2, 2)))
    b_down = bell_draw(key_of[12], (L, D), 0.2, 3.0, ((0, 2),))
    return {"inputs": inputs, "cotangent": cotangent, "lengths": lengths, "w_qkv": w_qkv, "b_qv": b_qv, "w_out": w_out, "b_out": b_out, "ln_gain": ln_gain, "ln_bias": ln_bias, "w_up": w_up, "b_up": b_up, "w_down": w_down, "b_down": b_down}


EPS = 1e-05
MASKED = -1000000000.0
HIGHEST = lax.Precision.HIGHEST

@jax.custom_vjp
def low(v):
    return lax.optimization_barrier(v.astype(jnp.bfloat16)).astype(jnp.float32)

@jax.custom_vjp
def low_back(v):
    return v

def low_keep(v):
    return (low(v), None)

def low_pass(kept, grad):
    return (grad,)

def back_keep(v):
    return (v, None)

def back_low(kept, grad):
    return (low(grad),)
low.defvjp(low_keep, low_pass)
low_back.defvjp(back_keep, back_low)

def layer_norm(values, gain, shift):
    mean = lax.optimization_barrier(jnp.mean(values, axis=-1, keepdims=True))
    centred = values - mean
    spread = lax.optimization_barrier(jnp.mean(centred * centred, axis=-1, keepdims=True))
    return centred * lax.rsqrt(spread + EPS) * gain + shift

def alibi_slopes(first, count, heads):
    index = (first + jnp.arange(count)).astype(jnp.float32)
    return jnp.exp2(-8.0 * (index + 1.0) / heads)

def attend(projected, qv_bias, slopes, key_ok, precision):
    rows = projected.shape[0]
    width = projected.shape[2]
    count = slopes.shape[0]
    size = width // count
    query = low(low_back(projected[:, 0] + qv_bias[0])).reshape(rows, count, size)
    key = low(low_back(projected[:, 1])).reshape(rows, count, size)
    value = low(low_back(projected[:, 2] + qv_bias[1])).reshape(rows, count, size)
    place = jnp.arange(rows).astype(jnp.float32)
    distance = jnp.abs(place[:, None] - place[None, :])
    scale = 1.0 / math.sqrt(size)
    scores = jnp.einsum('qhd,khd->hqk', query, key, precision=precision) * scale - slopes[:, None, None] * distance[None]
    scores = low_back(scores)
    scores = jnp.where(key_ok[None, None, :], scores, MASKED)
    weights = low(jax.nn.softmax(scores, axis=-1))
    mixed = jnp.einsum('hqk,khd->qhd', weights, value, precision=precision)
    return low(low_back(mixed.reshape(rows, width)))

def geglu(lifted, up_bias):
    both = low_back(lifted + up_bias[None])
    return low(jax.nn.gelu(both[:, 0], approximate=False) * both[:, 1])

def layer(inputs, params, length):
    w_qkv, b_qv, w_out, b_out, gains, shifts, w_up, b_up, w_down, b_down = params
    rows, width = inputs.shape
    projected = jnp.dot(low(inputs), w_qkv.reshape(width, -1), precision=HIGHEST).reshape(rows, 3, -1)
    key_ok = jnp.arange(rows) < length
    mixed = attend(projected, b_qv, alibi_slopes(0, H, H), key_ok, HIGHEST)
    attended = low_back(jnp.dot(mixed, w_out, precision=HIGHEST))
    normed = layer_norm(inputs + attended + b_out, gains[0], shifts[0])
    lifted = jnp.einsum('sd,gdf->sgf', low(normed), w_up, precision=HIGHEST)
    hidden = geglu(lifted, b_up)
    lowered = low_back(jnp.einsum('sf,df->sd', hidden, w_down, precision=HIGHEST))
    return layer_norm(normed + lowered + b_down, gains[1], shifts[1])

def apply_layer(weights, batch, lens):
    return jax.vmap(layer, in_axes=(0, None, 0))(batch, weights, lens)

def reference(inputs, cotangent, lengths, w_qkv, b_qv, w_out, b_out, ln_gain, ln_bias, w_up, b_up, w_down, b_down):
    params = tuple((item.astype(jnp.float32) for item in (w_qkv, b_qv, w_out, b_out, ln_gain, ln_bias, w_up, b_up, w_down, b_down)))
    first = tuple((item[0] for item in params))
    second = tuple((item[1] for item in params))
    group = math.gcd(SEQS, max(1, 4096 // S))
    blocks = SEQS // group
    shaped_inputs = inputs.reshape(blocks, group, S, D)
    shaped_outer = cotangent.reshape(blocks, group, S, D)
    shaped_lengths = lengths.reshape(blocks, group)

    def run(totals, block):
        batch, outer, lens = block
        middle, back_first = jax.vjp(lambda values, weights: apply_layer(weights, values, lens), batch.astype(jnp.float32), first)
        middle = low(middle)
        final, back_second = jax.vjp(lambda values, weights: apply_layer(weights, values, lens), middle, second)
        row_mask = (jnp.arange(S)[None, :] < lens[:, None]).astype(jnp.float32)
        grad_middle, grad_second = back_second(outer.astype(jnp.float32) * row_mask[:, :, None])
        grad_inputs, grad_first = back_first(low(grad_middle))
        totals = (jax.tree.map(jnp.add, totals[0], grad_first), jax.tree.map(jnp.add, totals[1], grad_second))
        return (totals, (middle.astype(jnp.bfloat16), final.astype(jnp.bfloat16), grad_inputs, grad_middle))
    zeros = tuple((jnp.zeros_like(item) for item in first))
    totals, results = lax.scan(run, (zeros, zeros), (shaped_inputs, shaped_outer, shaped_lengths))
    middle_all = results[0].reshape(SEQS, S, D)
    final_all = results[1].reshape(SEQS, S, D)
    grad_inputs_all = results[2].reshape(SEQS, S, D)
    grad_middle_all = results[3].reshape(SEQS, S, D)
    layer_outputs = jnp.stack([middle_all, final_all])
    input_grads = jnp.stack([grad_inputs_all, grad_middle_all])
    grads = tuple((jnp.stack([totals[0][index], totals[1][index]]) for index in range(10)))
    return (layer_outputs, input_grads, grads[0], grads[1], grads[2], grads[3], grads[4], grads[5], grads[6], grads[7], grads[8], grads[9])
```

```python
import functools
import math

import jax
import jax.numpy as jnp
from jax import lax
from jax.experimental import pallas as pl
from jax.experimental.pallas import tpu as pltpu
from jax.sharding import PartitionSpec as P

H = 16
HD = 64
EPS = 1e-05
BF = jnp.bfloat16
F32 = jnp.float32
VMEM_LIMIT = 62 * 1024 * 1024
ANY = pl.BlockSpec(memory_space=pl.ANY)
NN = (((1,), (0,)), ((), ()))
NT = (((1,), (1,)), ((), ()))
TN = (((0,), (0,)), ((), ()))


def dot(a, b, dims=NN):
    return lax.dot_general(a, b, dims, preferred_element_type=F32)


def call(kernel, grid, inputs, outputs, scratch, meta, chain, deps, name, flops, nbytes):
    args = [a for a, _ in inputs]
    specs = [s for _, s in inputs]
    n_in = len(args)
    aliases = {}
    if chain is not None:
        chained = [index for index, item in enumerate(outputs) if item[3]]
        for buffer, index in zip(chain, chained):
            aliases[1 + len(args)] = index
            args.append(buffer)
            specs.append(ANY)
    for item in deps:
        args.append(item)
        specs.append(ANY)
    n_args = len(args)

    def body(meta_ref, *refs):
        kernel(meta_ref, refs[:n_in], refs[n_args : n_args + len(outputs)], refs[n_args + len(outputs) :])

    return pl.pallas_call(
        body,
        grid_spec=pltpu.PrefetchScalarGridSpec(
            num_scalar_prefetch=1,
            grid=grid,
            in_specs=specs,
            out_specs=[o[2] for o in outputs],
            scratch_shapes=scratch,
        ),
        out_shape=[jax.ShapeDtypeStruct(o[0], o[1]) for o in outputs],
        input_output_aliases=aliases,
        compiler_params=pltpu.CompilerParams(
            dimension_semantics=("arbitrary",) * len(grid), vmem_limit_bytes=VMEM_LIMIT
        ),
        cost_estimate=pl.CostEstimate(flops=flops, bytes_accessed=nbytes, transcendentals=0),
        name=name,
    )(meta, *args)


def own_map(count, make):
    return lambda i, meta: make(jnp.minimum(i, count - 1) * meta[1])


def oth_map(count, make):
    return lambda i, meta: make(jnp.maximum(i - count, 0) * meta[1])


def tile_map(make):
    return lambda i, meta: make(meta[0], i * meta[1])


def fixed(shape):
    zeros = (0,) * len(shape)
    return pl.BlockSpec(shape, lambda i, meta: zeros, pipeline_mode=pl.Buffered(1))


def fill_distance(dist_ref, length):
    rows = dist_ref.shape[0]
    keys = lax.broadcasted_iota(jnp.int32, (rows, rows), 0)
    places = lax.broadcasted_iota(jnp.int32, (rows, rows), 1)
    distance = jnp.abs(keys - places).astype(F32)
    dist_ref[...] = jnp.where(keys < length, distance, 1e12)


def attention_forward(x, w_own, w_oth, bias, slopes, meta, chain, deps, slots):
    rows, width = x.shape
    local = w_own.shape[2]
    cw = 256
    per = cw // HD
    count = local // cw
    steps = 2 * count
    total = 2 * local

    def kernel(meta_ref, ins, outs, scratch):
        x_ref, own_ref, oth_ref, bias_ref, slope_ref = ins
        q_ref, k_ref, v_ref, mixed_ref, lse_ref = outs
        (dist_ref,) = scratch
        i = pl.program_id(0)

        def work(w_ref):
            values = x_ref[...]
            b = bias_ref[...]
            q_ref[0] = (dot(values, w_ref[0]) + b[0:1]).astype(BF)
            k_ref[0] = dot(values, w_ref[1]).astype(BF)
            v_ref[0] = (dot(values, w_ref[2]) + b[1:2]).astype(BF)
            for head in range(per):
                cols = slice(head * HD, (head + 1) * HD)
                query = q_ref[0, :, cols] * BF(1.0 / math.sqrt(HD))
                scores = dot(k_ref[0, :, cols], query, NT)
                scores = scores - dist_ref[...] * slope_ref[i * per + head]
                top = jnp.max(scores, axis=0, keepdims=True)
                weights = jnp.exp(scores - top)
                total_weight = jnp.sum(weights, axis=0, keepdims=True)
                low = (weights * (1.0 / total_weight)).astype(BF)
                mixed_ref[0, :, cols] = dot(low, v_ref[0, :, cols], TN).astype(BF)
                lse_ref[0, 0, head : head + 1, :] = top + jnp.log(total_weight)

        @pl.when(meta_ref[1] == 1)
        def _():
            @pl.when(i == 0)
            def _():
                fill_distance(dist_ref, meta_ref[2])

            @pl.when(i < count)
            def _():
                work(own_ref)

            @pl.when(i >= count)
            def _():
                work(oth_ref)

    wide = pl.BlockSpec((1, rows, cw), tile_map(lambda s, i: (s, 0, i)))
    return call(
        kernel,
        (steps,),
        [
            (x, fixed((rows, width))),
            (w_own, pl.BlockSpec((3, width, cw), own_map(count, lambda i: (0, 0, i)))),
            (w_oth, pl.BlockSpec((3, width, cw), oth_map(count, lambda i: (0, 0, i)))),
            (bias, pl.BlockSpec((2, cw), lambda i, meta: (0, i * meta[1]))),
            (slopes, pl.BlockSpec(memory_space=pltpu.SMEM)),
        ],
        [((slots, rows, total), BF, wide, True)] * 4
        + [
            (
                (slots, steps, 8, rows),
                F32,
                pl.BlockSpec((1, 1, 8, rows), tile_map(lambda s, i: (s, i, 0, 0))),
                True,
            )
        ],
        [pltpu.VMEM((rows, rows), F32)],
        meta,
        chain,
        deps,
        "attention_forward",
        2 * rows * width * 3 * total + 4 * rows * rows * total,
        12 << 20,
    )


def normalize(v):
    mean = jnp.mean(v, axis=1, keepdims=True)
    centred = v - mean
    rstd = lax.rsqrt(jnp.mean(centred * centred, axis=1, keepdims=True) + EPS)
    return centred * rstd, rstd


def ffn_forward(x, mixed, o_own, o_oth, up_own, up_oth, down_own, down_oth, vecs, up_bias, meta, chain, deps, slots):
    rows, width = x.shape
    local = o_own.shape[0]
    units = up_own.shape[2]
    ft = min(512, units)
    count = units // ft
    steps = 2 * count

    def kernel(meta_ref, ins, outs, scratch):
        x_ref, mixed_ref, o_own_ref, o_oth_ref, u_own_ref, u_oth_ref, d_own_ref, d_oth_ref, vec_ref, ub_ref = ins
        a_ref, b_ref, h_ref, n_ref, u1_ref, u2_ref, r1_ref, r2_ref, y_ref = outs
        normed_ref, acc_ref = scratch
        i = pl.program_id(0)
        vec = vec_ref[...]

        def work(up_ref, down_ref):
            for part in range(2):
                rs = slice(part * rows // 2, (part + 1) * rows // 2)
                low = n_ref[0, rs, :]
                gate = dot(low, up_ref[0]) + ub_ref[0:1]
                lift = dot(low, up_ref[1]) + ub_ref[1:2]
                cdf = 0.5 * lax.erf(gate * (1.0 / math.sqrt(2.0))) + 0.5
                act = gate * cdf
                slope = cdf + gate * (jnp.exp(gate * gate * -0.5) * (1.0 / math.sqrt(2.0 * math.pi)))
                a_ref[0, rs, :] = act.astype(BF)
                b_ref[0, rs, :] = (lift * slope).astype(BF)
                hidden = (act * lift).astype(BF)
                h_ref[0, rs, :] = hidden
                acc_ref[rs, :] += dot(hidden, down_ref[...], NT)

        @pl.when(meta_ref[1] == 1)
        def _():
            @pl.when(i == 0)
            def _():
                attended = dot(mixed_ref[0, :, :local], o_own_ref[...])
                attended += dot(mixed_ref[0, :, local:], o_oth_ref[...])
                u, rstd = normalize(x_ref[...].astype(F32) + attended + vec[0:1])
                normed = u * vec[1:2] + vec[2:3]
                normed_ref[...] = normed
                n_ref[0] = normed.astype(BF)
                u1_ref[0] = u.astype(BF)
                r1_ref[0] = jnp.broadcast_to(rstd, (rows, 128))
                acc_ref[...] = jnp.zeros_like(acc_ref)

            @pl.when(i < count)
            def _():
                work(u_own_ref, d_own_ref)

            @pl.when(i >= count)
            def _():
                work(u_oth_ref, d_oth_ref)

            @pl.when(i == steps - 1)
            def _():
                u, rstd = normalize(normed_ref[...] + acc_ref[...] + vec[3:4])
                u2_ref[0] = u.astype(BF)
                r2_ref[0] = jnp.broadcast_to(rstd, (rows, 128))
                y_ref[...] = (u * vec[4:5] + vec[5:6]).astype(BF)

    tile = pl.BlockSpec((1, rows, ft), tile_map(lambda s, i: (s, 0, i)))
    whole = pl.BlockSpec((1, rows, width), lambda i, meta: (meta[0], 0, 0))
    stat = pl.BlockSpec((1, rows, 128), lambda i, meta: (meta[0], 0, 0))
    return call(
        kernel,
        (steps,),
        [
            (x, fixed((rows, width))),
            (mixed, pl.BlockSpec((1, rows, 2 * local), lambda i, meta: (meta[0], 0, 0), pipeline_mode=pl.Buffered(1))),
            (o_own, fixed((local, width))),
            (o_oth, fixed((local, width))),
            (up_own, pl.BlockSpec((2, width, ft), own_map(count, lambda i: (0, 0, i)))),
            (up_oth, pl.BlockSpec((2, width, ft), oth_map(count, lambda i: (0, 0, i)))),
            (down_own, pl.BlockSpec((width, ft), own_map(count, lambda i: (0, i)))),
            (down_oth, pl.BlockSpec((width, ft), oth_map(count, lambda i: (0, i)))),
            (vecs, fixed((8, width))),
            (up_bias, pl.BlockSpec((2, ft), lambda i, meta: (0, i * meta[1]))),
        ],
        [((slots, rows, 2 * units), BF, tile, True)] * 3
        + [((slots, rows, width), BF, whole, True)] * 3
        + [((slots, rows, 128), F32, stat, True)] * 2
        + [((rows, width), BF, pl.BlockSpec((rows, width), lambda i, meta: (0, 0)), False)],
        [pltpu.VMEM((rows, width), F32), pltpu.VMEM((rows, width), F32)],
        meta,
        chain,
        deps,
        "ffn_forward",
        2 * rows * width * (6 * units + 2 * local),
        45 << 20,
    )


def ffn_backward(grad, u2, r2, u1, r1, act, slope, up_own, up_oth, down_own, down_oth, vecs, meta, chain, deps, slots):
    rows, width = grad.shape
    units = up_own.shape[2]
    ft = min(512, units)
    count = units // ft
    steps = 2 * count

    def kernel(meta_ref, ins, outs, scratch):
        g_ref, u2_ref, r2_ref, u1_ref, r1_ref, a_ref, b_ref, u_own_ref, u_oth_ref, d_own_ref, d_oth_ref, vec_ref = ins
        gg0_ref, gg1_ref, gl_ref, ga_ref, gaf_ref, sums_ref, ub_ref = outs
        (acc_ref,) = scratch
        i = pl.program_id(0)
        vec = vec_ref[...]

        def norm_back(grad_z, u, rstd, gain):
            t = grad_z * gain
            return rstd * (
                t - jnp.mean(t, axis=1, keepdims=True) - u * jnp.mean(t * u, axis=1, keepdims=True)
            )

        def work(up_ref, down_ref):
            s0 = jnp.zeros((1, ft), F32)
            s1 = jnp.zeros((1, ft), F32)
            for part in range(2):
                rs = slice(part * rows // 2, (part + 1) * rows // 2)
                gh = dot(gl_ref[0, rs, :], down_ref[...])
                g0 = (gh * b_ref[0, rs, :].astype(F32)).astype(BF)
                g1 = (gh * a_ref[0, rs, :].astype(F32)).astype(BF)
                gg0_ref[0, rs, :] = g0
                gg1_ref[0, rs, :] = g1
                s0 += jnp.sum(g0.astype(F32), axis=0, keepdims=True)
                s1 += jnp.sum(g1.astype(F32), axis=0, keepdims=True)
                acc_ref[rs, :] += dot(g0, up_ref[0], NT) + dot(g1, up_ref[1], NT)
            ub_ref[...] = jnp.concatenate([s0, s1, jnp.zeros((6, ft), F32)], axis=0)

        @pl.when(meta_ref[1] == 1)
        def _():
            @pl.when(i == 0)
            def _():
                grad_y = g_ref[...].astype(F32)
                u = u2_ref[0].astype(F32)
                grad_c = norm_back(grad_y, u, r2_ref[0, :, 0:1], vec[4:5])
                acc_ref[...] = grad_c
                gl_ref[0] = grad_c.astype(BF)
                sums_ref[0:1, :] = jnp.sum(grad_y * u, axis=0, keepdims=True)
                sums_ref[1:2, :] = jnp.sum(grad_y, axis=0, keepdims=True)
                sums_ref[2:3, :] = jnp.sum(grad_c, axis=0, keepdims=True)

            @pl.when(i < count)
            def _():
                work(u_own_ref, d_own_ref)

            @pl.when(i >= count)
            def _():
                work(u_oth_ref, d_oth_ref)

            @pl.when(i == steps - 1)
            def _():
                grad_n = acc_ref[...]
                u = u1_ref[0].astype(F32)
                grad_a = norm_back(grad_n, u, r1_ref[0, :, 0:1], vec[1:2])
                ga_ref[0] = grad_a.astype(BF)
                gaf_ref[...] = grad_a
                sums_ref[3:4, :] = jnp.sum(grad_n * u, axis=0, keepdims=True)
                sums_ref[4:5, :] = jnp.sum(grad_n, axis=0, keepdims=True)
                sums_ref[5:6, :] = jnp.sum(grad_a, axis=0, keepdims=True)
                sums_ref[6:8, :] = jnp.zeros((2, width), F32)

    tile = pl.BlockSpec((1, rows, ft), tile_map(lambda s, i: (s, 0, i)))
    whole = pl.BlockSpec((1, rows, width), lambda i, meta: (meta[0], 0, 0))
    whole1 = pl.BlockSpec((1, rows, width), lambda i, meta: (meta[0], 0, 0), pipeline_mode=pl.Buffered(1))
    stat = pl.BlockSpec((1, rows, 128), lambda i, meta: (meta[0], 0, 0))
    return call(
        kernel,
        (steps,),
        [
            (grad, fixed((rows, width))),
            (u2, whole1),
            (r2, stat),
            (u1, whole1),
            (r1, stat),
            (act, tile),
            (slope, tile),
            (up_own, pl.BlockSpec((2, width, ft), own_map(count, lambda i: (0, 0, i)))),
            (up_oth, pl.BlockSpec((2, width, ft), oth_map(count, lambda i: (0, 0, i)))),
            (down_own, pl.BlockSpec((width, ft), own_map(count, lambda i: (0, i)))),
            (down_oth, pl.BlockSpec((width, ft), oth_map(count, lambda i: (0, i)))),
            (vecs, fixed((8, width))),
        ],
        [((slots, rows, 2 * units), BF, tile, True)] * 2
        + [((slots, rows, width), BF, whole, True)] * 2
        + [
            ((rows, width), F32, pl.BlockSpec((rows, width), lambda i, meta: (0, 0)), False),
            ((8, width), F32, pl.BlockSpec((8, width), lambda i, meta: (0, 0)), False),
            ((8, 2 * units), F32, pl.BlockSpec((8, ft), lambda i, meta: (0, i)), False),
        ],
        [pltpu.VMEM((rows, width), F32)],
        meta,
        chain,
        deps,
        "ffn_backward",
        2 * rows * width * 6 * units,
        50 << 20,
    )


def attention_backward(ga, gaf, q, k, v, lse, o_own, o_oth, w_own, w_oth, slopes, meta, chain, deps, slots):
    rows, width = gaf.shape
    local = w_own.shape[2]
    cw = 256
    per = cw // HD
    count = local // cw
    steps = 2 * count
    total = 2 * local

    def kernel(meta_ref, ins, outs, scratch):
        ga_ref, gaf_ref, q_ref, k_ref, v_ref, lse_ref, o_own_ref, o_oth_ref, w_own_ref, w_oth_ref, slope_ref = ins
        gq_ref, gk_ref, gv_ref, gx_ref, gxl_ref, sums_ref = outs
        dist_ref, gm_ref, acc_ref = scratch
        i = pl.program_id(0)
        scale = BF(1.0 / math.sqrt(HD))

        def work(o_ref, w_ref):
            gm_ref[...] = dot(ga_ref[0], o_ref[...], NT).astype(BF)
            for head in range(per):
                cols = slice(head * HD, (head + 1) * HD)
                query = q_ref[0, :, cols] * scale
                key = k_ref[0, :, cols]
                gm = gm_ref[:, cols]
                scores = dot(key, query, NT)
                scores = scores - dist_ref[...] * slope_ref[i * per + head]
                weights = jnp.exp(scores - lse_ref[0, 0, head : head + 1, :])
                gv_ref[0, :, cols] = dot(weights.astype(BF), gm).astype(BF)
                gw = dot(v_ref[0, :, cols], gm, NT)
                t = weights * gw
                inner = jnp.sum(t, axis=0, keepdims=True)
                gs = (t - weights * inner).astype(BF)
                gk_ref[0, :, cols] = dot(gs, query).astype(BF)
                gq_ref[0, :, cols] = dot(gs, key * scale, TN).astype(BF)
            acc_ref[...] += (
                dot(gq_ref[0], w_ref[0], NT) + dot(gk_ref[0], w_ref[1], NT) + dot(gv_ref[0], w_ref[2], NT)
            )
            sums_ref[...] = jnp.concatenate(
                [
                    jnp.sum(gq_ref[0].astype(F32), axis=0, keepdims=True),
                    jnp.sum(gv_ref[0].astype(F32), axis=0, keepdims=True),
                    jnp.zeros((6, cw), F32),
                ],
                axis=0,
            )

        @pl.when(meta_ref[1] == 1)
        def _():
            @pl.when(i == 0)
            def _():
                fill_distance(dist_ref, meta_ref[2])
                acc_ref[...] = gaf_ref[...]

            @pl.when(i < count)
            def _():
                work(o_own_ref, w_own_ref)

            @pl.when(i >= count)
            def _():
                work(o_oth_ref, w_oth_ref)

            @pl.when(i == steps - 1)
            def _():
                gx_ref[...] = acc_ref[...]
                gxl_ref[...] = acc_ref[...].astype(BF)

    tile = pl.BlockSpec((1, rows, cw), tile_map(lambda s, i: (s, 0, i)))
    return call(
        kernel,
        (steps,),
        [
            (ga, pl.BlockSpec((1, rows, width), lambda i, meta: (meta[0], 0, 0), pipeline_mode=pl.Buffered(1))),
            (gaf, fixed((rows, width))),
            (q, tile),
            (k, tile),
            (v, tile),
            (lse, pl.BlockSpec((1, 1, 8, rows), tile_map(lambda s, i: (s, i, 0, 0)))),
            (o_own, pl.BlockSpec((cw, width), own_map(count, lambda i: (i, 0)))),
            (o_oth, pl.BlockSpec((cw, width), oth_map(count, lambda i: (i, 0)))),
            (w_own, pl.BlockSpec((3, width, cw), own_map(count, lambda i: (0, 0, i)))),
            (w_oth, pl.BlockSpec((3, width, cw), oth_map(count, lambda i: (0, 0, i)))),
            (slopes, pl.BlockSpec(memory_space=pltpu.SMEM)),
        ],
        [((slots, rows, total), BF, tile, True)] * 3
        + [
            ((rows, width), F32, pl.BlockSpec((rows, width), lambda i, meta: (0, 0)), False),
            ((rows, width), BF, pl.BlockSpec((rows, width), lambda i, meta: (0, 0)), False),
            ((8, total), F32, pl.BlockSpec((8, cw), lambda i, meta: (0, i)), False),
        ],
        [pltpu.VMEM((rows, rows), F32), pltpu.VMEM((rows, cw), BF), pltpu.VMEM((rows, width), F32)],
        meta,
        chain,
        deps,
        "attention_backward",
        2 * rows * width * 4 * total + 10 * rows * rows * total,
        20 << 20,
    )


def weight_grads(left, rights, seqs, name):
    rows, depth = left.shape[1:]
    width = rights[0].shape[2]
    nt = 512
    n = len(rights)

    def kernel(*refs):
        left_ref, ins, outs, flip_ref = refs[0], refs[1 : 1 + n], refs[1 + n : 1 + 2 * n], refs[1 + 2 * n]

        @pl.when(pl.program_id(0) == 0)
        def _():
            for s in range(seqs):
                flip_ref[:, s * rows : (s + 1) * rows] = left_ref[s].T

        for a, b in zip(ins, outs):
            total = dot(flip_ref[:, :rows], a[0])
            for s in range(1, seqs):
                total += dot(flip_ref[:, s * rows : (s + 1) * rows], a[s])
            b[...] = total.astype(BF)

    return pl.pallas_call(
        kernel,
        grid=(width // nt,),
        in_specs=[pl.BlockSpec((seqs, rows, depth), lambda j: (0, 0, 0), pipeline_mode=pl.Buffered(1))]
        + [pl.BlockSpec((seqs, rows, nt), lambda j: (0, 0, j))] * n,
        out_specs=[pl.BlockSpec((depth, nt), lambda j: (0, j))] * n,
        out_shape=[jax.ShapeDtypeStruct((depth, width), BF)] * n,
        scratch_shapes=[pltpu.VMEM((depth, seqs * rows), BF)],
        compiler_params=pltpu.CompilerParams(
            dimension_semantics=("arbitrary",), vmem_limit_bytes=VMEM_LIMIT
        ),
        cost_estimate=pl.CostEstimate(
            flops=2 * seqs * rows * depth * width * n,
            bytes_accessed=(seqs * rows + depth) * width * n * 2,
            transcendentals=0,
        ),
        name=name,
    )(left, *rights)


MASKED = -1000000000.0


def shifted(value, axis, steps):
    count = lax.axis_size(axis)
    first, last = (max(0, -steps), min(count, count - steps))
    return lax.ppermute(value, axis, [(source, source + steps) for source in range(first, last)])


def layer_norm(values, gain, shift):
    mean = jnp.mean(values, axis=-1, keepdims=True)
    centred = values - mean
    spread = jnp.mean(centred * centred, axis=-1, keepdims=True)
    return centred * lax.rsqrt(spread + EPS) * gain + shift


def alibi_slopes(first, count, heads):
    index = (first + jnp.arange(count)).astype(jnp.float32)
    return jnp.exp2(-8.0 * (index + 1.0) / heads)


def attention_core(projected, qv_bias, slopes, key_ok):
    rows = projected.shape[0]
    width = projected.shape[2]
    count = slopes.shape[0]
    size = width // count
    query = (projected[:, 0] + qv_bias[0]).astype(jnp.bfloat16).reshape(rows, count, size)
    key = projected[:, 1].astype(jnp.bfloat16).reshape(rows, count, size)
    value = (projected[:, 2] + qv_bias[1]).astype(jnp.bfloat16).reshape(rows, count, size)
    place = jnp.arange(rows).astype(jnp.float32)
    distance = jnp.abs(place[:, None] - place[None, :])
    scale = 1.0 / math.sqrt(size)
    scores = (
        jnp.einsum("qhd,khd->hqk", query, key, preferred_element_type=jnp.float32) * scale
        - slopes[:, None, None] * distance[None]
    )
    scores = jnp.where(key_ok[None, None, :], scores, MASKED)
    weights = jax.nn.softmax(scores, axis=-1)
    weights_low = weights.astype(jnp.bfloat16)
    mixed = jnp.einsum("hqk,khd->qhd", weights_low, value, preferred_element_type=jnp.float32)
    mixed = mixed.reshape(rows, width).astype(jnp.bfloat16)
    return (query, key, value, weights, weights_low, mixed)


def attention_back(parts, grad_mixed, key_ok):
    query, key, value, weights, weights_low, mixed = parts
    rows, count, size = query.shape
    scale = 1.0 / math.sqrt(size)
    grad_low = grad_mixed.astype(jnp.bfloat16).reshape(rows, count, size)
    grad_weights = jnp.einsum("qhd,khd->hqk", grad_low, value, preferred_element_type=jnp.float32)
    grad_value = jnp.einsum(
        "hqk,qhd->khd", weights_low, grad_low, preferred_element_type=jnp.float32
    )
    inner = jnp.sum(weights * grad_weights, axis=-1, keepdims=True)
    grad_scores = weights * (grad_weights - inner)
    grad_scores = jnp.where(key_ok[None, None, :], grad_scores, 0.0).astype(jnp.bfloat16)
    grad_query = (
        jnp.einsum("hqk,khd->qhd", grad_scores, key, preferred_element_type=jnp.float32) * scale
    ).astype(jnp.bfloat16)
    grad_key = (
        jnp.einsum("hqk,qhd->khd", grad_scores, query, preferred_element_type=jnp.float32) * scale
    ).astype(jnp.bfloat16)
    grad_value = grad_value.astype(jnp.bfloat16)
    width = count * size
    grad_query = grad_query.reshape(rows, width)
    grad_key = grad_key.reshape(rows, width)
    grad_value = grad_value.reshape(rows, width)
    grad_projected = jnp.stack([grad_query, grad_key, grad_value], axis=1).reshape(rows, 3 * width)
    qv_grad = jnp.stack(
        [
            jnp.sum(grad_query.astype(jnp.float32), axis=0),
            jnp.sum(grad_value.astype(jnp.float32), axis=0),
        ]
    )
    return (grad_projected, qv_grad)


def gelu_product(both):
    return jax.nn.gelu(both[:, 0], approximate=False) * both[:, 1]


def geglu(lifted, up_bias):
    return gelu_product(lifted + up_bias[None])


def ffn_grads(rows_low, grad_low, up_weight, up_bias, down_weight):
    lifted = jnp.einsum("sd,gdf->sgf", rows_low, up_weight, preferred_element_type=jnp.float32)
    hidden, geglu_back = jax.vjp(gelu_product, lifted + up_bias[None])
    grad_hidden = jnp.einsum("sd,df->sf", grad_low, down_weight, preferred_element_type=jnp.float32)
    (grad_both,) = geglu_back(grad_hidden)
    grad_lifted = grad_both.astype(jnp.bfloat16)
    grad_bias = jnp.sum(grad_lifted.astype(jnp.float32), axis=0)
    up_grad = jnp.einsum("sd,sgf->gdf", rows_low, grad_lifted, preferred_element_type=jnp.float32)
    down_grad = jnp.einsum(
        "sd,sf->df", grad_low, hidden.astype(jnp.bfloat16), preferred_element_type=jnp.float32
    )
    return (grad_lifted, grad_bias, up_grad, down_grad)


def on_device(
    inputs,
    cotangent,
    lengths,
    w_qkv,
    b_qv,
    w_out,
    b_out,
    ln_gain,
    ln_bias,
    w_up,
    b_up,
    w_down,
    b_down,
):
    batches, shard_rows, width = inputs.shape
    parts = lax.axis_size("tensor")
    place = lax.axis_index("tensor")
    section = lax.axis_index("section")
    last_section = lax.axis_size("section") - 1
    full_rows = shard_rows * parts
    local_width = w_qkv.shape[3]
    local_heads = local_width // HD
    qkv_flat = w_qkv[0].reshape(width, 3 * local_width)
    out_weight = w_out[0]
    qv_bias = b_qv[0].astype(jnp.float32)
    out_bias = b_out[0].astype(jnp.float32)
    gains = ln_gain[0].astype(jnp.float32)
    shifts = ln_bias[0].astype(jnp.float32)
    down_bias = b_down[0].astype(jnp.float32)
    slopes = alibi_slopes(place * local_heads, local_heads, H)
    row_place = place * shard_rows + jnp.arange(shard_rows)
    kept_rows = 0

    def key_mask(length):
        return jnp.arange(full_rows) < length

    def after_attention(values, attended, bias, gain_rows, shift_rows):
        return layer_norm(values + attended + bias, gain_rows[0], shift_rows[0])

    def after_ffn(normed, lowered, bias, gain_rows, shift_rows):
        return layer_norm(normed + lowered + bias, gain_rows[1], shift_rows[1])

    def gather_inputs(values):
        return lax.all_gather(values.astype(jnp.bfloat16), "tensor", axis=0, tiled=True)

    def project(gathered):
        return jnp.dot(gathered, qkv_flat, preferred_element_type=jnp.float32).reshape(
            full_rows, 3, local_width
        )

    def attention_forward(values, length):
        gathered = gather_inputs(values)
        projected = project(gathered)
        mixed = attention_core(projected, qv_bias, slopes, key_mask(length))[5]

        def term(start, count):
            return jnp.dot(mixed, out_weight, preferred_element_type=jnp.float32)

        return (
            lax.psum_scatter(
                term(jnp.int32(0), shard_rows * lax.axis_size("tensor")).astype(jnp.bfloat16),
                "tensor",
                scatter_dimension=0,
                tiled=True,
            ).astype(jnp.float32),
            gathered,
            projected,
        )

    up_local = w_up[0]
    up_bias_local = b_up[0].astype(jnp.float32)
    down_local = w_down[0]

    def gather_normed(normed):
        return lax.all_gather(normed.astype(jnp.bfloat16), "tensor", axis=0, tiled=True)

    def ffn_forward(normed):
        lifted = jnp.einsum(
            "sd,gdf->sgf", gather_normed(normed), up_local, preferred_element_type=jnp.float32
        )
        hidden = geglu(lifted, up_bias_local).astype(jnp.bfloat16)

        def term(start, count):
            return jnp.einsum("sf,df->sd", hidden, down_local, preferred_element_type=jnp.float32)

        return lax.psum_scatter(
            term(jnp.int32(0), shard_rows * lax.axis_size("tensor")).astype(jnp.bfloat16),
            "tensor",
            scatter_dimension=0,
            tiled=True,
        ).astype(jnp.float32)

    def ffn_backward(normed, grad_lowered):
        gathered = gather_normed(normed)
        grad_whole = lax.all_gather(grad_lowered.astype(jnp.bfloat16), "tensor", axis=0, tiled=True)
        grad_lifted, grad_bias, up_grad, down_grad = ffn_grads(
            gathered, grad_whole, up_local, up_bias_local, down_local
        )

        def term(start, count):
            return jnp.einsum(
                "sgf,gdf->sd", grad_lifted, up_local, preferred_element_type=jnp.float32
            )

        grad_normed = lax.psum_scatter(
            term(jnp.int32(0), shard_rows * lax.axis_size("tensor")).astype(jnp.bfloat16),
            "tensor",
            scatter_dimension=0,
            tiled=True,
        ).astype(jnp.float32)
        return (grad_normed, (up_grad, grad_bias, down_grad))

    ffn_shapes = (up_local.shape, up_bias_local.shape, down_local.shape)

    def layer_forward(values, length):
        attended, gathered, projected = attention_forward(values, length)
        normed = after_attention(values, attended, out_bias, gains, shifts)
        lowered = ffn_forward(normed)
        return (
            after_ffn(normed, lowered, down_bias, gains, shifts),
            attended,
            lowered,
            gathered,
            projected,
        )

    def layer_backward(values, attended, lowered, length, grad_output):
        normed, attention_norm_back = jax.vjp(
            after_attention, values, attended, out_bias, gains, shifts
        )
        outcome, ffn_norm_back = jax.vjp(after_ffn, normed, lowered, down_bias, gains, shifts)
        grad_normed, grad_lowered, grad_down_bias, gain_late, shift_late = ffn_norm_back(
            grad_output
        )
        grad_from_ffn, ffn_terms = ffn_backward(normed, grad_lowered)
        grad_values, grad_attended, grad_out_bias, gain_early, shift_early = attention_norm_back(
            grad_normed + grad_from_ffn
        )
        gathered = gather_inputs(values)
        projected = project(gathered)
        grad_whole = lax.all_gather(
            grad_attended.astype(jnp.bfloat16), "tensor", axis=0, tiled=True
        )
        mask = key_mask(length)
        pieces = attention_core(projected, qv_bias, slopes, mask)
        mixed_low = pieces[5]
        out_grad = jnp.einsum(
            "se,sd->ed", mixed_low, grad_whole, preferred_element_type=jnp.float32
        )
        grad_mixed = jnp.einsum(
            "sd,ed->se", grad_whole, out_weight, preferred_element_type=jnp.float32
        )
        grad_projected, qv_grad = attention_back(pieces, grad_mixed, mask)
        qkv_grad = jnp.einsum(
            "sd,sx->dx", gathered, grad_projected, preferred_element_type=jnp.float32
        )

        def term(start, count):
            return jnp.einsum(
                "sx,dx->sd", grad_projected, qkv_flat, preferred_element_type=jnp.float32
            )

        grad_inputs = grad_values + lax.psum_scatter(
            term(jnp.int32(0), shard_rows * lax.axis_size("tensor")).astype(jnp.bfloat16),
            "tensor",
            scatter_dimension=0,
            tiled=True,
        ).astype(jnp.float32)
        terms = (
            qkv_grad,
            qv_grad,
            out_grad,
            grad_out_bias,
            gain_early + gain_late,
            shift_early + shift_late,
            ffn_terms[0],
            ffn_terms[1],
            ffn_terms[2],
            grad_down_bias,
        )
        return (grad_inputs, terms)

    def keep(store, item, batch, valid):
        old = lax.dynamic_index_in_dim(store, batch, 0, keepdims=False)
        return lax.dynamic_update_index_in_dim(store, jnp.where(valid, item, old), batch, 0)

    def forward_step(step, carry):
        (
            received,
            kept_values,
            kept_attended,
            kept_lowered,
            produced,
            kept_gathered,
            kept_projected,
        ) = carry
        index = step - section
        valid = (index >= 0) & (index < batches)
        batch = jnp.clip(index, 0, batches - 1)
        fresh = lax.dynamic_index_in_dim(
            inputs, jnp.minimum(step, batches - 1), 0, keepdims=False
        ).astype(jnp.float32)
        values = jnp.where(section == 0, fresh, received.astype(jnp.float32))
        output, attended, lowered, gathered, projected = layer_forward(values, lengths[batch])
        sent = output.astype(jnp.bfloat16)
        kept_values = keep(kept_values, values, batch, valid)
        kept_attended = keep(kept_attended, attended, batch, valid)
        kept_lowered = keep(kept_lowered, lowered, batch, valid)
        produced = keep(produced, sent, batch, valid)
        kept_gathered = keep(kept_gathered, gathered[:kept_rows], batch, valid)
        kept_projected = keep(kept_projected, projected[:kept_rows], batch, valid)
        received = shifted(sent, "section", 1)
        return (
            received,
            kept_values,
            kept_attended,
            kept_lowered,
            produced,
            kept_gathered,
            kept_projected,
        )

    store_zeros = jnp.zeros((batches, shard_rows, width), jnp.float32)
    gathered_zeros = jnp.zeros((batches, kept_rows, width), jnp.bfloat16)
    projected_zeros = jnp.zeros((batches, kept_rows, 3, local_width), jnp.float32)
    start_forward = (
        jnp.zeros((shard_rows, width), jnp.bfloat16),
        store_zeros,
        store_zeros,
        store_zeros,
        jnp.zeros((batches, shard_rows, width), jnp.bfloat16),
        gathered_zeros,
        projected_zeros,
    )
    received, kept_values, kept_attended, kept_lowered, produced, kept_gathered, kept_projected = (
        lax.fori_loop(0, batches + last_section, forward_step, start_forward)
    )

    def backward_step(step, carry):
        received, totals, grads_in = carry
        index = step - (last_section - section)
        valid = (index >= 0) & (index < batches)
        batch = jnp.clip(index, 0, batches - 1)
        length = lengths[batch]
        outer = lax.dynamic_index_in_dim(cotangent, batch, 0, keepdims=False).astype(jnp.float32)
        outer = outer * (row_place < length).astype(jnp.float32)[:, None]
        grad_output = jnp.where(section == last_section, outer, received.astype(jnp.float32))
        grad_output = jnp.where(valid, grad_output, 0.0)
        values = lax.dynamic_index_in_dim(kept_values, batch, 0, keepdims=False)
        attended = lax.dynamic_index_in_dim(kept_attended, batch, 0, keepdims=False)
        lowered = lax.dynamic_index_in_dim(kept_lowered, batch, 0, keepdims=False)
        grad_inputs, terms = layer_backward(values, attended, lowered, length, grad_output)
        totals = jax.tree.map(jnp.add, totals, terms)
        grads_in = keep(grads_in, grad_inputs, batch, valid)
        received = shifted(grad_inputs.astype(jnp.bfloat16), "section", -1)
        return (received, totals, grads_in)

    start_totals = (
        jnp.zeros((width, 3 * local_width), jnp.float32),
        jnp.zeros((2, local_width), jnp.float32),
        jnp.zeros((local_width, width), jnp.float32),
        jnp.zeros((width,), jnp.float32),
        jnp.zeros((2, width), jnp.float32),
        jnp.zeros((2, width), jnp.float32),
        jnp.zeros(ffn_shapes[0], jnp.float32),
        jnp.zeros(ffn_shapes[1], jnp.float32),
        jnp.zeros(ffn_shapes[2], jnp.float32),
        jnp.zeros((width,), jnp.float32),
    )
    start_backward = (jnp.zeros((shard_rows, width), jnp.bfloat16), start_totals, store_zeros)
    received, totals, grads_in = lax.fori_loop(
        0, batches + last_section, backward_step, start_backward
    )
    (
        qkv_total,
        qv_total,
        out_total,
        out_bias_total,
        gain_total,
        shift_total,
        up_total,
        up_bias_total,
        down_total,
        down_bias_total,
    ) = totals
    qkv_sum, qv_sum, out_sum, up_sum, up_bias_sum, down_sum = (
        lax.psum(qkv_total.astype(jnp.bfloat16), "dp").astype(jnp.float32),
        lax.psum(qv_total.astype(jnp.bfloat16), "dp").astype(jnp.float32),
        lax.psum(out_total.astype(jnp.bfloat16), "dp").astype(jnp.float32),
        lax.psum(up_total.astype(jnp.bfloat16), "dp").astype(jnp.float32),
        lax.psum(up_bias_total.astype(jnp.bfloat16), "dp").astype(jnp.float32),
        lax.psum(down_total.astype(jnp.bfloat16), "dp").astype(jnp.float32),
    )
    out_bias_sum, gain_sum, shift_sum, down_bias_sum = lax.psum(
        (out_bias_total, gain_total, shift_total, down_bias_total), ("tensor", "dp")
    )
    return (
        produced[None],
        grads_in[None],
        qkv_sum.reshape(1, width, 3, local_width),
        qv_sum[None],
        out_sum[None],
        out_bias_sum[None],
        gain_sum[None],
        shift_sum[None],
        up_sum[None],
        up_bias_sum[None],
        down_sum[None],
        down_bias_sum[None],
    )


def join(first, second, swapped):
    return jnp.where(
        swapped, jnp.concatenate([second, first], axis=0), jnp.concatenate([first, second], axis=0)
    )


def by_sequence(
    inputs,
    cotangent,
    lengths,
    w_qkv,
    b_qv,
    w_out,
    b_out,
    ln_gain,
    ln_bias,
    w_up,
    b_up,
    w_down,
    b_down,
):
    batches, shard_rows, width = inputs.shape
    place = lax.axis_index("tensor")
    section = lax.axis_index("section")
    groups = lax.axis_size("dp")
    group = lax.axis_index("dp")
    core = group % 2
    rows = 2 * shard_rows
    seqs = batches // 2
    slots = seqs + 1
    local = w_qkv.shape[3]
    units = w_up.shape[3]
    heads = local // HD
    pair = [(index, index ^ 1) for index in range(groups)]

    def across(value):
        return lax.ppermute(value, "tensor", [(0, 1), (1, 0)])

    def partner(value):
        return lax.ppermute(value, "dp", pair)

    def whole_rows(value):
        mine = lax.dynamic_slice_in_dim(value, place * seqs, seqs, 0)
        sent = lax.dynamic_slice_in_dim(value, (1 - place) * seqs, seqs, 0)
        got = across(sent)
        return [join(mine[m], got[m], place == 1) for m in range(seqs)]

    def own_rows(values, low):
        kept = [lax.dynamic_slice_in_dim(v, place * shard_rows, shard_rows, 0) for v in values]
        sent = [lax.dynamic_slice_in_dim(v, (1 - place) * shard_rows, shard_rows, 0) for v in low]
        got = [across(v) for v in sent]
        return join(jnp.stack(kept), jnp.stack(got).astype(values[0].dtype), place == 1)

    def fetch(weight):
        half = weight.shape[0] // 2
        got = across(lax.dynamic_slice_in_dim(weight, core * half, half, 0))
        return join(got, partner(got), core == 1)

    def fetch_wide(weight):
        part = weight.shape[0] // groups
        got = across(lax.dynamic_slice_in_dim(weight, group * part, part, 0))
        return lax.all_gather(got, "dp", axis=0, tiled=True)

    qkv_own = jnp.transpose(w_qkv[0], (1, 0, 2))
    out_own = w_out[0]
    up_own = w_up[0]
    down_own = w_down[0]
    x_first = whole_rows(inputs)
    small = across(jnp.concatenate([b_qv[0], b_up[0]], axis=1))
    qkv_oth = fetch(qkv_own.reshape(3 * width, local)).reshape(3, width, local)
    out_oth = fetch(out_own)
    up_oth = fetch_wide(up_own.reshape(2 * width, units)).reshape(2, width, units)
    down_oth = fetch(down_own)
    outer = whole_rows(cotangent)

    bias = jnp.concatenate([b_qv[0], small[:, :local]], axis=1).astype(F32)
    up_bias = jnp.concatenate([b_up[0], small[:, local:]], axis=1).astype(F32)
    vecs = jnp.stack(
        [b_out[0], ln_gain[0, 0], ln_bias[0, 0], b_down[0], ln_gain[0, 1], ln_bias[0, 1], b_out[0], b_out[0]]
    ).astype(F32)
    slopes = jnp.concatenate(
        [alibi_slopes(place * heads, heads, H), alibi_slopes((1 - place) * heads, heads, H)]
    )
    own_lengths = lax.dynamic_slice_in_dim(lengths, place * seqs, seqs, 0)

    def meta(m, turn):
        active = section == turn
        return jnp.stack([jnp.where(active, m, seqs), active.astype(jnp.int32), own_lengths[m]])

    metas = [[meta(m, turn) for m in range(seqs)] for turn in range(2)]
    att = ffn = None
    deps = []

    def attention(x, m, turn):
        nonlocal att, deps
        att = attention_forward(x, qkv_own, qkv_oth, bias, slopes, metas[turn][m], att, deps, slots)
        deps = [att[4]]

    def feed(x, m, turn):
        nonlocal ffn, deps
        ffn = ffn_forward(
            x, att[3], out_own, out_oth, up_own, up_oth, down_own, down_oth, vecs, up_bias,
            metas[turn][m], ffn, deps, slots,
        )
        *ffn, y = ffn
        deps = [y]
        return y

    for m in range(seqs):
        attention(x_first[m], m, 0)
    y_first = [feed(x_first[m], m, 0) for m in range(seqs)]
    x_second = [lax.ppermute(y, "section", [(0, 1)]) for y in y_first]
    y_second = []
    for m in range(seqs):
        attention(x_second[m], m, 1)
        y_second.append(feed(x_second[m], m, 1))

    bff = bat = None
    sums = [[None] * seqs, [None] * seqs]

    def back(grad, m, turn):
        nonlocal bff, bat, deps
        act, slope, hidden, normed, u1, u2, r1, r2 = ffn
        *bff, gaf, norm_sums, up_sums = ffn_backward(
            grad, u2, r2, u1, r1, act, slope, up_own, up_oth, down_own, down_oth, vecs,
            metas[turn][m], bff, deps, slots,
        )
        deps = [norm_sums]
        *bat, gx, gx_low, qv_sums = attention_backward(
            bff[3], gaf, att[0], att[1], att[2], att[4], out_own, out_oth, qkv_own, qkv_oth, slopes,
            metas[turn][m], bat, deps, slots,
        )
        deps = [qv_sums]
        sums[turn][m] = (norm_sums, up_sums, qv_sums)
        return gx, gx_low

    row = jnp.arange(rows)[:, None]
    gx_second = [
        back(jnp.where(row < own_lengths[m], outer[m], 0), m, 1) for m in range(seqs)
    ]
    grad_middle = [lax.ppermute(gx_second[m][1], "section", [(1, 0)]) for m in range(seqs)]
    gx_first = [back(grad_middle[m], m, 0) for m in range(seqs)]

    first = section == 0
    hidden, normed = ffn[2], ffn[3]
    mixed = att[3]
    x_all = jnp.stack([jnp.where(first, x_first[m], x_second[m]) for m in range(seqs)])
    gg0, gg1, gl, ga = bff
    d_up = weight_grads(normed, [gg0, gg1], seqs, "grad_up")
    (d_down,) = weight_grads(gl, [hidden], seqs, "grad_down")
    d_qkv = weight_grads(x_all, bat, seqs, "grad_qkv")
    (d_out,) = weight_grads(mixed, [ga], seqs, "grad_out")

    produced = own_rows(*[[jnp.where(first, a, b) for a, b in zip(y_first, y_second)]] * 2)
    grads_in = own_rows(
        [jnp.where(first, a[0], b[0]) for a, b in zip(gx_first, gx_second)],
        [jnp.where(first, a[1], b[1]) for a, b in zip(gx_first, gx_second)],
    )

    def reduce_columns(grad, count):
        total = grad[:, :count] + across(grad[:, count:])
        return lax.psum(total, "dp").astype(F32)

    up_sum = jnp.stack([reduce_columns(g, units) for g in d_up])
    down_sum = reduce_columns(d_down, units)
    qkv_sum = jnp.stack([reduce_columns(g, local) for g in d_qkv], axis=1)
    out_sum = lax.psum(d_out[:local] + across(d_out[local:]), "dp").astype(F32)

    picked = [
        sum(jnp.where(first, sums[0][m][index], sums[1][m][index]) for m in range(seqs))
        for index in range(3)
    ]
    norm_sums, up_sums, qv_sums = picked

    def ordered(values, count):
        return jnp.where(
            place == 0, values, jnp.concatenate([values[:, count:], values[:, :count]], axis=1)
        )

    packed = jnp.concatenate(
        [norm_sums[:6].reshape(-1), ordered(up_sums[:2], units).reshape(-1), ordered(qv_sums[:2], local).reshape(-1)]
    )
    packed = lax.psum(packed, ("tensor", "dp"))
    norm_total = packed[: 6 * width].reshape(6, width)
    up_total = packed[6 * width : 6 * width + 4 * units].reshape(2, 2 * units)
    qv_total = packed[6 * width + 4 * units :].reshape(2, 2 * local)
    up_bias_sum = lax.dynamic_slice_in_dim(up_total, place * units, units, 1)
    qv_sum = lax.dynamic_slice_in_dim(qv_total, place * local, local, 1)
    gain_sum = jnp.stack([norm_total[3], norm_total[0]])
    shift_sum = jnp.stack([norm_total[4], norm_total[1]])
    return (
        produced[None],
        grads_in[None],
        qkv_sum[None],
        qv_sum[None],
        out_sum[None],
        norm_total[5][None],
        gain_sum[None],
        shift_sum[None],
        up_sum[None],
        up_bias_sum[None],
        down_sum[None],
        norm_total[2][None],
    )


def solution(mesh):
    sections, parts, groups = (mesh.shape[name] for name in ("section", "tensor", "dp"))

    def run(*args):
        paired = sections == 2 and parts == 2 and groups % 2 == 0 and args[0].shape[0] == 4
        return (by_sequence if paired else on_device)(*args)

    return jax.shard_map(
        run,
        mesh=mesh,
        in_specs=(
            P("dp", "tensor", None),
            P("dp", "tensor", None),
            P("dp"),
            P("section", None, None, "tensor"),
            P("section", None, "tensor"),
            P("section", "tensor", None),
            P("section", None),
            P("section", None, None),
            P("section", None, None),
            P("section", None, None, "tensor"),
            P("section", None, "tensor"),
            P("section", None, "tensor"),
            P("section", None),
        ),
        out_specs=(
            P("section", "dp", "tensor", None),
            P("section", "dp", "tensor", None),
            P("section", None, None, "tensor"),
            P("section", None, "tensor"),
            P("section", "tensor", None),
            P("section", None),
            P("section", None, None),
            P("section", None, None),
            P("section", None, None, "tensor"),
            P("section", None, "tensor"),
            P("section", None, "tensor"),
            P("section", None),
        ),
        check_vma=False,
    )
```

```python
import functools
import math

import jax
import jax.numpy as jnp
from jax import lax
from jax.experimental import pallas as pl
from jax.experimental.pallas import tpu as pltpu
from jax.sharding import PartitionSpec as P

H = 16
HD = 64
EPS = 1e-05
BF = jnp.bfloat16
F32 = jnp.float32
VMEM_LIMIT = 62 * 1024 * 1024
ANY = pl.BlockSpec(memory_space=pl.ANY)
NN = (((1,), (0,)), ((), ()))
NT = (((1,), (1,)), ((), ()))
TN = (((0,), (0,)), ((), ()))


def dot(a, b, dims=NN):
    return lax.dot_general(a, b, dims, preferred_element_type=F32)


def call(kernel, grid, inputs, outputs, scratch, meta, chain, deps, name, flops, nbytes):
    args = [a for a, _ in inputs]
    specs = [s for _, s in inputs]
    n_in = len(args)
    aliases = {}
    if chain is not None:
        chained = [index for index, item in enumerate(outputs) if item[3]]
        for buffer, index in zip(chain, chained):
            aliases[1 + len(args)] = index
            args.append(buffer)
            specs.append(ANY)
    for item in deps:
        args.append(item)
        specs.append(ANY)
    n_args = len(args)

    def body(meta_ref, *refs):
        kernel(meta_ref, refs[:n_in], refs[n_args : n_args + len(outputs)], refs[n_args + len(outputs) :])

    return pl.pallas_call(
        body,
        grid_spec=pltpu.PrefetchScalarGridSpec(
            num_scalar_prefetch=1,
            grid=grid,
            in_specs=specs,
            out_specs=[o[2] for o in outputs],
            scratch_shapes=scratch,
        ),
        out_shape=[jax.ShapeDtypeStruct(o[0], o[1]) for o in outputs],
        input_output_aliases=aliases,
        compiler_params=pltpu.CompilerParams(
            dimension_semantics=("arbitrary",) * len(grid), vmem_limit_bytes=VMEM_LIMIT
        ),
        cost_estimate=pl.CostEstimate(flops=flops, bytes_accessed=nbytes, transcendentals=0),
        name=name,
    )(meta, *args)


def own_map(count, make):
    return lambda i, meta: make(jnp.minimum(i, count - 1) * meta[1])


def oth_map(count, make):
    return lambda i, meta: make(jnp.maximum(i - count, 0) * meta[1])


def tile_map(make):
    return lambda i, meta: make(meta[0], i * meta[1])


def fixed(shape):
    zeros = (0,) * len(shape)
    return pl.BlockSpec(shape, lambda i, meta: zeros, pipeline_mode=pl.Buffered(1))


def fill_distance(dist_ref, length):
    rows = dist_ref.shape[0]
    keys = lax.broadcasted_iota(jnp.int32, (rows, rows), 0)
    places = lax.broadcasted_iota(jnp.int32, (rows, rows), 1)
    distance = jnp.abs(keys - places).astype(F32)
    dist_ref[...] = jnp.where(keys < length, distance, 1e12)


def attention_forward(x, w_own, w_oth, bias, slopes, meta, chain, deps, slots):
    rows, width = x.shape
    local = w_own.shape[2]
    cw = 256
    per = cw // HD
    count = local // cw
    steps = 2 * count
    total = 2 * local

    def kernel(meta_ref, ins, outs, scratch):
        x_ref, own_ref, oth_ref, bias_ref, slope_ref = ins
        q_ref, k_ref, v_ref, mixed_ref, lse_ref = outs
        (dist_ref,) = scratch
        i = pl.program_id(0)

        def work(w_ref):
            values = x_ref[...]
            b = bias_ref[...]
            q_ref[0] = (dot(values, w_ref[0]) + b[0:1]).astype(BF)
            k_ref[0] = dot(values, w_ref[1]).astype(BF)
            v_ref[0] = (dot(values, w_ref[2]) + b[1:2]).astype(BF)
            for head in range(per):
                cols = slice(head * HD, (head + 1) * HD)
                query = q_ref[0, :, cols] * BF(1.0 / math.sqrt(HD))
                scores = dot(k_ref[0, :, cols], query, NT)
                scores = scores - dist_ref[...] * slope_ref[i * per + head]
                top = jnp.max(scores, axis=0, keepdims=True)
                weights = jnp.exp(scores - top)
                total_weight = jnp.sum(weights, axis=0, keepdims=True)
                low = (weights * (1.0 / total_weight)).astype(BF)
                mixed_ref[0, :, cols] = dot(low, v_ref[0, :, cols], TN).astype(BF)
                lse_ref[0, 0, head : head + 1, :] = top + jnp.log(total_weight)

        @pl.when(meta_ref[1] == 1)
        def _():
            @pl.when(i == 0)
            def _():
                fill_distance(dist_ref, meta_ref[2])

            @pl.when(i < count)
            def _():
                work(own_ref)

            @pl.when(i >= count)
            def _():
                work(oth_ref)

    wide = pl.BlockSpec((1, rows, cw), tile_map(lambda s, i: (s, 0, i)))
    return call(
        kernel,
        (steps,),
        [
            (x, fixed((rows, width))),
            (w_own, pl.BlockSpec((3, width, cw), own_map(count, lambda i: (0, 0, i)))),
            (w_oth, pl.BlockSpec((3, width, cw), oth_map(count, lambda i: (0, 0, i)))),
            (bias, pl.BlockSpec((2, cw), lambda i, meta: (0, i * meta[1]))),
            (slopes, pl.BlockSpec(memory_space=pltpu.SMEM)),
        ],
        [((slots, rows, total), BF, wide, True)] * 4
        + [
            (
                (slots, steps, 8, rows),
                F32,
                pl.BlockSpec((1, 1, 8, rows), tile_map(lambda s, i: (s, i, 0, 0))),
                True,
            )
        ],
        [pltpu.VMEM((rows, rows), F32)],
        meta,
        chain,
        deps,
        "attention_forward",
        2 * rows * width * 3 * total + 4 * rows * rows * total,
        12 << 20,
    )


def normalize(v):
    mean = jnp.mean(v, axis=1, keepdims=True)
    centred = v - mean
    rstd = lax.rsqrt(jnp.mean(centred * centred, axis=1, keepdims=True) + EPS)
    return centred * rstd, rstd


def ffn_forward(x, mixed, o_own, o_oth, up_own, up_oth, down_own, down_oth, vecs, up_bias, meta, chain, deps, slots):
    rows, width = x.shape
    local = o_own.shape[0]
    units = up_own.shape[2]
    ft = min(512, units)
    count = units // ft
    steps = 2 * count

    def kernel(meta_ref, ins, outs, scratch):
        x_ref, mixed_ref, o_own_ref, o_oth_ref, u_own_ref, u_oth_ref, d_own_ref, d_oth_ref, vec_ref, ub_ref = ins
        a_ref, b_ref, h_ref, n_ref, u1_ref, u2_ref, r1_ref, r2_ref, y_ref = outs
        normed_ref, acc_ref = scratch
        i = pl.program_id(0)
        vec = vec_ref[...]

        def work(up_ref, down_ref):
            for part in range(2):
                rs = slice(part * rows // 2, (part + 1) * rows // 2)
                low = n_ref[0, rs, :]
                gate = dot(low, up_ref[0]) + ub_ref[0:1]
                lift = dot(low, up_ref[1]) + ub_ref[1:2]
                cdf = 0.5 * lax.erf(gate * (1.0 / math.sqrt(2.0))) + 0.5
                act = gate * cdf
                slope = cdf + gate * (jnp.exp(gate * gate * -0.5) * (1.0 / math.sqrt(2.0 * math.pi)))
                a_ref[0, rs, :] = act.astype(BF)
                b_ref[0, rs, :] = (lift * slope).astype(BF)
                hidden = (act * lift).astype(BF)
                h_ref[0, rs, :] = hidden
                acc_ref[rs, :] += dot(hidden, down_ref[...], NT)

        @pl.when(meta_ref[1] == 1)
        def _():
            @pl.when(i == 0)
            def _():
                attended = dot(mixed_ref[0, :, :local], o_own_ref[...])
                attended += dot(mixed_ref[0, :, local:], o_oth_ref[...])
                u, rstd = normalize(x_ref[...].astype(F32) + attended + vec[0:1])
                normed = u * vec[1:2] + vec[2:3]
                normed_ref[...] = normed
                n_ref[0] = normed.astype(BF)
                u1_ref[0] = u.astype(BF)
                r1_ref[0] = jnp.broadcast_to(rstd, (rows, 128))
                acc_ref[...] = jnp.zeros_like(acc_ref)

            @pl.when(i < count)
            def _():
                work(u_own_ref, d_own_ref)

            @pl.when(i >= count)
            def _():
                work(u_oth_ref, d_oth_ref)

            @pl.when(i == steps - 1)
            def _():
                u, rstd = normalize(normed_ref[...] + acc_ref[...] + vec[3:4])
                u2_ref[0] = u.astype(BF)
                r2_ref[0] = jnp.broadcast_to(rstd, (rows, 128))
                y_ref[...] = (u * vec[4:5] + vec[5:6]).astype(BF)

    tile = pl.BlockSpec((1, rows, ft), tile_map(lambda s, i: (s, 0, i)))
    whole = pl.BlockSpec((1, rows, width), lambda i, meta: (meta[0], 0, 0))
    stat = pl.BlockSpec((1, rows, 128), lambda i, meta: (meta[0], 0, 0))
    return call(
        kernel,
        (steps,),
        [
            (x, fixed((rows, width))),
            (mixed, pl.BlockSpec((1, rows, 2 * local), lambda i, meta: (meta[0], 0, 0), pipeline_mode=pl.Buffered(1))),
            (o_own, fixed((local, width))),
            (o_oth, fixed((local, width))),
            (up_own, pl.BlockSpec((2, width, ft), own_map(count, lambda i: (0, 0, i)))),
            (up_oth, pl.BlockSpec((2, width, ft), oth_map(count, lambda i: (0, 0, i)))),
            (down_own, pl.BlockSpec((width, ft), own_map(count, lambda i: (0, i)))),
            (down_oth, pl.BlockSpec((width, ft), oth_map(count, lambda i: (0, i)))),
            (vecs, fixed((8, width))),
            (up_bias, pl.BlockSpec((2, ft), lambda i, meta: (0, i * meta[1]))),
        ],
        [((slots, rows, 2 * units), BF, tile, True)] * 3
        + [((slots, rows, width), BF, whole, True)] * 3
        + [((slots, rows, 128), F32, stat, True)] * 2
        + [((rows, width), BF, pl.BlockSpec((rows, width), lambda i, meta: (0, 0)), False)],
        [pltpu.VMEM((rows, width), F32), pltpu.VMEM((rows, width), F32)],
        meta,
        chain,
        deps,
        "ffn_forward",
        2 * rows * width * (6 * units + 2 * local),
        45 << 20,
    )


def ffn_backward(grad, u2, r2, u1, r1, act, slope, up_own, up_oth, down_own, down_oth, vecs, meta, chain, deps, slots):
    rows, width = grad.shape
    units = up_own.shape[2]
    ft = min(512, units)
    count = units // ft
    steps = 2 * count

    def kernel(meta_ref, ins, outs, scratch):
        g_ref, u2_ref, r2_ref, u1_ref, r1_ref, a_ref, b_ref, u_own_ref, u_oth_ref, d_own_ref, d_oth_ref, vec_ref = ins
        gg0_ref, gg1_ref, gl_ref, ga_ref, gaf_ref, sums_ref, ub_ref = outs
        (acc_ref,) = scratch
        i = pl.program_id(0)
        vec = vec_ref[...]

        def norm_back(grad_z, u, rstd, gain):
            t = grad_z * gain
            return rstd * (
                t - jnp.mean(t, axis=1, keepdims=True) - u * jnp.mean(t * u, axis=1, keepdims=True)
            )

        def work(up_ref, down_ref):
            s0 = jnp.zeros((1, ft), F32)
            s1 = jnp.zeros((1, ft), F32)
            for part in range(2):
                rs = slice(part * rows // 2, (part + 1) * rows // 2)
                gh = dot(gl_ref[0, rs, :], down_ref[...])
                g0 = (gh * b_ref[0, rs, :].astype(F32)).astype(BF)
                g1 = (gh * a_ref[0, rs, :].astype(F32)).astype(BF)
                gg0_ref[0, rs, :] = g0
                gg1_ref[0, rs, :] = g1
                s0 += jnp.sum(g0.astype(F32), axis=0, keepdims=True)
                s1 += jnp.sum(g1.astype(F32), axis=0, keepdims=True)
                acc_ref[rs, :] += dot(g0, up_ref[0], NT) + dot(g1, up_ref[1], NT)
            ub_ref[...] = jnp.concatenate([s0, s1, jnp.zeros((6, ft), F32)], axis=0)

        @pl.when(meta_ref[1] == 1)
        def _():
            @pl.when(i == 0)
            def _():
                grad_y = g_ref[...].astype(F32)
                u = u2_ref[0].astype(F32)
                grad_c = norm_back(grad_y, u, r2_ref[0, :, 0:1], vec[4:5])
                acc_ref[...] = grad_c
                gl_ref[0] = grad_c.astype(BF)
                sums_ref[0:1, :] = jnp.sum(grad_y * u, axis=0, keepdims=True)
                sums_ref[1:2, :] = jnp.sum(grad_y, axis=0, keepdims=True)
                sums_ref[2:3, :] = jnp.sum(grad_c, axis=0, keepdims=True)

            @pl.when(i < count)
            def _():
                work(u_own_ref, d_own_ref)

            @pl.when(i >= count)
            def _():
                work(u_oth_ref, d_oth_ref)

            @pl.when(i == steps - 1)
            def _():
                grad_n = acc_ref[...]
                u = u1_ref[0].astype(F32)
                grad_a = norm_back(grad_n, u, r1_ref[0, :, 0:1], vec[1:2])
                ga_ref[0] = grad_a.astype(BF)
                gaf_ref[...] = grad_a
                sums_ref[3:4, :] = jnp.sum(grad_n * u, axis=0, keepdims=True)
                sums_ref[4:5, :] = jnp.sum(grad_n, axis=0, keepdims=True)
                sums_ref[5:6, :] = jnp.sum(grad_a, axis=0, keepdims=True)
                sums_ref[6:8, :] = jnp.zeros((2, width), F32)

    tile = pl.BlockSpec((1, rows, ft), tile_map(lambda s, i: (s, 0, i)))
    whole = pl.BlockSpec((1, rows, width), lambda i, meta: (meta[0], 0, 0))
    whole1 = pl.BlockSpec((1, rows, width), lambda i, meta: (meta[0], 0, 0), pipeline_mode=pl.Buffered(1))
    stat = pl.BlockSpec((1, rows, 128), lambda i, meta: (meta[0], 0, 0))
    return call(
        kernel,
        (steps,),
        [
            (grad, fixed((rows, width))),
            (u2, whole1),
            (r2, stat),
            (u1, whole1),
            (r1, stat),
            (act, tile),
            (slope, tile),
            (up_own, pl.BlockSpec((2, width, ft), own_map(count, lambda i: (0, 0, i)))),
            (up_oth, pl.BlockSpec((2, width, ft), oth_map(count, lambda i: (0, 0, i)))),
            (down_own, pl.BlockSpec((width, ft), own_map(count, lambda i: (0, i)))),
            (down_oth, pl.BlockSpec((width, ft), oth_map(count, lambda i: (0, i)))),
            (vecs, fixed((8, width))),
        ],
        [((slots, rows, 2 * units), BF, tile, True)] * 2
        + [((slots, rows, width), BF, whole, True)] * 2
        + [
            ((rows, width), F32, pl.BlockSpec((rows, width), lambda i, meta: (0, 0)), False),
            ((8, width), F32, pl.BlockSpec((8, width), lambda i, meta: (0, 0)), False),
            ((8, 2 * units), F32, pl.BlockSpec((8, ft), lambda i, meta: (0, i)), False),
        ],
        [pltpu.VMEM((rows, width), F32)],
        meta,
        chain,
        deps,
        "ffn_backward",
        2 * rows * width * 6 * units,
        50 << 20,
    )


def attention_backward(ga, gaf, q, k, v, lse, o_own, o_oth, w_own, w_oth, slopes, meta, chain, deps, slots):
    rows, width = gaf.shape
    local = w_own.shape[2]
    cw = 256
    per = cw // HD
    count = local // cw
    steps = 2 * count
    total = 2 * local

    def kernel(meta_ref, ins, outs, scratch):
        ga_ref, gaf_ref, q_ref, k_ref, v_ref, lse_ref, o_own_ref, o_oth_ref, w_own_ref, w_oth_ref, slope_ref = ins
        gq_ref, gk_ref, gv_ref, gx_ref, gxl_ref, sums_ref = outs
        dist_ref, gm_ref, acc_ref = scratch
        i = pl.program_id(0)
        scale = BF(1.0 / math.sqrt(HD))

        def work(o_ref, w_ref):
            gm_ref[...] = dot(ga_ref[0], o_ref[...], NT).astype(BF)
            for head in range(per):
                cols = slice(head * HD, (head + 1) * HD)
                query = q_ref[0, :, cols] * scale
                key = k_ref[0, :, cols]
                gm = gm_ref[:, cols]
                scores = dot(key, query, NT)
                scores = scores - dist_ref[...] * slope_ref[i * per + head]
                weights = jnp.exp(scores - lse_ref[0, 0, head : head + 1, :])
                gv_ref[0, :, cols] = dot(weights.astype(BF), gm).astype(BF)
                gw = dot(v_ref[0, :, cols], gm, NT)
                t = weights * gw
                inner = jnp.sum(t, axis=0, keepdims=True)
                gs = (t - weights * inner).astype(BF)
                gk_ref[0, :, cols] = dot(gs, query).astype(BF)
                gq_ref[0, :, cols] = dot(gs, key * scale, TN).astype(BF)
            acc_ref[...] += (
                dot(gq_ref[0], w_ref[0], NT) + dot(gk_ref[0], w_ref[1], NT) + dot(gv_ref[0], w_ref[2], NT)
            )
            sums_ref[...] = jnp.concatenate(
                [
                    jnp.sum(gq_ref[0].astype(F32), axis=0, keepdims=True),
                    jnp.sum(gv_ref[0].astype(F32), axis=0, keepdims=True),
                    jnp.zeros((6, cw), F32),
                ],
                axis=0,
            )

        @pl.when(meta_ref[1] == 1)
        def _():
            @pl.when(i == 0)
            def _():
                fill_distance(dist_ref, meta_ref[2])
                acc_ref[...] = gaf_ref[...]

            @pl.when(i < count)
            def _():
                work(o_own_ref, w_own_ref)

            @pl.when(i >= count)
            def _():
                work(o_oth_ref, w_oth_ref)

            @pl.when(i == steps - 1)
            def _():
                gx_ref[...] = acc_ref[...]
                gxl_ref[...] = acc_ref[...].astype(BF)

    tile = pl.BlockSpec((1, rows, cw), tile_map(lambda s, i: (s, 0, i)))
    return call(
        kernel,
        (steps,),
        [
            (ga, pl.BlockSpec((1, rows, width), lambda i, meta: (meta[0], 0, 0), pipeline_mode=pl.Buffered(1))),
            (gaf, fixed((rows, width))),
            (q, tile),
            (k, tile),
            (v, tile),
            (lse, pl.BlockSpec((1, 1, 8, rows), tile_map(lambda s, i: (s, i, 0, 0)))),
            (o_own, pl.BlockSpec((cw, width), own_map(count, lambda i: (i, 0)))),
            (o_oth, pl.BlockSpec((cw, width), oth_map(count, lambda i: (i, 0)))),
            (w_own, pl.BlockSpec((3, width, cw), own_map(count, lambda i: (0, 0, i)))),
            (w_oth, pl.BlockSpec((3, width, cw), oth_map(count, lambda i: (0, 0, i)))),
            (slopes, pl.BlockSpec(memory_space=pltpu.SMEM)),
        ],
        [((slots, rows, total), BF, tile, True)] * 3
        + [
            ((rows, width), F32, pl.BlockSpec((rows, width), lambda i, meta: (0, 0)), False),
            ((rows, width), BF, pl.BlockSpec((rows, width), lambda i, meta: (0, 0)), False),
            ((8, total), F32, pl.BlockSpec((8, cw), lambda i, meta: (0, i)), False),
        ],
        [pltpu.VMEM((rows, rows), F32), pltpu.VMEM((rows, cw), BF), pltpu.VMEM((rows, width), F32)],
        meta,
        chain,
        deps,
        "attention_backward",
        2 * rows * width * 4 * total + 10 * rows * rows * total,
        20 << 20,
    )


def weight_grads(left, rights, seqs, name, packed=False):
    rows, depth = left.shape[1:]
    width = rights[0].shape[2]
    nt = 512
    n = len(rights)
    fold = 2 if packed else 1

    def kernel(*refs):
        left_ref, ins, outs, flip_ref = refs[0], refs[1 : 1 + n], refs[1 + n : 1 + 2 * n], refs[1 + 2 * n]

        @pl.when(pl.program_id(0) == 0)
        def _():
            for s in range(seqs):
                flip_ref[:, s * rows : (s + 1) * rows] = left_ref[s].T

        for a, b in zip(ins, outs):
            total = dot(flip_ref[:, :rows], a[0])
            for s in range(1, seqs):
                total += dot(flip_ref[:, s * rows : (s + 1) * rows], a[s])
            if packed:
                b[:, :nt] = total[: depth // 2].astype(BF)
                b[:, nt:] = total[depth // 2 :].astype(BF)
            else:
                b[...] = total.astype(BF)

    return pl.pallas_call(
        kernel,
        grid=(width // nt,),
        in_specs=[pl.BlockSpec((seqs, rows, depth), lambda j: (0, 0, 0), pipeline_mode=pl.Buffered(1))]
        + [pl.BlockSpec((seqs, rows, nt), lambda j: (0, 0, j))] * n,
        out_specs=[pl.BlockSpec((depth // fold, nt * fold), lambda j: (0, j))] * n,
        out_shape=[jax.ShapeDtypeStruct((depth // fold, width * fold), BF)] * n,
        scratch_shapes=[pltpu.VMEM((depth, seqs * rows), BF)],
        compiler_params=pltpu.CompilerParams(
            dimension_semantics=("arbitrary",), vmem_limit_bytes=VMEM_LIMIT
        ),
        cost_estimate=pl.CostEstimate(
            flops=2 * seqs * rows * depth * width * n,
            bytes_accessed=(seqs * rows + depth) * width * n * 2,
            transcendentals=0,
        ),
        name=name,
    )(left, *rights)


def reduce_grads(bigs, packs, out_grad, step_rows=32):
    depth, double = bigs[0].shape
    columns = double // 2
    half = columns // 2
    r = step_rows
    per_core = depth // 2
    quarter = packs[0].shape[0] // 2
    n_big = per_core // r
    n_small = quarter // (2 * r)
    smalls = len(packs) + 1
    total = len(bigs) * n_big + smalls * n_small
    n_in = len(bigs) + smalls
    n_out = n_in

    def kernel(*refs):
        ins = refs[:n_in]
        outs = refs[n_in : n_in + n_out]
        (own, oth, from_x, from_z, final, mine, send_sem, core_sem, x_sem, z_sem, f_sem, load_sem, store_sem, give_sem) = refs[
            n_in + n_out :
        ]
        t = lax.axis_index("tensor")
        d = lax.axis_index("dp")
        chips = lax.axis_size("dp") // 2
        c = lax.rem(d, 2)
        z = d // 2
        last = chips - 1
        other_core = {"dp": d + 1 - 2 * c}
        other_x = {"tensor": 1 - t}
        above = {"dp": d + 2}
        below = {"dp": d - 2}
        MESH = pl.DeviceIdType.MESH

        barrier = pltpu.get_barrier_semaphore()
        pl.semaphore_signal(barrier, inc=1, device_id=other_core, device_id_type=MESH)
        pl.semaphore_signal(barrier, inc=1, device_id=other_x, device_id_type=MESH)

        @pl.when(z < last)
        def _():
            pl.semaphore_signal(barrier, inc=1, device_id=above, device_id_type=MESH)

        @pl.when(z > 0)
        def _():
            pl.semaphore_signal(barrier, inc=1, device_id=below, device_id_type=MESH)

        pl.semaphore_wait(barrier, 2 + jnp.where(z < last, 1, 0) + jnp.where(z > 0, 1, 0))

        def pieces(k, core, side, visit):
            for m in range(len(bigs)):
                @pl.when((k >= m * n_big) & (k < (m + 1) * n_big))
                def _(m=m):
                    start = pl.multiple_of(core * per_core + (k - m * n_big) * r, r)
                    visit(m, ins[m].at[pl.ds(start, r), pl.ds(side * columns, columns)], pl.ds(start, r), slice(0, columns))

            for m in range(smalls):
                base = len(bigs) * n_big + m * n_small

                @pl.when((k >= base) & (k < base + n_small))
                def _(m=m, base=base):
                    for part in range(2):
                        start = pl.multiple_of(core * quarter + (2 * (k - base) + part) * r, r)
                        index = len(bigs) + m
                        if m < len(packs):
                            source = ins[index].at[pl.ds(start, r), pl.ds(side * half, half)]
                        else:
                            source = ins[index].at[pl.ds(side * 2 * quarter + start, r), :]
                        visit(index, source, pl.ds(start, r), slice(part * half, (part + 1) * half))

        def remote(src, dst, kind, sem, device):
            return pltpu.make_async_remote_copy(
                src_ref=src, dst_ref=dst, send_sem=send_sem.at[kind], recv_sem=sem, device_id=device, device_id_type=MESH
            )

        def arrived(dst, sem):
            pltpu.make_async_copy(dst, dst, sem).wait()

        up = slice(0, half)
        down = slice(half, columns)
        sides = ((up, 0, z, above, below), (down, 1, last - z, below, above))

        def guarded(k, extra=None):
            ok = (k >= 0) & (k < total)
            return ok if extra is None else ok & extra

        @pl.loop(0, total + 2 * last + 3)
        def _(s):
            @pl.when(guarded(s))
            def _():
                k = s
                slot = lax.rem(k, 2)

                def visit_oth(index, source, rows, cols):
                    remote(source, oth.at[k, :, cols], 0, core_sem.at[0, k], other_core).start()

                def visit_own(index, source, rows, cols):
                    remote(source, own.at[k, :, cols], 1, core_sem.at[1, k], other_core).start()

                def load_oth(index, source, rows, cols):
                    pltpu.make_async_copy(source, mine.at[slot, 0, :, cols], load_sem.at[slot, 0]).start()

                def load_own(index, source, rows, cols):
                    pltpu.make_async_copy(source, mine.at[slot, 1, :, cols], load_sem.at[slot, 1]).start()

                pieces(k, 1 - c, 1, visit_oth)
                pieces(k, 1 - c, 0, visit_own)
                pieces(k, c, 1, load_oth)
                pieces(k, c, 0, load_own)

            k1 = s - 1

            @pl.when(guarded(k1))
            def _():
                slot = lax.rem(k1, 2)
                arrived(oth.at[k1], core_sem.at[0, k1])
                arrived(mine.at[slot, 0], load_sem.at[slot, 0])
                oth[k1] = (oth[k1].astype(F32) + mine[slot, 0].astype(F32)).astype(BF)
                arrived(own.at[k1], core_sem.at[1, k1])
                arrived(mine.at[slot, 1], load_sem.at[slot, 1])
                own[k1] = (own[k1].astype(F32) + mine[slot, 1].astype(F32)).astype(BF)
                remote(oth.at[k1], from_x.at[k1], 2, x_sem.at[k1], other_x).start()

            k2 = s - 2

            @pl.when(guarded(k2))
            def _():
                arrived(from_x.at[k2], x_sem.at[k2])
                own[k2] = (own[k2].astype(F32) + from_x[k2].astype(F32)).astype(BF)

            for cols, way, place, ahead, behind in sides:
                k3 = s - 2 - place

                @pl.when(guarded(k3, place > 0))
                def _(cols=cols, way=way, k3=k3):
                    arrived(from_z.at[k3, :, cols], z_sem.at[way, k3])
                    own[k3, :, cols] = (own[k3, :, cols].astype(F32) + from_z[k3, :, cols].astype(F32)).astype(BF)

                @pl.when(guarded(k3, place < last))
                def _(cols=cols, way=way, k3=k3, ahead=ahead):
                    remote(own.at[k3, :, cols], from_z.at[k3, :, cols], 3 + way, z_sem.at[way, k3], ahead).start()

                k4 = s - 2 - last - (last - place)

                @pl.when(guarded(k4, place == last))
                def _(cols=cols, k4=k4):
                    final[k4, :, cols] = own[k4, :, cols]

                @pl.when(guarded(k4, place < last))
                def _(cols=cols, way=way, k4=k4):
                    arrived(final.at[k4, :, cols], f_sem.at[way, k4])

                @pl.when(guarded(k4, place > 0))
                def _(cols=cols, way=way, k4=k4, behind=behind):
                    remote(final.at[k4, :, cols], final.at[k4, :, cols], 5 + way, f_sem.at[way, k4], behind).start()

            k5 = s - 2 - 2 * last

            @pl.when(guarded(k5))
            def _():
                def store(index, source, rows, cols):
                    pltpu.make_async_copy(final.at[k5, :, cols], target(index, rows, cols), store_sem).start()
                    remote(final.at[k5, :, cols], target(index, rows, cols), 7, give_sem, other_core).start()

                def target(index, rows, cols):
                    return outs[index].at[rows, :]

                pieces(k5, c, 0, store)

        def drained(ref, sem):
            pltpu.make_async_copy(ref, ref, sem).wait()

        drained(oth, send_sem.at[0])
        drained(own, send_sem.at[1])
        drained(oth, send_sem.at[2])
        for cols, way, place, ahead, behind in sides:
            @pl.when(place < last)
            def _(cols=cols, way=way):
                drained(from_z.at[:, :, cols], send_sem.at[3 + way])

            @pl.when(place > 0)
            def _(cols=cols, way=way):
                drained(final.at[:, :, cols], send_sem.at[5 + way])

        drained(final, send_sem.at[7])
        drained(final, store_sem)
        drained(final, give_sem)

    buffer = pltpu.VMEM((total, r, columns), BF)
    moved = 2 * total * r * columns
    return pl.pallas_call(
        kernel,
        in_specs=[ANY] * n_in,
        out_specs=[ANY] * n_out,
        out_shape=[jax.ShapeDtypeStruct((depth, columns), BF)] * len(bigs)
        + [jax.ShapeDtypeStruct((2 * quarter, half), BF)] * smalls,
        scratch_shapes=[buffer] * 5
        + [
            pltpu.VMEM((2, 2, r, columns), BF),
            pltpu.SemaphoreType.DMA((8,)),
            pltpu.SemaphoreType.DMA((2, total)),
            pltpu.SemaphoreType.DMA((total,)),
            pltpu.SemaphoreType.DMA((2, total)),
            pltpu.SemaphoreType.DMA((2, total)),
            pltpu.SemaphoreType.DMA((2, 2)),
            pltpu.SemaphoreType.DMA,
            pltpu.SemaphoreType.DMA,
        ],
        compiler_params=pltpu.CompilerParams(
            collective_id=0, has_side_effects=True, vmem_limit_bytes=VMEM_LIMIT
        ),
        cost_estimate=pl.CostEstimate(flops=4 * moved, bytes_accessed=12 * moved, transcendentals=0),
        name="reduce_grads",
    )(*bigs, *packs, out_grad)


MASKED = -1000000000.0


def shifted(value, axis, steps):
    count = lax.axis_size(axis)
    first, last = (max(0, -steps), min(count, count - steps))
    return lax.ppermute(value, axis, [(source, source + steps) for source in range(first, last)])


def layer_norm(values, gain, shift):
    mean = jnp.mean(values, axis=-1, keepdims=True)
    centred = values - mean
    spread = jnp.mean(centred * centred, axis=-1, keepdims=True)
    return centred * lax.rsqrt(spread + EPS) * gain + shift


def alibi_slopes(first, count, heads):
    index = (first + jnp.arange(count)).astype(jnp.float32)
    return jnp.exp2(-8.0 * (index + 1.0) / heads)


def attention_core(projected, qv_bias, slopes, key_ok):
    rows = projected.shape[0]
    width = projected.shape[2]
    count = slopes.shape[0]
    size = width // count
    query = (projected[:, 0] + qv_bias[0]).astype(jnp.bfloat16).reshape(rows, count, size)
    key = projected[:, 1].astype(jnp.bfloat16).reshape(rows, count, size)
    value = (projected[:, 2] + qv_bias[1]).astype(jnp.bfloat16).reshape(rows, count, size)
    place = jnp.arange(rows).astype(jnp.float32)
    distance = jnp.abs(place[:, None] - place[None, :])
    scale = 1.0 / math.sqrt(size)
    scores = (
        jnp.einsum("qhd,khd->hqk", query, key, preferred_element_type=jnp.float32) * scale
        - slopes[:, None, None] * distance[None]
    )
    scores = jnp.where(key_ok[None, None, :], scores, MASKED)
    weights = jax.nn.softmax(scores, axis=-1)
    weights_low = weights.astype(jnp.bfloat16)
    mixed = jnp.einsum("hqk,khd->qhd", weights_low, value, preferred_element_type=jnp.float32)
    mixed = mixed.reshape(rows, width).astype(jnp.bfloat16)
    return (query, key, value, weights, weights_low, mixed)


def attention_back(parts, grad_mixed, key_ok):
    query, key, value, weights, weights_low, mixed = parts
    rows, count, size = query.shape
    scale = 1.0 / math.sqrt(size)
    grad_low = grad_mixed.astype(jnp.bfloat16).reshape(rows, count, size)
    grad_weights = jnp.einsum("qhd,khd->hqk", grad_low, value, preferred_element_type=jnp.float32)
    grad_value = jnp.einsum(
        "hqk,qhd->khd", weights_low, grad_low, preferred_element_type=jnp.float32
    )
    inner = jnp.sum(weights * grad_weights, axis=-1, keepdims=True)
    grad_scores = weights * (grad_weights - inner)
    grad_scores = jnp.where(key_ok[None, None, :], grad_scores, 0.0).astype(jnp.bfloat16)
    grad_query = (
        jnp.einsum("hqk,khd->qhd", grad_scores, key, preferred_element_type=jnp.float32) * scale
    ).astype(jnp.bfloat16)
    grad_key = (
        jnp.einsum("hqk,qhd->khd", grad_scores, query, preferred_element_type=jnp.float32) * scale
    ).astype(jnp.bfloat16)
    grad_value = grad_value.astype(jnp.bfloat16)
    width = count * size
    grad_query = grad_query.reshape(rows, width)
    grad_key = grad_key.reshape(rows, width)
    grad_value = grad_value.reshape(rows, width)
    grad_projected = jnp.stack([grad_query, grad_key, grad_value], axis=1).reshape(rows, 3 * width)
    qv_grad = jnp.stack(
        [
            jnp.sum(grad_query.astype(jnp.float32), axis=0),
            jnp.sum(grad_value.astype(jnp.float32), axis=0),
        ]
    )
    return (grad_projected, qv_grad)


def gelu_product(both):
    return jax.nn.gelu(both[:, 0], approximate=False) * both[:, 1]


def geglu(lifted, up_bias):
    return gelu_product(lifted + up_bias[None])


def ffn_grads(rows_low, grad_low, up_weight, up_bias, down_weight):
    lifted = jnp.einsum("sd,gdf->sgf", rows_low, up_weight, preferred_element_type=jnp.float32)
    hidden, geglu_back = jax.vjp(gelu_product, lifted + up_bias[None])
    grad_hidden = jnp.einsum("sd,df->sf", grad_low, down_weight, preferred_element_type=jnp.float32)
    (grad_both,) = geglu_back(grad_hidden)
    grad_lifted = grad_both.astype(jnp.bfloat16)
    grad_bias = jnp.sum(grad_lifted.astype(jnp.float32), axis=0)
    up_grad = jnp.einsum("sd,sgf->gdf", rows_low, grad_lifted, preferred_element_type=jnp.float32)
    down_grad = jnp.einsum(
        "sd,sf->df", grad_low, hidden.astype(jnp.bfloat16), preferred_element_type=jnp.float32
    )
    return (grad_lifted, grad_bias, up_grad, down_grad)


def on_device(
    inputs,
    cotangent,
    lengths,
    w_qkv,
    b_qv,
    w_out,
    b_out,
    ln_gain,
    ln_bias,
    w_up,
    b_up,
    w_down,
    b_down,
):
    batches, shard_rows, width = inputs.shape
    parts = lax.axis_size("tensor")
    place = lax.axis_index("tensor")
    section = lax.axis_index("section")
    last_section = lax.axis_size("section") - 1
    full_rows = shard_rows * parts
    local_width = w_qkv.shape[3]
    local_heads = local_width // HD
    qkv_flat = w_qkv[0].reshape(width, 3 * local_width)
    out_weight = w_out[0]
    qv_bias = b_qv[0].astype(jnp.float32)
    out_bias = b_out[0].astype(jnp.float32)
    gains = ln_gain[0].astype(jnp.float32)
    shifts = ln_bias[0].astype(jnp.float32)
    down_bias = b_down[0].astype(jnp.float32)
    slopes = alibi_slopes(place * local_heads, local_heads, H)
    row_place = place * shard_rows + jnp.arange(shard_rows)
    kept_rows = 0

    def key_mask(length):
        return jnp.arange(full_rows) < length

    def after_attention(values, attended, bias, gain_rows, shift_rows):
        return layer_norm(values + attended + bias, gain_rows[0], shift_rows[0])

    def after_ffn(normed, lowered, bias, gain_rows, shift_rows):
        return layer_norm(normed + lowered + bias, gain_rows[1], shift_rows[1])

    def gather_inputs(values):
        return lax.all_gather(values.astype(jnp.bfloat16), "tensor", axis=0, tiled=True)

    def project(gathered):
        return jnp.dot(gathered, qkv_flat, preferred_element_type=jnp.float32).reshape(
            full_rows, 3, local_width
        )

    def attention_forward(values, length):
        gathered = gather_inputs(values)
        projected = project(gathered)
        mixed = attention_core(projected, qv_bias, slopes, key_mask(length))[5]

        def term(start, count):
            return jnp.dot(mixed, out_weight, preferred_element_type=jnp.float32)

        return (
            lax.psum_scatter(
                term(jnp.int32(0), shard_rows * lax.axis_size("tensor")).astype(jnp.bfloat16),
                "tensor",
                scatter_dimension=0,
                tiled=True,
            ).astype(jnp.float32),
            gathered,
            projected,
        )

    up_local = w_up[0]
    up_bias_local = b_up[0].astype(jnp.float32)
    down_local = w_down[0]

    def gather_normed(normed):
        return lax.all_gather(normed.astype(jnp.bfloat16), "tensor", axis=0, tiled=True)

    def ffn_forward(normed):
        lifted = jnp.einsum(
            "sd,gdf->sgf", gather_normed(normed), up_local, preferred_element_type=jnp.float32
        )
        hidden = geglu(lifted, up_bias_local).astype(jnp.bfloat16)

        def term(start, count):
            return jnp.einsum("sf,df->sd", hidden, down_local, preferred_element_type=jnp.float32)

        return lax.psum_scatter(
            term(jnp.int32(0), shard_rows * lax.axis_size("tensor")).astype(jnp.bfloat16),
            "tensor",
            scatter_dimension=0,
            tiled=True,
        ).astype(jnp.float32)

    def ffn_backward(normed, grad_lowered):
        gathered = gather_normed(normed)
        grad_whole = lax.all_gather(grad_lowered.astype(jnp.bfloat16), "tensor", axis=0, tiled=True)
        grad_lifted, grad_bias, up_grad, down_grad = ffn_grads(
            gathered, grad_whole, up_local, up_bias_local, down_local
        )

        def term(start, count):
            return jnp.einsum(
                "sgf,gdf->sd", grad_lifted, up_local, preferred_element_type=jnp.float32
            )

        grad_normed = lax.psum_scatter(
            term(jnp.int32(0), shard_rows * lax.axis_size("tensor")).astype(jnp.bfloat16),
            "tensor",
            scatter_dimension=0,
            tiled=True,
        ).astype(jnp.float32)
        return (grad_normed, (up_grad, grad_bias, down_grad))

    ffn_shapes = (up_local.shape, up_bias_local.shape, down_local.shape)

    def layer_forward(values, length):
        attended, gathered, projected = attention_forward(values, length)
        normed = after_attention(values, attended, out_bias, gains, shifts)
        lowered = ffn_forward(normed)
        return (
            after_ffn(normed, lowered, down_bias, gains, shifts),
            attended,
            lowered,
            gathered,
            projected,
        )

    def layer_backward(values, attended, lowered, length, grad_output):
        normed, attention_norm_back = jax.vjp(
            after_attention, values, attended, out_bias, gains, shifts
        )
        outcome, ffn_norm_back = jax.vjp(after_ffn, normed, lowered, down_bias, gains, shifts)
        grad_normed, grad_lowered, grad_down_bias, gain_late, shift_late = ffn_norm_back(
            grad_output
        )
        grad_from_ffn, ffn_terms = ffn_backward(normed, grad_lowered)
        grad_values, grad_attended, grad_out_bias, gain_early, shift_early = attention_norm_back(
            grad_normed + grad_from_ffn
        )
        gathered = gather_inputs(values)
        projected = project(gathered)
        grad_whole = lax.all_gather(
            grad_attended.astype(jnp.bfloat16), "tensor", axis=0, tiled=True
        )
        mask = key_mask(length)
        pieces = attention_core(projected, qv_bias, slopes, mask)
        mixed_low = pieces[5]
        out_grad = jnp.einsum(
            "se,sd->ed", mixed_low, grad_whole, preferred_element_type=jnp.float32
        )
        grad_mixed = jnp.einsum(
            "sd,ed->se", grad_whole, out_weight, preferred_element_type=jnp.float32
        )
        grad_projected, qv_grad = attention_back(pieces, grad_mixed, mask)
        qkv_grad = jnp.einsum(
            "sd,sx->dx", gathered, grad_projected, preferred_element_type=jnp.float32
        )

        def term(start, count):
            return jnp.einsum(
                "sx,dx->sd", grad_projected, qkv_flat, preferred_element_type=jnp.float32
            )

        grad_inputs = grad_values + lax.psum_scatter(
            term(jnp.int32(0), shard_rows * lax.axis_size("tensor")).astype(jnp.bfloat16),
            "tensor",
            scatter_dimension=0,
            tiled=True,
        ).astype(jnp.float32)
        terms = (
            qkv_grad,
            qv_grad,
            out_grad,
            grad_out_bias,
            gain_early + gain_late,
            shift_early + shift_late,
            ffn_terms[0],
            ffn_terms[1],
            ffn_terms[2],
            grad_down_bias,
        )
        return (grad_inputs, terms)

    def keep(store, item, batch, valid):
        old = lax.dynamic_index_in_dim(store, batch, 0, keepdims=False)
        return lax.dynamic_update_index_in_dim(store, jnp.where(valid, item, old), batch, 0)

    def forward_step(step, carry):
        (
            received,
            kept_values,
            kept_attended,
            kept_lowered,
            produced,
            kept_gathered,
            kept_projected,
        ) = carry
        index = step - section
        valid = (index >= 0) & (index < batches)
        batch = jnp.clip(index, 0, batches - 1)
        fresh = lax.dynamic_index_in_dim(
            inputs, jnp.minimum(step, batches - 1), 0, keepdims=False
        ).astype(jnp.float32)
        values = jnp.where(section == 0, fresh, received.astype(jnp.float32))
        output, attended, lowered, gathered, projected = layer_forward(values, lengths[batch])
        sent = output.astype(jnp.bfloat16)
        kept_values = keep(kept_values, values, batch, valid)
        kept_attended = keep(kept_attended, attended, batch, valid)
        kept_lowered = keep(kept_lowered, lowered, batch, valid)
        produced = keep(produced, sent, batch, valid)
        kept_gathered = keep(kept_gathered, gathered[:kept_rows], batch, valid)
        kept_projected = keep(kept_projected, projected[:kept_rows], batch, valid)
        received = shifted(sent, "section", 1)
        return (
            received,
            kept_values,
            kept_attended,
            kept_lowered,
            produced,
            kept_gathered,
            kept_projected,
        )

    store_zeros = jnp.zeros((batches, shard_rows, width), jnp.float32)
    gathered_zeros = jnp.zeros((batches, kept_rows, width), jnp.bfloat16)
    projected_zeros = jnp.zeros((batches, kept_rows, 3, local_width), jnp.float32)
    start_forward = (
        jnp.zeros((shard_rows, width), jnp.bfloat16),
        store_zeros,
        store_zeros,
        store_zeros,
        jnp.zeros((batches, shard_rows, width), jnp.bfloat16),
        gathered_zeros,
        projected_zeros,
    )
    received, kept_values, kept_attended, kept_lowered, produced, kept_gathered, kept_projected = (
        lax.fori_loop(0, batches + last_section, forward_step, start_forward)
    )

    def backward_step(step, carry):
        received, totals, grads_in = carry
        index = step - (last_section - section)
        valid = (index >= 0) & (index < batches)
        batch = jnp.clip(index, 0, batches - 1)
        length = lengths[batch]
        outer = lax.dynamic_index_in_dim(cotangent, batch, 0, keepdims=False).astype(jnp.float32)
        outer = outer * (row_place < length).astype(jnp.float32)[:, None]
        grad_output = jnp.where(section == last_section, outer, received.astype(jnp.float32))
        grad_output = jnp.where(valid, grad_output, 0.0)
        values = lax.dynamic_index_in_dim(kept_values, batch, 0, keepdims=False)
        attended = lax.dynamic_index_in_dim(kept_attended, batch, 0, keepdims=False)
        lowered = lax.dynamic_index_in_dim(kept_lowered, batch, 0, keepdims=False)
        grad_inputs, terms = layer_backward(values, attended, lowered, length, grad_output)
        totals = jax.tree.map(jnp.add, totals, terms)
        grads_in = keep(grads_in, grad_inputs, batch, valid)
        received = shifted(grad_inputs.astype(jnp.bfloat16), "section", -1)
        return (received, totals, grads_in)

    start_totals = (
        jnp.zeros((width, 3 * local_width), jnp.float32),
        jnp.zeros((2, local_width), jnp.float32),
        jnp.zeros((local_width, width), jnp.float32),
        jnp.zeros((width,), jnp.float32),
        jnp.zeros((2, width), jnp.float32),
        jnp.zeros((2, width), jnp.float32),
        jnp.zeros(ffn_shapes[0], jnp.float32),
        jnp.zeros(ffn_shapes[1], jnp.float32),
        jnp.zeros(ffn_shapes[2], jnp.float32),
        jnp.zeros((width,), jnp.float32),
    )
    start_backward = (jnp.zeros((shard_rows, width), jnp.bfloat16), start_totals, store_zeros)
    received, totals, grads_in = lax.fori_loop(
        0, batches + last_section, backward_step, start_backward
    )
    (
        qkv_total,
        qv_total,
        out_total,
        out_bias_total,
        gain_total,
        shift_total,
        up_total,
        up_bias_total,
        down_total,
        down_bias_total,
    ) = totals
    qkv_sum, qv_sum, out_sum, up_sum, up_bias_sum, down_sum = (
        lax.psum(qkv_total.astype(jnp.bfloat16), "dp").astype(jnp.float32),
        lax.psum(qv_total.astype(jnp.bfloat16), "dp").astype(jnp.float32),
        lax.psum(out_total.astype(jnp.bfloat16), "dp").astype(jnp.float32),
        lax.psum(up_total.astype(jnp.bfloat16), "dp").astype(jnp.float32),
        lax.psum(up_bias_total.astype(jnp.bfloat16), "dp").astype(jnp.float32),
        lax.psum(down_total.astype(jnp.bfloat16), "dp").astype(jnp.float32),
    )
    out_bias_sum, gain_sum, shift_sum, down_bias_sum = lax.psum(
        (out_bias_total, gain_total, shift_total, down_bias_total), ("tensor", "dp")
    )
    return (
        produced[None],
        grads_in[None],
        qkv_sum.reshape(1, width, 3, local_width),
        qv_sum[None],
        out_sum[None],
        out_bias_sum[None],
        gain_sum[None],
        shift_sum[None],
        up_sum[None],
        up_bias_sum[None],
        down_sum[None],
        down_bias_sum[None],
    )


def join(first, second, swapped):
    return jnp.where(
        swapped, jnp.concatenate([second, first], axis=0), jnp.concatenate([first, second], axis=0)
    )


def by_sequence(
    inputs,
    cotangent,
    lengths,
    w_qkv,
    b_qv,
    w_out,
    b_out,
    ln_gain,
    ln_bias,
    w_up,
    b_up,
    w_down,
    b_down,
):
    batches, shard_rows, width = inputs.shape
    place = lax.axis_index("tensor")
    section = lax.axis_index("section")
    groups = lax.axis_size("dp")
    group = lax.axis_index("dp")
    core = group % 2
    rows = 2 * shard_rows
    seqs = batches // 2
    slots = seqs + 1
    local = w_qkv.shape[3]
    units = w_up.shape[3]
    heads = local // HD
    pair = [(index, index ^ 1) for index in range(groups)]

    def across(value):
        return lax.ppermute(value, "tensor", [(0, 1), (1, 0)])

    def partner(value):
        return lax.ppermute(value, "dp", pair)

    def whole_rows(value):
        mine = lax.dynamic_slice_in_dim(value, place * seqs, seqs, 0)
        sent = lax.dynamic_slice_in_dim(value, (1 - place) * seqs, seqs, 0)
        got = across(sent)
        return [join(mine[m], got[m], place == 1) for m in range(seqs)]

    def own_rows(values, low):
        kept = [lax.dynamic_slice_in_dim(v, place * shard_rows, shard_rows, 0) for v in values]
        sent = [lax.dynamic_slice_in_dim(v, (1 - place) * shard_rows, shard_rows, 0) for v in low]
        got = [across(v) for v in sent]
        return join(jnp.stack(kept), jnp.stack(got).astype(values[0].dtype), place == 1)

    def fetch(weight):
        half = weight.shape[0] // 2
        got = across(lax.dynamic_slice_in_dim(weight, core * half, half, 0))
        return join(got, partner(got), core == 1)

    def fetch_wide(weight):
        part = weight.shape[0] // groups
        got = across(lax.dynamic_slice_in_dim(weight, group * part, part, 0))
        return lax.all_gather(got, "dp", axis=0, tiled=True)

    qkv_own = jnp.transpose(w_qkv[0], (1, 0, 2))
    out_own = w_out[0]
    up_own = w_up[0]
    down_own = w_down[0]
    x_first = whole_rows(inputs)
    small = across(jnp.concatenate([b_qv[0], b_up[0]], axis=1))
    qkv_oth = fetch(qkv_own.reshape(3 * width, local)).reshape(3, width, local)
    out_oth = fetch(out_own)
    up_oth = fetch_wide(up_own.reshape(2 * width, units)).reshape(2, width, units)
    down_oth = fetch(down_own)
    outer = whole_rows(cotangent)

    bias = jnp.concatenate([b_qv[0], small[:, :local]], axis=1).astype(F32)
    up_bias = jnp.concatenate([b_up[0], small[:, local:]], axis=1).astype(F32)
    vecs = jnp.stack(
        [b_out[0], ln_gain[0, 0], ln_bias[0, 0], b_down[0], ln_gain[0, 1], ln_bias[0, 1], b_out[0], b_out[0]]
    ).astype(F32)
    slopes = jnp.concatenate(
        [alibi_slopes(place * heads, heads, H), alibi_slopes((1 - place) * heads, heads, H)]
    )
    own_lengths = lax.dynamic_slice_in_dim(lengths, place * seqs, seqs, 0)

    def meta(m, turn):
        active = section == turn
        return jnp.stack([jnp.where(active, m, seqs), active.astype(jnp.int32), own_lengths[m]])

    metas = [[meta(m, turn) for m in range(seqs)] for turn in range(2)]
    att = ffn = None
    deps = []

    def attention(x, m, turn):
        nonlocal att, deps
        att = attention_forward(x, qkv_own, qkv_oth, bias, slopes, metas[turn][m], att, deps, slots)
        deps = [att[4]]

    def feed(x, m, turn):
        nonlocal ffn, deps
        ffn = ffn_forward(
            x, att[3], out_own, out_oth, up_own, up_oth, down_own, down_oth, vecs, up_bias,
            metas[turn][m], ffn, deps, slots,
        )
        *ffn, y = ffn
        deps = [y]
        return y

    for m in range(seqs):
        attention(x_first[m], m, 0)
    y_first = [feed(x_first[m], m, 0) for m in range(seqs)]
    x_second = [lax.ppermute(y, "section", [(0, 1)]) for y in y_first]
    y_second = []
    for m in range(seqs):
        attention(x_second[m], m, 1)
        y_second.append(feed(x_second[m], m, 1))

    bff = bat = None
    sums = [[None] * seqs, [None] * seqs]

    def back(grad, m, turn):
        nonlocal bff, bat, deps
        act, slope, hidden, normed, u1, u2, r1, r2 = ffn
        *bff, gaf, norm_sums, up_sums = ffn_backward(
            grad, u2, r2, u1, r1, act, slope, up_own, up_oth, down_own, down_oth, vecs,
            metas[turn][m], bff, deps, slots,
        )
        deps = [norm_sums]
        *bat, gx, gx_low, qv_sums = attention_backward(
            bff[3], gaf, att[0], att[1], att[2], att[4], out_own, out_oth, qkv_own, qkv_oth, slopes,
            metas[turn][m], bat, deps, slots,
        )
        deps = [qv_sums]
        sums[turn][m] = (norm_sums, up_sums, qv_sums)
        return gx, gx_low

    row = jnp.arange(rows)[:, None]
    gx_second = [
        back(jnp.where(row < own_lengths[m], outer[m], 0), m, 1) for m in range(seqs)
    ]
    grad_middle = [lax.ppermute(gx_second[m][1], "section", [(1, 0)]) for m in range(seqs)]
    gx_first = [back(grad_middle[m], m, 0) for m in range(seqs)]

    first = section == 0
    hidden, normed = ffn[2], ffn[3]
    mixed = att[3]
    x_all = jnp.stack([jnp.where(first, x_first[m], x_second[m]) for m in range(seqs)])
    gg0, gg1, gl, ga = bff
    d_up = weight_grads(normed, [gg0, gg1], seqs, "grad_up")
    (d_down,) = weight_grads(gl, [hidden], seqs, "grad_down")
    d_qkv = weight_grads(x_all, bat, seqs, "grad_qkv", packed=True)
    (d_out,) = weight_grads(mixed, [ga], seqs, "grad_out")

    produced = own_rows(*[[jnp.where(first, a, b) for a, b in zip(y_first, y_second)]] * 2)
    grads_in = own_rows(
        [jnp.where(first, a[0], b[0]) for a, b in zip(gx_first, gx_second)],
        [jnp.where(first, a[1], b[1]) for a, b in zip(gx_first, gx_second)],
    )

    *sums_big, sum_q, sum_k, sum_v, out_sum = reduce_grads([*d_up, d_down], d_qkv, d_out)
    up_sum = jnp.stack(sums_big[:2]).astype(F32)
    down_sum = sums_big[2].astype(F32)
    qkv_sum = jnp.stack(
        [
            jnp.concatenate([item[:, :local], item[:, local:]], axis=0)
            for item in (sum_q, sum_k, sum_v)
        ],
        axis=1,
    ).astype(F32)
    out_sum = out_sum.astype(F32)

    picked = [
        sum(jnp.where(first, sums[0][m][index], sums[1][m][index]) for m in range(seqs))
        for index in range(3)
    ]
    norm_sums, up_sums, qv_sums = picked

    def ordered(values, count):
        return jnp.where(
            place == 0, values, jnp.concatenate([values[:, count:], values[:, :count]], axis=1)
        )

    packed = jnp.concatenate(
        [norm_sums[:6].reshape(-1), ordered(up_sums[:2], units).reshape(-1), ordered(qv_sums[:2], local).reshape(-1)]
    )
    packed = lax.psum(packed, ("tensor", "dp"))
    norm_total = packed[: 6 * width].reshape(6, width)
    up_total = packed[6 * width : 6 * width + 4 * units].reshape(2, 2 * units)
    qv_total = packed[6 * width + 4 * units :].reshape(2, 2 * local)
    up_bias_sum = lax.dynamic_slice_in_dim(up_total, place * units, units, 1)
    qv_sum = lax.dynamic_slice_in_dim(qv_total, place * local, local, 1)
    gain_sum = jnp.stack([norm_total[3], norm_total[0]])
    shift_sum = jnp.stack([norm_total[4], norm_total[1]])
    return (
        produced[None],
        grads_in[None],
        qkv_sum[None],
        qv_sum[None],
        out_sum[None],
        norm_total[5][None],
        gain_sum[None],
        shift_sum[None],
        up_sum[None],
        up_bias_sum[None],
        down_sum[None],
        norm_total[2][None],
    )


def solution(mesh):
    sections, parts, groups = (mesh.shape[name] for name in ("section", "tensor", "dp"))

    def run(*args):
        paired = sections == 2 and parts == 2 and groups % 2 == 0 and args[0].shape[0] == 4
        return (by_sequence if paired else on_device)(*args)

    return jax.shard_map(
        run,
        mesh=mesh,
        in_specs=(
            P("dp", "tensor", None),
            P("dp", "tensor", None),
            P("dp"),
            P("section", None, None, "tensor"),
            P("section", None, "tensor"),
            P("section", "tensor", None),
            P("section", None),
            P("section", None, None),
            P("section", None, None),
            P("section", None, None, "tensor"),
            P("section", None, "tensor"),
            P("section", None, "tensor"),
            P("section", None),
        ),
        out_specs=(
            P("section", "dp", "tensor", None),
            P("section", "dp", "tensor", None),
            P("section", None, None, "tensor"),
            P("section", None, "tensor"),
            P("section", "tensor", None),
            P("section", None),
            P("section", None, None),
            P("section", None, None),
            P("section", None, None, "tensor"),
            P("section", None, "tensor"),
            P("section", None, "tensor"),
            P("section", None),
        ),
        check_vma=False,
    )
```

```python
import functools
import math

import jax
import jax.numpy as jnp
from jax import lax
from jax.experimental import pallas as pl
from jax.experimental.pallas import tpu as pltpu
from jax.sharding import PartitionSpec as P

H = 16
HD = 64
EPS = 1e-05
BF = jnp.bfloat16
F32 = jnp.float32
VMEM_LIMIT = 62 * 1024 * 1024
ANY = pl.BlockSpec(memory_space=pl.ANY)
NN = (((1,), (0,)), ((), ()))
NT = (((1,), (1,)), ((), ()))
TN = (((0,), (0,)), ((), ()))


def dot(a, b, dims=NN):
    return lax.dot_general(a, b, dims, preferred_element_type=F32)


def call(kernel, grid, inputs, outputs, scratch, meta, chain, deps, name, flops, nbytes):
    args = [a for a, _ in inputs]
    specs = [s for _, s in inputs]
    n_in = len(args)
    aliases = {}
    if chain is not None:
        chained = [index for index, item in enumerate(outputs) if item[3]]
        for buffer, index in zip(chain, chained):
            aliases[1 + len(args)] = index
            args.append(buffer)
            specs.append(ANY)
    for item in deps:
        args.append(item)
        specs.append(ANY)
    n_args = len(args)

    def body(meta_ref, *refs):
        kernel(meta_ref, refs[:n_in], refs[n_args : n_args + len(outputs)], refs[n_args + len(outputs) :])

    return pl.pallas_call(
        body,
        grid_spec=pltpu.PrefetchScalarGridSpec(
            num_scalar_prefetch=1,
            grid=grid,
            in_specs=specs,
            out_specs=[o[2] for o in outputs],
            scratch_shapes=scratch,
        ),
        out_shape=[jax.ShapeDtypeStruct(o[0], o[1]) for o in outputs],
        input_output_aliases=aliases,
        compiler_params=pltpu.CompilerParams(
            dimension_semantics=("arbitrary",) * len(grid), vmem_limit_bytes=VMEM_LIMIT
        ),
        cost_estimate=pl.CostEstimate(flops=flops, bytes_accessed=nbytes, transcendentals=0),
        name=name,
    )(meta, *args)


def own_map(count, make):
    return lambda i, meta: make(jnp.minimum(i, count - 1) * meta[1])


def oth_map(count, make):
    return lambda i, meta: make(jnp.maximum(i - count, 0) * meta[1])


def tile_map(make):
    return lambda i, meta: make(meta[0], i * meta[1])


def fixed(shape):
    zeros = (0,) * len(shape)
    return pl.BlockSpec(shape, lambda i, meta: zeros, pipeline_mode=pl.Buffered(1))


def fill_distance(dist_ref, length):
    rows = dist_ref.shape[0]
    keys = lax.broadcasted_iota(jnp.int32, (rows, rows), 0)
    places = lax.broadcasted_iota(jnp.int32, (rows, rows), 1)
    distance = jnp.abs(keys - places).astype(F32)
    dist_ref[...] = jnp.where(keys < length, distance, 1e12)


def attention_forward(x, w_own, w_oth, bias, slopes, meta, chain, deps, slots):
    rows, width = x.shape
    local = w_own.shape[2]
    cw = 256
    per = cw // HD
    count = local // cw
    steps = 2 * count
    total = 2 * local

    def kernel(meta_ref, ins, outs, scratch):
        x_ref, own_ref, oth_ref, bias_ref, slope_ref = ins
        q_ref, k_ref, v_ref, mixed_ref, lse_ref = outs
        (dist_ref,) = scratch
        i = pl.program_id(0)

        def work(w_ref):
            values = x_ref[...]
            b = bias_ref[...]
            q_ref[0] = (dot(values, w_ref[0]) + b[0:1]).astype(BF)
            k_ref[0] = dot(values, w_ref[1]).astype(BF)
            v_ref[0] = (dot(values, w_ref[2]) + b[1:2]).astype(BF)
            for head in range(per):
                cols = slice(head * HD, (head + 1) * HD)
                query = q_ref[0, :, cols] * BF(1.0 / math.sqrt(HD))
                scores = dot(k_ref[0, :, cols], query, NT)
                scores = scores - dist_ref[...] * slope_ref[i * per + head]
                top = jnp.max(scores, axis=0, keepdims=True)
                weights = jnp.exp(scores - top)
                total_weight = jnp.sum(weights, axis=0, keepdims=True)
                low = (weights * (1.0 / total_weight)).astype(BF)
                mixed_ref[0, :, cols] = dot(low, v_ref[0, :, cols], TN).astype(BF)
                lse_ref[0, 0, head : head + 1, :] = top + jnp.log(total_weight)

        @pl.when(meta_ref[1] == 1)
        def _():
            @pl.when(i == 0)
            def _():
                fill_distance(dist_ref, meta_ref[2])

            @pl.when(i < count)
            def _():
                work(own_ref)

            @pl.when(i >= count)
            def _():
                work(oth_ref)

    wide = pl.BlockSpec((1, rows, cw), tile_map(lambda s, i: (s, 0, i)))
    return call(
        kernel,
        (steps,),
        [
            (x, fixed((rows, width))),
            (w_own, pl.BlockSpec((3, width, cw), own_map(count, lambda i: (0, 0, i)))),
            (w_oth, pl.BlockSpec((3, width, cw), oth_map(count, lambda i: (0, 0, i)))),
            (bias, pl.BlockSpec((2, cw), lambda i, meta: (0, i * meta[1]))),
            (slopes, pl.BlockSpec(memory_space=pltpu.SMEM)),
        ],
        [((slots, rows, total), BF, wide, True)] * 4
        + [
            (
                (slots, steps, 8, rows),
                F32,
                pl.BlockSpec((1, 1, 8, rows), tile_map(lambda s, i: (s, i, 0, 0))),
                True,
            )
        ],
        [pltpu.VMEM((rows, rows), F32)],
        meta,
        chain,
        deps,
        "attention_forward",
        2 * rows * width * 3 * total + 4 * rows * rows * total,
        12 << 20,
    )


def normalize(v):
    mean = jnp.mean(v, axis=1, keepdims=True)
    centred = v - mean
    rstd = lax.rsqrt(jnp.mean(centred * centred, axis=1, keepdims=True) + EPS)
    return centred * rstd, rstd


def ffn_forward(x, mixed, o_own, o_oth, up_own, up_oth, down_own, down_oth, vecs, up_bias, meta, chain, deps, slots):
    rows, width = x.shape
    local = o_own.shape[0]
    units = up_own.shape[2]
    ft = min(512, units)
    count = units // ft
    steps = 2 * count

    def kernel(meta_ref, ins, outs, scratch):
        x_ref, mixed_ref, o_own_ref, o_oth_ref, u_own_ref, u_oth_ref, d_own_ref, d_oth_ref, vec_ref, ub_ref = ins
        a_ref, b_ref, h_ref, n_ref, u1_ref, u2_ref, r1_ref, r2_ref, y_ref = outs
        normed_ref, acc_ref = scratch
        i = pl.program_id(0)
        vec = vec_ref[...]

        def work(up_ref, down_ref):
            for part in range(2):
                rs = slice(part * rows // 2, (part + 1) * rows // 2)
                low = n_ref[0, rs, :]
                gate = dot(low, up_ref[0]) + ub_ref[0:1]
                lift = dot(low, up_ref[1]) + ub_ref[1:2]
                cdf = 0.5 * lax.erf(gate * (1.0 / math.sqrt(2.0))) + 0.5
                act = gate * cdf
                slope = cdf + gate * (jnp.exp(gate * gate * -0.5) * (1.0 / math.sqrt(2.0 * math.pi)))
                a_ref[0, rs, :] = act.astype(BF)
                b_ref[0, rs, :] = (lift * slope).astype(BF)
                hidden = (act * lift).astype(BF)
                h_ref[0, rs, :] = hidden
                acc_ref[rs, :] += dot(hidden, down_ref[...], NT)

        @pl.when(meta_ref[1] == 1)
        def _():
            @pl.when(i == 0)
            def _():
                attended = dot(mixed_ref[0, :, :local], o_own_ref[...])
                attended += dot(mixed_ref[0, :, local:], o_oth_ref[...])
                u, rstd = normalize(x_ref[...].astype(F32) + attended + vec[0:1])
                normed = u * vec[1:2] + vec[2:3]
                normed_ref[...] = normed
                n_ref[0] = normed.astype(BF)
                u1_ref[0] = u.astype(BF)
                r1_ref[0] = jnp.broadcast_to(rstd, (rows, 128))
                acc_ref[...] = jnp.zeros_like(acc_ref)

            @pl.when(i < count)
            def _():
                work(u_own_ref, d_own_ref)

            @pl.when(i >= count)
            def _():
                work(u_oth_ref, d_oth_ref)

            @pl.when(i == steps - 1)
            def _():
                u, rstd = normalize(normed_ref[...] + acc_ref[...] + vec[3:4])
                u2_ref[0] = u.astype(BF)
                r2_ref[0] = jnp.broadcast_to(rstd, (rows, 128))
                y_ref[...] = (u * vec[4:5] + vec[5:6]).astype(BF)

    tile = pl.BlockSpec((1, rows, ft), tile_map(lambda s, i: (s, 0, i)))
    whole = pl.BlockSpec((1, rows, width), lambda i, meta: (meta[0], 0, 0))
    stat = pl.BlockSpec((1, rows, 128), lambda i, meta: (meta[0], 0, 0))
    return call(
        kernel,
        (steps,),
        [
            (x, fixed((rows, width))),
            (mixed, pl.BlockSpec((1, rows, 2 * local), lambda i, meta: (meta[0], 0, 0), pipeline_mode=pl.Buffered(1))),
            (o_own, fixed((local, width))),
            (o_oth, fixed((local, width))),
            (up_own, pl.BlockSpec((2, width, ft), own_map(count, lambda i: (0, 0, i)))),
            (up_oth, pl.BlockSpec((2, width, ft), oth_map(count, lambda i: (0, 0, i)))),
            (down_own, pl.BlockSpec((width, ft), own_map(count, lambda i: (0, i)))),
            (down_oth, pl.BlockSpec((width, ft), oth_map(count, lambda i: (0, i)))),
            (vecs, fixed((8, width))),
            (up_bias, pl.BlockSpec((2, ft), lambda i, meta: (0, i * meta[1]))),
        ],
        [((slots, rows, 2 * units), BF, tile, True)] * 3
        + [((slots, rows, width), BF, whole, True)] * 3
        + [((slots, rows, 128), F32, stat, True)] * 2
        + [((rows, width), BF, pl.BlockSpec((rows, width), lambda i, meta: (0, 0)), False)],
        [pltpu.VMEM((rows, width), F32), pltpu.VMEM((rows, width), F32)],
        meta,
        chain,
        deps,
        "ffn_forward",
        2 * rows * width * (6 * units + 2 * local),
        45 << 20,
    )


def ffn_backward(grad, u2, r2, u1, r1, act, slope, up_own, up_oth, down_own, down_oth, vecs, meta, chain, deps, slots):
    rows, width = grad.shape
    units = up_own.shape[2]
    ft = min(512, units)
    count = units // ft
    steps = 2 * count

    def kernel(meta_ref, ins, outs, scratch):
        g_ref, u2_ref, r2_ref, u1_ref, r1_ref, a_ref, b_ref, u_own_ref, u_oth_ref, d_own_ref, d_oth_ref, vec_ref = ins
        gg0_ref, gg1_ref, gl_ref, ga_ref, gaf_ref, sums_ref, ub_ref = outs
        (acc_ref,) = scratch
        i = pl.program_id(0)
        vec = vec_ref[...]

        def norm_back(grad_z, u, rstd, gain):
            t = grad_z * gain
            return rstd * (
                t - jnp.mean(t, axis=1, keepdims=True) - u * jnp.mean(t * u, axis=1, keepdims=True)
            )

        def work(up_ref, down_ref):
            s0 = jnp.zeros((1, ft), F32)
            s1 = jnp.zeros((1, ft), F32)
            for part in range(2):
                rs = slice(part * rows // 2, (part + 1) * rows // 2)
                gh = dot(gl_ref[0, rs, :], down_ref[...])
                g0 = (gh * b_ref[0, rs, :].astype(F32)).astype(BF)
                g1 = (gh * a_ref[0, rs, :].astype(F32)).astype(BF)
                gg0_ref[0, rs, :] = g0
                gg1_ref[0, rs, :] = g1
                s0 += jnp.sum(g0.astype(F32), axis=0, keepdims=True)
                s1 += jnp.sum(g1.astype(F32), axis=0, keepdims=True)
                acc_ref[rs, :] += dot(g0, up_ref[0], NT) + dot(g1, up_ref[1], NT)
            ub_ref[...] = jnp.concatenate([s0, s1, jnp.zeros((6, ft), F32)], axis=0)

        @pl.when(meta_ref[1] == 1)
        def _():
            @pl.when(i == 0)
            def _():
                grad_y = g_ref[...].astype(F32)
                u = u2_ref[0].astype(F32)
                grad_c = norm_back(grad_y, u, r2_ref[0, :, 0:1], vec[4:5])
                acc_ref[...] = grad_c
                gl_ref[0] = grad_c.astype(BF)
                sums_ref[0:1, :] = jnp.sum(grad_y * u, axis=0, keepdims=True)
                sums_ref[1:2, :] = jnp.sum(grad_y, axis=0, keepdims=True)
                sums_ref[2:3, :] = jnp.sum(grad_c, axis=0, keepdims=True)

            @pl.when(i < count)
            def _():
                work(u_own_ref, d_own_ref)

            @pl.when(i >= count)
            def _():
                work(u_oth_ref, d_oth_ref)

            @pl.when(i == steps - 1)
            def _():
                grad_n = acc_ref[...]
                u = u1_ref[0].astype(F32)
                grad_a = norm_back(grad_n, u, r1_ref[0, :, 0:1], vec[1:2])
                ga_ref[0] = grad_a.astype(BF)
                gaf_ref[...] = grad_a
                sums_ref[3:4, :] = jnp.sum(grad_n * u, axis=0, keepdims=True)
                sums_ref[4:5, :] = jnp.sum(grad_n, axis=0, keepdims=True)
                sums_ref[5:6, :] = jnp.sum(grad_a, axis=0, keepdims=True)
                sums_ref[6:8, :] = jnp.zeros((2, width), F32)

    tile = pl.BlockSpec((1, rows, ft), tile_map(lambda s, i: (s, 0, i)))
    whole = pl.BlockSpec((1, rows, width), lambda i, meta: (meta[0], 0, 0))
    whole1 = pl.BlockSpec((1, rows, width), lambda i, meta: (meta[0], 0, 0), pipeline_mode=pl.Buffered(1))
    stat = pl.BlockSpec((1, rows, 128), lambda i, meta: (meta[0], 0, 0))
    return call(
        kernel,
        (steps,),
        [
            (grad, fixed((rows, width))),
            (u2, whole1),
            (r2, stat),
            (u1, whole1),
            (r1, stat),
            (act, tile),
            (slope, tile),
            (up_own, pl.BlockSpec((2, width, ft), own_map(count, lambda i: (0, 0, i)))),
            (up_oth, pl.BlockSpec((2, width, ft), oth_map(count, lambda i: (0, 0, i)))),
            (down_own, pl.BlockSpec((width, ft), own_map(count, lambda i: (0, i)))),
            (down_oth, pl.BlockSpec((width, ft), oth_map(count, lambda i: (0, i)))),
            (vecs, fixed((8, width))),
        ],
        [((slots, rows, 2 * units), BF, tile, True)] * 2
        + [((slots, rows, width), BF, whole, True)] * 2
        + [
            ((rows, width), F32, pl.BlockSpec((rows, width), lambda i, meta: (0, 0)), False),
            ((8, width), F32, pl.BlockSpec((8, width), lambda i, meta: (0, 0)), False),
            ((8, 2 * units), F32, pl.BlockSpec((8, ft), lambda i, meta: (0, i)), False),
        ],
        [pltpu.VMEM((rows, width), F32)],
        meta,
        chain,
        deps,
        "ffn_backward",
        2 * rows * width * 6 * units,
        50 << 20,
    )


def attention_backward(ga, gaf, q, k, v, lse, o_own, o_oth, w_own, w_oth, slopes, meta, chain, deps, slots):
    rows, width = gaf.shape
    local = w_own.shape[2]
    cw = 256
    per = cw // HD
    count = local // cw
    steps = 2 * count
    total = 2 * local

    def kernel(meta_ref, ins, outs, scratch):
        ga_ref, gaf_ref, q_ref, k_ref, v_ref, lse_ref, o_own_ref, o_oth_ref, w_own_ref, w_oth_ref, slope_ref = ins
        gq_ref, gk_ref, gv_ref, gx_ref, gxl_ref, sums_ref = outs
        dist_ref, gm_ref, acc_ref = scratch
        i = pl.program_id(0)
        scale = BF(1.0 / math.sqrt(HD))

        def work(o_ref, w_ref):
            gm_ref[...] = dot(ga_ref[0], o_ref[...], NT).astype(BF)
            for head in range(per):
                cols = slice(head * HD, (head + 1) * HD)
                query = q_ref[0, :, cols] * scale
                key = k_ref[0, :, cols]
                gm = gm_ref[:, cols]
                scores = dot(key, query, NT)
                scores = scores - dist_ref[...] * slope_ref[i * per + head]
                weights = jnp.exp(scores - lse_ref[0, 0, head : head + 1, :])
                gv_ref[0, :, cols] = dot(weights.astype(BF), gm).astype(BF)
                gw = dot(v_ref[0, :, cols], gm, NT)
                t = weights * gw
                inner = jnp.sum(t, axis=0, keepdims=True)
                gs = (t - weights * inner).astype(BF)
                gk_ref[0, :, cols] = dot(gs, query).astype(BF)
                gq_ref[0, :, cols] = dot(gs, key * scale, TN).astype(BF)
            acc_ref[...] += (
                dot(gq_ref[0], w_ref[0], NT) + dot(gk_ref[0], w_ref[1], NT) + dot(gv_ref[0], w_ref[2], NT)
            )
            sums_ref[...] = jnp.concatenate(
                [
                    jnp.sum(gq_ref[0].astype(F32), axis=0, keepdims=True),
                    jnp.sum(gv_ref[0].astype(F32), axis=0, keepdims=True),
                    jnp.zeros((6, cw), F32),
                ],
                axis=0,
            )

        @pl.when(meta_ref[1] == 1)
        def _():
            @pl.when(i == 0)
            def _():
                fill_distance(dist_ref, meta_ref[2])
                acc_ref[...] = gaf_ref[...]

            @pl.when(i < count)
            def _():
                work(o_own_ref, w_own_ref)

            @pl.when(i >= count)
            def _():
                work(o_oth_ref, w_oth_ref)

            @pl.when(i == steps - 1)
            def _():
                gx_ref[...] = acc_ref[...]
                gxl_ref[...] = acc_ref[...].astype(BF)

    tile = pl.BlockSpec((1, rows, cw), tile_map(lambda s, i: (s, 0, i)))
    return call(
        kernel,
        (steps,),
        [
            (ga, pl.BlockSpec((1, rows, width), lambda i, meta: (meta[0], 0, 0), pipeline_mode=pl.Buffered(1))),
            (gaf, fixed((rows, width))),
            (q, tile),
            (k, tile),
            (v, tile),
            (lse, pl.BlockSpec((1, 1, 8, rows), tile_map(lambda s, i: (s, i, 0, 0)))),
            (o_own, pl.BlockSpec((cw, width), own_map(count, lambda i: (i, 0)))),
            (o_oth, pl.BlockSpec((cw, width), oth_map(count, lambda i: (i, 0)))),
            (w_own, pl.BlockSpec((3, width, cw), own_map(count, lambda i: (0, 0, i)))),
            (w_oth, pl.BlockSpec((3, width, cw), oth_map(count, lambda i: (0, 0, i)))),
            (slopes, pl.BlockSpec(memory_space=pltpu.SMEM)),
        ],
        [((slots, rows, total), BF, tile, True)] * 3
        + [
            ((rows, width), F32, pl.BlockSpec((rows, width), lambda i, meta: (0, 0)), False),
            ((rows, width), BF, pl.BlockSpec((rows, width), lambda i, meta: (0, 0)), False),
            ((8, total), F32, pl.BlockSpec((8, cw), lambda i, meta: (0, i)), False),
        ],
        [pltpu.VMEM((rows, rows), F32), pltpu.VMEM((rows, cw), BF), pltpu.VMEM((rows, width), F32)],
        meta,
        chain,
        deps,
        "attention_backward",
        2 * rows * width * 4 * total + 10 * rows * rows * total,
        20 << 20,
    )


MESH = pl.DeviceIdType.MESH
CORE_LAG = 3
CROSS_LAG = 3
CHAIN_LAG = 2


def arrived(ref, sem):
    pltpu.make_async_copy(ref, ref, sem).wait()


def neighbours():
    t = lax.axis_index("tensor")
    d = lax.axis_index("dp")
    last = lax.axis_size("dp") // 2 - 1
    c = lax.rem(d, 2)
    z = d // 2
    return t, c, z, last, {"dp": d + 1 - 2 * c}, {"tensor": 1 - t}, {"dp": d + 2}, {"dp": d - 2}


def greet(c, z, chips, core, cross):
    barrier = pltpu.get_barrier_semaphore()
    pl.semaphore_signal(barrier, inc=1, device_id=core, device_id_type=MESH)
    pl.semaphore_signal(barrier, inc=1, device_id=cross, device_id_type=MESH)
    for shift in range(1, chips):
        chip = lax.rem(z + shift, chips)
        pl.semaphore_signal(barrier, inc=1, device_id={"dp": chip * 2 + c}, device_id_type=MESH)
    pl.semaphore_wait(barrier, 1 + chips)


def fetch_other_half(qkv, out, up, down, held, chips):
    weights = [qkv, out, up, down]
    seqs = held.shape[0] // 2
    shard_rows = held.shape[1]
    groups = 2 * chips

    def rows_of(item):
        return weights[item].shape[0]

    plan = []
    up_piece = rows_of(2) // groups
    parts = 4
    for part in range(parts):
        plan.append((2, True, 0, up_piece, part * up_piece // parts, up_piece // parts))
    spread = rows_of(3) // 2
    plan.append((3, True, 0, spread // groups, 0, spread // groups))
    n_spread = len(plan)
    plan.append((-1, False, 0, 0, 0, 0))
    for part in range(3):
        size = rows_of(0) // 6
        plan.append((0, False, 0, rows_of(0) // 2, part * size, size))
    plan.append((1, False, 0, rows_of(1) // 2, 0, rows_of(1) // 2))
    plan.append((-1, False, 0, 0, 0, 1))
    direct = (rows_of(3) - spread) // 2
    for part in range(2):
        plan.append((3, False, spread, direct, part * direct // 2, direct // 2))
    n = len(plan)

    def kernel(*refs):
        ins, held_ref = refs[:4], refs[4]
        outs, rows_ref = refs[5:9], refs[9]
        stage, x_send, x_recv, c_send, c_recv, u_send, u_recv, d_send, d_recv, l_sem = refs[10:]
        t, c, z, last, core, cross, above, below = neighbours()
        greet(c, z, chips, core, cross)

        def rows(index, chip, on):
            item, is_spread, base, piece, offset, size = plan[index]
            place = chip * 2 + on if is_spread else on
            return item, pl.ds(pl.multiple_of(base + place * piece + offset, size), size)

        def cross_copy(index):
            if plan[index][0] < 0:
                m = plan[index][5]
                src = held_ref.at[(1 - t) * seqs + m]
                dst = rows_ref.at[m, pl.ds(pl.multiple_of(t * shard_rows, shard_rows), shard_rows)]
            else:
                item, where = rows(index, z, c)
                src, dst = ins[item].at[where], outs[item].at[where]
            return pltpu.make_async_remote_copy(
                src_ref=src, dst_ref=dst, send_sem=x_send.at[index], recv_sem=x_recv.at[index],
                device_id=cross, device_id_type=MESH,
            )

        def pass_on(index, chip, send, recv, device):
            item, where = rows(index, chip, c)
            place = outs[item].at[where]
            return pltpu.make_async_remote_copy(
                src_ref=place, dst_ref=place, send_sem=send.at[index, chip], recv_sem=recv.at[index, chip],
                device_id=device, device_id_type=MESH,
            )

        def got(index, chip, on, sem):
            item, where = rows(index, chip, on)
            arrived(outs[item].at[where], sem)

        for index in range(n):
            cross_copy(index).start()
        mine = pltpu.make_async_copy(held_ref.at[pl.ds(t * seqs, seqs)], stage, l_sem)
        mine.start()
        mine.wait()
        for m in range(seqs):
            pltpu.make_async_copy(
                stage.at[m], rows_ref.at[m, pl.ds(pl.multiple_of(t * shard_rows, shard_rows), shard_rows)], l_sem
            ).start()

        def handle(index, hop):
            if hop == 0:
                if plan[index][0] < 0:
                    m = plan[index][5]
                    arrived(
                        rows_ref.at[m, pl.ds(pl.multiple_of((1 - t) * shard_rows, shard_rows), shard_rows)],
                        x_recv.at[index],
                    )
                    return
                got(index, z, c, x_recv.at[index])
                pass_on(index, z, c_send, c_recv, core).start()
                if plan[index][1]:
                    @pl.when(z < last)
                    def _():
                        pass_on(index, z, u_send, u_recv, above).start()

                    @pl.when(z > 0)
                    def _():
                        pass_on(index, z, d_send, d_recv, below).start()
                return

            @pl.when(z - hop >= 0)
            def _():
                got(index, z - hop, c, u_recv.at[index, z - hop])

                @pl.when(z < last)
                def _():
                    pass_on(index, z - hop, u_send, u_recv, above).start()

                pass_on(index, z - hop, c_send, c_recv, core).start()

            @pl.when(z + hop <= last)
            def _():
                got(index, z + hop, c, d_recv.at[index, z + hop])

                @pl.when(z > 0)
                def _():
                    pass_on(index, z + hop, d_send, d_recv, below).start()

                pass_on(index, z + hop, c_send, c_recv, core).start()

        for round_ in range(max(n, n_spread + chips - 1)):
            if round_ < n:
                handle(round_, 0)
            for hop in range(1, chips):
                if 0 <= round_ - hop < n_spread:
                    handle(round_ - hop, hop)

        for m in range(seqs):
            arrived(stage.at[m], l_sem)
        for index in range(n):
            item, is_spread = plan[index][:2]
            cross_copy(index).wait_send()
            if item < 0:
                continue
            if not is_spread:
                got(index, z, 1 - c, c_recv.at[index, z])
                pass_on(index, z, c_send, c_recv, core).wait_send()
                continue
            for chip in range(chips):
                got(index, chip, 1 - c, c_recv.at[index, chip])
                pass_on(index, chip, c_send, c_recv, core).wait_send()

                @pl.when((chip <= z) & (z < last))
                def _(chip=chip):
                    pass_on(index, chip, u_send, u_recv, above).wait_send()

                @pl.when((chip >= z) & (z > 0))
                def _(chip=chip):
                    pass_on(index, chip, d_send, d_recv, below).wait_send()

    sem = pltpu.SemaphoreType.DMA
    moved = sum(w.size for w in weights) * 2
    return pl.pallas_call(
        kernel,
        in_specs=[ANY] * 5,
        out_specs=[ANY] * 5,
        out_shape=[jax.ShapeDtypeStruct(w.shape, BF) for w in weights]
        + [jax.ShapeDtypeStruct((seqs, 2 * shard_rows, held.shape[2]), BF)],
        scratch_shapes=[pltpu.VMEM((seqs,) + held.shape[1:], BF)]
        + [sem((n,)), sem((n,))]
        + [sem((n, chips))] * 6
        + [sem],
        compiler_params=pltpu.CompilerParams(collective_id=1, has_side_effects=True),
        cost_estimate=pl.CostEstimate(flops=0, bytes_accessed=2 * moved, transcendentals=0),
        name="fetch_other_half",
    )(*weights, held)


def weight_grads_reduced(groups, sums, chips):
    seqs = 2
    rows, depth = groups[0][0].shape[1:]
    lefts = [g[0] for g in groups]
    rights = [r for g in groups for r in g[1]]
    bt = 128
    half = depth // 2
    quarter = half // 2
    blocks = [r.shape[2] // (2 * bt) for r in rights]
    starts = [sum(blocks[:index]) for index in range(len(rights))]
    total = sum(blocks)
    group_starts = []
    index = 0
    for _, members in groups:
        group_starts.append(starts[index])
        index += len(members)
    n_left, n_right = len(lefts), len(rights)
    tiles, mines, gives = 4, CORE_LAG + 1, 4
    last_static = chips - 1
    drain = CORE_LAG + CROSS_LAG + 2 * last_static * CHAIN_LAG + 1
    vec_shape = sums.shape

    def kernel(*refs):
        left_refs = refs[:n_left]
        right_refs = refs[n_left : n_left + n_right]
        sums_ref = refs[n_left + n_right]
        outs = refs[n_left + n_right + 1 : n_left + 2 * n_right + 1]
        sums_out = refs[n_left + 2 * n_right + 1]
        (
            acc, from_x, from_z, final, flip, stage, tile, mine, give, vec, vec_in, vec_all,
            tile_sem, stage_sem, give_send, core_recv, x_send, x_recv, z_send, z_recv, f_send, f_recv,
            store_sem, out_send, out_recv, v_load, v_send, v_recv,
        ) = refs[n_left + 2 * n_right + 2 :]
        t, c, z, last, core, cross, above, below = neighbours()
        greet(c, z, chips, core, cross)

        def remote(src, dst, send, recv, device):
            return pltpu.make_async_remote_copy(
                src_ref=src, dst_ref=dst, send_sem=send, recv_sem=recv, device_id=device, device_id_type=MESH
            )

        def valid(k):
            return (k >= 0) & (k < total)

        def member(k, visit):
            for m in range(n_right):
                @pl.when((k >= starts[m]) & (k < starts[m] + blocks[m]))
                def _(m=m):
                    visit(m, k - starts[m])

        def load_tile(k):
            slot = lax.rem(k, tiles)

            def visit(m, j):
                for side in range(2):
                    at = pl.multiple_of((side * blocks[m] + j) * bt, bt)
                    pltpu.make_async_copy(
                        right_refs[m].at[pl.ds(0, seqs), :, pl.ds(at, bt)],
                        tile.at[slot, :, :, pl.ds(side * bt, bt)],
                        tile_sem.at[slot],
                    ).start()

            member(k, visit)

        def load_left(g):
            return pltpu.make_async_copy(left_refs[g].at[pl.ds(0, seqs)], stage, stage_sem)

        vec_load = pltpu.make_async_copy(sums_ref, vec.at[0], v_load)
        vec_load.start()
        load_left(0).start()
        for k in range(tiles - 1):
            load_tile(jnp.int32(k))
        vec_load.wait()
        vec_core = remote(vec.at[0], vec_in.at[0], v_send.at[0], v_recv.at[0], core)
        vec_cross = remote(vec.at[1], vec_in.at[1], v_send.at[1], v_recv.at[1], cross)
        vec_core.start()

        up = pl.ds(0, quarter)
        down = pl.ds(quarter, quarter)
        sides = ((up, 0, z, above, below), (down, 1, last - z, below, above))

        @pl.loop(0, total + drain)
        def _(s):
            @pl.when(valid(s))
            def _():
                for g in range(n_left):
                    @pl.when(s == group_starts[g])
                    def _(g=g):
                        load_left(g).wait()
                        for m in range(seqs):
                            flip[:, m * rows : (m + 1) * rows] = stage[m].T
                        if g + 1 < n_left:
                            load_left(g + 1).start()

                slot = lax.rem(s, tiles)
                arrived(tile.at[slot], tile_sem.at[slot])
                give_slot = lax.rem(s, gives)

                @pl.when(s >= gives)
                def _():
                    arrived(give.at[give_slot], give_send.at[give_slot])

                for place, ring, at in ((1 - c, give, give_slot), (c, mine, lax.rem(s, mines))):
                    here = pl.ds(pl.multiple_of(place * half, half), half)
                    block = dot(flip[here, :rows], tile[slot, 0])
                    for m in range(1, seqs):
                        block += dot(flip[here, m * rows : (m + 1) * rows], tile[slot, m])
                    ring[at, 1] = block[:, :bt].astype(BF)
                    ring[at, 0] = block[:, bt:].astype(BF)

            @pl.when(s + tiles - 1 < total)
            def _():
                load_tile(s + tiles - 1)

            k1 = s - CORE_LAG

            @pl.when(valid(k1))
            def _():
                arrived(acc.at[k1], core_recv.at[k1])
                at = lax.rem(k1, mines)
                for side in range(2):
                    acc[k1, side] = (acc[k1, side].astype(F32) + mine[at, side].astype(F32)).astype(BF)

            k2 = k1 - CROSS_LAG

            @pl.when(valid(k2))
            def _():
                arrived(from_x.at[k2], x_recv.at[k2])
                acc[k2, 1] = (acc[k2, 1].astype(F32) + from_x[k2].astype(F32)).astype(BF)

            for span, way, place, ahead, behind in sides:
                k3 = k2 - CHAIN_LAG * place

                @pl.when(valid(k3) & (place > 0))
                def _(span=span, way=way, k3=k3):
                    arrived(from_z.at[k3, span], z_recv.at[way, k3])
                    acc[k3, 1, span] = (acc[k3, 1, span].astype(F32) + from_z[k3, span].astype(F32)).astype(BF)

                k4 = k2 - CHAIN_LAG * (2 * last - place)

                @pl.when(valid(k4) & (place == last))
                def _(span=span, k4=k4):
                    final[k4, span] = acc[k4, 1, span]

                @pl.when(valid(k4) & (place < last))
                def _(span=span, way=way, k4=k4):
                    arrived(final.at[k4, span], f_recv.at[way, k4])

            @pl.when(valid(s))
            def _():
                at = lax.rem(s, gives)
                remote(give.at[at], acc.at[s], give_send.at[at], core_recv.at[s], core).start()

            @pl.when(valid(k1))
            def _():
                remote(acc.at[k1, 0], from_x.at[k1], x_send, x_recv.at[k1], cross).start()

            for span, way, place, ahead, behind in sides:
                k3 = k2 - CHAIN_LAG * place

                @pl.when(valid(k3) & (place < last))
                def _(span=span, way=way, k3=k3, ahead=ahead):
                    remote(acc.at[k3, 1, span], from_z.at[k3, span], z_send.at[way], z_recv.at[way, k3], ahead).start()

                k4 = k2 - CHAIN_LAG * (2 * last - place)

                @pl.when(valid(k4) & (place > 0))
                def _(span=span, way=way, k4=k4, behind=behind):
                    remote(final.at[k4, span], final.at[k4, span], f_send.at[way], f_recv.at[way, k4], behind).start()

            k5 = k2 - CHAIN_LAG * 2 * last

            @pl.when(valid(k5))
            def _():
                def visit(m, j):
                    dst = outs[m].at[
                        pl.ds(pl.multiple_of(c * half, half), half), pl.ds(pl.multiple_of(j * bt, bt), bt)
                    ]
                    pltpu.make_async_copy(final.at[k5], dst, store_sem).start()
                    remote(final.at[k5], dst, out_send, out_recv, core).start()

                member(k5, visit)

            @pl.when(s == 4)
            def _():
                vec_core.wait_recv()
                vec[1] = vec[0] + vec_in[0]

            @pl.when(s == 5)
            def _():
                vec_cross.start()

            @pl.when(s == 10)
            def _():
                vec_cross.wait_recv()
                vec_all[z] = vec[1] + vec_in[1]

            @pl.when(s == 11)
            def _():
                for shift in range(1, chips):
                    to = lax.rem(z + shift, chips)
                    remote(
                        vec_all.at[z], vec_all.at[z], v_send.at[1 + shift], v_recv.at[1 + shift], {"dp": to * 2 + c}
                    ).start()

        vec_core.wait_send()
        vec_cross.wait_send()
        for shift in range(1, chips):
            origin = lax.rem(z + chips - shift, chips)
            arrived(vec_all.at[origin], v_recv.at[1 + shift])
            arrived(vec_all.at[z], v_send.at[1 + shift])
        whole = vec_all[0]
        for chip in range(1, chips):
            whole += vec_all[chip]
        sums_out[...] = whole
        for at in range(gives):
            arrived(give.at[at], give_send.at[at])
        arrived(acc.at[:, 0], x_send)
        for span, way, place, ahead, behind in sides:
            @pl.when(place < last)
            def _(span=span, way=way):
                arrived(from_z.at[:, span], z_send.at[way])

            @pl.when(place > 0)
            def _(span=span, way=way):
                arrived(final.at[:, span], f_send.at[way])

        arrived(final, out_send)
        arrived(final, store_sem)
        arrived(final, out_recv)

    sem = pltpu.SemaphoreType.DMA
    flops = 2 * seqs * rows * depth * 2 * bt * total
    return pl.pallas_call(
        kernel,
        in_specs=[ANY] * (n_left + n_right + 1),
        out_specs=[ANY] * n_right + [pl.BlockSpec(memory_space=pltpu.VMEM)],
        out_shape=[jax.ShapeDtypeStruct((depth, r.shape[2] // 2), BF) for r in rights]
        + [jax.ShapeDtypeStruct(vec_shape, F32)],
        scratch_shapes=[
            pltpu.VMEM((total, 2, half, bt), BF),
            pltpu.VMEM((total, half, bt), BF),
            pltpu.VMEM((total, half, bt), BF),
            pltpu.VMEM((total, half, bt), BF),
            pltpu.VMEM((depth, seqs * rows), BF),
            pltpu.VMEM((seqs, rows, depth), BF),
            pltpu.VMEM((tiles, seqs, rows, 2 * bt), BF),
            pltpu.VMEM((mines, 2, half, bt), BF),
            pltpu.VMEM((gives, 2, half, bt), BF),
            pltpu.VMEM((2,) + vec_shape, F32),
            pltpu.VMEM((2,) + vec_shape, F32),
            pltpu.VMEM((chips,) + vec_shape, F32),
            sem((tiles,)), sem, sem((gives,)), sem((total,)), sem, sem((total,)),
            sem((2,)), sem((2, total)), sem((2,)), sem((2, total)),
            sem, sem, sem, sem, sem((chips + 1,)), sem((chips + 1,)),
        ],
        compiler_params=pltpu.CompilerParams(
            collective_id=0, has_side_effects=True, vmem_limit_bytes=VMEM_LIMIT
        ),
        cost_estimate=pl.CostEstimate(flops=flops, bytes_accessed=64 << 20, transcendentals=0),
        name="weight_grads_reduced",
    )(*lefts, *rights, sums)


MASKED = -1000000000.0


def shifted(value, axis, steps):
    count = lax.axis_size(axis)
    first, last = (max(0, -steps), min(count, count - steps))
    return lax.ppermute(value, axis, [(source, source + steps) for source in range(first, last)])


def layer_norm(values, gain, shift):
    mean = jnp.mean(values, axis=-1, keepdims=True)
    centred = values - mean
    spread = jnp.mean(centred * centred, axis=-1, keepdims=True)
    return centred * lax.rsqrt(spread + EPS) * gain + shift


def alibi_slopes(first, count, heads):
    index = (first + jnp.arange(count)).astype(jnp.float32)
    return jnp.exp2(-8.0 * (index + 1.0) / heads)


def attention_core(projected, qv_bias, slopes, key_ok):
    rows = projected.shape[0]
    width = projected.shape[2]
    count = slopes.shape[0]
    size = width // count
    query = (projected[:, 0] + qv_bias[0]).astype(jnp.bfloat16).reshape(rows, count, size)
    key = projected[:, 1].astype(jnp.bfloat16).reshape(rows, count, size)
    value = (projected[:, 2] + qv_bias[1]).astype(jnp.bfloat16).reshape(rows, count, size)
    place = jnp.arange(rows).astype(jnp.float32)
    distance = jnp.abs(place[:, None] - place[None, :])
    scale = 1.0 / math.sqrt(size)
    scores = (
        jnp.einsum("qhd,khd->hqk", query, key, preferred_element_type=jnp.float32) * scale
        - slopes[:, None, None] * distance[None]
    )
    scores = jnp.where(key_ok[None, None, :], scores, MASKED)
    weights = jax.nn.softmax(scores, axis=-1)
    weights_low = weights.astype(jnp.bfloat16)
    mixed = jnp.einsum("hqk,khd->qhd", weights_low, value, preferred_element_type=jnp.float32)
    mixed = mixed.reshape(rows, width).astype(jnp.bfloat16)
    return (query, key, value, weights, weights_low, mixed)


def attention_back(parts, grad_mixed, key_ok):
    query, key, value, weights, weights_low, mixed = parts
    rows, count, size = query.shape
    scale = 1.0 / math.sqrt(size)
    grad_low = grad_mixed.astype(jnp.bfloat16).reshape(rows, count, size)
    grad_weights = jnp.einsum("qhd,khd->hqk", grad_low, value, preferred_element_type=jnp.float32)
    grad_value = jnp.einsum(
        "hqk,qhd->khd", weights_low, grad_low, preferred_element_type=jnp.float32
    )
    inner = jnp.sum(weights * grad_weights, axis=-1, keepdims=True)
    grad_scores = weights * (grad_weights - inner)
    grad_scores = jnp.where(key_ok[None, None, :], grad_scores, 0.0).astype(jnp.bfloat16)
    grad_query = (
        jnp.einsum("hqk,khd->qhd", grad_scores, key, preferred_element_type=jnp.float32) * scale
    ).astype(jnp.bfloat16)
    grad_key = (
        jnp.einsum("hqk,qhd->khd", grad_scores, query, preferred_element_type=jnp.float32) * scale
    ).astype(jnp.bfloat16)
    grad_value = grad_value.astype(jnp.bfloat16)
    width = count * size
    grad_query = grad_query.reshape(rows, width)
    grad_key = grad_key.reshape(rows, width)
    grad_value = grad_value.reshape(rows, width)
    grad_projected = jnp.stack([grad_query, grad_key, grad_value], axis=1).reshape(rows, 3 * width)
    qv_grad = jnp.stack(
        [
            jnp.sum(grad_query.astype(jnp.float32), axis=0),
            jnp.sum(grad_value.astype(jnp.float32), axis=0),
        ]
    )
    return (grad_projected, qv_grad)


def gelu_product(both):
    return jax.nn.gelu(both[:, 0], approximate=False) * both[:, 1]


def geglu(lifted, up_bias):
    return gelu_product(lifted + up_bias[None])


def ffn_grads(rows_low, grad_low, up_weight, up_bias, down_weight):
    lifted = jnp.einsum("sd,gdf->sgf", rows_low, up_weight, preferred_element_type=jnp.float32)
    hidden, geglu_back = jax.vjp(gelu_product, lifted + up_bias[None])
    grad_hidden = jnp.einsum("sd,df->sf", grad_low, down_weight, preferred_element_type=jnp.float32)
    (grad_both,) = geglu_back(grad_hidden)
    grad_lifted = grad_both.astype(jnp.bfloat16)
    grad_bias = jnp.sum(grad_lifted.astype(jnp.float32), axis=0)
    up_grad = jnp.einsum("sd,sgf->gdf", rows_low, grad_lifted, preferred_element_type=jnp.float32)
    down_grad = jnp.einsum(
        "sd,sf->df", grad_low, hidden.astype(jnp.bfloat16), preferred_element_type=jnp.float32
    )
    return (grad_lifted, grad_bias, up_grad, down_grad)


def on_device(
    inputs,
    cotangent,
    lengths,
    w_qkv,
    b_qv,
    w_out,
    b_out,
    ln_gain,
    ln_bias,
    w_up,
    b_up,
    w_down,
    b_down,
):
    batches, shard_rows, width = inputs.shape
    parts = lax.axis_size("tensor")
    place = lax.axis_index("tensor")
    section = lax.axis_index("section")
    last_section = lax.axis_size("section") - 1
    full_rows = shard_rows * parts
    local_width = w_qkv.shape[3]
    local_heads = local_width // HD
    qkv_flat = w_qkv[0].reshape(width, 3 * local_width)
    out_weight = w_out[0]
    qv_bias = b_qv[0].astype(jnp.float32)
    out_bias = b_out[0].astype(jnp.float32)
    gains = ln_gain[0].astype(jnp.float32)
    shifts = ln_bias[0].astype(jnp.float32)
    down_bias = b_down[0].astype(jnp.float32)
    slopes = alibi_slopes(place * local_heads, local_heads, H)
    row_place = place * shard_rows + jnp.arange(shard_rows)
    kept_rows = 0

    def key_mask(length):
        return jnp.arange(full_rows) < length

    def after_attention(values, attended, bias, gain_rows, shift_rows):
        return layer_norm(values + attended + bias, gain_rows[0], shift_rows[0])

    def after_ffn(normed, lowered, bias, gain_rows, shift_rows):
        return layer_norm(normed + lowered + bias, gain_rows[1], shift_rows[1])

    def gather_inputs(values):
        return lax.all_gather(values.astype(jnp.bfloat16), "tensor", axis=0, tiled=True)

    def project(gathered):
        return jnp.dot(gathered, qkv_flat, preferred_element_type=jnp.float32).reshape(
            full_rows, 3, local_width
        )

    def attention_forward(values, length):
        gathered = gather_inputs(values)
        projected = project(gathered)
        mixed = attention_core(projected, qv_bias, slopes, key_mask(length))[5]

        def term(start, count):
            return jnp.dot(mixed, out_weight, preferred_element_type=jnp.float32)

        return (
            lax.psum_scatter(
                term(jnp.int32(0), shard_rows * lax.axis_size("tensor")).astype(jnp.bfloat16),
                "tensor",
                scatter_dimension=0,
                tiled=True,
            ).astype(jnp.float32),
            gathered,
            projected,
        )

    up_local = w_up[0]
    up_bias_local = b_up[0].astype(jnp.float32)
    down_local = w_down[0]

    def gather_normed(normed):
        return lax.all_gather(normed.astype(jnp.bfloat16), "tensor", axis=0, tiled=True)

    def ffn_forward(normed):
        lifted = jnp.einsum(
            "sd,gdf->sgf", gather_normed(normed), up_local, preferred_element_type=jnp.float32
        )
        hidden = geglu(lifted, up_bias_local).astype(jnp.bfloat16)

        def term(start, count):
            return jnp.einsum("sf,df->sd", hidden, down_local, preferred_element_type=jnp.float32)

        return lax.psum_scatter(
            term(jnp.int32(0), shard_rows * lax.axis_size("tensor")).astype(jnp.bfloat16),
            "tensor",
            scatter_dimension=0,
            tiled=True,
        ).astype(jnp.float32)

    def ffn_backward(normed, grad_lowered):
        gathered = gather_normed(normed)
        grad_whole = lax.all_gather(grad_lowered.astype(jnp.bfloat16), "tensor", axis=0, tiled=True)
        grad_lifted, grad_bias, up_grad, down_grad = ffn_grads(
            gathered, grad_whole, up_local, up_bias_local, down_local
        )

        def term(start, count):
            return jnp.einsum(
                "sgf,gdf->sd", grad_lifted, up_local, preferred_element_type=jnp.float32
            )

        grad_normed = lax.psum_scatter(
            term(jnp.int32(0), shard_rows * lax.axis_size("tensor")).astype(jnp.bfloat16),
            "tensor",
            scatter_dimension=0,
            tiled=True,
        ).astype(jnp.float32)
        return (grad_normed, (up_grad, grad_bias, down_grad))

    ffn_shapes = (up_local.shape, up_bias_local.shape, down_local.shape)

    def layer_forward(values, length):
        attended, gathered, projected = attention_forward(values, length)
        normed = after_attention(values, attended, out_bias, gains, shifts)
        lowered = ffn_forward(normed)
        return (
            after_ffn(normed, lowered, down_bias, gains, shifts),
            attended,
            lowered,
            gathered,
            projected,
        )

    def layer_backward(values, attended, lowered, length, grad_output):
        normed, attention_norm_back = jax.vjp(
            after_attention, values, attended, out_bias, gains, shifts
        )
        outcome, ffn_norm_back = jax.vjp(after_ffn, normed, lowered, down_bias, gains, shifts)
        grad_normed, grad_lowered, grad_down_bias, gain_late, shift_late = ffn_norm_back(
            grad_output
        )
        grad_from_ffn, ffn_terms = ffn_backward(normed, grad_lowered)
        grad_values, grad_attended, grad_out_bias, gain_early, shift_early = attention_norm_back(
            grad_normed + grad_from_ffn
        )
        gathered = gather_inputs(values)
        projected = project(gathered)
        grad_whole = lax.all_gather(
            grad_attended.astype(jnp.bfloat16), "tensor", axis=0, tiled=True
        )
        mask = key_mask(length)
        pieces = attention_core(projected, qv_bias, slopes, mask)
        mixed_low = pieces[5]
        out_grad = jnp.einsum(
            "se,sd->ed", mixed_low, grad_whole, preferred_element_type=jnp.float32
        )
        grad_mixed = jnp.einsum(
            "sd,ed->se", grad_whole, out_weight, preferred_element_type=jnp.float32
        )
        grad_projected, qv_grad = attention_back(pieces, grad_mixed, mask)
        qkv_grad = jnp.einsum(
            "sd,sx->dx", gathered, grad_projected, preferred_element_type=jnp.float32
        )

        def term(start, count):
            return jnp.einsum(
                "sx,dx->sd", grad_projected, qkv_flat, preferred_element_type=jnp.float32
            )

        grad_inputs = grad_values + lax.psum_scatter(
            term(jnp.int32(0), shard_rows * lax.axis_size("tensor")).astype(jnp.bfloat16),
            "tensor",
            scatter_dimension=0,
            tiled=True,
        ).astype(jnp.float32)
        terms = (
            qkv_grad,
            qv_grad,
            out_grad,
            grad_out_bias,
            gain_early + gain_late,
            shift_early + shift_late,
            ffn_terms[0],
            ffn_terms[1],
            ffn_terms[2],
            grad_down_bias,
        )
        return (grad_inputs, terms)

    def keep(store, item, batch, valid):
        old = lax.dynamic_index_in_dim(store, batch, 0, keepdims=False)
        return lax.dynamic_update_index_in_dim(store, jnp.where(valid, item, old), batch, 0)

    def forward_step(step, carry):
        (
            received,
            kept_values,
            kept_attended,
            kept_lowered,
            produced,
            kept_gathered,
            kept_projected,
        ) = carry
        index = step - section
        valid = (index >= 0) & (index < batches)
        batch = jnp.clip(index, 0, batches - 1)
        fresh = lax.dynamic_index_in_dim(
            inputs, jnp.minimum(step, batches - 1), 0, keepdims=False
        ).astype(jnp.float32)
        values = jnp.where(section == 0, fresh, received.astype(jnp.float32))
        output, attended, lowered, gathered, projected = layer_forward(values, lengths[batch])
        sent = output.astype(jnp.bfloat16)
        kept_values = keep(kept_values, values, batch, valid)
        kept_attended = keep(kept_attended, attended, batch, valid)
        kept_lowered = keep(kept_lowered, lowered, batch, valid)
        produced = keep(produced, sent, batch, valid)
        kept_gathered = keep(kept_gathered, gathered[:kept_rows], batch, valid)
        kept_projected = keep(kept_projected, projected[:kept_rows], batch, valid)
        received = shifted(sent, "section", 1)
        return (
            received,
            kept_values,
            kept_attended,
            kept_lowered,
            produced,
            kept_gathered,
            kept_projected,
        )

    store_zeros = jnp.zeros((batches, shard_rows, width), jnp.float32)
    gathered_zeros = jnp.zeros((batches, kept_rows, width), jnp.bfloat16)
    projected_zeros = jnp.zeros((batches, kept_rows, 3, local_width), jnp.float32)
    start_forward = (
        jnp.zeros((shard_rows, width), jnp.bfloat16),
        store_zeros,
        store_zeros,
        store_zeros,
        jnp.zeros((batches, shard_rows, width), jnp.bfloat16),
        gathered_zeros,
        projected_zeros,
    )
    received, kept_values, kept_attended, kept_lowered, produced, kept_gathered, kept_projected = (
        lax.fori_loop(0, batches + last_section, forward_step, start_forward)
    )

    def backward_step(step, carry):
        received, totals, grads_in = carry
        index = step - (last_section - section)
        valid = (index >= 0) & (index < batches)
        batch = jnp.clip(index, 0, batches - 1)
        length = lengths[batch]
        outer = lax.dynamic_index_in_dim(cotangent, batch, 0, keepdims=False).astype(jnp.float32)
        outer = outer * (row_place < length).astype(jnp.float32)[:, None]
        grad_output = jnp.where(section == last_section, outer, received.astype(jnp.float32))
        grad_output = jnp.where(valid, grad_output, 0.0)
        values = lax.dynamic_index_in_dim(kept_values, batch, 0, keepdims=False)
        attended = lax.dynamic_index_in_dim(kept_attended, batch, 0, keepdims=False)
        lowered = lax.dynamic_index_in_dim(kept_lowered, batch, 0, keepdims=False)
        grad_inputs, terms = layer_backward(values, attended, lowered, length, grad_output)
        totals = jax.tree.map(jnp.add, totals, terms)
        grads_in = keep(grads_in, grad_inputs, batch, valid)
        received = shifted(grad_inputs.astype(jnp.bfloat16), "section", -1)
        return (received, totals, grads_in)

    start_totals = (
        jnp.zeros((width, 3 * local_width), jnp.float32),
        jnp.zeros((2, local_width), jnp.float32),
        jnp.zeros((local_width, width), jnp.float32),
        jnp.zeros((width,), jnp.float32),
        jnp.zeros((2, width), jnp.float32),
        jnp.zeros((2, width), jnp.float32),
        jnp.zeros(ffn_shapes[0], jnp.float32),
        jnp.zeros(ffn_shapes[1], jnp.float32),
        jnp.zeros(ffn_shapes[2], jnp.float32),
        jnp.zeros((width,), jnp.float32),
    )
    start_backward = (jnp.zeros((shard_rows, width), jnp.bfloat16), start_totals, store_zeros)
    received, totals, grads_in = lax.fori_loop(
        0, batches + last_section, backward_step, start_backward
    )
    (
        qkv_total,
        qv_total,
        out_total,
        out_bias_total,
        gain_total,
        shift_total,
        up_total,
        up_bias_total,
        down_total,
        down_bias_total,
    ) = totals
    qkv_sum, qv_sum, out_sum, up_sum, up_bias_sum, down_sum = (
        lax.psum(qkv_total.astype(jnp.bfloat16), "dp").astype(jnp.float32),
        lax.psum(qv_total.astype(jnp.bfloat16), "dp").astype(jnp.float32),
        lax.psum(out_total.astype(jnp.bfloat16), "dp").astype(jnp.float32),
        lax.psum(up_total.astype(jnp.bfloat16), "dp").astype(jnp.float32),
        lax.psum(up_bias_total.astype(jnp.bfloat16), "dp").astype(jnp.float32),
        lax.psum(down_total.astype(jnp.bfloat16), "dp").astype(jnp.float32),
    )
    out_bias_sum, gain_sum, shift_sum, down_bias_sum = lax.psum(
        (out_bias_total, gain_total, shift_total, down_bias_total), ("tensor", "dp")
    )
    return (
        produced[None],
        grads_in[None],
        qkv_sum.reshape(1, width, 3, local_width),
        qv_sum[None],
        out_sum[None],
        out_bias_sum[None],
        gain_sum[None],
        shift_sum[None],
        up_sum[None],
        up_bias_sum[None],
        down_sum[None],
        down_bias_sum[None],
    )


def join(first, second, swapped):
    return jnp.where(
        swapped, jnp.concatenate([second, first], axis=0), jnp.concatenate([first, second], axis=0)
    )


def by_sequence(
    inputs,
    cotangent,
    lengths,
    w_qkv,
    b_qv,
    w_out,
    b_out,
    ln_gain,
    ln_bias,
    w_up,
    b_up,
    w_down,
    b_down,
):
    batches, shard_rows, width = inputs.shape
    place = lax.axis_index("tensor")
    section = lax.axis_index("section")
    groups = lax.axis_size("dp")
    rows = 2 * shard_rows
    seqs = batches // 2
    slots = seqs + 1
    local = w_qkv.shape[3]
    units = w_up.shape[3]
    heads = local // HD
    chips = groups // 2

    def across(value):
        return lax.ppermute(value, "tensor", [(0, 1), (1, 0)])

    def own_rows(values, low):
        kept = [lax.dynamic_slice_in_dim(v, place * shard_rows, shard_rows, 0) for v in values]
        sent = [lax.dynamic_slice_in_dim(v, (1 - place) * shard_rows, shard_rows, 0) for v in low]
        got = [across(v) for v in sent]
        return join(jnp.stack(kept), jnp.stack(got).astype(values[0].dtype), place == 1)

    qkv_own = jnp.transpose(w_qkv[0], (1, 0, 2))
    out_own = w_out[0]
    up_own = w_up[0]
    down_own = w_down[0]
    small = across(jnp.concatenate([b_qv[0], b_up[0]], axis=1))
    first = section == 0
    qkv_oth, out_oth, up_oth, down_oth, held = fetch_other_half(
        qkv_own.reshape(3 * width, local),
        out_own,
        up_own.reshape(2 * width, units),
        down_own,
        jnp.where(first, inputs, cotangent),
        chips,
    )
    qkv_oth = qkv_oth.reshape(3, width, local)
    up_oth = up_oth.reshape(2, width, units)
    x_first = outer = [held[m] for m in range(seqs)]

    bias = jnp.concatenate([b_qv[0], small[:, :local]], axis=1).astype(F32)
    up_bias = jnp.concatenate([b_up[0], small[:, local:]], axis=1).astype(F32)
    vecs = jnp.stack(
        [b_out[0], ln_gain[0, 0], ln_bias[0, 0], b_down[0], ln_gain[0, 1], ln_bias[0, 1], b_out[0], b_out[0]]
    ).astype(F32)
    slopes = jnp.concatenate(
        [alibi_slopes(place * heads, heads, H), alibi_slopes((1 - place) * heads, heads, H)]
    )
    own_lengths = lax.dynamic_slice_in_dim(lengths, place * seqs, seqs, 0)

    def meta(m, turn):
        active = section == turn
        return jnp.stack([jnp.where(active, m, seqs), active.astype(jnp.int32), own_lengths[m]])

    metas = [[meta(m, turn) for m in range(seqs)] for turn in range(2)]
    att = ffn = None
    deps = []

    def attention(x, m, turn):
        nonlocal att, deps
        att = attention_forward(x, qkv_own, qkv_oth, bias, slopes, metas[turn][m], att, deps, slots)
        deps = [att[4]]

    def feed(x, m, turn):
        nonlocal ffn, deps
        ffn = ffn_forward(
            x, att[3], out_own, out_oth, up_own, up_oth, down_own, down_oth, vecs, up_bias,
            metas[turn][m], ffn, deps, slots,
        )
        *ffn, y = ffn
        deps = [y]
        return y

    for m in range(seqs):
        attention(x_first[m], m, 0)
    y_first = [feed(x_first[m], m, 0) for m in range(seqs)]
    x_second = [lax.ppermute(y, "section", [(0, 1)]) for y in y_first]
    y_second = []
    for m in range(seqs):
        attention(x_second[m], m, 1)
        y_second.append(feed(x_second[m], m, 1))

    bff = bat = None
    sums = [[None] * seqs, [None] * seqs]

    def back(grad, m, turn):
        nonlocal bff, bat, deps
        act, slope, hidden, normed, u1, u2, r1, r2 = ffn
        *bff, gaf, norm_sums, up_sums = ffn_backward(
            grad, u2, r2, u1, r1, act, slope, up_own, up_oth, down_own, down_oth, vecs,
            metas[turn][m], bff, deps, slots,
        )
        deps = [norm_sums]
        *bat, gx, gx_low, qv_sums = attention_backward(
            bff[3], gaf, att[0], att[1], att[2], att[4], out_own, out_oth, qkv_own, qkv_oth, slopes,
            metas[turn][m], bat, deps, slots,
        )
        deps = [qv_sums]
        sums[turn][m] = (norm_sums, up_sums, qv_sums)
        return gx, gx_low

    row = jnp.arange(rows)[:, None]
    gx_second = [
        back(jnp.where(row < own_lengths[m], outer[m], 0), m, 1) for m in range(seqs)
    ]
    grad_middle = [lax.ppermute(gx_second[m][1], "section", [(1, 0)]) for m in range(seqs)]
    gx_first = [back(grad_middle[m], m, 0) for m in range(seqs)]

    hidden, normed = ffn[2], ffn[3]
    mixed = att[3]
    x_all = jnp.stack([jnp.where(first, x_first[m], x_second[m]) for m in range(seqs)])
    gg0, gg1, gl, ga = bff
    produced = own_rows(*[[jnp.where(first, a, b) for a, b in zip(y_first, y_second)]] * 2)
    grads_in = own_rows(
        [jnp.where(first, a[0], b[0]) for a, b in zip(gx_first, gx_second)],
        [jnp.where(first, a[1], b[1]) for a, b in zip(gx_first, gx_second)],
    )

    picked = [
        sum(jnp.where(first, sums[0][m][index], sums[1][m][index]) for m in range(seqs))
        for index in range(3)
    ]
    norm_sums, up_sums, qv_sums = picked

    def ordered(values, count):
        return jnp.where(
            place == 0, values, jnp.concatenate([values[:, count:], values[:, :count]], axis=1)
        ).reshape(-1, width)

    packed = jnp.concatenate([norm_sums[:6], ordered(up_sums[:2], units), ordered(qv_sums[:2], local)])
    down_sum, *up_sum, sum_q, sum_k, sum_v, out_sum, packed = weight_grads_reduced(
        [(gl, [hidden]), (normed, [gg0, gg1]), (x_all, bat), (ga, [mixed])], packed, chips
    )
    up_sum = jnp.stack(up_sum).astype(F32)
    down_sum = down_sum.astype(F32)
    qkv_sum = jnp.stack([sum_q, sum_k, sum_v], axis=1).astype(F32)
    out_sum = out_sum.T.astype(F32)
    norm_total = packed[:6]
    up_total = packed[6 : 6 + 4 * units // width].reshape(2, 2 * units)
    qv_total = packed[6 + 4 * units // width :].reshape(2, 2 * local)
    up_bias_sum = lax.dynamic_slice_in_dim(up_total, place * units, units, 1)
    qv_sum = lax.dynamic_slice_in_dim(qv_total, place * local, local, 1)
    gain_sum = jnp.stack([norm_total[3], norm_total[0]])
    shift_sum = jnp.stack([norm_total[4], norm_total[1]])
    return (
        produced[None],
        grads_in[None],
        qkv_sum[None],
        qv_sum[None],
        out_sum[None],
        norm_total[5][None],
        gain_sum[None],
        shift_sum[None],
        up_sum[None],
        up_bias_sum[None],
        down_sum[None],
        norm_total[2][None],
    )


def solution(mesh):
    sections, parts, groups = (mesh.shape[name] for name in ("section", "tensor", "dp"))

    def run(*args):
        paired = sections == 2 and parts == 2 and groups % 2 == 0 and args[0].shape[0] == 4
        return (by_sequence if paired else on_device)(*args)

    return jax.shard_map(
        run,
        mesh=mesh,
        in_specs=(
            P("dp", "tensor", None),
            P("dp", "tensor", None),
            P("dp"),
            P("section", None, None, "tensor"),
            P("section", None, "tensor"),
            P("section", "tensor", None),
            P("section", None),
            P("section", None, None),
            P("section", None, None),
            P("section", None, None, "tensor"),
            P("section", None, "tensor"),
            P("section", None, "tensor"),
            P("section", None),
        ),
        out_specs=(
            P("section", "dp", "tensor", None),
            P("section", "dp", "tensor", None),
            P("section", None, None, "tensor"),
            P("section", None, "tensor"),
            P("section", "tensor", None),
            P("section", None),
            P("section", None, None),
            P("section", None, None),
            P("section", None, None, "tensor"),
            P("section", None, "tensor"),
            P("section", None, "tensor"),
            P("section", None),
        ),
        check_vma=False,
    )
```

```python
import math

import jax
import jax.numpy as jnp
from jax import lax
from jax.experimental import pallas as pl
from jax.experimental.pallas import tpu as pltpu
from jax.sharding import PartitionSpec as P

H = 16
HD = 64
EPS = 1e-05
BF = jnp.bfloat16
F32 = jnp.float32
VMEM_LIMIT = 62 * 1024 * 1024
ANY = pl.BlockSpec(memory_space=pl.ANY)
SMEM = pl.BlockSpec(memory_space=pltpu.SMEM)
WHOLE = pl.BlockSpec(memory_space=pltpu.VMEM)
NN = (((1,), (0,)), ((), ()))
NT = (((1,), (1,)), ((), ()))
TN = (((0,), (0,)), ((), ()))
CW = 256
PER = CW // HD


def dot(a, b, dims=NN):
    return lax.dot_general(a, b, dims, preferred_element_type=F32)


def arrived(ref, sem):
    pltpu.make_async_copy(ref, ref, sem).wait()


def call(kernel, inputs, outputs, scratch, meta, chain, deps, name, flops, nbytes):
    pairs = [item if isinstance(item, tuple) else (item, ANY) for item in inputs]
    args = [meta] + [p[0] for p in pairs]
    specs = [SMEM] + [p[1] for p in pairs]
    n_in = len(args)
    aliases = {}
    if chain is not None:
        for buffer, index in zip(chain, [index for index, item in enumerate(outputs) if item[2]]):
            aliases[len(args)] = index
            args.append(buffer)
            specs.append(ANY)
    args += deps
    specs += [ANY] * len(deps)
    n_args, n_out = len(args), len(outputs)

    def body(*refs):
        @pl.when(refs[0][1] == 1)
        def _():
            kernel(refs[0], refs[1:n_in], refs[n_args : n_args + n_out], refs[n_args + n_out :])

    return pl.pallas_call(
        body,
        in_specs=specs,
        out_specs=[ANY] * n_out,
        out_shape=[jax.ShapeDtypeStruct(o[0], o[1]) for o in outputs],
        scratch_shapes=scratch,
        input_output_aliases=aliases,
        compiler_params=pltpu.CompilerParams(vmem_limit_bytes=VMEM_LIMIT),
        cost_estimate=pl.CostEstimate(flops=flops, bytes_accessed=nbytes, transcendentals=0),
        name=name,
    )(*args)


def pick(k, count, own, oth, make):
    @pl.when(k < count)
    def _():
        for src, dst, sem in make(own, k):
            pltpu.make_async_copy(src, dst, sem).start()

    @pl.when(k >= count)
    def _():
        for src, dst, sem in make(oth, k - count):
            pltpu.make_async_copy(src, dst, sem).start()


def block(index, size):
    return pl.ds(pl.multiple_of(index * size, size), size)


def copy(src, dst, sem):
    return pltpu.make_async_copy(src, dst, sem)


def fill_distance(dist_ref, length):
    rows = dist_ref.shape[0]
    keys = lax.broadcasted_iota(jnp.int32, (rows, rows), 0)
    places = lax.broadcasted_iota(jnp.int32, (rows, rows), 1)
    distance = jnp.abs(keys - places).astype(F32)
    dist_ref[...] = jnp.where(keys < length, distance, 1e12)


def normalize(v):
    mean = jnp.mean(v, axis=1, keepdims=True)
    centred = v - mean
    rstd = lax.rsqrt(jnp.mean(centred * centred, axis=1, keepdims=True) + EPS)
    return centred * rstd, rstd


def halves(rows):
    return [slice(0, rows // 2), slice(rows // 2, rows)]


def layer_forward(x, weights, bias, slopes, vecs, up_bias, meta, chain, deps, slots):
    qkv_own, qkv_oth, o_own, o_oth, up_own, up_oth, down_own, down_oth = weights
    rows, width = x.shape
    local = qkv_own.shape[2]
    units = up_own.shape[2]
    heads_steps = local // CW
    ft = min(512, units)
    tiles = units // ft
    total = 2 * local

    def kernel(meta_ref, ins, outs, scratch):
        (x_hbm, qkv_own_ref, qkv_oth_ref, o_own_ref, o_oth_ref, up_own_ref, up_oth_ref, down_own_ref, down_oth_ref,
         bias_ref, slope_ref, vec_ref, ub_ref) = ins
        q_out, k_out, v_out, mixed_out, lse_out, a_out, b_out, h_out, n_out, u1_out, u2_out, r1_out, r2_out, y_out = outs
        (x_ref, w_ref, o_ref, up_ref, down_ref, qkv_ref, lse_ref, mixed_ref, dist_ref, normed_ref, acc_ref, low_ref,
         tile_ref, row_ref, stat_ref, x_sem, w_sem, o_sem, f_sem, q_sem, m_sem, t_sem, r_sem) = scratch
        slot = meta_ref[0]

        def start_w(k):
            s = lax.rem(k, 2)
            pick(k, heads_steps, qkv_own_ref, qkv_oth_ref,
                 lambda ref, j: [(ref.at[:, :, block(j, CW)], w_ref.at[s], w_sem.at[s])])

        def start_f(k):
            s = lax.rem(k, 2)
            pick(k, tiles, (up_own_ref, down_own_ref), (up_oth_ref, down_oth_ref),
                 lambda ref, j: [(ref[0].at[:, :, block(j, ft)], up_ref.at[s], f_sem.at[s, 0]),
                                 (ref[1].at[:, block(j, ft)], down_ref.at[s], f_sem.at[s, 1])])

        copy(x_hbm, x_ref, x_sem).start()
        start_w(jnp.int32(0))
        start_w(jnp.int32(1))
        copy(o_own_ref, o_ref.at[pl.ds(0, local)], o_sem).start()
        copy(o_oth_ref, o_ref.at[pl.ds(local, local)], o_sem).start()
        start_f(jnp.int32(0))
        start_f(jnp.int32(1))
        fill_distance(dist_ref, meta_ref[2])
        arrived(x_ref, x_sem)

        def write_qkv(i, s):
            cols = block(i, CW)
            return [copy(qkv_ref.at[s, c], out.at[slot, :, cols], q_sem.at[s, c])
                    for c, out in enumerate((q_out, k_out, v_out))] + [
                copy(lse_ref.at[s], lse_out.at[slot, i], q_sem.at[s, 3])]

        @pl.loop(0, 2 * heads_steps)
        def _(i):
            s = lax.rem(i, 2)
            arrived(w_ref.at[s], w_sem.at[s])

            @pl.when(i >= 2)
            def _():
                for item in write_qkv(i - 2, s):
                    item.wait()

            values = x_ref[...]
            b = bias_ref[:, block(i, CW)]
            qkv_ref[s, 0] = (dot(values, w_ref[s, 0]) + b[0:1]).astype(BF)
            qkv_ref[s, 1] = dot(values, w_ref[s, 1]).astype(BF)
            qkv_ref[s, 2] = (dot(values, w_ref[s, 2]) + b[1:2]).astype(BF)

            @pl.when(i + 2 < 2 * heads_steps)
            def _():
                start_w(i + 2)

            parts = []
            for head in range(PER):
                cols = slice(head * HD, (head + 1) * HD)
                query = qkv_ref[s, 0, :, cols] * BF(1.0 / math.sqrt(HD))
                scores = dot(qkv_ref[s, 1, :, cols], query, NT)
                scores = scores - dist_ref[...] * slope_ref[i * PER + head]
                top = jnp.max(scores, axis=0, keepdims=True)
                likely = jnp.exp(scores - top)
                mass = jnp.sum(likely, axis=0, keepdims=True)
                low = (likely * (1.0 / mass)).astype(BF)
                parts.append(dot(low, qkv_ref[s, 2, :, cols], TN).astype(BF))
                lse_ref[s, head : head + 1, :] = top + jnp.log(mass)
            mixed_ref[:, block(i, CW)] = jnp.concatenate(parts, axis=1)
            for item in write_qkv(i, s):
                item.start()

        copy(mixed_ref, mixed_out.at[slot], m_sem).start()
        arrived(o_ref, o_sem)
        vec = vec_ref[...]
        for rs in halves(rows):
            attended = dot(mixed_ref[rs, :], o_ref[...])
            u, rstd = normalize(x_ref[rs, :].astype(F32) + attended + vec[0:1])
            normed = u * vec[1:2] + vec[2:3]
            normed_ref[rs, :] = normed
            low_ref[rs, :] = normed.astype(BF)
            row_ref[0, rs, :] = u.astype(BF)
            stat_ref[0, rs, :] = jnp.broadcast_to(rstd, (rows // 2, 128))
            acc_ref[rs, :] = jnp.zeros((rows // 2, width), F32)
        for index, (src, dst) in enumerate(((low_ref, n_out), (row_ref.at[0], u1_out), (stat_ref.at[0], r1_out))):
            copy(src, dst.at[slot], r_sem.at[index]).start()

        def write_tiles(i, s):
            return [copy(tile_ref.at[s, c], out.at[slot, :, block(i, ft)], t_sem.at[s, c])
                    for c, out in enumerate((a_out, b_out, h_out))]

        @pl.loop(0, 2 * tiles)
        def _(i):
            s = lax.rem(i, 2)
            arrived(up_ref.at[s], f_sem.at[s, 0])
            arrived(down_ref.at[s], f_sem.at[s, 1])

            @pl.when(i >= 2)
            def _():
                for item in write_tiles(i - 2, s):
                    item.wait()

            b = ub_ref[:, block(i, ft)]
            for rs in halves(rows):
                low = low_ref[rs, :]
                gate = dot(low, up_ref[s, 0]) + b[0:1]
                lift = dot(low, up_ref[s, 1]) + b[1:2]
                cdf = 0.5 * lax.erf(gate * (1.0 / math.sqrt(2.0))) + 0.5
                act = gate * cdf
                slope = cdf + gate * (jnp.exp(gate * gate * -0.5) * (1.0 / math.sqrt(2.0 * math.pi)))
                tile_ref[s, 0, rs, :] = act.astype(BF)
                tile_ref[s, 1, rs, :] = (lift * slope).astype(BF)
                hidden = (act * lift).astype(BF)
                tile_ref[s, 2, rs, :] = hidden
                acc_ref[rs, :] += dot(hidden, down_ref[s], NT)

            @pl.when(i + 2 < 2 * tiles)
            def _():
                start_f(i + 2)

            for item in write_tiles(i, s):
                item.start()

        for rs in halves(rows):
            u, rstd = normalize(normed_ref[rs, :] + acc_ref[rs, :] + vec[3:4])
            row_ref[1, rs, :] = u.astype(BF)
            stat_ref[1, rs, :] = jnp.broadcast_to(rstd, (rows // 2, 128))
            row_ref[2, rs, :] = (u * vec[4:5] + vec[5:6]).astype(BF)
        ends = [(row_ref.at[1], u2_out.at[slot]), (stat_ref.at[1], r2_out.at[slot]), (row_ref.at[2], y_out)]
        for index, (src, dst) in enumerate(ends):
            copy(src, dst, r_sem.at[3 + index]).start()
        for index, (src, dst) in enumerate(
            [(low_ref, n_out.at[slot]), (row_ref.at[0], u1_out.at[slot]), (stat_ref.at[0], r1_out.at[slot])] + ends
        ):
            copy(src, dst, r_sem.at[index]).wait()
        copy(mixed_ref, mixed_out.at[slot], m_sem).wait()
        for i in (2 * heads_steps - 2, 2 * heads_steps - 1):
            for item in write_qkv(jnp.int32(i), i % 2):
                item.wait()
        for i in (2 * tiles - 2, 2 * tiles - 1):
            for item in write_tiles(jnp.int32(i), i % 2):
                item.wait()

    sem = pltpu.SemaphoreType.DMA
    return call(
        kernel,
        [x, *weights, (bias, WHOLE), (slopes, SMEM), (vecs, WHOLE), (up_bias, WHOLE)],
        [((slots, rows, total), BF, True)] * 4
        + [((slots, 2 * heads_steps, 8, rows), F32, True)]
        + [((slots, rows, 2 * units), BF, True)] * 3
        + [((slots, rows, width), BF, True)] * 3
        + [((slots, rows, 128), F32, True)] * 2
        + [((rows, width), BF, False)],
        [
            pltpu.VMEM((rows, width), BF),
            pltpu.VMEM((2, 3, width, CW), BF),
            pltpu.VMEM((total, width), BF),
            pltpu.VMEM((2, 2, width, ft), BF),
            pltpu.VMEM((2, width, ft), BF),
            pltpu.VMEM((2, 3, rows, CW), BF),
            pltpu.VMEM((2, 8, rows), F32),
            pltpu.VMEM((rows, total), BF),
            pltpu.VMEM((rows, rows), F32),
            pltpu.VMEM((rows, width), F32),
            pltpu.VMEM((rows, width), F32),
            pltpu.VMEM((rows, width), BF),
            pltpu.VMEM((2, 3, rows, ft), BF),
            pltpu.VMEM((3, rows, width), BF),
            pltpu.VMEM((2, rows, 128), F32),
            sem, sem((2,)), sem, sem((2, 2)), sem((2, 4)), sem, sem((2, 3)), sem((6,)),
        ],
        meta,
        chain,
        deps,
        "layer_forward",
        2 * rows * width * (4 * total + 6 * units) + 4 * rows * rows * total,
        54 << 20,
    )


def layer_backward(grad, kept, weights, slopes, vecs, meta, chain, deps, slots):
    qkv_own, qkv_oth, o_own, o_oth, up_own, up_oth, down_own, down_oth = weights
    q, k, v, _, lse, act, slope, _, _, u1, u2, r1, r2 = kept
    rows, width = grad.shape
    local = qkv_own.shape[2]
    units = up_own.shape[2]
    heads_steps = local // CW
    ft = min(512, units)
    tiles = units // ft
    total = 2 * local

    def norm_back(grad_z, u, rstd, gain):
        t = grad_z * gain
        return rstd * (t - jnp.mean(t, axis=1, keepdims=True) - u * jnp.mean(t * u, axis=1, keepdims=True))

    def row_sum(values):
        return jnp.sum(values, axis=0, keepdims=True)

    def kernel(meta_ref, ins, outs, scratch):
        (g_hbm, q_hbm, k_hbm, v_hbm, lse_hbm, a_hbm, b_hbm, u1_hbm, u2_hbm, r1_hbm, r2_hbm,
         qkv_own_ref, qkv_oth_ref, o_own_ref, o_oth_ref, up_own_ref, up_oth_ref, down_own_ref, down_oth_ref,
         slope_ref, vec_ref) = ins
        gg0_out, gg1_out, gl_out, ga_out, gq_out, gk_out, gv_out, gx_out, gxl_out, sums_out, ub_out, qv_out = outs
        (g_ref, u_ref, r_ref, up_ref, down_ref, ab_ref, gg_ref, low_ref, acc_ref, sums_ref, ub_ref, qv_ref,
         w_ref, o_ref, qkv_ref, lse_ref, gm_ref, dist_ref, gqkv_ref,
         g_sem, f_sem, t_sem, w_sem, q_sem, r_sem) = scratch
        slot = meta_ref[0]

        def start_f(i):
            s = lax.rem(i, 2)
            pick(i, tiles, (up_own_ref, down_own_ref), (up_oth_ref, down_oth_ref),
                 lambda ref, j: [(ref[0].at[:, :, block(j, ft)], up_ref.at[s], f_sem.at[s, 0]),
                                 (ref[1].at[:, block(j, ft)], down_ref.at[s], f_sem.at[s, 1])])
            for c, ref in enumerate((a_hbm, b_hbm)):
                copy(ref.at[slot, :, block(i, ft)], ab_ref.at[s, c], f_sem.at[s, 2 + c]).start()

        def start_w(i):
            s = lax.rem(i, 2)
            pick(i, heads_steps, (qkv_own_ref, o_own_ref), (qkv_oth_ref, o_oth_ref),
                 lambda ref, j: [(ref[0].at[:, :, block(j, CW)], w_ref.at[s], w_sem.at[s, 0]),
                                 (ref[1].at[block(j, CW)], o_ref.at[s], w_sem.at[s, 1])])
            for c, ref in enumerate((q_hbm, k_hbm, v_hbm)):
                copy(ref.at[slot, :, block(i, CW)], qkv_ref.at[s, c], w_sem.at[s, 2 + c]).start()
            copy(lse_hbm.at[slot, i], lse_ref.at[s], w_sem.at[s, 5]).start()

        firsts = [(g_hbm, g_ref), (u2_hbm.at[slot], u_ref.at[1]), (r2_hbm.at[slot], r_ref.at[1]),
                  (u1_hbm.at[slot], u_ref.at[0]), (r1_hbm.at[slot], r_ref.at[0])]
        for index, (src, dst) in enumerate(firsts):
            copy(src, dst, g_sem.at[index]).start()
            if index == 2:
                start_f(jnp.int32(0))
                start_f(jnp.int32(1))
        start_w(jnp.int32(0))
        start_w(jnp.int32(1))
        vec = vec_ref[...]
        fill_distance(dist_ref, meta_ref[2])
        for index, (src, dst) in enumerate(firsts[:3]):
            copy(src, dst, g_sem.at[index]).wait()
        sums = [jnp.zeros((1, width), F32)] * 3
        for rs in halves(rows):
            grad_y = g_ref[rs, :].astype(F32)
            u = u_ref[1, rs, :].astype(F32)
            grad_c = norm_back(grad_y, u, r_ref[1, rs, 0:1], vec[4:5])
            acc_ref[rs, :] = grad_c
            low_ref[0, rs, :] = grad_c.astype(BF)
            for index, values in enumerate((grad_y * u, grad_y, grad_c)):
                sums[index] += row_sum(values)
        for index in range(3):
            sums_ref[index : index + 1, :] = sums[index]
        copy(low_ref.at[0], gl_out.at[slot], r_sem.at[0]).start()

        def write_tiles(i, s):
            return [copy(gg_ref.at[s, c], out.at[slot, :, block(i, ft)], t_sem.at[s, c])
                    for c, out in enumerate((gg0_out, gg1_out))]

        @pl.loop(0, 2 * tiles)
        def _(i):
            s = lax.rem(i, 2)
            arrived(up_ref.at[s], f_sem.at[s, 0])
            arrived(down_ref.at[s], f_sem.at[s, 1])
            for c in range(2):
                arrived(ab_ref.at[s, c], f_sem.at[s, 2 + c])

            @pl.when(i >= 2)
            def _():
                for item in write_tiles(i - 2, s):
                    item.wait()

            s0 = jnp.zeros((1, ft), F32)
            s1 = jnp.zeros((1, ft), F32)
            for rs in halves(rows):
                gh = dot(low_ref[0, rs, :], down_ref[s])
                g0 = (gh * ab_ref[s, 1, rs, :].astype(F32)).astype(BF)
                g1 = (gh * ab_ref[s, 0, rs, :].astype(F32)).astype(BF)
                gg_ref[s, 0, rs, :] = g0
                gg_ref[s, 1, rs, :] = g1
                s0 += row_sum(g0.astype(F32))
                s1 += row_sum(g1.astype(F32))
                acc_ref[rs, :] += dot(g0, up_ref[s, 0], NT) + dot(g1, up_ref[s, 1], NT)
            ub_ref[0:1, block(i, ft)] = s0
            ub_ref[1:2, block(i, ft)] = s1

            @pl.when(i + 2 < 2 * tiles)
            def _():
                start_f(i + 2)

            for item in write_tiles(i, s):
                item.start()

        for index, (src, dst) in enumerate(firsts[3:]):
            copy(src, dst, g_sem.at[3 + index]).wait()
        sums = [jnp.zeros((1, width), F32)] * 3
        for rs in halves(rows):
            grad_n = acc_ref[rs, :]
            u = u_ref[0, rs, :].astype(F32)
            grad_a = norm_back(grad_n, u, r_ref[0, rs, 0:1], vec[1:2])
            low_ref[1, rs, :] = grad_a.astype(BF)
            acc_ref[rs, :] = grad_a
            for index, values in enumerate((grad_n * u, grad_n, grad_a)):
                sums[index] += row_sum(values)
        for index in range(3):
            sums_ref[3 + index : 4 + index, :] = sums[index]
        sums_ref[6:8, :] = jnp.zeros((2, width), F32)
        copy(low_ref.at[1], ga_out.at[slot], r_sem.at[1]).start()
        scale = BF(1.0 / math.sqrt(HD))

        def write_heads(i, s):
            return [copy(gqkv_ref.at[s, c], out.at[slot, :, block(i, CW)], q_sem.at[s, c])
                    for c, out in enumerate((gq_out, gk_out, gv_out))]

        @pl.loop(0, 2 * heads_steps)
        def _(i):
            s = lax.rem(i, 2)
            for index, ref in enumerate((w_ref.at[s], o_ref.at[s], qkv_ref.at[s, 0], qkv_ref.at[s, 1], qkv_ref.at[s, 2], lse_ref.at[s])):
                arrived(ref, w_sem.at[s, index])

            @pl.when(i >= 2)
            def _():
                for item in write_heads(i - 2, s):
                    item.wait()

            gm_ref[...] = dot(low_ref[1], o_ref[s], NT).astype(BF)
            parts = [[], [], []]
            for head in range(PER):
                cols = slice(head * HD, (head + 1) * HD)
                query = qkv_ref[s, 0, :, cols] * scale
                key = qkv_ref[s, 1, :, cols]
                gm = gm_ref[:, cols]
                scores = dot(key, query, NT)
                scores = scores - dist_ref[...] * slope_ref[i * PER + head]
                likely = jnp.exp(scores - lse_ref[s, head : head + 1, :])
                parts[2].append(dot(likely.astype(BF), gm).astype(BF))
                t = likely * dot(qkv_ref[s, 2, :, cols], gm, NT)
                inner = jnp.sum(t, axis=0, keepdims=True)
                gs = (t - likely * inner).astype(BF)
                parts[1].append(dot(gs, query).astype(BF))
                parts[0].append(dot(gs, key * scale, TN).astype(BF))
            for c in range(3):
                gqkv_ref[s, c] = jnp.concatenate(parts[c], axis=1)
            for index, c in enumerate((0, 2)):
                qv_ref[index : index + 1, block(i, CW)] = row_sum(gqkv_ref[s, c].astype(F32))
            acc_ref[...] += (
                dot(gqkv_ref[s, 0], w_ref[s, 0], NT)
                + dot(gqkv_ref[s, 1], w_ref[s, 1], NT)
                + dot(gqkv_ref[s, 2], w_ref[s, 2], NT)
            )

            @pl.when(i + 2 < 2 * heads_steps)
            def _():
                start_w(i + 2)

            for item in write_heads(i, s):
                item.start()

        g_ref[...] = acc_ref[...].astype(BF)
        ends = [(g_ref, gxl_out), (acc_ref, gx_out), (sums_ref, sums_out), (ub_ref, ub_out), (qv_ref, qv_out)]
        for index, (src, dst) in enumerate(ends):
            copy(src, dst, r_sem.at[2 + index]).start()
        for index, (src, dst) in enumerate([(low_ref.at[0], gl_out.at[slot]), (low_ref.at[1], ga_out.at[slot])] + ends):
            copy(src, dst, r_sem.at[index]).wait()
        for i in (2 * tiles - 2, 2 * tiles - 1):
            for item in write_tiles(jnp.int32(i), i % 2):
                item.wait()
        for i in (2 * heads_steps - 2, 2 * heads_steps - 1):
            for item in write_heads(jnp.int32(i), i % 2):
                item.wait()

    sem = pltpu.SemaphoreType.DMA
    return call(
        kernel,
        [grad, q, k, v, lse, act, slope, u1, u2, r1, r2, *weights, (slopes, SMEM), (vecs, WHOLE)],
        [((slots, rows, 2 * units), BF, True)] * 2
        + [((slots, rows, width), BF, True)] * 2
        + [((slots, rows, total), BF, True)] * 3
        + [
            ((rows, width), F32, False),
            ((rows, width), BF, False),
            ((8, width), F32, False),
            ((2, 2 * units), F32, False),
            ((2, total), F32, False),
        ],
        [
            pltpu.VMEM((rows, width), BF),
            pltpu.VMEM((2, rows, width), BF),
            pltpu.VMEM((2, rows, 128), F32),
            pltpu.VMEM((2, 2, width, ft), BF),
            pltpu.VMEM((2, width, ft), BF),
            pltpu.VMEM((2, 2, rows, ft), BF),
            pltpu.VMEM((2, 2, rows, ft), BF),
            pltpu.VMEM((2, rows, width), BF),
            pltpu.VMEM((rows, width), F32),
            pltpu.VMEM((8, width), F32),
            pltpu.VMEM((2, 2 * units), F32),
            pltpu.VMEM((2, total), F32),
            pltpu.VMEM((2, 3, width, CW), BF),
            pltpu.VMEM((2, CW, width), BF),
            pltpu.VMEM((2, 3, rows, CW), BF),
            pltpu.VMEM((2, 8, rows), F32),
            pltpu.VMEM((rows, CW), BF),
            pltpu.VMEM((rows, rows), F32),
            pltpu.VMEM((2, 3, rows, CW), BF),
            sem((5,)), sem((2, 4)), sem((2, 2)), sem((2, 6)), sem((2, 3)), sem((7,)),
        ],
        meta,
        chain,
        deps,
        "layer_backward",
        2 * rows * width * (4 * total + 6 * units) + 10 * rows * rows * total,
        70 << 20,
    )


MESH = pl.DeviceIdType.MESH
CORE_LAG = 3
CROSS_LAG = 3
CHAIN_LAG = 2


def neighbours():
    t = lax.axis_index("tensor")
    d = lax.axis_index("dp")
    last = lax.axis_size("dp") // 2 - 1
    c = lax.rem(d, 2)
    z = d // 2
    return t, c, z, last, {"dp": d + 1 - 2 * c}, {"tensor": 1 - t}, {"dp": d + 2}, {"dp": d - 2}


def greet(c, z, chips, core, cross):
    barrier = pltpu.get_barrier_semaphore()
    pl.semaphore_signal(barrier, inc=1, device_id=core, device_id_type=MESH)
    pl.semaphore_signal(barrier, inc=1, device_id=cross, device_id_type=MESH)
    for shift in range(1, chips):
        chip = lax.rem(z + shift, chips)
        pl.semaphore_signal(barrier, inc=1, device_id={"dp": chip * 2 + c}, device_id_type=MESH)
    pl.semaphore_wait(barrier, 1 + chips)


def fetch_other_half(qkv, out, up, down, held, chips):
    weights = [qkv, out, up, down]
    seqs = held.shape[0] // 2
    shard_rows = held.shape[1]
    groups = 2 * chips

    def rows_of(item):
        return weights[item].shape[0]

    plan = []
    up_piece = rows_of(2) // groups
    parts = 4
    for part in range(parts):
        plan.append((2, True, 0, up_piece, part * up_piece // parts, up_piece // parts))
    spread = rows_of(3) // 2
    plan.append((3, True, 0, spread // groups, 0, spread // groups))
    n_spread = len(plan)
    plan.append((-1, False, 0, 0, 0, 0))
    for part in range(3):
        size = rows_of(0) // 6
        plan.append((0, False, 0, rows_of(0) // 2, part * size, size))
    plan.append((1, False, 0, rows_of(1) // 2, 0, rows_of(1) // 2))
    plan.append((-1, False, 0, 0, 0, 1))
    direct = (rows_of(3) - spread) // 2
    for part in range(2):
        plan.append((3, False, spread, direct, part * direct // 2, direct // 2))
    n = len(plan)

    def kernel(*refs):
        ins, held_ref = refs[:4], refs[4]
        outs, rows_ref = refs[5:9], refs[9]
        stage, x_send, x_recv, c_send, c_recv, u_send, u_recv, d_send, d_recv, l_sem = refs[10:]
        t, c, z, last, core, cross, above, below = neighbours()
        greet(c, z, chips, core, cross)

        def rows(index, chip, on):
            item, is_spread, base, piece, offset, size = plan[index]
            place = chip * 2 + on if is_spread else on
            return item, pl.ds(pl.multiple_of(base + place * piece + offset, size), size)

        def cross_copy(index):
            if plan[index][0] < 0:
                m = plan[index][5]
                src = held_ref.at[(1 - t) * seqs + m]
                dst = rows_ref.at[m, pl.ds(pl.multiple_of(t * shard_rows, shard_rows), shard_rows)]
            else:
                item, where = rows(index, z, c)
                src, dst = ins[item].at[where], outs[item].at[where]
            return pltpu.make_async_remote_copy(
                src_ref=src, dst_ref=dst, send_sem=x_send.at[index], recv_sem=x_recv.at[index],
                device_id=cross, device_id_type=MESH,
            )

        def pass_on(index, chip, send, recv, device):
            item, where = rows(index, chip, c)
            place = outs[item].at[where]
            return pltpu.make_async_remote_copy(
                src_ref=place, dst_ref=place, send_sem=send.at[index, chip], recv_sem=recv.at[index, chip],
                device_id=device, device_id_type=MESH,
            )

        def got(index, chip, on, sem):
            item, where = rows(index, chip, on)
            arrived(outs[item].at[where], sem)

        for index in range(n):
            cross_copy(index).start()
        mine = pltpu.make_async_copy(held_ref.at[pl.ds(t * seqs, seqs)], stage, l_sem)
        mine.start()
        mine.wait()
        for m in range(seqs):
            pltpu.make_async_copy(
                stage.at[m], rows_ref.at[m, pl.ds(pl.multiple_of(t * shard_rows, shard_rows), shard_rows)], l_sem
            ).start()

        def handle(index, hop):
            if hop == 0:
                if plan[index][0] < 0:
                    m = plan[index][5]
                    arrived(
                        rows_ref.at[m, pl.ds(pl.multiple_of((1 - t) * shard_rows, shard_rows), shard_rows)],
                        x_recv.at[index],
                    )
                    return
                got(index, z, c, x_recv.at[index])
                pass_on(index, z, c_send, c_recv, core).start()
                if plan[index][1]:
                    @pl.when(z < last)
                    def _():
                        pass_on(index, z, u_send, u_recv, above).start()

                    @pl.when(z > 0)
                    def _():
                        pass_on(index, z, d_send, d_recv, below).start()
                return

            @pl.when(z - hop >= 0)
            def _():
                got(index, z - hop, c, u_recv.at[index, z - hop])

                @pl.when(z < last)
                def _():
                    pass_on(index, z - hop, u_send, u_recv, above).start()

                pass_on(index, z - hop, c_send, c_recv, core).start()

            @pl.when(z + hop <= last)
            def _():
                got(index, z + hop, c, d_recv.at[index, z + hop])

                @pl.when(z > 0)
                def _():
                    pass_on(index, z + hop, d_send, d_recv, below).start()

                pass_on(index, z + hop, c_send, c_recv, core).start()

        for round_ in range(max(n, n_spread + chips - 1)):
            if round_ < n:
                handle(round_, 0)
            for hop in range(1, chips):
                if 0 <= round_ - hop < n_spread:
                    handle(round_ - hop, hop)

        for m in range(seqs):
            arrived(stage.at[m], l_sem)
        for index in range(n):
            item, is_spread = plan[index][:2]
            cross_copy(index).wait_send()
            if item < 0:
                continue
            if not is_spread:
                got(index, z, 1 - c, c_recv.at[index, z])
                pass_on(index, z, c_send, c_recv, core).wait_send()
                continue
            for chip in range(chips):
                got(index, chip, 1 - c, c_recv.at[index, chip])
                pass_on(index, chip, c_send, c_recv, core).wait_send()

                @pl.when((chip <= z) & (z < last))
                def _(chip=chip):
                    pass_on(index, chip, u_send, u_recv, above).wait_send()

                @pl.when((chip >= z) & (z > 0))
                def _(chip=chip):
                    pass_on(index, chip, d_send, d_recv, below).wait_send()

    sem = pltpu.SemaphoreType.DMA
    moved = sum(w.size for w in weights) * 2
    return pl.pallas_call(
        kernel,
        in_specs=[ANY] * 5,
        out_specs=[ANY] * 5,
        out_shape=[jax.ShapeDtypeStruct(w.shape, BF) for w in weights]
        + [jax.ShapeDtypeStruct((seqs, 2 * shard_rows, held.shape[2]), BF)],
        scratch_shapes=[pltpu.VMEM((seqs,) + held.shape[1:], BF)]
        + [sem((n,)), sem((n,))]
        + [sem((n, chips))] * 6
        + [sem],
        compiler_params=pltpu.CompilerParams(collective_id=1, has_side_effects=True),
        cost_estimate=pl.CostEstimate(flops=0, bytes_accessed=2 * moved, transcendentals=0),
        name="fetch_other_half",
    )(*weights, held)


def weight_grads_reduced(groups, sums, chips):
    seqs = 2
    rows, depth = groups[0][0].shape[1:]
    lefts = [g[0] for g in groups]
    rights = [r for g in groups for r in g[1]]
    bt = 128
    half = depth // 2
    quarter = half // 2
    blocks = [r.shape[2] // (2 * bt) for r in rights]
    starts = [sum(blocks[:index]) for index in range(len(rights))]
    total = sum(blocks)
    group_starts = []
    index = 0
    for _, members in groups:
        group_starts.append(starts[index])
        index += len(members)
    n_left, n_right = len(lefts), len(rights)
    homes = [(g, index) for g, (_, members) in enumerate(groups) for index in range(len(members))]
    tiles, mines, gives = 4, CORE_LAG + 1, 4
    last_static = chips - 1
    drain = CORE_LAG + CROSS_LAG + 2 * last_static * CHAIN_LAG + 1
    vec_shape = sums.shape

    def kernel(*refs):
        left_refs = refs[:n_left]
        right_refs = refs[n_left : n_left + n_right]
        sums_ref = refs[n_left + n_right]
        outs = refs[n_left + n_right + 1 : 2 * n_left + n_right + 1]
        sums_out = refs[2 * n_left + n_right + 1]
        (
            acc, from_x, from_z, final, flip, stage, tile, mine, give, vec, vec_in, vec_all,
            tile_sem, stage_sem, give_send, core_recv, x_send, x_recv, z_send, z_recv, f_send, f_recv,
            store_sem, out_send, out_recv, v_load, v_send, v_recv,
        ) = refs[2 * n_left + n_right + 2 :]
        t, c, z, last, core, cross, above, below = neighbours()
        greet(c, z, chips, core, cross)

        def remote(src, dst, send, recv, device):
            return pltpu.make_async_remote_copy(
                src_ref=src, dst_ref=dst, send_sem=send, recv_sem=recv, device_id=device, device_id_type=MESH
            )

        def valid(k):
            return (k >= 0) & (k < total)

        def member(k, visit):
            for m in range(n_right):
                @pl.when((k >= starts[m]) & (k < starts[m] + blocks[m]))
                def _(m=m):
                    visit(m, k - starts[m])

        def load_tile(k):
            slot = lax.rem(k, tiles)

            def visit(m, j):
                for side in range(2):
                    at = pl.multiple_of((side * blocks[m] + j) * bt, bt)
                    pltpu.make_async_copy(
                        right_refs[m].at[pl.ds(0, seqs), :, pl.ds(at, bt)],
                        tile.at[slot, :, :, pl.ds(side * bt, bt)],
                        tile_sem.at[slot],
                    ).start()

            member(k, visit)

        def load_left(g):
            return pltpu.make_async_copy(left_refs[g].at[pl.ds(0, seqs)], stage, stage_sem)

        vec_load = pltpu.make_async_copy(sums_ref, vec.at[0], v_load)
        vec_load.start()
        load_left(0).start()
        for k in range(tiles - 1):
            load_tile(jnp.int32(k))
        vec_load.wait()
        vec_core = remote(vec.at[0], vec_in.at[0], v_send.at[0], v_recv.at[0], core)
        vec_cross = remote(vec.at[1], vec_in.at[1], v_send.at[1], v_recv.at[1], cross)
        vec_core.start()

        up = pl.ds(0, quarter)
        down = pl.ds(quarter, quarter)
        sides = ((up, 0, z, above, below), (down, 1, last - z, below, above))

        @pl.loop(0, total + drain)
        def _(s):
            @pl.when(valid(s))
            def _():
                for g in range(n_left):
                    @pl.when(s == group_starts[g])
                    def _(g=g):
                        load_left(g).wait()
                        for m in range(seqs):
                            flip[:, m * rows : (m + 1) * rows] = stage[m].T
                        if g + 1 < n_left:
                            load_left(g + 1).start()

                slot = lax.rem(s, tiles)
                arrived(tile.at[slot], tile_sem.at[slot])
                give_slot = lax.rem(s, gives)

                @pl.when(s >= gives)
                def _():
                    arrived(give.at[give_slot], give_send.at[give_slot])

                for place, ring, at in ((1 - c, give, give_slot), (c, mine, lax.rem(s, mines))):
                    here = pl.ds(pl.multiple_of(place * half, half), half)
                    block = dot(flip[here, :rows], tile[slot, 0])
                    for m in range(1, seqs):
                        block += dot(flip[here, m * rows : (m + 1) * rows], tile[slot, m])
                    ring[at, 1] = block[:, :bt].astype(BF)
                    ring[at, 0] = block[:, bt:].astype(BF)

            @pl.when(s + tiles - 1 < total)
            def _():
                load_tile(s + tiles - 1)

            k1 = s - CORE_LAG

            @pl.when(valid(k1))
            def _():
                arrived(acc.at[k1], core_recv.at[k1])
                at = lax.rem(k1, mines)
                for side in range(2):
                    acc[k1, side] = (acc[k1, side].astype(F32) + mine[at, side].astype(F32)).astype(BF)

            k2 = k1 - CROSS_LAG

            @pl.when(valid(k2))
            def _():
                arrived(from_x.at[k2], x_recv.at[k2])
                acc[k2, 1] = (acc[k2, 1].astype(F32) + from_x[k2].astype(F32)).astype(BF)

            for span, way, place, ahead, behind in sides:
                k3 = k2 - CHAIN_LAG * place

                @pl.when(valid(k3) & (place > 0))
                def _(span=span, way=way, k3=k3):
                    arrived(from_z.at[k3, span], z_recv.at[way, k3])
                    acc[k3, 1, span] = (acc[k3, 1, span].astype(F32) + from_z[k3, span].astype(F32)).astype(BF)

                k4 = k2 - CHAIN_LAG * (2 * last - place)

                @pl.when(valid(k4) & (place == last))
                def _(span=span, k4=k4):
                    final[k4, span] = acc[k4, 1, span]

                @pl.when(valid(k4) & (place < last))
                def _(span=span, way=way, k4=k4):
                    arrived(final.at[k4, span], f_recv.at[way, k4])

            @pl.when(valid(s))
            def _():
                at = lax.rem(s, gives)
                remote(give.at[at], acc.at[s], give_send.at[at], core_recv.at[s], core).start()

            @pl.when(valid(k1))
            def _():
                remote(acc.at[k1, 0], from_x.at[k1], x_send, x_recv.at[k1], cross).start()

            for span, way, place, ahead, behind in sides:
                k3 = k2 - CHAIN_LAG * place

                @pl.when(valid(k3) & (place < last))
                def _(span=span, way=way, k3=k3, ahead=ahead):
                    remote(acc.at[k3, 1, span], from_z.at[k3, span], z_send.at[way], z_recv.at[way, k3], ahead).start()

                k4 = k2 - CHAIN_LAG * (2 * last - place)

                @pl.when(valid(k4) & (place > 0))
                def _(span=span, way=way, k4=k4, behind=behind):
                    remote(final.at[k4, span], final.at[k4, span], f_send.at[way], f_recv.at[way, k4], behind).start()

            k5 = k2 - CHAIN_LAG * 2 * last

            @pl.when(valid(k5))
            def _():
                def visit(m, j):
                    dst = outs[homes[m][0]].at[
                        homes[m][1], pl.ds(pl.multiple_of(c * half, half), half), pl.ds(pl.multiple_of(j * bt, bt), bt)
                    ]
                    pltpu.make_async_copy(final.at[k5], dst, store_sem).start()
                    remote(final.at[k5], dst, out_send, out_recv, core).start()

                member(k5, visit)

            @pl.when(s == 4)
            def _():
                vec_core.wait_recv()
                vec[1] = vec[0] + vec_in[0]

            @pl.when(s == 5)
            def _():
                vec_cross.start()

            @pl.when(s == 10)
            def _():
                vec_cross.wait_recv()
                vec_all[z] = vec[1] + vec_in[1]

            @pl.when(s == 11)
            def _():
                for shift in range(1, chips):
                    to = lax.rem(z + shift, chips)
                    remote(
                        vec_all.at[z], vec_all.at[z], v_send.at[1 + shift], v_recv.at[1 + shift], {"dp": to * 2 + c}
                    ).start()

        vec_core.wait_send()
        vec_cross.wait_send()
        for shift in range(1, chips):
            origin = lax.rem(z + chips - shift, chips)
            arrived(vec_all.at[origin], v_recv.at[1 + shift])
            arrived(vec_all.at[z], v_send.at[1 + shift])
        whole = vec_all[0]
        for chip in range(1, chips):
            whole += vec_all[chip]
        sums_out[...] = whole
        for at in range(gives):
            arrived(give.at[at], give_send.at[at])
        arrived(acc.at[:, 0], x_send)
        for span, way, place, ahead, behind in sides:
            @pl.when(place < last)
            def _(span=span, way=way):
                arrived(from_z.at[:, span], z_send.at[way])

            @pl.when(place > 0)
            def _(span=span, way=way):
                arrived(final.at[:, span], f_send.at[way])

        arrived(final, out_send)
        arrived(final, store_sem)
        arrived(final, out_recv)

    sem = pltpu.SemaphoreType.DMA
    flops = 2 * seqs * rows * depth * 2 * bt * total
    return pl.pallas_call(
        kernel,
        in_specs=[ANY] * (n_left + n_right + 1),
        out_specs=[ANY] * n_left + [WHOLE],
        out_shape=[jax.ShapeDtypeStruct((len(g[1]), depth, g[1][0].shape[2] // 2), BF) for g in groups]
        + [jax.ShapeDtypeStruct(vec_shape, F32)],
        scratch_shapes=[
            pltpu.VMEM((total, 2, half, bt), BF),
            pltpu.VMEM((total, half, bt), BF),
            pltpu.VMEM((total, half, bt), BF),
            pltpu.VMEM((total, half, bt), BF),
            pltpu.VMEM((depth, seqs * rows), BF),
            pltpu.VMEM((seqs, rows, depth), BF),
            pltpu.VMEM((tiles, seqs, rows, 2 * bt), BF),
            pltpu.VMEM((mines, 2, half, bt), BF),
            pltpu.VMEM((gives, 2, half, bt), BF),
            pltpu.VMEM((2,) + vec_shape, F32),
            pltpu.VMEM((2,) + vec_shape, F32),
            pltpu.VMEM((chips,) + vec_shape, F32),
            sem((tiles,)), sem, sem((gives,)), sem((total,)), sem, sem((total,)),
            sem((2,)), sem((2, total)), sem((2,)), sem((2, total)),
            sem, sem, sem, sem, sem((chips + 1,)), sem((chips + 1,)),
        ],
        compiler_params=pltpu.CompilerParams(
            collective_id=0, has_side_effects=True, vmem_limit_bytes=VMEM_LIMIT
        ),
        cost_estimate=pl.CostEstimate(flops=flops, bytes_accessed=64 << 20, transcendentals=0),
        name="weight_grads_reduced",
    )(*lefts, *rights, sums)


MASKED = -1000000000.0


def shifted(value, axis, steps):
    count = lax.axis_size(axis)
    first, last = (max(0, -steps), min(count, count - steps))
    return lax.ppermute(value, axis, [(source, source + steps) for source in range(first, last)])


def layer_norm(values, gain, shift):
    mean = jnp.mean(values, axis=-1, keepdims=True)
    centred = values - mean
    spread = jnp.mean(centred * centred, axis=-1, keepdims=True)
    return centred * lax.rsqrt(spread + EPS) * gain + shift


def alibi_slopes(first, count, heads):
    index = (first + jnp.arange(count)).astype(jnp.float32)
    return jnp.exp2(-8.0 * (index + 1.0) / heads)


def attention_core(projected, qv_bias, slopes, key_ok):
    rows = projected.shape[0]
    width = projected.shape[2]
    count = slopes.shape[0]
    size = width // count
    query = (projected[:, 0] + qv_bias[0]).astype(jnp.bfloat16).reshape(rows, count, size)
    key = projected[:, 1].astype(jnp.bfloat16).reshape(rows, count, size)
    value = (projected[:, 2] + qv_bias[1]).astype(jnp.bfloat16).reshape(rows, count, size)
    place = jnp.arange(rows).astype(jnp.float32)
    distance = jnp.abs(place[:, None] - place[None, :])
    scale = 1.0 / math.sqrt(size)
    scores = (
        jnp.einsum("qhd,khd->hqk", query, key, preferred_element_type=jnp.float32) * scale
        - slopes[:, None, None] * distance[None]
    )
    scores = jnp.where(key_ok[None, None, :], scores, MASKED)
    weights = jax.nn.softmax(scores, axis=-1)
    weights_low = weights.astype(jnp.bfloat16)
    mixed = jnp.einsum("hqk,khd->qhd", weights_low, value, preferred_element_type=jnp.float32)
    mixed = mixed.reshape(rows, width).astype(jnp.bfloat16)
    return (query, key, value, weights, weights_low, mixed)


def attention_back(parts, grad_mixed, key_ok):
    query, key, value, weights, weights_low, mixed = parts
    rows, count, size = query.shape
    scale = 1.0 / math.sqrt(size)
    grad_low = grad_mixed.astype(jnp.bfloat16).reshape(rows, count, size)
    grad_weights = jnp.einsum("qhd,khd->hqk", grad_low, value, preferred_element_type=jnp.float32)
    grad_value = jnp.einsum(
        "hqk,qhd->khd", weights_low, grad_low, preferred_element_type=jnp.float32
    )
    inner = jnp.sum(weights * grad_weights, axis=-1, keepdims=True)
    grad_scores = weights * (grad_weights - inner)
    grad_scores = jnp.where(key_ok[None, None, :], grad_scores, 0.0).astype(jnp.bfloat16)
    grad_query = (
        jnp.einsum("hqk,khd->qhd", grad_scores, key, preferred_element_type=jnp.float32) * scale
    ).astype(jnp.bfloat16)
    grad_key = (
        jnp.einsum("hqk,qhd->khd", grad_scores, query, preferred_element_type=jnp.float32) * scale
    ).astype(jnp.bfloat16)
    grad_value = grad_value.astype(jnp.bfloat16)
    width = count * size
    grad_query = grad_query.reshape(rows, width)
    grad_key = grad_key.reshape(rows, width)
    grad_value = grad_value.reshape(rows, width)
    grad_projected = jnp.stack([grad_query, grad_key, grad_value], axis=1).reshape(rows, 3 * width)
    qv_grad = jnp.stack(
        [
            jnp.sum(grad_query.astype(jnp.float32), axis=0),
            jnp.sum(grad_value.astype(jnp.float32), axis=0),
        ]
    )
    return (grad_projected, qv_grad)


def gelu_product(both):
    return jax.nn.gelu(both[:, 0], approximate=False) * both[:, 1]


def geglu(lifted, up_bias):
    return gelu_product(lifted + up_bias[None])


def ffn_grads(rows_low, grad_low, up_weight, up_bias, down_weight):
    lifted = jnp.einsum("sd,gdf->sgf", rows_low, up_weight, preferred_element_type=jnp.float32)
    hidden, geglu_back = jax.vjp(gelu_product, lifted + up_bias[None])
    grad_hidden = jnp.einsum("sd,df->sf", grad_low, down_weight, preferred_element_type=jnp.float32)
    (grad_both,) = geglu_back(grad_hidden)
    grad_lifted = grad_both.astype(jnp.bfloat16)
    grad_bias = jnp.sum(grad_lifted.astype(jnp.float32), axis=0)
    up_grad = jnp.einsum("sd,sgf->gdf", rows_low, grad_lifted, preferred_element_type=jnp.float32)
    down_grad = jnp.einsum(
        "sd,sf->df", grad_low, hidden.astype(jnp.bfloat16), preferred_element_type=jnp.float32
    )
    return (grad_lifted, grad_bias, up_grad, down_grad)


def on_device(
    inputs,
    cotangent,
    lengths,
    w_qkv,
    b_qv,
    w_out,
    b_out,
    ln_gain,
    ln_bias,
    w_up,
    b_up,
    w_down,
    b_down,
):
    batches, shard_rows, width = inputs.shape
    parts = lax.axis_size("tensor")
    place = lax.axis_index("tensor")
    section = lax.axis_index("section")
    last_section = lax.axis_size("section") - 1
    full_rows = shard_rows * parts
    local_width = w_qkv.shape[3]
    local_heads = local_width // HD
    qkv_flat = w_qkv[0].reshape(width, 3 * local_width)
    out_weight = w_out[0]
    qv_bias = b_qv[0].astype(jnp.float32)
    out_bias = b_out[0].astype(jnp.float32)
    gains = ln_gain[0].astype(jnp.float32)
    shifts = ln_bias[0].astype(jnp.float32)
    down_bias = b_down[0].astype(jnp.float32)
    slopes = alibi_slopes(place * local_heads, local_heads, H)
    row_place = place * shard_rows + jnp.arange(shard_rows)
    kept_rows = 0

    def key_mask(length):
        return jnp.arange(full_rows) < length

    def after_attention(values, attended, bias, gain_rows, shift_rows):
        return layer_norm(values + attended + bias, gain_rows[0], shift_rows[0])

    def after_ffn(normed, lowered, bias, gain_rows, shift_rows):
        return layer_norm(normed + lowered + bias, gain_rows[1], shift_rows[1])

    def gather_inputs(values):
        return lax.all_gather(values.astype(jnp.bfloat16), "tensor", axis=0, tiled=True)

    def project(gathered):
        return jnp.dot(gathered, qkv_flat, preferred_element_type=jnp.float32).reshape(
            full_rows, 3, local_width
        )

    def attention_forward(values, length):
        gathered = gather_inputs(values)
        projected = project(gathered)
        mixed = attention_core(projected, qv_bias, slopes, key_mask(length))[5]

        def term(start, count):
            return jnp.dot(mixed, out_weight, preferred_element_type=jnp.float32)

        return (
            lax.psum_scatter(
                term(jnp.int32(0), shard_rows * lax.axis_size("tensor")).astype(jnp.bfloat16),
                "tensor",
                scatter_dimension=0,
                tiled=True,
            ).astype(jnp.float32),
            gathered,
            projected,
        )

    up_local = w_up[0]
    up_bias_local = b_up[0].astype(jnp.float32)
    down_local = w_down[0]

    def gather_normed(normed):
        return lax.all_gather(normed.astype(jnp.bfloat16), "tensor", axis=0, tiled=True)

    def ffn_forward(normed):
        lifted = jnp.einsum(
            "sd,gdf->sgf", gather_normed(normed), up_local, preferred_element_type=jnp.float32
        )
        hidden = geglu(lifted, up_bias_local).astype(jnp.bfloat16)

        def term(start, count):
            return jnp.einsum("sf,df->sd", hidden, down_local, preferred_element_type=jnp.float32)

        return lax.psum_scatter(
            term(jnp.int32(0), shard_rows * lax.axis_size("tensor")).astype(jnp.bfloat16),
            "tensor",
            scatter_dimension=0,
            tiled=True,
        ).astype(jnp.float32)

    def ffn_backward(normed, grad_lowered):
        gathered = gather_normed(normed)
        grad_whole = lax.all_gather(grad_lowered.astype(jnp.bfloat16), "tensor", axis=0, tiled=True)
        grad_lifted, grad_bias, up_grad, down_grad = ffn_grads(
            gathered, grad_whole, up_local, up_bias_local, down_local
        )

        def term(start, count):
            return jnp.einsum(
                "sgf,gdf->sd", grad_lifted, up_local, preferred_element_type=jnp.float32
            )

        grad_normed = lax.psum_scatter(
            term(jnp.int32(0), shard_rows * lax.axis_size("tensor")).astype(jnp.bfloat16),
            "tensor",
            scatter_dimension=0,
            tiled=True,
        ).astype(jnp.float32)
        return (grad_normed, (up_grad, grad_bias, down_grad))

    ffn_shapes = (up_local.shape, up_bias_local.shape, down_local.shape)

    def layer_forward(values, length):
        attended, gathered, projected = attention_forward(values, length)
        normed = after_attention(values, attended, out_bias, gains, shifts)
        lowered = ffn_forward(normed)
        return (
            after_ffn(normed, lowered, down_bias, gains, shifts),
            attended,
            lowered,
            gathered,
            projected,
        )

    def layer_backward(values, attended, lowered, length, grad_output):
        normed, attention_norm_back = jax.vjp(
            after_attention, values, attended, out_bias, gains, shifts
        )
        outcome, ffn_norm_back = jax.vjp(after_ffn, normed, lowered, down_bias, gains, shifts)
        grad_normed, grad_lowered, grad_down_bias, gain_late, shift_late = ffn_norm_back(
            grad_output
        )
        grad_from_ffn, ffn_terms = ffn_backward(normed, grad_lowered)
        grad_values, grad_attended, grad_out_bias, gain_early, shift_early = attention_norm_back(
            grad_normed + grad_from_ffn
        )
        gathered = gather_inputs(values)
        projected = project(gathered)
        grad_whole = lax.all_gather(
            grad_attended.astype(jnp.bfloat16), "tensor", axis=0, tiled=True
        )
        mask = key_mask(length)
        pieces = attention_core(projected, qv_bias, slopes, mask)
        mixed_low = pieces[5]
        out_grad = jnp.einsum(
            "se,sd->ed", mixed_low, grad_whole, preferred_element_type=jnp.float32
        )
        grad_mixed = jnp.einsum(
            "sd,ed->se", grad_whole, out_weight, preferred_element_type=jnp.float32
        )
        grad_projected, qv_grad = attention_back(pieces, grad_mixed, mask)
        qkv_grad = jnp.einsum(
            "sd,sx->dx", gathered, grad_projected, preferred_element_type=jnp.float32
        )

        def term(start, count):
            return jnp.einsum(
                "sx,dx->sd", grad_projected, qkv_flat, preferred_element_type=jnp.float32
            )

        grad_inputs = grad_values + lax.psum_scatter(
            term(jnp.int32(0), shard_rows * lax.axis_size("tensor")).astype(jnp.bfloat16),
            "tensor",
            scatter_dimension=0,
            tiled=True,
        ).astype(jnp.float32)
        terms = (
            qkv_grad,
            qv_grad,
            out_grad,
            grad_out_bias,
            gain_early + gain_late,
            shift_early + shift_late,
            ffn_terms[0],
            ffn_terms[1],
            ffn_terms[2],
            grad_down_bias,
        )
        return (grad_inputs, terms)

    def keep(store, item, batch, valid):
        old = lax.dynamic_index_in_dim(store, batch, 0, keepdims=False)
        return lax.dynamic_update_index_in_dim(store, jnp.where(valid, item, old), batch, 0)

    def forward_step(step, carry):
        (
            received,
            kept_values,
            kept_attended,
            kept_lowered,
            produced,
            kept_gathered,
            kept_projected,
        ) = carry
        index = step - section
        valid = (index >= 0) & (index < batches)
        batch = jnp.clip(index, 0, batches - 1)
        fresh = lax.dynamic_index_in_dim(
            inputs, jnp.minimum(step, batches - 1), 0, keepdims=False
        ).astype(jnp.float32)
        values = jnp.where(section == 0, fresh, received.astype(jnp.float32))
        output, attended, lowered, gathered, projected = layer_forward(values, lengths[batch])
        sent = output.astype(jnp.bfloat16)
        kept_values = keep(kept_values, values, batch, valid)
        kept_attended = keep(kept_attended, attended, batch, valid)
        kept_lowered = keep(kept_lowered, lowered, batch, valid)
        produced = keep(produced, sent, batch, valid)
        kept_gathered = keep(kept_gathered, gathered[:kept_rows], batch, valid)
        kept_projected = keep(kept_projected, projected[:kept_rows], batch, valid)
        received = shifted(sent, "section", 1)
        return (
            received,
            kept_values,
            kept_attended,
            kept_lowered,
            produced,
            kept_gathered,
            kept_projected,
        )

    store_zeros = jnp.zeros((batches, shard_rows, width), jnp.float32)
    gathered_zeros = jnp.zeros((batches, kept_rows, width), jnp.bfloat16)
    projected_zeros = jnp.zeros((batches, kept_rows, 3, local_width), jnp.float32)
    start_forward = (
        jnp.zeros((shard_rows, width), jnp.bfloat16),
        store_zeros,
        store_zeros,
        store_zeros,
        jnp.zeros((batches, shard_rows, width), jnp.bfloat16),
        gathered_zeros,
        projected_zeros,
    )
    received, kept_values, kept_attended, kept_lowered, produced, kept_gathered, kept_projected = (
        lax.fori_loop(0, batches + last_section, forward_step, start_forward)
    )

    def backward_step(step, carry):
        received, totals, grads_in = carry
        index = step - (last_section - section)
        valid = (index >= 0) & (index < batches)
        batch = jnp.clip(index, 0, batches - 1)
        length = lengths[batch]
        outer = lax.dynamic_index_in_dim(cotangent, batch, 0, keepdims=False).astype(jnp.float32)
        outer = outer * (row_place < length).astype(jnp.float32)[:, None]
        grad_output = jnp.where(section == last_section, outer, received.astype(jnp.float32))
        grad_output = jnp.where(valid, grad_output, 0.0)
        values = lax.dynamic_index_in_dim(kept_values, batch, 0, keepdims=False)
        attended = lax.dynamic_index_in_dim(kept_attended, batch, 0, keepdims=False)
        lowered = lax.dynamic_index_in_dim(kept_lowered, batch, 0, keepdims=False)
        grad_inputs, terms = layer_backward(values, attended, lowered, length, grad_output)
        totals = jax.tree.map(jnp.add, totals, terms)
        grads_in = keep(grads_in, grad_inputs, batch, valid)
        received = shifted(grad_inputs.astype(jnp.bfloat16), "section", -1)
        return (received, totals, grads_in)

    start_totals = (
        jnp.zeros((width, 3 * local_width), jnp.float32),
        jnp.zeros((2, local_width), jnp.float32),
        jnp.zeros((local_width, width), jnp.float32),
        jnp.zeros((width,), jnp.float32),
        jnp.zeros((2, width), jnp.float32),
        jnp.zeros((2, width), jnp.float32),
        jnp.zeros(ffn_shapes[0], jnp.float32),
        jnp.zeros(ffn_shapes[1], jnp.float32),
        jnp.zeros(ffn_shapes[2], jnp.float32),
        jnp.zeros((width,), jnp.float32),
    )
    start_backward = (jnp.zeros((shard_rows, width), jnp.bfloat16), start_totals, store_zeros)
    received, totals, grads_in = lax.fori_loop(
        0, batches + last_section, backward_step, start_backward
    )
    (
        qkv_total,
        qv_total,
        out_total,
        out_bias_total,
        gain_total,
        shift_total,
        up_total,
        up_bias_total,
        down_total,
        down_bias_total,
    ) = totals
    qkv_sum, qv_sum, out_sum, up_sum, up_bias_sum, down_sum = (
        lax.psum(qkv_total.astype(jnp.bfloat16), "dp").astype(jnp.float32),
        lax.psum(qv_total.astype(jnp.bfloat16), "dp").astype(jnp.float32),
        lax.psum(out_total.astype(jnp.bfloat16), "dp").astype(jnp.float32),
        lax.psum(up_total.astype(jnp.bfloat16), "dp").astype(jnp.float32),
        lax.psum(up_bias_total.astype(jnp.bfloat16), "dp").astype(jnp.float32),
        lax.psum(down_total.astype(jnp.bfloat16), "dp").astype(jnp.float32),
    )
    out_bias_sum, gain_sum, shift_sum, down_bias_sum = lax.psum(
        (out_bias_total, gain_total, shift_total, down_bias_total), ("tensor", "dp")
    )
    return (
        produced[None],
        grads_in[None],
        qkv_sum.reshape(1, width, 3, local_width),
        qv_sum[None],
        out_sum[None],
        out_bias_sum[None],
        gain_sum[None],
        shift_sum[None],
        up_sum[None],
        up_bias_sum[None],
        down_sum[None],
        down_bias_sum[None],
    )


def join(first, second, swapped):
    return jnp.where(
        swapped, jnp.concatenate([second, first], axis=0), jnp.concatenate([first, second], axis=0)
    )


def by_sequence(
    inputs,
    cotangent,
    lengths,
    w_qkv,
    b_qv,
    w_out,
    b_out,
    ln_gain,
    ln_bias,
    w_up,
    b_up,
    w_down,
    b_down,
):
    batches, shard_rows, width = inputs.shape
    place = lax.axis_index("tensor")
    section = lax.axis_index("section")
    groups = lax.axis_size("dp")
    rows = 2 * shard_rows
    seqs = batches // 2
    local = w_qkv.shape[3]
    units = w_up.shape[3]
    heads = local // HD
    chips = groups // 2

    def across(value):
        return lax.ppermute(value, "tensor", [(0, 1), (1, 0)])

    def part_rows(value, part):
        return lax.dynamic_slice_in_dim(value, part * shard_rows, shard_rows, 0)

    def own_rows(values, got):
        kept_rows = jnp.stack([part_rows(v, place) for v in values])
        return join(kept_rows, jnp.stack(got).astype(kept_rows.dtype), place == 1)

    qkv_own = jnp.transpose(w_qkv[0], (1, 0, 2))
    out_own = w_out[0]
    up_own = w_up[0]
    down_own = w_down[0]
    small = across(jnp.concatenate([b_qv[0], b_up[0]], axis=1))
    first = section == 0
    qkv_oth, out_oth, up_oth, down_oth, held = fetch_other_half(
        qkv_own.reshape(3 * width, local),
        out_own,
        up_own.reshape(2 * width, units),
        down_own,
        jnp.where(first, inputs, cotangent),
        chips,
    )
    qkv_oth = qkv_oth.reshape(3, width, local)
    up_oth = up_oth.reshape(2, width, units)
    x_first = outer = [held[m] for m in range(seqs)]

    bias = jnp.concatenate([b_qv[0], small[:, :local]], axis=1).astype(F32)
    up_bias = jnp.concatenate([b_up[0], small[:, local:]], axis=1).astype(F32)
    vecs = jnp.stack(
        [b_out[0], ln_gain[0, 0], ln_bias[0, 0], b_down[0], ln_gain[0, 1], ln_bias[0, 1], b_out[0], b_out[0]]
    ).astype(F32)
    slopes = jnp.concatenate(
        [alibi_slopes(place * heads, heads, H), alibi_slopes((1 - place) * heads, heads, H)]
    )
    own_lengths = lax.dynamic_slice_in_dim(lengths, place * seqs, seqs, 0)

    def meta(m, turn):
        active = section == turn
        return jnp.stack([jnp.int32(m), active.astype(jnp.int32), own_lengths[m]])

    metas = [[meta(m, turn) for m in range(seqs)] for turn in range(2)]
    weights = (qkv_own, qkv_oth, out_own, out_oth, up_own, up_oth, down_own, down_oth)
    kept = None
    deps = []

    def forward(x, m, turn):
        nonlocal kept, deps
        *kept, y = layer_forward(x, weights, bias, slopes, vecs, up_bias, metas[turn][m], kept, deps, seqs)
        deps = [y]
        return y

    y_first = [forward(x_first[m], m, 0) for m in range(seqs)]
    x_second = [lax.ppermute(y, "section", [(0, 1)]) for y in y_first]
    y_second = [forward(x_second[m], m, 1) for m in range(seqs)]

    back = None
    sums = [[None] * seqs, [None] * seqs]

    def backward(grad, m, turn):
        nonlocal back, deps
        *back, gx, gx_low, norm_sums, up_sums, qv_sums = layer_backward(
            grad, kept, weights, slopes, vecs, metas[turn][m], back, deps, seqs
        )
        deps = [norm_sums]
        sums[turn][m] = (norm_sums, up_sums, qv_sums)
        return gx, gx_low

    row = jnp.arange(rows)[:, None]
    gx_second = [
        backward(jnp.where(row < own_lengths[m], outer[m], 0), m, 1) for m in range(seqs)
    ]
    grad_middle = [lax.ppermute(gx_second[m][1], "section", [(1, 0)]) for m in range(seqs)]
    gx_first = [backward(grad_middle[m], m, 0) for m in range(seqs)]

    mixed, hidden, normed = kept[3], kept[7], kept[8]
    x_all = jnp.stack([jnp.where(first, x_first[m], x_second[m]) for m in range(seqs)])
    gg0, gg1, gl, ga, *gqkv = back

    y_own = [jnp.where(first, a, b) for a, b in zip(y_first, y_second)]
    produced = own_rows(y_own, [across(part_rows(y, 1 - place)) for y in y_own])
    gx_own = [jnp.where(first, a[0], b[0]) for a, b in zip(gx_first, gx_second)]
    gx_sent = [part_rows(jnp.where(first, a[1], b[1]), 1 - place) for a, b in zip(gx_first, gx_second)]

    picked = [
        sum(jnp.where(first, sums[0][m][index], sums[1][m][index]) for m in range(seqs))
        for index in range(3)
    ]
    norm_sums, up_sums, qv_sums = picked

    def ordered(values, count):
        return jnp.where(
            place == 0, values, jnp.concatenate([values[:, count:], values[:, :count]], axis=1)
        ).reshape(-1, width)

    packed = jnp.concatenate([norm_sums[:6], ordered(up_sums[:2], units), ordered(qv_sums[:2], local)])
    packed, produced, gx_sent = lax.optimization_barrier((packed, produced, gx_sent))
    gx_got = [across(value) for value in gx_sent]
    down_sum, up_sum, qkv_sum, out_sum, packed = weight_grads_reduced(
        [(gl, [hidden]), (normed, [gg0, gg1]), (x_all, gqkv), (ga, [mixed])], packed, chips
    )
    grads_in = own_rows(gx_own, gx_got)
    up_sum = up_sum.astype(F32)
    down_sum = down_sum[0].astype(F32)
    qkv_sum = jnp.transpose(qkv_sum, (1, 0, 2)).astype(F32)
    out_sum = out_sum[0].T.astype(F32)
    norm_total = packed[:6]
    up_total = packed[6 : 6 + 4 * units // width].reshape(2, 2 * units)
    qv_total = packed[6 + 4 * units // width :].reshape(2, 2 * local)
    up_bias_sum = lax.dynamic_slice_in_dim(up_total, place * units, units, 1)
    qv_sum = lax.dynamic_slice_in_dim(qv_total, place * local, local, 1)
    gain_sum = jnp.stack([norm_total[3], norm_total[0]])
    shift_sum = jnp.stack([norm_total[4], norm_total[1]])
    return (
        produced[None],
        grads_in[None],
        qkv_sum[None],
        qv_sum[None],
        out_sum[None],
        norm_total[5][None],
        gain_sum[None],
        shift_sum[None],
        up_sum[None],
        up_bias_sum[None],
        down_sum[None],
        norm_total[2][None],
    )


def solution(mesh):
    sections, parts, groups = (mesh.shape[name] for name in ("section", "tensor", "dp"))

    def run(*args):
        paired = sections == 2 and parts == 2 and groups % 2 == 0 and args[0].shape[0] == 4
        return (by_sequence if paired else on_device)(*args)

    return jax.shard_map(
        run,
        mesh=mesh,
        in_specs=(
            P("dp", "tensor", None),
            P("dp", "tensor", None),
            P("dp"),
            P("section", None, None, "tensor"),
            P("section", None, "tensor"),
            P("section", "tensor", None),
            P("section", None),
            P("section", None, None),
            P("section", None, None),
            P("section", None, None, "tensor"),
            P("section", None, "tensor"),
            P("section", None, "tensor"),
            P("section", None),
        ),
        out_specs=(
            P("section", "dp", "tensor", None),
            P("section", "dp", "tensor", None),
            P("section", None, None, "tensor"),
            P("section", None, "tensor"),
            P("section", "tensor", None),
            P("section", None),
            P("section", None, None),
            P("section", None, None),
            P("section", None, None, "tensor"),
            P("section", None, "tensor"),
            P("section", None, "tensor"),
            P("section", None),
        ),
        check_vma=False,
    )
```

```python
import math

import jax
import jax.numpy as jnp
import numpy as np
from jax import lax
from jax.experimental import pallas as pl
from jax.experimental.pallas import tpu as pltpu
from jax.sharding import PartitionSpec as P

H = 16
HD = 64
EPS = 1e-05
BF = jnp.bfloat16
F32 = jnp.float32
VMEM_LIMIT = 62 * 1024 * 1024
ANY = pl.BlockSpec(memory_space=pl.ANY)
SMEM = pl.BlockSpec(memory_space=pltpu.SMEM)
WHOLE = pl.BlockSpec(memory_space=pltpu.VMEM)
NN = (((1,), (0,)), ((), ()))
NT = (((1,), (1,)), ((), ()))
TN = (((0,), (0,)), ((), ()))
CW = 256
PER = CW // HD


def dot(a, b, dims=NN):
    return lax.dot_general(a, b, dims, preferred_element_type=F32)


def arrived(ref, sem):
    pltpu.make_async_copy(ref, ref, sem).wait()


def call(kernel, inputs, outputs, scratch, meta, chain, deps, name, flops, nbytes):
    pairs = [item if isinstance(item, tuple) else (item, ANY) for item in inputs]
    args = [meta] + [p[0] for p in pairs]
    specs = [SMEM] + [p[1] for p in pairs]
    n_in = len(args)
    aliases = {}
    if chain is not None:
        for buffer, index in zip(chain, [index for index, item in enumerate(outputs) if item[2]]):
            aliases[len(args)] = index
            args.append(buffer)
            specs.append(ANY)
    args += deps
    specs += [ANY] * len(deps)
    n_args, n_out = len(args), len(outputs)

    def body(*refs):
        @pl.when(refs[0][1] == 1)
        def _():
            kernel(refs[0], refs[1:n_in], refs[n_args : n_args + n_out], refs[n_args + n_out :])

    return pl.pallas_call(
        body,
        in_specs=specs,
        out_specs=[ANY] * n_out,
        out_shape=[jax.ShapeDtypeStruct(o[0], o[1]) for o in outputs],
        scratch_shapes=scratch,
        input_output_aliases=aliases,
        compiler_params=pltpu.CompilerParams(vmem_limit_bytes=VMEM_LIMIT),
        cost_estimate=pl.CostEstimate(flops=flops, bytes_accessed=nbytes, transcendentals=0),
        name=name,
    )(*args)


def pick(k, count, own, oth, make):
    @pl.when(k < count)
    def _():
        for src, dst, sem in make(own, k):
            pltpu.make_async_copy(src, dst, sem).start()

    @pl.when(k >= count)
    def _():
        for src, dst, sem in make(oth, k - count):
            pltpu.make_async_copy(src, dst, sem).start()


def block(index, size):
    return pl.ds(pl.multiple_of(index * size, size), size)


def copy(src, dst, sem):
    return pltpu.make_async_copy(src, dst, sem)


def fill_distance(dist_ref, length):
    rows = dist_ref.shape[0]
    keys = lax.broadcasted_iota(jnp.int32, (rows, rows), 0)
    places = lax.broadcasted_iota(jnp.int32, (rows, rows), 1)
    distance = jnp.abs(keys - places).astype(F32)
    dist_ref[...] = jnp.where(keys < length, distance, 1e12)


def normalize(v):
    mean = jnp.mean(v, axis=1, keepdims=True)
    centred = v - mean
    rstd = lax.rsqrt(jnp.mean(centred * centred, axis=1, keepdims=True) + EPS)
    return centred * rstd, rstd


def halves(rows):
    return [slice(0, rows // 2), slice(rows // 2, rows)]


def layer_forward(x, weights, bias, slopes, vecs, up_bias, meta, chain, deps, slots):
    qkv_own, qkv_oth, o_own, o_oth, up_own, up_oth, down_own, down_oth = weights
    rows, width = x.shape
    local = qkv_own.shape[2]
    units = up_own.shape[2]
    heads_steps = local // CW
    ft = min(512, units)
    tiles = units // ft
    total = 2 * local

    def kernel(meta_ref, ins, outs, scratch):
        (x_hbm, qkv_own_ref, qkv_oth_ref, o_own_ref, o_oth_ref, up_own_ref, up_oth_ref, down_own_ref, down_oth_ref,
         bias_ref, slope_ref, vec_ref, ub_ref) = ins
        q_out, k_out, v_out, mixed_out, lse_out, a_out, b_out, h_out, n_out, u1_out, u2_out, r1_out, r2_out, y_out = outs
        (x_ref, w_ref, o_ref, up_ref, down_ref, qkv_ref, lse_ref, mixed_ref, dist_ref, normed_ref, acc_ref, low_ref,
         tile_ref, row_ref, stat_ref, x_sem, w_sem, o_sem, f_sem, q_sem, m_sem, t_sem, r_sem) = scratch
        slot = meta_ref[0]

        def start_w(k):
            s = lax.rem(k, 2)
            pick(k, heads_steps, qkv_own_ref, qkv_oth_ref,
                 lambda ref, j: [(ref.at[:, :, block(j, CW)], w_ref.at[s], w_sem.at[s])])

        def start_f(k):
            s = lax.rem(k, 2)
            pick(k, tiles, (up_own_ref, down_own_ref), (up_oth_ref, down_oth_ref),
                 lambda ref, j: [(ref[0].at[:, :, block(j, ft)], up_ref.at[s], f_sem.at[s, 0]),
                                 (ref[1].at[:, block(j, ft)], down_ref.at[s], f_sem.at[s, 1])])

        copy(x_hbm, x_ref, x_sem).start()
        start_w(jnp.int32(0))
        start_w(jnp.int32(1))
        copy(o_own_ref, o_ref.at[pl.ds(0, local)], o_sem).start()
        copy(o_oth_ref, o_ref.at[pl.ds(local, local)], o_sem).start()
        start_f(jnp.int32(0))
        start_f(jnp.int32(1))
        fill_distance(dist_ref, meta_ref[2])
        arrived(x_ref, x_sem)

        def write_qkv(i, s):
            cols = block(i, CW)
            return [copy(qkv_ref.at[s, c], out.at[slot, :, cols], q_sem.at[s, c])
                    for c, out in enumerate((q_out, k_out, v_out))] + [
                copy(lse_ref.at[s], lse_out.at[slot, i], q_sem.at[s, 3])]

        @pl.loop(0, 2 * heads_steps)
        def _(i):
            s = lax.rem(i, 2)
            arrived(w_ref.at[s], w_sem.at[s])

            @pl.when(i >= 2)
            def _():
                for item in write_qkv(i - 2, s):
                    item.wait()

            values = x_ref[...]
            b = bias_ref[:, block(i, CW)]
            qkv_ref[s, 0] = (dot(values, w_ref[s, 0]) + b[0:1]).astype(BF)
            qkv_ref[s, 1] = dot(values, w_ref[s, 1]).astype(BF)
            qkv_ref[s, 2] = (dot(values, w_ref[s, 2]) + b[1:2]).astype(BF)

            @pl.when(i + 2 < 2 * heads_steps)
            def _():
                start_w(i + 2)

            parts = []
            for head in range(PER):
                cols = slice(head * HD, (head + 1) * HD)
                query = qkv_ref[s, 0, :, cols] * BF(1.0 / math.sqrt(HD))
                scores = dot(qkv_ref[s, 1, :, cols], query, NT)
                scores = scores - dist_ref[...] * slope_ref[i * PER + head]
                top = jnp.max(scores, axis=0, keepdims=True)
                likely = jnp.exp(scores - top)
                mass = jnp.sum(likely, axis=0, keepdims=True)
                low = (likely * (1.0 / mass)).astype(BF)
                parts.append(dot(low, qkv_ref[s, 2, :, cols], TN).astype(BF))
                lse_ref[s, head : head + 1, :] = top + jnp.log(mass)
            mixed_ref[:, block(i, CW)] = jnp.concatenate(parts, axis=1)
            for item in write_qkv(i, s):
                item.start()

        copy(mixed_ref, mixed_out.at[slot], m_sem).start()
        arrived(o_ref, o_sem)
        vec = vec_ref[...]
        for rs in halves(rows):
            attended = dot(mixed_ref[rs, :], o_ref[...])
            u, rstd = normalize(x_ref[rs, :].astype(F32) + attended + vec[0:1])
            normed = u * vec[1:2] + vec[2:3]
            normed_ref[rs, :] = normed
            low_ref[rs, :] = normed.astype(BF)
            row_ref[0, rs, :] = u.astype(BF)
            stat_ref[0, rs, :] = jnp.broadcast_to(rstd, (rows // 2, 128))
            acc_ref[rs, :] = jnp.zeros((rows // 2, width), F32)
        for index, (src, dst) in enumerate(((low_ref, n_out), (row_ref.at[0], u1_out), (stat_ref.at[0], r1_out))):
            copy(src, dst.at[slot], r_sem.at[index]).start()

        def write_tiles(i, s):
            return [copy(tile_ref.at[s, c], out.at[slot, :, block(i, ft)], t_sem.at[s, c])
                    for c, out in enumerate((a_out, b_out, h_out))]

        @pl.loop(0, 2 * tiles)
        def _(i):
            s = lax.rem(i, 2)
            arrived(up_ref.at[s], f_sem.at[s, 0])
            arrived(down_ref.at[s], f_sem.at[s, 1])

            @pl.when(i >= 2)
            def _():
                for item in write_tiles(i - 2, s):
                    item.wait()

            b = ub_ref[:, block(i, ft)]
            for rs in halves(rows):
                low = low_ref[rs, :]
                gate = dot(low, up_ref[s, 0]) + b[0:1]
                lift = dot(low, up_ref[s, 1]) + b[1:2]
                cdf = 0.5 * lax.erf(gate * (1.0 / math.sqrt(2.0))) + 0.5
                act = gate * cdf
                slope = cdf + gate * (jnp.exp(gate * gate * -0.5) * (1.0 / math.sqrt(2.0 * math.pi)))
                tile_ref[s, 0, rs, :] = act.astype(BF)
                tile_ref[s, 1, rs, :] = (lift * slope).astype(BF)
                hidden = (act * lift).astype(BF)
                tile_ref[s, 2, rs, :] = hidden
                acc_ref[rs, :] += dot(hidden, down_ref[s], NT)

            @pl.when(i + 2 < 2 * tiles)
            def _():
                start_f(i + 2)

            for item in write_tiles(i, s):
                item.start()

        for rs in halves(rows):
            u, rstd = normalize(normed_ref[rs, :] + acc_ref[rs, :] + vec[3:4])
            row_ref[1, rs, :] = u.astype(BF)
            stat_ref[1, rs, :] = jnp.broadcast_to(rstd, (rows // 2, 128))
            row_ref[2, rs, :] = (u * vec[4:5] + vec[5:6]).astype(BF)
        ends = [(row_ref.at[1], u2_out.at[slot]), (stat_ref.at[1], r2_out.at[slot]), (row_ref.at[2], y_out)]
        for index, (src, dst) in enumerate(ends):
            copy(src, dst, r_sem.at[3 + index]).start()
        for index, (src, dst) in enumerate(
            [(low_ref, n_out.at[slot]), (row_ref.at[0], u1_out.at[slot]), (stat_ref.at[0], r1_out.at[slot])] + ends
        ):
            copy(src, dst, r_sem.at[index]).wait()
        copy(mixed_ref, mixed_out.at[slot], m_sem).wait()
        for i in (2 * heads_steps - 2, 2 * heads_steps - 1):
            for item in write_qkv(jnp.int32(i), i % 2):
                item.wait()
        for i in (2 * tiles - 2, 2 * tiles - 1):
            for item in write_tiles(jnp.int32(i), i % 2):
                item.wait()

    sem = pltpu.SemaphoreType.DMA
    return call(
        kernel,
        [x, *weights, (bias, WHOLE), (slopes, SMEM), (vecs, WHOLE), (up_bias, WHOLE)],
        [((slots, rows, total), BF, True)] * 4
        + [((slots, 2 * heads_steps, 8, rows), F32, True)]
        + [((slots, rows, 2 * units), BF, True)] * 3
        + [((slots, rows, width), BF, True)] * 3
        + [((slots, rows, 128), F32, True)] * 2
        + [((rows, width), BF, False)],
        [
            pltpu.VMEM((rows, width), BF),
            pltpu.VMEM((2, 3, width, CW), BF),
            pltpu.VMEM((total, width), BF),
            pltpu.VMEM((2, 2, width, ft), BF),
            pltpu.VMEM((2, width, ft), BF),
            pltpu.VMEM((2, 3, rows, CW), BF),
            pltpu.VMEM((2, 8, rows), F32),
            pltpu.VMEM((rows, total), BF),
            pltpu.VMEM((rows, rows), F32),
            pltpu.VMEM((rows, width), F32),
            pltpu.VMEM((rows, width), F32),
            pltpu.VMEM((rows, width), BF),
            pltpu.VMEM((2, 3, rows, ft), BF),
            pltpu.VMEM((3, rows, width), BF),
            pltpu.VMEM((2, rows, 128), F32),
            sem, sem((2,)), sem, sem((2, 2)), sem((2, 4)), sem, sem((2, 3)), sem((6,)),
        ],
        meta,
        chain,
        deps,
        "layer_forward",
        2 * rows * width * (4 * total + 6 * units) + 4 * rows * rows * total,
        54 << 20,
    )


def layer_backward(grad, kept, weights, slopes, vecs, meta, chain, deps, slots):
    qkv_own, qkv_oth, o_own, o_oth, up_own, up_oth, down_own, down_oth = weights
    q, k, v, _, lse, act, slope, _, _, u1, u2, r1, r2 = kept
    rows, width = grad.shape
    local = qkv_own.shape[2]
    units = up_own.shape[2]
    heads_steps = local // CW
    ft = min(512, units)
    tiles = units // ft
    total = 2 * local

    def norm_back(grad_z, u, rstd, gain):
        t = grad_z * gain
        return rstd * (t - jnp.mean(t, axis=1, keepdims=True) - u * jnp.mean(t * u, axis=1, keepdims=True))

    def row_sum(values):
        return jnp.sum(values, axis=0, keepdims=True)

    def kernel(meta_ref, ins, outs, scratch):
        (g_hbm, q_hbm, k_hbm, v_hbm, lse_hbm, a_hbm, b_hbm, u1_hbm, u2_hbm, r1_hbm, r2_hbm,
         qkv_own_ref, qkv_oth_ref, o_own_ref, o_oth_ref, up_own_ref, up_oth_ref, down_own_ref, down_oth_ref,
         slope_ref, vec_ref) = ins
        gg0_out, gg1_out, gl_out, ga_out, gq_out, gk_out, gv_out, gx_out, gxl_out, sums_out, ub_out, qv_out = outs
        (g_ref, u_ref, r_ref, up_ref, down_ref, ab_ref, gg_ref, low_ref, acc_ref, sums_ref, ub_ref, qv_ref,
         w_ref, o_ref, qkv_ref, lse_ref, gm_ref, dist_ref, gqkv_ref,
         g_sem, f_sem, t_sem, w_sem, q_sem, r_sem) = scratch
        slot = meta_ref[0]

        def start_f(i):
            s = lax.rem(i, 2)
            pick(i, tiles, (up_own_ref, down_own_ref), (up_oth_ref, down_oth_ref),
                 lambda ref, j: [(ref[0].at[:, :, block(j, ft)], up_ref.at[s], f_sem.at[s, 0]),
                                 (ref[1].at[:, block(j, ft)], down_ref.at[s], f_sem.at[s, 1])])
            for c, ref in enumerate((a_hbm, b_hbm)):
                copy(ref.at[slot, :, block(i, ft)], ab_ref.at[s, c], f_sem.at[s, 2 + c]).start()

        def start_w(i):
            s = lax.rem(i, 2)
            pick(i, heads_steps, (qkv_own_ref, o_own_ref), (qkv_oth_ref, o_oth_ref),
                 lambda ref, j: [(ref[0].at[:, :, block(j, CW)], w_ref.at[s], w_sem.at[s, 0]),
                                 (ref[1].at[block(j, CW)], o_ref.at[s], w_sem.at[s, 1])])
            for c, ref in enumerate((q_hbm, k_hbm, v_hbm)):
                copy(ref.at[slot, :, block(i, CW)], qkv_ref.at[s, c], w_sem.at[s, 2 + c]).start()
            copy(lse_hbm.at[slot, i], lse_ref.at[s], w_sem.at[s, 5]).start()

        firsts = [(g_hbm, g_ref), (u2_hbm.at[slot], u_ref.at[1]), (r2_hbm.at[slot], r_ref.at[1]),
                  (u1_hbm.at[slot], u_ref.at[0]), (r1_hbm.at[slot], r_ref.at[0])]
        for index, (src, dst) in enumerate(firsts):
            copy(src, dst, g_sem.at[index]).start()
            if index == 2:
                start_f(jnp.int32(0))
                start_f(jnp.int32(1))
        start_w(jnp.int32(0))
        start_w(jnp.int32(1))
        vec = vec_ref[...]
        fill_distance(dist_ref, meta_ref[2])
        for index, (src, dst) in enumerate(firsts[:3]):
            copy(src, dst, g_sem.at[index]).wait()
        sums = [jnp.zeros((1, width), F32)] * 3
        for rs in halves(rows):
            places = lax.broadcasted_iota(jnp.int32, (rows // 2, width), 0) + rs.start
            grad_y = jnp.where(places < meta_ref[3], g_ref[rs, :].astype(F32), 0.0)
            u = u_ref[1, rs, :].astype(F32)
            grad_c = norm_back(grad_y, u, r_ref[1, rs, 0:1], vec[4:5])
            acc_ref[rs, :] = grad_c
            low_ref[0, rs, :] = grad_c.astype(BF)
            for index, values in enumerate((grad_y * u, grad_y, grad_c)):
                sums[index] += row_sum(values)
        for index in range(3):
            sums_ref[index : index + 1, :] = sums[index]
        copy(low_ref.at[0], gl_out.at[slot], r_sem.at[0]).start()

        def write_tiles(i, s):
            return [copy(gg_ref.at[s, c], out.at[slot, :, block(i, ft)], t_sem.at[s, c])
                    for c, out in enumerate((gg0_out, gg1_out))]

        @pl.loop(0, 2 * tiles)
        def _(i):
            s = lax.rem(i, 2)
            arrived(up_ref.at[s], f_sem.at[s, 0])
            arrived(down_ref.at[s], f_sem.at[s, 1])
            for c in range(2):
                arrived(ab_ref.at[s, c], f_sem.at[s, 2 + c])

            @pl.when(i >= 2)
            def _():
                for item in write_tiles(i - 2, s):
                    item.wait()

            s0 = jnp.zeros((1, ft), F32)
            s1 = jnp.zeros((1, ft), F32)
            for rs in halves(rows):
                gh = dot(low_ref[0, rs, :], down_ref[s])
                g0 = (gh * ab_ref[s, 1, rs, :].astype(F32)).astype(BF)
                g1 = (gh * ab_ref[s, 0, rs, :].astype(F32)).astype(BF)
                gg_ref[s, 0, rs, :] = g0
                gg_ref[s, 1, rs, :] = g1
                s0 += row_sum(g0.astype(F32))
                s1 += row_sum(g1.astype(F32))
                acc_ref[rs, :] += dot(g0, up_ref[s, 0], NT) + dot(g1, up_ref[s, 1], NT)
            ub_ref[0:1, block(i, ft)] = s0
            ub_ref[1:2, block(i, ft)] = s1

            @pl.when(i + 2 < 2 * tiles)
            def _():
                start_f(i + 2)

            for item in write_tiles(i, s):
                item.start()

        for index, (src, dst) in enumerate(firsts[3:]):
            copy(src, dst, g_sem.at[3 + index]).wait()
        sums = [jnp.zeros((1, width), F32)] * 3
        for rs in halves(rows):
            grad_n = acc_ref[rs, :]
            u = u_ref[0, rs, :].astype(F32)
            grad_a = norm_back(grad_n, u, r_ref[0, rs, 0:1], vec[1:2])
            low_ref[1, rs, :] = grad_a.astype(BF)
            acc_ref[rs, :] = grad_a
            for index, values in enumerate((grad_n * u, grad_n, grad_a)):
                sums[index] += row_sum(values)
        for index in range(3):
            sums_ref[3 + index : 4 + index, :] = sums[index]
        sums_ref[6:8, :] = jnp.zeros((2, width), F32)
        copy(low_ref.at[1], ga_out.at[slot], r_sem.at[1]).start()
        scale = BF(1.0 / math.sqrt(HD))

        def write_heads(i, s):
            return [copy(gqkv_ref.at[s, c], out.at[slot, :, block(i, CW)], q_sem.at[s, c])
                    for c, out in enumerate((gq_out, gk_out, gv_out))]

        @pl.loop(0, 2 * heads_steps)
        def _(i):
            s = lax.rem(i, 2)
            for index, ref in enumerate((w_ref.at[s], o_ref.at[s], qkv_ref.at[s, 0], qkv_ref.at[s, 1], qkv_ref.at[s, 2], lse_ref.at[s])):
                arrived(ref, w_sem.at[s, index])

            @pl.when(i >= 2)
            def _():
                for item in write_heads(i - 2, s):
                    item.wait()

            gm_ref[...] = dot(low_ref[1], o_ref[s], NT).astype(BF)
            parts = [[], [], []]
            for head in range(PER):
                cols = slice(head * HD, (head + 1) * HD)
                query = qkv_ref[s, 0, :, cols] * scale
                key = qkv_ref[s, 1, :, cols]
                gm = gm_ref[:, cols]
                scores = dot(key, query, NT)
                scores = scores - dist_ref[...] * slope_ref[i * PER + head]
                likely = jnp.exp(scores - lse_ref[s, head : head + 1, :])
                parts[2].append(dot(likely.astype(BF), gm).astype(BF))
                t = likely * dot(qkv_ref[s, 2, :, cols], gm, NT)
                inner = jnp.sum(t, axis=0, keepdims=True)
                gs = (t - likely * inner).astype(BF)
                parts[1].append(dot(gs, query).astype(BF))
                parts[0].append(dot(gs, key * scale, TN).astype(BF))
            for c in range(3):
                gqkv_ref[s, c] = jnp.concatenate(parts[c], axis=1)
            for index, c in enumerate((0, 2)):
                qv_ref[index : index + 1, block(i, CW)] = row_sum(gqkv_ref[s, c].astype(F32))
            acc_ref[...] += (
                dot(gqkv_ref[s, 0], w_ref[s, 0], NT)
                + dot(gqkv_ref[s, 1], w_ref[s, 1], NT)
                + dot(gqkv_ref[s, 2], w_ref[s, 2], NT)
            )

            @pl.when(i + 2 < 2 * heads_steps)
            def _():
                start_w(i + 2)

            for item in write_heads(i, s):
                item.start()

        g_ref[...] = acc_ref[...].astype(BF)
        ends = [(g_ref, gxl_out), (acc_ref, gx_out), (sums_ref, sums_out), (ub_ref, ub_out), (qv_ref, qv_out)]
        for index, (src, dst) in enumerate(ends):
            copy(src, dst, r_sem.at[2 + index]).start()
        for index, (src, dst) in enumerate([(low_ref.at[0], gl_out.at[slot]), (low_ref.at[1], ga_out.at[slot])] + ends):
            copy(src, dst, r_sem.at[index]).wait()
        for i in (2 * tiles - 2, 2 * tiles - 1):
            for item in write_tiles(jnp.int32(i), i % 2):
                item.wait()
        for i in (2 * heads_steps - 2, 2 * heads_steps - 1):
            for item in write_heads(jnp.int32(i), i % 2):
                item.wait()

    sem = pltpu.SemaphoreType.DMA
    return call(
        kernel,
        [grad, q, k, v, lse, act, slope, u1, u2, r1, r2, *weights, (slopes, SMEM), (vecs, WHOLE)],
        [((slots, rows, 2 * units), BF, True)] * 2
        + [((slots, rows, width), BF, True)] * 2
        + [((slots, rows, total), BF, True)] * 3
        + [
            ((rows, width), F32, False),
            ((rows, width), BF, False),
            ((8, width), F32, False),
            ((2, 2 * units), F32, False),
            ((2, total), F32, False),
        ],
        [
            pltpu.VMEM((rows, width), BF),
            pltpu.VMEM((2, rows, width), BF),
            pltpu.VMEM((2, rows, 128), F32),
            pltpu.VMEM((2, 2, width, ft), BF),
            pltpu.VMEM((2, width, ft), BF),
            pltpu.VMEM((2, 2, rows, ft), BF),
            pltpu.VMEM((2, 2, rows, ft), BF),
            pltpu.VMEM((2, rows, width), BF),
            pltpu.VMEM((rows, width), F32),
            pltpu.VMEM((8, width), F32),
            pltpu.VMEM((2, 2 * units), F32),
            pltpu.VMEM((2, total), F32),
            pltpu.VMEM((2, 3, width, CW), BF),
            pltpu.VMEM((2, CW, width), BF),
            pltpu.VMEM((2, 3, rows, CW), BF),
            pltpu.VMEM((2, 8, rows), F32),
            pltpu.VMEM((rows, CW), BF),
            pltpu.VMEM((rows, rows), F32),
            pltpu.VMEM((2, 3, rows, CW), BF),
            sem((5,)), sem((2, 4)), sem((2, 2)), sem((2, 6)), sem((2, 3)), sem((7,)),
        ],
        meta,
        chain,
        deps,
        "layer_backward",
        2 * rows * width * (4 * total + 6 * units) + 10 * rows * rows * total,
        70 << 20,
    )


MESH = pl.DeviceIdType.MESH
CORE_LAG = 3
CROSS_LAG = 3
CHAIN_LAG = 2


def neighbours():
    t = lax.axis_index("tensor")
    d = lax.axis_index("dp")
    last = lax.axis_size("dp") // 2 - 1
    c = lax.rem(d, 2)
    z = d // 2
    return t, c, z, last, {"dp": d + 1 - 2 * c}, {"tensor": 1 - t}, {"dp": d + 2}, {"dp": d - 2}


def greet(c, z, chips, core, cross):
    barrier = pltpu.get_barrier_semaphore()
    pl.semaphore_signal(barrier, inc=1, device_id=core, device_id_type=MESH)
    pl.semaphore_signal(barrier, inc=1, device_id=cross, device_id_type=MESH)
    for shift in range(1, chips):
        chip = lax.rem(z + shift, chips)
        pl.semaphore_signal(barrier, inc=1, device_id={"dp": chip * 2 + c}, device_id_type=MESH)
    pl.semaphore_wait(barrier, 1 + chips)


def fetch_other_half(qkv, out, up, down, qv_bias, up_bias, inputs, cotangent, chips):
    weights = [qkv, out, up, down]
    biases = [qv_bias, up_bias]
    seqs = inputs.shape[0] // 2
    shard_rows, width = inputs.shape[1:]
    groups = 2 * chips

    def rows_of(item):
        return weights[item].shape[0]

    plan = []
    up_piece = rows_of(2) // groups
    parts = 4
    for part in range(parts):
        plan.append((2, True, 0, up_piece, part * up_piece // parts, up_piece // parts))
    spread = rows_of(3) // 2
    plan.append((3, True, 0, spread // groups, 0, spread // groups))
    n_spread = len(plan)
    plan.append((-1, False, 0, 0, 0, 0))
    plan.append((-2, False, 0, 0, 0, 0))
    plan.append((-2, False, 0, 0, 0, 1))
    for part in range(3):
        size = rows_of(0) // 6
        plan.append((0, False, 0, rows_of(0) // 2, part * size, size))
    plan.append((1, False, 0, rows_of(1) // 2, 0, rows_of(1) // 2))
    plan.append((-1, False, 0, 0, 0, 1))
    direct = (rows_of(3) - spread) // 2
    for part in range(2):
        plan.append((3, False, spread, direct, part * direct // 2, direct // 2))
    n = len(plan)

    def kernel(*refs):
        ins, bias_ins, held_refs = refs[:4], refs[4:6], refs[6:8]
        outs, bias_outs, row_refs = refs[8:12], refs[12:14], refs[14 : 14 + seqs]
        stage, x_send, x_recv, c_send, c_recv, u_send, u_recv, d_send, d_recv, l_sem = refs[14 + seqs :]
        t, c, z, last, core, cross, above, below = neighbours()
        section = lax.axis_index("section")
        greet(c, z, chips, core, cross)

        def rows(index, chip, on):
            item, is_spread, base, piece, offset, size = plan[index]
            place = chip * 2 + on if is_spread else on
            return item, pl.ds(pl.multiple_of(base + place * piece + offset, size), size)

        def span(part):
            return block(part, shard_rows)

        def cross_copy(index, held_ref=None):
            m = plan[index][5]
            if plan[index][0] == -1:
                src = (held_refs[0] if held_ref is None else held_ref).at[(1 - t) * seqs + m]
                dst = row_refs[m].at[span(t)]
            elif plan[index][0] == -2:
                src, dst = bias_ins[m], bias_outs[m]
            else:
                item, where = rows(index, z, c)
                src, dst = ins[item].at[where], outs[item].at[where]
            return pltpu.make_async_remote_copy(
                src_ref=src, dst_ref=dst, send_sem=x_send.at[index], recv_sem=x_recv.at[index],
                device_id=cross, device_id_type=MESH,
            )

        def pass_on(index, chip, send, recv, device):
            item, where = rows(index, chip, c)
            place = outs[item].at[where]
            return pltpu.make_async_remote_copy(
                src_ref=place, dst_ref=place, send_sem=send.at[index, chip], recv_sem=recv.at[index, chip],
                device_id=device, device_id_type=MESH,
            )

        def got(index, chip, on, sem):
            item, where = rows(index, chip, on)
            arrived(outs[item].at[where], sem)

        for index in range(n):
            if plan[index][0] == -1:
                for turn in range(2):
                    @pl.when(section == turn)
                    def _(index=index, turn=turn):
                        cross_copy(index, held_refs[turn]).start()
            else:
                cross_copy(index).start()
        for turn in range(2):
            @pl.when(section == turn)
            def _(turn=turn):
                copy(held_refs[turn].at[pl.ds(t * seqs, seqs)], stage, l_sem).start()

        arrived(stage, l_sem)
        for m in range(seqs):
            copy(stage.at[m], row_refs[m].at[span(t)], l_sem).start()

        def handle(index, hop):
            if hop == 0:
                m = plan[index][5]
                if plan[index][0] == -1:
                    arrived(row_refs[m].at[span(1 - t)], x_recv.at[index])
                    return
                if plan[index][0] == -2:
                    arrived(bias_outs[m], x_recv.at[index])
                    return
                got(index, z, c, x_recv.at[index])
                pass_on(index, z, c_send, c_recv, core).start()
                if plan[index][1]:
                    @pl.when(z < last)
                    def _():
                        pass_on(index, z, u_send, u_recv, above).start()

                    @pl.when(z > 0)
                    def _():
                        pass_on(index, z, d_send, d_recv, below).start()
                return

            @pl.when(z - hop >= 0)
            def _():
                got(index, z - hop, c, u_recv.at[index, z - hop])

                @pl.when(z < last)
                def _():
                    pass_on(index, z - hop, u_send, u_recv, above).start()

                pass_on(index, z - hop, c_send, c_recv, core).start()

            @pl.when(z + hop <= last)
            def _():
                got(index, z + hop, c, d_recv.at[index, z + hop])

                @pl.when(z > 0)
                def _():
                    pass_on(index, z + hop, d_send, d_recv, below).start()

                pass_on(index, z + hop, c_send, c_recv, core).start()

        for round_ in range(max(n, n_spread + chips - 1)):
            if round_ < n:
                handle(round_, 0)
            for hop in range(1, chips):
                if 0 <= round_ - hop < n_spread:
                    handle(round_ - hop, hop)

        for m in range(seqs):
            arrived(stage.at[m], l_sem)
        for index in range(n):
            item, is_spread = plan[index][:2]
            cross_copy(index).wait_send()
            if item < 0:
                continue
            if not is_spread:
                got(index, z, 1 - c, c_recv.at[index, z])
                pass_on(index, z, c_send, c_recv, core).wait_send()
                continue
            for chip in range(chips):
                got(index, chip, 1 - c, c_recv.at[index, chip])
                pass_on(index, chip, c_send, c_recv, core).wait_send()

                @pl.when((chip <= z) & (z < last))
                def _(chip=chip):
                    pass_on(index, chip, u_send, u_recv, above).wait_send()

                @pl.when((chip >= z) & (z > 0))
                def _(chip=chip):
                    pass_on(index, chip, d_send, d_recv, below).wait_send()

    sem = pltpu.SemaphoreType.DMA
    moved = sum(w.size for w in weights) * 2
    return pl.pallas_call(
        kernel,
        in_specs=[ANY] * 8,
        out_specs=[ANY] * (6 + seqs),
        out_shape=[jax.ShapeDtypeStruct(w.shape, BF) for w in weights + biases]
        + [jax.ShapeDtypeStruct((2 * shard_rows, width), BF)] * seqs,
        scratch_shapes=[pltpu.VMEM((seqs, shard_rows, width), BF)]
        + [sem((n,)), sem((n,))]
        + [sem((n, chips))] * 6
        + [sem],
        compiler_params=pltpu.CompilerParams(collective_id=1, has_side_effects=True),
        cost_estimate=pl.CostEstimate(flops=0, bytes_accessed=2 * moved, transcendentals=0),
        name="fetch_other_half",
    )(*weights, *biases, inputs, cotangent)


def weight_grads_reduced(groups, sums, row_grads, chips):
    seqs = 2
    rows, depth = groups[0][0].shape[1:]
    lefts = [g[0] for g in groups]
    rights = [r for g in groups for r in g[1]]
    bt = 128
    half = depth // 2
    quarter = half // 2
    blocks = [r.shape[2] // (2 * bt) for r in rights]
    starts = [sum(blocks[:index]) for index in range(len(rights))]
    total = sum(blocks)
    group_starts = []
    index = 0
    for _, members in groups:
        group_starts.append(starts[index])
        index += len(members)
    n_left, n_right = len(lefts), len(rights)
    homes = [(g, index) for g, (_, members) in enumerate(groups) for index in range(len(members))]
    tiles, mines, gives = 4, CORE_LAG + 1, 4
    last_static = chips - 1
    drain = CORE_LAG + CROSS_LAG + 2 * last_static * CHAIN_LAG + 1
    vec_shape = sums.shape
    n_in = n_left + n_right + 1 + 2 * seqs
    shard_rows = rows // 2

    def kernel(*refs):
        left_refs = refs[:n_left]
        right_refs = refs[n_left : n_left + n_right]
        sums_ref = refs[n_left + n_right]
        row_refs = refs[n_left + n_right + 1 : n_in]
        outs = refs[n_in : n_in + n_left]
        sums_out, rows_out = refs[n_in + n_left : n_in + n_left + 2]
        (
            acc, from_x, from_z, final, flip, stage, tile, mine, give, vec, vec_in, vec_all,
            tile_sem, stage_sem, give_send, core_recv, x_send, x_recv, z_send, z_recv, f_send, f_recv,
            store_sem, out_send, out_recv, v_load, v_send, v_recv, r_send, r_recv,
        ) = refs[n_in + n_left + 2 :]
        t, c, z, last, core, cross, above, below = neighbours()
        section = lax.axis_index("section")
        greet(c, z, chips, core, cross)

        def remote(src, dst, send, recv, device):
            return pltpu.make_async_remote_copy(
                src_ref=src, dst_ref=dst, send_sem=send, recv_sem=recv, device_id=device, device_id_type=MESH
            )

        def valid(k):
            return (k >= 0) & (k < total)

        def member(k, visit):
            for m in range(n_right):
                @pl.when((k >= starts[m]) & (k < starts[m] + blocks[m]))
                def _(m=m):
                    visit(m, k - starts[m])

        def load_tile(k):
            slot = lax.rem(k, tiles)

            def visit(m, j):
                for side in range(2):
                    at = pl.multiple_of((side * blocks[m] + j) * bt, bt)
                    pltpu.make_async_copy(
                        right_refs[m].at[pl.ds(0, seqs), :, pl.ds(at, bt)],
                        tile.at[slot, :, :, pl.ds(side * bt, bt)],
                        tile_sem.at[slot],
                    ).start()

            member(k, visit)

        def load_left(g):
            return pltpu.make_async_copy(left_refs[g].at[pl.ds(0, seqs)], stage, stage_sem)

        vec_load = pltpu.make_async_copy(sums_ref, vec.at[0], v_load)
        vec_load.start()
        load_left(0).start()
        for k in range(tiles - 1):
            load_tile(jnp.int32(k))
        vec_load.wait()
        vec_core = remote(vec.at[0], vec_in.at[0], v_send.at[0], v_recv.at[0], core)
        vec_cross = remote(vec.at[1], vec_in.at[1], v_send.at[1], v_recv.at[1], cross)
        vec_core.start()
        for turn in range(2):
            @pl.when(section == turn)
            def _(turn=turn):
                for m in range(seqs):
                    source = row_refs[turn * seqs + m].at[block(1 - t, shard_rows)]
                    remote(source, rows_out.at[m], r_send.at[m], r_recv.at[m], cross).start()

        up = pl.ds(0, quarter)
        down = pl.ds(quarter, quarter)
        sides = ((up, 0, z, above, below), (down, 1, last - z, below, above))

        @pl.loop(0, total + drain)
        def _(s):
            @pl.when(valid(s))
            def _():
                for g in range(n_left):
                    @pl.when(s == group_starts[g])
                    def _(g=g):
                        load_left(g).wait()
                        for m in range(seqs):
                            flip[:, m * rows : (m + 1) * rows] = stage[m].T
                        if g + 1 < n_left:
                            load_left(g + 1).start()

                slot = lax.rem(s, tiles)
                arrived(tile.at[slot], tile_sem.at[slot])
                give_slot = lax.rem(s, gives)

                @pl.when(s >= gives)
                def _():
                    arrived(give.at[give_slot], give_send.at[give_slot])

                for place, ring, at in ((1 - c, give, give_slot), (c, mine, lax.rem(s, mines))):
                    here = pl.ds(pl.multiple_of(place * half, half), half)
                    block = dot(flip[here, :rows], tile[slot, 0])
                    for m in range(1, seqs):
                        block += dot(flip[here, m * rows : (m + 1) * rows], tile[slot, m])
                    ring[at, 1] = block[:, :bt].astype(BF)
                    ring[at, 0] = block[:, bt:].astype(BF)

            @pl.when(s + tiles - 1 < total)
            def _():
                load_tile(s + tiles - 1)

            k1 = s - CORE_LAG

            @pl.when(valid(k1))
            def _():
                arrived(acc.at[k1], core_recv.at[k1])
                at = lax.rem(k1, mines)
                for side in range(2):
                    acc[k1, side] = (acc[k1, side].astype(F32) + mine[at, side].astype(F32)).astype(BF)

            k2 = k1 - CROSS_LAG

            @pl.when(valid(k2))
            def _():
                arrived(from_x.at[k2], x_recv.at[k2])
                acc[k2, 1] = (acc[k2, 1].astype(F32) + from_x[k2].astype(F32)).astype(BF)

            for span, way, place, ahead, behind in sides:
                k3 = k2 - CHAIN_LAG * place

                @pl.when(valid(k3) & (place > 0))
                def _(span=span, way=way, k3=k3):
                    arrived(from_z.at[k3, span], z_recv.at[way, k3])
                    acc[k3, 1, span] = (acc[k3, 1, span].astype(F32) + from_z[k3, span].astype(F32)).astype(BF)

                k4 = k2 - CHAIN_LAG * (2 * last - place)

                @pl.when(valid(k4) & (place == last))
                def _(span=span, k4=k4):
                    final[k4, span] = acc[k4, 1, span]

                @pl.when(valid(k4) & (place < last))
                def _(span=span, way=way, k4=k4):
                    arrived(final.at[k4, span], f_recv.at[way, k4])

            @pl.when(valid(s))
            def _():
                at = lax.rem(s, gives)
                remote(give.at[at], acc.at[s], give_send.at[at], core_recv.at[s], core).start()

            @pl.when(valid(k1))
            def _():
                remote(acc.at[k1, 0], from_x.at[k1], x_send, x_recv.at[k1], cross).start()

            for span, way, place, ahead, behind in sides:
                k3 = k2 - CHAIN_LAG * place

                @pl.when(valid(k3) & (place < last))
                def _(span=span, way=way, k3=k3, ahead=ahead):
                    remote(acc.at[k3, 1, span], from_z.at[k3, span], z_send.at[way], z_recv.at[way, k3], ahead).start()

                k4 = k2 - CHAIN_LAG * (2 * last - place)

                @pl.when(valid(k4) & (place > 0))
                def _(span=span, way=way, k4=k4, behind=behind):
                    remote(final.at[k4, span], final.at[k4, span], f_send.at[way], f_recv.at[way, k4], behind).start()

            k5 = k2 - CHAIN_LAG * 2 * last

            @pl.when(valid(k5))
            def _():
                def visit(m, j):
                    dst = outs[homes[m][0]].at[
                        homes[m][1], pl.ds(pl.multiple_of(c * half, half), half), pl.ds(pl.multiple_of(j * bt, bt), bt)
                    ]
                    pltpu.make_async_copy(final.at[k5], dst, store_sem).start()
                    remote(final.at[k5], dst, out_send, out_recv, core).start()

                member(k5, visit)

            @pl.when(s == 4)
            def _():
                vec_core.wait_recv()
                vec[1] = vec[0] + vec_in[0]

            @pl.when(s == 5)
            def _():
                vec_cross.start()

            @pl.when(s == 10)
            def _():
                vec_cross.wait_recv()
                vec_all[z] = vec[1] + vec_in[1]

            @pl.when(s == 11)
            def _():
                for shift in range(1, chips):
                    to = lax.rem(z + shift, chips)
                    remote(
                        vec_all.at[z], vec_all.at[z], v_send.at[1 + shift], v_recv.at[1 + shift], {"dp": to * 2 + c}
                    ).start()

        for m in range(seqs):
            arrived(rows_out.at[m], r_recv.at[m])
            arrived(rows_out.at[m], r_send.at[m])
        vec_core.wait_send()
        vec_cross.wait_send()
        for shift in range(1, chips):
            origin = lax.rem(z + chips - shift, chips)
            arrived(vec_all.at[origin], v_recv.at[1 + shift])
            arrived(vec_all.at[z], v_send.at[1 + shift])
        whole = vec_all[0]
        for chip in range(1, chips):
            whole += vec_all[chip]
        sums_out[...] = whole
        for at in range(gives):
            arrived(give.at[at], give_send.at[at])
        arrived(acc.at[:, 0], x_send)
        for span, way, place, ahead, behind in sides:
            @pl.when(place < last)
            def _(span=span, way=way):
                arrived(from_z.at[:, span], z_send.at[way])

            @pl.when(place > 0)
            def _(span=span, way=way):
                arrived(final.at[:, span], f_send.at[way])

        arrived(final, out_send)
        arrived(final, store_sem)
        arrived(final, out_recv)

    sem = pltpu.SemaphoreType.DMA
    flops = 2 * seqs * rows * depth * 2 * bt * total
    return pl.pallas_call(
        kernel,
        in_specs=[ANY] * n_in,
        out_specs=[ANY] * n_left + [WHOLE, ANY],
        out_shape=[jax.ShapeDtypeStruct((len(g[1]), depth, g[1][0].shape[2] // 2), BF) for g in groups]
        + [jax.ShapeDtypeStruct(vec_shape, F32), jax.ShapeDtypeStruct((seqs, shard_rows, depth), BF)],
        scratch_shapes=[
            pltpu.VMEM((total, 2, half, bt), BF),
            pltpu.VMEM((total, half, bt), BF),
            pltpu.VMEM((total, half, bt), BF),
            pltpu.VMEM((total, half, bt), BF),
            pltpu.VMEM((depth, seqs * rows), BF),
            pltpu.VMEM((seqs, rows, depth), BF),
            pltpu.VMEM((tiles, seqs, rows, 2 * bt), BF),
            pltpu.VMEM((mines, 2, half, bt), BF),
            pltpu.VMEM((gives, 2, half, bt), BF),
            pltpu.VMEM((2,) + vec_shape, F32),
            pltpu.VMEM((2,) + vec_shape, F32),
            pltpu.VMEM((chips,) + vec_shape, F32),
            sem((tiles,)), sem, sem((gives,)), sem((total,)), sem, sem((total,)),
            sem((2,)), sem((2, total)), sem((2,)), sem((2, total)),
            sem, sem, sem, sem, sem((chips + 1,)), sem((chips + 1,)), sem((seqs,)), sem((seqs,)),
        ],
        compiler_params=pltpu.CompilerParams(
            collective_id=0, has_side_effects=True, vmem_limit_bytes=VMEM_LIMIT
        ),
        cost_estimate=pl.CostEstimate(flops=flops, bytes_accessed=64 << 20, transcendentals=0),
        name="weight_grads_reduced",
    )(*lefts, *rights, sums, *row_grads)


def widen(reduced, row_grads, got):
    seqs, shard_rows, width = got.shape
    n = len(reduced)
    jobs = []
    for index, array in enumerate(reduced):
        lead, depth, columns = array.shape
        step = 512 * 1024 // columns
        if index == n - 1:
            jobs += [(index, 0, at, depth // 2, columns) for at in range(0, depth, depth // 2)]
        else:
            jobs += [(index, part, at, step, columns) for part in range(lead) for at in range(0, depth, step)]
    jobs += [(n, m, 0, shard_rows, width) for m in range(seqs)] + [(n + 1, m, 0, shard_rows, width) for m in range(seqs)]
    ring = 3
    size = 512 * 1024

    def kernel(*refs):
        ins = refs[:n]
        grad_refs = refs[n : n + 2 * seqs]
        got_ref = refs[n + 2 * seqs]
        outs = refs[n + 2 * seqs + 1 : 2 * n + 2 * seqs + 2]
        shapes = sorted({(j[3], j[4]) for j in jobs if j[0] != n})
        buffers = refs[2 * n + 2 * seqs + 2 :]
        wide_rows, in_sem, out_sem = buffers[0], buffers[1], buffers[2]
        low = {s: buffers[3 + 2 * i] for i, s in enumerate(shapes)}
        wide = {s: buffers[4 + 2 * i] for i, s in enumerate(shapes)}
        t = lax.axis_index("tensor")
        section = lax.axis_index("section")

        def load(number):
            index, part, at, rows, columns = jobs[number]
            s = number % ring
            if index < n:
                copy(ins[index].at[part, pl.ds(at, rows)], low[rows, columns].at[s], in_sem.at[s]).start()
            elif index == n:
                for turn in range(2):
                    @pl.when(section == turn)
                    def _(turn=turn):
                        source = grad_refs[turn * seqs + part].at[block(t, shard_rows)]
                        copy(source, wide_rows.at[part], in_sem.at[s]).start()
            else:
                copy(got_ref.at[part], low[rows, columns].at[s], in_sem.at[s]).start()

        def store(number):
            index, part, at, rows, columns = jobs[number]
            s = number % ring
            if index < n - 1:
                return copy(wide[rows, columns].at[s], outs[index].at[part, pl.ds(at, rows)], out_sem.at[s])
            if index == n - 1:
                return copy(wide[rows, columns].at[s], outs[index].at[:, pl.ds(at, rows)], out_sem.at[s])
            if index == n:
                return copy(wide_rows.at[part], outs[n].at[t * seqs + part], out_sem.at[s])
            return copy(wide[rows, columns].at[s], outs[n].at[(1 - t) * seqs + part], out_sem.at[s])

        for number in range(ring):
            load(number)
        for number, (index, part, at, rows, columns) in enumerate(jobs):
            s = number % ring
            if index == n:
                arrived(wide_rows.at[part], in_sem.at[s])
            else:
                arrived(low[rows, columns].at[s], in_sem.at[s])
            if number >= ring:
                store(number - ring).wait()
            if index == n - 1:
                wide[rows, columns][s] = low[rows, columns][s].astype(F32).T
            elif index != n:
                wide[rows, columns][s] = low[rows, columns][s].astype(F32)
            store(number).start()
            if number + ring < len(jobs):
                load(number + ring)
        for number in range(len(jobs) - ring, len(jobs)):
            store(number).wait()

    shapes = sorted({(j[3], j[4]) for j in jobs if j[0] != n})
    square = (reduced[-1].shape[1] // 2, reduced[-1].shape[2])
    last = reduced[-1].shape
    sem = pltpu.SemaphoreType.DMA
    buffers = []
    for s in shapes:
        buffers += [pltpu.VMEM((ring,) + s, BF), pltpu.VMEM((ring,) + ((s[1], s[0]) if s == square else s), F32)]
    return pl.pallas_call(
        kernel,
        in_specs=[ANY] * (n + 2 * seqs + 1),
        out_specs=[ANY] * (n + 1),
        out_shape=[jax.ShapeDtypeStruct(r.shape, F32) for r in reduced[:-1]]
        + [jax.ShapeDtypeStruct((last[2], last[1]), F32), jax.ShapeDtypeStruct((2 * seqs, shard_rows, width), F32)],
        scratch_shapes=[pltpu.VMEM((seqs, shard_rows, width), F32), sem((ring,)), sem((ring,))] + buffers,
        compiler_params=pltpu.CompilerParams(vmem_limit_bytes=VMEM_LIMIT),
        cost_estimate=pl.CostEstimate(flops=0, bytes_accessed=56 << 20, transcendentals=0),
        name="widen",
    )(*reduced, *row_grads, got)


MASKED = -1000000000.0


def shifted(value, axis, steps):
    count = lax.axis_size(axis)
    first, last = (max(0, -steps), min(count, count - steps))
    return lax.ppermute(value, axis, [(source, source + steps) for source in range(first, last)])


def layer_norm(values, gain, shift):
    mean = jnp.mean(values, axis=-1, keepdims=True)
    centred = values - mean
    spread = jnp.mean(centred * centred, axis=-1, keepdims=True)
    return centred * lax.rsqrt(spread + EPS) * gain + shift


def alibi_slopes(first, count, heads):
    index = (first + jnp.arange(count)).astype(jnp.float32)
    return jnp.exp2(-8.0 * (index + 1.0) / heads)


def attention_core(projected, qv_bias, slopes, key_ok):
    rows = projected.shape[0]
    width = projected.shape[2]
    count = slopes.shape[0]
    size = width // count
    query = (projected[:, 0] + qv_bias[0]).astype(jnp.bfloat16).reshape(rows, count, size)
    key = projected[:, 1].astype(jnp.bfloat16).reshape(rows, count, size)
    value = (projected[:, 2] + qv_bias[1]).astype(jnp.bfloat16).reshape(rows, count, size)
    place = jnp.arange(rows).astype(jnp.float32)
    distance = jnp.abs(place[:, None] - place[None, :])
    scale = 1.0 / math.sqrt(size)
    scores = (
        jnp.einsum("qhd,khd->hqk", query, key, preferred_element_type=jnp.float32) * scale
        - slopes[:, None, None] * distance[None]
    )
    scores = jnp.where(key_ok[None, None, :], scores, MASKED)
    weights = jax.nn.softmax(scores, axis=-1)
    weights_low = weights.astype(jnp.bfloat16)
    mixed = jnp.einsum("hqk,khd->qhd", weights_low, value, preferred_element_type=jnp.float32)
    mixed = mixed.reshape(rows, width).astype(jnp.bfloat16)
    return (query, key, value, weights, weights_low, mixed)


def attention_back(parts, grad_mixed, key_ok):
    query, key, value, weights, weights_low, mixed = parts
    rows, count, size = query.shape
    scale = 1.0 / math.sqrt(size)
    grad_low = grad_mixed.astype(jnp.bfloat16).reshape(rows, count, size)
    grad_weights = jnp.einsum("qhd,khd->hqk", grad_low, value, preferred_element_type=jnp.float32)
    grad_value = jnp.einsum(
        "hqk,qhd->khd", weights_low, grad_low, preferred_element_type=jnp.float32
    )
    inner = jnp.sum(weights * grad_weights, axis=-1, keepdims=True)
    grad_scores = weights * (grad_weights - inner)
    grad_scores = jnp.where(key_ok[None, None, :], grad_scores, 0.0).astype(jnp.bfloat16)
    grad_query = (
        jnp.einsum("hqk,khd->qhd", grad_scores, key, preferred_element_type=jnp.float32) * scale
    ).astype(jnp.bfloat16)
    grad_key = (
        jnp.einsum("hqk,qhd->khd", grad_scores, query, preferred_element_type=jnp.float32) * scale
    ).astype(jnp.bfloat16)
    grad_value = grad_value.astype(jnp.bfloat16)
    width = count * size
    grad_query = grad_query.reshape(rows, width)
    grad_key = grad_key.reshape(rows, width)
    grad_value = grad_value.reshape(rows, width)
    grad_projected = jnp.stack([grad_query, grad_key, grad_value], axis=1).reshape(rows, 3 * width)
    qv_grad = jnp.stack(
        [
            jnp.sum(grad_query.astype(jnp.float32), axis=0),
            jnp.sum(grad_value.astype(jnp.float32), axis=0),
        ]
    )
    return (grad_projected, qv_grad)


def gelu_product(both):
    return jax.nn.gelu(both[:, 0], approximate=False) * both[:, 1]


def geglu(lifted, up_bias):
    return gelu_product(lifted + up_bias[None])


def ffn_grads(rows_low, grad_low, up_weight, up_bias, down_weight):
    lifted = jnp.einsum("sd,gdf->sgf", rows_low, up_weight, preferred_element_type=jnp.float32)
    hidden, geglu_back = jax.vjp(gelu_product, lifted + up_bias[None])
    grad_hidden = jnp.einsum("sd,df->sf", grad_low, down_weight, preferred_element_type=jnp.float32)
    (grad_both,) = geglu_back(grad_hidden)
    grad_lifted = grad_both.astype(jnp.bfloat16)
    grad_bias = jnp.sum(grad_lifted.astype(jnp.float32), axis=0)
    up_grad = jnp.einsum("sd,sgf->gdf", rows_low, grad_lifted, preferred_element_type=jnp.float32)
    down_grad = jnp.einsum(
        "sd,sf->df", grad_low, hidden.astype(jnp.bfloat16), preferred_element_type=jnp.float32
    )
    return (grad_lifted, grad_bias, up_grad, down_grad)


def on_device(
    inputs,
    cotangent,
    lengths,
    w_qkv,
    b_qv,
    w_out,
    b_out,
    ln_gain,
    ln_bias,
    w_up,
    b_up,
    w_down,
    b_down,
):
    batches, shard_rows, width = inputs.shape
    parts = lax.axis_size("tensor")
    place = lax.axis_index("tensor")
    section = lax.axis_index("section")
    last_section = lax.axis_size("section") - 1
    full_rows = shard_rows * parts
    local_width = w_qkv.shape[3]
    local_heads = local_width // HD
    qkv_flat = w_qkv[0].reshape(width, 3 * local_width)
    out_weight = w_out[0]
    qv_bias = b_qv[0].astype(jnp.float32)
    out_bias = b_out[0].astype(jnp.float32)
    gains = ln_gain[0].astype(jnp.float32)
    shifts = ln_bias[0].astype(jnp.float32)
    down_bias = b_down[0].astype(jnp.float32)
    slopes = alibi_slopes(place * local_heads, local_heads, H)
    row_place = place * shard_rows + jnp.arange(shard_rows)
    kept_rows = 0

    def key_mask(length):
        return jnp.arange(full_rows) < length

    def after_attention(values, attended, bias, gain_rows, shift_rows):
        return layer_norm(values + attended + bias, gain_rows[0], shift_rows[0])

    def after_ffn(normed, lowered, bias, gain_rows, shift_rows):
        return layer_norm(normed + lowered + bias, gain_rows[1], shift_rows[1])

    def gather_inputs(values):
        return lax.all_gather(values.astype(jnp.bfloat16), "tensor", axis=0, tiled=True)

    def project(gathered):
        return jnp.dot(gathered, qkv_flat, preferred_element_type=jnp.float32).reshape(
            full_rows, 3, local_width
        )

    def attention_forward(values, length):
        gathered = gather_inputs(values)
        projected = project(gathered)
        mixed = attention_core(projected, qv_bias, slopes, key_mask(length))[5]

        def term(start, count):
            return jnp.dot(mixed, out_weight, preferred_element_type=jnp.float32)

        return (
            lax.psum_scatter(
                term(jnp.int32(0), shard_rows * lax.axis_size("tensor")).astype(jnp.bfloat16),
                "tensor",
                scatter_dimension=0,
                tiled=True,
            ).astype(jnp.float32),
            gathered,
            projected,
        )

    up_local = w_up[0]
    up_bias_local = b_up[0].astype(jnp.float32)
    down_local = w_down[0]

    def gather_normed(normed):
        return lax.all_gather(normed.astype(jnp.bfloat16), "tensor", axis=0, tiled=True)

    def ffn_forward(normed):
        lifted = jnp.einsum(
            "sd,gdf->sgf", gather_normed(normed), up_local, preferred_element_type=jnp.float32
        )
        hidden = geglu(lifted, up_bias_local).astype(jnp.bfloat16)

        def term(start, count):
            return jnp.einsum("sf,df->sd", hidden, down_local, preferred_element_type=jnp.float32)

        return lax.psum_scatter(
            term(jnp.int32(0), shard_rows * lax.axis_size("tensor")).astype(jnp.bfloat16),
            "tensor",
            scatter_dimension=0,
            tiled=True,
        ).astype(jnp.float32)

    def ffn_backward(normed, grad_lowered):
        gathered = gather_normed(normed)
        grad_whole = lax.all_gather(grad_lowered.astype(jnp.bfloat16), "tensor", axis=0, tiled=True)
        grad_lifted, grad_bias, up_grad, down_grad = ffn_grads(
            gathered, grad_whole, up_local, up_bias_local, down_local
        )

        def term(start, count):
            return jnp.einsum(
                "sgf,gdf->sd", grad_lifted, up_local, preferred_element_type=jnp.float32
            )

        grad_normed = lax.psum_scatter(
            term(jnp.int32(0), shard_rows * lax.axis_size("tensor")).astype(jnp.bfloat16),
            "tensor",
            scatter_dimension=0,
            tiled=True,
        ).astype(jnp.float32)
        return (grad_normed, (up_grad, grad_bias, down_grad))

    ffn_shapes = (up_local.shape, up_bias_local.shape, down_local.shape)

    def layer_forward(values, length):
        attended, gathered, projected = attention_forward(values, length)
        normed = after_attention(values, attended, out_bias, gains, shifts)
        lowered = ffn_forward(normed)
        return (
            after_ffn(normed, lowered, down_bias, gains, shifts),
            attended,
            lowered,
            gathered,
            projected,
        )

    def layer_backward(values, attended, lowered, length, grad_output):
        normed, attention_norm_back = jax.vjp(
            after_attention, values, attended, out_bias, gains, shifts
        )
        outcome, ffn_norm_back = jax.vjp(after_ffn, normed, lowered, down_bias, gains, shifts)
        grad_normed, grad_lowered, grad_down_bias, gain_late, shift_late = ffn_norm_back(
            grad_output
        )
        grad_from_ffn, ffn_terms = ffn_backward(normed, grad_lowered)
        grad_values, grad_attended, grad_out_bias, gain_early, shift_early = attention_norm_back(
            grad_normed + grad_from_ffn
        )
        gathered = gather_inputs(values)
        projected = project(gathered)
        grad_whole = lax.all_gather(
            grad_attended.astype(jnp.bfloat16), "tensor", axis=0, tiled=True
        )
        mask = key_mask(length)
        pieces = attention_core(projected, qv_bias, slopes, mask)
        mixed_low = pieces[5]
        out_grad = jnp.einsum(
            "se,sd->ed", mixed_low, grad_whole, preferred_element_type=jnp.float32
        )
        grad_mixed = jnp.einsum(
            "sd,ed->se", grad_whole, out_weight, preferred_element_type=jnp.float32
        )
        grad_projected, qv_grad = attention_back(pieces, grad_mixed, mask)
        qkv_grad = jnp.einsum(
            "sd,sx->dx", gathered, grad_projected, preferred_element_type=jnp.float32
        )

        def term(start, count):
            return jnp.einsum(
                "sx,dx->sd", grad_projected, qkv_flat, preferred_element_type=jnp.float32
            )

        grad_inputs = grad_values + lax.psum_scatter(
            term(jnp.int32(0), shard_rows * lax.axis_size("tensor")).astype(jnp.bfloat16),
            "tensor",
            scatter_dimension=0,
            tiled=True,
        ).astype(jnp.float32)
        terms = (
            qkv_grad,
            qv_grad,
            out_grad,
            grad_out_bias,
            gain_early + gain_late,
            shift_early + shift_late,
            ffn_terms[0],
            ffn_terms[1],
            ffn_terms[2],
            grad_down_bias,
        )
        return (grad_inputs, terms)

    def keep(store, item, batch, valid):
        old = lax.dynamic_index_in_dim(store, batch, 0, keepdims=False)
        return lax.dynamic_update_index_in_dim(store, jnp.where(valid, item, old), batch, 0)

    def forward_step(step, carry):
        (
            received,
            kept_values,
            kept_attended,
            kept_lowered,
            produced,
            kept_gathered,
            kept_projected,
        ) = carry
        index = step - section
        valid = (index >= 0) & (index < batches)
        batch = jnp.clip(index, 0, batches - 1)
        fresh = lax.dynamic_index_in_dim(
            inputs, jnp.minimum(step, batches - 1), 0, keepdims=False
        ).astype(jnp.float32)
        values = jnp.where(section == 0, fresh, received.astype(jnp.float32))
        output, attended, lowered, gathered, projected = layer_forward(values, lengths[batch])
        sent = output.astype(jnp.bfloat16)
        kept_values = keep(kept_values, values, batch, valid)
        kept_attended = keep(kept_attended, attended, batch, valid)
        kept_lowered = keep(kept_lowered, lowered, batch, valid)
        produced = keep(produced, sent, batch, valid)
        kept_gathered = keep(kept_gathered, gathered[:kept_rows], batch, valid)
        kept_projected = keep(kept_projected, projected[:kept_rows], batch, valid)
        received = shifted(sent, "section", 1)
        return (
            received,
            kept_values,
            kept_attended,
            kept_lowered,
            produced,
            kept_gathered,
            kept_projected,
        )

    store_zeros = jnp.zeros((batches, shard_rows, width), jnp.float32)
    gathered_zeros = jnp.zeros((batches, kept_rows, width), jnp.bfloat16)
    projected_zeros = jnp.zeros((batches, kept_rows, 3, local_width), jnp.float32)
    start_forward = (
        jnp.zeros((shard_rows, width), jnp.bfloat16),
        store_zeros,
        store_zeros,
        store_zeros,
        jnp.zeros((batches, shard_rows, width), jnp.bfloat16),
        gathered_zeros,
        projected_zeros,
    )
    received, kept_values, kept_attended, kept_lowered, produced, kept_gathered, kept_projected = (
        lax.fori_loop(0, batches + last_section, forward_step, start_forward)
    )

    def backward_step(step, carry):
        received, totals, grads_in = carry
        index = step - (last_section - section)
        valid = (index >= 0) & (index < batches)
        batch = jnp.clip(index, 0, batches - 1)
        length = lengths[batch]
        outer = lax.dynamic_index_in_dim(cotangent, batch, 0, keepdims=False).astype(jnp.float32)
        outer = outer * (row_place < length).astype(jnp.float32)[:, None]
        grad_output = jnp.where(section == last_section, outer, received.astype(jnp.float32))
        grad_output = jnp.where(valid, grad_output, 0.0)
        values = lax.dynamic_index_in_dim(kept_values, batch, 0, keepdims=False)
        attended = lax.dynamic_index_in_dim(kept_attended, batch, 0, keepdims=False)
        lowered = lax.dynamic_index_in_dim(kept_lowered, batch, 0, keepdims=False)
        grad_inputs, terms = layer_backward(values, attended, lowered, length, grad_output)
        totals = jax.tree.map(jnp.add, totals, terms)
        grads_in = keep(grads_in, grad_inputs, batch, valid)
        received = shifted(grad_inputs.astype(jnp.bfloat16), "section", -1)
        return (received, totals, grads_in)

    start_totals = (
        jnp.zeros((width, 3 * local_width), jnp.float32),
        jnp.zeros((2, local_width), jnp.float32),
        jnp.zeros((local_width, width), jnp.float32),
        jnp.zeros((width,), jnp.float32),
        jnp.zeros((2, width), jnp.float32),
        jnp.zeros((2, width), jnp.float32),
        jnp.zeros(ffn_shapes[0], jnp.float32),
        jnp.zeros(ffn_shapes[1], jnp.float32),
        jnp.zeros(ffn_shapes[2], jnp.float32),
        jnp.zeros((width,), jnp.float32),
    )
    start_backward = (jnp.zeros((shard_rows, width), jnp.bfloat16), start_totals, store_zeros)
    received, totals, grads_in = lax.fori_loop(
        0, batches + last_section, backward_step, start_backward
    )
    (
        qkv_total,
        qv_total,
        out_total,
        out_bias_total,
        gain_total,
        shift_total,
        up_total,
        up_bias_total,
        down_total,
        down_bias_total,
    ) = totals
    qkv_sum, qv_sum, out_sum, up_sum, up_bias_sum, down_sum = (
        lax.psum(qkv_total.astype(jnp.bfloat16), "dp").astype(jnp.float32),
        lax.psum(qv_total.astype(jnp.bfloat16), "dp").astype(jnp.float32),
        lax.psum(out_total.astype(jnp.bfloat16), "dp").astype(jnp.float32),
        lax.psum(up_total.astype(jnp.bfloat16), "dp").astype(jnp.float32),
        lax.psum(up_bias_total.astype(jnp.bfloat16), "dp").astype(jnp.float32),
        lax.psum(down_total.astype(jnp.bfloat16), "dp").astype(jnp.float32),
    )
    out_bias_sum, gain_sum, shift_sum, down_bias_sum = lax.psum(
        (out_bias_total, gain_total, shift_total, down_bias_total), ("tensor", "dp")
    )
    return (
        produced[None],
        grads_in[None],
        qkv_sum.reshape(1, width, 3, local_width),
        qv_sum[None],
        out_sum[None],
        out_bias_sum[None],
        gain_sum[None],
        shift_sum[None],
        up_sum[None],
        up_bias_sum[None],
        down_sum[None],
        down_bias_sum[None],
    )


def join(first, second, swapped):
    return jnp.where(
        swapped, jnp.concatenate([second, first], axis=0), jnp.concatenate([first, second], axis=0)
    )


def by_sequence(
    inputs,
    cotangent,
    lengths,
    w_qkv,
    b_qv,
    w_out,
    b_out,
    ln_gain,
    ln_bias,
    w_up,
    b_up,
    w_down,
    b_down,
):
    batches, shard_rows, width = inputs.shape
    place = lax.axis_index("tensor")
    section = lax.axis_index("section")
    groups = lax.axis_size("dp")
    rows = 2 * shard_rows
    seqs = batches // 2
    local = w_qkv.shape[3]
    units = w_up.shape[3]
    heads = local // HD
    chips = groups // 2

    def across(value):
        return lax.ppermute(value, "tensor", [(0, 1), (1, 0)])

    def part_rows(value, part):
        return lax.dynamic_slice_in_dim(value, part * shard_rows, shard_rows, 0)

    qkv_own = jnp.transpose(w_qkv[0], (1, 0, 2))
    out_own = w_out[0]
    up_own = w_up[0]
    down_own = w_down[0]
    first = section == 0
    qkv_oth, out_oth, up_oth, down_oth, qv_oth, ub_oth, *held = fetch_other_half(
        qkv_own.reshape(3 * width, local),
        out_own,
        up_own.reshape(2 * width, units),
        down_own,
        b_qv[0],
        b_up[0],
        inputs,
        cotangent,
        chips,
    )
    qkv_oth = qkv_oth.reshape(3, width, local)
    up_oth = up_oth.reshape(2, width, units)
    x_first = outer = held

    bias = jnp.concatenate([b_qv[0], qv_oth], axis=1).astype(F32)
    up_bias = jnp.concatenate([b_up[0], ub_oth], axis=1).astype(F32)
    vecs = jnp.stack(
        [b_out[0], ln_gain[0, 0], ln_bias[0, 0], b_down[0], ln_gain[0, 1], ln_bias[0, 1], b_out[0], b_out[0]]
    ).astype(F32)
    slope_table = np.exp2(-8.0 * (np.arange(2 * heads, dtype=np.float32) + 1.0) / H).astype(np.float32)
    slopes = jnp.where(place == 0, slope_table, np.roll(slope_table, heads))
    own_lengths = lax.dynamic_slice_in_dim(lengths, place * seqs, seqs, 0)

    def meta(m, turn):
        active = section == turn
        return jnp.stack([jnp.int32(m), active.astype(jnp.int32), own_lengths[m], own_lengths[m] if turn == 1 else jnp.int32(rows)])

    metas = [[meta(m, turn) for m in range(seqs)] for turn in range(2)]
    weights = (qkv_own, qkv_oth, out_own, out_oth, up_own, up_oth, down_own, down_oth)
    kept = None
    deps = []

    def forward(x, m, turn):
        nonlocal kept, deps
        *kept, y = layer_forward(x, weights, bias, slopes, vecs, up_bias, metas[turn][m], kept, deps, seqs)
        deps = [y]
        return y

    y_first = [forward(x_first[m], m, 0) for m in range(seqs)]
    x_second = [lax.ppermute(y, "section", [(0, 1)]) for y in y_first]
    y_second = [forward(x_second[m], m, 1) for m in range(seqs)]

    back = None
    sums = [[None] * seqs, [None] * seqs]

    def backward(grad, m, turn):
        nonlocal back, deps
        *back, gx, gx_low, norm_sums, up_sums, qv_sums = layer_backward(
            grad, kept, weights, slopes, vecs, metas[turn][m], back, deps, seqs
        )
        deps = [norm_sums]
        sums[turn][m] = (norm_sums, up_sums, qv_sums)
        return gx, gx_low

    gx_second = [backward(outer[m], m, 1) for m in range(seqs)]
    grad_middle = [lax.ppermute(gx_second[m][1], "section", [(1, 0)]) for m in range(seqs)]
    y_all, _ = lax.optimization_barrier(((y_first, y_second), deps))
    y_own = [jnp.where(first, a, b) for a, b in zip(*y_all)]
    y_kept = jnp.stack([part_rows(y, place) for y in y_own])
    y_got = jnp.stack([across(part_rows(y, 1 - place)) for y in y_own])
    produced = join(y_kept, y_got, place == 1)
    x_all = jnp.stack([jnp.where(first, x_first[m], x_second[m]) for m in range(seqs)])
    deps = deps + [x_all]
    gx_first = [backward(grad_middle[m], m, 0) for m in range(seqs)]

    mixed, hidden, normed = kept[3], kept[7], kept[8]
    gg0, gg1, gl, ga, *gqkv = back

    picked = [
        sum(jnp.where(first, sums[0][m][index], sums[1][m][index]) for m in range(seqs))
        for index in range(3)
    ]
    norm_sums, up_sums, qv_sums = picked

    def ordered(values, count):
        return jnp.where(
            place == 0, values, jnp.concatenate([values[:, count:], values[:, :count]], axis=1)
        ).reshape(-1, width)

    packed = jnp.concatenate([norm_sums[:6], ordered(up_sums[:2], units), ordered(qv_sums[:2], local)])
    low_grads = [g[1] for g in gx_first + gx_second]
    *reduced, packed, got = weight_grads_reduced(
        [(gl, [hidden]), (normed, [gg0, gg1]), (x_all, gqkv), (ga, [mixed])], packed, low_grads, chips
    )
    down_sum, up_sum, qkv_sum, out_sum, grads_in = widen(reduced, [g[0] for g in gx_first + gx_second], got)
    down_sum = down_sum[0]
    qkv_sum = jnp.transpose(qkv_sum, (1, 0, 2))
    norm_total = packed[:6]
    up_total = packed[6 : 6 + 4 * units // width].reshape(2, 2 * units)
    qv_total = packed[6 + 4 * units // width :].reshape(2, 2 * local)
    up_bias_sum = lax.dynamic_slice_in_dim(up_total, place * units, units, 1)
    qv_sum = lax.dynamic_slice_in_dim(qv_total, place * local, local, 1)
    gain_sum = jnp.stack([norm_total[3], norm_total[0]])
    shift_sum = jnp.stack([norm_total[4], norm_total[1]])
    return (
        produced[None],
        grads_in[None],
        qkv_sum[None],
        qv_sum[None],
        out_sum[None],
        norm_total[5][None],
        gain_sum[None],
        shift_sum[None],
        up_sum[None],
        up_bias_sum[None],
        down_sum[None],
        norm_total[2][None],
    )


def solution(mesh):
    sections, parts, groups = (mesh.shape[name] for name in ("section", "tensor", "dp"))

    def run(*args):
        paired = sections == 2 and parts == 2 and groups % 2 == 0 and args[0].shape[0] == 4
        return (by_sequence if paired else on_device)(*args)

    return jax.shard_map(
        run,
        mesh=mesh,
        in_specs=(
            P("dp", "tensor", None),
            P("dp", "tensor", None),
            P("dp"),
            P("section", None, None, "tensor"),
            P("section", None, "tensor"),
            P("section", "tensor", None),
            P("section", None),
            P("section", None, None),
            P("section", None, None),
            P("section", None, None, "tensor"),
            P("section", None, "tensor"),
            P("section", None, "tensor"),
            P("section", None),
        ),
        out_specs=(
            P("section", "dp", "tensor", None),
            P("section", "dp", "tensor", None),
            P("section", None, None, "tensor"),
            P("section", None, "tensor"),
            P("section", "tensor", None),
            P("section", None),
            P("section", None, None),
            P("section", None, None),
            P("section", None, None, "tensor"),
            P("section", None, "tensor"),
            P("section", None, "tensor"),
            P("section", None),
        ),
        check_vma=False,
    )
```

```python
import math

import jax
import jax.numpy as jnp
import numpy as np
from jax import lax
from jax.experimental import pallas as pl
from jax.experimental.pallas import tpu as pltpu
from jax.sharding import PartitionSpec as P

H = 16
HD = 64
EPS = 1e-05
BF = jnp.bfloat16
F32 = jnp.float32
VMEM_LIMIT = 62 * 1024 * 1024
ANY = pl.BlockSpec(memory_space=pl.ANY)
SMEM = pl.BlockSpec(memory_space=pltpu.SMEM)
WHOLE = pl.BlockSpec(memory_space=pltpu.VMEM)
NN = (((1,), (0,)), ((), ()))
NT = (((1,), (1,)), ((), ()))
TN = (((0,), (0,)), ((), ()))
CW = 256
PER = CW // HD


def dot(a, b, dims=NN):
    return lax.dot_general(a, b, dims, preferred_element_type=F32)


def arrived(ref, sem):
    pltpu.make_async_copy(ref, ref, sem).wait()


def call(kernel, inputs, outputs, scratch, meta, chain, deps, name, flops, nbytes):
    pairs = [item if isinstance(item, tuple) else (item, ANY) for item in inputs]
    args = [meta] + [p[0] for p in pairs]
    specs = [SMEM] + [p[1] for p in pairs]
    n_in = len(args)
    aliases = {}
    if chain is not None:
        for buffer, index in zip(chain, [index for index, item in enumerate(outputs) if item[2]]):
            aliases[len(args)] = index
            args.append(buffer)
            specs.append(ANY)
    args += deps
    specs += [ANY] * len(deps)
    n_args, n_out = len(args), len(outputs)

    def body(*refs):
        @pl.when(refs[0][1] == 1)
        def _():
            kernel(refs[0], refs[1:n_in], refs[n_args : n_args + n_out], refs[n_args + n_out :])

    return pl.pallas_call(
        body,
        in_specs=specs,
        out_specs=[ANY] * n_out,
        out_shape=[jax.ShapeDtypeStruct(o[0], o[1]) for o in outputs],
        scratch_shapes=scratch,
        input_output_aliases=aliases,
        compiler_params=pltpu.CompilerParams(vmem_limit_bytes=VMEM_LIMIT),
        cost_estimate=pl.CostEstimate(flops=flops, bytes_accessed=nbytes, transcendentals=0),
        name=name,
    )(*args)


def pick(k, count, own, oth, make):
    @pl.when(k < count)
    def _():
        for src, dst, sem in make(own, k):
            pltpu.make_async_copy(src, dst, sem).start()

    @pl.when(k >= count)
    def _():
        for src, dst, sem in make(oth, k - count):
            pltpu.make_async_copy(src, dst, sem).start()


def block(index, size):
    return pl.ds(pl.multiple_of(index * size, size), size)


def copy(src, dst, sem):
    return pltpu.make_async_copy(src, dst, sem)


def fill_distance(dist_ref, length):
    rows = dist_ref.shape[0]
    keys = lax.broadcasted_iota(jnp.int32, (rows, rows), 0)
    places = lax.broadcasted_iota(jnp.int32, (rows, rows), 1)
    distance = jnp.abs(keys - places).astype(F32)
    dist_ref[...] = jnp.where(keys < length, distance, 1e12)


def normalize(v):
    mean = jnp.mean(v, axis=1, keepdims=True)
    centred = v - mean
    rstd = lax.rsqrt(jnp.mean(centred * centred, axis=1, keepdims=True) + EPS)
    return centred * rstd, rstd


def halves(rows):
    return [slice(0, rows // 2), slice(rows // 2, rows)]


def layer_forward(x, weights, bias, slopes, vecs, up_bias, meta, chain, deps, slots):
    qkv_own, qkv_oth, o_own, o_oth, up_own, up_oth, down_own, down_oth = weights
    rows, width = x.shape
    local = qkv_own.shape[2]
    units = up_own.shape[2]
    heads_steps = local // CW
    ft = min(512, units)
    tiles = units // ft
    total = 2 * local

    def kernel(meta_ref, ins, outs, scratch):
        (x_hbm, qkv_own_ref, qkv_oth_ref, o_own_ref, o_oth_ref, up_own_ref, up_oth_ref, down_own_ref, down_oth_ref,
         bias_ref, slope_ref, vec_ref, ub_ref) = ins
        q_out, k_out, v_out, mixed_out, lse_out, a_out, b_out, h_out, n_out, u1_out, u2_out, r1_out, r2_out, y_out = outs
        (x_ref, w_ref, o_ref, up_ref, down_ref, qkv_ref, lse_ref, mixed_ref, dist_ref, normed_ref, acc_ref, low_ref,
         tile_ref, row_ref, stat_ref, x_sem, w_sem, o_sem, f_sem, q_sem, m_sem, t_sem, r_sem) = scratch
        slot = meta_ref[0]

        def start_w(k):
            s = lax.rem(k, 2)
            pick(k, heads_steps, qkv_own_ref, qkv_oth_ref,
                 lambda ref, j: [(ref.at[:, :, block(j, CW)], w_ref.at[s], w_sem.at[s])])

        def start_f(k):
            s = lax.rem(k, 2)
            pick(k, tiles, (up_own_ref, down_own_ref), (up_oth_ref, down_oth_ref),
                 lambda ref, j: [(ref[0].at[:, :, block(j, ft)], up_ref.at[s], f_sem.at[s, 0]),
                                 (ref[1].at[:, block(j, ft)], down_ref.at[s], f_sem.at[s, 1])])

        copy(x_hbm, x_ref, x_sem).start()
        start_w(jnp.int32(0))
        start_w(jnp.int32(1))
        copy(o_own_ref, o_ref.at[pl.ds(0, local)], o_sem).start()
        copy(o_oth_ref, o_ref.at[pl.ds(local, local)], o_sem).start()
        start_f(jnp.int32(0))
        start_f(jnp.int32(1))
        fill_distance(dist_ref, meta_ref[2])
        arrived(x_ref, x_sem)

        def write_qkv(i, s):
            cols = block(i, CW)
            return [copy(qkv_ref.at[s, c], out.at[slot, :, cols], q_sem.at[s, c])
                    for c, out in enumerate((q_out, k_out, v_out))] + [
                copy(lse_ref.at[s], lse_out.at[slot, i], q_sem.at[s, 3])]

        @pl.loop(0, 2 * heads_steps)
        def _(i):
            s = lax.rem(i, 2)
            arrived(w_ref.at[s], w_sem.at[s])

            @pl.when(i >= 2)
            def _():
                for item in write_qkv(i - 2, s):
                    item.wait()

            values = x_ref[...]
            b = bias_ref[:, block(i, CW)].astype(F32)
            qkv_ref[s, 0] = (dot(values, w_ref[s, 0]) + b[0:1]).astype(BF)
            qkv_ref[s, 1] = dot(values, w_ref[s, 1]).astype(BF)
            qkv_ref[s, 2] = (dot(values, w_ref[s, 2]) + b[1:2]).astype(BF)

            @pl.when(i + 2 < 2 * heads_steps)
            def _():
                start_w(i + 2)

            parts = []
            for head in range(PER):
                cols = slice(head * HD, (head + 1) * HD)
                query = qkv_ref[s, 0, :, cols] * BF(1.0 / math.sqrt(HD))
                scores = dot(qkv_ref[s, 1, :, cols], query, NT)
                scores = scores - dist_ref[...] * slope_ref[i * PER + head]
                top = jnp.max(scores, axis=0, keepdims=True)
                likely = jnp.exp(scores - top)
                mass = jnp.sum(likely, axis=0, keepdims=True)
                low = (likely * (1.0 / mass)).astype(BF)
                parts.append(dot(low, qkv_ref[s, 2, :, cols], TN).astype(BF))
                lse_ref[s, head : head + 1, :] = top + jnp.log(mass)
            mixed_ref[:, block(i, CW)] = jnp.concatenate(parts, axis=1)
            for item in write_qkv(i, s):
                item.start()

        copy(mixed_ref, mixed_out.at[slot], m_sem).start()
        arrived(o_ref, o_sem)
        vec = vec_ref[...]
        for rs in halves(rows):
            attended = dot(mixed_ref[rs, :], o_ref[...])
            u, rstd = normalize(x_ref[rs, :].astype(F32) + attended + vec[0:1])
            normed = u * vec[1:2] + vec[2:3]
            normed_ref[rs, :] = normed
            low_ref[rs, :] = normed.astype(BF)
            row_ref[0, rs, :] = u.astype(BF)
            stat_ref[0, rs, :] = jnp.broadcast_to(rstd, (rows // 2, 128))
            acc_ref[rs, :] = jnp.zeros((rows // 2, width), F32)
        for index, (src, dst) in enumerate(((low_ref, n_out), (row_ref.at[0], u1_out), (stat_ref.at[0], r1_out))):
            copy(src, dst.at[slot], r_sem.at[index]).start()

        def write_tiles(i, s):
            return [copy(tile_ref.at[s, c], out.at[slot, :, block(i, ft)], t_sem.at[s, c])
                    for c, out in enumerate((a_out, b_out, h_out))]

        @pl.loop(0, 2 * tiles)
        def _(i):
            s = lax.rem(i, 2)
            arrived(up_ref.at[s], f_sem.at[s, 0])
            arrived(down_ref.at[s], f_sem.at[s, 1])

            @pl.when(i >= 2)
            def _():
                for item in write_tiles(i - 2, s):
                    item.wait()

            b = ub_ref[:, block(i, ft)].astype(F32)
            for rs in halves(rows):
                low = low_ref[rs, :]
                gate = dot(low, up_ref[s, 0]) + b[0:1]
                lift = dot(low, up_ref[s, 1]) + b[1:2]
                cdf = 0.5 * lax.erf(gate * (1.0 / math.sqrt(2.0))) + 0.5
                act = gate * cdf
                slope = cdf + gate * (jnp.exp(gate * gate * -0.5) * (1.0 / math.sqrt(2.0 * math.pi)))
                tile_ref[s, 0, rs, :] = act.astype(BF)
                tile_ref[s, 1, rs, :] = (lift * slope).astype(BF)
                hidden = (act * lift).astype(BF)
                tile_ref[s, 2, rs, :] = hidden
                acc_ref[rs, :] += dot(hidden, down_ref[s], NT)

            @pl.when(i + 2 < 2 * tiles)
            def _():
                start_f(i + 2)

            for item in write_tiles(i, s):
                item.start()

        for rs in halves(rows):
            u, rstd = normalize(normed_ref[rs, :] + acc_ref[rs, :] + vec[3:4])
            row_ref[1, rs, :] = u.astype(BF)
            stat_ref[1, rs, :] = jnp.broadcast_to(rstd, (rows // 2, 128))
            row_ref[2, rs, :] = (u * vec[4:5] + vec[5:6]).astype(BF)
        ends = [(row_ref.at[1], u2_out.at[slot]), (stat_ref.at[1], r2_out.at[slot]), (row_ref.at[2], y_out)]
        for index, (src, dst) in enumerate(ends):
            copy(src, dst, r_sem.at[3 + index]).start()
        for index, (src, dst) in enumerate(
            [(low_ref, n_out.at[slot]), (row_ref.at[0], u1_out.at[slot]), (stat_ref.at[0], r1_out.at[slot])] + ends
        ):
            copy(src, dst, r_sem.at[index]).wait()
        copy(mixed_ref, mixed_out.at[slot], m_sem).wait()
        for i in (2 * heads_steps - 2, 2 * heads_steps - 1):
            for item in write_qkv(jnp.int32(i), i % 2):
                item.wait()
        for i in (2 * tiles - 2, 2 * tiles - 1):
            for item in write_tiles(jnp.int32(i), i % 2):
                item.wait()

    sem = pltpu.SemaphoreType.DMA
    return call(
        kernel,
        [x, *weights, (bias, WHOLE), (slopes, SMEM), (vecs, WHOLE), (up_bias, WHOLE)],
        [((slots, rows, total), BF, True)] * 4
        + [((slots, 2 * heads_steps, 8, rows), F32, True)]
        + [((slots, rows, 2 * units), BF, True)] * 3
        + [((slots, rows, width), BF, True)] * 3
        + [((slots, rows, 128), F32, True)] * 2
        + [((rows, width), BF, False)],
        [
            pltpu.VMEM((rows, width), BF),
            pltpu.VMEM((2, 3, width, CW), BF),
            pltpu.VMEM((total, width), BF),
            pltpu.VMEM((2, 2, width, ft), BF),
            pltpu.VMEM((2, width, ft), BF),
            pltpu.VMEM((2, 3, rows, CW), BF),
            pltpu.VMEM((2, 8, rows), F32),
            pltpu.VMEM((rows, total), BF),
            pltpu.VMEM((rows, rows), F32),
            pltpu.VMEM((rows, width), F32),
            pltpu.VMEM((rows, width), F32),
            pltpu.VMEM((rows, width), BF),
            pltpu.VMEM((2, 3, rows, ft), BF),
            pltpu.VMEM((3, rows, width), BF),
            pltpu.VMEM((2, rows, 128), F32),
            sem, sem((2,)), sem, sem((2, 2)), sem((2, 4)), sem, sem((2, 3)), sem((6,)),
        ],
        meta,
        chain,
        deps,
        "layer_forward",
        2 * rows * width * (4 * total + 6 * units) + 4 * rows * rows * total,
        54 << 20,
    )


def layer_backward(grad, kept, weights, slopes, vecs, meta, chain, deps, slots):
    qkv_own, qkv_oth, o_own, o_oth, up_own, up_oth, down_own, down_oth = weights
    q, k, v, _, lse, act, slope, _, _, u1, u2, r1, r2 = kept
    rows, width = grad.shape
    local = qkv_own.shape[2]
    units = up_own.shape[2]
    heads_steps = local // CW
    ft = min(512, units)
    tiles = units // ft
    total = 2 * local

    def norm_back(grad_z, u, rstd, gain):
        t = grad_z * gain
        return rstd * (t - jnp.mean(t, axis=1, keepdims=True) - u * jnp.mean(t * u, axis=1, keepdims=True))

    def row_sum(values):
        return jnp.sum(values, axis=0, keepdims=True)

    def kernel(meta_ref, ins, outs, scratch):
        (g_hbm, q_hbm, k_hbm, v_hbm, lse_hbm, a_hbm, b_hbm, u1_hbm, u2_hbm, r1_hbm, r2_hbm,
         qkv_own_ref, qkv_oth_ref, o_own_ref, o_oth_ref, up_own_ref, up_oth_ref, down_own_ref, down_oth_ref,
         slope_ref, vec_ref) = ins
        gg0_out, gg1_out, gl_out, ga_out, gq_out, gk_out, gv_out, gx_out, gxl_out, sums_out, ub_out, qv_out = outs
        (g_ref, u_ref, r_ref, up_ref, down_ref, ab_ref, gg_ref, low_ref, acc_ref, sums_ref, ub_ref, qv_ref,
         w_ref, o_ref, qkv_ref, lse_ref, gm_ref, dist_ref, gqkv_ref,
         g_sem, f_sem, t_sem, w_sem, q_sem, r_sem) = scratch
        slot = meta_ref[0]

        def start_f(i):
            s = lax.rem(i, 2)
            pick(i, tiles, (up_own_ref, down_own_ref), (up_oth_ref, down_oth_ref),
                 lambda ref, j: [(ref[0].at[:, :, block(j, ft)], up_ref.at[s], f_sem.at[s, 0]),
                                 (ref[1].at[:, block(j, ft)], down_ref.at[s], f_sem.at[s, 1])])
            for c, ref in enumerate((a_hbm, b_hbm)):
                copy(ref.at[slot, :, block(i, ft)], ab_ref.at[s, c], f_sem.at[s, 2 + c]).start()

        def start_w(i):
            s = lax.rem(i, 2)
            pick(i, heads_steps, (qkv_own_ref, o_own_ref), (qkv_oth_ref, o_oth_ref),
                 lambda ref, j: [(ref[0].at[:, :, block(j, CW)], w_ref.at[s], w_sem.at[s, 0]),
                                 (ref[1].at[block(j, CW)], o_ref.at[s], w_sem.at[s, 1])])
            for c, ref in enumerate((q_hbm, k_hbm, v_hbm)):
                copy(ref.at[slot, :, block(i, CW)], qkv_ref.at[s, c], w_sem.at[s, 2 + c]).start()
            copy(lse_hbm.at[slot, i], lse_ref.at[s], w_sem.at[s, 5]).start()

        firsts = [(g_hbm, g_ref), (u2_hbm.at[slot], u_ref.at[1]), (r2_hbm.at[slot], r_ref.at[1]),
                  (u1_hbm.at[slot], u_ref.at[0]), (r1_hbm.at[slot], r_ref.at[0])]
        for index, (src, dst) in enumerate(firsts):
            copy(src, dst, g_sem.at[index]).start()
            if index == 2:
                start_f(jnp.int32(0))
                start_f(jnp.int32(1))
        start_w(jnp.int32(0))
        start_w(jnp.int32(1))
        vec = vec_ref[...]
        fill_distance(dist_ref, meta_ref[2])
        for index, (src, dst) in enumerate(firsts[:3]):
            copy(src, dst, g_sem.at[index]).wait()
        sums = [jnp.zeros((1, width), F32)] * 3
        for rs in halves(rows):
            places = lax.broadcasted_iota(jnp.int32, (rows // 2, width), 0) + rs.start
            grad_y = jnp.where(places < meta_ref[3], g_ref[rs, :].astype(F32), 0.0)
            u = u_ref[1, rs, :].astype(F32)
            grad_c = norm_back(grad_y, u, r_ref[1, rs, 0:1], vec[4:5])
            acc_ref[rs, :] = grad_c
            low_ref[0, rs, :] = grad_c.astype(BF)
            for index, values in enumerate((grad_y * u, grad_y, grad_c)):
                sums[index] += row_sum(values)
        for index in range(3):
            sums_ref[index : index + 1, :] = sums[index]
        copy(low_ref.at[0], gl_out.at[slot], r_sem.at[0]).start()

        def write_tiles(i, s):
            return [copy(gg_ref.at[s, c], out.at[slot, :, block(i, ft)], t_sem.at[s, c])
                    for c, out in enumerate((gg0_out, gg1_out))]

        @pl.loop(0, 2 * tiles)
        def _(i):
            s = lax.rem(i, 2)
            arrived(up_ref.at[s], f_sem.at[s, 0])
            arrived(down_ref.at[s], f_sem.at[s, 1])
            for c in range(2):
                arrived(ab_ref.at[s, c], f_sem.at[s, 2 + c])

            @pl.when(i >= 2)
            def _():
                for item in write_tiles(i - 2, s):
                    item.wait()

            s0 = jnp.zeros((1, ft), F32)
            s1 = jnp.zeros((1, ft), F32)
            for rs in halves(rows):
                gh = dot(low_ref[0, rs, :], down_ref[s])
                g0 = (gh * ab_ref[s, 1, rs, :].astype(F32)).astype(BF)
                g1 = (gh * ab_ref[s, 0, rs, :].astype(F32)).astype(BF)
                gg_ref[s, 0, rs, :] = g0
                gg_ref[s, 1, rs, :] = g1
                s0 += row_sum(g0.astype(F32))
                s1 += row_sum(g1.astype(F32))
                acc_ref[rs, :] += dot(g0, up_ref[s, 0], NT) + dot(g1, up_ref[s, 1], NT)
            ub_ref[0:1, block(i, ft)] = s0
            ub_ref[1:2, block(i, ft)] = s1

            @pl.when(i + 2 < 2 * tiles)
            def _():
                start_f(i + 2)

            for item in write_tiles(i, s):
                item.start()

        for index, (src, dst) in enumerate(firsts[3:]):
            copy(src, dst, g_sem.at[3 + index]).wait()
        sums = [jnp.zeros((1, width), F32)] * 3
        for rs in halves(rows):
            grad_n = acc_ref[rs, :]
            u = u_ref[0, rs, :].astype(F32)
            grad_a = norm_back(grad_n, u, r_ref[0, rs, 0:1], vec[1:2])
            low_ref[1, rs, :] = grad_a.astype(BF)
            acc_ref[rs, :] = grad_a
            for index, values in enumerate((grad_n * u, grad_n, grad_a)):
                sums[index] += row_sum(values)
        for index in range(3):
            sums_ref[3 + index : 4 + index, :] = sums[index]
        sums_ref[6:8, :] = jnp.zeros((2, width), F32)
        copy(low_ref.at[1], ga_out.at[slot], r_sem.at[1]).start()
        scale = BF(1.0 / math.sqrt(HD))

        def write_heads(i, s):
            return [copy(gqkv_ref.at[s, c], out.at[slot, :, block(i, CW)], q_sem.at[s, c])
                    for c, out in enumerate((gq_out, gk_out, gv_out))]

        @pl.loop(0, 2 * heads_steps)
        def _(i):
            s = lax.rem(i, 2)
            for index, ref in enumerate((w_ref.at[s], o_ref.at[s], qkv_ref.at[s, 0], qkv_ref.at[s, 1], qkv_ref.at[s, 2], lse_ref.at[s])):
                arrived(ref, w_sem.at[s, index])

            @pl.when(i >= 2)
            def _():
                for item in write_heads(i - 2, s):
                    item.wait()

            gm_ref[...] = dot(low_ref[1], o_ref[s], NT).astype(BF)
            parts = [[], [], []]
            for head in range(PER):
                cols = slice(head * HD, (head + 1) * HD)
                query = qkv_ref[s, 0, :, cols] * scale
                key = qkv_ref[s, 1, :, cols]
                gm = gm_ref[:, cols]
                scores = dot(key, query, NT)
                scores = scores - dist_ref[...] * slope_ref[i * PER + head]
                likely = jnp.exp(scores - lse_ref[s, head : head + 1, :])
                parts[2].append(dot(likely.astype(BF), gm).astype(BF))
                t = likely * dot(qkv_ref[s, 2, :, cols], gm, NT)
                inner = jnp.sum(t, axis=0, keepdims=True)
                gs = (t - likely * inner).astype(BF)
                parts[1].append(dot(gs, query).astype(BF))
                parts[0].append(dot(gs, key * scale, TN).astype(BF))
            for c in range(3):
                gqkv_ref[s, c] = jnp.concatenate(parts[c], axis=1)
            for index, c in enumerate((0, 2)):
                qv_ref[index : index + 1, block(i, CW)] = row_sum(gqkv_ref[s, c].astype(F32))
            acc_ref[...] += (
                dot(gqkv_ref[s, 0], w_ref[s, 0], NT)
                + dot(gqkv_ref[s, 1], w_ref[s, 1], NT)
                + dot(gqkv_ref[s, 2], w_ref[s, 2], NT)
            )

            @pl.when(i + 2 < 2 * heads_steps)
            def _():
                start_w(i + 2)

            for item in write_heads(i, s):
                item.start()

        g_ref[...] = acc_ref[...].astype(BF)
        ends = [(g_ref, gxl_out), (acc_ref, gx_out), (sums_ref, sums_out), (ub_ref, ub_out), (qv_ref, qv_out)]
        for index, (src, dst) in enumerate(ends):
            copy(src, dst, r_sem.at[2 + index]).start()
        for index, (src, dst) in enumerate([(low_ref.at[0], gl_out.at[slot]), (low_ref.at[1], ga_out.at[slot])] + ends):
            copy(src, dst, r_sem.at[index]).wait()
        for i in (2 * tiles - 2, 2 * tiles - 1):
            for item in write_tiles(jnp.int32(i), i % 2):
                item.wait()
        for i in (2 * heads_steps - 2, 2 * heads_steps - 1):
            for item in write_heads(jnp.int32(i), i % 2):
                item.wait()

    sem = pltpu.SemaphoreType.DMA
    return call(
        kernel,
        [grad, q, k, v, lse, act, slope, u1, u2, r1, r2, *weights, (slopes, SMEM), (vecs, WHOLE)],
        [((slots, rows, 2 * units), BF, True)] * 2
        + [((slots, rows, width), BF, True)] * 2
        + [((slots, rows, total), BF, True)] * 3
        + [
            ((rows, width), F32, False),
            ((rows, width), BF, False),
            ((8, width), F32, False),
            ((2, 2 * units), F32, False),
            ((2, total), F32, False),
        ],
        [
            pltpu.VMEM((rows, width), BF),
            pltpu.VMEM((2, rows, width), BF),
            pltpu.VMEM((2, rows, 128), F32),
            pltpu.VMEM((2, 2, width, ft), BF),
            pltpu.VMEM((2, width, ft), BF),
            pltpu.VMEM((2, 2, rows, ft), BF),
            pltpu.VMEM((2, 2, rows, ft), BF),
            pltpu.VMEM((2, rows, width), BF),
            pltpu.VMEM((rows, width), F32),
            pltpu.VMEM((8, width), F32),
            pltpu.VMEM((2, 2 * units), F32),
            pltpu.VMEM((2, total), F32),
            pltpu.VMEM((2, 3, width, CW), BF),
            pltpu.VMEM((2, CW, width), BF),
            pltpu.VMEM((2, 3, rows, CW), BF),
            pltpu.VMEM((2, 8, rows), F32),
            pltpu.VMEM((rows, CW), BF),
            pltpu.VMEM((rows, rows), F32),
            pltpu.VMEM((2, 3, rows, CW), BF),
            sem((5,)), sem((2, 4)), sem((2, 2)), sem((2, 6)), sem((2, 3)), sem((7,)),
        ],
        meta,
        chain,
        deps,
        "layer_backward",
        2 * rows * width * (4 * total + 6 * units) + 10 * rows * rows * total,
        70 << 20,
    )


MESH = pl.DeviceIdType.MESH
CORE_LAG = 3
CROSS_LAG = 3
CHAIN_LAG = 2


def neighbours():
    t = lax.axis_index("tensor")
    d = lax.axis_index("dp")
    last = lax.axis_size("dp") // 2 - 1
    c = lax.rem(d, 2)
    z = d // 2
    return t, c, z, last, {"dp": d + 1 - 2 * c}, {"tensor": 1 - t}, {"dp": d + 2}, {"dp": d - 2}


def greet(c, z, chips, core, cross):
    barrier = pltpu.get_barrier_semaphore()
    pl.semaphore_signal(barrier, inc=1, device_id=core, device_id_type=MESH)
    pl.semaphore_signal(barrier, inc=1, device_id=cross, device_id_type=MESH)
    for shift in range(1, chips):
        chip = lax.rem(z + shift, chips)
        pl.semaphore_signal(barrier, inc=1, device_id={"dp": chip * 2 + c}, device_id_type=MESH)
    pl.semaphore_wait(barrier, 1 + chips)


def fetch_other_half(qkv, out, up, down, qv_bias, up_bias, inputs, cotangent, chips):
    weights = [qkv, out, up, down]
    biases = [qv_bias, up_bias]
    bias_widths = [b.shape[1] for b in biases]
    seqs = inputs.shape[0] // 2
    shard_rows, width = inputs.shape[1:]
    groups = 2 * chips

    def rows_of(item):
        return weights[item].shape[0]

    plan = []
    up_piece = rows_of(2) // groups
    parts = 4
    for part in range(parts):
        plan.append((2, True, 0, up_piece, part * up_piece // parts, up_piece // parts))
    spread = rows_of(3) * 3 // 4
    down_piece = spread // groups
    for part in range(3):
        plan.append((3, True, 0, down_piece, part * down_piece // 3, down_piece // 3))
    n_spread = len(plan)
    plan.append((-1, False, 0, 0, 0, 0))
    plan.append((-2, False, 0, 0, 0, 0))
    plan.append((-2, False, 0, 0, 0, 1))
    for part in range(3):
        size = rows_of(0) // 6
        plan.append((0, False, 0, rows_of(0) // 2, part * size, size))
    plan.append((1, False, 0, rows_of(1) // 2, 0, rows_of(1) // 2))
    plan.append((-1, False, 0, 0, 0, 1))
    direct = (rows_of(3) - spread) // 2
    for part in range(2):
        plan.append((3, False, spread, direct, part * direct // 2, direct // 2))
    n = len(plan)

    def kernel(*refs):
        ins, bias_ins, held_refs = refs[:4], refs[4:6], refs[6:8]
        outs, bias_outs, row_refs = refs[8:12], refs[12:14], refs[14 : 14 + seqs]
        stage, x_send, x_recv, c_send, c_recv, u_send, u_recv, d_send, d_recv, l_sem, b_sem = refs[14 + seqs :]
        t, c, z, last, core, cross, above, below = neighbours()
        section = lax.axis_index("section")
        greet(c, z, chips, core, cross)

        def rows(index, chip, on):
            item, is_spread, base, piece, offset, size = plan[index]
            place = chip * 2 + on if is_spread else on
            return item, pl.ds(pl.multiple_of(base + place * piece + offset, size), size)

        def span(part):
            return block(part, shard_rows)

        def bias_part(m, side):
            return bias_outs[m].at[:, pl.ds(side * bias_widths[m], bias_widths[m])]

        def cross_copy(index, held_ref=None):
            m = plan[index][5]
            if plan[index][0] == -1:
                src = (held_refs[0] if held_ref is None else held_ref).at[(1 - t) * seqs + m]
                dst = row_refs[m].at[span(t)]
            elif plan[index][0] == -2:
                src, dst = bias_ins[m], bias_part(m, 1)
            else:
                item, where = rows(index, z, c)
                src, dst = ins[item].at[where], outs[item].at[where]
            return pltpu.make_async_remote_copy(
                src_ref=src, dst_ref=dst, send_sem=x_send.at[index], recv_sem=x_recv.at[index],
                device_id=cross, device_id_type=MESH,
            )

        def pass_on(index, chip, send, recv, device):
            item, where = rows(index, chip, c)
            place = outs[item].at[where]
            return pltpu.make_async_remote_copy(
                src_ref=place, dst_ref=place, send_sem=send.at[index, chip], recv_sem=recv.at[index, chip],
                device_id=device, device_id_type=MESH,
            )

        def got(index, chip, on, sem):
            item, where = rows(index, chip, on)
            arrived(outs[item].at[where], sem)

        for m in range(2):
            copy(bias_ins[m], bias_part(m, 0), b_sem.at[m]).start()
        for index in range(n):
            if plan[index][0] == -1:
                for turn in range(2):
                    @pl.when(section == turn)
                    def _(index=index, turn=turn):
                        cross_copy(index, held_refs[turn]).start()
            else:
                cross_copy(index).start()
        for turn in range(2):
            @pl.when(section == turn)
            def _(turn=turn):
                copy(held_refs[turn].at[pl.ds(t * seqs, seqs)], stage, l_sem).start()

        arrived(stage, l_sem)
        for m in range(seqs):
            copy(stage.at[m], row_refs[m].at[span(t)], l_sem).start()

        def handle(index, hop):
            if hop == 0:
                m = plan[index][5]
                if plan[index][0] == -1:
                    arrived(row_refs[m].at[span(1 - t)], x_recv.at[index])
                    return
                if plan[index][0] == -2:
                    arrived(bias_part(m, 1), x_recv.at[index])
                    return
                got(index, z, c, x_recv.at[index])
                pass_on(index, z, c_send, c_recv, core).start()
                if plan[index][1]:
                    @pl.when(z < last)
                    def _():
                        pass_on(index, z, u_send, u_recv, above).start()

                    @pl.when(z > 0)
                    def _():
                        pass_on(index, z, d_send, d_recv, below).start()
                return

            @pl.when(z - hop >= 0)
            def _():
                got(index, z - hop, c, u_recv.at[index, z - hop])

                @pl.when(z < last)
                def _():
                    pass_on(index, z - hop, u_send, u_recv, above).start()

                pass_on(index, z - hop, c_send, c_recv, core).start()

            @pl.when(z + hop <= last)
            def _():
                got(index, z + hop, c, d_recv.at[index, z + hop])

                @pl.when(z > 0)
                def _():
                    pass_on(index, z + hop, d_send, d_recv, below).start()

                pass_on(index, z + hop, c_send, c_recv, core).start()

        for round_ in range(max(n, n_spread + chips - 1)):
            if round_ < n:
                handle(round_, 0)
            for hop in range(1, chips):
                if 0 <= round_ - hop < n_spread:
                    handle(round_ - hop, hop)

        for m in range(2):
            copy(bias_ins[m], bias_part(m, 0), b_sem.at[m]).wait()
        for m in range(seqs):
            arrived(stage.at[m], l_sem)
        for index in range(n):
            item, is_spread = plan[index][:2]
            cross_copy(index).wait_send()
            if item < 0:
                continue
            if not is_spread:
                got(index, z, 1 - c, c_recv.at[index, z])
                pass_on(index, z, c_send, c_recv, core).wait_send()
                continue
            for chip in range(chips):
                got(index, chip, 1 - c, c_recv.at[index, chip])
                pass_on(index, chip, c_send, c_recv, core).wait_send()

                @pl.when((chip <= z) & (z < last))
                def _(chip=chip):
                    pass_on(index, chip, u_send, u_recv, above).wait_send()

                @pl.when((chip >= z) & (z > 0))
                def _(chip=chip):
                    pass_on(index, chip, d_send, d_recv, below).wait_send()

    sem = pltpu.SemaphoreType.DMA
    moved = sum(w.size for w in weights) * 2
    return pl.pallas_call(
        kernel,
        in_specs=[ANY] * 8,
        out_specs=[ANY] * (6 + seqs),
        out_shape=[jax.ShapeDtypeStruct(w.shape, BF) for w in weights]
        + [jax.ShapeDtypeStruct((2, 2 * size), BF) for size in bias_widths]
        + [jax.ShapeDtypeStruct((2 * shard_rows, width), BF)] * seqs,
        scratch_shapes=[pltpu.VMEM((seqs, shard_rows, width), BF)]
        + [sem((n,)), sem((n,))]
        + [sem((n, chips))] * 6
        + [sem, sem((2,))],
        compiler_params=pltpu.CompilerParams(collective_id=1, has_side_effects=True),
        cost_estimate=pl.CostEstimate(flops=0, bytes_accessed=2 * moved, transcendentals=0),
        name="fetch_other_half",
    )(*weights, *biases, inputs, cotangent)


def weight_grads_reduced(groups, sums, row_grads, chips):
    seqs = 2
    rows, depth = groups[0][0].shape[1:]
    lefts = [g[0] for g in groups]
    rights = [r for g in groups for r in g[1]]
    bt = 128
    half = depth // 2
    quarter = half // 2
    blocks = [r.shape[2] // (2 * bt) for r in rights]
    starts = [sum(blocks[:index]) for index in range(len(rights))]
    total = sum(blocks)
    group_starts = []
    index = 0
    for _, members in groups:
        group_starts.append(starts[index])
        index += len(members)
    n_left, n_right = len(lefts), len(rights)
    homes = [(g, index) for g, (_, members) in enumerate(groups) for index in range(len(members))]
    tiles, mines, gives = 4, CORE_LAG + 1, 4
    last_static = chips - 1
    drain = CORE_LAG + CROSS_LAG + 2 * last_static * CHAIN_LAG + 1
    vec_shape = sums.shape
    n_in = n_left + n_right + 1 + seqs
    shard_rows = rows // 2

    def kernel(*refs):
        left_refs = refs[:n_left]
        right_refs = refs[n_left : n_left + n_right]
        sums_ref = refs[n_left + n_right]
        row_refs = refs[n_left + n_right + 1 : n_in]
        outs = refs[n_in : n_in + n_left]
        sums_out, rows_out = refs[n_in + n_left : n_in + n_left + 2]
        (
            acc, from_x, from_z, final, flip, stage, tile, mine, give, vec, vec_in, vec_all,
            tile_sem, stage_sem, give_send, core_recv, x_send, x_recv, z_send, z_recv, f_send, f_recv,
            store_sem, out_send, out_recv, v_load, v_send, v_recv, r_send, r_recv,
        ) = refs[n_in + n_left + 2 :]
        t, c, z, last, core, cross, above, below = neighbours()
        section = lax.axis_index("section")
        greet(c, z, chips, core, cross)

        def remote(src, dst, send, recv, device):
            return pltpu.make_async_remote_copy(
                src_ref=src, dst_ref=dst, send_sem=send, recv_sem=recv, device_id=device, device_id_type=MESH
            )

        def valid(k):
            return (k >= 0) & (k < total)

        def member(k, visit):
            for m in range(n_right):
                @pl.when((k >= starts[m]) & (k < starts[m] + blocks[m]))
                def _(m=m):
                    visit(m, k - starts[m])

        def load_tile(k):
            slot = lax.rem(k, tiles)

            def visit(m, j):
                for side in range(2):
                    at = pl.multiple_of((side * blocks[m] + j) * bt, bt)
                    pltpu.make_async_copy(
                        right_refs[m].at[pl.ds(0, seqs), :, pl.ds(at, bt)],
                        tile.at[slot, :, :, pl.ds(side * bt, bt)],
                        tile_sem.at[slot],
                    ).start()

            member(k, visit)

        def load_left(g):
            return pltpu.make_async_copy(left_refs[g].at[pl.ds(0, seqs)], stage, stage_sem)

        vec_load = pltpu.make_async_copy(sums_ref, vec.at[0], v_load)
        vec_load.start()
        load_left(0).start()
        for k in range(tiles - 1):
            load_tile(jnp.int32(k))
        vec_load.wait()
        vec_core = remote(vec.at[0], vec_in.at[0], v_send.at[0], v_recv.at[0], core)
        vec_cross = remote(vec.at[1], vec_in.at[1], v_send.at[1], v_recv.at[1], cross)
        vec_core.start()
        def row_copy(m):
            source = row_refs[m].at[block(1 - t, shard_rows)]
            return remote(source, rows_out.at[m], r_send.at[m], r_recv.at[m], cross)

        up = pl.ds(0, quarter)
        down = pl.ds(quarter, quarter)
        sides = ((up, 0, z, above, below), (down, 1, last - z, below, above))

        @pl.loop(0, total + drain)
        def _(s):
            @pl.when(valid(s))
            def _():
                for g in range(n_left):
                    @pl.when(s == group_starts[g])
                    def _(g=g):
                        load_left(g).wait()
                        for m in range(seqs):
                            flip[:, m * rows : (m + 1) * rows] = stage[m].T
                        if g + 1 < n_left:
                            load_left(g + 1).start()

                slot = lax.rem(s, tiles)
                arrived(tile.at[slot], tile_sem.at[slot])
                give_slot = lax.rem(s, gives)

                @pl.when(s >= gives)
                def _():
                    arrived(give.at[give_slot], give_send.at[give_slot])

                for place, ring, at in ((1 - c, give, give_slot), (c, mine, lax.rem(s, mines))):
                    here = pl.ds(pl.multiple_of(place * half, half), half)
                    block = dot(flip[here, :rows], tile[slot, 0])
                    for m in range(1, seqs):
                        block += dot(flip[here, m * rows : (m + 1) * rows], tile[slot, m])
                    ring[at, 1] = block[:, :bt].astype(BF)
                    ring[at, 0] = block[:, bt:].astype(BF)

            @pl.when(s + tiles - 1 < total)
            def _():
                load_tile(s + tiles - 1)

            k1 = s - CORE_LAG

            @pl.when(valid(k1))
            def _():
                arrived(acc.at[k1], core_recv.at[k1])
                at = lax.rem(k1, mines)
                for side in range(2):
                    acc[k1, side] = (acc[k1, side].astype(F32) + mine[at, side].astype(F32)).astype(BF)

            k2 = k1 - CROSS_LAG

            @pl.when(valid(k2))
            def _():
                arrived(from_x.at[k2], x_recv.at[k2])
                acc[k2, 1] = (acc[k2, 1].astype(F32) + from_x[k2].astype(F32)).astype(BF)

            for span, way, place, ahead, behind in sides:
                k3 = k2 - CHAIN_LAG * place

                @pl.when(valid(k3) & (place > 0))
                def _(span=span, way=way, k3=k3):
                    arrived(from_z.at[k3, span], z_recv.at[way, k3])
                    acc[k3, 1, span] = (acc[k3, 1, span].astype(F32) + from_z[k3, span].astype(F32)).astype(BF)

                k4 = k2 - CHAIN_LAG * (2 * last - place)

                @pl.when(valid(k4) & (place == last))
                def _(span=span, k4=k4):
                    final[k4, span] = acc[k4, 1, span]

                @pl.when(valid(k4) & (place < last))
                def _(span=span, way=way, k4=k4):
                    arrived(final.at[k4, span], f_recv.at[way, k4])

            @pl.when(valid(s))
            def _():
                at = lax.rem(s, gives)
                remote(give.at[at], acc.at[s], give_send.at[at], core_recv.at[s], core).start()

            @pl.when(valid(k1))
            def _():
                remote(acc.at[k1, 0], from_x.at[k1], x_send, x_recv.at[k1], cross).start()

            @pl.when((k1 == total - 1) & (section == 0))
            def _():
                for m in range(seqs):
                    row_copy(m).start()

            for span, way, place, ahead, behind in sides:
                k3 = k2 - CHAIN_LAG * place

                @pl.when(valid(k3) & (place < last))
                def _(span=span, way=way, k3=k3, ahead=ahead):
                    remote(acc.at[k3, 1, span], from_z.at[k3, span], z_send.at[way], z_recv.at[way, k3], ahead).start()

                k4 = k2 - CHAIN_LAG * (2 * last - place)

                @pl.when(valid(k4) & (place > 0))
                def _(span=span, way=way, k4=k4, behind=behind):
                    remote(final.at[k4, span], final.at[k4, span], f_send.at[way], f_recv.at[way, k4], behind).start()

            k5 = k2 - CHAIN_LAG * 2 * last

            @pl.when(valid(k5))
            def _():
                def visit(m, j):
                    dst = outs[homes[m][0]].at[
                        homes[m][1], pl.ds(pl.multiple_of(c * half, half), half), pl.ds(pl.multiple_of(j * bt, bt), bt)
                    ]
                    pltpu.make_async_copy(final.at[k5], dst, store_sem).start()
                    remote(final.at[k5], dst, out_send, out_recv, core).start()

                member(k5, visit)

            @pl.when(s == 4)
            def _():
                vec_core.wait_recv()
                vec[1] = vec[0] + vec_in[0]

            @pl.when(s == 5)
            def _():
                vec_cross.start()

            @pl.when(s == 10)
            def _():
                vec_cross.wait_recv()
                vec_all[z] = vec[1] + vec_in[1]

            @pl.when(s == 11)
            def _():
                for shift in range(1, chips):
                    to = lax.rem(z + shift, chips)
                    remote(
                        vec_all.at[z], vec_all.at[z], v_send.at[1 + shift], v_recv.at[1 + shift], {"dp": to * 2 + c}
                    ).start()


        @pl.when(section == 0)
        def _():
            for m in range(seqs):
                row_copy(m).wait()

        vec_core.wait_send()
        vec_cross.wait_send()
        for shift in range(1, chips):
            origin = lax.rem(z + chips - shift, chips)
            arrived(vec_all.at[origin], v_recv.at[1 + shift])
            arrived(vec_all.at[z], v_send.at[1 + shift])
        whole = vec_all[0]
        for chip in range(1, chips):
            whole += vec_all[chip]
        sums_out[...] = whole
        for at in range(gives):
            arrived(give.at[at], give_send.at[at])
        arrived(acc.at[:, 0], x_send)
        for span, way, place, ahead, behind in sides:
            @pl.when(place < last)
            def _(span=span, way=way):
                arrived(from_z.at[:, span], z_send.at[way])

            @pl.when(place > 0)
            def _(span=span, way=way):
                arrived(final.at[:, span], f_send.at[way])

        arrived(final, out_send)
        arrived(final, store_sem)
        arrived(final, out_recv)

    sem = pltpu.SemaphoreType.DMA
    flops = 2 * seqs * rows * depth * 2 * bt * total
    return pl.pallas_call(
        kernel,
        in_specs=[ANY] * n_in,
        out_specs=[ANY] * n_left + [WHOLE, ANY],
        out_shape=[jax.ShapeDtypeStruct((len(g[1]), depth, g[1][0].shape[2] // 2), BF) for g in groups]
        + [jax.ShapeDtypeStruct(vec_shape, F32), jax.ShapeDtypeStruct((seqs, shard_rows, depth), BF)],
        scratch_shapes=[
            pltpu.VMEM((total, 2, half, bt), BF),
            pltpu.VMEM((total, half, bt), BF),
            pltpu.VMEM((total, half, bt), BF),
            pltpu.VMEM((total, half, bt), BF),
            pltpu.VMEM((depth, seqs * rows), BF),
            pltpu.VMEM((seqs, rows, depth), BF),
            pltpu.VMEM((tiles, seqs, rows, 2 * bt), BF),
            pltpu.VMEM((mines, 2, half, bt), BF),
            pltpu.VMEM((gives, 2, half, bt), BF),
            pltpu.VMEM((2,) + vec_shape, F32),
            pltpu.VMEM((2,) + vec_shape, F32),
            pltpu.VMEM((chips,) + vec_shape, F32),
            sem((tiles,)), sem, sem((gives,)), sem((total,)), sem, sem((total,)),
            sem((2,)), sem((2, total)), sem((2,)), sem((2, total)),
            sem, sem, sem, sem, sem((chips + 1,)), sem((chips + 1,)), sem((seqs,)), sem((seqs,)),
        ],
        compiler_params=pltpu.CompilerParams(
            collective_id=0, has_side_effects=True, vmem_limit_bytes=VMEM_LIMIT
        ),
        cost_estimate=pl.CostEstimate(flops=flops, bytes_accessed=64 << 20, transcendentals=0),
        name="weight_grads_reduced",
    )(*lefts, *rights, sums, *row_grads)


def exchange_rows(first, second, grads):
    seqs = len(first)
    rows, width = first[0].shape
    shard_rows = rows // 2

    def kernel(*refs):
        outputs = (refs[:seqs], refs[seqs : 2 * seqs])
        grad_refs = refs[2 * seqs : 3 * seqs]
        out_ref, got_ref, stage, send, recv, l_sem = refs[3 * seqs :]
        t = lax.axis_index("tensor")
        section = lax.axis_index("section")
        cross = {"tensor": 1 - t}
        barrier = pltpu.get_barrier_semaphore()
        pl.semaphore_signal(barrier, inc=1, device_id=cross, device_id_type=MESH)
        pl.semaphore_wait(barrier, 1)

        def remote(src, dst, index):
            return pltpu.make_async_remote_copy(
                src_ref=src, dst_ref=dst, send_sem=send.at[index], recv_sem=recv.at[index],
                device_id=cross, device_id_type=MESH,
            )

        for turn in range(2):
            @pl.when(section == turn)
            def _(turn=turn):
                sent = [
                    remote(outputs[turn][m].at[block(1 - t, shard_rows)], out_ref.at[t * seqs + m], m) for m in range(seqs)
                ]
                if turn == 1:
                    sent += [
                        remote(grad_refs[m].at[block(1 - t, shard_rows)], got_ref.at[m], seqs + m) for m in range(seqs)
                    ]
                for item in sent:
                    item.start()
                for m in range(seqs):
                    copy(outputs[turn][m].at[block(t, shard_rows)], stage.at[m], l_sem.at[m]).start()
                for m in range(seqs):
                    arrived(stage.at[m], l_sem.at[m])
                    copy(stage.at[m], out_ref.at[t * seqs + m], l_sem.at[m]).start()
                for m in range(seqs):
                    arrived(stage.at[m], l_sem.at[m])
                for m in range(seqs):
                    arrived(out_ref.at[(1 - t) * seqs + m], recv.at[m])
                    arrived(stage.at[m], send.at[m])
                if turn == 1:
                    for m in range(seqs):
                        sent[seqs + m].wait()

    sem = pltpu.SemaphoreType.DMA
    return pl.pallas_call(
        kernel,
        in_specs=[ANY] * (3 * seqs),
        out_specs=[ANY] * 2,
        out_shape=[
            jax.ShapeDtypeStruct((2 * seqs, shard_rows, width), BF),
            jax.ShapeDtypeStruct((seqs, shard_rows, width), BF),
        ],
        scratch_shapes=[
            pltpu.VMEM((seqs, shard_rows, width), BF), sem((2 * seqs,)), sem((2 * seqs,)), sem((seqs,)),
        ],
        compiler_params=pltpu.CompilerParams(collective_id=2, has_side_effects=True),
        cost_estimate=pl.CostEstimate(flops=0, bytes_accessed=0, transcendentals=0),
        name="exchange_rows",
    )(*first, *second, *grads)


def widen(reduced, row_grads, gots, sums, units, local):
    seqs, shard_rows, width = gots[0].shape
    n = len(reduced)
    jobs = []
    for index, array in enumerate(reduced):
        lead, depth, columns = array.shape
        step = 512 * 1024 // columns
        if index == n - 1:
            jobs += [(index, 0, at, depth // 2, columns) for at in range(0, depth, depth // 2)]
        else:
            jobs += [(index, part, at, step, columns) for part in range(lead) for at in range(0, depth, step)]
    jobs += [(n, m, 0, shard_rows, width) for m in range(seqs)] + [(n + 1, m, 0, shard_rows, width) for m in range(seqs)]
    ring = 3
    n_in = n + 2 * seqs + 3
    parts = units // width

    def kernel(*refs):
        ins = refs[:n]
        grad_refs = refs[n : n + 2 * seqs]
        got_refs = refs[n + 2 * seqs : n + 2 * seqs + 2]
        sums_ref = refs[n + 2 * seqs + 2]
        outs = refs[n_in : n_in + n + 1]
        qv_ref, out_bias_ref, gain_ref, shift_ref, ub_ref, down_bias_ref = refs[n_in + n + 1 : n_in + n + 7]
        shapes = sorted({(j[3], j[4]) for j in jobs if j[0] != n})
        buffers = refs[n_in + n + 7 :]
        wide_rows, in_sem, out_sem = buffers[0], buffers[1], buffers[2]
        low = {s: buffers[3 + 2 * i] for i, s in enumerate(shapes)}
        wide = {s: buffers[4 + 2 * i] for i, s in enumerate(shapes)}
        t = lax.axis_index("tensor")
        section = lax.axis_index("section")

        def load(number):
            index, part, at, rows, columns = jobs[number]
            s = number % ring
            if index < n:
                copy(ins[index].at[part, pl.ds(at, rows)], low[rows, columns].at[s], in_sem.at[s]).start()
            elif index == n:
                for turn in range(2):
                    @pl.when(section == turn)
                    def _(turn=turn):
                        source = grad_refs[turn * seqs + part].at[block(t, shard_rows)]
                        copy(source, wide_rows.at[part], in_sem.at[s]).start()
            else:
                for turn in range(2):
                    @pl.when(section == turn)
                    def _(turn=turn):
                        copy(got_refs[turn].at[part], low[rows, columns].at[s], in_sem.at[s]).start()

        def store(number):
            index, part, at, rows, columns = jobs[number]
            s = number % ring
            if index < n - 1:
                return copy(wide[rows, columns].at[s], outs[index].at[part, pl.ds(at, rows)], out_sem.at[s])
            if index == n - 1:
                return copy(wide[rows, columns].at[s], outs[index].at[:, pl.ds(at, rows)], out_sem.at[s])
            if index == n:
                return copy(wide_rows.at[part], outs[n].at[t * seqs + part], out_sem.at[s])
            return copy(wide[rows, columns].at[s], outs[n].at[(1 - t) * seqs + part], out_sem.at[s])

        for number in range(ring):
            load(number)
        gain_ref[0:1] = sums_ref[3:4]
        gain_ref[1:2] = sums_ref[0:1]
        shift_ref[0:1] = sums_ref[4:5]
        shift_ref[1:2] = sums_ref[1:2]
        out_bias_ref[...] = sums_ref[5:6]
        down_bias_ref[...] = sums_ref[2:3]
        for half in range(2):
            @pl.when(t == half)
            def _(half=half):
                for g in range(2):
                    for j in range(parts):
                        at = 6 + (2 * g + half) * parts + j
                        ub_ref[g : g + 1, j * width : (j + 1) * width] = sums_ref[at : at + 1]
                    at = 6 + 4 * parts + g
                    qv_ref[g : g + 1] = sums_ref[at : at + 1, half * local : (half + 1) * local]

        for number, (index, part, at, rows, columns) in enumerate(jobs):
            s = number % ring
            if index == n:
                arrived(wide_rows.at[part], in_sem.at[s])
            else:
                arrived(low[rows, columns].at[s], in_sem.at[s])
            if number >= ring:
                store(number - ring).wait()
            if index == n - 1:
                wide[rows, columns][s] = low[rows, columns][s].astype(F32).T
            elif index != n:
                wide[rows, columns][s] = low[rows, columns][s].astype(F32)
            store(number).start()
            if number + ring < len(jobs):
                load(number + ring)
        for number in range(len(jobs) - ring, len(jobs)):
            store(number).wait()

    shapes = sorted({(j[3], j[4]) for j in jobs if j[0] != n})
    square = (reduced[-1].shape[1] // 2, reduced[-1].shape[2])
    last = reduced[-1].shape
    sem = pltpu.SemaphoreType.DMA
    buffers = []
    for s in shapes:
        buffers += [pltpu.VMEM((ring,) + s, BF), pltpu.VMEM((ring,) + ((s[1], s[0]) if s == square else s), F32)]
    return pl.pallas_call(
        kernel,
        in_specs=[ANY] * (n + 2 * seqs + 2) + [WHOLE],
        out_specs=[ANY] * (n + 1) + [WHOLE] * 6,
        out_shape=[jax.ShapeDtypeStruct(r.shape, F32) for r in reduced[:-1]]
        + [jax.ShapeDtypeStruct((last[2], last[1]), F32), jax.ShapeDtypeStruct((2 * seqs, shard_rows, width), F32)]
        + [
            jax.ShapeDtypeStruct(shape, F32)
            for shape in ((2, local), (1, width), (2, width), (2, width), (2, units), (1, width))
        ],
        scratch_shapes=[pltpu.VMEM((seqs, shard_rows, width), F32), sem((ring,)), sem((ring,))] + buffers,
        compiler_params=pltpu.CompilerParams(vmem_limit_bytes=VMEM_LIMIT),
        cost_estimate=pl.CostEstimate(flops=0, bytes_accessed=56 << 20, transcendentals=0),
        name="widen",
    )(*reduced, *row_grads, *gots, sums)


MASKED = -1000000000.0


def shifted(value, axis, steps):
    count = lax.axis_size(axis)
    first, last = (max(0, -steps), min(count, count - steps))
    return lax.ppermute(value, axis, [(source, source + steps) for source in range(first, last)])


def layer_norm(values, gain, shift):
    mean = jnp.mean(values, axis=-1, keepdims=True)
    centred = values - mean
    spread = jnp.mean(centred * centred, axis=-1, keepdims=True)
    return centred * lax.rsqrt(spread + EPS) * gain + shift


def alibi_slopes(first, count, heads):
    index = (first + jnp.arange(count)).astype(jnp.float32)
    return jnp.exp2(-8.0 * (index + 1.0) / heads)


def attention_core(projected, qv_bias, slopes, key_ok):
    rows = projected.shape[0]
    width = projected.shape[2]
    count = slopes.shape[0]
    size = width // count
    query = (projected[:, 0] + qv_bias[0]).astype(jnp.bfloat16).reshape(rows, count, size)
    key = projected[:, 1].astype(jnp.bfloat16).reshape(rows, count, size)
    value = (projected[:, 2] + qv_bias[1]).astype(jnp.bfloat16).reshape(rows, count, size)
    place = jnp.arange(rows).astype(jnp.float32)
    distance = jnp.abs(place[:, None] - place[None, :])
    scale = 1.0 / math.sqrt(size)
    scores = (
        jnp.einsum("qhd,khd->hqk", query, key, preferred_element_type=jnp.float32) * scale
        - slopes[:, None, None] * distance[None]
    )
    scores = jnp.where(key_ok[None, None, :], scores, MASKED)
    weights = jax.nn.softmax(scores, axis=-1)
    weights_low = weights.astype(jnp.bfloat16)
    mixed = jnp.einsum("hqk,khd->qhd", weights_low, value, preferred_element_type=jnp.float32)
    mixed = mixed.reshape(rows, width).astype(jnp.bfloat16)
    return (query, key, value, weights, weights_low, mixed)


def attention_back(parts, grad_mixed, key_ok):
    query, key, value, weights, weights_low, mixed = parts
    rows, count, size = query.shape
    scale = 1.0 / math.sqrt(size)
    grad_low = grad_mixed.astype(jnp.bfloat16).reshape(rows, count, size)
    grad_weights = jnp.einsum("qhd,khd->hqk", grad_low, value, preferred_element_type=jnp.float32)
    grad_value = jnp.einsum(
        "hqk,qhd->khd", weights_low, grad_low, preferred_element_type=jnp.float32
    )
    inner = jnp.sum(weights * grad_weights, axis=-1, keepdims=True)
    grad_scores = weights * (grad_weights - inner)
    grad_scores = jnp.where(key_ok[None, None, :], grad_scores, 0.0).astype(jnp.bfloat16)
    grad_query = (
        jnp.einsum("hqk,khd->qhd", grad_scores, key, preferred_element_type=jnp.float32) * scale
    ).astype(jnp.bfloat16)
    grad_key = (
        jnp.einsum("hqk,qhd->khd", grad_scores, query, preferred_element_type=jnp.float32) * scale
    ).astype(jnp.bfloat16)
    grad_value = grad_value.astype(jnp.bfloat16)
    width = count * size
    grad_query = grad_query.reshape(rows, width)
    grad_key = grad_key.reshape(rows, width)
    grad_value = grad_value.reshape(rows, width)
    grad_projected = jnp.stack([grad_query, grad_key, grad_value], axis=1).reshape(rows, 3 * width)
    qv_grad = jnp.stack(
        [
            jnp.sum(grad_query.astype(jnp.float32), axis=0),
            jnp.sum(grad_value.astype(jnp.float32), axis=0),
        ]
    )
    return (grad_projected, qv_grad)


def gelu_product(both):
    return jax.nn.gelu(both[:, 0], approximate=False) * both[:, 1]


def geglu(lifted, up_bias):
    return gelu_product(lifted + up_bias[None])


def ffn_grads(rows_low, grad_low, up_weight, up_bias, down_weight):
    lifted = jnp.einsum("sd,gdf->sgf", rows_low, up_weight, preferred_element_type=jnp.float32)
    hidden, geglu_back = jax.vjp(gelu_product, lifted + up_bias[None])
    grad_hidden = jnp.einsum("sd,df->sf", grad_low, down_weight, preferred_element_type=jnp.float32)
    (grad_both,) = geglu_back(grad_hidden)
    grad_lifted = grad_both.astype(jnp.bfloat16)
    grad_bias = jnp.sum(grad_lifted.astype(jnp.float32), axis=0)
    up_grad = jnp.einsum("sd,sgf->gdf", rows_low, grad_lifted, preferred_element_type=jnp.float32)
    down_grad = jnp.einsum(
        "sd,sf->df", grad_low, hidden.astype(jnp.bfloat16), preferred_element_type=jnp.float32
    )
    return (grad_lifted, grad_bias, up_grad, down_grad)


def on_device(
    inputs,
    cotangent,
    lengths,
    w_qkv,
    b_qv,
    w_out,
    b_out,
    ln_gain,
    ln_bias,
    w_up,
    b_up,
    w_down,
    b_down,
):
    batches, shard_rows, width = inputs.shape
    parts = lax.axis_size("tensor")
    place = lax.axis_index("tensor")
    section = lax.axis_index("section")
    last_section = lax.axis_size("section") - 1
    full_rows = shard_rows * parts
    local_width = w_qkv.shape[3]
    local_heads = local_width // HD
    qkv_flat = w_qkv[0].reshape(width, 3 * local_width)
    out_weight = w_out[0]
    qv_bias = b_qv[0].astype(jnp.float32)
    out_bias = b_out[0].astype(jnp.float32)
    gains = ln_gain[0].astype(jnp.float32)
    shifts = ln_bias[0].astype(jnp.float32)
    down_bias = b_down[0].astype(jnp.float32)
    slopes = alibi_slopes(place * local_heads, local_heads, H)
    row_place = place * shard_rows + jnp.arange(shard_rows)
    kept_rows = 0

    def key_mask(length):
        return jnp.arange(full_rows) < length

    def after_attention(values, attended, bias, gain_rows, shift_rows):
        return layer_norm(values + attended + bias, gain_rows[0], shift_rows[0])

    def after_ffn(normed, lowered, bias, gain_rows, shift_rows):
        return layer_norm(normed + lowered + bias, gain_rows[1], shift_rows[1])

    def gather_inputs(values):
        return lax.all_gather(values.astype(jnp.bfloat16), "tensor", axis=0, tiled=True)

    def project(gathered):
        return jnp.dot(gathered, qkv_flat, preferred_element_type=jnp.float32).reshape(
            full_rows, 3, local_width
        )

    def attention_forward(values, length):
        gathered = gather_inputs(values)
        projected = project(gathered)
        mixed = attention_core(projected, qv_bias, slopes, key_mask(length))[5]

        def term(start, count):
            return jnp.dot(mixed, out_weight, preferred_element_type=jnp.float32)

        return (
            lax.psum_scatter(
                term(jnp.int32(0), shard_rows * lax.axis_size("tensor")).astype(jnp.bfloat16),
                "tensor",
                scatter_dimension=0,
                tiled=True,
            ).astype(jnp.float32),
            gathered,
            projected,
        )

    up_local = w_up[0]
    up_bias_local = b_up[0].astype(jnp.float32)
    down_local = w_down[0]

    def gather_normed(normed):
        return lax.all_gather(normed.astype(jnp.bfloat16), "tensor", axis=0, tiled=True)

    def ffn_forward(normed):
        lifted = jnp.einsum(
            "sd,gdf->sgf", gather_normed(normed), up_local, preferred_element_type=jnp.float32
        )
        hidden = geglu(lifted, up_bias_local).astype(jnp.bfloat16)

        def term(start, count):
            return jnp.einsum("sf,df->sd", hidden, down_local, preferred_element_type=jnp.float32)

        return lax.psum_scatter(
            term(jnp.int32(0), shard_rows * lax.axis_size("tensor")).astype(jnp.bfloat16),
            "tensor",
            scatter_dimension=0,
            tiled=True,
        ).astype(jnp.float32)

    def ffn_backward(normed, grad_lowered):
        gathered = gather_normed(normed)
        grad_whole = lax.all_gather(grad_lowered.astype(jnp.bfloat16), "tensor", axis=0, tiled=True)
        grad_lifted, grad_bias, up_grad, down_grad = ffn_grads(
            gathered, grad_whole, up_local, up_bias_local, down_local
        )

        def term(start, count):
            return jnp.einsum(
                "sgf,gdf->sd", grad_lifted, up_local, preferred_element_type=jnp.float32
            )

        grad_normed = lax.psum_scatter(
            term(jnp.int32(0), shard_rows * lax.axis_size("tensor")).astype(jnp.bfloat16),
            "tensor",
            scatter_dimension=0,
            tiled=True,
        ).astype(jnp.float32)
        return (grad_normed, (up_grad, grad_bias, down_grad))

    ffn_shapes = (up_local.shape, up_bias_local.shape, down_local.shape)

    def layer_forward(values, length):
        attended, gathered, projected = attention_forward(values, length)
        normed = after_attention(values, attended, out_bias, gains, shifts)
        lowered = ffn_forward(normed)
        return (
            after_ffn(normed, lowered, down_bias, gains, shifts),
            attended,
            lowered,
            gathered,
            projected,
        )

    def layer_backward(values, attended, lowered, length, grad_output):
        normed, attention_norm_back = jax.vjp(
            after_attention, values, attended, out_bias, gains, shifts
        )
        outcome, ffn_norm_back = jax.vjp(after_ffn, normed, lowered, down_bias, gains, shifts)
        grad_normed, grad_lowered, grad_down_bias, gain_late, shift_late = ffn_norm_back(
            grad_output
        )
        grad_from_ffn, ffn_terms = ffn_backward(normed, grad_lowered)
        grad_values, grad_attended, grad_out_bias, gain_early, shift_early = attention_norm_back(
            grad_normed + grad_from_ffn
        )
        gathered = gather_inputs(values)
        projected = project(gathered)
        grad_whole = lax.all_gather(
            grad_attended.astype(jnp.bfloat16), "tensor", axis=0, tiled=True
        )
        mask = key_mask(length)
        pieces = attention_core(projected, qv_bias, slopes, mask)
        mixed_low = pieces[5]
        out_grad = jnp.einsum(
            "se,sd->ed", mixed_low, grad_whole, preferred_element_type=jnp.float32
        )
        grad_mixed = jnp.einsum(
            "sd,ed->se", grad_whole, out_weight, preferred_element_type=jnp.float32
        )
        grad_projected, qv_grad = attention_back(pieces, grad_mixed, mask)
        qkv_grad = jnp.einsum(
            "sd,sx->dx", gathered, grad_projected, preferred_element_type=jnp.float32
        )

        def term(start, count):
            return jnp.einsum(
                "sx,dx->sd", grad_projected, qkv_flat, preferred_element_type=jnp.float32
            )

        grad_inputs = grad_values + lax.psum_scatter(
            term(jnp.int32(0), shard_rows * lax.axis_size("tensor")).astype(jnp.bfloat16),
            "tensor",
            scatter_dimension=0,
            tiled=True,
        ).astype(jnp.float32)
        terms = (
            qkv_grad,
            qv_grad,
            out_grad,
            grad_out_bias,
            gain_early + gain_late,
            shift_early + shift_late,
            ffn_terms[0],
            ffn_terms[1],
            ffn_terms[2],
            grad_down_bias,
        )
        return (grad_inputs, terms)

    def keep(store, item, batch, valid):
        old = lax.dynamic_index_in_dim(store, batch, 0, keepdims=False)
        return lax.dynamic_update_index_in_dim(store, jnp.where(valid, item, old), batch, 0)

    def forward_step(step, carry):
        (
            received,
            kept_values,
            kept_attended,
            kept_lowered,
            produced,
            kept_gathered,
            kept_projected,
        ) = carry
        index = step - section
        valid = (index >= 0) & (index < batches)
        batch = jnp.clip(index, 0, batches - 1)
        fresh = lax.dynamic_index_in_dim(
            inputs, jnp.minimum(step, batches - 1), 0, keepdims=False
        ).astype(jnp.float32)
        values = jnp.where(section == 0, fresh, received.astype(jnp.float32))
        output, attended, lowered, gathered, projected = layer_forward(values, lengths[batch])
        sent = output.astype(jnp.bfloat16)
        kept_values = keep(kept_values, values, batch, valid)
        kept_attended = keep(kept_attended, attended, batch, valid)
        kept_lowered = keep(kept_lowered, lowered, batch, valid)
        produced = keep(produced, sent, batch, valid)
        kept_gathered = keep(kept_gathered, gathered[:kept_rows], batch, valid)
        kept_projected = keep(kept_projected, projected[:kept_rows], batch, valid)
        received = shifted(sent, "section", 1)
        return (
            received,
            kept_values,
            kept_attended,
            kept_lowered,
            produced,
            kept_gathered,
            kept_projected,
        )

    store_zeros = jnp.zeros((batches, shard_rows, width), jnp.float32)
    gathered_zeros = jnp.zeros((batches, kept_rows, width), jnp.bfloat16)
    projected_zeros = jnp.zeros((batches, kept_rows, 3, local_width), jnp.float32)
    start_forward = (
        jnp.zeros((shard_rows, width), jnp.bfloat16),
        store_zeros,
        store_zeros,
        store_zeros,
        jnp.zeros((batches, shard_rows, width), jnp.bfloat16),
        gathered_zeros,
        projected_zeros,
    )
    received, kept_values, kept_attended, kept_lowered, produced, kept_gathered, kept_projected = (
        lax.fori_loop(0, batches + last_section, forward_step, start_forward)
    )

    def backward_step(step, carry):
        received, totals, grads_in = carry
        index = step - (last_section - section)
        valid = (index >= 0) & (index < batches)
        batch = jnp.clip(index, 0, batches - 1)
        length = lengths[batch]
        outer = lax.dynamic_index_in_dim(cotangent, batch, 0, keepdims=False).astype(jnp.float32)
        outer = outer * (row_place < length).astype(jnp.float32)[:, None]
        grad_output = jnp.where(section == last_section, outer, received.astype(jnp.float32))
        grad_output = jnp.where(valid, grad_output, 0.0)
        values = lax.dynamic_index_in_dim(kept_values, batch, 0, keepdims=False)
        attended = lax.dynamic_index_in_dim(kept_attended, batch, 0, keepdims=False)
        lowered = lax.dynamic_index_in_dim(kept_lowered, batch, 0, keepdims=False)
        grad_inputs, terms = layer_backward(values, attended, lowered, length, grad_output)
        totals = jax.tree.map(jnp.add, totals, terms)
        grads_in = keep(grads_in, grad_inputs, batch, valid)
        received = shifted(grad_inputs.astype(jnp.bfloat16), "section", -1)
        return (received, totals, grads_in)

    start_totals = (
        jnp.zeros((width, 3 * local_width), jnp.float32),
        jnp.zeros((2, local_width), jnp.float32),
        jnp.zeros((local_width, width), jnp.float32),
        jnp.zeros((width,), jnp.float32),
        jnp.zeros((2, width), jnp.float32),
        jnp.zeros((2, width), jnp.float32),
        jnp.zeros(ffn_shapes[0], jnp.float32),
        jnp.zeros(ffn_shapes[1], jnp.float32),
        jnp.zeros(ffn_shapes[2], jnp.float32),
        jnp.zeros((width,), jnp.float32),
    )
    start_backward = (jnp.zeros((shard_rows, width), jnp.bfloat16), start_totals, store_zeros)
    received, totals, grads_in = lax.fori_loop(
        0, batches + last_section, backward_step, start_backward
    )
    (
        qkv_total,
        qv_total,
        out_total,
        out_bias_total,
        gain_total,
        shift_total,
        up_total,
        up_bias_total,
        down_total,
        down_bias_total,
    ) = totals
    qkv_sum, qv_sum, out_sum, up_sum, up_bias_sum, down_sum = (
        lax.psum(qkv_total.astype(jnp.bfloat16), "dp").astype(jnp.float32),
        lax.psum(qv_total.astype(jnp.bfloat16), "dp").astype(jnp.float32),
        lax.psum(out_total.astype(jnp.bfloat16), "dp").astype(jnp.float32),
        lax.psum(up_total.astype(jnp.bfloat16), "dp").astype(jnp.float32),
        lax.psum(up_bias_total.astype(jnp.bfloat16), "dp").astype(jnp.float32),
        lax.psum(down_total.astype(jnp.bfloat16), "dp").astype(jnp.float32),
    )
    out_bias_sum, gain_sum, shift_sum, down_bias_sum = lax.psum(
        (out_bias_total, gain_total, shift_total, down_bias_total), ("tensor", "dp")
    )
    return (
        produced[None],
        grads_in[None],
        qkv_sum.reshape(1, width, 3, local_width),
        qv_sum[None],
        out_sum[None],
        out_bias_sum[None],
        gain_sum[None],
        shift_sum[None],
        up_sum[None],
        up_bias_sum[None],
        down_sum[None],
        down_bias_sum[None],
    )


def by_sequence(
    inputs,
    cotangent,
    lengths,
    w_qkv,
    b_qv,
    w_out,
    b_out,
    ln_gain,
    ln_bias,
    w_up,
    b_up,
    w_down,
    b_down,
):
    batches, shard_rows, width = inputs.shape
    place = lax.axis_index("tensor")
    section = lax.axis_index("section")
    groups = lax.axis_size("dp")
    rows = 2 * shard_rows
    seqs = batches // 2
    local = w_qkv.shape[3]
    units = w_up.shape[3]
    heads = local // HD
    chips = groups // 2

    qkv_own = jnp.transpose(w_qkv[0], (1, 0, 2))
    out_own = w_out[0]
    up_own = w_up[0]
    down_own = w_down[0]
    first = section == 0
    qkv_oth, out_oth, up_oth, down_oth, bias, up_bias, *held = fetch_other_half(
        qkv_own.reshape(3 * width, local),
        out_own,
        up_own.reshape(2 * width, units),
        down_own,
        b_qv[0],
        b_up[0],
        inputs,
        cotangent,
        chips,
    )
    qkv_oth = qkv_oth.reshape(3, width, local)
    up_oth = up_oth.reshape(2, width, units)
    x_first = outer = held

    vecs = jnp.stack(
        [b_out[0], ln_gain[0, 0], ln_bias[0, 0], b_down[0], ln_gain[0, 1], ln_bias[0, 1], b_out[0], b_out[0]]
    ).astype(F32)
    slope_table = np.exp2(-8.0 * (np.arange(2 * heads, dtype=np.float32) + 1.0) / H).astype(np.float32)
    slopes = jnp.where(place == 0, slope_table, np.roll(slope_table, heads))
    own_lengths = lax.dynamic_slice_in_dim(lengths, place * seqs, seqs, 0)

    def meta(m, turn):
        active = section == turn
        return jnp.stack([jnp.int32(m), active.astype(jnp.int32), own_lengths[m], own_lengths[m] if turn == 1 else jnp.int32(rows)])

    metas = [[meta(m, turn) for m in range(seqs)] for turn in range(2)]
    weights = (qkv_own, qkv_oth, out_own, out_oth, up_own, up_oth, down_own, down_oth)
    kept = None
    deps = []

    def forward(x, m, turn):
        nonlocal kept, deps
        *kept, y = layer_forward(x, weights, bias, slopes, vecs, up_bias, metas[turn][m], kept, deps, seqs)
        deps = [y]
        return y

    y_first = [forward(x_first[m], m, 0) for m in range(seqs)]
    x_second = [lax.ppermute(y, "section", [(0, 1)]) for y in y_first]
    y_second = [forward(x_second[m], m, 1) for m in range(seqs)]

    back = None
    sums = [[None] * seqs, [None] * seqs]

    def backward(grad, m, turn):
        nonlocal back, deps
        *back, gx, gx_low, norm_sums, up_sums, qv_sums = layer_backward(
            grad, kept, weights, slopes, vecs, metas[turn][m], back, deps, seqs
        )
        deps = [norm_sums]
        sums[turn][m] = (norm_sums, up_sums, qv_sums)
        return gx, gx_low

    gx_second = [backward(outer[m], m, 1) for m in range(seqs)]
    grad_middle = [lax.ppermute(gx_second[m][1], "section", [(1, 0)]) for m in range(seqs)]
    produced, got_second = exchange_rows(y_first, y_second, [g[1] for g in gx_second])
    x_all = jnp.stack([jnp.where(first, x_first[m], x_second[m]) for m in range(seqs)])
    deps = deps + [x_all, produced]
    gx_first = [backward(grad_middle[m], m, 0) for m in range(seqs)]

    mixed, hidden, normed = kept[3], kept[7], kept[8]
    gg0, gg1, gl, ga, *gqkv = back

    picked = [
        sum(jnp.where(first, sums[0][m][index], sums[1][m][index]) for m in range(seqs))
        for index in range(3)
    ]
    norm_sums, up_sums, qv_sums = picked

    def ordered(values, count):
        return jnp.where(
            place == 0, values, jnp.concatenate([values[:, count:], values[:, :count]], axis=1)
        ).reshape(-1, width)

    packed = jnp.concatenate([norm_sums[:6], ordered(up_sums[:2], units), ordered(qv_sums[:2], local)])
    *reduced, packed, got_first = weight_grads_reduced(
        [(gl, [hidden]), (normed, [gg0, gg1]), (x_all, gqkv), (ga, [mixed])], packed, [g[1] for g in gx_first], chips
    )
    down_sum, up_sum, qkv_sum, out_sum, grads_in, qv_sum, out_bias_sum, gain_sum, shift_sum, up_bias_sum, down_bias_sum = (
        widen(reduced, [g[0] for g in gx_first + gx_second], [got_first, got_second], packed, units, local)
    )
    return (
        produced[None],
        grads_in[None],
        jnp.transpose(qkv_sum, (1, 0, 2))[None],
        qv_sum[None],
        out_sum[None],
        out_bias_sum,
        gain_sum[None],
        shift_sum[None],
        up_sum[None],
        up_bias_sum[None],
        down_sum,
        down_bias_sum,
    )


def solution(mesh):
    sections, parts, groups = (mesh.shape[name] for name in ("section", "tensor", "dp"))

    def run(*args):
        paired = sections == 2 and parts == 2 and groups % 2 == 0 and args[0].shape[0] == 4
        return (by_sequence if paired else on_device)(*args)

    return jax.shard_map(
        run,
        mesh=mesh,
        in_specs=(
            P("dp", "tensor", None),
            P("dp", "tensor", None),
            P("dp"),
            P("section", None, None, "tensor"),
            P("section", None, "tensor"),
            P("section", "tensor", None),
            P("section", None),
            P("section", None, None),
            P("section", None, None),
            P("section", None, None, "tensor"),
            P("section", None, "tensor"),
            P("section", None, "tensor"),
            P("section", None),
        ),
        out_specs=(
            P("section", "dp", "tensor", None),
            P("section", "dp", "tensor", None),
            P("section", None, None, "tensor"),
            P("section", None, "tensor"),
            P("section", "tensor", None),
            P("section", None),
            P("section", None, None),
            P("section", None, None),
            P("section", None, None, "tensor"),
            P("section", None, "tensor"),
            P("section", None, "tensor"),
            P("section", None),
        ),
        check_vma=False,
    )
```

```python
import math

import jax
import jax.numpy as jnp
import numpy as np
from jax import lax
from jax.experimental import pallas as pl
from jax.experimental.pallas import tpu as pltpu
from jax.sharding import PartitionSpec as P

H = 16
HD = 64
EPS = 1e-05
BF = jnp.bfloat16
F32 = jnp.float32
VMEM_LIMIT = 62 * 1024 * 1024
ANY = pl.BlockSpec(memory_space=pl.ANY)
SMEM = pl.BlockSpec(memory_space=pltpu.SMEM)
WHOLE = pl.BlockSpec(memory_space=pltpu.VMEM)
NN = (((1,), (0,)), ((), ()))
NT = (((1,), (1,)), ((), ()))
TN = (((0,), (0,)), ((), ()))
CW = 256
PER = CW // HD


def dot(a, b, dims=NN):
    return lax.dot_general(a, b, dims, preferred_element_type=F32)


def arrived(ref, sem):
    pltpu.make_async_copy(ref, ref, sem).wait()


def call(kernel, inputs, outputs, scratch, meta, chain, deps, name, flops, nbytes):
    pairs = [item if isinstance(item, tuple) else (item, ANY) for item in inputs]
    args = [meta] + [p[0] for p in pairs]
    specs = [SMEM] + [p[1] for p in pairs]
    n_in = len(args)
    aliases = {}
    if chain is not None:
        for buffer, index in zip(chain, [index for index, item in enumerate(outputs) if item[2]]):
            aliases[len(args)] = index
            args.append(buffer)
            specs.append(ANY)
    args += deps
    specs += [ANY] * len(deps)
    n_args, n_out = len(args), len(outputs)

    def body(*refs):
        @pl.when(refs[0][1] == 1)
        def _():
            kernel(refs[0], refs[1:n_in], refs[n_args : n_args + n_out], refs[n_args + n_out :])

    return pl.pallas_call(
        body,
        in_specs=specs,
        out_specs=[ANY] * n_out,
        out_shape=[jax.ShapeDtypeStruct(o[0], o[1]) for o in outputs],
        scratch_shapes=scratch,
        input_output_aliases=aliases,
        compiler_params=pltpu.CompilerParams(vmem_limit_bytes=VMEM_LIMIT),
        cost_estimate=pl.CostEstimate(flops=flops, bytes_accessed=nbytes, transcendentals=0),
        name=name,
    )(*args)


def pick(k, count, own, oth, make):
    @pl.when(k < count)
    def _():
        for src, dst, sem in make(own, k):
            pltpu.make_async_copy(src, dst, sem).start()

    @pl.when(k >= count)
    def _():
        for src, dst, sem in make(oth, k - count):
            pltpu.make_async_copy(src, dst, sem).start()


def block(index, size):
    return pl.ds(pl.multiple_of(index * size, size), size)


def copy(src, dst, sem):
    return pltpu.make_async_copy(src, dst, sem)


def fill_distance(dist_ref, length):
    rows = dist_ref.shape[0]
    keys = lax.broadcasted_iota(jnp.int32, (rows, rows), 0)
    places = lax.broadcasted_iota(jnp.int32, (rows, rows), 1)
    distance = jnp.abs(keys - places).astype(F32)
    dist_ref[...] = jnp.where(keys < length, distance, 1e12)


def normalize(v):
    mean = jnp.mean(v, axis=1, keepdims=True)
    centred = v - mean
    rstd = lax.rsqrt(jnp.mean(centred * centred, axis=1, keepdims=True) + EPS)
    return centred * rstd, rstd


def halves(rows):
    return [slice(0, rows // 2), slice(rows // 2, rows)]


def layer_forward(x, weights, bias, slopes, vecs, up_bias, meta, chain, deps, slots):
    qkv_own, qkv_oth, o_own, o_oth, up_own, up_oth, down_own, down_oth = weights
    rows, width = x.shape
    local = qkv_own.shape[2]
    units = up_own.shape[2]
    heads_steps = local // CW
    ft = min(512, units)
    tiles = units // ft
    total = 2 * local

    def kernel(meta_ref, ins, outs, scratch):
        (x_hbm, qkv_own_ref, qkv_oth_ref, o_own_ref, o_oth_ref, up_own_ref, up_oth_ref, down_own_ref, down_oth_ref,
         bias_ref, slope_ref, vec_ref, ub_ref) = ins
        q_out, k_out, v_out, mixed_out, lse_out, a_out, b_out, h_out, n_out, u1_out, u2_out, r1_out, r2_out, y_out = outs
        (x_ref, w_ref, o_ref, up_ref, down_ref, qkv_ref, lse_ref, mixed_ref, dist_ref, normed_ref, acc_ref, low_ref,
         tile_ref, row_ref, stat_ref, x_sem, w_sem, o_sem, f_sem, q_sem, m_sem, t_sem, r_sem) = scratch
        slot = meta_ref[0]

        def start_w(k):
            s = lax.rem(k, 2)
            pick(k, heads_steps, qkv_own_ref, qkv_oth_ref,
                 lambda ref, j: [(ref.at[:, :, block(j, CW)], w_ref.at[s], w_sem.at[s])])

        def start_f(k):
            s = lax.rem(k, 2)
            pick(k, tiles, (up_own_ref, down_own_ref), (up_oth_ref, down_oth_ref),
                 lambda ref, j: [(ref[0].at[:, :, block(j, ft)], up_ref.at[s], f_sem.at[s, 0]),
                                 (ref[1].at[:, block(j, ft)], down_ref.at[s], f_sem.at[s, 1])])

        copy(x_hbm, x_ref, x_sem).start()
        start_w(jnp.int32(0))
        start_w(jnp.int32(1))
        copy(o_own_ref, o_ref.at[pl.ds(0, local)], o_sem).start()
        copy(o_oth_ref, o_ref.at[pl.ds(local, local)], o_sem).start()
        start_f(jnp.int32(0))
        start_f(jnp.int32(1))
        fill_distance(dist_ref, meta_ref[2])
        arrived(x_ref, x_sem)

        def write_qkv(i, s):
            cols = block(i, CW)
            return [copy(qkv_ref.at[s, c], out.at[slot, :, cols], q_sem.at[s, c])
                    for c, out in enumerate((q_out, k_out, v_out))] + [
                copy(lse_ref.at[s], lse_out.at[slot, i], q_sem.at[s, 3])]

        @pl.loop(0, 2 * heads_steps)
        def _(i):
            s = lax.rem(i, 2)
            arrived(w_ref.at[s], w_sem.at[s])

            @pl.when(i >= 2)
            def _():
                for item in write_qkv(i - 2, s):
                    item.wait()

            values = x_ref[...]
            b = bias_ref[:, block(i, CW)].astype(F32)
            qkv_ref[s, 0] = (dot(values, w_ref[s, 0]) + b[0:1]).astype(BF)
            qkv_ref[s, 1] = dot(values, w_ref[s, 1]).astype(BF)
            qkv_ref[s, 2] = (dot(values, w_ref[s, 2]) + b[1:2]).astype(BF)

            @pl.when(i + 2 < 2 * heads_steps)
            def _():
                start_w(i + 2)

            parts = []
            for head in range(PER):
                cols = slice(head * HD, (head + 1) * HD)
                query = qkv_ref[s, 0, :, cols] * BF(1.0 / math.sqrt(HD))
                scores = dot(qkv_ref[s, 1, :, cols], query, NT)
                scores = scores - dist_ref[...] * slope_ref[i * PER + head]
                top = jnp.max(scores, axis=0, keepdims=True)
                likely = jnp.exp(scores - top)
                mass = jnp.sum(likely, axis=0, keepdims=True)
                low = (likely * (1.0 / mass)).astype(BF)
                parts.append(dot(low, qkv_ref[s, 2, :, cols], TN).astype(BF))
                lse_ref[s, head : head + 1, :] = top + jnp.log(mass)
            mixed_ref[:, block(i, CW)] = jnp.concatenate(parts, axis=1)
            for item in write_qkv(i, s):
                item.start()

        copy(mixed_ref, mixed_out.at[slot], m_sem).start()
        arrived(o_ref, o_sem)
        vec = vec_ref[...]
        for rs in halves(rows):
            attended = dot(mixed_ref[rs, :], o_ref[...])
            u, rstd = normalize(x_ref[rs, :].astype(F32) + attended + vec[0:1])
            normed = u * vec[1:2] + vec[2:3]
            normed_ref[rs, :] = normed
            low_ref[rs, :] = normed.astype(BF)
            row_ref[0, rs, :] = u.astype(BF)
            stat_ref[0, rs, :] = jnp.broadcast_to(rstd, (rows // 2, 128))
            acc_ref[rs, :] = jnp.zeros((rows // 2, width), F32)
        for index, (src, dst) in enumerate(((low_ref, n_out), (row_ref.at[0], u1_out), (stat_ref.at[0], r1_out))):
            copy(src, dst.at[slot], r_sem.at[index]).start()

        def write_tiles(i, s):
            return [copy(tile_ref.at[s, c], out.at[slot, :, block(i, ft)], t_sem.at[s, c])
                    for c, out in enumerate((a_out, b_out, h_out))]

        @pl.loop(0, 2 * tiles)
        def _(i):
            s = lax.rem(i, 2)
            arrived(up_ref.at[s], f_sem.at[s, 0])
            arrived(down_ref.at[s], f_sem.at[s, 1])

            @pl.when(i >= 2)
            def _():
                for item in write_tiles(i - 2, s):
                    item.wait()

            b = ub_ref[:, block(i, ft)].astype(F32)
            for rs in halves(rows):
                low = low_ref[rs, :]
                gate = dot(low, up_ref[s, 0]) + b[0:1]
                lift = dot(low, up_ref[s, 1]) + b[1:2]
                cdf = 0.5 * lax.erf(gate * (1.0 / math.sqrt(2.0))) + 0.5
                act = gate * cdf
                slope = cdf + gate * (jnp.exp(gate * gate * -0.5) * (1.0 / math.sqrt(2.0 * math.pi)))
                tile_ref[s, 0, rs, :] = act.astype(BF)
                tile_ref[s, 1, rs, :] = (lift * slope).astype(BF)
                hidden = (act * lift).astype(BF)
                tile_ref[s, 2, rs, :] = hidden
                acc_ref[rs, :] += dot(hidden, down_ref[s], NT)

            @pl.when(i + 2 < 2 * tiles)
            def _():
                start_f(i + 2)

            for item in write_tiles(i, s):
                item.start()

        for rs in halves(rows):
            u, rstd = normalize(normed_ref[rs, :] + acc_ref[rs, :] + vec[3:4])
            row_ref[1, rs, :] = u.astype(BF)
            stat_ref[1, rs, :] = jnp.broadcast_to(rstd, (rows // 2, 128))
            row_ref[2, rs, :] = (u * vec[4:5] + vec[5:6]).astype(BF)
        ends = [(row_ref.at[1], u2_out.at[slot]), (stat_ref.at[1], r2_out.at[slot]), (row_ref.at[2], y_out)]
        for index, (src, dst) in enumerate(ends):
            copy(src, dst, r_sem.at[3 + index]).start()
        for index, (src, dst) in enumerate(
            [(low_ref, n_out.at[slot]), (row_ref.at[0], u1_out.at[slot]), (stat_ref.at[0], r1_out.at[slot])] + ends
        ):
            copy(src, dst, r_sem.at[index]).wait()
        copy(mixed_ref, mixed_out.at[slot], m_sem).wait()
        for i in (2 * heads_steps - 2, 2 * heads_steps - 1):
            for item in write_qkv(jnp.int32(i), i % 2):
                item.wait()
        for i in (2 * tiles - 2, 2 * tiles - 1):
            for item in write_tiles(jnp.int32(i), i % 2):
                item.wait()

    sem = pltpu.SemaphoreType.DMA
    return call(
        kernel,
        [x, *weights, (bias, WHOLE), (slopes, SMEM), (vecs, WHOLE), (up_bias, WHOLE)],
        [((slots, rows, total), BF, True)] * 4
        + [((slots, 2 * heads_steps, 8, rows), F32, True)]
        + [((slots, rows, 2 * units), BF, True)] * 3
        + [((slots, rows, width), BF, True)] * 3
        + [((slots, rows, 128), F32, True)] * 2
        + [((rows, width), BF, False)],
        [
            pltpu.VMEM((rows, width), BF),
            pltpu.VMEM((2, 3, width, CW), BF),
            pltpu.VMEM((total, width), BF),
            pltpu.VMEM((2, 2, width, ft), BF),
            pltpu.VMEM((2, width, ft), BF),
            pltpu.VMEM((2, 3, rows, CW), BF),
            pltpu.VMEM((2, 8, rows), F32),
            pltpu.VMEM((rows, total), BF),
            pltpu.VMEM((rows, rows), F32),
            pltpu.VMEM((rows, width), F32),
            pltpu.VMEM((rows, width), F32),
            pltpu.VMEM((rows, width), BF),
            pltpu.VMEM((2, 3, rows, ft), BF),
            pltpu.VMEM((3, rows, width), BF),
            pltpu.VMEM((2, rows, 128), F32),
            sem, sem((2,)), sem, sem((2, 2)), sem((2, 4)), sem, sem((2, 3)), sem((6,)),
        ],
        meta,
        chain,
        deps,
        "layer_forward",
        2 * rows * width * (4 * total + 6 * units) + 4 * rows * rows * total,
        54 << 20,
    )


def layer_backward(grad, kept, weights, slopes, vecs, meta, chain, deps, slots):
    qkv_own, qkv_oth, o_own, o_oth, up_own, up_oth, down_own, down_oth = weights
    q, k, v, _, lse, act, slope, _, _, u1, u2, r1, r2 = kept
    rows, width = grad.shape
    local = qkv_own.shape[2]
    units = up_own.shape[2]
    heads_steps = local // CW
    ft = min(512, units)
    tiles = units // ft
    total = 2 * local

    def norm_back(grad_z, u, rstd, gain):
        t = grad_z * gain
        return rstd * (t - jnp.mean(t, axis=1, keepdims=True) - u * jnp.mean(t * u, axis=1, keepdims=True))

    def row_sum(values):
        return jnp.sum(values, axis=0, keepdims=True)

    def kernel(meta_ref, ins, outs, scratch):
        (g_hbm, q_hbm, k_hbm, v_hbm, lse_hbm, a_hbm, b_hbm, u1_hbm, u2_hbm, r1_hbm, r2_hbm,
         qkv_own_ref, qkv_oth_ref, o_own_ref, o_oth_ref, up_own_ref, up_oth_ref, down_own_ref, down_oth_ref,
         slope_ref, vec_ref) = ins
        gg0_out, gg1_out, gl_out, ga_out, gq_out, gk_out, gv_out, gx_out, gxl_out, sums_out, ub_out, qv_out = outs
        (g_ref, u_ref, r_ref, up_ref, down_ref, ab_ref, gg_ref, low_ref, acc_ref, sums_ref, ub_ref, qv_ref,
         w_ref, o_ref, qkv_ref, lse_ref, gm_ref, dist_ref, gqkv_ref,
         g_sem, f_sem, t_sem, w_sem, q_sem, r_sem) = scratch
        slot = meta_ref[0]

        def start_f(i):
            s = lax.rem(i, 2)
            pick(i, tiles, (up_own_ref, down_own_ref), (up_oth_ref, down_oth_ref),
                 lambda ref, j: [(ref[0].at[:, :, block(j, ft)], up_ref.at[s], f_sem.at[s, 0]),
                                 (ref[1].at[:, block(j, ft)], down_ref.at[s], f_sem.at[s, 1])])
            for c, ref in enumerate((a_hbm, b_hbm)):
                copy(ref.at[slot, :, block(i, ft)], ab_ref.at[s, c], f_sem.at[s, 2 + c]).start()

        def start_w(i):
            s = lax.rem(i, 2)
            pick(i, heads_steps, (qkv_own_ref, o_own_ref), (qkv_oth_ref, o_oth_ref),
                 lambda ref, j: [(ref[0].at[:, :, block(j, CW)], w_ref.at[s], w_sem.at[s, 0]),
                                 (ref[1].at[block(j, CW)], o_ref.at[s], w_sem.at[s, 1])])
            for c, ref in enumerate((q_hbm, k_hbm, v_hbm)):
                copy(ref.at[slot, :, block(i, CW)], qkv_ref.at[s, c], w_sem.at[s, 2 + c]).start()
            copy(lse_hbm.at[slot, i], lse_ref.at[s], w_sem.at[s, 5]).start()

        firsts = [(g_hbm, g_ref), (u2_hbm.at[slot], u_ref.at[1]), (r2_hbm.at[slot], r_ref.at[1]),
                  (u1_hbm.at[slot], u_ref.at[0]), (r1_hbm.at[slot], r_ref.at[0])]
        for index, (src, dst) in enumerate(firsts):
            copy(src, dst, g_sem.at[index]).start()
            if index == 2:
                start_f(jnp.int32(0))
                start_f(jnp.int32(1))
        start_w(jnp.int32(0))
        start_w(jnp.int32(1))
        vec = vec_ref[...]
        fill_distance(dist_ref, meta_ref[2])
        for index, (src, dst) in enumerate(firsts[:3]):
            copy(src, dst, g_sem.at[index]).wait()
        sums = [jnp.zeros((1, width), F32)] * 3
        for rs in halves(rows):
            places = lax.broadcasted_iota(jnp.int32, (rows // 2, width), 0) + rs.start
            grad_y = jnp.where(places < meta_ref[3], g_ref[rs, :].astype(F32), 0.0)
            u = u_ref[1, rs, :].astype(F32)
            grad_c = norm_back(grad_y, u, r_ref[1, rs, 0:1], vec[4:5])
            acc_ref[rs, :] = grad_c
            low_ref[0, rs, :] = grad_c.astype(BF)
            for index, values in enumerate((grad_y * u, grad_y, grad_c)):
                sums[index] += row_sum(values)
        for index in range(3):
            sums_ref[index : index + 1, :] = sums[index]
        copy(low_ref.at[0], gl_out.at[slot], r_sem.at[0]).start()

        def write_tiles(i, s):
            return [copy(gg_ref.at[s, c], out.at[slot, :, block(i, ft)], t_sem.at[s, c])
                    for c, out in enumerate((gg0_out, gg1_out))]

        @pl.loop(0, 2 * tiles)
        def _(i):
            s = lax.rem(i, 2)
            arrived(up_ref.at[s], f_sem.at[s, 0])
            arrived(down_ref.at[s], f_sem.at[s, 1])
            for c in range(2):
                arrived(ab_ref.at[s, c], f_sem.at[s, 2 + c])

            @pl.when(i >= 2)
            def _():
                for item in write_tiles(i - 2, s):
                    item.wait()

            s0 = jnp.zeros((1, ft), F32)
            s1 = jnp.zeros((1, ft), F32)
            for rs in halves(rows):
                gh = dot(low_ref[0, rs, :], down_ref[s])
                g0 = (gh * ab_ref[s, 1, rs, :].astype(F32)).astype(BF)
                g1 = (gh * ab_ref[s, 0, rs, :].astype(F32)).astype(BF)
                gg_ref[s, 0, rs, :] = g0
                gg_ref[s, 1, rs, :] = g1
                s0 += row_sum(g0.astype(F32))
                s1 += row_sum(g1.astype(F32))
                acc_ref[rs, :] += dot(g0, up_ref[s, 0], NT) + dot(g1, up_ref[s, 1], NT)
            ub_ref[0:1, block(i, ft)] = s0
            ub_ref[1:2, block(i, ft)] = s1

            @pl.when(i + 2 < 2 * tiles)
            def _():
                start_f(i + 2)

            for item in write_tiles(i, s):
                item.start()

        for index, (src, dst) in enumerate(firsts[3:]):
            copy(src, dst, g_sem.at[3 + index]).wait()
        sums = [jnp.zeros((1, width), F32)] * 3
        for rs in halves(rows):
            grad_n = acc_ref[rs, :]
            u = u_ref[0, rs, :].astype(F32)
            grad_a = norm_back(grad_n, u, r_ref[0, rs, 0:1], vec[1:2])
            low_ref[1, rs, :] = grad_a.astype(BF)
            acc_ref[rs, :] = grad_a
            for index, values in enumerate((grad_n * u, grad_n, grad_a)):
                sums[index] += row_sum(values)
        for index in range(3):
            sums_ref[3 + index : 4 + index, :] = sums[index]
        sums_ref[6:8, :] = jnp.zeros((2, width), F32)
        copy(low_ref.at[1], ga_out.at[slot], r_sem.at[1]).start()
        scale = BF(1.0 / math.sqrt(HD))

        def write_heads(i, s):
            return [copy(gqkv_ref.at[s, c], out.at[slot, :, block(i, CW)], q_sem.at[s, c])
                    for c, out in enumerate((gq_out, gk_out, gv_out))]

        @pl.loop(0, 2 * heads_steps)
        def _(i):
            s = lax.rem(i, 2)
            for index, ref in enumerate((w_ref.at[s], o_ref.at[s], qkv_ref.at[s, 0], qkv_ref.at[s, 1], qkv_ref.at[s, 2], lse_ref.at[s])):
                arrived(ref, w_sem.at[s, index])

            @pl.when(i >= 2)
            def _():
                for item in write_heads(i - 2, s):
                    item.wait()

            gm_ref[...] = dot(low_ref[1], o_ref[s], NT).astype(BF)
            parts = [[], [], []]
            for head in range(PER):
                cols = slice(head * HD, (head + 1) * HD)
                query = qkv_ref[s, 0, :, cols] * scale
                key = qkv_ref[s, 1, :, cols]
                gm = gm_ref[:, cols]
                scores = dot(key, query, NT)
                scores = scores - dist_ref[...] * slope_ref[i * PER + head]
                likely = jnp.exp(scores - lse_ref[s, head : head + 1, :])
                parts[2].append(dot(likely.astype(BF), gm).astype(BF))
                t = likely * dot(qkv_ref[s, 2, :, cols], gm, NT)
                inner = jnp.sum(t, axis=0, keepdims=True)
                gs = (t - likely * inner).astype(BF)
                parts[1].append(dot(gs, query).astype(BF))
                parts[0].append(dot(gs, key * scale, TN).astype(BF))
            for c in range(3):
                gqkv_ref[s, c] = jnp.concatenate(parts[c], axis=1)
            for index, c in enumerate((0, 2)):
                qv_ref[index : index + 1, block(i, CW)] = row_sum(gqkv_ref[s, c].astype(F32))
            acc_ref[...] += (
                dot(gqkv_ref[s, 0], w_ref[s, 0], NT)
                + dot(gqkv_ref[s, 1], w_ref[s, 1], NT)
                + dot(gqkv_ref[s, 2], w_ref[s, 2], NT)
            )

            @pl.when(i + 2 < 2 * heads_steps)
            def _():
                start_w(i + 2)

            for item in write_heads(i, s):
                item.start()

        g_ref[...] = acc_ref[...].astype(BF)
        ends = [(g_ref, gxl_out), (acc_ref, gx_out), (sums_ref, sums_out), (ub_ref, ub_out), (qv_ref, qv_out)]
        for index, (src, dst) in enumerate(ends):
            copy(src, dst, r_sem.at[2 + index]).start()
        for index, (src, dst) in enumerate([(low_ref.at[0], gl_out.at[slot]), (low_ref.at[1], ga_out.at[slot])] + ends):
            copy(src, dst, r_sem.at[index]).wait()
        for i in (2 * tiles - 2, 2 * tiles - 1):
            for item in write_tiles(jnp.int32(i), i % 2):
                item.wait()
        for i in (2 * heads_steps - 2, 2 * heads_steps - 1):
            for item in write_heads(jnp.int32(i), i % 2):
                item.wait()

    sem = pltpu.SemaphoreType.DMA
    return call(
        kernel,
        [grad, q, k, v, lse, act, slope, u1, u2, r1, r2, *weights, (slopes, SMEM), (vecs, WHOLE)],
        [((slots, rows, 2 * units), BF, True)] * 2
        + [((slots, rows, width), BF, True)] * 2
        + [((slots, rows, total), BF, True)] * 3
        + [
            ((rows, width), F32, False),
            ((rows, width), BF, False),
            ((8, width), F32, False),
            ((2, 2 * units), F32, False),
            ((2, total), F32, False),
        ],
        [
            pltpu.VMEM((rows, width), BF),
            pltpu.VMEM((2, rows, width), BF),
            pltpu.VMEM((2, rows, 128), F32),
            pltpu.VMEM((2, 2, width, ft), BF),
            pltpu.VMEM((2, width, ft), BF),
            pltpu.VMEM((2, 2, rows, ft), BF),
            pltpu.VMEM((2, 2, rows, ft), BF),
            pltpu.VMEM((2, rows, width), BF),
            pltpu.VMEM((rows, width), F32),
            pltpu.VMEM((8, width), F32),
            pltpu.VMEM((2, 2 * units), F32),
            pltpu.VMEM((2, total), F32),
            pltpu.VMEM((2, 3, width, CW), BF),
            pltpu.VMEM((2, CW, width), BF),
            pltpu.VMEM((2, 3, rows, CW), BF),
            pltpu.VMEM((2, 8, rows), F32),
            pltpu.VMEM((rows, CW), BF),
            pltpu.VMEM((rows, rows), F32),
            pltpu.VMEM((2, 3, rows, CW), BF),
            sem((5,)), sem((2, 4)), sem((2, 2)), sem((2, 6)), sem((2, 3)), sem((7,)),
        ],
        meta,
        chain,
        deps,
        "layer_backward",
        2 * rows * width * (4 * total + 6 * units) + 10 * rows * rows * total,
        70 << 20,
    )


MESH = pl.DeviceIdType.MESH
CORE_LAG = 3
CROSS_LAG = 3
CHAIN_LAG = 2


def neighbours():
    t = lax.axis_index("tensor")
    d = lax.axis_index("dp")
    last = lax.axis_size("dp") // 2 - 1
    c = lax.rem(d, 2)
    z = d // 2
    return t, c, z, last, {"dp": d + 1 - 2 * c}, {"tensor": 1 - t}, {"dp": d + 2}, {"dp": d - 2}


def greet(c, z, chips, core, cross):
    barrier = pltpu.get_barrier_semaphore()
    pl.semaphore_signal(barrier, inc=1, device_id=core, device_id_type=MESH)
    pl.semaphore_signal(barrier, inc=1, device_id=cross, device_id_type=MESH)
    for shift in range(1, chips):
        chip = lax.rem(z + shift, chips)
        pl.semaphore_signal(barrier, inc=1, device_id={"dp": chip * 2 + c}, device_id_type=MESH)
    pl.semaphore_wait(barrier, 1 + chips)


def fetch_other_half(qkv, out, up, down, qv_bias, up_bias, inputs, cotangent, chips):
    weights = [qkv, out, up, down]
    biases = [qv_bias, up_bias]
    bias_widths = [b.shape[1] for b in biases]
    seqs = inputs.shape[0] // 2
    shard_rows, width = inputs.shape[1:]
    groups = 2 * chips

    def rows_of(item):
        return weights[item].shape[0]

    plan = []
    up_piece = rows_of(2) // groups
    parts = 4
    for part in range(parts):
        plan.append((2, True, 0, up_piece, part * up_piece // parts, up_piece // parts))
    spread = rows_of(3) * 3 // 4
    down_piece = spread // groups
    for part in range(3):
        plan.append((3, True, 0, down_piece, part * down_piece // 3, down_piece // 3))
    n_spread = len(plan)
    plan.append((-1, False, 0, 0, 0, 0))
    plan.append((-2, False, 0, 0, 0, 0))
    plan.append((-2, False, 0, 0, 0, 1))
    for part in range(3):
        size = rows_of(0) // 6
        plan.append((0, False, 0, rows_of(0) // 2, part * size, size))
    plan.append((1, False, 0, rows_of(1) // 2, 0, rows_of(1) // 2))
    plan.append((-1, False, 0, 0, 0, 1))
    direct = (rows_of(3) - spread) // 2
    for part in range(2):
        plan.append((3, False, spread, direct, part * direct // 2, direct // 2))
    n = len(plan)

    def kernel(*refs):
        ins, bias_ins, held_refs = refs[:4], refs[4:6], refs[6:8]
        outs, bias_outs, row_refs = refs[8:12], refs[12:14], refs[14 : 14 + seqs]
        stage, x_send, x_recv, c_send, c_recv, u_send, u_recv, d_send, d_recv, l_sem, b_sem = refs[14 + seqs :]
        t, c, z, last, core, cross, above, below = neighbours()
        section = lax.axis_index("section")
        greet(c, z, chips, core, cross)

        def rows(index, chip, on):
            item, is_spread, base, piece, offset, size = plan[index]
            place = chip * 2 + on if is_spread else on
            return item, pl.ds(pl.multiple_of(base + place * piece + offset, size), size)

        def span(part):
            return block(part, shard_rows)

        def bias_part(m, side):
            return bias_outs[m].at[:, pl.ds(side * bias_widths[m], bias_widths[m])]

        def cross_copy(index, held_ref=None):
            m = plan[index][5]
            if plan[index][0] == -1:
                src = (held_refs[0] if held_ref is None else held_ref).at[(1 - t) * seqs + m]
                dst = row_refs[m].at[span(t)]
            elif plan[index][0] == -2:
                src, dst = bias_ins[m], bias_part(m, 1)
            else:
                item, where = rows(index, z, c)
                src, dst = ins[item].at[where], outs[item].at[where]
            return pltpu.make_async_remote_copy(
                src_ref=src, dst_ref=dst, send_sem=x_send.at[index], recv_sem=x_recv.at[index],
                device_id=cross, device_id_type=MESH,
            )

        def pass_on(index, chip, send, recv, device):
            item, where = rows(index, chip, c)
            place = outs[item].at[where]
            return pltpu.make_async_remote_copy(
                src_ref=place, dst_ref=place, send_sem=send.at[index, chip], recv_sem=recv.at[index, chip],
                device_id=device, device_id_type=MESH,
            )

        def got(index, chip, on, sem):
            item, where = rows(index, chip, on)
            arrived(outs[item].at[where], sem)

        for m in range(2):
            copy(bias_ins[m], bias_part(m, 0), b_sem.at[m]).start()
        for index in range(n):
            if plan[index][0] == -1:
                for turn in range(2):
                    @pl.when(section == turn)
                    def _(index=index, turn=turn):
                        cross_copy(index, held_refs[turn]).start()
            else:
                cross_copy(index).start()
        for turn in range(2):
            @pl.when(section == turn)
            def _(turn=turn):
                copy(held_refs[turn].at[pl.ds(t * seqs, seqs)], stage, l_sem).start()

        arrived(stage, l_sem)
        for m in range(seqs):
            copy(stage.at[m], row_refs[m].at[span(t)], l_sem).start()

        def handle(index, hop):
            if hop == 0:
                m = plan[index][5]
                if plan[index][0] == -1:
                    arrived(row_refs[m].at[span(1 - t)], x_recv.at[index])
                    return
                if plan[index][0] == -2:
                    arrived(bias_part(m, 1), x_recv.at[index])
                    return
                got(index, z, c, x_recv.at[index])
                pass_on(index, z, c_send, c_recv, core).start()
                if plan[index][1]:
                    @pl.when(z < last)
                    def _():
                        pass_on(index, z, u_send, u_recv, above).start()

                    @pl.when(z > 0)
                    def _():
                        pass_on(index, z, d_send, d_recv, below).start()
                return

            @pl.when(z - hop >= 0)
            def _():
                got(index, z - hop, c, u_recv.at[index, z - hop])

                @pl.when(z < last)
                def _():
                    pass_on(index, z - hop, u_send, u_recv, above).start()

                pass_on(index, z - hop, c_send, c_recv, core).start()

            @pl.when(z + hop <= last)
            def _():
                got(index, z + hop, c, d_recv.at[index, z + hop])

                @pl.when(z > 0)
                def _():
                    pass_on(index, z + hop, d_send, d_recv, below).start()

                pass_on(index, z + hop, c_send, c_recv, core).start()

        for round_ in range(max(n, n_spread + chips - 1)):
            if round_ < n:
                handle(round_, 0)
            for hop in range(1, chips):
                if 0 <= round_ - hop < n_spread:
                    handle(round_ - hop, hop)

        for m in range(2):
            copy(bias_ins[m], bias_part(m, 0), b_sem.at[m]).wait()
        for m in range(seqs):
            arrived(stage.at[m], l_sem)
        for index in range(n):
            item, is_spread = plan[index][:2]
            cross_copy(index).wait_send()
            if item < 0:
                continue
            if not is_spread:
                got(index, z, 1 - c, c_recv.at[index, z])
                pass_on(index, z, c_send, c_recv, core).wait_send()
                continue
            for chip in range(chips):
                got(index, chip, 1 - c, c_recv.at[index, chip])
                pass_on(index, chip, c_send, c_recv, core).wait_send()

                @pl.when((chip <= z) & (z < last))
                def _(chip=chip):
                    pass_on(index, chip, u_send, u_recv, above).wait_send()

                @pl.when((chip >= z) & (z > 0))
                def _(chip=chip):
                    pass_on(index, chip, d_send, d_recv, below).wait_send()

    sem = pltpu.SemaphoreType.DMA
    moved = sum(w.size for w in weights) * 2
    return pl.pallas_call(
        kernel,
        in_specs=[ANY] * 8,
        out_specs=[ANY] * (6 + seqs),
        out_shape=[jax.ShapeDtypeStruct(w.shape, BF) for w in weights]
        + [jax.ShapeDtypeStruct((2, 2 * size), BF) for size in bias_widths]
        + [jax.ShapeDtypeStruct((2 * shard_rows, width), BF)] * seqs,
        scratch_shapes=[pltpu.VMEM((seqs, shard_rows, width), BF)]
        + [sem((n,)), sem((n,))]
        + [sem((n, chips))] * 6
        + [sem, sem((2,))],
        compiler_params=pltpu.CompilerParams(collective_id=1, has_side_effects=True),
        cost_estimate=pl.CostEstimate(flops=0, bytes_accessed=2 * moved, transcendentals=0),
        name="fetch_other_half",
    )(*weights, *biases, inputs, cotangent)


def weight_grads_reduced(groups, sums, row_grads, chips):
    seqs = 2
    rows, depth = groups[0][0].shape[1:]
    lefts = [g[0] for g in groups]
    rights = [r for g in groups for r in g[1]]
    bt = 128
    half = depth // 2
    quarter = half // 2
    blocks = [r.shape[2] // (2 * bt) for r in rights]
    starts = [sum(blocks[:index]) for index in range(len(rights))]
    total = sum(blocks)
    group_starts = []
    index = 0
    for _, members in groups:
        group_starts.append(starts[index])
        index += len(members)
    n_left, n_right = len(lefts), len(rights)
    homes = [(g, index) for g, (_, members) in enumerate(groups) for index in range(len(members))]
    tiles, mines, gives = 4, CORE_LAG + 1, 4
    last_static = chips - 1
    drain = CORE_LAG + CROSS_LAG + 2 * last_static * CHAIN_LAG + 1
    vec_shape = sums.shape
    n_in = n_left + n_right + 1 + seqs
    shard_rows = rows // 2

    def kernel(*refs):
        left_refs = refs[:n_left]
        right_refs = refs[n_left : n_left + n_right]
        sums_ref = refs[n_left + n_right]
        row_refs = refs[n_left + n_right + 1 : n_in]
        outs = refs[n_in : n_in + n_left]
        sums_out, rows_out = refs[n_in + n_left : n_in + n_left + 2]
        (
            acc, from_x, from_z, final, flip, stage, tile, mine, give, vec, vec_in, vec_all,
            tile_sem, stage_sem, give_send, core_recv, x_send, x_recv, z_send, z_recv, f_send, f_recv,
            store_sem, out_send, out_recv, v_load, v_send, v_recv, r_send, r_recv,
        ) = refs[n_in + n_left + 2 :]
        t, c, z, last, core, cross, above, below = neighbours()
        section = lax.axis_index("section")
        greet(c, z, chips, core, cross)

        def remote(src, dst, send, recv, device):
            return pltpu.make_async_remote_copy(
                src_ref=src, dst_ref=dst, send_sem=send, recv_sem=recv, device_id=device, device_id_type=MESH
            )

        def valid(k):
            return (k >= 0) & (k < total)

        def member(k, visit):
            for m in range(n_right):
                @pl.when((k >= starts[m]) & (k < starts[m] + blocks[m]))
                def _(m=m):
                    visit(m, k - starts[m])

        def load_tile(k):
            slot = lax.rem(k, tiles)

            def visit(m, j):
                for side in range(2):
                    at = pl.multiple_of((side * blocks[m] + j) * bt, bt)
                    pltpu.make_async_copy(
                        right_refs[m].at[pl.ds(0, seqs), :, pl.ds(at, bt)],
                        tile.at[slot, :, :, pl.ds(side * bt, bt)],
                        tile_sem.at[slot],
                    ).start()

            member(k, visit)

        def load_left(g):
            return pltpu.make_async_copy(left_refs[g].at[pl.ds(0, seqs)], stage, stage_sem)

        vec_load = pltpu.make_async_copy(sums_ref, vec.at[0], v_load)
        vec_load.start()
        load_left(0).start()
        for k in range(tiles - 1):
            load_tile(jnp.int32(k))
        vec_load.wait()
        vec_core = remote(vec.at[0], vec_in.at[0], v_send.at[0], v_recv.at[0], core)
        vec_cross = remote(vec.at[1], vec_in.at[1], v_send.at[1], v_recv.at[1], cross)
        vec_core.start()
        def row_copy(m):
            source = row_refs[m].at[block(1 - t, shard_rows)]
            return remote(source, rows_out.at[m], r_send.at[m], r_recv.at[m], cross)

        up = pl.ds(0, quarter)
        down = pl.ds(quarter, quarter)
        sides = ((up, 0, z, above, below), (down, 1, last - z, below, above))

        @pl.loop(0, total + drain)
        def _(s):
            @pl.when(valid(s))
            def _():
                for g in range(n_left):
                    @pl.when(s == group_starts[g])
                    def _(g=g):
                        load_left(g).wait()
                        for m in range(seqs):
                            flip[:, m * rows : (m + 1) * rows] = stage[m].T
                        if g + 1 < n_left:
                            load_left(g + 1).start()

                slot = lax.rem(s, tiles)
                arrived(tile.at[slot], tile_sem.at[slot])
                give_slot = lax.rem(s, gives)

                @pl.when(s >= gives)
                def _():
                    arrived(give.at[give_slot], give_send.at[give_slot])

                for place, ring, at in ((1 - c, give, give_slot), (c, mine, lax.rem(s, mines))):
                    here = pl.ds(pl.multiple_of(place * half, half), half)
                    block = dot(flip[here, :rows], tile[slot, 0])
                    for m in range(1, seqs):
                        block += dot(flip[here, m * rows : (m + 1) * rows], tile[slot, m])
                    ring[at, 1] = block[:, :bt].astype(BF)
                    ring[at, 0] = block[:, bt:].astype(BF)

            @pl.when(s + tiles - 1 < total)
            def _():
                load_tile(s + tiles - 1)

            k1 = s - CORE_LAG

            @pl.when(valid(k1))
            def _():
                arrived(acc.at[k1], core_recv.at[k1])
                at = lax.rem(k1, mines)
                for side in range(2):
                    acc[k1, side] = (acc[k1, side].astype(F32) + mine[at, side].astype(F32)).astype(BF)

            k2 = k1 - CROSS_LAG

            @pl.when(valid(k2))
            def _():
                arrived(from_x.at[k2], x_recv.at[k2])
                acc[k2, 1] = (acc[k2, 1].astype(F32) + from_x[k2].astype(F32)).astype(BF)

            for span, way, place, ahead, behind in sides:
                k3 = k2 - CHAIN_LAG * place

                @pl.when(valid(k3) & (place > 0))
                def _(span=span, way=way, k3=k3):
                    arrived(from_z.at[k3, span], z_recv.at[way, k3])
                    acc[k3, 1, span] = (acc[k3, 1, span].astype(F32) + from_z[k3, span].astype(F32)).astype(BF)

                k4 = k2 - CHAIN_LAG * (2 * last - place)

                @pl.when(valid(k4) & (place == last))
                def _(span=span, k4=k4):
                    final[k4, span] = acc[k4, 1, span]

                @pl.when(valid(k4) & (place < last))
                def _(span=span, way=way, k4=k4):
                    arrived(final.at[k4, span], f_recv.at[way, k4])

            @pl.when(valid(s))
            def _():
                at = lax.rem(s, gives)
                remote(give.at[at], acc.at[s], give_send.at[at], core_recv.at[s], core).start()

            @pl.when(valid(k1))
            def _():
                remote(acc.at[k1, 0], from_x.at[k1], x_send, x_recv.at[k1], cross).start()

            @pl.when((k1 == total - 1) & (section == 0))
            def _():
                for m in range(seqs):
                    row_copy(m).start()

            for span, way, place, ahead, behind in sides:
                k3 = k2 - CHAIN_LAG * place

                @pl.when(valid(k3) & (place < last))
                def _(span=span, way=way, k3=k3, ahead=ahead):
                    remote(acc.at[k3, 1, span], from_z.at[k3, span], z_send.at[way], z_recv.at[way, k3], ahead).start()

                k4 = k2 - CHAIN_LAG * (2 * last - place)

                @pl.when(valid(k4) & (place > 0))
                def _(span=span, way=way, k4=k4, behind=behind):
                    remote(final.at[k4, span], final.at[k4, span], f_send.at[way], f_recv.at[way, k4], behind).start()

            k5 = k2 - CHAIN_LAG * 2 * last

            @pl.when(valid(k5))
            def _():
                def visit(m, j):
                    dst = outs[homes[m][0]].at[
                        homes[m][1], pl.ds(pl.multiple_of(c * half, half), half), pl.ds(pl.multiple_of(j * bt, bt), bt)
                    ]
                    pltpu.make_async_copy(final.at[k5], dst, store_sem).start()
                    remote(final.at[k5], dst, out_send, out_recv, core).start()

                member(k5, visit)

            @pl.when(s == 4)
            def _():
                vec_core.wait_recv()
                vec[1] = vec[0] + vec_in[0]

            @pl.when(s == 5)
            def _():
                vec_cross.start()

            @pl.when(s == 10)
            def _():
                vec_cross.wait_recv()
                vec_all[z] = vec[1] + vec_in[1]

            @pl.when(s == 11)
            def _():
                for shift in range(1, chips):
                    to = lax.rem(z + shift, chips)
                    remote(
                        vec_all.at[z], vec_all.at[z], v_send.at[1 + shift], v_recv.at[1 + shift], {"dp": to * 2 + c}
                    ).start()


        @pl.when(section == 0)
        def _():
            for m in range(seqs):
                row_copy(m).wait()

        vec_core.wait_send()
        vec_cross.wait_send()
        for shift in range(1, chips):
            origin = lax.rem(z + chips - shift, chips)
            arrived(vec_all.at[origin], v_recv.at[1 + shift])
            arrived(vec_all.at[z], v_send.at[1 + shift])
        whole = vec_all[0]
        for chip in range(1, chips):
            whole += vec_all[chip]
        sums_out[...] = whole
        for at in range(gives):
            arrived(give.at[at], give_send.at[at])
        arrived(acc.at[:, 0], x_send)
        for span, way, place, ahead, behind in sides:
            @pl.when(place < last)
            def _(span=span, way=way):
                arrived(from_z.at[:, span], z_send.at[way])

            @pl.when(place > 0)
            def _(span=span, way=way):
                arrived(final.at[:, span], f_send.at[way])

        arrived(final, out_send)
        arrived(final, store_sem)
        arrived(final, out_recv)

    sem = pltpu.SemaphoreType.DMA
    flops = 2 * seqs * rows * depth * 2 * bt * total
    return pl.pallas_call(
        kernel,
        in_specs=[ANY] * n_in,
        out_specs=[ANY] * n_left + [WHOLE, ANY],
        out_shape=[jax.ShapeDtypeStruct((len(g[1]), depth, g[1][0].shape[2] // 2), BF) for g in groups]
        + [jax.ShapeDtypeStruct(vec_shape, F32), jax.ShapeDtypeStruct((seqs, shard_rows, depth), BF)],
        scratch_shapes=[
            pltpu.VMEM((total, 2, half, bt), BF),
            pltpu.VMEM((total, half, bt), BF),
            pltpu.VMEM((total, half, bt), BF),
            pltpu.VMEM((total, half, bt), BF),
            pltpu.VMEM((depth, seqs * rows), BF),
            pltpu.VMEM((seqs, rows, depth), BF),
            pltpu.VMEM((tiles, seqs, rows, 2 * bt), BF),
            pltpu.VMEM((mines, 2, half, bt), BF),
            pltpu.VMEM((gives, 2, half, bt), BF),
            pltpu.VMEM((2,) + vec_shape, F32),
            pltpu.VMEM((2,) + vec_shape, F32),
            pltpu.VMEM((chips,) + vec_shape, F32),
            sem((tiles,)), sem, sem((gives,)), sem((total,)), sem, sem((total,)),
            sem((2,)), sem((2, total)), sem((2,)), sem((2, total)),
            sem, sem, sem, sem, sem((chips + 1,)), sem((chips + 1,)), sem((seqs,)), sem((seqs,)),
        ],
        compiler_params=pltpu.CompilerParams(
            collective_id=0, has_side_effects=True, vmem_limit_bytes=VMEM_LIMIT
        ),
        cost_estimate=pl.CostEstimate(flops=flops, bytes_accessed=64 << 20, transcendentals=0),
        name="weight_grads_reduced",
    )(*lefts, *rights, sums, *row_grads)


def exchange_rows(outputs, grads, turn, earlier, deps):
    seqs = len(outputs)
    rows, width = outputs[0].shape
    shard_rows = rows // 2
    n_in = seqs + len(grads) + len(earlier) + len(deps)
    n_out = 2 if grads else 1

    def kernel(*refs):
        y_refs, grad_refs = refs[:seqs], refs[seqs : seqs + len(grads)]
        out_ref = refs[n_in]
        stage, send, recv, l_sem = refs[n_in + n_out :]
        t = lax.axis_index("tensor")
        cross = {"tensor": 1 - t}

        def remote(src, dst, index):
            return pltpu.make_async_remote_copy(
                src_ref=src, dst_ref=dst, send_sem=send.at[index], recv_sem=recv.at[index],
                device_id=cross, device_id_type=MESH,
            )

        barrier = pltpu.get_barrier_semaphore()
        pl.semaphore_signal(barrier, inc=1, device_id=cross, device_id_type=MESH)
        pl.semaphore_wait(barrier, 1)

        @pl.when(lax.axis_index("section") == turn)
        def _():
            sent = [remote(y_refs[m].at[block(1 - t, shard_rows)], out_ref.at[t * seqs + m], m) for m in range(seqs)]
            for m, ref in enumerate(grad_refs):
                sent.append(remote(ref.at[block(1 - t, shard_rows)], refs[n_in + 1].at[m], seqs + m))
            for item in sent:
                item.start()
            for m in range(seqs):
                copy(y_refs[m].at[block(t, shard_rows)], stage.at[m], l_sem.at[m]).start()
            for m in range(seqs):
                arrived(stage.at[m], l_sem.at[m])
                copy(stage.at[m], out_ref.at[t * seqs + m], l_sem.at[m]).start()
            for m in range(seqs):
                arrived(stage.at[m], l_sem.at[m])
            for m in range(seqs):
                arrived(out_ref.at[(1 - t) * seqs + m], recv.at[m])
                arrived(stage.at[m], send.at[m])
            for item in sent[seqs:]:
                item.wait()

    sem = pltpu.SemaphoreType.DMA
    shapes = [
        jax.ShapeDtypeStruct((2 * seqs, shard_rows, width), BF),
        jax.ShapeDtypeStruct((seqs, shard_rows, width), BF),
    ]
    return pl.pallas_call(
        kernel,
        in_specs=[ANY] * n_in,
        out_specs=[ANY] * n_out,
        out_shape=shapes[:n_out],
        scratch_shapes=[
            pltpu.VMEM((seqs, shard_rows, width), BF), sem((2 * seqs,)), sem((2 * seqs,)), sem((seqs,)),
        ],
        input_output_aliases={seqs + len(grads): 0} if earlier else {},
        compiler_params=pltpu.CompilerParams(collective_id=2 + turn, has_side_effects=True),
        cost_estimate=pl.CostEstimate(flops=0, bytes_accessed=0, transcendentals=0),
        name="exchange_rows",
    )(*outputs, *grads, *earlier, *deps)


def widen(reduced, row_grads, gots, sums, units, local):
    seqs, shard_rows, width = gots[0].shape
    n = len(reduced)
    jobs = []
    for index, array in enumerate(reduced):
        lead, depth, columns = array.shape
        step = 512 * 1024 // columns
        if index == n - 1:
            jobs += [(index, 0, at, depth // 2, columns) for at in range(0, depth, depth // 2)]
        else:
            jobs += [(index, part, at, step, columns) for part in range(lead) for at in range(0, depth, step)]
    jobs += [(n, m, 0, shard_rows, width) for m in range(seqs)] + [(n + 1, m, 0, shard_rows, width) for m in range(seqs)]
    ring = 3
    n_in = n + 2 * seqs + 3
    parts = units // width

    def kernel(*refs):
        ins = refs[:n]
        grad_refs = refs[n : n + 2 * seqs]
        got_refs = refs[n + 2 * seqs : n + 2 * seqs + 2]
        sums_ref = refs[n + 2 * seqs + 2]
        outs = refs[n_in : n_in + n + 1]
        qv_ref, out_bias_ref, gain_ref, shift_ref, ub_ref, down_bias_ref = refs[n_in + n + 1 : n_in + n + 7]
        shapes = sorted({(j[3], j[4]) for j in jobs if j[0] != n})
        buffers = refs[n_in + n + 7 :]
        wide_rows, in_sem, out_sem = buffers[0], buffers[1], buffers[2]
        low = {s: buffers[3 + 2 * i] for i, s in enumerate(shapes)}
        wide = {s: buffers[4 + 2 * i] for i, s in enumerate(shapes)}
        t = lax.axis_index("tensor")
        section = lax.axis_index("section")

        def load(number):
            index, part, at, rows, columns = jobs[number]
            s = number % ring
            if index < n:
                copy(ins[index].at[part, pl.ds(at, rows)], low[rows, columns].at[s], in_sem.at[s]).start()
            elif index == n:
                for turn in range(2):
                    @pl.when(section == turn)
                    def _(turn=turn):
                        source = grad_refs[turn * seqs + part].at[block(t, shard_rows)]
                        copy(source, wide_rows.at[part], in_sem.at[s]).start()
            else:
                for turn in range(2):
                    @pl.when(section == turn)
                    def _(turn=turn):
                        copy(got_refs[turn].at[part], low[rows, columns].at[s], in_sem.at[s]).start()

        def store(number):
            index, part, at, rows, columns = jobs[number]
            s = number % ring
            if index < n - 1:
                return copy(wide[rows, columns].at[s], outs[index].at[part, pl.ds(at, rows)], out_sem.at[s])
            if index == n - 1:
                return copy(wide[rows, columns].at[s], outs[index].at[:, pl.ds(at, rows)], out_sem.at[s])
            if index == n:
                return copy(wide_rows.at[part], outs[n].at[t * seqs + part], out_sem.at[s])
            return copy(wide[rows, columns].at[s], outs[n].at[(1 - t) * seqs + part], out_sem.at[s])

        for number in range(ring):
            load(number)
        gain_ref[0:1] = sums_ref[3:4]
        gain_ref[1:2] = sums_ref[0:1]
        shift_ref[0:1] = sums_ref[4:5]
        shift_ref[1:2] = sums_ref[1:2]
        out_bias_ref[...] = sums_ref[5:6]
        down_bias_ref[...] = sums_ref[2:3]
        for half in range(2):
            @pl.when(t == half)
            def _(half=half):
                for g in range(2):
                    for j in range(parts):
                        at = 6 + (2 * g + half) * parts + j
                        ub_ref[g : g + 1, j * width : (j + 1) * width] = sums_ref[at : at + 1]
                    at = 6 + 4 * parts + g
                    qv_ref[g : g + 1] = sums_ref[at : at + 1, half * local : (half + 1) * local]

        for number, (index, part, at, rows, columns) in enumerate(jobs):
            s = number % ring
            if index == n:
                arrived(wide_rows.at[part], in_sem.at[s])
            else:
                arrived(low[rows, columns].at[s], in_sem.at[s])
            if number >= ring:
                store(number - ring).wait()
            if index == n - 1:
                wide[rows, columns][s] = low[rows, columns][s].astype(F32).T
            elif index != n:
                wide[rows, columns][s] = low[rows, columns][s].astype(F32)
            store(number).start()
            if number + ring < len(jobs):
                load(number + ring)
        for number in range(len(jobs) - ring, len(jobs)):
            store(number).wait()

    shapes = sorted({(j[3], j[4]) for j in jobs if j[0] != n})
    square = (reduced[-1].shape[1] // 2, reduced[-1].shape[2])
    last = reduced[-1].shape
    sem = pltpu.SemaphoreType.DMA
    buffers = []
    for s in shapes:
        buffers += [pltpu.VMEM((ring,) + s, BF), pltpu.VMEM((ring,) + ((s[1], s[0]) if s == square else s), F32)]
    return pl.pallas_call(
        kernel,
        in_specs=[ANY] * (n + 2 * seqs + 2) + [WHOLE],
        out_specs=[ANY] * (n + 1) + [WHOLE] * 6,
        out_shape=[jax.ShapeDtypeStruct(r.shape, F32) for r in reduced[:-1]]
        + [jax.ShapeDtypeStruct((last[2], last[1]), F32), jax.ShapeDtypeStruct((2 * seqs, shard_rows, width), F32)]
        + [
            jax.ShapeDtypeStruct(shape, F32)
            for shape in ((2, local), (1, width), (2, width), (2, width), (2, units), (1, width))
        ],
        scratch_shapes=[pltpu.VMEM((seqs, shard_rows, width), F32), sem((ring,)), sem((ring,))] + buffers,
        compiler_params=pltpu.CompilerParams(vmem_limit_bytes=VMEM_LIMIT),
        cost_estimate=pl.CostEstimate(flops=0, bytes_accessed=56 << 20, transcendentals=0),
        name="widen",
    )(*reduced, *row_grads, *gots, sums)


MASKED = -1000000000.0


def shifted(value, axis, steps):
    count = lax.axis_size(axis)
    first, last = (max(0, -steps), min(count, count - steps))
    return lax.ppermute(value, axis, [(source, source + steps) for source in range(first, last)])


def layer_norm(values, gain, shift):
    mean = jnp.mean(values, axis=-1, keepdims=True)
    centred = values - mean
    spread = jnp.mean(centred * centred, axis=-1, keepdims=True)
    return centred * lax.rsqrt(spread + EPS) * gain + shift


def alibi_slopes(first, count, heads):
    index = (first + jnp.arange(count)).astype(jnp.float32)
    return jnp.exp2(-8.0 * (index + 1.0) / heads)


def attention_core(projected, qv_bias, slopes, key_ok):
    rows = projected.shape[0]
    width = projected.shape[2]
    count = slopes.shape[0]
    size = width // count
    query = (projected[:, 0] + qv_bias[0]).astype(jnp.bfloat16).reshape(rows, count, size)
    key = projected[:, 1].astype(jnp.bfloat16).reshape(rows, count, size)
    value = (projected[:, 2] + qv_bias[1]).astype(jnp.bfloat16).reshape(rows, count, size)
    place = jnp.arange(rows).astype(jnp.float32)
    distance = jnp.abs(place[:, None] - place[None, :])
    scale = 1.0 / math.sqrt(size)
    scores = (
        jnp.einsum("qhd,khd->hqk", query, key, preferred_element_type=jnp.float32) * scale
        - slopes[:, None, None] * distance[None]
    )
    scores = jnp.where(key_ok[None, None, :], scores, MASKED)
    weights = jax.nn.softmax(scores, axis=-1)
    weights_low = weights.astype(jnp.bfloat16)
    mixed = jnp.einsum("hqk,khd->qhd", weights_low, value, preferred_element_type=jnp.float32)
    mixed = mixed.reshape(rows, width).astype(jnp.bfloat16)
    return (query, key, value, weights, weights_low, mixed)


def attention_back(parts, grad_mixed, key_ok):
    query, key, value, weights, weights_low, mixed = parts
    rows, count, size = query.shape
    scale = 1.0 / math.sqrt(size)
    grad_low = grad_mixed.astype(jnp.bfloat16).reshape(rows, count, size)
    grad_weights = jnp.einsum("qhd,khd->hqk", grad_low, value, preferred_element_type=jnp.float32)
    grad_value = jnp.einsum(
        "hqk,qhd->khd", weights_low, grad_low, preferred_element_type=jnp.float32
    )
    inner = jnp.sum(weights * grad_weights, axis=-1, keepdims=True)
    grad_scores = weights * (grad_weights - inner)
    grad_scores = jnp.where(key_ok[None, None, :], grad_scores, 0.0).astype(jnp.bfloat16)
    grad_query = (
        jnp.einsum("hqk,khd->qhd", grad_scores, key, preferred_element_type=jnp.float32) * scale
    ).astype(jnp.bfloat16)
    grad_key = (
        jnp.einsum("hqk,qhd->khd", grad_scores, query, preferred_element_type=jnp.float32) * scale
    ).astype(jnp.bfloat16)
    grad_value = grad_value.astype(jnp.bfloat16)
    width = count * size
    grad_query = grad_query.reshape(rows, width)
    grad_key = grad_key.reshape(rows, width)
    grad_value = grad_value.reshape(rows, width)
    grad_projected = jnp.stack([grad_query, grad_key, grad_value], axis=1).reshape(rows, 3 * width)
    qv_grad = jnp.stack(
        [
            jnp.sum(grad_query.astype(jnp.float32), axis=0),
            jnp.sum(grad_value.astype(jnp.float32), axis=0),
        ]
    )
    return (grad_projected, qv_grad)


def gelu_product(both):
    return jax.nn.gelu(both[:, 0], approximate=False) * both[:, 1]


def geglu(lifted, up_bias):
    return gelu_product(lifted + up_bias[None])


def ffn_grads(rows_low, grad_low, up_weight, up_bias, down_weight):
    lifted = jnp.einsum("sd,gdf->sgf", rows_low, up_weight, preferred_element_type=jnp.float32)
    hidden, geglu_back = jax.vjp(gelu_product, lifted + up_bias[None])
    grad_hidden = jnp.einsum("sd,df->sf", grad_low, down_weight, preferred_element_type=jnp.float32)
    (grad_both,) = geglu_back(grad_hidden)
    grad_lifted = grad_both.astype(jnp.bfloat16)
    grad_bias = jnp.sum(grad_lifted.astype(jnp.float32), axis=0)
    up_grad = jnp.einsum("sd,sgf->gdf", rows_low, grad_lifted, preferred_element_type=jnp.float32)
    down_grad = jnp.einsum(
        "sd,sf->df", grad_low, hidden.astype(jnp.bfloat16), preferred_element_type=jnp.float32
    )
    return (grad_lifted, grad_bias, up_grad, down_grad)


def on_device(
    inputs,
    cotangent,
    lengths,
    w_qkv,
    b_qv,
    w_out,
    b_out,
    ln_gain,
    ln_bias,
    w_up,
    b_up,
    w_down,
    b_down,
):
    batches, shard_rows, width = inputs.shape
    parts = lax.axis_size("tensor")
    place = lax.axis_index("tensor")
    section = lax.axis_index("section")
    last_section = lax.axis_size("section") - 1
    full_rows = shard_rows * parts
    local_width = w_qkv.shape[3]
    local_heads = local_width // HD
    qkv_flat = w_qkv[0].reshape(width, 3 * local_width)
    out_weight = w_out[0]
    qv_bias = b_qv[0].astype(jnp.float32)
    out_bias = b_out[0].astype(jnp.float32)
    gains = ln_gain[0].astype(jnp.float32)
    shifts = ln_bias[0].astype(jnp.float32)
    down_bias = b_down[0].astype(jnp.float32)
    slopes = alibi_slopes(place * local_heads, local_heads, H)
    row_place = place * shard_rows + jnp.arange(shard_rows)
    kept_rows = 0

    def key_mask(length):
        return jnp.arange(full_rows) < length

    def after_attention(values, attended, bias, gain_rows, shift_rows):
        return layer_norm(values + attended + bias, gain_rows[0], shift_rows[0])

    def after_ffn(normed, lowered, bias, gain_rows, shift_rows):
        return layer_norm(normed + lowered + bias, gain_rows[1], shift_rows[1])

    def gather_inputs(values):
        return lax.all_gather(values.astype(jnp.bfloat16), "tensor", axis=0, tiled=True)

    def project(gathered):
        return jnp.dot(gathered, qkv_flat, preferred_element_type=jnp.float32).reshape(
            full_rows, 3, local_width
        )

    def attention_forward(values, length):
        gathered = gather_inputs(values)
        projected = project(gathered)
        mixed = attention_core(projected, qv_bias, slopes, key_mask(length))[5]

        def term(start, count):
            return jnp.dot(mixed, out_weight, preferred_element_type=jnp.float32)

        return (
            lax.psum_scatter(
                term(jnp.int32(0), shard_rows * lax.axis_size("tensor")).astype(jnp.bfloat16),
                "tensor",
                scatter_dimension=0,
                tiled=True,
            ).astype(jnp.float32),
            gathered,
            projected,
        )

    up_local = w_up[0]
    up_bias_local = b_up[0].astype(jnp.float32)
    down_local = w_down[0]

    def gather_normed(normed):
        return lax.all_gather(normed.astype(jnp.bfloat16), "tensor", axis=0, tiled=True)

    def ffn_forward(normed):
        lifted = jnp.einsum(
            "sd,gdf->sgf", gather_normed(normed), up_local, preferred_element_type=jnp.float32
        )
        hidden = geglu(lifted, up_bias_local).astype(jnp.bfloat16)

        def term(start, count):
            return jnp.einsum("sf,df->sd", hidden, down_local, preferred_element_type=jnp.float32)

        return lax.psum_scatter(
            term(jnp.int32(0), shard_rows * lax.axis_size("tensor")).astype(jnp.bfloat16),
            "tensor",
            scatter_dimension=0,
            tiled=True,
        ).astype(jnp.float32)

    def ffn_backward(normed, grad_lowered):
        gathered = gather_normed(normed)
        grad_whole = lax.all_gather(grad_lowered.astype(jnp.bfloat16), "tensor", axis=0, tiled=True)
        grad_lifted, grad_bias, up_grad, down_grad = ffn_grads(
            gathered, grad_whole, up_local, up_bias_local, down_local
        )

        def term(start, count):
            return jnp.einsum(
                "sgf,gdf->sd", grad_lifted, up_local, preferred_element_type=jnp.float32
            )

        grad_normed = lax.psum_scatter(
            term(jnp.int32(0), shard_rows * lax.axis_size("tensor")).astype(jnp.bfloat16),
            "tensor",
            scatter_dimension=0,
            tiled=True,
        ).astype(jnp.float32)
        return (grad_normed, (up_grad, grad_bias, down_grad))

    ffn_shapes = (up_local.shape, up_bias_local.shape, down_local.shape)

    def layer_forward(values, length):
        attended, gathered, projected = attention_forward(values, length)
        normed = after_attention(values, attended, out_bias, gains, shifts)
        lowered = ffn_forward(normed)
        return (
            after_ffn(normed, lowered, down_bias, gains, shifts),
            attended,
            lowered,
            gathered,
            projected,
        )

    def layer_backward(values, attended, lowered, length, grad_output):
        normed, attention_norm_back = jax.vjp(
            after_attention, values, attended, out_bias, gains, shifts
        )
        outcome, ffn_norm_back = jax.vjp(after_ffn, normed, lowered, down_bias, gains, shifts)
        grad_normed, grad_lowered, grad_down_bias, gain_late, shift_late = ffn_norm_back(
            grad_output
        )
        grad_from_ffn, ffn_terms = ffn_backward(normed, grad_lowered)
        grad_values, grad_attended, grad_out_bias, gain_early, shift_early = attention_norm_back(
            grad_normed + grad_from_ffn
        )
        gathered = gather_inputs(values)
        projected = project(gathered)
        grad_whole = lax.all_gather(
            grad_attended.astype(jnp.bfloat16), "tensor", axis=0, tiled=True
        )
        mask = key_mask(length)
        pieces = attention_core(projected, qv_bias, slopes, mask)
        mixed_low = pieces[5]
        out_grad = jnp.einsum(
            "se,sd->ed", mixed_low, grad_whole, preferred_element_type=jnp.float32
        )
        grad_mixed = jnp.einsum(
            "sd,ed->se", grad_whole, out_weight, preferred_element_type=jnp.float32
        )
        grad_projected, qv_grad = attention_back(pieces, grad_mixed, mask)
        qkv_grad = jnp.einsum(
            "sd,sx->dx", gathered, grad_projected, preferred_element_type=jnp.float32
        )

        def term(start, count):
            return jnp.einsum(
                "sx,dx->sd", grad_projected, qkv_flat, preferred_element_type=jnp.float32
            )

        grad_inputs = grad_values + lax.psum_scatter(
            term(jnp.int32(0), shard_rows * lax.axis_size("tensor")).astype(jnp.bfloat16),
            "tensor",
            scatter_dimension=0,
            tiled=True,
        ).astype(jnp.float32)
        terms = (
            qkv_grad,
            qv_grad,
            out_grad,
            grad_out_bias,
            gain_early + gain_late,
            shift_early + shift_late,
            ffn_terms[0],
            ffn_terms[1],
            ffn_terms[2],
            grad_down_bias,
        )
        return (grad_inputs, terms)

    def keep(store, item, batch, valid):
        old = lax.dynamic_index_in_dim(store, batch, 0, keepdims=False)
        return lax.dynamic_update_index_in_dim(store, jnp.where(valid, item, old), batch, 0)

    def forward_step(step, carry):
        (
            received,
            kept_values,
            kept_attended,
            kept_lowered,
            produced,
            kept_gathered,
            kept_projected,
        ) = carry
        index = step - section
        valid = (index >= 0) & (index < batches)
        batch = jnp.clip(index, 0, batches - 1)
        fresh = lax.dynamic_index_in_dim(
            inputs, jnp.minimum(step, batches - 1), 0, keepdims=False
        ).astype(jnp.float32)
        values = jnp.where(section == 0, fresh, received.astype(jnp.float32))
        output, attended, lowered, gathered, projected = layer_forward(values, lengths[batch])
        sent = output.astype(jnp.bfloat16)
        kept_values = keep(kept_values, values, batch, valid)
        kept_attended = keep(kept_attended, attended, batch, valid)
        kept_lowered = keep(kept_lowered, lowered, batch, valid)
        produced = keep(produced, sent, batch, valid)
        kept_gathered = keep(kept_gathered, gathered[:kept_rows], batch, valid)
        kept_projected = keep(kept_projected, projected[:kept_rows], batch, valid)
        received = shifted(sent, "section", 1)
        return (
            received,
            kept_values,
            kept_attended,
            kept_lowered,
            produced,
            kept_gathered,
            kept_projected,
        )

    store_zeros = jnp.zeros((batches, shard_rows, width), jnp.float32)
    gathered_zeros = jnp.zeros((batches, kept_rows, width), jnp.bfloat16)
    projected_zeros = jnp.zeros((batches, kept_rows, 3, local_width), jnp.float32)
    start_forward = (
        jnp.zeros((shard_rows, width), jnp.bfloat16),
        store_zeros,
        store_zeros,
        store_zeros,
        jnp.zeros((batches, shard_rows, width), jnp.bfloat16),
        gathered_zeros,
        projected_zeros,
    )
    received, kept_values, kept_attended, kept_lowered, produced, kept_gathered, kept_projected = (
        lax.fori_loop(0, batches + last_section, forward_step, start_forward)
    )

    def backward_step(step, carry):
        received, totals, grads_in = carry
        index = step - (last_section - section)
        valid = (index >= 0) & (index < batches)
        batch = jnp.clip(index, 0, batches - 1)
        length = lengths[batch]
        outer = lax.dynamic_index_in_dim(cotangent, batch, 0, keepdims=False).astype(jnp.float32)
        outer = outer * (row_place < length).astype(jnp.float32)[:, None]
        grad_output = jnp.where(section == last_section, outer, received.astype(jnp.float32))
        grad_output = jnp.where(valid, grad_output, 0.0)
        values = lax.dynamic_index_in_dim(kept_values, batch, 0, keepdims=False)
        attended = lax.dynamic_index_in_dim(kept_attended, batch, 0, keepdims=False)
        lowered = lax.dynamic_index_in_dim(kept_lowered, batch, 0, keepdims=False)
        grad_inputs, terms = layer_backward(values, attended, lowered, length, grad_output)
        totals = jax.tree.map(jnp.add, totals, terms)
        grads_in = keep(grads_in, grad_inputs, batch, valid)
        received = shifted(grad_inputs.astype(jnp.bfloat16), "section", -1)
        return (received, totals, grads_in)

    start_totals = (
        jnp.zeros((width, 3 * local_width), jnp.float32),
        jnp.zeros((2, local_width), jnp.float32),
        jnp.zeros((local_width, width), jnp.float32),
        jnp.zeros((width,), jnp.float32),
        jnp.zeros((2, width), jnp.float32),
        jnp.zeros((2, width), jnp.float32),
        jnp.zeros(ffn_shapes[0], jnp.float32),
        jnp.zeros(ffn_shapes[1], jnp.float32),
        jnp.zeros(ffn_shapes[2], jnp.float32),
        jnp.zeros((width,), jnp.float32),
    )
    start_backward = (jnp.zeros((shard_rows, width), jnp.bfloat16), start_totals, store_zeros)
    received, totals, grads_in = lax.fori_loop(
        0, batches + last_section, backward_step, start_backward
    )
    (
        qkv_total,
        qv_total,
        out_total,
        out_bias_total,
        gain_total,
        shift_total,
        up_total,
        up_bias_total,
        down_total,
        down_bias_total,
    ) = totals
    qkv_sum, qv_sum, out_sum, up_sum, up_bias_sum, down_sum = (
        lax.psum(qkv_total.astype(jnp.bfloat16), "dp").astype(jnp.float32),
        lax.psum(qv_total.astype(jnp.bfloat16), "dp").astype(jnp.float32),
        lax.psum(out_total.astype(jnp.bfloat16), "dp").astype(jnp.float32),
        lax.psum(up_total.astype(jnp.bfloat16), "dp").astype(jnp.float32),
        lax.psum(up_bias_total.astype(jnp.bfloat16), "dp").astype(jnp.float32),
        lax.psum(down_total.astype(jnp.bfloat16), "dp").astype(jnp.float32),
    )
    out_bias_sum, gain_sum, shift_sum, down_bias_sum = lax.psum(
        (out_bias_total, gain_total, shift_total, down_bias_total), ("tensor", "dp")
    )
    return (
        produced[None],
        grads_in[None],
        qkv_sum.reshape(1, width, 3, local_width),
        qv_sum[None],
        out_sum[None],
        out_bias_sum[None],
        gain_sum[None],
        shift_sum[None],
        up_sum[None],
        up_bias_sum[None],
        down_sum[None],
        down_bias_sum[None],
    )


def by_sequence(
    inputs,
    cotangent,
    lengths,
    w_qkv,
    b_qv,
    w_out,
    b_out,
    ln_gain,
    ln_bias,
    w_up,
    b_up,
    w_down,
    b_down,
):
    batches, shard_rows, width = inputs.shape
    place = lax.axis_index("tensor")
    section = lax.axis_index("section")
    groups = lax.axis_size("dp")
    rows = 2 * shard_rows
    seqs = batches // 2
    local = w_qkv.shape[3]
    units = w_up.shape[3]
    heads = local // HD
    chips = groups // 2

    qkv_own = jnp.transpose(w_qkv[0], (1, 0, 2))
    out_own = w_out[0]
    up_own = w_up[0]
    down_own = w_down[0]
    first = section == 0
    qkv_oth, out_oth, up_oth, down_oth, bias, up_bias, *held = fetch_other_half(
        qkv_own.reshape(3 * width, local),
        out_own,
        up_own.reshape(2 * width, units),
        down_own,
        b_qv[0],
        b_up[0],
        inputs,
        cotangent,
        chips,
    )
    qkv_oth = qkv_oth.reshape(3, width, local)
    up_oth = up_oth.reshape(2, width, units)
    x_first = outer = held

    vecs = jnp.stack(
        [b_out[0], ln_gain[0, 0], ln_bias[0, 0], b_down[0], ln_gain[0, 1], ln_bias[0, 1], b_out[0], b_out[0]]
    ).astype(F32)
    slope_table = np.exp2(-8.0 * (np.arange(2 * heads, dtype=np.float32) + 1.0) / H).astype(np.float32)
    slopes = jnp.where(place == 0, slope_table, np.roll(slope_table, heads))
    own_lengths = lax.dynamic_slice_in_dim(lengths, place * seqs, seqs, 0)

    def meta(m, turn):
        active = section == turn
        return jnp.stack([jnp.int32(m), active.astype(jnp.int32), own_lengths[m], own_lengths[m] if turn == 1 else jnp.int32(rows)])

    metas = [[meta(m, turn) for m in range(seqs)] for turn in range(2)]
    weights = (qkv_own, qkv_oth, out_own, out_oth, up_own, up_oth, down_own, down_oth)
    kept = None
    deps = []

    def forward(x, m, turn):
        nonlocal kept, deps
        *kept, y = layer_forward(x, weights, bias, slopes, vecs, up_bias, metas[turn][m], kept, deps, seqs)
        deps = [y]
        return y

    y_first = [forward(x_first[m], m, 0) for m in range(seqs)]
    x_second = [lax.ppermute(y, "section", [(0, 1)]) for y in y_first]
    y_second = [forward(x_second[0], 0, 1)]
    (produced,) = exchange_rows(y_first, [], 0, [], deps)
    deps = [produced]
    y_second += [forward(x_second[m], m, 1) for m in range(1, seqs)]

    back = None
    sums = [[None] * seqs, [None] * seqs]

    def backward(grad, m, turn):
        nonlocal back, deps
        *back, gx, gx_low, norm_sums, up_sums, qv_sums = layer_backward(
            grad, kept, weights, slopes, vecs, metas[turn][m], back, deps, seqs
        )
        deps = [norm_sums]
        sums[turn][m] = (norm_sums, up_sums, qv_sums)
        return gx, gx_low

    gx_second = [backward(outer[m], m, 1) for m in range(seqs)]
    grad_middle = [lax.ppermute(gx_second[m][1], "section", [(1, 0)]) for m in range(seqs)]
    x_all = jnp.stack([jnp.where(first, x_first[m], x_second[m]) for m in range(seqs)])
    deps = deps + [x_all]
    gx_first = [backward(grad_middle[m], m, 0) for m in range(seqs)]
    produced, got_second = exchange_rows(y_second, [g[1] for g in gx_second], 1, [produced], deps)

    mixed, hidden, normed = kept[3], kept[7], kept[8]
    gg0, gg1, gl, ga, *gqkv = back

    picked = [
        sum(jnp.where(first, sums[0][m][index], sums[1][m][index]) for m in range(seqs))
        for index in range(3)
    ]
    norm_sums, up_sums, qv_sums = picked

    def ordered(values, count):
        return jnp.where(
            place == 0, values, jnp.concatenate([values[:, count:], values[:, :count]], axis=1)
        ).reshape(-1, width)

    packed = jnp.concatenate([norm_sums[:6], ordered(up_sums[:2], units), ordered(qv_sums[:2], local)])
    *reduced, packed, got_first = weight_grads_reduced(
        [(gl, [hidden]), (normed, [gg0, gg1]), (x_all, gqkv), (ga, [mixed])], packed, [g[1] for g in gx_first], chips
    )
    down_sum, up_sum, qkv_sum, out_sum, grads_in, qv_sum, out_bias_sum, gain_sum, shift_sum, up_bias_sum, down_bias_sum = (
        widen(reduced, [g[0] for g in gx_first + gx_second], [got_first, got_second], packed, units, local)
    )
    return (
        produced[None],
        grads_in[None],
        jnp.transpose(qkv_sum, (1, 0, 2))[None],
        qv_sum[None],
        out_sum[None],
        out_bias_sum,
        gain_sum[None],
        shift_sum[None],
        up_sum[None],
        up_bias_sum[None],
        down_sum,
        down_bias_sum,
    )


def solution(mesh):
    sections, parts, groups = (mesh.shape[name] for name in ("section", "tensor", "dp"))

    def run(*args):
        paired = sections == 2 and parts == 2 and groups % 2 == 0 and args[0].shape[0] == 4
        return (by_sequence if paired else on_device)(*args)

    return jax.shard_map(
        run,
        mesh=mesh,
        in_specs=(
            P("dp", "tensor", None),
            P("dp", "tensor", None),
            P("dp"),
            P("section", None, None, "tensor"),
            P("section", None, "tensor"),
            P("section", "tensor", None),
            P("section", None),
            P("section", None, None),
            P("section", None, None),
            P("section", None, None, "tensor"),
            P("section", None, "tensor"),
            P("section", None, "tensor"),
            P("section", None),
        ),
        out_specs=(
            P("section", "dp", "tensor", None),
            P("section", "dp", "tensor", None),
            P("section", None, None, "tensor"),
            P("section", None, "tensor"),
            P("section", "tensor", None),
            P("section", None),
            P("section", None, None),
            P("section", None, None),
            P("section", None, None, "tensor"),
            P("section", None, "tensor"),
            P("section", None, "tensor"),
            P("section", None),
        ),
        check_vma=False,
    )
```

```python
import math

import jax
import jax.numpy as jnp
import numpy as np
from jax import lax
from jax.experimental import pallas as pl
from jax.experimental.pallas import tpu as pltpu
from jax.sharding import PartitionSpec as P

H = 16
HD = 64
EPS = 1e-05
BF = jnp.bfloat16
F32 = jnp.float32
VMEM_LIMIT = 62 * 1024 * 1024
ANY = pl.BlockSpec(memory_space=pl.ANY)
SMEM = pl.BlockSpec(memory_space=pltpu.SMEM)
WHOLE = pl.BlockSpec(memory_space=pltpu.VMEM)
NN = (((1,), (0,)), ((), ()))
NT = (((1,), (1,)), ((), ()))
TN = (((0,), (0,)), ((), ()))
CW = 256
PER = CW // HD


def dot(a, b, dims=NN):
    return lax.dot_general(a, b, dims, preferred_element_type=F32)


def arrived(ref, sem):
    pltpu.make_async_copy(ref, ref, sem).wait()


def call(kernel, inputs, outputs, scratch, meta, chain, deps, name, flops, nbytes):
    pairs = [item if isinstance(item, tuple) else (item, ANY) for item in inputs]
    args = [meta] + [p[0] for p in pairs]
    specs = [SMEM] + [p[1] for p in pairs]
    n_in = len(args)
    aliases = {}
    if chain is not None:
        for buffer, index in zip(chain, [index for index, item in enumerate(outputs) if item[2]]):
            aliases[len(args)] = index
            args.append(buffer)
            specs.append(ANY)
    args += deps
    specs += [ANY] * len(deps)
    n_args, n_out = len(args), len(outputs)

    def body(*refs):
        @pl.when(refs[0][1] == 1)
        def _():
            kernel(refs[0], refs[1:n_in], refs[n_args : n_args + n_out], refs[n_args + n_out :])

    return pl.pallas_call(
        body,
        in_specs=specs,
        out_specs=[ANY] * n_out,
        out_shape=[jax.ShapeDtypeStruct(o[0], o[1]) for o in outputs],
        scratch_shapes=scratch,
        input_output_aliases=aliases,
        compiler_params=pltpu.CompilerParams(vmem_limit_bytes=VMEM_LIMIT),
        cost_estimate=pl.CostEstimate(flops=flops, bytes_accessed=nbytes, transcendentals=0),
        name=name,
    )(*args)


def pick(k, count, own, oth, make):
    @pl.when(k < count)
    def _():
        for src, dst, sem in make(own, k):
            pltpu.make_async_copy(src, dst, sem).start()

    @pl.when(k >= count)
    def _():
        for src, dst, sem in make(oth, k - count):
            pltpu.make_async_copy(src, dst, sem).start()


def block(index, size):
    return pl.ds(pl.multiple_of(index * size, size), size)


def copy(src, dst, sem):
    return pltpu.make_async_copy(src, dst, sem)


def fill_distance(dist_ref, length):
    rows = dist_ref.shape[0]
    keys = lax.broadcasted_iota(jnp.int32, (rows, rows), 0)
    places = lax.broadcasted_iota(jnp.int32, (rows, rows), 1)
    distance = jnp.abs(keys - places).astype(F32)
    dist_ref[...] = jnp.where(keys < length, distance, 1e12)


def normalize(v):
    mean = jnp.mean(v, axis=1, keepdims=True)
    centred = v - mean
    rstd = lax.rsqrt(jnp.mean(centred * centred, axis=1, keepdims=True) + EPS)
    return centred * rstd, rstd


def halves(rows):
    return [slice(0, rows // 2), slice(rows // 2, rows)]


class Forward:
    def __init__(self, rows, width, local, units):
        self.rows, self.width, self.local, self.units = rows, width, local, units
        self.ft = min(512, units)
        self.tiles = units // self.ft
        self.heads_steps = local // CW
        self.total = 2 * local

    def kept(self, slots):
        rows, width = self.rows, self.width
        shapes = [((slots, rows, self.total), BF)] * 4
        shapes += [((slots, 2 * self.heads_steps, 8, rows), F32)]
        shapes += [((slots, rows, 2 * self.units), BF)] * 3
        return shapes + [((slots, rows, width), BF)] * 3 + [((slots, rows, 128), F32)] * 2

    def scratch(self):
        rows, width, ft, total = self.rows, self.width, self.ft, self.total
        sem = pltpu.SemaphoreType.DMA
        return [
            pltpu.VMEM((rows, width), BF),
            pltpu.VMEM((2, 3, width, CW), BF),
            pltpu.VMEM((total, width), BF),
            pltpu.VMEM((2, 2, width, ft), BF),
            pltpu.VMEM((2, width, ft), BF),
            pltpu.VMEM((2, 3, rows, CW), BF),
            pltpu.VMEM((2, 8, rows), F32),
            pltpu.VMEM((rows, total), BF),
            pltpu.VMEM((rows, rows), F32),
            pltpu.VMEM((rows, width), F32),
            pltpu.VMEM((rows, width), F32),
            pltpu.VMEM((rows, width), BF),
            pltpu.VMEM((2, 3, rows, ft), BF),
            pltpu.VMEM((3, rows, width), BF),
            pltpu.VMEM((2, rows, 128), F32),
            sem, sem((2,)), sem((2,)), sem((2, 2)), sem((2, 4)), sem, sem((2, 3)), sem((6,)),
        ]

    def bind(self, x, weights, bias, slopes, vecs, up_bias, slot, outs, scratch):
        self.x_hbm, self.weights, self.bias, self.slopes, self.vecs, self.up_bias = x, weights, bias, slopes, vecs, up_bias
        self.slot, self.outs = slot, outs
        (self.x, self.w, self.o, self.up, self.down, self.qkv, self.lse, self.mixed, self.dist, self.normed, self.acc,
         self.low, self.tile, self.row, self.stat, self.x_sem, self.w_sem, self.o_sem, self.f_sem, self.q_sem, self.m_sem,
         self.t_sem, self.r_sem) = scratch

    def start_x(self):
        copy(self.x_hbm, self.x, self.x_sem).start()

    def start_w(self, k):
        s = lax.rem(k, 2)
        pick(k, self.heads_steps, self.weights[0], self.weights[1],
             lambda ref, j: [(ref.at[:, :, block(j, CW)], self.w.at[s], self.w_sem.at[s])])

    def start_o(self, side):
        copy(self.weights[2 + side], self.o.at[pl.ds(side * self.local, self.local)], self.o_sem.at[side]).start()

    def start_f(self, k):
        s = lax.rem(k, 2)
        ft = self.ft
        pick(k, self.tiles, (self.weights[4], self.weights[6]), (self.weights[5], self.weights[7]),
             lambda ref, j: [(ref[0].at[:, :, block(j, ft)], self.up.at[s], self.f_sem.at[s, 0]),
                             (ref[1].at[:, block(j, ft)], self.down.at[s], self.f_sem.at[s, 1])])

    def write_qkv(self, i, s):
        cols = block(i, CW)
        return [copy(self.qkv.at[s, c], out.at[self.slot, :, cols], self.q_sem.at[s, c])
                for c, out in enumerate(self.outs[:3])] + [
            copy(self.lse.at[s], self.outs[4].at[self.slot, i], self.q_sem.at[s, 3])]

    def attention_step(self, i, ahead):
        s = lax.rem(i, 2)
        qkv = self.qkv
        arrived(self.w.at[s], self.w_sem.at[s])

        @pl.when(i >= 2)
        def _():
            for item in self.write_qkv(i - 2, s):
                item.wait()

        values = self.x[...]
        b = self.bias[:, block(i, CW)].astype(F32)
        qkv[s, 0] = (dot(values, self.w[s, 0]) + b[0:1]).astype(BF)
        qkv[s, 1] = dot(values, self.w[s, 1]).astype(BF)
        qkv[s, 2] = (dot(values, self.w[s, 2]) + b[1:2]).astype(BF)

        @pl.when(i + 2 < ahead)
        def _():
            self.start_w(i + 2)

        parts = []
        for head in range(PER):
            cols = slice(head * HD, (head + 1) * HD)
            query = qkv[s, 0, :, cols] * BF(1.0 / math.sqrt(HD))
            scores = dot(qkv[s, 1, :, cols], query, NT)
            scores = scores - self.dist[...] * self.slopes[i * PER + head]
            top = jnp.max(scores, axis=0, keepdims=True)
            likely = jnp.exp(scores - top)
            mass = jnp.sum(likely, axis=0, keepdims=True)
            low = (likely * (1.0 / mass)).astype(BF)
            parts.append(dot(low, qkv[s, 2, :, cols], TN).astype(BF))
            self.lse[s, head : head + 1, :] = top + jnp.log(mass)
        self.mixed[:, block(i, CW)] = jnp.concatenate(parts, axis=1)
        for item in self.write_qkv(i, s):
            item.start()

    def middle(self):
        rows, width = self.rows, self.width
        copy(self.mixed, self.outs[3].at[self.slot], self.m_sem).start()
        for side in range(2):
            arrived(self.o.at[pl.ds(side * self.local, self.local)], self.o_sem.at[side])
        vec = self.vecs[...]
        for rs in halves(rows):
            attended = dot(self.mixed[rs, :], self.o[...])
            u, rstd = normalize(self.x[rs, :].astype(F32) + attended + vec[0:1])
            normed = u * vec[1:2] + vec[2:3]
            self.normed[rs, :] = normed
            self.low[rs, :] = normed.astype(BF)
            self.row[0, rs, :] = u.astype(BF)
            self.stat[0, rs, :] = jnp.broadcast_to(rstd, (rows // 2, 128))
            self.acc[rs, :] = jnp.zeros((rows // 2, width), F32)
        for index, item in enumerate(self.first_rows()):
            copy(*item, self.r_sem.at[index]).start()

    def first_rows(self):
        return [(self.low, self.outs[8].at[self.slot]), (self.row.at[0], self.outs[9].at[self.slot]),
                (self.stat.at[0], self.outs[11].at[self.slot])]

    def write_tiles(self, i, s):
        return [copy(self.tile.at[s, c], out.at[self.slot, :, block(i, self.ft)], self.t_sem.at[s, c])
                for c, out in enumerate(self.outs[5:8])]

    def ffn_step(self, i, ahead):
        s = lax.rem(i, 2)
        arrived(self.up.at[s], self.f_sem.at[s, 0])
        arrived(self.down.at[s], self.f_sem.at[s, 1])

        @pl.when(i >= 2)
        def _():
            for item in self.write_tiles(i - 2, s):
                item.wait()

        b = self.up_bias[:, block(i, self.ft)].astype(F32)
        low = self.low[...]
        gate = dot(low, self.up[s, 0]) + b[0:1]
        lift = dot(low, self.up[s, 1]) + b[1:2]
        cdf = 0.5 * lax.erf(gate * (1.0 / math.sqrt(2.0))) + 0.5
        act = gate * cdf
        slope = cdf + gate * (jnp.exp(gate * gate * -0.5) * (1.0 / math.sqrt(2.0 * math.pi)))
        self.tile[s, 0] = act.astype(BF)
        self.tile[s, 1] = (lift * slope).astype(BF)
        hidden = (act * lift).astype(BF)
        self.tile[s, 2] = hidden
        self.acc[...] += dot(hidden, self.down[s], NT)

        @pl.when(i + 2 < ahead)
        def _():
            self.start_f(i + 2)

        for item in self.write_tiles(i, s):
            item.start()

    def finish(self, y_out):
        rows = self.rows
        vec = self.vecs[...]
        for rs in halves(rows):
            u, rstd = normalize(self.normed[rs, :] + self.acc[rs, :] + vec[3:4])
            self.row[1, rs, :] = u.astype(BF)
            self.stat[1, rs, :] = jnp.broadcast_to(rstd, (rows // 2, 128))
            self.row[2, rs, :] = (u * vec[4:5] + vec[5:6]).astype(BF)
        ends = [(self.row.at[1], self.outs[10].at[self.slot]), (self.stat.at[1], self.outs[12].at[self.slot]),
                (self.row.at[2], y_out)]
        for index, item in enumerate(ends):
            copy(*item, self.r_sem.at[3 + index]).start()
        for index, item in enumerate(self.first_rows() + ends):
            copy(*item, self.r_sem.at[index]).wait()
        copy(self.mixed, self.outs[3].at[self.slot], self.m_sem).wait()
        for i in (2 * self.heads_steps - 2, 2 * self.heads_steps - 1):
            for item in self.write_qkv(jnp.int32(i), i % 2):
                item.wait()
        for i in (2 * self.tiles - 2, 2 * self.tiles - 1):
            for item in self.write_tiles(jnp.int32(i), i % 2):
                item.wait()

    def flops(self):
        rows, width, total = self.rows, self.width, self.total
        return 2 * rows * width * (4 * total + 6 * self.units) + 4 * rows * rows * total


def layer_forward(x, weights, bias, slopes, vecs, up_bias, meta, chain, deps, slots):
    rows, width = x.shape
    step = Forward(rows, width, weights[0].shape[2], weights[4].shape[2])

    def kernel(meta_ref, ins, outs, scratch):
        step.bind(ins[0], ins[1:9], *ins[9:13], meta_ref[0], outs[:13], scratch)
        step.start_x()
        for k in range(2):
            step.start_w(jnp.int32(k))
        for side in range(2):
            step.start_o(side)
        for k in range(2):
            step.start_f(jnp.int32(k))
        fill_distance(step.dist, meta_ref[2])
        arrived(step.x, step.x_sem)

        @pl.loop(0, 2 * step.heads_steps)
        def _(i):
            step.attention_step(i, 2 * step.heads_steps)

        step.middle()

        @pl.loop(0, 2 * step.tiles)
        def _(i):
            step.ffn_step(i, 2 * step.tiles)

        step.finish(outs[13])

    return call(
        kernel,
        [x, *weights, (bias, WHOLE), (slopes, SMEM), (vecs, WHOLE), (up_bias, WHOLE)],
        [shape + (True,) for shape in step.kept(slots)] + [((rows, width), BF, False)],
        step.scratch(),
        meta,
        chain,
        deps,
        "layer_forward",
        step.flops(),
        54 << 20,
    )


def layer_backward(grad, kept, weights, slopes, vecs, meta, chain, deps, slots):
    qkv_own, qkv_oth, o_own, o_oth, up_own, up_oth, down_own, down_oth = weights
    q, k, v, _, lse, act, slope, _, _, u1, u2, r1, r2 = kept
    rows, width = grad.shape
    local = qkv_own.shape[2]
    units = up_own.shape[2]
    heads_steps = local // CW
    ft = min(512, units)
    tiles = units // ft
    total = 2 * local

    def norm_back(grad_z, u, rstd, gain):
        t = grad_z * gain
        return rstd * (t - jnp.mean(t, axis=1, keepdims=True) - u * jnp.mean(t * u, axis=1, keepdims=True))

    def row_sum(values):
        return jnp.sum(values, axis=0, keepdims=True)

    def kernel(meta_ref, ins, outs, scratch):
        (g_hbm, q_hbm, k_hbm, v_hbm, lse_hbm, a_hbm, b_hbm, u1_hbm, u2_hbm, r1_hbm, r2_hbm,
         qkv_own_ref, qkv_oth_ref, o_own_ref, o_oth_ref, up_own_ref, up_oth_ref, down_own_ref, down_oth_ref,
         slope_ref, vec_ref) = ins
        gg0_out, gg1_out, gl_out, ga_out, gq_out, gk_out, gv_out, gx_out, gxl_out, sums_out, ub_out, qv_out = outs
        (g_ref, u_ref, r_ref, up_ref, down_ref, ab_ref, gg_ref, low_ref, acc_ref, sums_ref, ub_ref, qv_ref,
         w_ref, o_ref, qkv_ref, lse_ref, gm_ref, dist_ref, gqkv_ref,
         g_sem, f_sem, t_sem, w_sem, q_sem, r_sem) = scratch
        slot = meta_ref[0]

        def start_f(i):
            s = lax.rem(i, 2)
            pick(i, tiles, (up_own_ref, down_own_ref), (up_oth_ref, down_oth_ref),
                 lambda ref, j: [(ref[0].at[:, :, block(j, ft)], up_ref.at[s], f_sem.at[s, 0]),
                                 (ref[1].at[:, block(j, ft)], down_ref.at[s], f_sem.at[s, 1])])
            for c, ref in enumerate((a_hbm, b_hbm)):
                copy(ref.at[slot, :, block(i, ft)], ab_ref.at[s, c], f_sem.at[s, 2 + c]).start()

        def start_w(i):
            s = lax.rem(i, 2)
            pick(i, heads_steps, (qkv_own_ref, o_own_ref), (qkv_oth_ref, o_oth_ref),
                 lambda ref, j: [(ref[0].at[:, :, block(j, CW)], w_ref.at[s], w_sem.at[s, 0]),
                                 (ref[1].at[block(j, CW)], o_ref.at[s], w_sem.at[s, 1])])
            for c, ref in enumerate((q_hbm, k_hbm, v_hbm)):
                copy(ref.at[slot, :, block(i, CW)], qkv_ref.at[s, c], w_sem.at[s, 2 + c]).start()
            copy(lse_hbm.at[slot, i], lse_ref.at[s], w_sem.at[s, 5]).start()

        firsts = [(g_hbm, g_ref), (u2_hbm.at[slot], u_ref.at[1]), (r2_hbm.at[slot], r_ref.at[1]),
                  (u1_hbm.at[slot], u_ref.at[0]), (r1_hbm.at[slot], r_ref.at[0])]
        for index, (src, dst) in enumerate(firsts):
            copy(src, dst, g_sem.at[index]).start()
            if index == 2:
                start_f(jnp.int32(0))
                start_f(jnp.int32(1))
        start_w(jnp.int32(0))
        start_w(jnp.int32(1))
        vec = vec_ref[...]
        fill_distance(dist_ref, meta_ref[2])
        for index, (src, dst) in enumerate(firsts[:3]):
            copy(src, dst, g_sem.at[index]).wait()
        sums = [jnp.zeros((1, width), F32)] * 3
        for rs in halves(rows):
            places = lax.broadcasted_iota(jnp.int32, (rows // 2, width), 0) + rs.start
            grad_y = jnp.where(places < meta_ref[3], g_ref[rs, :].astype(F32), 0.0)
            u = u_ref[1, rs, :].astype(F32)
            grad_c = norm_back(grad_y, u, r_ref[1, rs, 0:1], vec[4:5])
            acc_ref[rs, :] = grad_c
            low_ref[0, rs, :] = grad_c.astype(BF)
            for index, values in enumerate((grad_y * u, grad_y, grad_c)):
                sums[index] += row_sum(values)
        for index in range(3):
            sums_ref[index : index + 1, :] = sums[index]
        copy(low_ref.at[0], gl_out.at[slot], r_sem.at[0]).start()

        def write_tiles(i, s):
            return [copy(gg_ref.at[s, c], out.at[slot, :, block(i, ft)], t_sem.at[s, c])
                    for c, out in enumerate((gg0_out, gg1_out))]

        @pl.loop(0, 2 * tiles)
        def _(i):
            s = lax.rem(i, 2)
            arrived(up_ref.at[s], f_sem.at[s, 0])
            arrived(down_ref.at[s], f_sem.at[s, 1])
            for c in range(2):
                arrived(ab_ref.at[s, c], f_sem.at[s, 2 + c])

            @pl.when(i >= 2)
            def _():
                for item in write_tiles(i - 2, s):
                    item.wait()

            gh = dot(low_ref[0], down_ref[s])
            g0 = (gh * ab_ref[s, 1].astype(F32)).astype(BF)
            g1 = (gh * ab_ref[s, 0].astype(F32)).astype(BF)
            gg_ref[s, 0] = g0
            gg_ref[s, 1] = g1
            ub_ref[0:1, block(i, ft)] = row_sum(g0.astype(F32))
            ub_ref[1:2, block(i, ft)] = row_sum(g1.astype(F32))
            acc_ref[...] += dot(g0, up_ref[s, 0], NT) + dot(g1, up_ref[s, 1], NT)

            @pl.when(i + 2 < 2 * tiles)
            def _():
                start_f(i + 2)

            for item in write_tiles(i, s):
                item.start()

        for index, (src, dst) in enumerate(firsts[3:]):
            copy(src, dst, g_sem.at[3 + index]).wait()
        sums = [jnp.zeros((1, width), F32)] * 3
        for rs in halves(rows):
            grad_n = acc_ref[rs, :]
            u = u_ref[0, rs, :].astype(F32)
            grad_a = norm_back(grad_n, u, r_ref[0, rs, 0:1], vec[1:2])
            low_ref[1, rs, :] = grad_a.astype(BF)
            acc_ref[rs, :] = grad_a
            for index, values in enumerate((grad_n * u, grad_n, grad_a)):
                sums[index] += row_sum(values)
        for index in range(3):
            sums_ref[3 + index : 4 + index, :] = sums[index]
        sums_ref[6:8, :] = jnp.zeros((2, width), F32)
        copy(low_ref.at[1], ga_out.at[slot], r_sem.at[1]).start()
        scale = BF(1.0 / math.sqrt(HD))

        def write_heads(i, s):
            return [copy(gqkv_ref.at[s, c], out.at[slot, :, block(i, CW)], q_sem.at[s, c])
                    for c, out in enumerate((gq_out, gk_out, gv_out))]

        @pl.loop(0, 2 * heads_steps)
        def _(i):
            s = lax.rem(i, 2)
            for index, ref in enumerate((w_ref.at[s], o_ref.at[s], qkv_ref.at[s, 0], qkv_ref.at[s, 1], qkv_ref.at[s, 2], lse_ref.at[s])):
                arrived(ref, w_sem.at[s, index])

            @pl.when(i >= 2)
            def _():
                for item in write_heads(i - 2, s):
                    item.wait()

            gm_ref[...] = dot(low_ref[1], o_ref[s], NT).astype(BF)
            parts = [[], [], []]
            for head in range(PER):
                cols = slice(head * HD, (head + 1) * HD)
                query = qkv_ref[s, 0, :, cols] * scale
                key = qkv_ref[s, 1, :, cols]
                gm = gm_ref[:, cols]
                scores = dot(key, query, NT)
                scores = scores - dist_ref[...] * slope_ref[i * PER + head]
                likely = jnp.exp(scores - lse_ref[s, head : head + 1, :])
                parts[2].append(dot(likely.astype(BF), gm).astype(BF))
                t = likely * dot(qkv_ref[s, 2, :, cols], gm, NT)
                inner = jnp.sum(t, axis=0, keepdims=True)
                gs = (t - likely * inner).astype(BF)
                parts[1].append(dot(gs, query).astype(BF))
                parts[0].append(dot(gs, key * scale, TN).astype(BF))
            for c in range(3):
                gqkv_ref[s, c] = jnp.concatenate(parts[c], axis=1)
            for index, c in enumerate((0, 2)):
                qv_ref[index : index + 1, block(i, CW)] = row_sum(gqkv_ref[s, c].astype(F32))
            acc_ref[...] += (
                dot(gqkv_ref[s, 0], w_ref[s, 0], NT)
                + dot(gqkv_ref[s, 1], w_ref[s, 1], NT)
                + dot(gqkv_ref[s, 2], w_ref[s, 2], NT)
            )

            @pl.when(i + 2 < 2 * heads_steps)
            def _():
                start_w(i + 2)

            for item in write_heads(i, s):
                item.start()

        g_ref[...] = acc_ref[...].astype(BF)
        ends = [(g_ref, gxl_out), (acc_ref, gx_out), (sums_ref, sums_out), (ub_ref, ub_out), (qv_ref, qv_out)]
        for index, (src, dst) in enumerate(ends):
            copy(src, dst, r_sem.at[2 + index]).start()
        for index, (src, dst) in enumerate([(low_ref.at[0], gl_out.at[slot]), (low_ref.at[1], ga_out.at[slot])] + ends):
            copy(src, dst, r_sem.at[index]).wait()
        for i in (2 * tiles - 2, 2 * tiles - 1):
            for item in write_tiles(jnp.int32(i), i % 2):
                item.wait()
        for i in (2 * heads_steps - 2, 2 * heads_steps - 1):
            for item in write_heads(jnp.int32(i), i % 2):
                item.wait()

    sem = pltpu.SemaphoreType.DMA
    return call(
        kernel,
        [grad, q, k, v, lse, act, slope, u1, u2, r1, r2, *weights, (slopes, SMEM), (vecs, WHOLE)],
        [((slots, rows, 2 * units), BF, True)] * 2
        + [((slots, rows, width), BF, True)] * 2
        + [((slots, rows, total), BF, True)] * 3
        + [
            ((rows, width), F32, False),
            ((rows, width), BF, False),
            ((8, width), F32, False),
            ((2, 2 * units), F32, False),
            ((2, total), F32, False),
        ],
        [
            pltpu.VMEM((rows, width), BF),
            pltpu.VMEM((2, rows, width), BF),
            pltpu.VMEM((2, rows, 128), F32),
            pltpu.VMEM((2, 2, width, ft), BF),
            pltpu.VMEM((2, width, ft), BF),
            pltpu.VMEM((2, 2, rows, ft), BF),
            pltpu.VMEM((2, 2, rows, ft), BF),
            pltpu.VMEM((2, rows, width), BF),
            pltpu.VMEM((rows, width), F32),
            pltpu.VMEM((8, width), F32),
            pltpu.VMEM((2, 2 * units), F32),
            pltpu.VMEM((2, total), F32),
            pltpu.VMEM((2, 3, width, CW), BF),
            pltpu.VMEM((2, CW, width), BF),
            pltpu.VMEM((2, 3, rows, CW), BF),
            pltpu.VMEM((2, 8, rows), F32),
            pltpu.VMEM((rows, CW), BF),
            pltpu.VMEM((rows, rows), F32),
            pltpu.VMEM((2, 3, rows, CW), BF),
            sem((5,)), sem((2, 4)), sem((2, 2)), sem((2, 6)), sem((2, 3)), sem((7,)),
        ],
        meta,
        chain,
        deps,
        "layer_backward",
        2 * rows * width * (4 * total + 6 * units) + 10 * rows * rows * total,
        70 << 20,
    )


MESH = pl.DeviceIdType.MESH
CORE_LAG = 3
CROSS_LAG = 3
CHAIN_LAG = 2


def neighbours():
    t = lax.axis_index("tensor")
    d = lax.axis_index("dp")
    last = lax.axis_size("dp") // 2 - 1
    c = lax.rem(d, 2)
    z = d // 2
    return t, c, z, last, {"dp": d + 1 - 2 * c}, {"tensor": 1 - t}, {"dp": d + 2}, {"dp": d - 2}


def greet(c, z, chips, core, cross):
    barrier = pltpu.get_barrier_semaphore()
    pl.semaphore_signal(barrier, inc=1, device_id=core, device_id_type=MESH)
    pl.semaphore_signal(barrier, inc=1, device_id=cross, device_id_type=MESH)
    for shift in range(1, chips):
        chip = lax.rem(z + shift, chips)
        pl.semaphore_signal(barrier, inc=1, device_id={"dp": chip * 2 + c}, device_id_type=MESH)
    pl.semaphore_wait(barrier, 1 + chips)


def fetch_and_forward(weights, biases, inputs, cotangent, slopes, vecs, meta, chips, slots):
    seqs = inputs.shape[0] // 2
    shard_rows, width = inputs.shape[1:]
    rows = 2 * shard_rows
    groups = 2 * chips
    qkv, out, up, down = weights
    local, units = qkv.shape[2], up.shape[2]
    step = Forward(rows, width, local, units)
    ft, tiles = step.ft, step.tiles
    bias_widths = [b.shape[1] for b in biases]
    QKV, OUT, UP, DOWN, ROWS, BIAS = range(6)

    plan = [(UP, 0, groups), (ROWS, 0, 0), (BIAS, 0, 0), (BIAS, 1, 0)]
    plan += [(UP, part, groups) for part in range(1, tiles)]
    plan += [(DOWN, part, groups) for part in range(tiles - 1)]
    plan += [(QKV, part, 2) for part in range(3)] + [(OUT, 0, 2), (DOWN, tiles - 1, 2)]
    plan += [(ROWS, part, 0) for part in range(1, seqs)]
    n = len(plan)
    number = {item[:2]: index for index, item in enumerate(plan)}

    def size(index):
        kind, part, pieces = plan[index]
        whole = {QKV: width * local, OUT: local * width, UP: 2 * width * ft, DOWN: width * ft, ROWS: shard_rows * width, BIAS: 64}
        return whole[kind] / max(1, pieces)

    events, clock, busy = [], 0.0, 0.0
    for index, (kind, part, pieces) in enumerate(plan):
        clock += size(index)
        events.append((clock, index, 0))
        if pieces == groups:
            start = max(clock, busy)
            busy = start + size(index) * (chips - 1)
            events += [(start + size(index) * hop * 1.001, index, hop) for hop in range(1, chips)]
    events.sort()
    when = {event[1:]: event[0] for event in events}

    def ready(*keys):
        return max(when[key] for k in keys for key in when if key[0] == number[k])

    needs = [[(ROWS, 0), (BIAS, 0)], []] + [[(QKV, part) for part in range(3)], []] + [[(OUT, 0), (BIAS, 1)]]
    needs += [[] for _ in range(tiles - 1)]
    fetches = {5 + tiles - 1 + part: tiles + part for part in range(tiles)}
    needs += [[(UP, part), (DOWN, part)] for part in range(tiles)] + [[]]
    assert step.heads_steps == 2
    rounds, taken = [], 0
    for need in needs:
        mine = []
        if need:
            limit = ready(*need)
            while taken < len(events) and events[taken][0] <= limit:
                mine.append(events[taken][1:])
                taken += 1
        rounds.append((mine, need))
    rest = [event[1:] for event in events[taken:]]
    n_rounds = len(rounds)
    n_kept = len(step.kept(slots))

    def kernel(*refs):
        meta_ref, slope_ref, vec_ref = refs[:3]
        ins, bias_ins, held_refs = refs[3:7], refs[7:9], refs[9:11]
        outs, bias_outs, row_refs = refs[11:15], refs[15:17], refs[17 : 17 + seqs]
        kept_refs = refs[17 + seqs : 17 + seqs + n_kept]
        y_ref = refs[17 + seqs + n_kept]
        stage, qv_bias, ub_bias, x_send, x_recv, c_send, c_recv, u_send, u_recv, d_send, d_recv, l_sem, b_sem = refs[
            18 + seqs + n_kept : 31 + seqs + n_kept
        ]
        t, c, z, last, core, cross, above, below = neighbours()
        section = lax.axis_index("section")
        greet(c, z, chips, core, cross)
        paired = [item for pair in zip(ins, outs) for item in pair]
        step.bind(
            row_refs[0], paired, qv_bias, slope_ref, vec_ref, ub_bias, 0, kept_refs, refs[31 + seqs + n_kept :]
        )

        def span(part):
            return block(part, shard_rows)

        def bias_part(m, side):
            return bias_outs[m].at[:, pl.ds(side * bias_widths[m], bias_widths[m])]

        def piece(side, index, chip, on):
            kind, part, pieces = plan[index]
            place = chip * 2 + on if pieces == groups else on
            ref = (ins, outs)[side][kind]
            if kind == QKV:
                return ref.at[part, block(place, width // pieces)]
            if kind == OUT:
                return ref.at[block(place, local // pieces)]
            cols = pl.ds(part * ft, ft)
            if kind == DOWN:
                return ref.at[block(place, width // pieces), cols]
            per = pieces // 2
            return ref.at[place // per, block(lax.rem(place, per), width // per), cols]

        def cross_copy(index, held_ref=None):
            kind, m, pieces = plan[index]
            if kind == ROWS:
                src = (held_refs[0] if held_ref is None else held_ref).at[(1 - t) * seqs + m]
                dst = row_refs[m].at[span(t)]
            elif kind == BIAS:
                src, dst = bias_ins[m], bias_part(m, 1)
            else:
                src, dst = piece(0, index, z, c), piece(1, index, z, c)
            return pltpu.make_async_remote_copy(
                src_ref=src, dst_ref=dst, send_sem=x_send.at[index], recv_sem=x_recv.at[index],
                device_id=cross, device_id_type=MESH,
            )

        def pass_on(index, chip, send, recv, device):
            place = piece(1, index, chip, c)
            return pltpu.make_async_remote_copy(
                src_ref=place, dst_ref=place, send_sem=send.at[index, chip], recv_sem=recv.at[index, chip],
                device_id=device, device_id_type=MESH,
            )

        def got(index, chip, on, sem):
            arrived(piece(1, index, chip, on), sem)

        for m in range(2):
            copy(bias_ins[m], bias_part(m, 0), b_sem.at[m]).start()
        for index in range(n):
            if plan[index][0] == ROWS:
                for turn in range(2):
                    @pl.when(section == turn)
                    def _(index=index, turn=turn):
                        cross_copy(index, held_refs[turn]).start()
            else:
                cross_copy(index).start()
        for turn in range(2):
            @pl.when(section == turn)
            def _(turn=turn):
                copy(held_refs[turn].at[pl.ds(t * seqs, seqs)], stage, l_sem.at[0]).start()

        @pl.when(section == 0)
        def _():
            for k in range(2):
                step.start_w(jnp.int32(k))
            step.start_o(0)
            for k in range(2):
                step.start_f(jnp.int32(k))
            fill_distance(step.dist, meta_ref[2])

        arrived(stage, l_sem.at[0])
        for m in range(seqs):
            copy(stage.at[m], row_refs[m].at[span(t)], l_sem.at[m]).start()
        for m in range(seqs):
            arrived(stage.at[m], l_sem.at[m])
        for m in range(2):
            copy(bias_ins[m], bias_part(m, 0), b_sem.at[m]).wait()

        def handle(index, hop):
            kind, m, pieces = plan[index]
            if kind == ROWS:
                arrived(row_refs[m].at[span(1 - t)], x_recv.at[index])
            elif kind == BIAS:
                arrived(bias_part(m, 1), x_recv.at[index])
            elif hop == 0:
                got(index, z, c, x_recv.at[index])
                if pieces == groups:
                    @pl.when(z < last)
                    def _():
                        pass_on(index, z, u_send, u_recv, above).start()

                    @pl.when(z > 0)
                    def _():
                        pass_on(index, z, d_send, d_recv, below).start()

                pass_on(index, z, c_send, c_recv, core).start()
            else:
                @pl.when(z - hop >= 0)
                def _():
                    got(index, z - hop, c, u_recv.at[index, z - hop])

                    @pl.when(z < last)
                    def _():
                        pass_on(index, z - hop, u_send, u_recv, above).start()

                    pass_on(index, z - hop, c_send, c_recv, core).start()

                @pl.when(z + hop <= last)
                def _():
                    got(index, z + hop, c, d_recv.at[index, z + hop])

                    @pl.when(z > 0)
                    def _():
                        pass_on(index, z + hop, d_send, d_recv, below).start()

                    pass_on(index, z + hop, c_send, c_recv, core).start()

        def from_core(key):
            index = number[key]
            kind, m, pieces = plan[index]
            if pieces == groups:
                for chip in range(chips):
                    got(index, chip, 1 - c, c_recv.at[index, chip])
            elif pieces:
                got(index, z, 1 - c, c_recv.at[index, z])

        @pl.loop(0, n_rounds)
        def _(tau):
            for number_, (mine, need) in enumerate(rounds):
                if not (mine or need):
                    continue

                @pl.when(tau == number_)
                def _(number_=number_, mine=mine, need=need):
                    for index, hop in mine:
                        handle(index, hop)
                    for key in need:
                        from_core(key)
                    for key in need:
                        if key == (BIAS, 0):
                            @pl.when(section == 0)
                            def _():
                                step.start_x()
                                copy(bias_outs[0], qv_bias, b_sem.at[0]).start()
                                copy(bias_outs[0], qv_bias, b_sem.at[0]).wait()
                                arrived(step.x, step.x_sem)
                        elif key == (QKV, 2):
                            @pl.when(section == 0)
                            def _():
                                for k in range(2, 4):
                                    step.start_w(jnp.int32(k))
                        elif key == (OUT, 0):
                            @pl.when(section == 0)
                            def _():
                                step.start_o(1)
                        elif key == (BIAS, 1):
                            @pl.when(section == 0)
                            def _():
                                copy(bias_outs[1], ub_bias, b_sem.at[1]).start()
                                copy(bias_outs[1], ub_bias, b_sem.at[1]).wait()
                        elif key[0] == DOWN:
                            @pl.when(section == 0)
                            def _(key=key):
                                step.start_f(jnp.int32(tiles + key[1]))

            @pl.when(section == 0)
            def _():
                @pl.when(tau < 4)
                def _():
                    step.attention_step(tau, 2)

                @pl.when(tau == 4)
                def _():
                    step.middle()

                @pl.when(tau > 4)
                def _():
                    step.ffn_step(tau - 5, tiles)

        @pl.when(section == 0)
        def _():
            step.finish(y_ref)

        for index, hop in rest:
            handle(index, hop)
        for index in range(n):
            kind, part, pieces = plan[index]
            cross_copy(index).wait_send()
            if pieces == 2:
                pass_on(index, z, c_send, c_recv, core).wait_send()
            if pieces != groups:
                continue
            for chip in range(chips):
                pass_on(index, chip, c_send, c_recv, core).wait_send()

                @pl.when((chip <= z) & (z < last))
                def _(chip=chip):
                    pass_on(index, chip, u_send, u_recv, above).wait_send()

                @pl.when((chip >= z) & (z > 0))
                def _(chip=chip):
                    pass_on(index, chip, d_send, d_recv, below).wait_send()

    sem = pltpu.SemaphoreType.DMA
    return pl.pallas_call(
        kernel,
        in_specs=[SMEM, SMEM, WHOLE] + [ANY] * 8,
        out_specs=[ANY] * (7 + seqs + n_kept),
        out_shape=[jax.ShapeDtypeStruct(w.shape, BF) for w in weights]
        + [jax.ShapeDtypeStruct((2, 2 * size_), BF) for size_ in bias_widths]
        + [jax.ShapeDtypeStruct((rows, width), BF)] * seqs
        + [jax.ShapeDtypeStruct(*shape) for shape in step.kept(slots)]
        + [jax.ShapeDtypeStruct((rows, width), BF)],
        scratch_shapes=[pltpu.VMEM((seqs, shard_rows, width), BF)]
        + [pltpu.VMEM((2, 2 * size_), BF) for size_ in bias_widths]
        + [sem((n,)), sem((n,))]
        + [sem((n, chips))] * 6
        + [sem((seqs,)), sem((2,))]
        + step.scratch(),
        compiler_params=pltpu.CompilerParams(collective_id=1, has_side_effects=True, vmem_limit_bytes=VMEM_LIMIT),
        cost_estimate=pl.CostEstimate(flops=step.flops(), bytes_accessed=90 << 20, transcendentals=0),
        name="fetch_and_forward",
    )(meta, slopes, vecs, *weights, *biases, inputs, cotangent)


def weight_grads_reduced(groups, sums, row_grads, chips):
    seqs = 2
    rows, depth = groups[0][0].shape[1:]
    lefts = [g[0] for g in groups]
    rights = [r for g in groups for r in g[1]]
    bt = 128
    half = depth // 2
    quarter = half // 2
    blocks = [r.shape[2] // (2 * bt) for r in rights]
    starts = [sum(blocks[:index]) for index in range(len(rights))]
    total = sum(blocks)
    group_starts = []
    index = 0
    for _, members in groups:
        group_starts.append(starts[index])
        index += len(members)
    n_left, n_right = len(lefts), len(rights)
    homes = [(g, index) for g, (_, members) in enumerate(groups) for index in range(len(members))]
    tiles, mines, gives = 4, CORE_LAG + 1, 4
    last_static = chips - 1
    drain = CORE_LAG + CROSS_LAG + 2 * last_static * CHAIN_LAG + 1
    vec_shape = sums.shape
    n_in = n_left + n_right + 1 + seqs
    shard_rows = rows // 2

    def kernel(*refs):
        left_refs = refs[:n_left]
        right_refs = refs[n_left : n_left + n_right]
        sums_ref = refs[n_left + n_right]
        row_refs = refs[n_left + n_right + 1 : n_in]
        outs = refs[n_in : n_in + n_left]
        sums_out, rows_out = refs[n_in + n_left : n_in + n_left + 2]
        (
            acc, from_x, from_z, final, flip, stage, tile, mine, give, vec, vec_in, vec_all,
            tile_sem, stage_sem, give_send, core_recv, x_send, x_recv, z_send, z_recv, f_send, f_recv,
            store_sem, out_send, out_recv, v_load, v_send, v_recv, r_send, r_recv,
        ) = refs[n_in + n_left + 2 :]
        t, c, z, last, core, cross, above, below = neighbours()
        section = lax.axis_index("section")
        greet(c, z, chips, core, cross)

        def remote(src, dst, send, recv, device):
            return pltpu.make_async_remote_copy(
                src_ref=src, dst_ref=dst, send_sem=send, recv_sem=recv, device_id=device, device_id_type=MESH
            )

        def valid(k):
            return (k >= 0) & (k < total)

        def member(k, visit):
            for m in range(n_right):
                @pl.when((k >= starts[m]) & (k < starts[m] + blocks[m]))
                def _(m=m):
                    visit(m, k - starts[m])

        def load_tile(k):
            slot = lax.rem(k, tiles)

            def visit(m, j):
                for side in range(2):
                    at = pl.multiple_of((side * blocks[m] + j) * bt, bt)
                    pltpu.make_async_copy(
                        right_refs[m].at[pl.ds(0, seqs), :, pl.ds(at, bt)],
                        tile.at[slot, :, :, pl.ds(side * bt, bt)],
                        tile_sem.at[slot],
                    ).start()

            member(k, visit)

        def load_left(g):
            return pltpu.make_async_copy(left_refs[g].at[pl.ds(0, seqs)], stage, stage_sem)

        vec_load = pltpu.make_async_copy(sums_ref, vec.at[0], v_load)
        vec_load.start()
        load_left(0).start()
        for k in range(tiles - 1):
            load_tile(jnp.int32(k))
        vec_load.wait()
        vec_core = remote(vec.at[0], vec_in.at[0], v_send.at[0], v_recv.at[0], core)
        vec_cross = remote(vec.at[1], vec_in.at[1], v_send.at[1], v_recv.at[1], cross)
        vec_core.start()
        def row_copy(m):
            source = row_refs[m].at[block(1 - t, shard_rows)]
            return remote(source, rows_out.at[m], r_send.at[m], r_recv.at[m], cross)

        up = pl.ds(0, quarter)
        down = pl.ds(quarter, quarter)
        sides = ((up, 0, z, above, below), (down, 1, last - z, below, above))

        @pl.loop(0, total + drain)
        def _(s):
            @pl.when(valid(s))
            def _():
                for g in range(n_left):
                    @pl.when(s == group_starts[g])
                    def _(g=g):
                        load_left(g).wait()
                        for m in range(seqs):
                            flip[:, m * rows : (m + 1) * rows] = stage[m].T
                        if g + 1 < n_left:
                            load_left(g + 1).start()

                slot = lax.rem(s, tiles)
                arrived(tile.at[slot], tile_sem.at[slot])
                give_slot = lax.rem(s, gives)

                @pl.when(s >= gives)
                def _():
                    arrived(give.at[give_slot], give_send.at[give_slot])

                for place, ring, at in ((1 - c, give, give_slot), (c, mine, lax.rem(s, mines))):
                    here = pl.ds(pl.multiple_of(place * half, half), half)
                    block = dot(flip[here, :rows], tile[slot, 0])
                    for m in range(1, seqs):
                        block += dot(flip[here, m * rows : (m + 1) * rows], tile[slot, m])
                    ring[at, 1] = block[:, :bt].astype(BF)
                    ring[at, 0] = block[:, bt:].astype(BF)

            @pl.when(s + tiles - 1 < total)
            def _():
                load_tile(s + tiles - 1)

            k1 = s - CORE_LAG

            @pl.when(valid(k1))
            def _():
                arrived(acc.at[k1], core_recv.at[k1])
                at = lax.rem(k1, mines)
                for side in range(2):
                    acc[k1, side] = (acc[k1, side].astype(F32) + mine[at, side].astype(F32)).astype(BF)

            k2 = k1 - CROSS_LAG

            @pl.when(valid(k2))
            def _():
                arrived(from_x.at[k2], x_recv.at[k2])
                acc[k2, 1] = (acc[k2, 1].astype(F32) + from_x[k2].astype(F32)).astype(BF)

            for span, way, place, ahead, behind in sides:
                k3 = k2 - CHAIN_LAG * place

                @pl.when(valid(k3) & (place > 0))
                def _(span=span, way=way, k3=k3):
                    arrived(from_z.at[k3, span], z_recv.at[way, k3])
                    acc[k3, 1, span] = (acc[k3, 1, span].astype(F32) + from_z[k3, span].astype(F32)).astype(BF)

                k4 = k2 - CHAIN_LAG * (2 * last - place)

                @pl.when(valid(k4) & (place == last))
                def _(span=span, k4=k4):
                    final[k4, span] = acc[k4, 1, span]

                @pl.when(valid(k4) & (place < last))
                def _(span=span, way=way, k4=k4):
                    arrived(final.at[k4, span], f_recv.at[way, k4])

            @pl.when(valid(s))
            def _():
                at = lax.rem(s, gives)
                remote(give.at[at], acc.at[s], give_send.at[at], core_recv.at[s], core).start()

            @pl.when(valid(k1))
            def _():
                remote(acc.at[k1, 0], from_x.at[k1], x_send, x_recv.at[k1], cross).start()

            @pl.when((k1 == total - 1) & (section == 0))
            def _():
                for m in range(seqs):
                    row_copy(m).start()

            for span, way, place, ahead, behind in sides:
                k3 = k2 - CHAIN_LAG * place

                @pl.when(valid(k3) & (place < last))
                def _(span=span, way=way, k3=k3, ahead=ahead):
                    remote(acc.at[k3, 1, span], from_z.at[k3, span], z_send.at[way], z_recv.at[way, k3], ahead).start()

                k4 = k2 - CHAIN_LAG * (2 * last - place)

                @pl.when(valid(k4) & (place > 0))
                def _(span=span, way=way, k4=k4, behind=behind):
                    remote(final.at[k4, span], final.at[k4, span], f_send.at[way], f_recv.at[way, k4], behind).start()

            k5 = k2 - CHAIN_LAG * 2 * last

            @pl.when(valid(k5))
            def _():
                def visit(m, j):
                    dst = outs[homes[m][0]].at[
                        homes[m][1], pl.ds(pl.multiple_of(c * half, half), half), pl.ds(pl.multiple_of(j * bt, bt), bt)
                    ]
                    pltpu.make_async_copy(final.at[k5], dst, store_sem).start()
                    remote(final.at[k5], dst, out_send, out_recv, core).start()

                member(k5, visit)

            @pl.when(s == 4)
            def _():
                vec_core.wait_recv()
                vec[1] = vec[0] + vec_in[0]

            @pl.when(s == 5)
            def _():
                vec_cross.start()

            @pl.when(s == 10)
            def _():
                vec_cross.wait_recv()
                vec_all[z] = vec[1] + vec_in[1]

            @pl.when(s == 11)
            def _():
                for shift in range(1, chips):
                    to = lax.rem(z + shift, chips)
                    remote(
                        vec_all.at[z], vec_all.at[z], v_send.at[1 + shift], v_recv.at[1 + shift], {"dp": to * 2 + c}
                    ).start()


        @pl.when(section == 0)
        def _():
            for m in range(seqs):
                row_copy(m).wait()

        vec_core.wait_send()
        vec_cross.wait_send()
        for shift in range(1, chips):
            origin = lax.rem(z + chips - shift, chips)
            arrived(vec_all.at[origin], v_recv.at[1 + shift])
            arrived(vec_all.at[z], v_send.at[1 + shift])
        whole = vec_all[0]
        for chip in range(1, chips):
            whole += vec_all[chip]
        sums_out[...] = whole
        for at in range(gives):
            arrived(give.at[at], give_send.at[at])
        arrived(acc.at[:, 0], x_send)
        for span, way, place, ahead, behind in sides:
            @pl.when(place < last)
            def _(span=span, way=way):
                arrived(from_z.at[:, span], z_send.at[way])

            @pl.when(place > 0)
            def _(span=span, way=way):
                arrived(final.at[:, span], f_send.at[way])

        arrived(final, out_send)
        arrived(final, store_sem)
        arrived(final, out_recv)

    sem = pltpu.SemaphoreType.DMA
    flops = 2 * seqs * rows * depth * 2 * bt * total
    return pl.pallas_call(
        kernel,
        in_specs=[ANY] * n_in,
        out_specs=[ANY] * n_left + [WHOLE, ANY],
        out_shape=[jax.ShapeDtypeStruct((len(g[1]), depth, g[1][0].shape[2] // 2), BF) for g in groups]
        + [jax.ShapeDtypeStruct(vec_shape, F32), jax.ShapeDtypeStruct((seqs, shard_rows, depth), BF)],
        scratch_shapes=[
            pltpu.VMEM((total, 2, half, bt), BF),
            pltpu.VMEM((total, half, bt), BF),
            pltpu.VMEM((total, half, bt), BF),
            pltpu.VMEM((total, half, bt), BF),
            pltpu.VMEM((depth, seqs * rows), BF),
            pltpu.VMEM((seqs, rows, depth), BF),
            pltpu.VMEM((tiles, seqs, rows, 2 * bt), BF),
            pltpu.VMEM((mines, 2, half, bt), BF),
            pltpu.VMEM((gives, 2, half, bt), BF),
            pltpu.VMEM((2,) + vec_shape, F32),
            pltpu.VMEM((2,) + vec_shape, F32),
            pltpu.VMEM((chips,) + vec_shape, F32),
            sem((tiles,)), sem, sem((gives,)), sem((total,)), sem, sem((total,)),
            sem((2,)), sem((2, total)), sem((2,)), sem((2, total)),
            sem, sem, sem, sem, sem((chips + 1,)), sem((chips + 1,)), sem((seqs,)), sem((seqs,)),
        ],
        compiler_params=pltpu.CompilerParams(
            collective_id=0, has_side_effects=True, vmem_limit_bytes=VMEM_LIMIT
        ),
        cost_estimate=pl.CostEstimate(flops=flops, bytes_accessed=64 << 20, transcendentals=0),
        name="weight_grads_reduced",
    )(*lefts, *rights, sums, *row_grads)


def exchange_rows(outputs, grads, turn, earlier, deps):
    seqs = len(outputs)
    rows, width = outputs[0].shape
    shard_rows = rows // 2
    n_in = seqs + len(grads) + len(earlier) + len(deps)
    n_out = 2 if grads else 1

    def kernel(*refs):
        y_refs, grad_refs = refs[:seqs], refs[seqs : seqs + len(grads)]
        out_ref = refs[n_in]
        stage, send, recv, l_sem = refs[n_in + n_out :]
        t = lax.axis_index("tensor")
        cross = {"tensor": 1 - t}

        def remote(src, dst, index):
            return pltpu.make_async_remote_copy(
                src_ref=src, dst_ref=dst, send_sem=send.at[index], recv_sem=recv.at[index],
                device_id=cross, device_id_type=MESH,
            )

        barrier = pltpu.get_barrier_semaphore()
        pl.semaphore_signal(barrier, inc=1, device_id=cross, device_id_type=MESH)
        pl.semaphore_wait(barrier, 1)

        @pl.when(lax.axis_index("section") == turn)
        def _():
            sent = [remote(y_refs[m].at[block(1 - t, shard_rows)], out_ref.at[t * seqs + m], m) for m in range(seqs)]
            for m, ref in enumerate(grad_refs):
                sent.append(remote(ref.at[block(1 - t, shard_rows)], refs[n_in + 1].at[m], seqs + m))
            for item in sent:
                item.start()
            for m in range(seqs):
                copy(y_refs[m].at[block(t, shard_rows)], stage.at[m], l_sem.at[m]).start()
            for m in range(seqs):
                arrived(stage.at[m], l_sem.at[m])
                copy(stage.at[m], out_ref.at[t * seqs + m], l_sem.at[m]).start()
            for m in range(seqs):
                arrived(stage.at[m], l_sem.at[m])
            for m in range(seqs):
                arrived(out_ref.at[(1 - t) * seqs + m], recv.at[m])
                arrived(stage.at[m], send.at[m])
            for item in sent[seqs:]:
                item.wait()

    sem = pltpu.SemaphoreType.DMA
    shapes = [
        jax.ShapeDtypeStruct((2 * seqs, shard_rows, width), BF),
        jax.ShapeDtypeStruct((seqs, shard_rows, width), BF),
    ]
    return pl.pallas_call(
        kernel,
        in_specs=[ANY] * n_in,
        out_specs=[ANY] * n_out,
        out_shape=shapes[:n_out],
        scratch_shapes=[
            pltpu.VMEM((seqs, shard_rows, width), BF), sem((2 * seqs,)), sem((2 * seqs,)), sem((seqs,)),
        ],
        input_output_aliases={seqs + len(grads): 0} if earlier else {},
        compiler_params=pltpu.CompilerParams(collective_id=2 + turn, has_side_effects=True),
        cost_estimate=pl.CostEstimate(flops=0, bytes_accessed=0, transcendentals=0),
        name="exchange_rows",
    )(*outputs, *grads, *earlier, *deps)


def widen(reduced, row_grads, gots, sums, units, local):
    seqs, shard_rows, width = gots[0].shape
    n = len(reduced)
    jobs = []
    for index, array in enumerate(reduced):
        lead, depth, columns = array.shape
        step = 512 * 1024 // columns
        if index == n - 1:
            jobs += [(index, 0, at, depth // 2, columns) for at in range(0, depth, depth // 2)]
        else:
            jobs += [(index, part, at, step, columns) for part in range(lead) for at in range(0, depth, step)]
    jobs += [(n, m, 0, shard_rows, width) for m in range(seqs)] + [(n + 1, m, 0, shard_rows, width) for m in range(seqs)]
    ring = 3
    n_in = n + 2 * seqs + 3
    parts = units // width

    def kernel(*refs):
        ins = refs[:n]
        grad_refs = refs[n : n + 2 * seqs]
        got_refs = refs[n + 2 * seqs : n + 2 * seqs + 2]
        sums_ref = refs[n + 2 * seqs + 2]
        outs = refs[n_in : n_in + n + 1]
        qv_ref, out_bias_ref, gain_ref, shift_ref, ub_ref, down_bias_ref = refs[n_in + n + 1 : n_in + n + 7]
        shapes = sorted({(j[3], j[4]) for j in jobs if j[0] != n})
        buffers = refs[n_in + n + 7 :]
        wide_rows, in_sem, out_sem = buffers[0], buffers[1], buffers[2]
        low = {s: buffers[3 + 2 * i] for i, s in enumerate(shapes)}
        wide = {s: buffers[4 + 2 * i] for i, s in enumerate(shapes)}
        t = lax.axis_index("tensor")
        section = lax.axis_index("section")

        def load(number):
            index, part, at, rows, columns = jobs[number]
            s = number % ring
            if index < n:
                copy(ins[index].at[part, pl.ds(at, rows)], low[rows, columns].at[s], in_sem.at[s]).start()
            elif index == n:
                for turn in range(2):
                    @pl.when(section == turn)
                    def _(turn=turn):
                        source = grad_refs[turn * seqs + part].at[block(t, shard_rows)]
                        copy(source, wide_rows.at[part], in_sem.at[s]).start()
            else:
                for turn in range(2):
                    @pl.when(section == turn)
                    def _(turn=turn):
                        copy(got_refs[turn].at[part], low[rows, columns].at[s], in_sem.at[s]).start()

        def store(number):
            index, part, at, rows, columns = jobs[number]
            s = number % ring
            if index < n - 1:
                return copy(wide[rows, columns].at[s], outs[index].at[part, pl.ds(at, rows)], out_sem.at[s])
            if index == n - 1:
                return copy(wide[rows, columns].at[s], outs[index].at[:, pl.ds(at, rows)], out_sem.at[s])
            if index == n:
                return copy(wide_rows.at[part], outs[n].at[t * seqs + part], out_sem.at[s])
            return copy(wide[rows, columns].at[s], outs[n].at[(1 - t) * seqs + part], out_sem.at[s])

        for number in range(ring):
            load(number)
        gain_ref[0:1] = sums_ref[3:4]
        gain_ref[1:2] = sums_ref[0:1]
        shift_ref[0:1] = sums_ref[4:5]
        shift_ref[1:2] = sums_ref[1:2]
        out_bias_ref[...] = sums_ref[5:6]
        down_bias_ref[...] = sums_ref[2:3]
        for half in range(2):
            @pl.when(t == half)
            def _(half=half):
                for g in range(2):
                    for j in range(parts):
                        at = 6 + (2 * g + half) * parts + j
                        ub_ref[g : g + 1, j * width : (j + 1) * width] = sums_ref[at : at + 1]
                    at = 6 + 4 * parts + g
                    qv_ref[g : g + 1] = sums_ref[at : at + 1, half * local : (half + 1) * local]

        for number, (index, part, at, rows, columns) in enumerate(jobs):
            s = number % ring
            if index == n:
                arrived(wide_rows.at[part], in_sem.at[s])
            else:
                arrived(low[rows, columns].at[s], in_sem.at[s])
            if number >= ring:
                store(number - ring).wait()
            if index == n - 1:
                wide[rows, columns][s] = low[rows, columns][s].astype(F32).T
            elif index != n:
                wide[rows, columns][s] = low[rows, columns][s].astype(F32)
            store(number).start()
            if number + ring < len(jobs):
                load(number + ring)
        for number in range(len(jobs) - ring, len(jobs)):
            store(number).wait()

    shapes = sorted({(j[3], j[4]) for j in jobs if j[0] != n})
    square = (reduced[-1].shape[1] // 2, reduced[-1].shape[2])
    last = reduced[-1].shape
    sem = pltpu.SemaphoreType.DMA
    buffers = []
    for s in shapes:
        buffers += [pltpu.VMEM((ring,) + s, BF), pltpu.VMEM((ring,) + ((s[1], s[0]) if s == square else s), F32)]
    return pl.pallas_call(
        kernel,
        in_specs=[ANY] * (n + 2 * seqs + 2) + [WHOLE],
        out_specs=[ANY] * (n + 1) + [WHOLE] * 6,
        out_shape=[jax.ShapeDtypeStruct(r.shape, F32) for r in reduced[:-1]]
        + [jax.ShapeDtypeStruct((last[2], last[1]), F32), jax.ShapeDtypeStruct((2 * seqs, shard_rows, width), F32)]
        + [
            jax.ShapeDtypeStruct(shape, F32)
            for shape in ((2, local), (1, width), (2, width), (2, width), (2, units), (1, width))
        ],
        scratch_shapes=[pltpu.VMEM((seqs, shard_rows, width), F32), sem((ring,)), sem((ring,))] + buffers,
        compiler_params=pltpu.CompilerParams(vmem_limit_bytes=VMEM_LIMIT),
        cost_estimate=pl.CostEstimate(flops=0, bytes_accessed=56 << 20, transcendentals=0),
        name="widen",
    )(*reduced, *row_grads, *gots, sums)


MASKED = -1000000000.0


def shifted(value, axis, steps):
    count = lax.axis_size(axis)
    first, last = (max(0, -steps), min(count, count - steps))
    return lax.ppermute(value, axis, [(source, source + steps) for source in range(first, last)])


def layer_norm(values, gain, shift):
    mean = jnp.mean(values, axis=-1, keepdims=True)
    centred = values - mean
    spread = jnp.mean(centred * centred, axis=-1, keepdims=True)
    return centred * lax.rsqrt(spread + EPS) * gain + shift


def alibi_slopes(first, count, heads):
    index = (first + jnp.arange(count)).astype(jnp.float32)
    return jnp.exp2(-8.0 * (index + 1.0) / heads)


def attention_core(projected, qv_bias, slopes, key_ok):
    rows = projected.shape[0]
    width = projected.shape[2]
    count = slopes.shape[0]
    size = width // count
    query = (projected[:, 0] + qv_bias[0]).astype(jnp.bfloat16).reshape(rows, count, size)
    key = projected[:, 1].astype(jnp.bfloat16).reshape(rows, count, size)
    value = (projected[:, 2] + qv_bias[1]).astype(jnp.bfloat16).reshape(rows, count, size)
    place = jnp.arange(rows).astype(jnp.float32)
    distance = jnp.abs(place[:, None] - place[None, :])
    scale = 1.0 / math.sqrt(size)
    scores = (
        jnp.einsum("qhd,khd->hqk", query, key, preferred_element_type=jnp.float32) * scale
        - slopes[:, None, None] * distance[None]
    )
    scores = jnp.where(key_ok[None, None, :], scores, MASKED)
    weights = jax.nn.softmax(scores, axis=-1)
    weights_low = weights.astype(jnp.bfloat16)
    mixed = jnp.einsum("hqk,khd->qhd", weights_low, value, preferred_element_type=jnp.float32)
    mixed = mixed.reshape(rows, width).astype(jnp.bfloat16)
    return (query, key, value, weights, weights_low, mixed)


def attention_back(parts, grad_mixed, key_ok):
    query, key, value, weights, weights_low, mixed = parts
    rows, count, size = query.shape
    scale = 1.0 / math.sqrt(size)
    grad_low = grad_mixed.astype(jnp.bfloat16).reshape(rows, count, size)
    grad_weights = jnp.einsum("qhd,khd->hqk", grad_low, value, preferred_element_type=jnp.float32)
    grad_value = jnp.einsum(
        "hqk,qhd->khd", weights_low, grad_low, preferred_element_type=jnp.float32
    )
    inner = jnp.sum(weights * grad_weights, axis=-1, keepdims=True)
    grad_scores = weights * (grad_weights - inner)
    grad_scores = jnp.where(key_ok[None, None, :], grad_scores, 0.0).astype(jnp.bfloat16)
    grad_query = (
        jnp.einsum("hqk,khd->qhd", grad_scores, key, preferred_element_type=jnp.float32) * scale
    ).astype(jnp.bfloat16)
    grad_key = (
        jnp.einsum("hqk,qhd->khd", grad_scores, query, preferred_element_type=jnp.float32) * scale
    ).astype(jnp.bfloat16)
    grad_value = grad_value.astype(jnp.bfloat16)
    width = count * size
    grad_query = grad_query.reshape(rows, width)
    grad_key = grad_key.reshape(rows, width)
    grad_value = grad_value.reshape(rows, width)
    grad_projected = jnp.stack([grad_query, grad_key, grad_value], axis=1).reshape(rows, 3 * width)
    qv_grad = jnp.stack(
        [
            jnp.sum(grad_query.astype(jnp.float32), axis=0),
            jnp.sum(grad_value.astype(jnp.float32), axis=0),
        ]
    )
    return (grad_projected, qv_grad)


def gelu_product(both):
    return jax.nn.gelu(both[:, 0], approximate=False) * both[:, 1]


def geglu(lifted, up_bias):
    return gelu_product(lifted + up_bias[None])


def ffn_grads(rows_low, grad_low, up_weight, up_bias, down_weight):
    lifted = jnp.einsum("sd,gdf->sgf", rows_low, up_weight, preferred_element_type=jnp.float32)
    hidden, geglu_back = jax.vjp(gelu_product, lifted + up_bias[None])
    grad_hidden = jnp.einsum("sd,df->sf", grad_low, down_weight, preferred_element_type=jnp.float32)
    (grad_both,) = geglu_back(grad_hidden)
    grad_lifted = grad_both.astype(jnp.bfloat16)
    grad_bias = jnp.sum(grad_lifted.astype(jnp.float32), axis=0)
    up_grad = jnp.einsum("sd,sgf->gdf", rows_low, grad_lifted, preferred_element_type=jnp.float32)
    down_grad = jnp.einsum(
        "sd,sf->df", grad_low, hidden.astype(jnp.bfloat16), preferred_element_type=jnp.float32
    )
    return (grad_lifted, grad_bias, up_grad, down_grad)


def on_device(
    inputs,
    cotangent,
    lengths,
    w_qkv,
    b_qv,
    w_out,
    b_out,
    ln_gain,
    ln_bias,
    w_up,
    b_up,
    w_down,
    b_down,
):
    batches, shard_rows, width = inputs.shape
    parts = lax.axis_size("tensor")
    place = lax.axis_index("tensor")
    section = lax.axis_index("section")
    last_section = lax.axis_size("section") - 1
    full_rows = shard_rows * parts
    local_width = w_qkv.shape[3]
    local_heads = local_width // HD
    qkv_flat = w_qkv[0].reshape(width, 3 * local_width)
    out_weight = w_out[0]
    qv_bias = b_qv[0].astype(jnp.float32)
    out_bias = b_out[0].astype(jnp.float32)
    gains = ln_gain[0].astype(jnp.float32)
    shifts = ln_bias[0].astype(jnp.float32)
    down_bias = b_down[0].astype(jnp.float32)
    slopes = alibi_slopes(place * local_heads, local_heads, H)
    row_place = place * shard_rows + jnp.arange(shard_rows)
    kept_rows = 0

    def key_mask(length):
        return jnp.arange(full_rows) < length

    def after_attention(values, attended, bias, gain_rows, shift_rows):
        return layer_norm(values + attended + bias, gain_rows[0], shift_rows[0])

    def after_ffn(normed, lowered, bias, gain_rows, shift_rows):
        return layer_norm(normed + lowered + bias, gain_rows[1], shift_rows[1])

    def gather_inputs(values):
        return lax.all_gather(values.astype(jnp.bfloat16), "tensor", axis=0, tiled=True)

    def project(gathered):
        return jnp.dot(gathered, qkv_flat, preferred_element_type=jnp.float32).reshape(
            full_rows, 3, local_width
        )

    def attention_forward(values, length):
        gathered = gather_inputs(values)
        projected = project(gathered)
        mixed = attention_core(projected, qv_bias, slopes, key_mask(length))[5]

        def term(start, count):
            return jnp.dot(mixed, out_weight, preferred_element_type=jnp.float32)

        return (
            lax.psum_scatter(
                term(jnp.int32(0), shard_rows * lax.axis_size("tensor")).astype(jnp.bfloat16),
                "tensor",
                scatter_dimension=0,
                tiled=True,
            ).astype(jnp.float32),
            gathered,
            projected,
        )

    up_local = w_up[0]
    up_bias_local = b_up[0].astype(jnp.float32)
    down_local = w_down[0]

    def gather_normed(normed):
        return lax.all_gather(normed.astype(jnp.bfloat16), "tensor", axis=0, tiled=True)

    def ffn_forward(normed):
        lifted = jnp.einsum(
            "sd,gdf->sgf", gather_normed(normed), up_local, preferred_element_type=jnp.float32
        )
        hidden = geglu(lifted, up_bias_local).astype(jnp.bfloat16)

        def term(start, count):
            return jnp.einsum("sf,df->sd", hidden, down_local, preferred_element_type=jnp.float32)

        return lax.psum_scatter(
            term(jnp.int32(0), shard_rows * lax.axis_size("tensor")).astype(jnp.bfloat16),
            "tensor",
            scatter_dimension=0,
            tiled=True,
        ).astype(jnp.float32)

    def ffn_backward(normed, grad_lowered):
        gathered = gather_normed(normed)
        grad_whole = lax.all_gather(grad_lowered.astype(jnp.bfloat16), "tensor", axis=0, tiled=True)
        grad_lifted, grad_bias, up_grad, down_grad = ffn_grads(
            gathered, grad_whole, up_local, up_bias_local, down_local
        )

        def term(start, count):
            return jnp.einsum(
                "sgf,gdf->sd", grad_lifted, up_local, preferred_element_type=jnp.float32
            )

        grad_normed = lax.psum_scatter(
            term(jnp.int32(0), shard_rows * lax.axis_size("tensor")).astype(jnp.bfloat16),
            "tensor",
            scatter_dimension=0,
            tiled=True,
        ).astype(jnp.float32)
        return (grad_normed, (up_grad, grad_bias, down_grad))

    ffn_shapes = (up_local.shape, up_bias_local.shape, down_local.shape)

    def layer_forward(values, length):
        attended, gathered, projected = attention_forward(values, length)
        normed = after_attention(values, attended, out_bias, gains, shifts)
        lowered = ffn_forward(normed)
        return (
            after_ffn(normed, lowered, down_bias, gains, shifts),
            attended,
            lowered,
            gathered,
            projected,
        )

    def layer_backward(values, attended, lowered, length, grad_output):
        normed, attention_norm_back = jax.vjp(
            after_attention, values, attended, out_bias, gains, shifts
        )
        outcome, ffn_norm_back = jax.vjp(after_ffn, normed, lowered, down_bias, gains, shifts)
        grad_normed, grad_lowered, grad_down_bias, gain_late, shift_late = ffn_norm_back(
            grad_output
        )
        grad_from_ffn, ffn_terms = ffn_backward(normed, grad_lowered)
        grad_values, grad_attended, grad_out_bias, gain_early, shift_early = attention_norm_back(
            grad_normed + grad_from_ffn
        )
        gathered = gather_inputs(values)
        projected = project(gathered)
        grad_whole = lax.all_gather(
            grad_attended.astype(jnp.bfloat16), "tensor", axis=0, tiled=True
        )
        mask = key_mask(length)
        pieces = attention_core(projected, qv_bias, slopes, mask)
        mixed_low = pieces[5]
        out_grad = jnp.einsum(
            "se,sd->ed", mixed_low, grad_whole, preferred_element_type=jnp.float32
        )
        grad_mixed = jnp.einsum(
            "sd,ed->se", grad_whole, out_weight, preferred_element_type=jnp.float32
        )
        grad_projected, qv_grad = attention_back(pieces, grad_mixed, mask)
        qkv_grad = jnp.einsum(
            "sd,sx->dx", gathered, grad_projected, preferred_element_type=jnp.float32
        )

        def term(start, count):
            return jnp.einsum(
                "sx,dx->sd", grad_projected, qkv_flat, preferred_element_type=jnp.float32
            )

        grad_inputs = grad_values + lax.psum_scatter(
            term(jnp.int32(0), shard_rows * lax.axis_size("tensor")).astype(jnp.bfloat16),
            "tensor",
            scatter_dimension=0,
            tiled=True,
        ).astype(jnp.float32)
        terms = (
            qkv_grad,
            qv_grad,
            out_grad,
            grad_out_bias,
            gain_early + gain_late,
            shift_early + shift_late,
            ffn_terms[0],
            ffn_terms[1],
            ffn_terms[2],
            grad_down_bias,
        )
        return (grad_inputs, terms)

    def keep(store, item, batch, valid):
        old = lax.dynamic_index_in_dim(store, batch, 0, keepdims=False)
        return lax.dynamic_update_index_in_dim(store, jnp.where(valid, item, old), batch, 0)

    def forward_step(step, carry):
        (
            received,
            kept_values,
            kept_attended,
            kept_lowered,
            produced,
            kept_gathered,
            kept_projected,
        ) = carry
        index = step - section
        valid = (index >= 0) & (index < batches)
        batch = jnp.clip(index, 0, batches - 1)
        fresh = lax.dynamic_index_in_dim(
            inputs, jnp.minimum(step, batches - 1), 0, keepdims=False
        ).astype(jnp.float32)
        values = jnp.where(section == 0, fresh, received.astype(jnp.float32))
        output, attended, lowered, gathered, projected = layer_forward(values, lengths[batch])
        sent = output.astype(jnp.bfloat16)
        kept_values = keep(kept_values, values, batch, valid)
        kept_attended = keep(kept_attended, attended, batch, valid)
        kept_lowered = keep(kept_lowered, lowered, batch, valid)
        produced = keep(produced, sent, batch, valid)
        kept_gathered = keep(kept_gathered, gathered[:kept_rows], batch, valid)
        kept_projected = keep(kept_projected, projected[:kept_rows], batch, valid)
        received = shifted(sent, "section", 1)
        return (
            received,
            kept_values,
            kept_attended,
            kept_lowered,
            produced,
            kept_gathered,
            kept_projected,
        )

    store_zeros = jnp.zeros((batches, shard_rows, width), jnp.float32)
    gathered_zeros = jnp.zeros((batches, kept_rows, width), jnp.bfloat16)
    projected_zeros = jnp.zeros((batches, kept_rows, 3, local_width), jnp.float32)
    start_forward = (
        jnp.zeros((shard_rows, width), jnp.bfloat16),
        store_zeros,
        store_zeros,
        store_zeros,
        jnp.zeros((batches, shard_rows, width), jnp.bfloat16),
        gathered_zeros,
        projected_zeros,
    )
    received, kept_values, kept_attended, kept_lowered, produced, kept_gathered, kept_projected = (
        lax.fori_loop(0, batches + last_section, forward_step, start_forward)
    )

    def backward_step(step, carry):
        received, totals, grads_in = carry
        index = step - (last_section - section)
        valid = (index >= 0) & (index < batches)
        batch = jnp.clip(index, 0, batches - 1)
        length = lengths[batch]
        outer = lax.dynamic_index_in_dim(cotangent, batch, 0, keepdims=False).astype(jnp.float32)
        outer = outer * (row_place < length).astype(jnp.float32)[:, None]
        grad_output = jnp.where(section == last_section, outer, received.astype(jnp.float32))
        grad_output = jnp.where(valid, grad_output, 0.0)
        values = lax.dynamic_index_in_dim(kept_values, batch, 0, keepdims=False)
        attended = lax.dynamic_index_in_dim(kept_attended, batch, 0, keepdims=False)
        lowered = lax.dynamic_index_in_dim(kept_lowered, batch, 0, keepdims=False)
        grad_inputs, terms = layer_backward(values, attended, lowered, length, grad_output)
        totals = jax.tree.map(jnp.add, totals, terms)
        grads_in = keep(grads_in, grad_inputs, batch, valid)
        received = shifted(grad_inputs.astype(jnp.bfloat16), "section", -1)
        return (received, totals, grads_in)

    start_totals = (
        jnp.zeros((width, 3 * local_width), jnp.float32),
        jnp.zeros((2, local_width), jnp.float32),
        jnp.zeros((local_width, width), jnp.float32),
        jnp.zeros((width,), jnp.float32),
        jnp.zeros((2, width), jnp.float32),
        jnp.zeros((2, width), jnp.float32),
        jnp.zeros(ffn_shapes[0], jnp.float32),
        jnp.zeros(ffn_shapes[1], jnp.float32),
        jnp.zeros(ffn_shapes[2], jnp.float32),
        jnp.zeros((width,), jnp.float32),
    )
    start_backward = (jnp.zeros((shard_rows, width), jnp.bfloat16), start_totals, store_zeros)
    received, totals, grads_in = lax.fori_loop(
        0, batches + last_section, backward_step, start_backward
    )
    (
        qkv_total,
        qv_total,
        out_total,
        out_bias_total,
        gain_total,
        shift_total,
        up_total,
        up_bias_total,
        down_total,
        down_bias_total,
    ) = totals
    qkv_sum, qv_sum, out_sum, up_sum, up_bias_sum, down_sum = (
        lax.psum(qkv_total.astype(jnp.bfloat16), "dp").astype(jnp.float32),
        lax.psum(qv_total.astype(jnp.bfloat16), "dp").astype(jnp.float32),
        lax.psum(out_total.astype(jnp.bfloat16), "dp").astype(jnp.float32),
        lax.psum(up_total.astype(jnp.bfloat16), "dp").astype(jnp.float32),
        lax.psum(up_bias_total.astype(jnp.bfloat16), "dp").astype(jnp.float32),
        lax.psum(down_total.astype(jnp.bfloat16), "dp").astype(jnp.float32),
    )
    out_bias_sum, gain_sum, shift_sum, down_bias_sum = lax.psum(
        (out_bias_total, gain_total, shift_total, down_bias_total), ("tensor", "dp")
    )
    return (
        produced[None],
        grads_in[None],
        qkv_sum.reshape(1, width, 3, local_width),
        qv_sum[None],
        out_sum[None],
        out_bias_sum[None],
        gain_sum[None],
        shift_sum[None],
        up_sum[None],
        up_bias_sum[None],
        down_sum[None],
        down_bias_sum[None],
    )


def by_sequence(
    inputs,
    cotangent,
    lengths,
    w_qkv,
    b_qv,
    w_out,
    b_out,
    ln_gain,
    ln_bias,
    w_up,
    b_up,
    w_down,
    b_down,
):
    batches, shard_rows, width = inputs.shape
    place = lax.axis_index("tensor")
    section = lax.axis_index("section")
    groups = lax.axis_size("dp")
    rows = 2 * shard_rows
    seqs = batches // 2
    local = w_qkv.shape[3]
    units = w_up.shape[3]
    heads = local // HD
    chips = groups // 2

    qkv_own = jnp.transpose(w_qkv[0], (1, 0, 2))
    out_own = w_out[0]
    up_own = w_up[0]
    down_own = w_down[0]
    first = section == 0
    vecs = jnp.stack(
        [b_out[0], ln_gain[0, 0], ln_bias[0, 0], b_down[0], ln_gain[0, 1], ln_bias[0, 1], b_out[0], b_out[0]]
    ).astype(F32)
    slope_table = np.exp2(-8.0 * (np.arange(2 * heads, dtype=np.float32) + 1.0) / H).astype(np.float32)
    slopes = jnp.where(place == 0, slope_table, np.roll(slope_table, heads))
    own_lengths = lax.dynamic_slice_in_dim(lengths, place * seqs, seqs, 0)

    def meta(m, turn):
        active = section == turn
        return jnp.stack([jnp.int32(m), active.astype(jnp.int32), own_lengths[m], own_lengths[m] if turn == 1 else jnp.int32(rows)])

    metas = [[meta(m, turn) for m in range(seqs)] for turn in range(2)]
    qkv_oth, out_oth, up_oth, down_oth, bias, up_bias, *rest = fetch_and_forward(
        (qkv_own, out_own, up_own, down_own),
        (b_qv[0], b_up[0]),
        inputs,
        cotangent,
        slopes,
        vecs,
        metas[0][0],
        chips,
        seqs,
    )
    weights = (qkv_own, qkv_oth, out_own, out_oth, up_own, up_oth, down_own, down_oth)
    x_first = outer = rest[:seqs]
    *kept, y = rest[seqs:]
    deps = [y]

    def forward(x, m, turn):
        nonlocal kept, deps
        *kept, y = layer_forward(x, weights, bias, slopes, vecs, up_bias, metas[turn][m], kept, deps, seqs)
        deps = [y]
        return y

    y_first = [y] + [forward(x_first[m], m, 0) for m in range(1, seqs)]
    x_second = [lax.ppermute(y, "section", [(0, 1)]) for y in y_first]
    y_second = [forward(x_second[0], 0, 1)]
    (produced,) = exchange_rows(y_first, [], 0, [], deps)
    deps = [produced]
    y_second += [forward(x_second[m], m, 1) for m in range(1, seqs)]

    back = None
    sums = [[None] * seqs, [None] * seqs]

    def backward(grad, m, turn):
        nonlocal back, deps
        *back, gx, gx_low, norm_sums, up_sums, qv_sums = layer_backward(
            grad, kept, weights, slopes, vecs, metas[turn][m], back, deps, seqs
        )
        deps = [norm_sums]
        sums[turn][m] = (norm_sums, up_sums, qv_sums)
        return gx, gx_low

    gx_second = [backward(outer[m], m, 1) for m in range(seqs)]
    grad_middle = [lax.ppermute(gx_second[m][1], "section", [(1, 0)]) for m in range(seqs)]
    x_all = jnp.stack([jnp.where(first, x_first[m], x_second[m]) for m in range(seqs)])
    deps = deps + [x_all]
    gx_first = [backward(grad_middle[m], m, 0) for m in range(seqs)]
    produced, got_second = exchange_rows(y_second, [g[1] for g in gx_second], 1, [produced], deps)

    mixed, hidden, normed = kept[3], kept[7], kept[8]
    gg0, gg1, gl, ga, *gqkv = back

    picked = [
        sum(jnp.where(first, sums[0][m][index], sums[1][m][index]) for m in range(seqs))
        for index in range(3)
    ]
    norm_sums, up_sums, qv_sums = picked

    def ordered(values, count):
        return jnp.where(
            place == 0, values, jnp.concatenate([values[:, count:], values[:, :count]], axis=1)
        ).reshape(-1, width)

    packed = jnp.concatenate([norm_sums[:6], ordered(up_sums[:2], units), ordered(qv_sums[:2], local)])
    *reduced, packed, got_first = weight_grads_reduced(
        [(gl, [hidden]), (normed, [gg0, gg1]), (x_all, gqkv), (ga, [mixed])], packed, [g[1] for g in gx_first], chips
    )
    down_sum, up_sum, qkv_sum, out_sum, grads_in, qv_sum, out_bias_sum, gain_sum, shift_sum, up_bias_sum, down_bias_sum = (
        widen(reduced, [g[0] for g in gx_first + gx_second], [got_first, got_second], packed, units, local)
    )
    return (
        produced[None],
        grads_in[None],
        jnp.transpose(qkv_sum, (1, 0, 2))[None],
        qv_sum[None],
        out_sum[None],
        out_bias_sum,
        gain_sum[None],
        shift_sum[None],
        up_sum[None],
        up_bias_sum[None],
        down_sum,
        down_bias_sum,
    )


def solution(mesh):
    sections, parts, groups = (mesh.shape[name] for name in ("section", "tensor", "dp"))

    def run(*args):
        paired = sections == 2 and parts == 2 and groups % 2 == 0 and args[0].shape[0] == 4
        return (by_sequence if paired else on_device)(*args)

    return jax.shard_map(
        run,
        mesh=mesh,
        in_specs=(
            P("dp", "tensor", None),
            P("dp", "tensor", None),
            P("dp"),
            P("section", None, None, "tensor"),
            P("section", None, "tensor"),
            P("section", "tensor", None),
            P("section", None),
            P("section", None, None),
            P("section", None, None),
            P("section", None, None, "tensor"),
            P("section", None, "tensor"),
            P("section", None, "tensor"),
            P("section", None),
        ),
        out_specs=(
            P("section", "dp", "tensor", None),
            P("section", "dp", "tensor", None),
            P("section", None, None, "tensor"),
            P("section", None, "tensor"),
            P("section", "tensor", None),
            P("section", None),
            P("section", None, None),
            P("section", None, None),
            P("section", None, None, "tensor"),
            P("section", None, "tensor"),
            P("section", None, "tensor"),
            P("section", None),
        ),
        check_vma=False,
    )
```

```python
import math

import jax
import jax.numpy as jnp
import numpy as np
from jax import lax
from jax.experimental import pallas as pl
from jax.experimental.pallas import tpu as pltpu
from jax.sharding import PartitionSpec as P

H = 16
HD = 64
EPS = 1e-05
BF = jnp.bfloat16
F32 = jnp.float32
VMEM_LIMIT = 62 * 1024 * 1024
ANY = pl.BlockSpec(memory_space=pl.ANY)
SMEM = pl.BlockSpec(memory_space=pltpu.SMEM)
WHOLE = pl.BlockSpec(memory_space=pltpu.VMEM)
NN = (((1,), (0,)), ((), ()))
NT = (((1,), (1,)), ((), ()))
TN = (((0,), (0,)), ((), ()))
CW = 256
PER = CW // HD


def dot(a, b, dims=NN):
    return lax.dot_general(a, b, dims, preferred_element_type=F32)


def arrived(ref, sem):
    pltpu.make_async_copy(ref, ref, sem).wait()


def call(kernel, inputs, outputs, scratch, meta, chain, deps, name, flops, nbytes):
    pairs = [item if isinstance(item, tuple) else (item, ANY) for item in inputs]
    args = [meta] + [p[0] for p in pairs]
    specs = [SMEM] + [p[1] for p in pairs]
    n_in = len(args)
    aliases = {}
    if chain is not None:
        for buffer, index in zip(chain, [index for index, item in enumerate(outputs) if item[2]]):
            aliases[len(args)] = index
            args.append(buffer)
            specs.append(ANY)
    args += deps
    specs += [ANY] * len(deps)
    n_args, n_out = len(args), len(outputs)

    def body(*refs):
        @pl.when(refs[0][1] == 1)
        def _():
            kernel(refs[0], refs[1:n_in], refs[n_args : n_args + n_out], refs[n_args + n_out :])

    return pl.pallas_call(
        body,
        in_specs=specs,
        out_specs=[ANY] * n_out,
        out_shape=[jax.ShapeDtypeStruct(o[0], o[1]) for o in outputs],
        scratch_shapes=scratch,
        input_output_aliases=aliases,
        compiler_params=pltpu.CompilerParams(vmem_limit_bytes=VMEM_LIMIT),
        cost_estimate=pl.CostEstimate(flops=flops, bytes_accessed=nbytes, transcendentals=0),
        name=name,
    )(*args)


def pick(k, count, own, oth, make):
    @pl.when(k < count)
    def _():
        for src, dst, sem in make(own, k):
            pltpu.make_async_copy(src, dst, sem).start()

    @pl.when(k >= count)
    def _():
        for src, dst, sem in make(oth, k - count):
            pltpu.make_async_copy(src, dst, sem).start()


def block(index, size):
    return pl.ds(pl.multiple_of(index * size, size), size)


def copy(src, dst, sem):
    return pltpu.make_async_copy(src, dst, sem)


def fill_distance(dist_ref, length):
    rows = dist_ref.shape[0]
    keys = lax.broadcasted_iota(jnp.int32, (rows, rows), 0)
    places = lax.broadcasted_iota(jnp.int32, (rows, rows), 1)
    distance = jnp.abs(keys - places).astype(F32)
    dist_ref[...] = jnp.where(keys < length, distance, 1e12)


def normalize(v):
    mean = jnp.mean(v, axis=1, keepdims=True)
    centred = v - mean
    rstd = lax.rsqrt(jnp.mean(centred * centred, axis=1, keepdims=True) + EPS)
    return centred * rstd, rstd


def halves(rows):
    return [slice(0, rows // 2), slice(rows // 2, rows)]


class Forward:
    def __init__(self, rows, width, local, units):
        self.rows, self.width, self.local, self.units = rows, width, local, units
        self.ft = min(512, units)
        self.tiles = units // self.ft
        self.heads_steps = local // CW
        self.total = 2 * local

    def kept(self, slots):
        rows, width = self.rows, self.width
        shapes = [((slots, rows, self.total), BF)] * 4
        shapes += [((slots, 2 * self.heads_steps, 8, rows), F32)]
        shapes += [((slots, rows, 2 * self.units), BF)] * 3
        return shapes + [((slots, rows, width), BF)] * 3 + [((slots, rows, 128), F32)] * 2

    def scratch(self):
        rows, width, ft, total = self.rows, self.width, self.ft, self.total
        sem = pltpu.SemaphoreType.DMA
        return [
            pltpu.VMEM((rows, width), BF),
            pltpu.VMEM((2, 3, width, CW), BF),
            pltpu.VMEM((total, width), BF),
            pltpu.VMEM((2, 2, width, ft), BF),
            pltpu.VMEM((2, width, ft), BF),
            pltpu.VMEM((2, 3, rows, CW), BF),
            pltpu.VMEM((2, 8, rows), F32),
            pltpu.VMEM((rows, total), BF),
            pltpu.VMEM((rows, rows), F32),
            pltpu.VMEM((rows, width), F32),
            pltpu.VMEM((rows, width), F32),
            pltpu.VMEM((rows, width), BF),
            pltpu.VMEM((2, 3, rows, ft), BF),
            pltpu.VMEM((3, rows, width), BF),
            pltpu.VMEM((2, rows, 128), F32),
            sem, sem((2,)), sem((2,)), sem((2, 2)), sem((2, 4)), sem, sem((2, 3)), sem((6,)),
        ]

    def bind(self, x, weights, bias, slopes, vecs, up_bias, slot, outs, scratch):
        self.x_hbm, self.weights, self.bias, self.slopes, self.vecs, self.up_bias = x, weights, bias, slopes, vecs, up_bias
        self.slot, self.outs = slot, outs
        (self.x, self.w, self.o, self.up, self.down, self.qkv, self.lse, self.mixed, self.dist, self.normed, self.acc,
         self.low, self.tile, self.row, self.stat, self.x_sem, self.w_sem, self.o_sem, self.f_sem, self.q_sem, self.m_sem,
         self.t_sem, self.r_sem) = scratch

    def start_x(self):
        copy(self.x_hbm, self.x, self.x_sem).start()

    def start_w(self, k):
        s = lax.rem(k, 2)
        pick(k, self.heads_steps, self.weights[0], self.weights[1],
             lambda ref, j: [(ref.at[:, :, block(j, CW)], self.w.at[s], self.w_sem.at[s])])

    def start_o(self, side):
        copy(self.weights[2 + side], self.o.at[pl.ds(side * self.local, self.local)], self.o_sem.at[side]).start()

    def start_f(self, k):
        s = lax.rem(k, 2)
        ft = self.ft
        pick(k, self.tiles, (self.weights[4], self.weights[6]), (self.weights[5], self.weights[7]),
             lambda ref, j: [(ref[0].at[:, :, block(j, ft)], self.up.at[s], self.f_sem.at[s, 0]),
                             (ref[1].at[:, block(j, ft)], self.down.at[s], self.f_sem.at[s, 1])])

    def write_qkv(self, i, s):
        cols = block(i, CW)
        return [copy(self.qkv.at[s, c], out.at[self.slot, :, cols], self.q_sem.at[s, c])
                for c, out in enumerate(self.outs[:3])] + [
            copy(self.lse.at[s], self.outs[4].at[self.slot, i], self.q_sem.at[s, 3])]

    def attention_step(self, i, ahead):
        s = lax.rem(i, 2)
        qkv = self.qkv
        arrived(self.w.at[s], self.w_sem.at[s])

        @pl.when(i >= 2)
        def _():
            for item in self.write_qkv(i - 2, s):
                item.wait()

        values = self.x[...]
        b = self.bias[:, block(i, CW)].astype(F32)
        qkv[s, 0] = (dot(values, self.w[s, 0]) + b[0:1]).astype(BF)
        qkv[s, 1] = dot(values, self.w[s, 1]).astype(BF)
        qkv[s, 2] = (dot(values, self.w[s, 2]) + b[1:2]).astype(BF)

        @pl.when(i + 2 < ahead)
        def _():
            self.start_w(i + 2)

        parts = []
        for head in range(PER):
            cols = slice(head * HD, (head + 1) * HD)
            query = qkv[s, 0, :, cols] * BF(1.0 / math.sqrt(HD))
            scores = dot(qkv[s, 1, :, cols], query, NT)
            scores = scores - self.dist[...] * self.slopes[i * PER + head]
            top = jnp.max(scores, axis=0, keepdims=True)
            likely = jnp.exp(scores - top)
            mass = jnp.sum(likely, axis=0, keepdims=True)
            low = (likely * (1.0 / mass)).astype(BF)
            parts.append(dot(low, qkv[s, 2, :, cols], TN).astype(BF))
            self.lse[s, head : head + 1, :] = top + jnp.log(mass)
        self.mixed[:, block(i, CW)] = jnp.concatenate(parts, axis=1)
        for item in self.write_qkv(i, s):
            item.start()

    def middle(self):
        rows, width = self.rows, self.width
        copy(self.mixed, self.outs[3].at[self.slot], self.m_sem).start()
        for side in range(2):
            arrived(self.o.at[pl.ds(side * self.local, self.local)], self.o_sem.at[side])
        vec = self.vecs[...]
        for rs in halves(rows):
            attended = dot(self.mixed[rs, :], self.o[...])
            u, rstd = normalize(self.x[rs, :].astype(F32) + attended + vec[0:1])
            normed = u * vec[1:2] + vec[2:3]
            self.normed[rs, :] = normed
            self.low[rs, :] = normed.astype(BF)
            self.row[0, rs, :] = u.astype(BF)
            self.stat[0, rs, :] = jnp.broadcast_to(rstd, (rows // 2, 128))
            self.acc[rs, :] = jnp.zeros((rows // 2, width), F32)
        for index, item in enumerate(self.first_rows()):
            copy(*item, self.r_sem.at[index]).start()

    def first_rows(self):
        return [(self.low, self.outs[8].at[self.slot]), (self.row.at[0], self.outs[9].at[self.slot]),
                (self.stat.at[0], self.outs[11].at[self.slot])]

    def write_tiles(self, i, s):
        return [copy(self.tile.at[s, c], out.at[self.slot, :, block(i, self.ft)], self.t_sem.at[s, c])
                for c, out in enumerate(self.outs[5:8])]

    def ffn_step(self, i, ahead):
        s = lax.rem(i, 2)
        arrived(self.up.at[s], self.f_sem.at[s, 0])
        arrived(self.down.at[s], self.f_sem.at[s, 1])

        @pl.when(i >= 2)
        def _():
            for item in self.write_tiles(i - 2, s):
                item.wait()

        b = self.up_bias[:, block(i, self.ft)].astype(F32)
        low = self.low[...]
        gate = dot(low, self.up[s, 0]) + b[0:1]
        lift = dot(low, self.up[s, 1]) + b[1:2]
        cdf = 0.5 * lax.erf(gate * (1.0 / math.sqrt(2.0))) + 0.5
        act = gate * cdf
        slope = cdf + gate * (jnp.exp(gate * gate * -0.5) * (1.0 / math.sqrt(2.0 * math.pi)))
        self.tile[s, 0] = act.astype(BF)
        self.tile[s, 1] = (lift * slope).astype(BF)
        hidden = (act * lift).astype(BF)
        self.tile[s, 2] = hidden
        self.acc[...] += dot(hidden, self.down[s], NT)

        @pl.when(i + 2 < ahead)
        def _():
            self.start_f(i + 2)

        for item in self.write_tiles(i, s):
            item.start()

    def finish(self, y_out):
        rows = self.rows
        vec = self.vecs[...]
        for rs in halves(rows):
            u, rstd = normalize(self.normed[rs, :] + self.acc[rs, :] + vec[3:4])
            self.row[1, rs, :] = u.astype(BF)
            self.stat[1, rs, :] = jnp.broadcast_to(rstd, (rows // 2, 128))
            self.row[2, rs, :] = (u * vec[4:5] + vec[5:6]).astype(BF)
        ends = [(self.row.at[1], self.outs[10].at[self.slot]), (self.stat.at[1], self.outs[12].at[self.slot]),
                (self.row.at[2], y_out)]
        for index, item in enumerate(ends):
            copy(*item, self.r_sem.at[3 + index]).start()
        for index, item in enumerate(self.first_rows() + ends):
            copy(*item, self.r_sem.at[index]).wait()
        copy(self.mixed, self.outs[3].at[self.slot], self.m_sem).wait()
        for i in (2 * self.heads_steps - 2, 2 * self.heads_steps - 1):
            for item in self.write_qkv(jnp.int32(i), i % 2):
                item.wait()
        for i in (2 * self.tiles - 2, 2 * self.tiles - 1):
            for item in self.write_tiles(jnp.int32(i), i % 2):
                item.wait()

    def flops(self):
        rows, width, total = self.rows, self.width, self.total
        return 2 * rows * width * (4 * total + 6 * self.units) + 4 * rows * rows * total


def layer_forward(x, weights, bias, slopes, vecs, up_bias, meta, chain, deps, slots):
    rows, width = x.shape
    step = Forward(rows, width, weights[0].shape[2], weights[4].shape[2])

    def kernel(meta_ref, ins, outs, scratch):
        step.bind(ins[0], ins[1:9], *ins[9:13], meta_ref[0], outs[:13], scratch)
        step.start_x()
        for k in range(2):
            step.start_w(jnp.int32(k))
        for side in range(2):
            step.start_o(side)
        for k in range(2):
            step.start_f(jnp.int32(k))
        fill_distance(step.dist, meta_ref[2])
        arrived(step.x, step.x_sem)

        @pl.loop(0, 2 * step.heads_steps)
        def _(i):
            step.attention_step(i, 2 * step.heads_steps)

        step.middle()

        @pl.loop(0, 2 * step.tiles)
        def _(i):
            step.ffn_step(i, 2 * step.tiles)

        step.finish(outs[13])

    return call(
        kernel,
        [x, *weights, (bias, WHOLE), (slopes, SMEM), (vecs, WHOLE), (up_bias, WHOLE)],
        [shape + (True,) for shape in step.kept(slots)] + [((rows, width), BF, False)],
        step.scratch(),
        meta,
        chain,
        deps,
        "layer_forward",
        step.flops(),
        54 << 20,
    )


def layer_backward(grad, kept, weights, slopes, vecs, meta, chain, deps, slots):
    qkv_own, qkv_oth, o_own, o_oth, up_own, up_oth, down_own, down_oth = weights
    q, k, v, _, lse, act, slope, _, _, u1, u2, r1, r2 = kept
    rows, width = grad.shape
    local = qkv_own.shape[2]
    units = up_own.shape[2]
    heads_steps = local // CW
    ft = min(512, units)
    tiles = units // ft
    total = 2 * local

    def norm_back(grad_z, u, rstd, gain):
        t = grad_z * gain
        return rstd * (t - jnp.mean(t, axis=1, keepdims=True) - u * jnp.mean(t * u, axis=1, keepdims=True))

    def row_sum(values):
        return jnp.sum(values, axis=0, keepdims=True)

    def kernel(meta_ref, ins, outs, scratch):
        (g_hbm, q_hbm, k_hbm, v_hbm, lse_hbm, a_hbm, b_hbm, u1_hbm, u2_hbm, r1_hbm, r2_hbm,
         qkv_own_ref, qkv_oth_ref, o_own_ref, o_oth_ref, up_own_ref, up_oth_ref, down_own_ref, down_oth_ref,
         slope_ref, vec_ref) = ins
        gg0_out, gg1_out, gl_out, ga_out, gq_out, gk_out, gv_out, gx_out, gxl_out, sums_out, ub_out, qv_out = outs
        (g_ref, u_ref, r_ref, up_ref, down_ref, ab_ref, gg_ref, low_ref, acc_ref, sums_ref, ub_ref, qv_ref,
         w_ref, o_ref, qkv_ref, lse_ref, gm_ref, dist_ref, gqkv_ref,
         g_sem, f_sem, t_sem, w_sem, q_sem, r_sem) = scratch
        slot = meta_ref[0]

        def start_f(i):
            s = lax.rem(i, 2)
            pick(i, tiles, (up_own_ref, down_own_ref), (up_oth_ref, down_oth_ref),
                 lambda ref, j: [(ref[0].at[:, :, block(j, ft)], up_ref.at[s], f_sem.at[s, 0]),
                                 (ref[1].at[:, block(j, ft)], down_ref.at[s], f_sem.at[s, 1])])
            for c, ref in enumerate((a_hbm, b_hbm)):
                copy(ref.at[slot, :, block(i, ft)], ab_ref.at[s, c], f_sem.at[s, 2 + c]).start()

        def start_w(i):
            s = lax.rem(i, 2)
            pick(i, heads_steps, (qkv_own_ref, o_own_ref), (qkv_oth_ref, o_oth_ref),
                 lambda ref, j: [(ref[0].at[:, :, block(j, CW)], w_ref.at[s], w_sem.at[s, 0]),
                                 (ref[1].at[block(j, CW)], o_ref.at[s], w_sem.at[s, 1])])
            for c, ref in enumerate((q_hbm, k_hbm, v_hbm)):
                copy(ref.at[slot, :, block(i, CW)], qkv_ref.at[s, c], w_sem.at[s, 2 + c]).start()
            copy(lse_hbm.at[slot, i], lse_ref.at[s], w_sem.at[s, 5]).start()

        firsts = [(g_hbm, g_ref), (u2_hbm.at[slot], u_ref.at[1]), (r2_hbm.at[slot], r_ref.at[1]),
                  (u1_hbm.at[slot], u_ref.at[0]), (r1_hbm.at[slot], r_ref.at[0])]
        for index, (src, dst) in enumerate(firsts):
            copy(src, dst, g_sem.at[index]).start()
            if index == 2:
                start_f(jnp.int32(0))
                start_f(jnp.int32(1))
        start_w(jnp.int32(0))
        start_w(jnp.int32(1))
        vec = vec_ref[...]
        fill_distance(dist_ref, meta_ref[2])
        for index, (src, dst) in enumerate(firsts[:3]):
            copy(src, dst, g_sem.at[index]).wait()
        sums = [jnp.zeros((1, width), F32)] * 3
        for rs in halves(rows):
            places = lax.broadcasted_iota(jnp.int32, (rows // 2, width), 0) + rs.start
            grad_y = jnp.where(places < meta_ref[3], g_ref[rs, :].astype(F32), 0.0)
            u = u_ref[1, rs, :].astype(F32)
            grad_c = norm_back(grad_y, u, r_ref[1, rs, 0:1], vec[4:5])
            acc_ref[rs, :] = grad_c
            low_ref[0, rs, :] = grad_c.astype(BF)
            for index, values in enumerate((grad_y * u, grad_y, grad_c)):
                sums[index] += row_sum(values)
        for index in range(3):
            sums_ref[index : index + 1, :] = sums[index]
        copy(low_ref.at[0], gl_out.at[slot], r_sem.at[0]).start()

        def write_tiles(i, s):
            return [copy(gg_ref.at[s, c], out.at[slot, :, block(i, ft)], t_sem.at[s, c])
                    for c, out in enumerate((gg0_out, gg1_out))]

        @pl.loop(0, 2 * tiles)
        def _(i):
            s = lax.rem(i, 2)
            arrived(up_ref.at[s], f_sem.at[s, 0])
            arrived(down_ref.at[s], f_sem.at[s, 1])
            for c in range(2):
                arrived(ab_ref.at[s, c], f_sem.at[s, 2 + c])

            @pl.when(i >= 2)
            def _():
                for item in write_tiles(i - 2, s):
                    item.wait()

            gh = dot(low_ref[0], down_ref[s])
            g0 = (gh * ab_ref[s, 1].astype(F32)).astype(BF)
            g1 = (gh * ab_ref[s, 0].astype(F32)).astype(BF)
            gg_ref[s, 0] = g0
            gg_ref[s, 1] = g1
            ub_ref[0:1, block(i, ft)] = row_sum(g0.astype(F32))
            ub_ref[1:2, block(i, ft)] = row_sum(g1.astype(F32))
            acc_ref[...] += dot(g0, up_ref[s, 0], NT) + dot(g1, up_ref[s, 1], NT)

            @pl.when(i + 2 < 2 * tiles)
            def _():
                start_f(i + 2)

            for item in write_tiles(i, s):
                item.start()

        for index, (src, dst) in enumerate(firsts[3:]):
            copy(src, dst, g_sem.at[3 + index]).wait()
        sums = [jnp.zeros((1, width), F32)] * 3
        for rs in halves(rows):
            grad_n = acc_ref[rs, :]
            u = u_ref[0, rs, :].astype(F32)
            grad_a = norm_back(grad_n, u, r_ref[0, rs, 0:1], vec[1:2])
            low_ref[1, rs, :] = grad_a.astype(BF)
            acc_ref[rs, :] = grad_a
            for index, values in enumerate((grad_n * u, grad_n, grad_a)):
                sums[index] += row_sum(values)
        for index in range(3):
            sums_ref[3 + index : 4 + index, :] = sums[index]
        sums_ref[6:8, :] = jnp.zeros((2, width), F32)
        copy(low_ref.at[1], ga_out.at[slot], r_sem.at[1]).start()
        scale = BF(1.0 / math.sqrt(HD))

        def write_heads(i, s):
            return [copy(gqkv_ref.at[s, c], out.at[slot, :, block(i, CW)], q_sem.at[s, c])
                    for c, out in enumerate((gq_out, gk_out, gv_out))]

        @pl.loop(0, 2 * heads_steps)
        def _(i):
            s = lax.rem(i, 2)
            for index, ref in enumerate((w_ref.at[s], o_ref.at[s], qkv_ref.at[s, 0], qkv_ref.at[s, 1], qkv_ref.at[s, 2], lse_ref.at[s])):
                arrived(ref, w_sem.at[s, index])

            @pl.when(i >= 2)
            def _():
                for item in write_heads(i - 2, s):
                    item.wait()

            gm_ref[...] = dot(low_ref[1], o_ref[s], NT).astype(BF)
            parts = [[], [], []]
            for head in range(PER):
                cols = slice(head * HD, (head + 1) * HD)
                query = qkv_ref[s, 0, :, cols] * scale
                key = qkv_ref[s, 1, :, cols]
                gm = gm_ref[:, cols]
                scores = dot(key, query, NT)
                scores = scores - dist_ref[...] * slope_ref[i * PER + head]
                likely = jnp.exp(scores - lse_ref[s, head : head + 1, :])
                parts[2].append(dot(likely.astype(BF), gm).astype(BF))
                t = likely * dot(qkv_ref[s, 2, :, cols], gm, NT)
                inner = jnp.sum(t, axis=0, keepdims=True)
                gs = (t - likely * inner).astype(BF)
                parts[1].append(dot(gs, query).astype(BF))
                parts[0].append(dot(gs, key * scale, TN).astype(BF))
            for c in range(3):
                gqkv_ref[s, c] = jnp.concatenate(parts[c], axis=1)
            for index, c in enumerate((0, 2)):
                qv_ref[index : index + 1, block(i, CW)] = row_sum(gqkv_ref[s, c].astype(F32))
            acc_ref[...] += (
                dot(gqkv_ref[s, 0], w_ref[s, 0], NT)
                + dot(gqkv_ref[s, 1], w_ref[s, 1], NT)
                + dot(gqkv_ref[s, 2], w_ref[s, 2], NT)
            )

            @pl.when(i + 2 < 2 * heads_steps)
            def _():
                start_w(i + 2)

            for item in write_heads(i, s):
                item.start()

        g_ref[...] = acc_ref[...].astype(BF)
        ends = [(g_ref, gxl_out), (acc_ref, gx_out), (sums_ref, sums_out), (ub_ref, ub_out), (qv_ref, qv_out)]
        for index, (src, dst) in enumerate(ends):
            copy(src, dst, r_sem.at[2 + index]).start()
        for index, (src, dst) in enumerate([(low_ref.at[0], gl_out.at[slot]), (low_ref.at[1], ga_out.at[slot])] + ends):
            copy(src, dst, r_sem.at[index]).wait()
        for i in (2 * tiles - 2, 2 * tiles - 1):
            for item in write_tiles(jnp.int32(i), i % 2):
                item.wait()
        for i in (2 * heads_steps - 2, 2 * heads_steps - 1):
            for item in write_heads(jnp.int32(i), i % 2):
                item.wait()

    sem = pltpu.SemaphoreType.DMA
    return call(
        kernel,
        [grad, q, k, v, lse, act, slope, u1, u2, r1, r2, *weights, (slopes, SMEM), (vecs, WHOLE)],
        [((slots, rows, 2 * units), BF, True)] * 2
        + [((slots, rows, width), BF, True)] * 2
        + [((slots, rows, total), BF, True)] * 3
        + [
            ((rows, width), F32, False),
            ((rows, width), BF, False),
            ((8, width), F32, False),
            ((2, 2 * units), F32, False),
            ((2, total), F32, False),
        ],
        [
            pltpu.VMEM((rows, width), BF),
            pltpu.VMEM((2, rows, width), BF),
            pltpu.VMEM((2, rows, 128), F32),
            pltpu.VMEM((2, 2, width, ft), BF),
            pltpu.VMEM((2, width, ft), BF),
            pltpu.VMEM((2, 2, rows, ft), BF),
            pltpu.VMEM((2, 2, rows, ft), BF),
            pltpu.VMEM((2, rows, width), BF),
            pltpu.VMEM((rows, width), F32),
            pltpu.VMEM((8, width), F32),
            pltpu.VMEM((2, 2 * units), F32),
            pltpu.VMEM((2, total), F32),
            pltpu.VMEM((2, 3, width, CW), BF),
            pltpu.VMEM((2, CW, width), BF),
            pltpu.VMEM((2, 3, rows, CW), BF),
            pltpu.VMEM((2, 8, rows), F32),
            pltpu.VMEM((rows, CW), BF),
            pltpu.VMEM((rows, rows), F32),
            pltpu.VMEM((2, 3, rows, CW), BF),
            sem((5,)), sem((2, 4)), sem((2, 2)), sem((2, 6)), sem((2, 3)), sem((7,)),
        ],
        meta,
        chain,
        deps,
        "layer_backward",
        2 * rows * width * (4 * total + 6 * units) + 10 * rows * rows * total,
        70 << 20,
    )


MESH = pl.DeviceIdType.MESH
CORE_LAG = 3
CROSS_LAG = 3
CHAIN_LAG = 2


def neighbours():
    t = lax.axis_index("tensor")
    d = lax.axis_index("dp")
    last = lax.axis_size("dp") // 2 - 1
    c = lax.rem(d, 2)
    z = d // 2
    return t, c, z, last, {"dp": d + 1 - 2 * c}, {"tensor": 1 - t}, {"dp": d + 2}, {"dp": d - 2}


def greet(c, z, chips, core, cross):
    barrier = pltpu.get_barrier_semaphore()
    pl.semaphore_signal(barrier, inc=1, device_id=core, device_id_type=MESH)
    pl.semaphore_signal(barrier, inc=1, device_id=cross, device_id_type=MESH)
    for shift in range(1, chips):
        chip = lax.rem(z + shift, chips)
        pl.semaphore_signal(barrier, inc=1, device_id={"dp": chip * 2 + c}, device_id_type=MESH)
    pl.semaphore_wait(barrier, 1 + chips)


def fetch_and_forward(weights, biases, inputs, cotangent, slopes, vecs, meta, chips, slots):
    seqs = inputs.shape[0] // 2
    shard_rows, width = inputs.shape[1:]
    rows = 2 * shard_rows
    groups = 2 * chips
    qkv, out, up, down = weights
    local, units = qkv.shape[2], up.shape[2]
    step = Forward(rows, width, local, units)
    ft, tiles = step.ft, step.tiles
    bias_widths = [b.shape[1] for b in biases]
    QKV, OUT, UP, DOWN, ROWS, BIAS = range(6)

    plan = [(UP, 0, groups), (ROWS, 0, 0), (BIAS, 0, 0), (BIAS, 1, 0)]
    plan += [(UP, part, groups) for part in range(1, tiles)]
    plan += [(DOWN, part, groups) for part in range(tiles - 1)]
    plan += [(QKV, part, 2) for part in range(3)] + [(OUT, 0, 2), (DOWN, tiles - 1, 2)]
    plan += [(ROWS, part, 0) for part in range(1, seqs)]
    n = len(plan)
    number = {item[:2]: index for index, item in enumerate(plan)}

    def size(index):
        kind, part, pieces = plan[index]
        whole = {QKV: width * local, OUT: local * width, UP: 2 * width * ft, DOWN: width * ft, ROWS: shard_rows * width, BIAS: 64}
        return whole[kind] / max(1, pieces)

    events, clock, busy = [], 0.0, 0.0
    for index, (kind, part, pieces) in enumerate(plan):
        clock += size(index)
        events.append((clock, index, 0))
        if pieces == groups:
            start = max(clock, busy)
            busy = start + size(index) * (chips - 1)
            events += [(start + size(index) * hop * 1.001, index, hop) for hop in range(1, chips)]
    events.sort()
    when = {event[1:]: event[0] for event in events}

    def ready(*keys):
        return max(when[key] for k in keys for key in when if key[0] == number[k])

    needs = [[(ROWS, 0), (BIAS, 0)], []] + [[(QKV, part) for part in range(3)], []] + [[(OUT, 0), (BIAS, 1)]]
    needs += [[] for _ in range(tiles - 1)]
    fetches = {5 + tiles - 1 + part: tiles + part for part in range(tiles)}
    needs += [[(UP, part), (DOWN, part)] for part in range(tiles)] + [[]]
    assert step.heads_steps == 2
    rounds, taken = [], 0
    for need in needs:
        mine = []
        if need:
            limit = ready(*need)
            while taken < len(events) and events[taken][0] <= limit:
                mine.append(events[taken][1:])
                taken += 1
        rounds.append((mine, need))
    rest = [event[1:] for event in events[taken:]]
    n_rounds = len(rounds)
    n_kept = len(step.kept(slots))

    def kernel(*refs):
        meta_ref, slope_ref, vec_ref = refs[:3]
        ins, bias_ins, held_refs = refs[3:7], refs[7:9], refs[9:11]
        outs, bias_outs, row_refs = refs[11:15], refs[15:17], refs[17 : 17 + seqs]
        kept_refs = refs[17 + seqs : 17 + seqs + n_kept]
        y_ref = refs[17 + seqs + n_kept]
        stage, qv_bias, ub_bias, x_send, x_recv, c_send, c_recv, u_send, u_recv, d_send, d_recv, l_sem, b_sem = refs[
            18 + seqs + n_kept : 31 + seqs + n_kept
        ]
        t, c, z, last, core, cross, above, below = neighbours()
        section = lax.axis_index("section")
        greet(c, z, chips, core, cross)
        paired = [item for pair in zip(ins, outs) for item in pair]
        step.bind(
            row_refs[0], paired, qv_bias, slope_ref, vec_ref, ub_bias, 0, kept_refs, refs[31 + seqs + n_kept :]
        )

        def span(part):
            return block(part, shard_rows)

        def bias_part(m, side):
            return bias_outs[m].at[:, pl.ds(side * bias_widths[m], bias_widths[m])]

        def piece(side, index, chip, on):
            kind, part, pieces = plan[index]
            place = chip * 2 + on if pieces == groups else on
            ref = (ins, outs)[side][kind]
            if kind == QKV:
                return ref.at[part, block(place, width // pieces)]
            if kind == OUT:
                return ref.at[block(place, local // pieces)]
            cols = pl.ds(part * ft, ft)
            if kind == DOWN:
                return ref.at[block(place, width // pieces), cols]
            per = pieces // 2
            return ref.at[place // per, block(lax.rem(place, per), width // per), cols]

        def cross_copy(index, held_ref=None):
            kind, m, pieces = plan[index]
            if kind == ROWS:
                src = (held_refs[0] if held_ref is None else held_ref).at[(1 - t) * seqs + m]
                dst = row_refs[m].at[span(t)]
            elif kind == BIAS:
                src, dst = bias_ins[m], bias_part(m, 1)
            else:
                src, dst = piece(0, index, z, c), piece(1, index, z, c)
            return pltpu.make_async_remote_copy(
                src_ref=src, dst_ref=dst, send_sem=x_send.at[index], recv_sem=x_recv.at[index],
                device_id=cross, device_id_type=MESH,
            )

        def pass_on(index, chip, send, recv, device):
            place = piece(1, index, chip, c)
            return pltpu.make_async_remote_copy(
                src_ref=place, dst_ref=place, send_sem=send.at[index, chip], recv_sem=recv.at[index, chip],
                device_id=device, device_id_type=MESH,
            )

        def got(index, chip, on, sem):
            arrived(piece(1, index, chip, on), sem)

        for m in range(2):
            copy(bias_ins[m], bias_part(m, 0), b_sem.at[m]).start()
        for index in range(n):
            if plan[index][0] == ROWS:
                for turn in range(2):
                    @pl.when(section == turn)
                    def _(index=index, turn=turn):
                        cross_copy(index, held_refs[turn]).start()
            else:
                cross_copy(index).start()
        for turn in range(2):
            @pl.when(section == turn)
            def _(turn=turn):
                copy(held_refs[turn].at[pl.ds(t * seqs, seqs)], stage, l_sem.at[0]).start()

        @pl.when(section == 0)
        def _():
            for k in range(2):
                step.start_w(jnp.int32(k))
            step.start_o(0)
            for k in range(2):
                step.start_f(jnp.int32(k))
            fill_distance(step.dist, meta_ref[2])

        arrived(stage, l_sem.at[0])
        for m in range(seqs):
            copy(stage.at[m], row_refs[m].at[span(t)], l_sem.at[m]).start()
        for m in range(seqs):
            arrived(stage.at[m], l_sem.at[m])
        for m in range(2):
            copy(bias_ins[m], bias_part(m, 0), b_sem.at[m]).wait()

        def handle(index, hop):
            kind, m, pieces = plan[index]
            if kind == ROWS:
                arrived(row_refs[m].at[span(1 - t)], x_recv.at[index])
            elif kind == BIAS:
                arrived(bias_part(m, 1), x_recv.at[index])
            elif hop == 0:
                got(index, z, c, x_recv.at[index])
                if pieces == groups:
                    @pl.when(z < last)
                    def _():
                        pass_on(index, z, u_send, u_recv, above).start()

                    @pl.when(z > 0)
                    def _():
                        pass_on(index, z, d_send, d_recv, below).start()

                pass_on(index, z, c_send, c_recv, core).start()
            else:
                @pl.when(z - hop >= 0)
                def _():
                    got(index, z - hop, c, u_recv.at[index, z - hop])

                    @pl.when(z < last)
                    def _():
                        pass_on(index, z - hop, u_send, u_recv, above).start()

                    pass_on(index, z - hop, c_send, c_recv, core).start()

                @pl.when(z + hop <= last)
                def _():
                    got(index, z + hop, c, d_recv.at[index, z + hop])

                    @pl.when(z > 0)
                    def _():
                        pass_on(index, z + hop, d_send, d_recv, below).start()

                    pass_on(index, z + hop, c_send, c_recv, core).start()

        def from_core(key):
            index = number[key]
            kind, m, pieces = plan[index]
            if pieces == groups:
                for chip in range(chips):
                    got(index, chip, 1 - c, c_recv.at[index, chip])
            elif pieces:
                got(index, z, 1 - c, c_recv.at[index, z])

        @pl.loop(0, n_rounds)
        def _(tau):
            for number_, (mine, need) in enumerate(rounds):
                if not (mine or need):
                    continue

                @pl.when(tau == number_)
                def _(number_=number_, mine=mine, need=need):
                    for index, hop in mine:
                        handle(index, hop)
                    for key in need:
                        from_core(key)
                    for key in need:
                        if key == (BIAS, 0):
                            @pl.when(section == 0)
                            def _():
                                step.start_x()
                                copy(bias_outs[0], qv_bias, b_sem.at[0]).start()
                                copy(bias_outs[0], qv_bias, b_sem.at[0]).wait()
                                arrived(step.x, step.x_sem)
                        elif key == (QKV, 2):
                            @pl.when(section == 0)
                            def _():
                                for k in range(2, 4):
                                    step.start_w(jnp.int32(k))
                        elif key == (OUT, 0):
                            @pl.when(section == 0)
                            def _():
                                step.start_o(1)
                        elif key == (BIAS, 1):
                            @pl.when(section == 0)
                            def _():
                                copy(bias_outs[1], ub_bias, b_sem.at[1]).start()
                                copy(bias_outs[1], ub_bias, b_sem.at[1]).wait()
                        elif key[0] == DOWN:
                            @pl.when(section == 0)
                            def _(key=key):
                                step.start_f(jnp.int32(tiles + key[1]))

            @pl.when(section == 0)
            def _():
                @pl.when(tau < 4)
                def _():
                    step.attention_step(tau, 2)

                @pl.when(tau == 4)
                def _():
                    step.middle()

                @pl.when(tau > 4)
                def _():
                    step.ffn_step(tau - 5, tiles)

        @pl.when(section == 0)
        def _():
            step.finish(y_ref)

        for index, hop in rest:
            handle(index, hop)
        for index in range(n):
            kind, part, pieces = plan[index]
            cross_copy(index).wait_send()
            if pieces == 2:
                pass_on(index, z, c_send, c_recv, core).wait_send()
            if pieces != groups:
                continue
            for chip in range(chips):
                pass_on(index, chip, c_send, c_recv, core).wait_send()

                @pl.when((chip <= z) & (z < last))
                def _(chip=chip):
                    pass_on(index, chip, u_send, u_recv, above).wait_send()

                @pl.when((chip >= z) & (z > 0))
                def _(chip=chip):
                    pass_on(index, chip, d_send, d_recv, below).wait_send()

    sem = pltpu.SemaphoreType.DMA
    return pl.pallas_call(
        kernel,
        in_specs=[SMEM, SMEM, WHOLE] + [ANY] * 8,
        out_specs=[ANY] * (7 + seqs + n_kept),
        out_shape=[jax.ShapeDtypeStruct(w.shape, BF) for w in weights]
        + [jax.ShapeDtypeStruct((2, 2 * size_), BF) for size_ in bias_widths]
        + [jax.ShapeDtypeStruct((rows, width), BF)] * seqs
        + [jax.ShapeDtypeStruct(*shape) for shape in step.kept(slots)]
        + [jax.ShapeDtypeStruct((rows, width), BF)],
        scratch_shapes=[pltpu.VMEM((seqs, shard_rows, width), BF)]
        + [pltpu.VMEM((2, 2 * size_), BF) for size_ in bias_widths]
        + [sem((n,)), sem((n,))]
        + [sem((n, chips))] * 6
        + [sem((seqs,)), sem((2,))]
        + step.scratch(),
        compiler_params=pltpu.CompilerParams(collective_id=1, has_side_effects=True, vmem_limit_bytes=VMEM_LIMIT),
        cost_estimate=pl.CostEstimate(flops=step.flops(), bytes_accessed=90 << 20, transcendentals=0),
        name="fetch_and_forward",
    )(meta, slopes, vecs, *weights, *biases, inputs, cotangent)


def norm_back(grad_z, u, rstd, gain):
    t = grad_z * gain
    return rstd * (t - jnp.mean(t, axis=1, keepdims=True) - u * jnp.mean(t * u, axis=1, keepdims=True))


def row_sum(values):
    return jnp.sum(values, axis=0, keepdims=True)


def backward_and_reduce(grad, kept, back, x_all, weights, slopes, vecs, meta, sums, low_grad, second, chips):
    q, k_, v, mixed_all, lse, act, slope, hidden_all, normed_all, u1, u2, r1, r2 = kept
    gg0, gg1, gl, ga, gq, gk, gv = back
    rows, width = grad.shape
    local, units = weights[0].shape[2], weights[4].shape[2]
    ft = CW
    tiles = units // ft
    heads_steps = local // CW
    seqs = 2
    bt = 128
    lefts = [gl, normed_all, x_all, ga]
    rights = [hidden_all, gg0, gg1, gq, gk, gv, mixed_all]
    group_of = [0, 1, 1, 2, 2, 2, 3]
    member_of = [0, 0, 1, 0, 1, 2, 0]
    half = width // 2
    quarter = half // 2
    per_pair = 2 * ft // bt
    pairs = tiles // 2
    ffn_blocks = 3 * per_pair * pairs
    head_blocks = local // bt
    total = ffn_blocks + 4 * head_blocks
    ring, mines, gives = 4, CORE_LAG + 1, 4
    ahead_of = 4
    drain = CORE_LAG + CROSS_LAG + 2 * (chips - 1) * CHAIN_LAG + 1
    vec_shape = sums.shape
    shard_rows = rows // 2
    norm_at = 2 * tiles
    head_at = norm_at + 1
    end_at = head_at + 4 * heads_steps
    x_flip, ga_flip = ffn_blocks - per_pair, ffn_blocks + per_pair
    up_rows = units // width
    assert ahead_of + ffn_blocks - ring > end_at

    def kernel(*refs):
        meta_ref, slope_ref, vec_ref = refs[:3]
        g_hbm, q_hbm, k_hbm, v_hbm, lse_hbm, a_hbm, b_hbm, u1_hbm, u2_hbm, r1_hbm, r2_hbm = refs[3:14]
        (qkv_own_ref, qkv_oth_ref, o_own_ref, o_oth_ref, up_own_ref, up_oth_ref, down_own_ref, down_oth_ref) = refs[14:22]
        left_refs, right_refs = refs[22:26], refs[26:33]
        sums_ref, low_grad_ref, second_refs = refs[33], refs[34], refs[35 : 35 + 2 * seqs]
        outs, sums_out, rows_out = refs[39:43], refs[43], refs[44]
        fresh = refs[45:50]
        gx_out, gxl_out = refs[50:52]
        (
            acc, from_x, from_z, flip, stage, tile, mine, give, vec, vec_in, vec_all,
            g_ref, u_ref, r_ref, low_ref, gacc_ref, w_ref, o_ref, qkv_ref, gqkv_ref, lse_ref, gm_ref, dist_ref,
            part_sums, ub_sums, qv_sums,
            tile_sem, stage_sem, give_send, core_recv, x_send, x_recv, z_send, z_recv, f_send, f_recv,
            store_sem, out_send, out_recv, v_load, v_send, v_recv, r_send, r_recv,
            g_sem, w_sem, t_sem, e_sem,
        ) = refs[52:]
        final = from_x
        t, c, z, last, core, cross, above, below = neighbours()
        section = lax.axis_index("section")
        first = section == 0
        greet(c, z, chips, core, cross)
        fresh_of = {1: fresh[0], 2: fresh[1], 3: fresh[2], 4: fresh[3], 5: fresh[4]}
        vec_w = vec_ref[...]

        def remote(src, dst, send, recv, device):
            return pltpu.make_async_remote_copy(
                src_ref=src, dst_ref=dst, send_sem=send, recv_sem=recv, device_id=device, device_id_type=MESH
            )

        def valid(k):
            return (k >= 0) & (k < total)

        def member(k, visit):
            for m in range(3):
                @pl.when((k < ffn_blocks) & (lax.rem(k, 3 * per_pair) // per_pair == m))
                def _(m=m):
                    visit(m, k // (3 * per_pair) * per_pair + lax.rem(k, per_pair))

            for m in range(3, 7):
                base = ffn_blocks + (m - 3) * head_blocks

                @pl.when((k >= base) & (k < base + head_blocks))
                def _(m=m, base=base):
                    visit(m, k - base)

        def load_tile(k):
            at = lax.rem(k, ring)

            def visit(m, j):
                count = right_refs[m].shape[2] // (2 * bt)
                for side in range(2):
                    cols = block(side * count + j, bt)
                    where = pl.ds(side * bt, bt)
                    copy(right_refs[m].at[0, :, cols], tile.at[at, 0, :, where], tile_sem.at[at]).start()
                    if m not in fresh_of:
                        copy(right_refs[m].at[1, :, cols], tile.at[at, 1, :, where], tile_sem.at[at]).start()
                        continue

                    @pl.when(first)
                    def _(cols=cols, where=where):
                        copy(fresh_of[m].at[:, cols], tile.at[at, 1, :, where], tile_sem.at[at]).start()

                    @pl.when(section == 1)
                    def _(cols=cols, where=where):
                        copy(right_refs[m].at[1, :, cols], tile.at[at, 1, :, where], tile_sem.at[at]).start()

            member(k, visit)

        def take_left(g, at, mine_low):
            copy(left_refs[g].at[0], stage.at[0], stage_sem.at[0]).start()
            if mine_low is None:
                copy(left_refs[g].at[1], stage.at[1], stage_sem.at[1]).start()
                arrived(stage.at[1], stage_sem.at[1])
            else:
                @pl.when(first)
                def _():
                    stage[1] = low_ref[mine_low]

                @pl.when(section == 1)
                def _():
                    copy(left_refs[g].at[1], stage.at[1], stage_sem.at[1]).start()
                    arrived(stage.at[1], stage_sem.at[1])

            arrived(stage.at[0], stage_sem.at[0])
            for m in range(seqs):
                flip[at, :, m * rows : (m + 1) * rows] = stage[m].T

        def place_of(u):
            within = lax.rem(u, 4)
            side = within // 2
            return side, u // 4 * 2 + lax.rem(within, 2)

        def start_f(u):
            at = lax.rem(u, 2)
            side, j = place_of(u)
            pick(side * tiles + j, tiles, (up_own_ref, down_own_ref), (up_oth_ref, down_oth_ref),
                 lambda ref, jj: [(ref[0].at[:, :, block(jj, ft)], w_ref.at[at, pl.ds(0, 2)], w_sem.at[at, 0]),
                                  (ref[1].at[:, block(jj, ft)], w_ref.at[at, 2], w_sem.at[at, 1])])
            for n, ref in enumerate((a_hbm, b_hbm)):
                copy(ref.at[1, :, block(side * tiles + j, ft)], qkv_ref.at[at, n], w_sem.at[at, 2 + n]).start()

        def write_tile(u):
            at = lax.rem(u, 2)
            side, j = place_of(u)
            return [copy(gqkv_ref.at[at, n], fresh[n].at[:, block(side * tiles + j, ft)], t_sem.at[at, n]) for n in range(2)]

        def start_w(i):
            at = lax.rem(i, 2)
            pick(i, heads_steps, (qkv_own_ref, o_own_ref), (qkv_oth_ref, o_oth_ref),
                 lambda ref, j: [(ref[0].at[:, :, block(j, CW)], w_ref.at[at], w_sem.at[at, 0]),
                                 (ref[1].at[block(j, CW)], o_ref.at[at], w_sem.at[at, 1])])
            for n, ref in enumerate((q_hbm, k_hbm, v_hbm)):
                copy(ref.at[1, :, block(i, CW)], qkv_ref.at[at, n], w_sem.at[at, 2 + n]).start()
            copy(lse_hbm.at[1, i], lse_ref.at[at], w_sem.at[at, 5]).start()

        def write_heads(i):
            at = lax.rem(i, 2)
            return [copy(gqkv_ref.at[at, n], fresh[2 + n].at[:, block(i, CW)], t_sem.at[at, n]) for n in range(3)]

        def norm_load(index, u_hbm, r_hbm):
            return [copy(u_hbm.at[1], u_ref, g_sem.at[index]), copy(r_hbm.at[1], r_ref, g_sem.at[index + 1])]

        def begin():
            copy(g_hbm, g_ref, g_sem.at[0]).start()
            for item in norm_load(1, u2_hbm, r2_hbm):
                item.start()
            start_f(jnp.int32(0))
            start_f(jnp.int32(1))
            copy(g_hbm, g_ref, g_sem.at[0]).wait()
            for item in norm_load(1, u2_hbm, r2_hbm):
                item.wait()
            totals = [jnp.zeros((1, width), F32)] * 3
            for rs in halves(rows):
                grad_y = g_ref[rs, :].astype(F32)
                u = u_ref[rs, :].astype(F32)
                grad_c = norm_back(grad_y, u, r_ref[rs, 0:1], vec_w[4:5])
                gacc_ref[rs, :] = grad_c
                low_ref[0, rs, :] = grad_c.astype(BF)
                for index, values in enumerate((grad_y * u, grad_y, grad_c)):
                    totals[index] += row_sum(values)
            for index in range(3):
                part_sums[index : index + 1, :] = totals[index]
            for item in norm_load(1, u1_hbm, r1_hbm):
                item.start()

        def ffn_unit(u):
            at = lax.rem(u, 2)

            @pl.when(u >= 1)
            def _():
                for item in write_tile(u - 1):
                    item.wait()

            arrived(w_ref.at[at, pl.ds(0, 2)], w_sem.at[at, 0])
            arrived(w_ref.at[at, 2], w_sem.at[at, 1])
            for n in range(2):
                arrived(qkv_ref.at[at, n], w_sem.at[at, 2 + n])
            gh = dot(low_ref[0], w_ref[at, 2])
            g0 = (gh * qkv_ref[at, 1].astype(F32)).astype(BF)
            g1 = (gh * qkv_ref[at, 0].astype(F32)).astype(BF)
            gqkv_ref[at, 0] = g0
            gqkv_ref[at, 1] = g1
            side, j = place_of(u)
            cols = block(side * tiles + j, ft)
            ub_sums[0:1, cols] = row_sum(g0.astype(F32))
            ub_sums[1:2, cols] = row_sum(g1.astype(F32))
            gacc_ref[...] += dot(g0, w_ref[at, 0], NT) + dot(g1, w_ref[at, 1], NT)

            @pl.when(u + 2 < 2 * tiles)
            def _():
                start_f(u + 2)

            for item in write_tile(u):
                item.start()

        def norm_unit():
            for item in write_tile(jnp.int32(2 * tiles - 1)):
                item.wait()
            for i in range(2):
                start_w(jnp.int32(i))
            for item in norm_load(1, u1_hbm, r1_hbm):
                item.wait()
            totals = [jnp.zeros((1, width), F32)] * 3
            for rs in halves(rows):
                grad_n = gacc_ref[rs, :]
                u = u_ref[rs, :].astype(F32)
                grad_a = norm_back(grad_n, u, r_ref[rs, 0:1], vec_w[1:2])
                low_ref[1, rs, :] = grad_a.astype(BF)
                gacc_ref[rs, :] = grad_a
                for index, values in enumerate((grad_n * u, grad_n, grad_a)):
                    totals[index] += row_sum(values)
            for index in range(3):
                part_sums[3 + index : 4 + index, :] = totals[index]

        def head_unit(a):
            i = a // 2
            pair = lax.rem(a, 2)
            at = lax.rem(i, 2)
            scale = BF(1.0 / math.sqrt(HD))

            @pl.when(pair == 0)
            def _():
                for index, ref in enumerate(
                    (w_ref.at[at], o_ref.at[at], qkv_ref.at[at, 0], qkv_ref.at[at, 1], qkv_ref.at[at, 2], lse_ref.at[at])
                ):
                    arrived(ref, w_sem.at[at, index])

                @pl.when(i >= 2)
                def _():
                    for item in write_heads(i - 2):
                        item.wait()

                gm_ref[...] = dot(low_ref[1], o_ref[at], NT).astype(BF)

            cols = block(pair, 2 * HD)
            query2 = qkv_ref[at, 0, :, cols] * scale
            key2 = qkv_ref[at, 1, :, cols]
            value2 = qkv_ref[at, 2, :, cols]
            gm2 = gm_ref[:, cols]
            parts = [[], [], []]
            for head in range(2):
                here = slice(head * HD, (head + 1) * HD)
                query, key, gm = query2[:, here], key2[:, here], gm2[:, here]
                scores = dot(key, query, NT)
                scores = scores - dist_ref[...] * slope_ref[i * PER + pair * 2 + head]
                likely = jnp.exp(scores - lse_ref[at, pl.ds(pair * 2 + head, 1), :])
                parts[2].append(dot(likely.astype(BF), gm).astype(BF))
                tt = likely * dot(value2[:, here], gm, NT)
                inner = jnp.sum(tt, axis=0, keepdims=True)
                gs = (tt - likely * inner).astype(BF)
                parts[1].append(dot(gs, query).astype(BF))
                parts[0].append(dot(gs, key * scale, TN).astype(BF))
            for n in range(3):
                gqkv_ref[at, n, :, cols] = jnp.concatenate(parts[n], axis=1)

            @pl.when(pair == 1)
            def _():
                for index, n in enumerate((0, 2)):
                    qv_sums[index : index + 1, block(i, CW)] = row_sum(gqkv_ref[at, n].astype(F32))
                gacc_ref[...] += (
                    dot(gqkv_ref[at, 0], w_ref[at, 0], NT)
                    + dot(gqkv_ref[at, 1], w_ref[at, 1], NT)
                    + dot(gqkv_ref[at, 2], w_ref[at, 2], NT)
                )

                @pl.when(i + 2 < 2 * heads_steps)
                def _():
                    start_w(i + 2)

                for item in write_heads(i):
                    item.start()

        ends = [(g_ref, gxl_out), (gacc_ref, gx_out)]

        def end_unit():
            for i in (2 * heads_steps - 2, 2 * heads_steps - 1):
                for item in write_heads(jnp.int32(i)):
                    item.wait()
            g_ref[...] = gacc_ref[...].astype(BF)
            for index, item in enumerate(ends):
                copy(*item, e_sem.at[index]).start()
            vec[0, 0:6] += part_sums[0:6]
            for own in range(2):
                @pl.when(t == own)
                def _(own=own):
                    for n in range(2):
                        for side in range(2):
                            place = own if side == 0 else 1 - own
                            for j in range(up_rows):
                                at = 6 + (2 * n + place) * up_rows + j
                                start = side * units + j * width
                                vec[0, at : at + 1] += ub_sums[n : n + 1, start : start + width]
                            at = 6 + 4 * up_rows + n
                            cols = slice(place * local, (place + 1) * local)
                            vec[0, at : at + 1, cols] += qv_sums[n : n + 1, side * local : (side + 1) * local]

            for index, item in enumerate(ends):
                copy(*item, e_sem.at[index]).wait()

        vec_load = copy(sums_ref, vec.at[0], v_load)
        vec_load.start()

        @pl.when(first)
        def _():
            begin()
            fill_distance(dist_ref, meta_ref[2])

        take_left(0, 0, 0)
        vec_load.wait()
        vec_core = remote(vec.at[0], vec_in.at[0], v_send.at[0], v_recv.at[0], core)
        vec_cross = remote(vec.at[1], vec_in.at[1], v_send.at[1], v_recv.at[1], cross)

        row_sources = ((low_grad_ref, gxl_out), second_refs)

        def row_copy(sources, m):
            source = sources[m].at[block(1 - t, shard_rows)]
            return remote(source, rows_out.at[m], r_send.at[m], r_recv.at[m], cross)

        up = pl.ds(0, quarter)
        down = pl.ds(quarter, quarter)
        sides = ((up, 0, z, above, below), (down, 1, last - z, below, above))

        @pl.loop(0, ahead_of + total + drain)
        def _(turn):
            s = turn - ahead_of

            @pl.when(first)
            def _():
                @pl.when(turn < norm_at)
                def _():
                    ffn_unit(turn)

                @pl.when(turn == norm_at)
                def _():
                    norm_unit()

                @pl.when((turn >= head_at) & (turn < end_at))
                def _():
                    head_unit(turn - head_at)

                @pl.when(turn == end_at)
                def _():
                    end_unit()

            @pl.when(s == 0)
            def _():
                for k in range(ring - 1):
                    load_tile(jnp.int32(k))

            @pl.when(valid(s))
            def _():
                @pl.when(s == per_pair - 2)
                def _():
                    take_left(1, 1, None)

                @pl.when(s == x_flip)
                def _():
                    take_left(2, 0, None)

                @pl.when(s == ga_flip)
                def _():
                    take_left(3, 1, 1)

                at = lax.rem(s, ring)
                arrived(tile.at[at], tile_sem.at[at])
                give_at = lax.rem(s, gives)

                @pl.when(s >= gives)
                def _():
                    arrived(give.at[give_at], give_send.at[give_at])

                ffn_flip = jnp.where(lax.rem(s, 3 * per_pair) // per_pair == 0, 0, 1)
                which = jnp.where(s < ffn_blocks, ffn_flip, jnp.where(s < ffn_blocks + 3 * head_blocks, 0, 1))
                for place, store, spot in ((1 - c, give, give_at), (c, mine, lax.rem(s, mines))):
                    here = block(place, half)
                    product = dot(flip[which, here, :rows], tile[at, 0])
                    for m in range(1, seqs):
                        product += dot(flip[which, here, m * rows : (m + 1) * rows], tile[at, m])
                    store[spot, 1] = product[:, :bt].astype(BF)
                    store[spot, 0] = product[:, bt:].astype(BF)

            @pl.when((s >= 0) & (s + ring - 1 < total))
            def _():
                load_tile(s + ring - 1)

            k1 = s - CORE_LAG

            @pl.when(valid(k1))
            def _():
                arrived(acc.at[k1], core_recv.at[k1])
                at = lax.rem(k1, mines)
                for side in range(2):
                    acc[k1, side] = (acc[k1, side].astype(F32) + mine[at, side].astype(F32)).astype(BF)

            k2 = k1 - CROSS_LAG

            @pl.when(valid(k2))
            def _():
                arrived(from_x.at[k2], x_recv.at[k2])
                acc[k2, 1] = (acc[k2, 1].astype(F32) + from_x[k2].astype(F32)).astype(BF)

            for rows_, way, place, ahead, behind in sides:
                k3 = k2 - CHAIN_LAG * place

                @pl.when(valid(k3) & (place > 0))
                def _(rows_=rows_, way=way, k3=k3):
                    arrived(from_z.at[k3, rows_], z_recv.at[way, k3])
                    acc[k3, 1, rows_] = (acc[k3, 1, rows_].astype(F32) + from_z[k3, rows_].astype(F32)).astype(BF)

                k4 = k2 - CHAIN_LAG * (2 * last - place)

                @pl.when(valid(k4) & (place == last))
                def _(rows_=rows_, k4=k4):
                    final[k4, rows_] = acc[k4, 1, rows_]

                @pl.when(valid(k4) & (place < last))
                def _(rows_=rows_, way=way, k4=k4):
                    arrived(final.at[k4, rows_], f_recv.at[way, k4])

            @pl.when(valid(s))
            def _():
                at = lax.rem(s, gives)
                remote(give.at[at], acc.at[s], give_send.at[at], core_recv.at[s], core).start()

            @pl.when(valid(k1))
            def _():
                remote(acc.at[k1, 0], from_x.at[k1], x_send, x_recv.at[k1], cross).start()

            for number, sources in enumerate(row_sources):
                @pl.when((k1 == total - 1) & (section == number))
                def _(sources=sources):
                    for m in range(len(sources)):
                        row_copy(sources, m).start()

            for rows_, way, place, ahead, behind in sides:
                k3 = k2 - CHAIN_LAG * place

                @pl.when(valid(k3) & (place < last))
                def _(rows_=rows_, way=way, k3=k3, ahead=ahead):
                    remote(acc.at[k3, 1, rows_], from_z.at[k3, rows_], z_send.at[way], z_recv.at[way, k3], ahead).start()

                k4 = k2 - CHAIN_LAG * (2 * last - place)

                @pl.when(valid(k4) & (place > 0))
                def _(rows_=rows_, way=way, k4=k4, behind=behind):
                    remote(final.at[k4, rows_], final.at[k4, rows_], f_send.at[way], f_recv.at[way, k4], behind).start()

            k5 = k2 - CHAIN_LAG * 2 * last

            @pl.when(valid(k5))
            def _():
                def visit(m, j):
                    dst = outs[group_of[m]].at[member_of[m], block(c, half), block(j, bt)]
                    copy(final.at[k5], dst, store_sem).start()
                    remote(final.at[k5], dst, out_send, out_recv, core).start()

                member(k5, visit)

            @pl.when(turn == end_at + 1)
            def _():
                vec_core.start()

            @pl.when(turn == end_at + 6)
            def _():
                vec_core.wait_recv()
                vec[1] = vec[0] + vec_in[0]

            @pl.when(turn == end_at + 7)
            def _():
                vec_cross.start()

            @pl.when(turn == end_at + 13)
            def _():
                vec_cross.wait_recv()
                vec_all[z] = vec[1] + vec_in[1]

            @pl.when(turn == end_at + 14)
            def _():
                for shift in range(1, chips):
                    to = lax.rem(z + shift, chips)
                    remote(
                        vec_all.at[z], vec_all.at[z], v_send.at[1 + shift], v_recv.at[1 + shift], {"dp": to * 2 + c}
                    ).start()

        for number, sources in enumerate(row_sources):
            @pl.when(section == number)
            def _(sources=sources):
                for m in range(len(sources)):
                    row_copy(sources, m).wait()

        vec_core.wait_send()
        vec_cross.wait_send()
        for shift in range(1, chips):
            origin = lax.rem(z + chips - shift, chips)
            arrived(vec_all.at[origin], v_recv.at[1 + shift])
            arrived(vec_all.at[z], v_send.at[1 + shift])
        whole = vec_all[0]
        for chip in range(1, chips):
            whole += vec_all[chip]
        sums_out[...] = whole
        for at in range(gives):
            arrived(give.at[at], give_send.at[at])
        arrived(acc.at[:, 0], x_send)
        for rows_, way, place, ahead, behind in sides:
            @pl.when(place < last)
            def _(rows_=rows_, way=way):
                arrived(from_z.at[:, rows_], z_send.at[way])

            @pl.when(place > 0)
            def _(rows_=rows_, way=way):
                arrived(final.at[:, rows_], f_send.at[way])

        arrived(final, out_send)
        arrived(final, store_sem)
        arrived(final, out_recv)

    sem = pltpu.SemaphoreType.DMA
    flops = 2 * seqs * rows * width * 2 * bt * total
    members = [member_of[index] for index in range(7)]
    shapes = [(sum(g == index for g in group_of), width, rights[group_of.index(index)].shape[2] // 2) for index in range(4)]
    return pl.pallas_call(
        kernel,
        in_specs=[SMEM, SMEM, WHOLE] + [ANY] * (32 + 2 * seqs),
        out_specs=[ANY] * 4 + [WHOLE] + [ANY] * 8,
        out_shape=[jax.ShapeDtypeStruct(s, BF) for s in shapes]
        + [jax.ShapeDtypeStruct(vec_shape, F32), jax.ShapeDtypeStruct((2 * seqs, shard_rows, width), BF)]
        + [jax.ShapeDtypeStruct((rows, 2 * units), BF)] * 2
        + [jax.ShapeDtypeStruct((rows, 2 * local), BF)] * 3
        + [jax.ShapeDtypeStruct((rows, width), F32), jax.ShapeDtypeStruct((rows, width), BF)],
        scratch_shapes=[
            pltpu.VMEM((total, 2, half, bt), BF),
            pltpu.VMEM((total, half, bt), BF),
            pltpu.VMEM((total, half, bt), BF),
            pltpu.VMEM((2, width, seqs * rows), BF),
            pltpu.VMEM((seqs, rows, width), BF),
            pltpu.VMEM((ring, seqs, rows, 2 * bt), BF),
            pltpu.VMEM((mines, 2, half, bt), BF),
            pltpu.VMEM((gives, 2, half, bt), BF),
            pltpu.VMEM((2,) + vec_shape, F32),
            pltpu.VMEM((2,) + vec_shape, F32),
            pltpu.VMEM((chips,) + vec_shape, F32),
            pltpu.VMEM((rows, width), BF),
            pltpu.VMEM((rows, width), BF),
            pltpu.VMEM((rows, 128), F32),
            pltpu.VMEM((2, rows, width), BF),
            pltpu.VMEM((rows, width), F32),
            pltpu.VMEM((2, 3, width, CW), BF),
            pltpu.VMEM((2, CW, width), BF),
            pltpu.VMEM((2, 3, rows, CW), BF),
            pltpu.VMEM((2, 3, rows, CW), BF),
            pltpu.VMEM((2, 8, rows), F32),
            pltpu.VMEM((rows, CW), BF),
            pltpu.VMEM((rows, rows), F32),
            pltpu.VMEM((8, width), F32),
            pltpu.VMEM((2, 2 * units), F32),
            pltpu.VMEM((2, 2 * local), F32),
            sem((ring,)), sem((2,)), sem((gives,)), sem((total,)), sem, sem((total,)),
            sem((2,)), sem((2, total)), sem((2,)), sem((2, total)),
            sem, sem, sem, sem, sem((chips + 1,)), sem((chips + 1,)), sem((2 * seqs,)), sem((2 * seqs,)),
            sem((3,)), sem((2, 6)), sem((2, 3)), sem((2,)),
        ],
        compiler_params=pltpu.CompilerParams(
            collective_id=0, has_side_effects=True, vmem_limit_bytes=67_000_000
        ),
        cost_estimate=pl.CostEstimate(flops=flops, bytes_accessed=100 << 20, transcendentals=0),
        name="backward_and_reduce",
    )(
        meta, slopes, vecs, grad, q, k_, v, lse, act, slope, u1, u2, r1, r2, *weights, *lefts, *rights, sums, low_grad, *second
    )


def exchange_rows(outputs, deps):
    seqs = len(outputs)
    rows, width = outputs[0].shape
    shard_rows = rows // 2
    n_in = seqs + len(deps)

    def kernel(*refs):
        y_refs, out_ref = refs[:seqs], refs[n_in]
        stage, send, recv, l_sem = refs[n_in + 1 :]
        t = lax.axis_index("tensor")
        cross = {"tensor": 1 - t}
        barrier = pltpu.get_barrier_semaphore()
        pl.semaphore_signal(barrier, inc=1, device_id=cross, device_id_type=MESH)
        pl.semaphore_wait(barrier, 1)

        @pl.when(lax.axis_index("section") == 0)
        def _():
            for m in range(seqs):
                pltpu.make_async_remote_copy(
                    src_ref=y_refs[m].at[block(1 - t, shard_rows)], dst_ref=out_ref.at[t * seqs + m],
                    send_sem=send.at[m], recv_sem=recv.at[m], device_id=cross, device_id_type=MESH,
                ).start()
            for m in range(seqs):
                copy(y_refs[m].at[block(t, shard_rows)], stage.at[m], l_sem.at[m]).start()
            for m in range(seqs):
                arrived(stage.at[m], l_sem.at[m])
                copy(stage.at[m], out_ref.at[t * seqs + m], l_sem.at[m]).start()
            for m in range(seqs):
                arrived(stage.at[m], l_sem.at[m])
            for m in range(seqs):
                arrived(out_ref.at[(1 - t) * seqs + m], recv.at[m])
                arrived(stage.at[m], send.at[m])

    sem = pltpu.SemaphoreType.DMA
    return pl.pallas_call(
        kernel,
        in_specs=[ANY] * n_in,
        out_specs=ANY,
        out_shape=jax.ShapeDtypeStruct((2 * seqs, shard_rows, width), BF),
        scratch_shapes=[pltpu.VMEM((seqs, shard_rows, width), BF), sem((seqs,)), sem((seqs,)), sem((seqs,))],
        compiler_params=pltpu.CompilerParams(collective_id=2, has_side_effects=True),
        cost_estimate=pl.CostEstimate(flops=0, bytes_accessed=0, transcendentals=0),
        name="exchange_rows",
    )(*outputs, *deps)


def widen(reduced, row_grads, got, produced, outputs, sums, units, local):
    shard_rows, width = got.shape[1:]
    seqs = got.shape[0] // 2
    n = len(reduced)
    jobs = []
    for index, array in enumerate(reduced):
        lead, depth, columns = array.shape
        step = 512 * 1024 // columns
        if index == n - 1:
            jobs += [(index, 0, at, depth // 2, columns) for at in range(0, depth, depth // 2)]
        else:
            jobs += [(index, part, at, step, columns) for part in range(lead) for at in range(0, depth, step)]
    jobs += [(n, m, 0, shard_rows, width) for m in range(seqs)] + [(n + 1, m, 0, shard_rows, width) for m in range(seqs)]
    jobs += [(n + 2, m, 0, shard_rows, width) for m in range(2 * seqs)]
    ring = 3
    n_in = n + 3 * seqs + 3
    parts = units // width

    def kernel(*refs):
        ins = refs[:n]
        grad_refs = refs[n : n + 2 * seqs]
        got_ref, produced_ref = refs[n + 2 * seqs : n + 2 * seqs + 2]
        y_refs, sums_ref = refs[n + 2 * seqs + 2 : n_in - 1], refs[n_in - 1]
        outs = refs[n_in : n_in + n + 2]
        qv_ref, out_bias_ref, gain_ref, shift_ref, ub_ref, down_bias_ref = refs[n_in + n + 2 : n_in + n + 8]
        shapes = sorted({(j[3], j[4]) for j in jobs if j[0] != n})
        buffers = refs[n_in + n + 8 :]
        wide_rows, in_sem, out_sem = buffers[0], buffers[1], buffers[2]
        low = {s: buffers[3 + 2 * i] for i, s in enumerate(shapes)}
        wide = {s: buffers[4 + 2 * i] for i, s in enumerate(shapes)}
        t = lax.axis_index("tensor")
        section = lax.axis_index("section")

        def load(number):
            index, part, at, rows, columns = jobs[number]
            s = number % ring
            if index < n:
                copy(ins[index].at[part, pl.ds(at, rows)], low[rows, columns].at[s], in_sem.at[s]).start()
            elif index == n:
                for turn in range(2):
                    @pl.when(section == turn)
                    def _(turn=turn):
                        source = grad_refs[turn * seqs + part].at[block(t, shard_rows)]
                        copy(source, wide_rows.at[part], in_sem.at[s]).start()
            elif index == n + 1:
                copy(got_ref.at[part], low[rows, columns].at[s], in_sem.at[s]).start()
            else:
                @pl.when(section == 0)
                def _():
                    copy(produced_ref.at[part], low[rows, columns].at[s], in_sem.at[s]).start()

                @pl.when(section == 1)
                def _():
                    source = y_refs[part].at[block(t, shard_rows)] if part < seqs else got_ref.at[part]
                    copy(source, low[rows, columns].at[s], in_sem.at[s]).start()

        def store(number):
            index, part, at, rows, columns = jobs[number]
            s = number % ring
            if index < n - 1:
                return copy(wide[rows, columns].at[s], outs[index].at[part, pl.ds(at, rows)], out_sem.at[s])
            if index == n - 1:
                return copy(wide[rows, columns].at[s], outs[index].at[:, pl.ds(at, rows)], out_sem.at[s])
            if index == n:
                return copy(wide_rows.at[part], outs[n].at[t * seqs + part], out_sem.at[s])
            if index == n + 1:
                return copy(wide[rows, columns].at[s], outs[n].at[(1 - t) * seqs + part], out_sem.at[s])
            side, m = divmod(part, seqs)
            spread = (t + side - 2 * t * side) * seqs + m
            return copy(low[rows, columns].at[s], outs[n + 1].at[jnp.where(section == 0, part, spread)], out_sem.at[s])

        for number in range(ring):
            load(number)
        gain_ref[0:1] = sums_ref[3:4]
        gain_ref[1:2] = sums_ref[0:1]
        shift_ref[0:1] = sums_ref[4:5]
        shift_ref[1:2] = sums_ref[1:2]
        out_bias_ref[...] = sums_ref[5:6]
        down_bias_ref[...] = sums_ref[2:3]
        for half in range(2):
            @pl.when(t == half)
            def _(half=half):
                for g in range(2):
                    for j in range(parts):
                        at = 6 + (2 * g + half) * parts + j
                        ub_ref[g : g + 1, j * width : (j + 1) * width] = sums_ref[at : at + 1]
                    at = 6 + 4 * parts + g
                    qv_ref[g : g + 1] = sums_ref[at : at + 1, half * local : (half + 1) * local]

        for number, (index, part, at, rows, columns) in enumerate(jobs):
            s = number % ring
            if index == n:
                arrived(wide_rows.at[part], in_sem.at[s])
            else:
                arrived(low[rows, columns].at[s], in_sem.at[s])
            if number >= ring and jobs[number - ring][0] != n + 2:
                store(number - ring).wait()
            if index == n - 1:
                wide[rows, columns][s] = low[rows, columns][s].astype(F32).T
            elif index not in (n, n + 2):
                wide[rows, columns][s] = low[rows, columns][s].astype(F32)
            store(number).start()
            if index == n + 2:
                store(number).wait()
            if number + ring < len(jobs):
                load(number + ring)
        for number in range(len(jobs) - ring, len(jobs)):
            if jobs[number][0] != n + 2:
                store(number).wait()

    shapes = sorted({(j[3], j[4]) for j in jobs if j[0] != n})
    square = (reduced[-1].shape[1] // 2, reduced[-1].shape[2])
    last = reduced[-1].shape
    sem = pltpu.SemaphoreType.DMA
    buffers = []
    for s in shapes:
        buffers += [pltpu.VMEM((ring,) + s, BF), pltpu.VMEM((ring,) + ((s[1], s[0]) if s == square else s), F32)]
    return pl.pallas_call(
        kernel,
        in_specs=[ANY] * (n_in - 1) + [WHOLE],
        out_specs=[ANY] * (n + 2) + [WHOLE] * 6,
        out_shape=[jax.ShapeDtypeStruct(r.shape, F32) for r in reduced[:-1]]
        + [jax.ShapeDtypeStruct((last[2], last[1]), F32), jax.ShapeDtypeStruct((2 * seqs, shard_rows, width), F32)]
        + [jax.ShapeDtypeStruct((2 * seqs, shard_rows, width), BF)]
        + [
            jax.ShapeDtypeStruct(shape, F32)
            for shape in ((2, local), (1, width), (2, width), (2, width), (2, units), (1, width))
        ],
        scratch_shapes=[pltpu.VMEM((seqs, shard_rows, width), F32), sem((ring,)), sem((ring,))] + buffers,
        compiler_params=pltpu.CompilerParams(vmem_limit_bytes=VMEM_LIMIT),
        cost_estimate=pl.CostEstimate(flops=0, bytes_accessed=56 << 20, transcendentals=0),
        name="widen",
    )(*reduced, *row_grads, got, produced, *outputs, sums)


MASKED = -1000000000.0


def shifted(value, axis, steps):
    count = lax.axis_size(axis)
    first, last = (max(0, -steps), min(count, count - steps))
    return lax.ppermute(value, axis, [(source, source + steps) for source in range(first, last)])


def layer_norm(values, gain, shift):
    mean = jnp.mean(values, axis=-1, keepdims=True)
    centred = values - mean
    spread = jnp.mean(centred * centred, axis=-1, keepdims=True)
    return centred * lax.rsqrt(spread + EPS) * gain + shift


def alibi_slopes(first, count, heads):
    index = (first + jnp.arange(count)).astype(jnp.float32)
    return jnp.exp2(-8.0 * (index + 1.0) / heads)


def attention_core(projected, qv_bias, slopes, key_ok):
    rows = projected.shape[0]
    width = projected.shape[2]
    count = slopes.shape[0]
    size = width // count
    query = (projected[:, 0] + qv_bias[0]).astype(jnp.bfloat16).reshape(rows, count, size)
    key = projected[:, 1].astype(jnp.bfloat16).reshape(rows, count, size)
    value = (projected[:, 2] + qv_bias[1]).astype(jnp.bfloat16).reshape(rows, count, size)
    place = jnp.arange(rows).astype(jnp.float32)
    distance = jnp.abs(place[:, None] - place[None, :])
    scale = 1.0 / math.sqrt(size)
    scores = (
        jnp.einsum("qhd,khd->hqk", query, key, preferred_element_type=jnp.float32) * scale
        - slopes[:, None, None] * distance[None]
    )
    scores = jnp.where(key_ok[None, None, :], scores, MASKED)
    weights = jax.nn.softmax(scores, axis=-1)
    weights_low = weights.astype(jnp.bfloat16)
    mixed = jnp.einsum("hqk,khd->qhd", weights_low, value, preferred_element_type=jnp.float32)
    mixed = mixed.reshape(rows, width).astype(jnp.bfloat16)
    return (query, key, value, weights, weights_low, mixed)


def attention_back(parts, grad_mixed, key_ok):
    query, key, value, weights, weights_low, mixed = parts
    rows, count, size = query.shape
    scale = 1.0 / math.sqrt(size)
    grad_low = grad_mixed.astype(jnp.bfloat16).reshape(rows, count, size)
    grad_weights = jnp.einsum("qhd,khd->hqk", grad_low, value, preferred_element_type=jnp.float32)
    grad_value = jnp.einsum(
        "hqk,qhd->khd", weights_low, grad_low, preferred_element_type=jnp.float32
    )
    inner = jnp.sum(weights * grad_weights, axis=-1, keepdims=True)
    grad_scores = weights * (grad_weights - inner)
    grad_scores = jnp.where(key_ok[None, None, :], grad_scores, 0.0).astype(jnp.bfloat16)
    grad_query = (
        jnp.einsum("hqk,khd->qhd", grad_scores, key, preferred_element_type=jnp.float32) * scale
    ).astype(jnp.bfloat16)
    grad_key = (
        jnp.einsum("hqk,qhd->khd", grad_scores, query, preferred_element_type=jnp.float32) * scale
    ).astype(jnp.bfloat16)
    grad_value = grad_value.astype(jnp.bfloat16)
    width = count * size
    grad_query = grad_query.reshape(rows, width)
    grad_key = grad_key.reshape(rows, width)
    grad_value = grad_value.reshape(rows, width)
    grad_projected = jnp.stack([grad_query, grad_key, grad_value], axis=1).reshape(rows, 3 * width)
    qv_grad = jnp.stack(
        [
            jnp.sum(grad_query.astype(jnp.float32), axis=0),
            jnp.sum(grad_value.astype(jnp.float32), axis=0),
        ]
    )
    return (grad_projected, qv_grad)


def gelu_product(both):
    return jax.nn.gelu(both[:, 0], approximate=False) * both[:, 1]


def geglu(lifted, up_bias):
    return gelu_product(lifted + up_bias[None])


def ffn_grads(rows_low, grad_low, up_weight, up_bias, down_weight):
    lifted = jnp.einsum("sd,gdf->sgf", rows_low, up_weight, preferred_element_type=jnp.float32)
    hidden, geglu_back = jax.vjp(gelu_product, lifted + up_bias[None])
    grad_hidden = jnp.einsum("sd,df->sf", grad_low, down_weight, preferred_element_type=jnp.float32)
    (grad_both,) = geglu_back(grad_hidden)
    grad_lifted = grad_both.astype(jnp.bfloat16)
    grad_bias = jnp.sum(grad_lifted.astype(jnp.float32), axis=0)
    up_grad = jnp.einsum("sd,sgf->gdf", rows_low, grad_lifted, preferred_element_type=jnp.float32)
    down_grad = jnp.einsum(
        "sd,sf->df", grad_low, hidden.astype(jnp.bfloat16), preferred_element_type=jnp.float32
    )
    return (grad_lifted, grad_bias, up_grad, down_grad)


def on_device(
    inputs,
    cotangent,
    lengths,
    w_qkv,
    b_qv,
    w_out,
    b_out,
    ln_gain,
    ln_bias,
    w_up,
    b_up,
    w_down,
    b_down,
):
    batches, shard_rows, width = inputs.shape
    parts = lax.axis_size("tensor")
    place = lax.axis_index("tensor")
    section = lax.axis_index("section")
    last_section = lax.axis_size("section") - 1
    full_rows = shard_rows * parts
    local_width = w_qkv.shape[3]
    local_heads = local_width // HD
    qkv_flat = w_qkv[0].reshape(width, 3 * local_width)
    out_weight = w_out[0]
    qv_bias = b_qv[0].astype(jnp.float32)
    out_bias = b_out[0].astype(jnp.float32)
    gains = ln_gain[0].astype(jnp.float32)
    shifts = ln_bias[0].astype(jnp.float32)
    down_bias = b_down[0].astype(jnp.float32)
    slopes = alibi_slopes(place * local_heads, local_heads, H)
    row_place = place * shard_rows + jnp.arange(shard_rows)
    kept_rows = 0

    def key_mask(length):
        return jnp.arange(full_rows) < length

    def after_attention(values, attended, bias, gain_rows, shift_rows):
        return layer_norm(values + attended + bias, gain_rows[0], shift_rows[0])

    def after_ffn(normed, lowered, bias, gain_rows, shift_rows):
        return layer_norm(normed + lowered + bias, gain_rows[1], shift_rows[1])

    def gather_inputs(values):
        return lax.all_gather(values.astype(jnp.bfloat16), "tensor", axis=0, tiled=True)

    def project(gathered):
        return jnp.dot(gathered, qkv_flat, preferred_element_type=jnp.float32).reshape(
            full_rows, 3, local_width
        )

    def attention_forward(values, length):
        gathered = gather_inputs(values)
        projected = project(gathered)
        mixed = attention_core(projected, qv_bias, slopes, key_mask(length))[5]

        def term(start, count):
            return jnp.dot(mixed, out_weight, preferred_element_type=jnp.float32)

        return (
            lax.psum_scatter(
                term(jnp.int32(0), shard_rows * lax.axis_size("tensor")).astype(jnp.bfloat16),
                "tensor",
                scatter_dimension=0,
                tiled=True,
            ).astype(jnp.float32),
            gathered,
            projected,
        )

    up_local = w_up[0]
    up_bias_local = b_up[0].astype(jnp.float32)
    down_local = w_down[0]

    def gather_normed(normed):
        return lax.all_gather(normed.astype(jnp.bfloat16), "tensor", axis=0, tiled=True)

    def ffn_forward(normed):
        lifted = jnp.einsum(
            "sd,gdf->sgf", gather_normed(normed), up_local, preferred_element_type=jnp.float32
        )
        hidden = geglu(lifted, up_bias_local).astype(jnp.bfloat16)

        def term(start, count):
            return jnp.einsum("sf,df->sd", hidden, down_local, preferred_element_type=jnp.float32)

        return lax.psum_scatter(
            term(jnp.int32(0), shard_rows * lax.axis_size("tensor")).astype(jnp.bfloat16),
            "tensor",
            scatter_dimension=0,
            tiled=True,
        ).astype(jnp.float32)

    def ffn_backward(normed, grad_lowered):
        gathered = gather_normed(normed)
        grad_whole = lax.all_gather(grad_lowered.astype(jnp.bfloat16), "tensor", axis=0, tiled=True)
        grad_lifted, grad_bias, up_grad, down_grad = ffn_grads(
            gathered, grad_whole, up_local, up_bias_local, down_local
        )

        def term(start, count):
            return jnp.einsum(
                "sgf,gdf->sd", grad_lifted, up_local, preferred_element_type=jnp.float32
            )

        grad_normed = lax.psum_scatter(
            term(jnp.int32(0), shard_rows * lax.axis_size("tensor")).astype(jnp.bfloat16),
            "tensor",
            scatter_dimension=0,
            tiled=True,
        ).astype(jnp.float32)
        return (grad_normed, (up_grad, grad_bias, down_grad))

    ffn_shapes = (up_local.shape, up_bias_local.shape, down_local.shape)

    def layer_forward(values, length):
        attended, gathered, projected = attention_forward(values, length)
        normed = after_attention(values, attended, out_bias, gains, shifts)
        lowered = ffn_forward(normed)
        return (
            after_ffn(normed, lowered, down_bias, gains, shifts),
            attended,
            lowered,
            gathered,
            projected,
        )

    def layer_backward(values, attended, lowered, length, grad_output):
        normed, attention_norm_back = jax.vjp(
            after_attention, values, attended, out_bias, gains, shifts
        )
        outcome, ffn_norm_back = jax.vjp(after_ffn, normed, lowered, down_bias, gains, shifts)
        grad_normed, grad_lowered, grad_down_bias, gain_late, shift_late = ffn_norm_back(
            grad_output
        )
        grad_from_ffn, ffn_terms = ffn_backward(normed, grad_lowered)
        grad_values, grad_attended, grad_out_bias, gain_early, shift_early = attention_norm_back(
            grad_normed + grad_from_ffn
        )
        gathered = gather_inputs(values)
        projected = project(gathered)
        grad_whole = lax.all_gather(
            grad_attended.astype(jnp.bfloat16), "tensor", axis=0, tiled=True
        )
        mask = key_mask(length)
        pieces = attention_core(projected, qv_bias, slopes, mask)
        mixed_low = pieces[5]
        out_grad = jnp.einsum(
            "se,sd->ed", mixed_low, grad_whole, preferred_element_type=jnp.float32
        )
        grad_mixed = jnp.einsum(
            "sd,ed->se", grad_whole, out_weight, preferred_element_type=jnp.float32
        )
        grad_projected, qv_grad = attention_back(pieces, grad_mixed, mask)
        qkv_grad = jnp.einsum(
            "sd,sx->dx", gathered, grad_projected, preferred_element_type=jnp.float32
        )

        def term(start, count):
            return jnp.einsum(
                "sx,dx->sd", grad_projected, qkv_flat, preferred_element_type=jnp.float32
            )

        grad_inputs = grad_values + lax.psum_scatter(
            term(jnp.int32(0), shard_rows * lax.axis_size("tensor")).astype(jnp.bfloat16),
            "tensor",
            scatter_dimension=0,
            tiled=True,
        ).astype(jnp.float32)
        terms = (
            qkv_grad,
            qv_grad,
            out_grad,
            grad_out_bias,
            gain_early + gain_late,
            shift_early + shift_late,
            ffn_terms[0],
            ffn_terms[1],
            ffn_terms[2],
            grad_down_bias,
        )
        return (grad_inputs, terms)

    def keep(store, item, batch, valid):
        old = lax.dynamic_index_in_dim(store, batch, 0, keepdims=False)
        return lax.dynamic_update_index_in_dim(store, jnp.where(valid, item, old), batch, 0)

    def forward_step(step, carry):
        (
            received,
            kept_values,
            kept_attended,
            kept_lowered,
            produced,
            kept_gathered,
            kept_projected,
        ) = carry
        index = step - section
        valid = (index >= 0) & (index < batches)
        batch = jnp.clip(index, 0, batches - 1)
        fresh = lax.dynamic_index_in_dim(
            inputs, jnp.minimum(step, batches - 1), 0, keepdims=False
        ).astype(jnp.float32)
        values = jnp.where(section == 0, fresh, received.astype(jnp.float32))
        output, attended, lowered, gathered, projected = layer_forward(values, lengths[batch])
        sent = output.astype(jnp.bfloat16)
        kept_values = keep(kept_values, values, batch, valid)
        kept_attended = keep(kept_attended, attended, batch, valid)
        kept_lowered = keep(kept_lowered, lowered, batch, valid)
        produced = keep(produced, sent, batch, valid)
        kept_gathered = keep(kept_gathered, gathered[:kept_rows], batch, valid)
        kept_projected = keep(kept_projected, projected[:kept_rows], batch, valid)
        received = shifted(sent, "section", 1)
        return (
            received,
            kept_values,
            kept_attended,
            kept_lowered,
            produced,
            kept_gathered,
            kept_projected,
        )

    store_zeros = jnp.zeros((batches, shard_rows, width), jnp.float32)
    gathered_zeros = jnp.zeros((batches, kept_rows, width), jnp.bfloat16)
    projected_zeros = jnp.zeros((batches, kept_rows, 3, local_width), jnp.float32)
    start_forward = (
        jnp.zeros((shard_rows, width), jnp.bfloat16),
        store_zeros,
        store_zeros,
        store_zeros,
        jnp.zeros((batches, shard_rows, width), jnp.bfloat16),
        gathered_zeros,
        projected_zeros,
    )
    received, kept_values, kept_attended, kept_lowered, produced, kept_gathered, kept_projected = (
        lax.fori_loop(0, batches + last_section, forward_step, start_forward)
    )

    def backward_step(step, carry):
        received, totals, grads_in = carry
        index = step - (last_section - section)
        valid = (index >= 0) & (index < batches)
        batch = jnp.clip(index, 0, batches - 1)
        length = lengths[batch]
        outer = lax.dynamic_index_in_dim(cotangent, batch, 0, keepdims=False).astype(jnp.float32)
        outer = outer * (row_place < length).astype(jnp.float32)[:, None]
        grad_output = jnp.where(section == last_section, outer, received.astype(jnp.float32))
        grad_output = jnp.where(valid, grad_output, 0.0)
        values = lax.dynamic_index_in_dim(kept_values, batch, 0, keepdims=False)
        attended = lax.dynamic_index_in_dim(kept_attended, batch, 0, keepdims=False)
        lowered = lax.dynamic_index_in_dim(kept_lowered, batch, 0, keepdims=False)
        grad_inputs, terms = layer_backward(values, attended, lowered, length, grad_output)
        totals = jax.tree.map(jnp.add, totals, terms)
        grads_in = keep(grads_in, grad_inputs, batch, valid)
        received = shifted(grad_inputs.astype(jnp.bfloat16), "section", -1)
        return (received, totals, grads_in)

    start_totals = (
        jnp.zeros((width, 3 * local_width), jnp.float32),
        jnp.zeros((2, local_width), jnp.float32),
        jnp.zeros((local_width, width), jnp.float32),
        jnp.zeros((width,), jnp.float32),
        jnp.zeros((2, width), jnp.float32),
        jnp.zeros((2, width), jnp.float32),
        jnp.zeros(ffn_shapes[0], jnp.float32),
        jnp.zeros(ffn_shapes[1], jnp.float32),
        jnp.zeros(ffn_shapes[2], jnp.float32),
        jnp.zeros((width,), jnp.float32),
    )
    start_backward = (jnp.zeros((shard_rows, width), jnp.bfloat16), start_totals, store_zeros)
    received, totals, grads_in = lax.fori_loop(
        0, batches + last_section, backward_step, start_backward
    )
    (
        qkv_total,
        qv_total,
        out_total,
        out_bias_total,
        gain_total,
        shift_total,
        up_total,
        up_bias_total,
        down_total,
        down_bias_total,
    ) = totals
    qkv_sum, qv_sum, out_sum, up_sum, up_bias_sum, down_sum = (
        lax.psum(qkv_total.astype(jnp.bfloat16), "dp").astype(jnp.float32),
        lax.psum(qv_total.astype(jnp.bfloat16), "dp").astype(jnp.float32),
        lax.psum(out_total.astype(jnp.bfloat16), "dp").astype(jnp.float32),
        lax.psum(up_total.astype(jnp.bfloat16), "dp").astype(jnp.float32),
        lax.psum(up_bias_total.astype(jnp.bfloat16), "dp").astype(jnp.float32),
        lax.psum(down_total.astype(jnp.bfloat16), "dp").astype(jnp.float32),
    )
    out_bias_sum, gain_sum, shift_sum, down_bias_sum = lax.psum(
        (out_bias_total, gain_total, shift_total, down_bias_total), ("tensor", "dp")
    )
    return (
        produced[None],
        grads_in[None],
        qkv_sum.reshape(1, width, 3, local_width),
        qv_sum[None],
        out_sum[None],
        out_bias_sum[None],
        gain_sum[None],
        shift_sum[None],
        up_sum[None],
        up_bias_sum[None],
        down_sum[None],
        down_bias_sum[None],
    )


def by_sequence(
    inputs,
    cotangent,
    lengths,
    w_qkv,
    b_qv,
    w_out,
    b_out,
    ln_gain,
    ln_bias,
    w_up,
    b_up,
    w_down,
    b_down,
):
    batches, shard_rows, width = inputs.shape
    place = lax.axis_index("tensor")
    section = lax.axis_index("section")
    groups = lax.axis_size("dp")
    rows = 2 * shard_rows
    seqs = batches // 2
    local = w_qkv.shape[3]
    units = w_up.shape[3]
    heads = local // HD
    chips = groups // 2

    qkv_own = jnp.transpose(w_qkv[0], (1, 0, 2))
    out_own = w_out[0]
    up_own = w_up[0]
    down_own = w_down[0]
    first = section == 0
    vecs = jnp.stack(
        [b_out[0], ln_gain[0, 0], ln_bias[0, 0], b_down[0], ln_gain[0, 1], ln_bias[0, 1], b_out[0], b_out[0]]
    ).astype(F32)
    slope_table = np.exp2(-8.0 * (np.arange(2 * heads, dtype=np.float32) + 1.0) / H).astype(np.float32)
    slopes = jnp.where(place == 0, slope_table, np.roll(slope_table, heads))
    own_lengths = lax.dynamic_slice_in_dim(lengths, place * seqs, seqs, 0)

    def meta(m, turn):
        active = section == turn
        return jnp.stack([jnp.int32(m), active.astype(jnp.int32), own_lengths[m], own_lengths[m] if turn == 1 else jnp.int32(rows)])

    metas = [[meta(m, turn) for m in range(seqs)] for turn in range(2)]
    qkv_oth, out_oth, up_oth, down_oth, bias, up_bias, *rest = fetch_and_forward(
        (qkv_own, out_own, up_own, down_own),
        (b_qv[0], b_up[0]),
        inputs,
        cotangent,
        slopes,
        vecs,
        metas[0][0],
        chips,
        seqs,
    )
    weights = (qkv_own, qkv_oth, out_own, out_oth, up_own, up_oth, down_own, down_oth)
    x_first = outer = rest[:seqs]
    *kept, y = rest[seqs:]
    deps = [y]

    def forward(x, m, turn):
        nonlocal kept, deps
        *kept, y = layer_forward(x, weights, bias, slopes, vecs, up_bias, metas[turn][m], kept, deps, seqs)
        deps = [y]
        return y

    y_first = [y] + [forward(x_first[m], m, 0) for m in range(1, seqs)]
    x_second = [lax.ppermute(y, "section", [(0, 1)]) for y in y_first]
    y_second = [forward(x_second[0], 0, 1)]
    produced = exchange_rows(y_first, deps)
    deps = [produced]
    y_second += [forward(x_second[m], m, 1) for m in range(1, seqs)]

    back = None
    sums = [[None] * seqs, [None] * seqs]

    def backward(grad, m, turn):
        nonlocal back, deps
        *back, gx, gx_low, norm_sums, up_sums, qv_sums = layer_backward(
            grad, kept, weights, slopes, vecs, metas[turn][m], back, deps, seqs
        )
        deps = [norm_sums]
        sums[turn][m] = (norm_sums, up_sums, qv_sums)
        return gx, gx_low

    gx_second = [backward(outer[m], m, 1) for m in range(seqs)]
    grad_middle = [lax.ppermute(gx_second[m][1], "section", [(1, 0)]) for m in range(seqs)]
    x_all = jnp.stack([jnp.where(first, x_first[m], x_second[m]) for m in range(seqs)])
    deps = deps + [x_all]
    gx_first = [backward(grad_middle[0], 0, 0)]

    norm_sums, up_sums, qv_sums = [
        jnp.where(first, sums[0][0][index], sum(item[index] for item in sums[1])) for index in range(3)
    ]

    def ordered(values, count):
        return jnp.where(
            place == 0, values, jnp.concatenate([values[:, count:], values[:, :count]], axis=1)
        ).reshape(-1, width)

    packed = jnp.concatenate([norm_sums[:6], ordered(up_sums[:2], units), ordered(qv_sums[:2], local)])
    *reduced, packed, got, _, _, _, _, _, gx, _ = backward_and_reduce(
        grad_middle[1], kept, back, x_all, weights, slopes, vecs, metas[0][1], packed, gx_first[0][1],
        [g[1] for g in gx_second] + y_second, chips,
    )
    gx_all = [gx_first[0][0], gx] + [g[0] for g in gx_second]
    (
        down_sum, up_sum, qkv_sum, out_sum, grads_in, produced,
        qv_sum, out_bias_sum, gain_sum, shift_sum, up_bias_sum, down_bias_sum,
    ) = widen(reduced, gx_all, got, produced, y_second, packed, units, local)
    return (
        produced[None],
        grads_in[None],
        jnp.transpose(qkv_sum, (1, 0, 2))[None],
        qv_sum[None],
        out_sum[None],
        out_bias_sum,
        gain_sum[None],
        shift_sum[None],
        up_sum[None],
        up_bias_sum[None],
        down_sum,
        down_bias_sum,
    )


def solution(mesh):
    sections, parts, groups = (mesh.shape[name] for name in ("section", "tensor", "dp"))

    def run(*args):
        paired = sections == 2 and parts == 2 and groups % 2 == 0 and args[0].shape[0] == 4
        return (by_sequence if paired else on_device)(*args)

    return jax.shard_map(
        run,
        mesh=mesh,
        in_specs=(
            P("dp", "tensor", None),
            P("dp", "tensor", None),
            P("dp"),
            P("section", None, None, "tensor"),
            P("section", None, "tensor"),
            P("section", "tensor", None),
            P("section", None),
            P("section", None, None),
            P("section", None, None),
            P("section", None, None, "tensor"),
            P("section", None, "tensor"),
            P("section", None, "tensor"),
            P("section", None),
        ),
        out_specs=(
            P("section", "dp", "tensor", None),
            P("section", "dp", "tensor", None),
            P("section", None, None, "tensor"),
            P("section", None, "tensor"),
            P("section", "tensor", None),
            P("section", None),
            P("section", None, None),
            P("section", None, None),
            P("section", None, None, "tensor"),
            P("section", None, "tensor"),
            P("section", None, "tensor"),
            P("section", None),
        ),
        check_vma=False,
    )
```

```python
import math

import jax
import jax.numpy as jnp
import numpy as np
from jax import lax
from jax.experimental import pallas as pl
from jax.experimental.pallas import tpu as pltpu
from jax.sharding import PartitionSpec as P

H = 16
HD = 64
EPS = 1e-05
BF = jnp.bfloat16
F32 = jnp.float32
VMEM_LIMIT = 62 * 1024 * 1024
ANY = pl.BlockSpec(memory_space=pl.ANY)
SMEM = pl.BlockSpec(memory_space=pltpu.SMEM)
WHOLE = pl.BlockSpec(memory_space=pltpu.VMEM)
NN = (((1,), (0,)), ((), ()))
NT = (((1,), (1,)), ((), ()))
TN = (((0,), (0,)), ((), ()))
CW = 256
PER = CW // HD


def dot(a, b, dims=NN):
    return lax.dot_general(a, b, dims, preferred_element_type=F32)


def arrived(ref, sem):
    pltpu.make_async_copy(ref, ref, sem).wait()


def call(kernel, inputs, outputs, scratch, meta, chain, deps, name, flops, nbytes, turn=None):
    pairs = [item if isinstance(item, tuple) else (item, ANY) for item in inputs]
    args = [meta] + [p[0] for p in pairs]
    specs = [SMEM] + [p[1] for p in pairs]
    n_in = len(args)
    aliases = {}
    if chain is not None:
        for buffer, index in zip(chain, [index for index, item in enumerate(outputs) if item[2]]):
            aliases[len(args)] = index
            args.append(buffer)
            specs.append(ANY)
    args += deps
    specs += [ANY] * len(deps)
    n_args, n_out = len(args), len(outputs)

    def body(*refs):
        @pl.when(refs[0][1] == 1 if turn is None else lax.axis_index("section") == turn)
        def _():
            kernel(refs[0], refs[1:n_in], refs[n_args : n_args + n_out], refs[n_args + n_out :])

    return pl.pallas_call(
        body,
        in_specs=specs,
        out_specs=[ANY] * n_out,
        out_shape=[jax.ShapeDtypeStruct(o[0], o[1]) for o in outputs],
        scratch_shapes=scratch,
        input_output_aliases=aliases,
        compiler_params=pltpu.CompilerParams(vmem_limit_bytes=VMEM_LIMIT)
        if turn is None
        else pltpu.CompilerParams(vmem_limit_bytes=VMEM_LIMIT, collective_id=3, has_side_effects=True),
        cost_estimate=pl.CostEstimate(flops=flops, bytes_accessed=nbytes, transcendentals=0),
        name=name,
    )(*args)


def pick(k, count, own, oth, make):
    @pl.when(k < count)
    def _():
        for src, dst, sem in make(own, k):
            pltpu.make_async_copy(src, dst, sem).start()

    @pl.when(k >= count)
    def _():
        for src, dst, sem in make(oth, k - count):
            pltpu.make_async_copy(src, dst, sem).start()


def block(index, size):
    return pl.ds(pl.multiple_of(index * size, size), size)


def copy(src, dst, sem):
    return pltpu.make_async_copy(src, dst, sem)


def fill_distance(dist_ref, length):
    rows = dist_ref.shape[0]
    keys = lax.broadcasted_iota(jnp.int32, (rows, rows), 0)
    places = lax.broadcasted_iota(jnp.int32, (rows, rows), 1)
    distance = jnp.abs(keys - places).astype(F32)
    dist_ref[...] = jnp.where(keys < length, distance, 1e12)


def normalize(v):
    mean = jnp.mean(v, axis=1, keepdims=True)
    centred = v - mean
    rstd = lax.rsqrt(jnp.mean(centred * centred, axis=1, keepdims=True) + EPS)
    return centred * rstd, rstd


def halves(rows):
    return [slice(0, rows // 2), slice(rows // 2, rows)]


class Forward:
    def __init__(self, rows, width, local, units):
        self.rows, self.width, self.local, self.units = rows, width, local, units
        self.ft = min(512, units)
        self.tiles = units // self.ft
        self.heads_steps = local // CW
        self.total = 2 * local

    def kept(self, slots):
        rows, width = self.rows, self.width
        shapes = [((slots, rows, self.total), BF)] * 4
        shapes += [((slots, 2 * self.heads_steps, 8, rows), F32)]
        shapes += [((slots, rows, 2 * self.units), BF)] * 3
        return shapes + [((slots, rows, width), BF)] * 3 + [((slots, rows, 128), F32)] * 2

    def scratch(self):
        rows, width, ft, total = self.rows, self.width, self.ft, self.total
        sem = pltpu.SemaphoreType.DMA
        return [
            pltpu.VMEM((rows, width), BF),
            pltpu.VMEM((2, 3, width, CW), BF),
            pltpu.VMEM((total, width), BF),
            pltpu.VMEM((2, 2, width, ft), BF),
            pltpu.VMEM((2, width, ft), BF),
            pltpu.VMEM((2, 3, rows, CW), BF),
            pltpu.VMEM((2, 8, rows), F32),
            pltpu.VMEM((rows, total), BF),
            pltpu.VMEM((rows, rows), F32),
            pltpu.VMEM((rows, width), F32),
            pltpu.VMEM((rows, width), F32),
            pltpu.VMEM((rows, width), BF),
            pltpu.VMEM((2, 3, rows, ft), BF),
            pltpu.VMEM((3, rows, width), BF),
            pltpu.VMEM((2, rows, 128), F32),
            sem, sem((2,)), sem((2,)), sem((2, 2)), sem((2, 4)), sem, sem((2, 3)), sem((6,)),
        ]

    def bind(self, x, weights, bias, slopes, vecs, up_bias, slot, outs, scratch):
        self.x_hbm, self.weights, self.bias, self.slopes, self.vecs, self.up_bias = x, weights, bias, slopes, vecs, up_bias
        self.slot, self.outs = slot, outs
        (self.x, self.w, self.o, self.up, self.down, self.qkv, self.lse, self.mixed, self.dist, self.normed, self.acc,
         self.low, self.tile, self.row, self.stat, self.x_sem, self.w_sem, self.o_sem, self.f_sem, self.q_sem, self.m_sem,
         self.t_sem, self.r_sem) = scratch

    def start_x(self):
        copy(self.x_hbm, self.x, self.x_sem).start()

    def start_w(self, k):
        s = lax.rem(k, 2)
        pick(k, self.heads_steps, self.weights[0], self.weights[1],
             lambda ref, j: [(ref.at[:, :, block(j, CW)], self.w.at[s], self.w_sem.at[s])])

    def start_o(self, side):
        copy(self.weights[2 + side], self.o.at[pl.ds(side * self.local, self.local)], self.o_sem.at[side]).start()

    def start_f(self, k):
        s = lax.rem(k, 2)
        ft = self.ft
        pick(k, self.tiles, (self.weights[4], self.weights[6]), (self.weights[5], self.weights[7]),
             lambda ref, j: [(ref[0].at[:, :, block(j, ft)], self.up.at[s], self.f_sem.at[s, 0]),
                             (ref[1].at[:, block(j, ft)], self.down.at[s], self.f_sem.at[s, 1])])

    def write_qkv(self, i, s):
        cols = block(i, CW)
        return [copy(self.qkv.at[s, c], out.at[self.slot, :, cols], self.q_sem.at[s, c])
                for c, out in enumerate(self.outs[:3])] + [
            copy(self.lse.at[s], self.outs[4].at[self.slot, i], self.q_sem.at[s, 3])]

    def attention_step(self, i, ahead):
        s = lax.rem(i, 2)
        qkv = self.qkv
        arrived(self.w.at[s], self.w_sem.at[s])

        @pl.when(i >= 2)
        def _():
            for item in self.write_qkv(i - 2, s):
                item.wait()

        values = self.x[...]
        b = self.bias[:, block(i, CW)].astype(F32)
        qkv[s, 0] = (dot(values, self.w[s, 0]) + b[0:1]).astype(BF)
        qkv[s, 1] = dot(values, self.w[s, 1]).astype(BF)
        qkv[s, 2] = (dot(values, self.w[s, 2]) + b[1:2]).astype(BF)

        @pl.when(i + 2 < ahead)
        def _():
            self.start_w(i + 2)

        parts = []
        for head in range(PER):
            cols = slice(head * HD, (head + 1) * HD)
            query = qkv[s, 0, :, cols] * BF(1.0 / math.sqrt(HD))
            scores = dot(qkv[s, 1, :, cols], query, NT)
            scores = scores - self.dist[...] * self.slopes[i * PER + head]
            top = jnp.max(scores, axis=0, keepdims=True)
            likely = jnp.exp(scores - top)
            mass = jnp.sum(likely, axis=0, keepdims=True)
            low = (likely * (1.0 / mass)).astype(BF)
            parts.append(dot(low, qkv[s, 2, :, cols], TN).astype(BF))
            self.lse[s, head : head + 1, :] = top + jnp.log(mass)
        self.mixed[:, block(i, CW)] = jnp.concatenate(parts, axis=1)
        for item in self.write_qkv(i, s):
            item.start()

    def middle(self):
        rows, width = self.rows, self.width
        copy(self.mixed, self.outs[3].at[self.slot], self.m_sem).start()
        for side in range(2):
            arrived(self.o.at[pl.ds(side * self.local, self.local)], self.o_sem.at[side])
        vec = self.vecs[...]
        for rs in halves(rows):
            attended = dot(self.mixed[rs, :], self.o[...])
            u, rstd = normalize(self.x[rs, :].astype(F32) + attended + vec[0:1])
            normed = u * vec[1:2] + vec[2:3]
            self.normed[rs, :] = normed
            self.low[rs, :] = normed.astype(BF)
            self.row[0, rs, :] = u.astype(BF)
            self.stat[0, rs, :] = jnp.broadcast_to(rstd, (rows // 2, 128))
            self.acc[rs, :] = jnp.zeros((rows // 2, width), F32)
        for index, item in enumerate(self.first_rows()):
            copy(*item, self.r_sem.at[index]).start()

    def first_rows(self):
        return [(self.low, self.outs[8].at[self.slot]), (self.row.at[0], self.outs[9].at[self.slot]),
                (self.stat.at[0], self.outs[11].at[self.slot])]

    def write_tiles(self, i, s):
        return [copy(self.tile.at[s, c], out.at[self.slot, :, block(i, self.ft)], self.t_sem.at[s, c])
                for c, out in enumerate(self.outs[5:8])]

    def ffn_step(self, i, ahead):
        s = lax.rem(i, 2)
        arrived(self.up.at[s], self.f_sem.at[s, 0])
        arrived(self.down.at[s], self.f_sem.at[s, 1])

        @pl.when(i >= 2)
        def _():
            for item in self.write_tiles(i - 2, s):
                item.wait()

        b = self.up_bias[:, block(i, self.ft)].astype(F32)
        low = self.low[...]
        gate = dot(low, self.up[s, 0]) + b[0:1]
        lift = dot(low, self.up[s, 1]) + b[1:2]
        cdf = 0.5 * lax.erf(gate * (1.0 / math.sqrt(2.0))) + 0.5
        act = gate * cdf
        slope = cdf + gate * (jnp.exp(gate * gate * -0.5) * (1.0 / math.sqrt(2.0 * math.pi)))
        self.tile[s, 0] = act.astype(BF)
        self.tile[s, 1] = (lift * slope).astype(BF)
        hidden = (act * lift).astype(BF)
        self.tile[s, 2] = hidden
        self.acc[...] += dot(hidden, self.down[s], NT)

        @pl.when(i + 2 < ahead)
        def _():
            self.start_f(i + 2)

        for item in self.write_tiles(i, s):
            item.start()

    def finish(self, y_out):
        rows = self.rows
        vec = self.vecs[...]
        for rs in halves(rows):
            u, rstd = normalize(self.normed[rs, :] + self.acc[rs, :] + vec[3:4])
            self.row[1, rs, :] = u.astype(BF)
            self.stat[1, rs, :] = jnp.broadcast_to(rstd, (rows // 2, 128))
            self.row[2, rs, :] = (u * vec[4:5] + vec[5:6]).astype(BF)
        ends = [(self.row.at[1], self.outs[10].at[self.slot]), (self.stat.at[1], self.outs[12].at[self.slot]),
                (self.row.at[2], y_out)]
        for index, item in enumerate(ends):
            copy(*item, self.r_sem.at[3 + index]).start()
        for index, item in enumerate(self.first_rows() + ends):
            copy(*item, self.r_sem.at[index]).wait()
        copy(self.mixed, self.outs[3].at[self.slot], self.m_sem).wait()
        for i in (2 * self.heads_steps - 2, 2 * self.heads_steps - 1):
            for item in self.write_qkv(jnp.int32(i), i % 2):
                item.wait()
        for i in (2 * self.tiles - 2, 2 * self.tiles - 1):
            for item in self.write_tiles(jnp.int32(i), i % 2):
                item.wait()

    def flops(self):
        rows, width, total = self.rows, self.width, self.total
        return 2 * rows * width * (4 * total + 6 * self.units) + 4 * rows * rows * total


def layer_forward(x, weights, bias, slopes, vecs, up_bias, meta, chain, deps, slots):
    rows, width = x.shape
    step = Forward(rows, width, weights[0].shape[2], weights[4].shape[2])

    def kernel(meta_ref, ins, outs, scratch):
        step.bind(ins[0], ins[1:9], *ins[9:13], meta_ref[0], outs[:13], scratch)
        step.start_x()
        for k in range(2):
            step.start_w(jnp.int32(k))
        for side in range(2):
            step.start_o(side)
        for k in range(2):
            step.start_f(jnp.int32(k))
        fill_distance(step.dist, meta_ref[2])
        arrived(step.x, step.x_sem)

        @pl.loop(0, 2 * step.heads_steps)
        def _(i):
            step.attention_step(i, 2 * step.heads_steps)

        step.middle()

        @pl.loop(0, 2 * step.tiles)
        def _(i):
            step.ffn_step(i, 2 * step.tiles)

        step.finish(outs[13])

    return call(
        kernel,
        [x, *weights, (bias, WHOLE), (slopes, SMEM), (vecs, WHOLE), (up_bias, WHOLE)],
        [shape + (True,) for shape in step.kept(slots)] + [((rows, width), BF, False)],
        step.scratch(),
        meta,
        chain,
        deps,
        "layer_forward",
        step.flops(),
        54 << 20,
    )


def layer_backward(grad, kept, weights, slopes, vecs, meta, chain, deps, slots, slot=None, turn=None, sent=()):
    qkv_own, qkv_oth, o_own, o_oth, up_own, up_oth, down_own, down_oth = weights
    q, k, v, _, lse, act, slope, _, _, u1, u2, r1, r2 = kept
    rows, width = grad.shape
    local = qkv_own.shape[2]
    units = up_own.shape[2]
    heads_steps = local // CW
    ft = min(512, units)
    tiles = units // ft
    total = 2 * local
    static_slot = slot

    def norm_back(grad_z, u, rstd, gain):
        t = grad_z * gain
        return rstd * (t - jnp.mean(t, axis=1, keepdims=True) - u * jnp.mean(t * u, axis=1, keepdims=True))

    def row_sum(values):
        return jnp.sum(values, axis=0, keepdims=True)

    def kernel(meta_ref, ins, outs, scratch):
        (g_hbm, q_hbm, k_hbm, v_hbm, lse_hbm, a_hbm, b_hbm, u1_hbm, u2_hbm, r1_hbm, r2_hbm,
         qkv_own_ref, qkv_oth_ref, o_own_ref, o_oth_ref, up_own_ref, up_oth_ref, down_own_ref, down_oth_ref,
         slope_ref, vec_ref) = ins[:21]
        gg0_out, gg1_out, gl_out, ga_out, gq_out, gk_out, gv_out, gx_out, gxl_out, sums_out, ub_out, qv_out = outs[:12]
        (g_ref, u_ref, r_ref, up_ref, down_ref, ab_ref, gg_ref, low_ref, acc_ref, sums_ref, ub_ref, qv_ref,
         w_ref, o_ref, qkv_ref, lse_ref, gm_ref, dist_ref, gqkv_ref,
         g_sem, f_sem, t_sem, w_sem, q_sem, r_sem, x_send, x_recv) = scratch
        slot = meta_ref[0] if static_slot is None else static_slot
        travelling = []
        if sent:
            t = lax.axis_index("tensor")
            cross = {"tensor": 1 - t}
            barrier = pltpu.get_barrier_semaphore()
            pl.semaphore_signal(barrier, inc=1, device_id=cross, device_id_type=pl.DeviceIdType.MESH)
            pl.semaphore_wait(barrier, 1)
            for index in range(len(sent)):
                travelling.append(
                    pltpu.make_async_remote_copy(
                        src_ref=ins[21 + index].at[block(1 - t, rows // 2)], dst_ref=outs[12].at[index],
                        send_sem=x_send.at[index], recv_sem=x_recv.at[index],
                        device_id=cross, device_id_type=pl.DeviceIdType.MESH,
                    )
                )
                travelling[-1].start()

        def start_f(i):
            s = lax.rem(i, 2)
            pick(i, tiles, (up_own_ref, down_own_ref), (up_oth_ref, down_oth_ref),
                 lambda ref, j: [(ref[0].at[:, :, block(j, ft)], up_ref.at[s], f_sem.at[s, 0]),
                                 (ref[1].at[:, block(j, ft)], down_ref.at[s], f_sem.at[s, 1])])
            for c, ref in enumerate((a_hbm, b_hbm)):
                copy(ref.at[slot, :, block(i, ft)], ab_ref.at[s, c], f_sem.at[s, 2 + c]).start()

        def start_w(i):
            s = lax.rem(i, 2)
            pick(i, heads_steps, (qkv_own_ref, o_own_ref), (qkv_oth_ref, o_oth_ref),
                 lambda ref, j: [(ref[0].at[:, :, block(j, CW)], w_ref.at[s], w_sem.at[s, 0]),
                                 (ref[1].at[block(j, CW)], o_ref.at[s], w_sem.at[s, 1])])
            for c, ref in enumerate((q_hbm, k_hbm, v_hbm)):
                copy(ref.at[slot, :, block(i, CW)], qkv_ref.at[s, c], w_sem.at[s, 2 + c]).start()
            copy(lse_hbm.at[slot, i], lse_ref.at[s], w_sem.at[s, 5]).start()

        firsts = [(g_hbm, g_ref), (u2_hbm.at[slot], u_ref.at[1]), (r2_hbm.at[slot], r_ref.at[1]),
                  (u1_hbm.at[slot], u_ref.at[0]), (r1_hbm.at[slot], r_ref.at[0])]
        for index, (src, dst) in enumerate(firsts):
            copy(src, dst, g_sem.at[index]).start()
            if index == 2:
                start_f(jnp.int32(0))
                start_f(jnp.int32(1))
        start_w(jnp.int32(0))
        start_w(jnp.int32(1))
        vec = vec_ref[...]
        fill_distance(dist_ref, meta_ref[2])
        for index, (src, dst) in enumerate(firsts[:3]):
            copy(src, dst, g_sem.at[index]).wait()
        sums = [jnp.zeros((1, width), F32)] * 3
        for rs in halves(rows):
            places = lax.broadcasted_iota(jnp.int32, (rows // 2, width), 0) + rs.start
            grad_y = jnp.where(places < meta_ref[3], g_ref[rs, :].astype(F32), 0.0)
            u = u_ref[1, rs, :].astype(F32)
            grad_c = norm_back(grad_y, u, r_ref[1, rs, 0:1], vec[4:5])
            acc_ref[rs, :] = grad_c
            low_ref[0, rs, :] = grad_c.astype(BF)
            for index, values in enumerate((grad_y * u, grad_y, grad_c)):
                sums[index] += row_sum(values)
        for index in range(3):
            sums_ref[index : index + 1, :] = sums[index]
        copy(low_ref.at[0], gl_out.at[slot], r_sem.at[0]).start()

        def write_tiles(i, s):
            return [copy(gg_ref.at[s, c], out.at[slot, :, block(i, ft)], t_sem.at[s, c])
                    for c, out in enumerate((gg0_out, gg1_out))]

        @pl.loop(0, 2 * tiles)
        def _(i):
            s = lax.rem(i, 2)
            arrived(up_ref.at[s], f_sem.at[s, 0])
            arrived(down_ref.at[s], f_sem.at[s, 1])
            for c in range(2):
                arrived(ab_ref.at[s, c], f_sem.at[s, 2 + c])

            @pl.when(i >= 2)
            def _():
                for item in write_tiles(i - 2, s):
                    item.wait()

            gh = dot(low_ref[0], down_ref[s])
            g0 = (gh * ab_ref[s, 1].astype(F32)).astype(BF)
            g1 = (gh * ab_ref[s, 0].astype(F32)).astype(BF)
            gg_ref[s, 0] = g0
            gg_ref[s, 1] = g1
            ub_ref[0:1, block(i, ft)] = row_sum(g0.astype(F32))
            ub_ref[1:2, block(i, ft)] = row_sum(g1.astype(F32))
            acc_ref[...] += dot(g0, up_ref[s, 0], NT) + dot(g1, up_ref[s, 1], NT)

            @pl.when(i + 2 < 2 * tiles)
            def _():
                start_f(i + 2)

            for item in write_tiles(i, s):
                item.start()

        for index, (src, dst) in enumerate(firsts[3:]):
            copy(src, dst, g_sem.at[3 + index]).wait()
        sums = [jnp.zeros((1, width), F32)] * 3
        for rs in halves(rows):
            grad_n = acc_ref[rs, :]
            u = u_ref[0, rs, :].astype(F32)
            grad_a = norm_back(grad_n, u, r_ref[0, rs, 0:1], vec[1:2])
            low_ref[1, rs, :] = grad_a.astype(BF)
            acc_ref[rs, :] = grad_a
            for index, values in enumerate((grad_n * u, grad_n, grad_a)):
                sums[index] += row_sum(values)
        for index in range(3):
            sums_ref[3 + index : 4 + index, :] = sums[index]
        sums_ref[6:8, :] = jnp.zeros((2, width), F32)
        copy(low_ref.at[1], ga_out.at[slot], r_sem.at[1]).start()
        scale = BF(1.0 / math.sqrt(HD))

        def write_heads(i, s):
            return [copy(gqkv_ref.at[s, c], out.at[slot, :, block(i, CW)], q_sem.at[s, c])
                    for c, out in enumerate((gq_out, gk_out, gv_out))]

        @pl.loop(0, 2 * heads_steps)
        def _(i):
            s = lax.rem(i, 2)
            for index, ref in enumerate((w_ref.at[s], o_ref.at[s], qkv_ref.at[s, 0], qkv_ref.at[s, 1], qkv_ref.at[s, 2], lse_ref.at[s])):
                arrived(ref, w_sem.at[s, index])

            @pl.when(i >= 2)
            def _():
                for item in write_heads(i - 2, s):
                    item.wait()

            gm_ref[...] = dot(low_ref[1], o_ref[s], NT).astype(BF)
            parts = [[], [], []]
            for head in range(PER):
                cols = slice(head * HD, (head + 1) * HD)
                query = qkv_ref[s, 0, :, cols] * scale
                key = qkv_ref[s, 1, :, cols]
                gm = gm_ref[:, cols]
                scores = dot(key, query, NT)
                scores = scores - dist_ref[...] * slope_ref[i * PER + head]
                likely = jnp.exp(scores - lse_ref[s, head : head + 1, :])
                parts[2].append(dot(likely.astype(BF), gm).astype(BF))
                t = likely * dot(qkv_ref[s, 2, :, cols], gm, NT)
                inner = jnp.sum(t, axis=0, keepdims=True)
                gs = (t - likely * inner).astype(BF)
                parts[1].append(dot(gs, query).astype(BF))
                parts[0].append(dot(gs, key * scale, TN).astype(BF))
            for c in range(3):
                gqkv_ref[s, c] = jnp.concatenate(parts[c], axis=1)
            for index, c in enumerate((0, 2)):
                qv_ref[index : index + 1, block(i, CW)] = row_sum(gqkv_ref[s, c].astype(F32))
            acc_ref[...] += (
                dot(gqkv_ref[s, 0], w_ref[s, 0], NT)
                + dot(gqkv_ref[s, 1], w_ref[s, 1], NT)
                + dot(gqkv_ref[s, 2], w_ref[s, 2], NT)
            )

            @pl.when(i + 2 < 2 * heads_steps)
            def _():
                start_w(i + 2)

            for item in write_heads(i, s):
                item.start()

        g_ref[...] = acc_ref[...].astype(BF)
        ends = [(g_ref, gxl_out), (acc_ref, gx_out), (sums_ref, sums_out), (ub_ref, ub_out), (qv_ref, qv_out)]
        for index, (src, dst) in enumerate(ends):
            copy(src, dst, r_sem.at[2 + index]).start()
        for index, (src, dst) in enumerate([(low_ref.at[0], gl_out.at[slot]), (low_ref.at[1], ga_out.at[slot])] + ends):
            copy(src, dst, r_sem.at[index]).wait()
        for i in (2 * tiles - 2, 2 * tiles - 1):
            for item in write_tiles(jnp.int32(i), i % 2):
                item.wait()
        for i in (2 * heads_steps - 2, 2 * heads_steps - 1):
            for item in write_heads(jnp.int32(i), i % 2):
                item.wait()
        for item in travelling:
            item.wait()

    sem = pltpu.SemaphoreType.DMA
    return call(
        kernel,
        [grad, q, k, v, lse, act, slope, u1, u2, r1, r2, *weights, (slopes, SMEM), (vecs, WHOLE), *sent],
        [((slots, rows, 2 * units), BF, True)] * 2
        + [((slots, rows, width), BF, True)] * 2
        + [((slots, rows, total), BF, True)] * 3
        + [
            ((rows, width), F32, False),
            ((rows, width), BF, False),
            ((8, width), F32, False),
            ((2, 2 * units), F32, False),
            ((2, total), F32, False),
        ]
        + ([((len(sent), rows // 2, width), BF, False)] if sent else []),
        [
            pltpu.VMEM((rows, width), BF),
            pltpu.VMEM((2, rows, width), BF),
            pltpu.VMEM((2, rows, 128), F32),
            pltpu.VMEM((2, 2, width, ft), BF),
            pltpu.VMEM((2, width, ft), BF),
            pltpu.VMEM((2, 2, rows, ft), BF),
            pltpu.VMEM((2, 2, rows, ft), BF),
            pltpu.VMEM((2, rows, width), BF),
            pltpu.VMEM((rows, width), F32),
            pltpu.VMEM((8, width), F32),
            pltpu.VMEM((2, 2 * units), F32),
            pltpu.VMEM((2, total), F32),
            pltpu.VMEM((2, 3, width, CW), BF),
            pltpu.VMEM((2, CW, width), BF),
            pltpu.VMEM((2, 3, rows, CW), BF),
            pltpu.VMEM((2, 8, rows), F32),
            pltpu.VMEM((rows, CW), BF),
            pltpu.VMEM((rows, rows), F32),
            pltpu.VMEM((2, 3, rows, CW), BF),
            sem((5,)), sem((2, 4)), sem((2, 2)), sem((2, 6)), sem((2, 3)), sem((7,)), sem((4,)), sem((4,)),
        ],
        meta,
        chain,
        deps,
        "layer_backward",
        2 * rows * width * (4 * total + 6 * units) + 10 * rows * rows * total,
        70 << 20,
        turn,
    )


MESH = pl.DeviceIdType.MESH
CORE_LAG = 3
CROSS_LAG = 3
CHAIN_LAG = 2


def neighbours():
    t = lax.axis_index("tensor")
    d = lax.axis_index("dp")
    last = lax.axis_size("dp") // 2 - 1
    c = lax.rem(d, 2)
    z = d // 2
    return t, c, z, last, {"dp": d + 1 - 2 * c}, {"tensor": 1 - t}, {"dp": d + 2}, {"dp": d - 2}


def greet(c, z, chips, core, cross):
    barrier = pltpu.get_barrier_semaphore()
    pl.semaphore_signal(barrier, inc=1, device_id=core, device_id_type=MESH)
    pl.semaphore_signal(barrier, inc=1, device_id=cross, device_id_type=MESH)
    for shift in range(1, chips):
        chip = lax.rem(z + shift, chips)
        pl.semaphore_signal(barrier, inc=1, device_id={"dp": chip * 2 + c}, device_id_type=MESH)
    pl.semaphore_wait(barrier, 1 + chips)


def fetch_and_forward(weights, biases, inputs, cotangent, slopes, vecs, meta, chips, slots):
    seqs = inputs.shape[0] // 2
    shard_rows, width = inputs.shape[1:]
    rows = 2 * shard_rows
    groups = 2 * chips
    qkv, out, up, down = weights
    local, units = qkv.shape[2], up.shape[2]
    step = Forward(rows, width, local, units)
    ft, tiles = step.ft, step.tiles
    bias_widths = [b.shape[1] for b in biases]
    QKV, OUT, UP, DOWN, ROWS, BIAS = range(6)

    plan = [(UP, 0, groups), (ROWS, 0, 0), (BIAS, 0, 0), (BIAS, 1, 0)]
    plan += [(UP, part, groups) for part in range(1, tiles)]
    plan += [(DOWN, part, groups) for part in range(tiles - 1)]
    plan += [(QKV, part, 2) for part in range(3)] + [(OUT, 0, 2), (DOWN, tiles - 1, 2)]
    plan += [(ROWS, part, 0) for part in range(1, seqs)]
    n = len(plan)
    number = {item[:2]: index for index, item in enumerate(plan)}

    def size(index):
        kind, part, pieces = plan[index]
        whole = {QKV: width * local, OUT: local * width, UP: 2 * width * ft, DOWN: width * ft, ROWS: shard_rows * width, BIAS: 64}
        return whole[kind] / max(1, pieces)

    events, clock, busy = [], 0.0, 0.0
    for index, (kind, part, pieces) in enumerate(plan):
        clock += size(index)
        events.append((clock, index, 0))
        if pieces == groups:
            start = max(clock, busy)
            busy = start + size(index) * (chips - 1)
            events += [(start + size(index) * hop * 1.001, index, hop) for hop in range(1, chips)]
    events.sort()
    when = {event[1:]: event[0] for event in events}

    def ready(*keys):
        return max(when[key] for k in keys for key in when if key[0] == number[k])

    needs = [[(ROWS, 0), (BIAS, 0)], []] + [[(QKV, part) for part in range(3)], []] + [[(OUT, 0), (BIAS, 1)]]
    needs += [[] for _ in range(tiles - 1)]
    fetches = {5 + tiles - 1 + part: tiles + part for part in range(tiles)}
    needs += [[(UP, part), (DOWN, part)] for part in range(tiles)] + [[]]
    assert step.heads_steps == 2
    rounds, taken = [], 0
    for need in needs:
        mine = []
        if need:
            limit = ready(*need)
            while taken < len(events) and events[taken][0] <= limit:
                mine.append(events[taken][1:])
                taken += 1
        rounds.append((mine, need))
    rest = [event[1:] for event in events[taken:]]
    n_rounds = len(rounds)
    n_kept = len(step.kept(slots))

    def kernel(*refs):
        meta_ref, slope_ref, vec_ref = refs[:3]
        ins, bias_ins, held_refs = refs[3:7], refs[7:9], refs[9:11]
        outs, bias_outs, row_refs = refs[11:15], refs[15:17], refs[17 : 17 + seqs]
        kept_refs = refs[17 + seqs : 17 + seqs + n_kept]
        y_ref = refs[17 + seqs + n_kept]
        stage, qv_bias, ub_bias, x_send, x_recv, c_send, c_recv, u_send, u_recv, d_send, d_recv, l_sem, b_sem = refs[
            18 + seqs + n_kept : 31 + seqs + n_kept
        ]
        t, c, z, last, core, cross, above, below = neighbours()
        section = lax.axis_index("section")
        greet(c, z, chips, core, cross)
        paired = [item for pair in zip(ins, outs) for item in pair]
        step.bind(
            row_refs[0], paired, qv_bias, slope_ref, vec_ref, ub_bias, 0, kept_refs, refs[31 + seqs + n_kept :]
        )

        def span(part):
            return block(part, shard_rows)

        def bias_part(m, side):
            return bias_outs[m].at[:, pl.ds(side * bias_widths[m], bias_widths[m])]

        def piece(side, index, chip, on):
            kind, part, pieces = plan[index]
            place = chip * 2 + on if pieces == groups else on
            ref = (ins, outs)[side][kind]
            if kind == QKV:
                return ref.at[part, block(place, width // pieces)]
            if kind == OUT:
                return ref.at[block(place, local // pieces)]
            cols = pl.ds(part * ft, ft)
            if kind == DOWN:
                return ref.at[block(place, width // pieces), cols]
            per = pieces // 2
            return ref.at[place // per, block(lax.rem(place, per), width // per), cols]

        def cross_copy(index, held_ref=None):
            kind, m, pieces = plan[index]
            if kind == ROWS:
                src = (held_refs[0] if held_ref is None else held_ref).at[(1 - t) * seqs + m]
                dst = row_refs[m].at[span(t)]
            elif kind == BIAS:
                src, dst = bias_ins[m], bias_part(m, 1)
            else:
                src, dst = piece(0, index, z, c), piece(1, index, z, c)
            return pltpu.make_async_remote_copy(
                src_ref=src, dst_ref=dst, send_sem=x_send.at[index], recv_sem=x_recv.at[index],
                device_id=cross, device_id_type=MESH,
            )

        def pass_on(index, chip, send, recv, device):
            place = piece(1, index, chip, c)
            return pltpu.make_async_remote_copy(
                src_ref=place, dst_ref=place, send_sem=send.at[index, chip], recv_sem=recv.at[index, chip],
                device_id=device, device_id_type=MESH,
            )

        def got(index, chip, on, sem):
            arrived(piece(1, index, chip, on), sem)

        for m in range(2):
            copy(bias_ins[m], bias_part(m, 0), b_sem.at[m]).start()
        for index in range(n):
            if plan[index][0] == ROWS:
                for turn in range(2):
                    @pl.when(section == turn)
                    def _(index=index, turn=turn):
                        cross_copy(index, held_refs[turn]).start()
            else:
                cross_copy(index).start()
        for turn in range(2):
            @pl.when(section == turn)
            def _(turn=turn):
                copy(held_refs[turn].at[pl.ds(t * seqs, seqs)], stage, l_sem.at[0]).start()

        @pl.when(section == 0)
        def _():
            for k in range(2):
                step.start_w(jnp.int32(k))
            step.start_o(0)
            for k in range(2):
                step.start_f(jnp.int32(k))
            fill_distance(step.dist, meta_ref[2])

        arrived(stage, l_sem.at[0])
        for m in range(seqs):
            copy(stage.at[m], row_refs[m].at[span(t)], l_sem.at[m]).start()
        for m in range(seqs):
            arrived(stage.at[m], l_sem.at[m])
        for m in range(2):
            copy(bias_ins[m], bias_part(m, 0), b_sem.at[m]).wait()

        def handle(index, hop):
            kind, m, pieces = plan[index]
            if kind == ROWS:
                arrived(row_refs[m].at[span(1 - t)], x_recv.at[index])
            elif kind == BIAS:
                arrived(bias_part(m, 1), x_recv.at[index])
            elif hop == 0:
                got(index, z, c, x_recv.at[index])
                if pieces == groups:
                    @pl.when(z < last)
                    def _():
                        pass_on(index, z, u_send, u_recv, above).start()

                    @pl.when(z > 0)
                    def _():
                        pass_on(index, z, d_send, d_recv, below).start()

                pass_on(index, z, c_send, c_recv, core).start()
            else:
                @pl.when(z - hop >= 0)
                def _():
                    got(index, z - hop, c, u_recv.at[index, z - hop])

                    @pl.when(z < last)
                    def _():
                        pass_on(index, z - hop, u_send, u_recv, above).start()

                    pass_on(index, z - hop, c_send, c_recv, core).start()

                @pl.when(z + hop <= last)
                def _():
                    got(index, z + hop, c, d_recv.at[index, z + hop])

                    @pl.when(z > 0)
                    def _():
                        pass_on(index, z + hop, d_send, d_recv, below).start()

                    pass_on(index, z + hop, c_send, c_recv, core).start()

        def from_core(key):
            index = number[key]
            kind, m, pieces = plan[index]
            if pieces == groups:
                for chip in range(chips):
                    got(index, chip, 1 - c, c_recv.at[index, chip])
            elif pieces:
                got(index, z, 1 - c, c_recv.at[index, z])

        @pl.loop(0, n_rounds)
        def _(tau):
            for number_, (mine, need) in enumerate(rounds):
                if not (mine or need):
                    continue

                @pl.when(tau == number_)
                def _(number_=number_, mine=mine, need=need):
                    for index, hop in mine:
                        handle(index, hop)
                    for key in need:
                        from_core(key)
                    for key in need:
                        if key == (BIAS, 0):
                            @pl.when(section == 0)
                            def _():
                                step.start_x()
                                copy(bias_outs[0], qv_bias, b_sem.at[0]).start()
                                copy(bias_outs[0], qv_bias, b_sem.at[0]).wait()
                                arrived(step.x, step.x_sem)
                        elif key == (QKV, 2):
                            @pl.when(section == 0)
                            def _():
                                for k in range(2, 4):
                                    step.start_w(jnp.int32(k))
                        elif key == (OUT, 0):
                            @pl.when(section == 0)
                            def _():
                                step.start_o(1)
                        elif key == (BIAS, 1):
                            @pl.when(section == 0)
                            def _():
                                copy(bias_outs[1], ub_bias, b_sem.at[1]).start()
                                copy(bias_outs[1], ub_bias, b_sem.at[1]).wait()
                        elif key[0] == DOWN:
                            @pl.when(section == 0)
                            def _(key=key):
                                step.start_f(jnp.int32(tiles + key[1]))

            @pl.when(section == 0)
            def _():
                @pl.when(tau < 4)
                def _():
                    step.attention_step(tau, 2)

                @pl.when(tau == 4)
                def _():
                    step.middle()

                @pl.when(tau > 4)
                def _():
                    step.ffn_step(tau - 5, tiles)

        @pl.when(section == 0)
        def _():
            step.finish(y_ref)

        for index, hop in rest:
            handle(index, hop)
        for index in range(n):
            kind, part, pieces = plan[index]
            cross_copy(index).wait_send()
            if pieces == 2:
                pass_on(index, z, c_send, c_recv, core).wait_send()
            if pieces != groups:
                continue
            for chip in range(chips):
                pass_on(index, chip, c_send, c_recv, core).wait_send()

                @pl.when((chip <= z) & (z < last))
                def _(chip=chip):
                    pass_on(index, chip, u_send, u_recv, above).wait_send()

                @pl.when((chip >= z) & (z > 0))
                def _(chip=chip):
                    pass_on(index, chip, d_send, d_recv, below).wait_send()

    sem = pltpu.SemaphoreType.DMA
    return pl.pallas_call(
        kernel,
        in_specs=[SMEM, SMEM, WHOLE] + [ANY] * 8,
        out_specs=[ANY] * (7 + seqs + n_kept),
        out_shape=[jax.ShapeDtypeStruct(w.shape, BF) for w in weights]
        + [jax.ShapeDtypeStruct((2, 2 * size_), BF) for size_ in bias_widths]
        + [jax.ShapeDtypeStruct((rows, width), BF)] * seqs
        + [jax.ShapeDtypeStruct(*shape) for shape in step.kept(slots)]
        + [jax.ShapeDtypeStruct((rows, width), BF)],
        scratch_shapes=[pltpu.VMEM((seqs, shard_rows, width), BF)]
        + [pltpu.VMEM((2, 2 * size_), BF) for size_ in bias_widths]
        + [sem((n,)), sem((n,))]
        + [sem((n, chips))] * 6
        + [sem((seqs,)), sem((2,))]
        + step.scratch(),
        compiler_params=pltpu.CompilerParams(collective_id=1, has_side_effects=True, vmem_limit_bytes=VMEM_LIMIT),
        cost_estimate=pl.CostEstimate(flops=step.flops(), bytes_accessed=90 << 20, transcendentals=0),
        name="fetch_and_forward",
    )(meta, slopes, vecs, *weights, *biases, inputs, cotangent)


def norm_back(grad_z, u, rstd, gain):
    t = grad_z * gain
    return rstd * (t - jnp.mean(t, axis=1, keepdims=True) - u * jnp.mean(t * u, axis=1, keepdims=True))


def row_sum(values):
    return jnp.sum(values, axis=0, keepdims=True)


def backward_and_reduce(grad, kept, back, x_all, weights, slopes, vecs, meta, sums, low_grad, second, chips):
    q, k_, v, mixed_all, lse, act, slope, hidden_all, normed_all, u1, u2, r1, r2 = kept
    gg0, gg1, gl, ga, gq, gk, gv = back
    rows, width = grad.shape
    local, units = weights[0].shape[2], weights[4].shape[2]
    ft = CW
    tiles = units // ft
    heads_steps = local // CW
    seqs = 2
    bt = 128
    lefts = [gl, normed_all, x_all, ga]
    rights = [hidden_all, gg0, gg1, gq, gk, gv, mixed_all]
    group_of = [0, 1, 1, 2, 2, 2, 3]
    member_of = [0, 0, 1, 0, 1, 2, 0]
    half = width // 2
    quarter = half // 2
    per_pair = 2 * ft // bt
    pairs = tiles // 2
    ffn_blocks = 3 * per_pair * pairs
    head_blocks = local // bt
    total = ffn_blocks + 4 * head_blocks
    ring, mines, gives = 4, CORE_LAG + 1, 4
    ahead_of = 4
    drain = CORE_LAG + CROSS_LAG + 2 * (chips - 1) * CHAIN_LAG + 1
    vec_shape = sums.shape
    shard_rows = rows // 2
    norm_at = 2 * tiles
    head_at = norm_at + 1
    end_at = head_at + 5 * 2 * heads_steps
    x_flip, ga_flip = ffn_blocks - per_pair, ffn_blocks + per_pair
    up_rows = units // width
    assert ahead_of + ffn_blocks - ring > end_at

    def kernel(*refs):
        meta_ref, slope_ref, vec_ref = refs[:3]
        g_hbm, q_hbm, k_hbm, v_hbm, lse_hbm, a_hbm, b_hbm, u1_hbm, u2_hbm, r1_hbm, r2_hbm = refs[3:14]
        (qkv_own_ref, qkv_oth_ref, o_own_ref, o_oth_ref, up_own_ref, up_oth_ref, down_own_ref, down_oth_ref) = refs[14:22]
        left_refs, right_refs = refs[22:26], refs[26:33]
        sums_ref, low_grad_ref, second_ref = refs[33:36]
        outs, sums_out, rows_out = refs[36:40], refs[40], refs[41]
        fresh = refs[42:47]
        gx_out, gxl_out = refs[47:49]
        (
            acc, from_x, from_z, flip, stage, tile, mine, give, vec, vec_in, vec_all,
            g_ref, u_ref, r_ref, low_ref, gacc_ref, w_ref, o_ref, qkv_ref, gqkv_ref, lse_ref, gm_ref, gs_ref, dist_ref,
            part_sums, ub_sums, qv_sums,
            tile_sem, stage_sem, give_send, core_recv, x_send, x_recv, z_send, z_recv, f_send, f_recv,
            store_sem, out_send, out_recv, v_load, v_send, v_recv, r_send, r_recv,
            g_sem, w_sem, t_sem, e_sem,
        ) = refs[49:]
        final = from_x
        t, c, z, last, core, cross, above, below = neighbours()
        section = lax.axis_index("section")
        first = section == 0
        greet(c, z, chips, core, cross)
        fresh_of = {1: fresh[0].at[0], 2: fresh[1].at[0], 3: fresh[2], 4: fresh[3], 5: fresh[4]}
        vec_w = vec_ref[...]

        def remote(src, dst, send, recv, device):
            return pltpu.make_async_remote_copy(
                src_ref=src, dst_ref=dst, send_sem=send, recv_sem=recv, device_id=device, device_id_type=MESH
            )

        def valid(k):
            return (k >= 0) & (k < total)

        def member(k, visit):
            for m in range(3):
                @pl.when((k < ffn_blocks) & (lax.rem(k, 3 * per_pair) // per_pair == m))
                def _(m=m):
                    visit(m, k // (3 * per_pair) * per_pair + lax.rem(k, per_pair))

            for m in range(3, 7):
                base = ffn_blocks + (m - 3) * head_blocks

                @pl.when((k >= base) & (k < base + head_blocks))
                def _(m=m, base=base):
                    visit(m, k - base)

        def load_tile(k):
            at = lax.rem(k, ring)

            def visit(m, j):
                count = right_refs[m].shape[2] // (2 * bt)
                for side in range(2):
                    cols = block(side * count + j, bt)
                    where = pl.ds(side * bt, bt)
                    copy(right_refs[m].at[0, :, cols], tile.at[at, 0, :, where], tile_sem.at[at]).start()
                    if m not in fresh_of:
                        copy(right_refs[m].at[1, :, cols], tile.at[at, 1, :, where], tile_sem.at[at]).start()
                        continue

                    @pl.when(first)
                    def _(cols=cols, where=where):
                        copy(fresh_of[m].at[:, cols], tile.at[at, 1, :, where], tile_sem.at[at]).start()

                    @pl.when(section == 1)
                    def _(cols=cols, where=where):
                        copy(right_refs[m].at[1, :, cols], tile.at[at, 1, :, where], tile_sem.at[at]).start()

            member(k, visit)

        def take_left(g, at, mine_low):
            copy(left_refs[g].at[0], stage.at[0], stage_sem.at[0]).start()
            if mine_low is None:
                copy(left_refs[g].at[1], stage.at[1], stage_sem.at[1]).start()
                arrived(stage.at[1], stage_sem.at[1])
            else:
                @pl.when(first)
                def _():
                    stage[1] = low_ref[mine_low]

                @pl.when(section == 1)
                def _():
                    copy(left_refs[g].at[1], stage.at[1], stage_sem.at[1]).start()
                    arrived(stage.at[1], stage_sem.at[1])

            arrived(stage.at[0], stage_sem.at[0])
            for m in range(seqs):
                flip[at, :, m * rows : (m + 1) * rows] = stage[m].T

        def place_of(u):
            within = lax.rem(u, 4)
            side = within // 2
            return side, u // 4 * 2 + lax.rem(within, 2)

        def start_f(u):
            at = lax.rem(u, 2)
            side, j = place_of(u)
            pick(side * tiles + j, tiles, (up_own_ref, down_own_ref), (up_oth_ref, down_oth_ref),
                 lambda ref, jj: [(ref[0].at[:, :, block(jj, ft)], w_ref.at[at, pl.ds(0, 2)], w_sem.at[at, 0]),
                                  (ref[1].at[:, block(jj, ft)], w_ref.at[at, 2], w_sem.at[at, 1])])
            for n, ref in enumerate((a_hbm, b_hbm)):
                copy(ref.at[1, :, block(side * tiles + j, ft)], qkv_ref.at[at, n], w_sem.at[at, 2 + n]).start()

        def write_tile(u):
            at = lax.rem(u, 2)
            side, j = place_of(u)
            return [copy(gqkv_ref.at[at, n], fresh[n].at[0, :, block(side * tiles + j, ft)], t_sem.at[at, n]) for n in range(2)]

        def start_w(i):
            at = lax.rem(i, 2)
            pick(i, heads_steps, (qkv_own_ref, o_own_ref), (qkv_oth_ref, o_oth_ref),
                 lambda ref, j: [(ref[0].at[:, :, block(j, CW)], w_ref.at[at], w_sem.at[at, 0]),
                                 (ref[1].at[block(j, CW)], o_ref.at[at], w_sem.at[at, 1])])
            for n, ref in enumerate((q_hbm, k_hbm, v_hbm)):
                copy(ref.at[1, :, block(i, CW)], qkv_ref.at[at, n], w_sem.at[at, 2 + n]).start()
            copy(lse_hbm.at[1, i], lse_ref.at[at], w_sem.at[at, 5]).start()

        def write_heads(i):
            at = lax.rem(i, 2)
            return [copy(gqkv_ref.at[at, n], fresh[2 + n].at[:, block(i, CW)], t_sem.at[at, n]) for n in range(3)]

        def norm_load(index, u_hbm, r_hbm):
            return [copy(u_hbm.at[1], u_ref, g_sem.at[index]), copy(r_hbm.at[1], r_ref, g_sem.at[index + 1])]

        def begin():
            copy(g_hbm, g_ref, g_sem.at[0]).start()
            for item in norm_load(1, u2_hbm, r2_hbm):
                item.start()
            start_f(jnp.int32(0))
            start_f(jnp.int32(1))
            copy(g_hbm, g_ref, g_sem.at[0]).wait()
            for item in norm_load(1, u2_hbm, r2_hbm):
                item.wait()
            totals = [jnp.zeros((1, width), F32)] * 3
            for rs in halves(rows):
                grad_y = g_ref[rs, :].astype(F32)
                u = u_ref[rs, :].astype(F32)
                grad_c = norm_back(grad_y, u, r_ref[rs, 0:1], vec_w[4:5])
                gacc_ref[rs, :] = grad_c
                low_ref[0, rs, :] = grad_c.astype(BF)
                for index, values in enumerate((grad_y * u, grad_y, grad_c)):
                    totals[index] += row_sum(values)
            for index in range(3):
                part_sums[index : index + 1, :] = totals[index]
            for item in norm_load(1, u1_hbm, r1_hbm):
                item.start()

        def ffn_unit(u):
            at = lax.rem(u, 2)

            @pl.when(u >= 1)
            def _():
                for item in write_tile(u - 1):
                    item.wait()

            arrived(w_ref.at[at, pl.ds(0, 2)], w_sem.at[at, 0])
            arrived(w_ref.at[at, 2], w_sem.at[at, 1])
            for n in range(2):
                arrived(qkv_ref.at[at, n], w_sem.at[at, 2 + n])
            gh = dot(low_ref[0], w_ref[at, 2])
            g0 = (gh * qkv_ref[at, 1].astype(F32)).astype(BF)
            g1 = (gh * qkv_ref[at, 0].astype(F32)).astype(BF)
            gqkv_ref[at, 0] = g0
            gqkv_ref[at, 1] = g1
            side, j = place_of(u)
            cols = block(side * tiles + j, ft)
            ub_sums[0:1, cols] = row_sum(g0.astype(F32))
            ub_sums[1:2, cols] = row_sum(g1.astype(F32))
            gacc_ref[...] += dot(g0, w_ref[at, 0], NT) + dot(g1, w_ref[at, 1], NT)

            @pl.when(u + 2 < 2 * tiles)
            def _():
                start_f(u + 2)

            for item in write_tile(u):
                item.start()

        def norm_unit():
            for item in write_tile(jnp.int32(2 * tiles - 1)):
                item.wait()
            for i in range(2):
                start_w(jnp.int32(i))
            fill_distance(dist_ref, meta_ref[2])
            for item in norm_load(1, u1_hbm, r1_hbm):
                item.wait()
            totals = [jnp.zeros((1, width), F32)] * 3
            for rs in halves(rows):
                grad_n = gacc_ref[rs, :]
                u = u_ref[rs, :].astype(F32)
                grad_a = norm_back(grad_n, u, r_ref[rs, 0:1], vec_w[1:2])
                low_ref[1, rs, :] = grad_a.astype(BF)
                gacc_ref[rs, :] = grad_a
                for index, values in enumerate((grad_n * u, grad_n, grad_a)):
                    totals[index] += row_sum(values)
            for index in range(3):
                part_sums[3 + index : 4 + index, :] = totals[index]

        def head_unit(a):
            i = a // 5
            phase = lax.rem(a, 5)
            pair = phase // 2
            at = lax.rem(i, 2)
            scale = BF(1.0 / math.sqrt(HD))
            cols = block(lax.rem(pair, 2), 2 * HD)

            @pl.when(phase == 0)
            def _():
                for index, ref in enumerate(
                    (w_ref.at[at], o_ref.at[at], qkv_ref.at[at, 0], qkv_ref.at[at, 1], qkv_ref.at[at, 2], lse_ref.at[at])
                ):
                    arrived(ref, w_sem.at[at, index])

                @pl.when(i >= 2)
                def _():
                    for item in write_heads(i - 2):
                        item.wait()

                gm_ref[...] = dot(low_ref[1], o_ref[at], NT).astype(BF)

            @pl.when((phase == 0) | (phase == 2))
            def _():
                query2 = qkv_ref[at, 0, :, cols] * scale
                key2 = qkv_ref[at, 1, :, cols]
                value2 = qkv_ref[at, 2, :, cols]
                gm2 = gm_ref[:, cols]
                parts = []
                for head in range(2):
                    here = slice(head * HD, (head + 1) * HD)
                    gm = gm2[:, here]
                    scores = dot(key2[:, here], query2[:, here], NT)
                    scores = scores - dist_ref[...] * slope_ref[i * PER + pair * 2 + head]
                    likely = jnp.exp(scores - lse_ref[at, pl.ds(pair * 2 + head, 1), :])
                    parts.append(dot(likely.astype(BF), gm).astype(BF))
                    tt = likely * dot(value2[:, here], gm, NT)
                    inner = jnp.sum(tt, axis=0, keepdims=True)
                    gs_ref[head] = (tt - likely * inner).astype(BF)
                gqkv_ref[at, 2, :, cols] = jnp.concatenate(parts, axis=1)

            @pl.when((phase == 1) | (phase == 3))
            def _():
                query2 = qkv_ref[at, 0, :, cols] * scale
                key2 = qkv_ref[at, 1, :, cols] * scale
                parts = [[], []]
                for head in range(2):
                    here = slice(head * HD, (head + 1) * HD)
                    gs = gs_ref[head]
                    parts[1].append(dot(gs, query2[:, here]).astype(BF))
                    parts[0].append(dot(gs, key2[:, here], TN).astype(BF))
                for n in range(2):
                    gqkv_ref[at, n, :, cols] = jnp.concatenate(parts[n], axis=1)

            @pl.when(phase == 4)
            def _():
                for index, n in enumerate((0, 2)):
                    qv_sums[index : index + 1, block(i, CW)] = row_sum(gqkv_ref[at, n].astype(F32))
                gacc_ref[...] += (
                    dot(gqkv_ref[at, 0], w_ref[at, 0], NT)
                    + dot(gqkv_ref[at, 1], w_ref[at, 1], NT)
                    + dot(gqkv_ref[at, 2], w_ref[at, 2], NT)
                )

                @pl.when(i + 2 < 2 * heads_steps)
                def _():
                    start_w(i + 2)

                for item in write_heads(i):
                    item.start()

        ends = [(g_ref, gxl_out), (gacc_ref, gx_out)]

        def end_unit():
            for i in (2 * heads_steps - 2, 2 * heads_steps - 1):
                for item in write_heads(jnp.int32(i)):
                    item.wait()
            g_ref[...] = gacc_ref[...].astype(BF)
            for index, item in enumerate(ends):
                copy(*item, e_sem.at[index]).start()
            vec[0, 0:6] += part_sums[0:6]
            for own in range(2):
                @pl.when(t == own)
                def _(own=own):
                    for n in range(2):
                        for side in range(2):
                            place = own if side == 0 else 1 - own
                            for j in range(up_rows):
                                at = 6 + (2 * n + place) * up_rows + j
                                start = side * units + j * width
                                vec[0, at : at + 1] += ub_sums[n : n + 1, start : start + width]
                            at = 6 + 4 * up_rows + n
                            cols = slice(place * local, (place + 1) * local)
                            vec[0, at : at + 1, cols] += qv_sums[n : n + 1, side * local : (side + 1) * local]

            for index, item in enumerate(ends):
                copy(*item, e_sem.at[index]).wait()

        vec_load = copy(sums_ref, vec.at[0], v_load)
        vec_load.start()

        @pl.when(first)
        def _():
            begin()

        take_left(0, 0, 0)
        vec_load.wait()
        vec_core = remote(vec.at[0], vec_in.at[0], v_send.at[0], v_recv.at[0], core)
        vec_cross = remote(vec.at[1], vec_in.at[1], v_send.at[1], v_recv.at[1], cross)

        def row_copy(m, source):
            return remote(
                source.at[block(1 - t, shard_rows)], rows_out.at[m], r_send.at[m], r_recv.at[m], cross
            )

        row_plan = [(0, 0, low_grad_ref, True), (0, 1, gxl_out, False), (1, 1, second_ref, True)]
        for number, m, source, early in row_plan:
            if early:
                @pl.when(section == number)
                def _(m=m, source=source):
                    row_copy(m, source).start()

        up = pl.ds(0, quarter)
        down = pl.ds(quarter, quarter)
        sides = ((up, 0, z, above, below), (down, 1, last - z, below, above))

        @pl.loop(0, ahead_of + total + drain)
        def _(turn):
            s = turn - ahead_of

            @pl.when(first)
            def _():
                @pl.when(turn < norm_at)
                def _():
                    ffn_unit(turn)

                @pl.when(turn == norm_at)
                def _():
                    norm_unit()

                @pl.when((turn >= head_at) & (turn < end_at))
                def _():
                    head_unit(turn - head_at)

                @pl.when(turn == end_at)
                def _():
                    end_unit()

            @pl.when(s == 0)
            def _():
                for k in range(ring - 1):
                    load_tile(jnp.int32(k))

            @pl.when(valid(s))
            def _():
                @pl.when(s == per_pair - 2)
                def _():
                    take_left(1, 1, None)

                @pl.when(s == x_flip)
                def _():
                    take_left(2, 0, None)

                @pl.when(s == ga_flip)
                def _():
                    take_left(3, 1, 1)

                at = lax.rem(s, ring)
                arrived(tile.at[at], tile_sem.at[at])
                give_at = lax.rem(s, gives)

                @pl.when(s >= gives)
                def _():
                    arrived(give.at[give_at], give_send.at[give_at])

                ffn_flip = jnp.where(lax.rem(s, 3 * per_pair) // per_pair == 0, 0, 1)
                which = jnp.where(s < ffn_blocks, ffn_flip, jnp.where(s < ffn_blocks + 3 * head_blocks, 0, 1))
                for place, store, spot in ((1 - c, give, give_at), (c, mine, lax.rem(s, mines))):
                    here = block(place, half)
                    product = dot(flip[which, here, :rows], tile[at, 0])
                    for m in range(1, seqs):
                        product += dot(flip[which, here, m * rows : (m + 1) * rows], tile[at, m])
                    store[spot, 1] = product[:, :bt].astype(BF)
                    store[spot, 0] = product[:, bt:].astype(BF)

            @pl.when((s >= 0) & (s + ring - 1 < total))
            def _():
                load_tile(s + ring - 1)

            k1 = s - CORE_LAG

            @pl.when(valid(k1))
            def _():
                arrived(acc.at[k1], core_recv.at[k1])
                at = lax.rem(k1, mines)
                for side in range(2):
                    acc[k1, side] = (acc[k1, side].astype(F32) + mine[at, side].astype(F32)).astype(BF)

            k2 = k1 - CROSS_LAG

            @pl.when(valid(k2))
            def _():
                arrived(from_x.at[k2], x_recv.at[k2])
                acc[k2, 1] = (acc[k2, 1].astype(F32) + from_x[k2].astype(F32)).astype(BF)

            for rows_, way, place, ahead, behind in sides:
                k3 = k2 - CHAIN_LAG * place

                @pl.when(valid(k3) & (place > 0))
                def _(rows_=rows_, way=way, k3=k3):
                    arrived(from_z.at[k3, rows_], z_recv.at[way, k3])
                    acc[k3, 1, rows_] = (acc[k3, 1, rows_].astype(F32) + from_z[k3, rows_].astype(F32)).astype(BF)

                k4 = k2 - CHAIN_LAG * (2 * last - place)

                @pl.when(valid(k4) & (place == last))
                def _(rows_=rows_, k4=k4):
                    final[k4, rows_] = acc[k4, 1, rows_]

                @pl.when(valid(k4) & (place < last))
                def _(rows_=rows_, way=way, k4=k4):
                    arrived(final.at[k4, rows_], f_recv.at[way, k4])

            @pl.when(valid(s))
            def _():
                at = lax.rem(s, gives)
                remote(give.at[at], acc.at[s], give_send.at[at], core_recv.at[s], core).start()

            @pl.when(valid(k1))
            def _():
                remote(acc.at[k1, 0], from_x.at[k1], x_send, x_recv.at[k1], cross).start()

            for number, m, source, early in row_plan:
                if not early:
                    @pl.when((k1 == total - 1) & (section == number))
                    def _(m=m, source=source):
                        row_copy(m, source).start()

            for rows_, way, place, ahead, behind in sides:
                k3 = k2 - CHAIN_LAG * place

                @pl.when(valid(k3) & (place < last))
                def _(rows_=rows_, way=way, k3=k3, ahead=ahead):
                    remote(acc.at[k3, 1, rows_], from_z.at[k3, rows_], z_send.at[way], z_recv.at[way, k3], ahead).start()

                k4 = k2 - CHAIN_LAG * (2 * last - place)

                @pl.when(valid(k4) & (place > 0))
                def _(rows_=rows_, way=way, k4=k4, behind=behind):
                    remote(final.at[k4, rows_], final.at[k4, rows_], f_send.at[way], f_recv.at[way, k4], behind).start()

            k5 = k2 - CHAIN_LAG * 2 * last

            @pl.when(valid(k5))
            def _():
                def visit(m, j):
                    dst = outs[group_of[m]].at[member_of[m], block(c, half), block(j, bt)]
                    copy(final.at[k5], dst, store_sem).start()
                    remote(final.at[k5], dst, out_send, out_recv, core).start()

                member(k5, visit)

            @pl.when(turn == end_at + 1)
            def _():
                vec_core.start()

            @pl.when(turn == end_at + 6)
            def _():
                vec_core.wait_recv()
                vec[1] = vec[0] + vec_in[0]

            @pl.when(turn == end_at + 7)
            def _():
                vec_cross.start()

            @pl.when(turn == end_at + 13)
            def _():
                vec_cross.wait_recv()
                vec_all[z] = vec[1] + vec_in[1]

            @pl.when(turn == end_at + 14)
            def _():
                for shift in range(1, chips):
                    to = lax.rem(z + shift, chips)
                    remote(
                        vec_all.at[z], vec_all.at[z], v_send.at[1 + shift], v_recv.at[1 + shift], {"dp": to * 2 + c}
                    ).start()

        for number, m, source, early in row_plan:
            @pl.when(section == number)
            def _(m=m, source=source):
                row_copy(m, source).wait()

        vec_core.wait_send()
        vec_cross.wait_send()
        for shift in range(1, chips):
            origin = lax.rem(z + chips - shift, chips)
            arrived(vec_all.at[origin], v_recv.at[1 + shift])
            arrived(vec_all.at[z], v_send.at[1 + shift])
        whole = vec_all[0]
        for chip in range(1, chips):
            whole += vec_all[chip]
        sums_out[...] = whole
        for at in range(gives):
            arrived(give.at[at], give_send.at[at])
        arrived(acc.at[:, 0], x_send)
        for rows_, way, place, ahead, behind in sides:
            @pl.when(place < last)
            def _(rows_=rows_, way=way):
                arrived(from_z.at[:, rows_], z_send.at[way])

            @pl.when(place > 0)
            def _(rows_=rows_, way=way):
                arrived(final.at[:, rows_], f_send.at[way])

        arrived(final, out_send)
        arrived(final, store_sem)
        arrived(final, out_recv)

    sem = pltpu.SemaphoreType.DMA
    flops = 2 * seqs * rows * width * 2 * bt * total
    members = [member_of[index] for index in range(7)]
    shapes = [(sum(g == index for g in group_of), width, rights[group_of.index(index)].shape[2] // 2) for index in range(4)]
    return pl.pallas_call(
        kernel,
        in_specs=[SMEM, SMEM, WHOLE] + [ANY] * 33,
        out_specs=[ANY] * 4 + [WHOLE] + [ANY] * 8,
        out_shape=[jax.ShapeDtypeStruct(s, BF) for s in shapes]
        + [jax.ShapeDtypeStruct(vec_shape, F32), jax.ShapeDtypeStruct((seqs, shard_rows, width), BF)]
        + [jax.ShapeDtypeStruct(act.shape, BF)] * 2
        + [jax.ShapeDtypeStruct((rows, 2 * local), BF)] * 3
        + [jax.ShapeDtypeStruct((rows, width), F32), jax.ShapeDtypeStruct((rows, width), BF)],
        scratch_shapes=[
            pltpu.VMEM((total, 2, half, bt), BF),
            pltpu.VMEM((total, half, bt), BF),
            pltpu.VMEM((total, half, bt), BF),
            pltpu.VMEM((2, width, seqs * rows), BF),
            pltpu.VMEM((seqs, rows, width), BF),
            pltpu.VMEM((ring, seqs, rows, 2 * bt), BF),
            pltpu.VMEM((mines, 2, half, bt), BF),
            pltpu.VMEM((gives, 2, half, bt), BF),
            pltpu.VMEM((2,) + vec_shape, F32),
            pltpu.VMEM((2,) + vec_shape, F32),
            pltpu.VMEM((chips,) + vec_shape, F32),
            pltpu.VMEM((rows, width), BF),
            pltpu.VMEM((rows, width), BF),
            pltpu.VMEM((rows, 128), F32),
            pltpu.VMEM((2, rows, width), BF),
            pltpu.VMEM((rows, width), F32),
            pltpu.VMEM((2, 3, width, CW), BF),
            pltpu.VMEM((2, CW, width), BF),
            pltpu.VMEM((2, 3, rows, CW), BF),
            pltpu.VMEM((2, 3, rows, CW), BF),
            pltpu.VMEM((2, 8, rows), F32),
            pltpu.VMEM((rows, CW), BF),
            pltpu.VMEM((2, rows, rows), BF),
            pltpu.VMEM((rows, rows), F32),
            pltpu.VMEM((8, width), F32),
            pltpu.VMEM((2, 2 * units), F32),
            pltpu.VMEM((2, 2 * local), F32),
            sem((ring,)), sem((2,)), sem((gives,)), sem((total,)), sem, sem((total,)),
            sem((2,)), sem((2, total)), sem((2,)), sem((2, total)),
            sem, sem, sem, sem, sem((chips + 1,)), sem((chips + 1,)), sem((seqs,)), sem((seqs,)),
            sem((3,)), sem((2, 6)), sem((2, 3)), sem((2,)),
        ],
        input_output_aliases={8: 6, 9: 7},
        compiler_params=pltpu.CompilerParams(
            collective_id=0, has_side_effects=True, vmem_limit_bytes=67_000_000
        ),
        cost_estimate=pl.CostEstimate(flops=flops, bytes_accessed=100 << 20, transcendentals=0),
        name="backward_and_reduce",
    )(
        meta, slopes, vecs, grad, q, k_, v, lse, act, slope, u1, u2, r1, r2, *weights, *lefts, *rights, sums, low_grad, second
    )


def exchange_rows(outputs, deps):
    seqs = len(outputs)
    rows, width = outputs[0].shape
    shard_rows = rows // 2
    n_in = seqs + len(deps)

    def kernel(*refs):
        y_refs, out_ref = refs[:seqs], refs[n_in]
        stage, send, recv, l_sem = refs[n_in + 1 :]
        t = lax.axis_index("tensor")
        cross = {"tensor": 1 - t}
        barrier = pltpu.get_barrier_semaphore()
        pl.semaphore_signal(barrier, inc=1, device_id=cross, device_id_type=MESH)
        pl.semaphore_wait(barrier, 1)

        @pl.when(lax.axis_index("section") == 0)
        def _():
            for m in range(seqs):
                pltpu.make_async_remote_copy(
                    src_ref=y_refs[m].at[block(1 - t, shard_rows)], dst_ref=out_ref.at[t * seqs + m],
                    send_sem=send.at[m], recv_sem=recv.at[m], device_id=cross, device_id_type=MESH,
                ).start()
            for m in range(seqs):
                copy(y_refs[m].at[block(t, shard_rows)], stage.at[m], l_sem.at[m]).start()
            for m in range(seqs):
                arrived(stage.at[m], l_sem.at[m])
                copy(stage.at[m], out_ref.at[t * seqs + m], l_sem.at[m]).start()
            for m in range(seqs):
                arrived(stage.at[m], l_sem.at[m])
            for m in range(seqs):
                arrived(out_ref.at[(1 - t) * seqs + m], recv.at[m])
                arrived(stage.at[m], send.at[m])

    sem = pltpu.SemaphoreType.DMA
    return pl.pallas_call(
        kernel,
        in_specs=[ANY] * n_in,
        out_specs=ANY,
        out_shape=jax.ShapeDtypeStruct((2 * seqs, shard_rows, width), BF),
        scratch_shapes=[pltpu.VMEM((seqs, shard_rows, width), BF), sem((seqs,)), sem((seqs,)), sem((seqs,))],
        compiler_params=pltpu.CompilerParams(collective_id=2, has_side_effects=True),
        cost_estimate=pl.CostEstimate(flops=0, bytes_accessed=0, transcendentals=0),
        name="exchange_rows",
    )(*outputs, *deps)


def widen(reduced, row_grads, got, got_second, produced, outputs, sums, units, local):
    shard_rows, width = got.shape[1:]
    seqs = got.shape[0]
    n = len(reduced)
    jobs = []
    for index, array in enumerate(reduced):
        lead, depth, columns = array.shape
        step = 512 * 1024 // columns
        if index == n - 1:
            jobs += [(index, 0, at, depth // 2, columns) for at in range(0, depth, depth // 2)]
        else:
            jobs += [(index, part, at, step, columns) for part in range(lead) for at in range(0, depth, step)]
    jobs += [(n, m, 0, shard_rows, width) for m in range(seqs)] + [(n + 1, m, 0, shard_rows, width) for m in range(seqs)]
    jobs += [(n + 2, m, 0, shard_rows, width) for m in range(2 * seqs)]
    ring = 3
    n_in = n + 3 * seqs + 4
    parts = units // width

    def kernel(*refs):
        ins = refs[:n]
        grad_refs = refs[n : n + 2 * seqs]
        got_ref, got_second_ref, produced_ref = refs[n + 2 * seqs : n + 2 * seqs + 3]
        y_refs, sums_ref = refs[n + 2 * seqs + 3 : n_in - 1], refs[n_in - 1]
        outs = refs[n_in : n_in + n + 2]
        qv_ref, out_bias_ref, gain_ref, shift_ref, ub_ref, down_bias_ref = refs[n_in + n + 2 : n_in + n + 8]
        shapes = sorted({(j[3], j[4]) for j in jobs if j[0] != n})
        buffers = refs[n_in + n + 8 :]
        wide_rows, in_sem, out_sem = buffers[0], buffers[1], buffers[2]
        low = {s: buffers[3 + 2 * i] for i, s in enumerate(shapes)}
        wide = {s: buffers[4 + 2 * i] for i, s in enumerate(shapes)}
        t = lax.axis_index("tensor")
        section = lax.axis_index("section")

        def load(number):
            index, part, at, rows, columns = jobs[number]
            s = number % ring
            if index < n:
                copy(ins[index].at[part, pl.ds(at, rows)], low[rows, columns].at[s], in_sem.at[s]).start()
            elif index == n:
                for turn in range(2):
                    @pl.when(section == turn)
                    def _(turn=turn):
                        source = grad_refs[turn * seqs + part].at[block(t, shard_rows)]
                        copy(source, wide_rows.at[part], in_sem.at[s]).start()
            elif index == n + 1:
                for number_ in range(2):
                    @pl.when(section == number_)
                    def _(number_=number_):
                        source = got_second_ref.at[seqs] if number_ == 1 and part == 0 else got_ref.at[part]
                        copy(source, low[rows, columns].at[s], in_sem.at[s]).start()
            else:
                @pl.when(section == 0)
                def _():
                    copy(produced_ref.at[part], low[rows, columns].at[s], in_sem.at[s]).start()

                @pl.when(section == 1)
                def _():
                    source = y_refs[part].at[block(t, shard_rows)] if part < seqs else got_second_ref.at[part - seqs]
                    copy(source, low[rows, columns].at[s], in_sem.at[s]).start()

        def store(number):
            index, part, at, rows, columns = jobs[number]
            s = number % ring
            if index < n - 1:
                return copy(wide[rows, columns].at[s], outs[index].at[part, pl.ds(at, rows)], out_sem.at[s])
            if index == n - 1:
                return copy(wide[rows, columns].at[s], outs[index].at[:, pl.ds(at, rows)], out_sem.at[s])
            if index == n:
                return copy(wide_rows.at[part], outs[n].at[t * seqs + part], out_sem.at[s])
            if index == n + 1:
                return copy(wide[rows, columns].at[s], outs[n].at[(1 - t) * seqs + part], out_sem.at[s])
            side, m = divmod(part, seqs)
            spread = (t + side - 2 * t * side) * seqs + m
            return copy(low[rows, columns].at[s], outs[n + 1].at[jnp.where(section == 0, part, spread)], out_sem.at[s])

        for number in range(ring):
            load(number)
        gain_ref[0:1] = sums_ref[3:4]
        gain_ref[1:2] = sums_ref[0:1]
        shift_ref[0:1] = sums_ref[4:5]
        shift_ref[1:2] = sums_ref[1:2]
        out_bias_ref[...] = sums_ref[5:6]
        down_bias_ref[...] = sums_ref[2:3]
        for half in range(2):
            @pl.when(t == half)
            def _(half=half):
                for g in range(2):
                    for j in range(parts):
                        at = 6 + (2 * g + half) * parts + j
                        ub_ref[g : g + 1, j * width : (j + 1) * width] = sums_ref[at : at + 1]
                    at = 6 + 4 * parts + g
                    qv_ref[g : g + 1] = sums_ref[at : at + 1, half * local : (half + 1) * local]

        for number, (index, part, at, rows, columns) in enumerate(jobs):
            s = number % ring
            if index == n:
                arrived(wide_rows.at[part], in_sem.at[s])
            else:
                arrived(low[rows, columns].at[s], in_sem.at[s])
            if number >= ring and jobs[number - ring][0] != n + 2:
                store(number - ring).wait()
            if index == n - 1:
                wide[rows, columns][s] = low[rows, columns][s].astype(F32).T
            elif index not in (n, n + 2):
                wide[rows, columns][s] = low[rows, columns][s].astype(F32)
            store(number).start()
            if index == n + 2:
                store(number).wait()
            if number + ring < len(jobs):
                load(number + ring)
        for number in range(len(jobs) - ring, len(jobs)):
            if jobs[number][0] != n + 2:
                store(number).wait()

    shapes = sorted({(j[3], j[4]) for j in jobs if j[0] != n})
    square = (reduced[-1].shape[1] // 2, reduced[-1].shape[2])
    last = reduced[-1].shape
    sem = pltpu.SemaphoreType.DMA
    buffers = []
    for s in shapes:
        buffers += [pltpu.VMEM((ring,) + s, BF), pltpu.VMEM((ring,) + ((s[1], s[0]) if s == square else s), F32)]
    return pl.pallas_call(
        kernel,
        in_specs=[ANY] * (n_in - 1) + [WHOLE],
        out_specs=[ANY] * (n + 2) + [WHOLE] * 6,
        out_shape=[jax.ShapeDtypeStruct(r.shape, F32) for r in reduced[:-1]]
        + [jax.ShapeDtypeStruct((last[2], last[1]), F32), jax.ShapeDtypeStruct((2 * seqs, shard_rows, width), F32)]
        + [jax.ShapeDtypeStruct((2 * seqs, shard_rows, width), BF)]
        + [
            jax.ShapeDtypeStruct(shape, F32)
            for shape in ((2, local), (1, width), (2, width), (2, width), (2, units), (1, width))
        ],
        scratch_shapes=[pltpu.VMEM((seqs, shard_rows, width), F32), sem((ring,)), sem((ring,))] + buffers,
        compiler_params=pltpu.CompilerParams(vmem_limit_bytes=VMEM_LIMIT),
        cost_estimate=pl.CostEstimate(flops=0, bytes_accessed=56 << 20, transcendentals=0),
        name="widen",
    )(*reduced, *row_grads, got, got_second, produced, *outputs, sums)


MASKED = -1000000000.0


def shifted(value, axis, steps):
    count = lax.axis_size(axis)
    first, last = (max(0, -steps), min(count, count - steps))
    return lax.ppermute(value, axis, [(source, source + steps) for source in range(first, last)])


def layer_norm(values, gain, shift):
    mean = jnp.mean(values, axis=-1, keepdims=True)
    centred = values - mean
    spread = jnp.mean(centred * centred, axis=-1, keepdims=True)
    return centred * lax.rsqrt(spread + EPS) * gain + shift


def alibi_slopes(first, count, heads):
    index = (first + jnp.arange(count)).astype(jnp.float32)
    return jnp.exp2(-8.0 * (index + 1.0) / heads)


def attention_core(projected, qv_bias, slopes, key_ok):
    rows = projected.shape[0]
    width = projected.shape[2]
    count = slopes.shape[0]
    size = width // count
    query = (projected[:, 0] + qv_bias[0]).astype(jnp.bfloat16).reshape(rows, count, size)
    key = projected[:, 1].astype(jnp.bfloat16).reshape(rows, count, size)
    value = (projected[:, 2] + qv_bias[1]).astype(jnp.bfloat16).reshape(rows, count, size)
    place = jnp.arange(rows).astype(jnp.float32)
    distance = jnp.abs(place[:, None] - place[None, :])
    scale = 1.0 / math.sqrt(size)
    scores = (
        jnp.einsum("qhd,khd->hqk", query, key, preferred_element_type=jnp.float32) * scale
        - slopes[:, None, None] * distance[None]
    )
    scores = jnp.where(key_ok[None, None, :], scores, MASKED)
    weights = jax.nn.softmax(scores, axis=-1)
    weights_low = weights.astype(jnp.bfloat16)
    mixed = jnp.einsum("hqk,khd->qhd", weights_low, value, preferred_element_type=jnp.float32)
    mixed = mixed.reshape(rows, width).astype(jnp.bfloat16)
    return (query, key, value, weights, weights_low, mixed)


def attention_back(parts, grad_mixed, key_ok):
    query, key, value, weights, weights_low, mixed = parts
    rows, count, size = query.shape
    scale = 1.0 / math.sqrt(size)
    grad_low = grad_mixed.astype(jnp.bfloat16).reshape(rows, count, size)
    grad_weights = jnp.einsum("qhd,khd->hqk", grad_low, value, preferred_element_type=jnp.float32)
    grad_value = jnp.einsum(
        "hqk,qhd->khd", weights_low, grad_low, preferred_element_type=jnp.float32
    )
    inner = jnp.sum(weights * grad_weights, axis=-1, keepdims=True)
    grad_scores = weights * (grad_weights - inner)
    grad_scores = jnp.where(key_ok[None, None, :], grad_scores, 0.0).astype(jnp.bfloat16)
    grad_query = (
        jnp.einsum("hqk,khd->qhd", grad_scores, key, preferred_element_type=jnp.float32) * scale
    ).astype(jnp.bfloat16)
    grad_key = (
        jnp.einsum("hqk,qhd->khd", grad_scores, query, preferred_element_type=jnp.float32) * scale
    ).astype(jnp.bfloat16)
    grad_value = grad_value.astype(jnp.bfloat16)
    width = count * size
    grad_query = grad_query.reshape(rows, width)
    grad_key = grad_key.reshape(rows, width)
    grad_value = grad_value.reshape(rows, width)
    grad_projected = jnp.stack([grad_query, grad_key, grad_value], axis=1).reshape(rows, 3 * width)
    qv_grad = jnp.stack(
        [
            jnp.sum(grad_query.astype(jnp.float32), axis=0),
            jnp.sum(grad_value.astype(jnp.float32), axis=0),
        ]
    )
    return (grad_projected, qv_grad)


def gelu_product(both):
    return jax.nn.gelu(both[:, 0], approximate=False) * both[:, 1]


def geglu(lifted, up_bias):
    return gelu_product(lifted + up_bias[None])


def ffn_grads(rows_low, grad_low, up_weight, up_bias, down_weight):
    lifted = jnp.einsum("sd,gdf->sgf", rows_low, up_weight, preferred_element_type=jnp.float32)
    hidden, geglu_back = jax.vjp(gelu_product, lifted + up_bias[None])
    grad_hidden = jnp.einsum("sd,df->sf", grad_low, down_weight, preferred_element_type=jnp.float32)
    (grad_both,) = geglu_back(grad_hidden)
    grad_lifted = grad_both.astype(jnp.bfloat16)
    grad_bias = jnp.sum(grad_lifted.astype(jnp.float32), axis=0)
    up_grad = jnp.einsum("sd,sgf->gdf", rows_low, grad_lifted, preferred_element_type=jnp.float32)
    down_grad = jnp.einsum(
        "sd,sf->df", grad_low, hidden.astype(jnp.bfloat16), preferred_element_type=jnp.float32
    )
    return (grad_lifted, grad_bias, up_grad, down_grad)


def on_device(
    inputs,
    cotangent,
    lengths,
    w_qkv,
    b_qv,
    w_out,
    b_out,
    ln_gain,
    ln_bias,
    w_up,
    b_up,
    w_down,
    b_down,
):
    batches, shard_rows, width = inputs.shape
    parts = lax.axis_size("tensor")
    place = lax.axis_index("tensor")
    section = lax.axis_index("section")
    last_section = lax.axis_size("section") - 1
    full_rows = shard_rows * parts
    local_width = w_qkv.shape[3]
    local_heads = local_width // HD
    qkv_flat = w_qkv[0].reshape(width, 3 * local_width)
    out_weight = w_out[0]
    qv_bias = b_qv[0].astype(jnp.float32)
    out_bias = b_out[0].astype(jnp.float32)
    gains = ln_gain[0].astype(jnp.float32)
    shifts = ln_bias[0].astype(jnp.float32)
    down_bias = b_down[0].astype(jnp.float32)
    slopes = alibi_slopes(place * local_heads, local_heads, H)
    row_place = place * shard_rows + jnp.arange(shard_rows)
    kept_rows = 0

    def key_mask(length):
        return jnp.arange(full_rows) < length

    def after_attention(values, attended, bias, gain_rows, shift_rows):
        return layer_norm(values + attended + bias, gain_rows[0], shift_rows[0])

    def after_ffn(normed, lowered, bias, gain_rows, shift_rows):
        return layer_norm(normed + lowered + bias, gain_rows[1], shift_rows[1])

    def gather_inputs(values):
        return lax.all_gather(values.astype(jnp.bfloat16), "tensor", axis=0, tiled=True)

    def project(gathered):
        return jnp.dot(gathered, qkv_flat, preferred_element_type=jnp.float32).reshape(
            full_rows, 3, local_width
        )

    def attention_forward(values, length):
        gathered = gather_inputs(values)
        projected = project(gathered)
        mixed = attention_core(projected, qv_bias, slopes, key_mask(length))[5]

        def term(start, count):
            return jnp.dot(mixed, out_weight, preferred_element_type=jnp.float32)

        return (
            lax.psum_scatter(
                term(jnp.int32(0), shard_rows * lax.axis_size("tensor")).astype(jnp.bfloat16),
                "tensor",
                scatter_dimension=0,
                tiled=True,
            ).astype(jnp.float32),
            gathered,
            projected,
        )

    up_local = w_up[0]
    up_bias_local = b_up[0].astype(jnp.float32)
    down_local = w_down[0]

    def gather_normed(normed):
        return lax.all_gather(normed.astype(jnp.bfloat16), "tensor", axis=0, tiled=True)

    def ffn_forward(normed):
        lifted = jnp.einsum(
            "sd,gdf->sgf", gather_normed(normed), up_local, preferred_element_type=jnp.float32
        )
        hidden = geglu(lifted, up_bias_local).astype(jnp.bfloat16)

        def term(start, count):
            return jnp.einsum("sf,df->sd", hidden, down_local, preferred_element_type=jnp.float32)

        return lax.psum_scatter(
            term(jnp.int32(0), shard_rows * lax.axis_size("tensor")).astype(jnp.bfloat16),
            "tensor",
            scatter_dimension=0,
            tiled=True,
        ).astype(jnp.float32)

    def ffn_backward(normed, grad_lowered):
        gathered = gather_normed(normed)
        grad_whole = lax.all_gather(grad_lowered.astype(jnp.bfloat16), "tensor", axis=0, tiled=True)
        grad_lifted, grad_bias, up_grad, down_grad = ffn_grads(
            gathered, grad_whole, up_local, up_bias_local, down_local
        )

        def term(start, count):
            return jnp.einsum(
                "sgf,gdf->sd", grad_lifted, up_local, preferred_element_type=jnp.float32
            )

        grad_normed = lax.psum_scatter(
            term(jnp.int32(0), shard_rows * lax.axis_size("tensor")).astype(jnp.bfloat16),
            "tensor",
            scatter_dimension=0,
            tiled=True,
        ).astype(jnp.float32)
        return (grad_normed, (up_grad, grad_bias, down_grad))

    ffn_shapes = (up_local.shape, up_bias_local.shape, down_local.shape)

    def layer_forward(values, length):
        attended, gathered, projected = attention_forward(values, length)
        normed = after_attention(values, attended, out_bias, gains, shifts)
        lowered = ffn_forward(normed)
        return (
            after_ffn(normed, lowered, down_bias, gains, shifts),
            attended,
            lowered,
            gathered,
            projected,
        )

    def layer_backward(values, attended, lowered, length, grad_output):
        normed, attention_norm_back = jax.vjp(
            after_attention, values, attended, out_bias, gains, shifts
        )
        outcome, ffn_norm_back = jax.vjp(after_ffn, normed, lowered, down_bias, gains, shifts)
        grad_normed, grad_lowered, grad_down_bias, gain_late, shift_late = ffn_norm_back(
            grad_output
        )
        grad_from_ffn, ffn_terms = ffn_backward(normed, grad_lowered)
        grad_values, grad_attended, grad_out_bias, gain_early, shift_early = attention_norm_back(
            grad_normed + grad_from_ffn
        )
        gathered = gather_inputs(values)
        projected = project(gathered)
        grad_whole = lax.all_gather(
            grad_attended.astype(jnp.bfloat16), "tensor", axis=0, tiled=True
        )
        mask = key_mask(length)
        pieces = attention_core(projected, qv_bias, slopes, mask)
        mixed_low = pieces[5]
        out_grad = jnp.einsum(
            "se,sd->ed", mixed_low, grad_whole, preferred_element_type=jnp.float32
        )
        grad_mixed = jnp.einsum(
            "sd,ed->se", grad_whole, out_weight, preferred_element_type=jnp.float32
        )
        grad_projected, qv_grad = attention_back(pieces, grad_mixed, mask)
        qkv_grad = jnp.einsum(
            "sd,sx->dx", gathered, grad_projected, preferred_element_type=jnp.float32
        )

        def term(start, count):
            return jnp.einsum(
                "sx,dx->sd", grad_projected, qkv_flat, preferred_element_type=jnp.float32
            )

        grad_inputs = grad_values + lax.psum_scatter(
            term(jnp.int32(0), shard_rows * lax.axis_size("tensor")).astype(jnp.bfloat16),
            "tensor",
            scatter_dimension=0,
            tiled=True,
        ).astype(jnp.float32)
        terms = (
            qkv_grad,
            qv_grad,
            out_grad,
            grad_out_bias,
            gain_early + gain_late,
            shift_early + shift_late,
            ffn_terms[0],
            ffn_terms[1],
            ffn_terms[2],
            grad_down_bias,
        )
        return (grad_inputs, terms)

    def keep(store, item, batch, valid):
        old = lax.dynamic_index_in_dim(store, batch, 0, keepdims=False)
        return lax.dynamic_update_index_in_dim(store, jnp.where(valid, item, old), batch, 0)

    def forward_step(step, carry):
        (
            received,
            kept_values,
            kept_attended,
            kept_lowered,
            produced,
            kept_gathered,
            kept_projected,
        ) = carry
        index = step - section
        valid = (index >= 0) & (index < batches)
        batch = jnp.clip(index, 0, batches - 1)
        fresh = lax.dynamic_index_in_dim(
            inputs, jnp.minimum(step, batches - 1), 0, keepdims=False
        ).astype(jnp.float32)
        values = jnp.where(section == 0, fresh, received.astype(jnp.float32))
        output, attended, lowered, gathered, projected = layer_forward(values, lengths[batch])
        sent = output.astype(jnp.bfloat16)
        kept_values = keep(kept_values, values, batch, valid)
        kept_attended = keep(kept_attended, attended, batch, valid)
        kept_lowered = keep(kept_lowered, lowered, batch, valid)
        produced = keep(produced, sent, batch, valid)
        kept_gathered = keep(kept_gathered, gathered[:kept_rows], batch, valid)
        kept_projected = keep(kept_projected, projected[:kept_rows], batch, valid)
        received = shifted(sent, "section", 1)
        return (
            received,
            kept_values,
            kept_attended,
            kept_lowered,
            produced,
            kept_gathered,
            kept_projected,
        )

    store_zeros = jnp.zeros((batches, shard_rows, width), jnp.float32)
    gathered_zeros = jnp.zeros((batches, kept_rows, width), jnp.bfloat16)
    projected_zeros = jnp.zeros((batches, kept_rows, 3, local_width), jnp.float32)
    start_forward = (
        jnp.zeros((shard_rows, width), jnp.bfloat16),
        store_zeros,
        store_zeros,
        store_zeros,
        jnp.zeros((batches, shard_rows, width), jnp.bfloat16),
        gathered_zeros,
        projected_zeros,
    )
    received, kept_values, kept_attended, kept_lowered, produced, kept_gathered, kept_projected = (
        lax.fori_loop(0, batches + last_section, forward_step, start_forward)
    )

    def backward_step(step, carry):
        received, totals, grads_in = carry
        index = step - (last_section - section)
        valid = (index >= 0) & (index < batches)
        batch = jnp.clip(index, 0, batches - 1)
        length = lengths[batch]
        outer = lax.dynamic_index_in_dim(cotangent, batch, 0, keepdims=False).astype(jnp.float32)
        outer = outer * (row_place < length).astype(jnp.float32)[:, None]
        grad_output = jnp.where(section == last_section, outer, received.astype(jnp.float32))
        grad_output = jnp.where(valid, grad_output, 0.0)
        values = lax.dynamic_index_in_dim(kept_values, batch, 0, keepdims=False)
        attended = lax.dynamic_index_in_dim(kept_attended, batch, 0, keepdims=False)
        lowered = lax.dynamic_index_in_dim(kept_lowered, batch, 0, keepdims=False)
        grad_inputs, terms = layer_backward(values, attended, lowered, length, grad_output)
        totals = jax.tree.map(jnp.add, totals, terms)
        grads_in = keep(grads_in, grad_inputs, batch, valid)
        received = shifted(grad_inputs.astype(jnp.bfloat16), "section", -1)
        return (received, totals, grads_in)

    start_totals = (
        jnp.zeros((width, 3 * local_width), jnp.float32),
        jnp.zeros((2, local_width), jnp.float32),
        jnp.zeros((local_width, width), jnp.float32),
        jnp.zeros((width,), jnp.float32),
        jnp.zeros((2, width), jnp.float32),
        jnp.zeros((2, width), jnp.float32),
        jnp.zeros(ffn_shapes[0], jnp.float32),
        jnp.zeros(ffn_shapes[1], jnp.float32),
        jnp.zeros(ffn_shapes[2], jnp.float32),
        jnp.zeros((width,), jnp.float32),
    )
    start_backward = (jnp.zeros((shard_rows, width), jnp.bfloat16), start_totals, store_zeros)
    received, totals, grads_in = lax.fori_loop(
        0, batches + last_section, backward_step, start_backward
    )
    (
        qkv_total,
        qv_total,
        out_total,
        out_bias_total,
        gain_total,
        shift_total,
        up_total,
        up_bias_total,
        down_total,
        down_bias_total,
    ) = totals
    qkv_sum, qv_sum, out_sum, up_sum, up_bias_sum, down_sum = (
        lax.psum(qkv_total.astype(jnp.bfloat16), "dp").astype(jnp.float32),
        lax.psum(qv_total.astype(jnp.bfloat16), "dp").astype(jnp.float32),
        lax.psum(out_total.astype(jnp.bfloat16), "dp").astype(jnp.float32),
        lax.psum(up_total.astype(jnp.bfloat16), "dp").astype(jnp.float32),
        lax.psum(up_bias_total.astype(jnp.bfloat16), "dp").astype(jnp.float32),
        lax.psum(down_total.astype(jnp.bfloat16), "dp").astype(jnp.float32),
    )
    out_bias_sum, gain_sum, shift_sum, down_bias_sum = lax.psum(
        (out_bias_total, gain_total, shift_total, down_bias_total), ("tensor", "dp")
    )
    return (
        produced[None],
        grads_in[None],
        qkv_sum.reshape(1, width, 3, local_width),
        qv_sum[None],
        out_sum[None],
        out_bias_sum[None],
        gain_sum[None],
        shift_sum[None],
        up_sum[None],
        up_bias_sum[None],
        down_sum[None],
        down_bias_sum[None],
    )


def by_sequence(
    inputs,
    cotangent,
    lengths,
    w_qkv,
    b_qv,
    w_out,
    b_out,
    ln_gain,
    ln_bias,
    w_up,
    b_up,
    w_down,
    b_down,
):
    batches, shard_rows, width = inputs.shape
    place = lax.axis_index("tensor")
    section = lax.axis_index("section")
    groups = lax.axis_size("dp")
    rows = 2 * shard_rows
    seqs = batches // 2
    local = w_qkv.shape[3]
    units = w_up.shape[3]
    heads = local // HD
    chips = groups // 2

    qkv_own = jnp.transpose(w_qkv[0], (1, 0, 2))
    out_own = w_out[0]
    up_own = w_up[0]
    down_own = w_down[0]
    first = section == 0
    vecs = jnp.stack(
        [b_out[0], ln_gain[0, 0], ln_bias[0, 0], b_down[0], ln_gain[0, 1], ln_bias[0, 1], b_out[0], b_out[0]]
    ).astype(F32)
    slope_table = np.exp2(-8.0 * (np.arange(2 * heads, dtype=np.float32) + 1.0) / H).astype(np.float32)
    slopes = jnp.where(place == 0, slope_table, np.roll(slope_table, heads))
    own_lengths = lax.dynamic_slice_in_dim(lengths, place * seqs, seqs, 0)

    def meta(m, turn):
        active = section == turn
        return jnp.stack([jnp.int32(m), active.astype(jnp.int32), own_lengths[m], own_lengths[m] if turn == 1 else jnp.int32(rows)])

    metas = [[meta(m, turn) for m in range(seqs)] for turn in range(2)]
    qkv_oth, out_oth, up_oth, down_oth, bias, up_bias, *rest = fetch_and_forward(
        (qkv_own, out_own, up_own, down_own),
        (b_qv[0], b_up[0]),
        inputs,
        cotangent,
        slopes,
        vecs,
        metas[0][0],
        chips,
        seqs,
    )
    weights = (qkv_own, qkv_oth, out_own, out_oth, up_own, up_oth, down_own, down_oth)
    x_first = outer = rest[:seqs]
    *kept, y = rest[seqs:]
    deps = [y]

    def forward(x, m, turn):
        nonlocal kept, deps
        *kept, y = layer_forward(x, weights, bias, slopes, vecs, up_bias, metas[turn][m], kept, deps, seqs)
        deps = [y]
        return y

    y_first = [y] + [forward(x_first[m], m, 0) for m in range(1, seqs)]
    x_second = [lax.ppermute(y, "section", [(0, 1)]) for y in y_first]
    y_second = [forward(x_second[0], 0, 1)]
    produced = exchange_rows(y_first, deps)
    deps = [produced]
    y_second += [forward(x_second[m], m, 1) for m in range(1, seqs)]

    back = None
    sums = [[None] * seqs, [None] * seqs]

    got_second = None

    def backward(grad, m, turn, *extra):
        nonlocal back, deps, got_second
        results = layer_backward(grad, kept, weights, slopes, vecs, metas[turn][m], back, deps, seqs, *extra)
        back, (gx, gx_low, norm_sums, up_sums, qv_sums) = results[:7], results[7:12]
        if extra:
            got_second = results[12]
        deps = [norm_sums]
        sums[turn][m] = (norm_sums, up_sums, qv_sums)
        return gx, gx_low

    gx_second = [backward(outer[0], 0, 1)]
    gx_second.append(backward(outer[1], 1, 1, 1, 1, [*y_second, gx_second[0][1]]))
    grad_middle = [lax.ppermute(gx_second[m][1], "section", [(1, 0)]) for m in range(seqs)]
    x_all = jnp.stack([jnp.where(first, x_first[m], x_second[m]) for m in range(seqs)])
    deps = deps + [x_all]
    gx_first = [backward(grad_middle[0], 0, 0)]

    norm_sums, up_sums, qv_sums = [
        jnp.where(first, sums[0][0][index], sum(item[index] for item in sums[1])) for index in range(3)
    ]

    def ordered(values, count):
        return jnp.where(
            place == 0, values, jnp.concatenate([values[:, count:], values[:, :count]], axis=1)
        ).reshape(-1, width)

    packed = jnp.concatenate([norm_sums[:6], ordered(up_sums[:2], units), ordered(qv_sums[:2], local)])
    *reduced, packed, got, _, _, _, _, _, gx, _ = backward_and_reduce(
        grad_middle[1], kept, back, x_all, weights, slopes, vecs, metas[0][1], packed, gx_first[0][1],
        gx_second[1][1], chips,
    )
    gx_all = [gx_first[0][0], gx] + [g[0] for g in gx_second]
    (
        down_sum, up_sum, qkv_sum, out_sum, grads_in, produced,
        qv_sum, out_bias_sum, gain_sum, shift_sum, up_bias_sum, down_bias_sum,
    ) = widen(reduced, gx_all, got, got_second, produced, y_second, packed, units, local)
    return (
        produced[None],
        grads_in[None],
        jnp.transpose(qkv_sum, (1, 0, 2))[None],
        qv_sum[None],
        out_sum[None],
        out_bias_sum,
        gain_sum[None],
        shift_sum[None],
        up_sum[None],
        up_bias_sum[None],
        down_sum,
        down_bias_sum,
    )


def solution(mesh):
    sections, parts, groups = (mesh.shape[name] for name in ("section", "tensor", "dp"))

    def run(*args):
        paired = sections == 2 and parts == 2 and groups % 2 == 0 and args[0].shape[0] == 4
        return (by_sequence if paired else on_device)(*args)

    return jax.shard_map(
        run,
        mesh=mesh,
        in_specs=(
            P("dp", "tensor", None),
            P("dp", "tensor", None),
            P("dp"),
            P("section", None, None, "tensor"),
            P("section", None, "tensor"),
            P("section", "tensor", None),
            P("section", None),
            P("section", None, None),
            P("section", None, None),
            P("section", None, None, "tensor"),
            P("section", None, "tensor"),
            P("section", None, "tensor"),
            P("section", None),
        ),
        out_specs=(
            P("section", "dp", "tensor", None),
            P("section", "dp", "tensor", None),
            P("section", None, None, "tensor"),
            P("section", None, "tensor"),
            P("section", "tensor", None),
            P("section", None),
            P("section", None, None),
            P("section", None, None),
            P("section", None, None, "tensor"),
            P("section", None, "tensor"),
            P("section", None, "tensor"),
            P("section", None),
        ),
        check_vma=False,
    )
```

```python
import math

import jax
import jax.numpy as jnp
import numpy as np
from jax import lax
from jax.experimental import pallas as pl
from jax.experimental.pallas import tpu as pltpu
from jax.sharding import PartitionSpec as P

H = 16
HD = 64
EPS = 1e-05
BF = jnp.bfloat16
F32 = jnp.float32
VMEM_LIMIT = 62 * 1024 * 1024
ANY = pl.BlockSpec(memory_space=pl.ANY)
SMEM = pl.BlockSpec(memory_space=pltpu.SMEM)
WHOLE = pl.BlockSpec(memory_space=pltpu.VMEM)
NN = (((1,), (0,)), ((), ()))
NT = (((1,), (1,)), ((), ()))
TN = (((0,), (0,)), ((), ()))
CW = 256
PER = CW // HD


def dot(a, b, dims=NN):
    return lax.dot_general(a, b, dims, preferred_element_type=F32)


def arrived(ref, sem):
    pltpu.make_async_copy(ref, ref, sem).wait()


def call(kernel, inputs, outputs, scratch, chain, deps, name, flops, nbytes, turn, remote=False):
    pairs = [item if isinstance(item, tuple) else (item, ANY) for item in inputs]
    args = [p[0] for p in pairs]
    specs = [p[1] for p in pairs]
    n_in = len(args)
    aliases = {}
    if chain is not None:
        for buffer, index in zip(chain, [index for index, item in enumerate(outputs) if item[2]]):
            aliases[len(args)] = index
            args.append(buffer)
            specs.append(ANY)
    args += deps
    specs += [ANY] * len(deps)
    n_args, n_out = len(args), len(outputs)
    params = {"collective_id": 3, "has_side_effects": True} if remote else {}

    def body(*refs):
        @pl.when(lax.axis_index("section") == turn)
        def _():
            kernel(refs[:n_in], refs[n_args : n_args + n_out], refs[n_args + n_out :])

    return pl.pallas_call(
        body,
        in_specs=specs,
        out_specs=[ANY] * n_out,
        out_shape=[jax.ShapeDtypeStruct(o[0], o[1]) for o in outputs],
        scratch_shapes=scratch,
        input_output_aliases=aliases,
        compiler_params=pltpu.CompilerParams(vmem_limit_bytes=VMEM_LIMIT, **params),
        cost_estimate=pl.CostEstimate(flops=flops, bytes_accessed=nbytes, transcendentals=0),
        name=name,
    )(*args)


NORM_SPECS = [WHOLE] * 4


def norm_rows(refs):
    out_bias, gain, shift, down_bias = refs
    rows = [out_bias[...], gain[0:1], shift[0:1], down_bias[...], gain[1:2], shift[1:2]]
    return [row.astype(F32) for row in rows]


def slope_of(table_ref, head):
    return table_ref[lax.axis_index("tensor") * (table_ref.shape[0] // 2) + head]


def pick(k, count, own, oth, make):
    @pl.when(k < count)
    def _():
        for src, dst, sem in make(own, k):
            pltpu.make_async_copy(src, dst, sem).start()

    @pl.when(k >= count)
    def _():
        for src, dst, sem in make(oth, k - count):
            pltpu.make_async_copy(src, dst, sem).start()


def block(index, size):
    return pl.ds(pl.multiple_of(index * size, size), size)


def copy(src, dst, sem):
    return pltpu.make_async_copy(src, dst, sem)


def fill_distance(dist_ref, length):
    rows = dist_ref.shape[0]
    keys = lax.broadcasted_iota(jnp.int32, (rows, rows), 0)
    places = lax.broadcasted_iota(jnp.int32, (rows, rows), 1)
    distance = jnp.abs(keys - places).astype(F32)
    dist_ref[...] = jnp.where(keys < length, distance, 1e12)


def normalize(v):
    mean = jnp.mean(v, axis=1, keepdims=True)
    centred = v - mean
    rstd = lax.rsqrt(jnp.mean(centred * centred, axis=1, keepdims=True) + EPS)
    return centred * rstd, rstd


def halves(rows):
    return [slice(0, rows // 2), slice(rows // 2, rows)]


class Forward:
    def __init__(self, rows, width, local, units):
        self.rows, self.width, self.local, self.units = rows, width, local, units
        self.ft = min(512, units)
        self.tiles = units // self.ft
        self.heads_steps = local // CW
        self.total = 2 * local

    def kept(self, slots):
        rows, width = self.rows, self.width
        shapes = [((slots, rows, self.total), BF)] * 4
        shapes += [((slots, 2 * self.heads_steps, 8, rows), F32)]
        shapes += [((slots, rows, 2 * self.units), BF)] * 3
        return shapes + [((slots, rows, width), BF)] * 3 + [((slots, rows, 128), F32)] * 2

    def scratch(self):
        rows, width, ft, total = self.rows, self.width, self.ft, self.total
        sem = pltpu.SemaphoreType.DMA
        return [
            pltpu.VMEM((rows, width), BF),
            pltpu.VMEM((2, 3, width, CW), BF),
            pltpu.VMEM((total, width), BF),
            pltpu.VMEM((2, 2, width, ft), BF),
            pltpu.VMEM((2, width, ft), BF),
            pltpu.VMEM((2, 3, rows, CW), BF),
            pltpu.VMEM((2, 8, rows), F32),
            pltpu.VMEM((rows, total), BF),
            pltpu.VMEM((rows, rows), F32),
            pltpu.VMEM((rows, width), F32),
            pltpu.VMEM((rows, width), F32),
            pltpu.VMEM((rows, width), BF),
            pltpu.VMEM((2, 3, rows, ft), BF),
            pltpu.VMEM((3, rows, width), BF),
            pltpu.VMEM((2, rows, 128), F32),
            sem, sem((2,)), sem((2,)), sem((2, 2)), sem((2, 4)), sem, sem((2, 3)), sem((6,)),
        ]

    def bind(self, x, weights, bias, up_bias, slopes, norms, slot, outs, scratch):
        self.x_hbm, self.weights, self.bias, self.up_bias, self.slopes, self.norms = x, weights, bias, up_bias, slopes, norms
        self.slot, self.outs = slot, outs
        (self.x, self.w, self.o, self.up, self.down, self.qkv, self.lse, self.mixed, self.dist, self.normed, self.acc,
         self.low, self.tile, self.row, self.stat, self.x_sem, self.w_sem, self.o_sem, self.f_sem, self.q_sem, self.m_sem,
         self.t_sem, self.r_sem) = scratch

    def start_x(self):
        copy(self.x_hbm, self.x, self.x_sem).start()

    def start_w(self, k):
        s = lax.rem(k, 2)
        pick(k, self.heads_steps, self.weights[0], self.weights[1],
             lambda ref, j: [(ref.at[:, :, block(j, CW)], self.w.at[s], self.w_sem.at[s])])

    def start_o(self, side):
        copy(self.weights[2 + side], self.o.at[pl.ds(side * self.local, self.local)], self.o_sem.at[side]).start()

    def start_f(self, k):
        s = lax.rem(k, 2)
        ft = self.ft
        pick(k, self.tiles, (self.weights[4], self.weights[6]), (self.weights[5], self.weights[7]),
             lambda ref, j: [(ref[0].at[:, :, block(j, ft)], self.up.at[s], self.f_sem.at[s, 0]),
                             (ref[1].at[:, block(j, ft)], self.down.at[s], self.f_sem.at[s, 1])])

    def write_qkv(self, i, s):
        cols = block(i, CW)
        return [copy(self.qkv.at[s, c], out.at[self.slot, :, cols], self.q_sem.at[s, c])
                for c, out in enumerate(self.outs[:3])] + [
            copy(self.lse.at[s], self.outs[4].at[self.slot, i], self.q_sem.at[s, 3])]

    def attention_step(self, i, ahead):
        s = lax.rem(i, 2)
        qkv = self.qkv
        arrived(self.w.at[s], self.w_sem.at[s])

        @pl.when(i >= 2)
        def _():
            for item in self.write_qkv(i - 2, s):
                item.wait()

        values = self.x[...]
        b = self.bias[:, block(i, CW)].astype(F32)
        qkv[s, 0] = (dot(values, self.w[s, 0]) + b[0:1]).astype(BF)
        qkv[s, 1] = dot(values, self.w[s, 1]).astype(BF)
        qkv[s, 2] = (dot(values, self.w[s, 2]) + b[1:2]).astype(BF)

        @pl.when(i + 2 < ahead)
        def _():
            self.start_w(i + 2)

        parts = []
        for head in range(PER):
            cols = slice(head * HD, (head + 1) * HD)
            query = qkv[s, 0, :, cols] * BF(1.0 / math.sqrt(HD))
            scores = dot(qkv[s, 1, :, cols], query, NT)
            scores = scores - self.dist[...] * slope_of(self.slopes, i * PER + head)
            top = jnp.max(scores, axis=0, keepdims=True)
            likely = jnp.exp(scores - top)
            mass = jnp.sum(likely, axis=0, keepdims=True)
            low = (likely * (1.0 / mass)).astype(BF)
            parts.append(dot(low, qkv[s, 2, :, cols], TN).astype(BF))
            self.lse[s, head : head + 1, :] = top + jnp.log(mass)
        self.mixed[:, block(i, CW)] = jnp.concatenate(parts, axis=1)
        for item in self.write_qkv(i, s):
            item.start()

    def middle(self):
        rows, width = self.rows, self.width
        copy(self.mixed, self.outs[3].at[self.slot], self.m_sem).start()
        for side in range(2):
            arrived(self.o.at[pl.ds(side * self.local, self.local)], self.o_sem.at[side])
        vec = norm_rows(self.norms)
        for rs in halves(rows):
            attended = dot(self.mixed[rs, :], self.o[...])
            u, rstd = normalize(self.x[rs, :].astype(F32) + attended + vec[0])
            normed = u * vec[1] + vec[2]
            self.normed[rs, :] = normed
            self.low[rs, :] = normed.astype(BF)
            self.row[0, rs, :] = u.astype(BF)
            self.stat[0, rs, :] = jnp.broadcast_to(rstd, (rows // 2, 128))
            self.acc[rs, :] = jnp.zeros((rows // 2, width), F32)
        for index, item in enumerate(self.first_rows()):
            copy(*item, self.r_sem.at[index]).start()

    def first_rows(self):
        return [(self.low, self.outs[8].at[self.slot]), (self.row.at[0], self.outs[9].at[self.slot]),
                (self.stat.at[0], self.outs[11].at[self.slot])]

    def write_tiles(self, i, s):
        return [copy(self.tile.at[s, c], out.at[self.slot, :, block(i, self.ft)], self.t_sem.at[s, c])
                for c, out in enumerate(self.outs[5:8])]

    def ffn_step(self, i, ahead):
        s = lax.rem(i, 2)
        arrived(self.up.at[s], self.f_sem.at[s, 0])
        arrived(self.down.at[s], self.f_sem.at[s, 1])

        @pl.when(i >= 2)
        def _():
            for item in self.write_tiles(i - 2, s):
                item.wait()

        b = self.up_bias[:, block(i, self.ft)].astype(F32)
        low = self.low[...]
        gate = dot(low, self.up[s, 0]) + b[0:1]
        lift = dot(low, self.up[s, 1]) + b[1:2]
        cdf = 0.5 * lax.erf(gate * (1.0 / math.sqrt(2.0))) + 0.5
        act = gate * cdf
        slope = cdf + gate * (jnp.exp(gate * gate * -0.5) * (1.0 / math.sqrt(2.0 * math.pi)))
        self.tile[s, 0] = act.astype(BF)
        self.tile[s, 1] = (lift * slope).astype(BF)
        hidden = (act * lift).astype(BF)
        self.tile[s, 2] = hidden
        self.acc[...] += dot(hidden, self.down[s], NT)

        @pl.when(i + 2 < ahead)
        def _():
            self.start_f(i + 2)

        for item in self.write_tiles(i, s):
            item.start()

    def finish(self, y_out):
        rows = self.rows
        vec = norm_rows(self.norms)
        for rs in halves(rows):
            u, rstd = normalize(self.normed[rs, :] + self.acc[rs, :] + vec[3])
            self.row[1, rs, :] = u.astype(BF)
            self.stat[1, rs, :] = jnp.broadcast_to(rstd, (rows // 2, 128))
            self.row[2, rs, :] = (u * vec[4] + vec[5]).astype(BF)
        ends = [(self.row.at[1], self.outs[10].at[self.slot]), (self.stat.at[1], self.outs[12].at[self.slot]),
                (self.row.at[2], y_out)]
        for index, item in enumerate(ends):
            copy(*item, self.r_sem.at[3 + index]).start()
        for index, item in enumerate(self.first_rows() + ends):
            copy(*item, self.r_sem.at[index]).wait()
        copy(self.mixed, self.outs[3].at[self.slot], self.m_sem).wait()
        for i in (2 * self.heads_steps - 2, 2 * self.heads_steps - 1):
            for item in self.write_qkv(jnp.int32(i), i % 2):
                item.wait()
        for i in (2 * self.tiles - 2, 2 * self.tiles - 1):
            for item in self.write_tiles(jnp.int32(i), i % 2):
                item.wait()

    def flops(self):
        rows, width, total = self.rows, self.width, self.total
        return 2 * rows * width * (4 * total + 6 * self.units) + 4 * rows * rows * total


def layer_forward(x, weights, biases, slopes, norms, lengths, m, turn, chain, deps, slots):
    rows, width = x.shape
    step = Forward(rows, width, weights[0].shape[2], weights[4].shape[2])

    def kernel(ins, outs, scratch):
        lengths_ref = ins[0]
        step.bind(ins[1], ins[2:10], ins[10], ins[11], ins[12], ins[13:17], m, outs[:13], scratch)
        step.start_x()
        for k in range(2):
            step.start_w(jnp.int32(k))
        for side in range(2):
            step.start_o(side)
        for k in range(2):
            step.start_f(jnp.int32(k))
        fill_distance(step.dist, lengths_ref[lax.axis_index("tensor") * slots + m])
        arrived(step.x, step.x_sem)

        @pl.loop(0, 2 * step.heads_steps)
        def _(i):
            step.attention_step(i, 2 * step.heads_steps)

        step.middle()

        @pl.loop(0, 2 * step.tiles)
        def _(i):
            step.ffn_step(i, 2 * step.tiles)

        step.finish(outs[13])

    return call(
        kernel,
        [(lengths, SMEM), x, *weights, *zip(biases, [WHOLE] * 2), (slopes, SMEM), *zip(norms, NORM_SPECS)],
        [shape + (True,) for shape in step.kept(slots)] + [((rows, width), BF, False)],
        step.scratch(),
        chain,
        deps,
        "layer_forward",
        step.flops(),
        54 << 20,
        turn,
    )


def layer_backward(grad, kept, weights, slopes, norms, lengths, m, turn, chain, deps, slots, sent=()):
    qkv_own, qkv_oth, o_own, o_oth, up_own, up_oth, down_own, down_oth = weights
    q, k, v, _, lse, act, slope, _, _, u1, u2, r1, r2 = kept
    rows, width = grad.shape
    local = qkv_own.shape[2]
    units = up_own.shape[2]
    heads_steps = local // CW
    ft = min(512, units)
    tiles = units // ft
    total = 2 * local

    def norm_back(grad_z, u, rstd, gain):
        t = grad_z * gain
        return rstd * (t - jnp.mean(t, axis=1, keepdims=True) - u * jnp.mean(t * u, axis=1, keepdims=True))

    def row_sum(values):
        return jnp.sum(values, axis=0, keepdims=True)

    def kernel(ins, outs, scratch):
        (lengths_ref, g_hbm, q_hbm, k_hbm, v_hbm, lse_hbm, a_hbm, b_hbm, u1_hbm, u2_hbm, r1_hbm, r2_hbm,
         qkv_own_ref, qkv_oth_ref, o_own_ref, o_oth_ref, up_own_ref, up_oth_ref, down_own_ref, down_oth_ref,
         slope_ref) = ins[:21]
        gg0_out, gg1_out, gl_out, ga_out, gq_out, gk_out, gv_out, gx_out, gxl_out, sums_out, ub_out, qv_out = outs[:12]
        (g_ref, u_ref, r_ref, up_ref, down_ref, ab_ref, gg_ref, low_ref, acc_ref, sums_ref, ub_ref, qv_ref,
         w_ref, o_ref, qkv_ref, lse_ref, gm_ref, dist_ref, gqkv_ref,
         g_sem, f_sem, t_sem, w_sem, q_sem, r_sem, x_send, x_recv) = scratch
        slot = m
        t = lax.axis_index("tensor")
        length = lengths_ref[t * slots + m]
        travelling = []
        if sent:
            cross = {"tensor": 1 - t}
            barrier = pltpu.get_barrier_semaphore()
            pl.semaphore_signal(barrier, inc=1, device_id=cross, device_id_type=pl.DeviceIdType.MESH)
            pl.semaphore_wait(barrier, 1)
            for index in range(len(sent)):
                travelling.append(
                    pltpu.make_async_remote_copy(
                        src_ref=ins[25 + index].at[block(1 - t, rows // 2)], dst_ref=outs[12].at[index],
                        send_sem=x_send.at[index], recv_sem=x_recv.at[index],
                        device_id=cross, device_id_type=pl.DeviceIdType.MESH,
                    )
                )
                travelling[-1].start()

        def start_f(i):
            s = lax.rem(i, 2)
            pick(i, tiles, (up_own_ref, down_own_ref), (up_oth_ref, down_oth_ref),
                 lambda ref, j: [(ref[0].at[:, :, block(j, ft)], up_ref.at[s], f_sem.at[s, 0]),
                                 (ref[1].at[:, block(j, ft)], down_ref.at[s], f_sem.at[s, 1])])
            for c, ref in enumerate((a_hbm, b_hbm)):
                copy(ref.at[slot, :, block(i, ft)], ab_ref.at[s, c], f_sem.at[s, 2 + c]).start()

        def start_w(i):
            s = lax.rem(i, 2)
            pick(i, heads_steps, (qkv_own_ref, o_own_ref), (qkv_oth_ref, o_oth_ref),
                 lambda ref, j: [(ref[0].at[:, :, block(j, CW)], w_ref.at[s], w_sem.at[s, 0]),
                                 (ref[1].at[block(j, CW)], o_ref.at[s], w_sem.at[s, 1])])
            for c, ref in enumerate((q_hbm, k_hbm, v_hbm)):
                copy(ref.at[slot, :, block(i, CW)], qkv_ref.at[s, c], w_sem.at[s, 2 + c]).start()
            copy(lse_hbm.at[slot, i], lse_ref.at[s], w_sem.at[s, 5]).start()

        firsts = [(g_hbm, g_ref), (u2_hbm.at[slot], u_ref.at[1]), (r2_hbm.at[slot], r_ref.at[1]),
                  (u1_hbm.at[slot], u_ref.at[0]), (r1_hbm.at[slot], r_ref.at[0])]
        for index, (src, dst) in enumerate(firsts):
            copy(src, dst, g_sem.at[index]).start()
            if index == 2:
                start_f(jnp.int32(0))
                start_f(jnp.int32(1))
        start_w(jnp.int32(0))
        start_w(jnp.int32(1))
        vec = norm_rows(ins[21:25])
        fill_distance(dist_ref, length)
        for index, (src, dst) in enumerate(firsts[:3]):
            copy(src, dst, g_sem.at[index]).wait()
        sums = [jnp.zeros((1, width), F32)] * 3
        for rs in halves(rows):
            grad_y = g_ref[rs, :].astype(F32)
            if turn == 1:
                places = lax.broadcasted_iota(jnp.int32, (rows // 2, width), 0) + rs.start
                grad_y = jnp.where(places < length, grad_y, 0.0)
            u = u_ref[1, rs, :].astype(F32)
            grad_c = norm_back(grad_y, u, r_ref[1, rs, 0:1], vec[4])
            acc_ref[rs, :] = grad_c
            low_ref[0, rs, :] = grad_c.astype(BF)
            for index, values in enumerate((grad_y * u, grad_y, grad_c)):
                sums[index] += row_sum(values)
        for index in range(3):
            sums_ref[index : index + 1, :] = sums[index]
        copy(low_ref.at[0], gl_out.at[slot], r_sem.at[0]).start()

        def write_tiles(i, s):
            return [copy(gg_ref.at[s, c], out.at[slot, :, block(i, ft)], t_sem.at[s, c])
                    for c, out in enumerate((gg0_out, gg1_out))]

        @pl.loop(0, 2 * tiles)
        def _(i):
            s = lax.rem(i, 2)
            arrived(up_ref.at[s], f_sem.at[s, 0])
            arrived(down_ref.at[s], f_sem.at[s, 1])
            for c in range(2):
                arrived(ab_ref.at[s, c], f_sem.at[s, 2 + c])

            @pl.when(i >= 2)
            def _():
                for item in write_tiles(i - 2, s):
                    item.wait()

            gh = dot(low_ref[0], down_ref[s])
            g0 = (gh * ab_ref[s, 1].astype(F32)).astype(BF)
            g1 = (gh * ab_ref[s, 0].astype(F32)).astype(BF)
            gg_ref[s, 0] = g0
            gg_ref[s, 1] = g1
            ub_ref[0:1, block(i, ft)] = row_sum(g0.astype(F32))
            ub_ref[1:2, block(i, ft)] = row_sum(g1.astype(F32))
            acc_ref[...] += dot(g0, up_ref[s, 0], NT) + dot(g1, up_ref[s, 1], NT)

            @pl.when(i + 2 < 2 * tiles)
            def _():
                start_f(i + 2)

            for item in write_tiles(i, s):
                item.start()

        for index, (src, dst) in enumerate(firsts[3:]):
            copy(src, dst, g_sem.at[3 + index]).wait()
        sums = [jnp.zeros((1, width), F32)] * 3
        for rs in halves(rows):
            grad_n = acc_ref[rs, :]
            u = u_ref[0, rs, :].astype(F32)
            grad_a = norm_back(grad_n, u, r_ref[0, rs, 0:1], vec[1])
            low_ref[1, rs, :] = grad_a.astype(BF)
            acc_ref[rs, :] = grad_a
            for index, values in enumerate((grad_n * u, grad_n, grad_a)):
                sums[index] += row_sum(values)
        for index in range(3):
            sums_ref[3 + index : 4 + index, :] = sums[index]
        sums_ref[6:8, :] = jnp.zeros((2, width), F32)
        copy(low_ref.at[1], ga_out.at[slot], r_sem.at[1]).start()
        scale = BF(1.0 / math.sqrt(HD))

        def write_heads(i, s):
            return [copy(gqkv_ref.at[s, c], out.at[slot, :, block(i, CW)], q_sem.at[s, c])
                    for c, out in enumerate((gq_out, gk_out, gv_out))]

        @pl.loop(0, 2 * heads_steps)
        def _(i):
            s = lax.rem(i, 2)
            for index, ref in enumerate((w_ref.at[s], o_ref.at[s], qkv_ref.at[s, 0], qkv_ref.at[s, 1], qkv_ref.at[s, 2], lse_ref.at[s])):
                arrived(ref, w_sem.at[s, index])

            @pl.when(i >= 2)
            def _():
                for item in write_heads(i - 2, s):
                    item.wait()

            gm_ref[...] = dot(low_ref[1], o_ref[s], NT).astype(BF)
            parts = [[], [], []]
            for head in range(PER):
                cols = slice(head * HD, (head + 1) * HD)
                query = qkv_ref[s, 0, :, cols] * scale
                key = qkv_ref[s, 1, :, cols]
                gm = gm_ref[:, cols]
                scores = dot(key, query, NT)
                scores = scores - dist_ref[...] * slope_of(slope_ref, i * PER + head)
                likely = jnp.exp(scores - lse_ref[s, head : head + 1, :])
                parts[2].append(dot(likely.astype(BF), gm).astype(BF))
                t = likely * dot(qkv_ref[s, 2, :, cols], gm, NT)
                inner = jnp.sum(t, axis=0, keepdims=True)
                gs = (t - likely * inner).astype(BF)
                parts[1].append(dot(gs, query).astype(BF))
                parts[0].append(dot(gs, key * scale, TN).astype(BF))
            for c in range(3):
                gqkv_ref[s, c] = jnp.concatenate(parts[c], axis=1)
            for index, c in enumerate((0, 2)):
                qv_ref[index : index + 1, block(i, CW)] = row_sum(gqkv_ref[s, c].astype(F32))
            acc_ref[...] += (
                dot(gqkv_ref[s, 0], w_ref[s, 0], NT)
                + dot(gqkv_ref[s, 1], w_ref[s, 1], NT)
                + dot(gqkv_ref[s, 2], w_ref[s, 2], NT)
            )

            @pl.when(i + 2 < 2 * heads_steps)
            def _():
                start_w(i + 2)

            for item in write_heads(i, s):
                item.start()

        g_ref[...] = acc_ref[...].astype(BF)
        ends = [(g_ref, gxl_out), (acc_ref, gx_out), (sums_ref, sums_out), (ub_ref, ub_out), (qv_ref, qv_out)]
        for index, (src, dst) in enumerate(ends):
            copy(src, dst, r_sem.at[2 + index]).start()
        for index, (src, dst) in enumerate([(low_ref.at[0], gl_out.at[slot]), (low_ref.at[1], ga_out.at[slot])] + ends):
            copy(src, dst, r_sem.at[index]).wait()
        for i in (2 * tiles - 2, 2 * tiles - 1):
            for item in write_tiles(jnp.int32(i), i % 2):
                item.wait()
        for i in (2 * heads_steps - 2, 2 * heads_steps - 1):
            for item in write_heads(jnp.int32(i), i % 2):
                item.wait()
        for item in travelling:
            item.wait()

    sem = pltpu.SemaphoreType.DMA
    return call(
        kernel,
        [(lengths, SMEM), grad, q, k, v, lse, act, slope, u1, u2, r1, r2, *weights, (slopes, SMEM), *zip(norms, NORM_SPECS), *sent],
        [((slots, rows, 2 * units), BF, True)] * 2
        + [((slots, rows, width), BF, True)] * 2
        + [((slots, rows, total), BF, True)] * 3
        + [
            ((rows, width), F32, False),
            ((rows, width), BF, False),
            ((8, width), F32, False),
            ((2, 2 * units), F32, False),
            ((2, total), F32, False),
        ]
        + ([((len(sent), rows // 2, width), BF, False)] if sent else []),
        [
            pltpu.VMEM((rows, width), BF),
            pltpu.VMEM((2, rows, width), BF),
            pltpu.VMEM((2, rows, 128), F32),
            pltpu.VMEM((2, 2, width, ft), BF),
            pltpu.VMEM((2, width, ft), BF),
            pltpu.VMEM((2, 2, rows, ft), BF),
            pltpu.VMEM((2, 2, rows, ft), BF),
            pltpu.VMEM((2, rows, width), BF),
            pltpu.VMEM((rows, width), F32),
            pltpu.VMEM((8, width), F32),
            pltpu.VMEM((2, 2 * units), F32),
            pltpu.VMEM((2, total), F32),
            pltpu.VMEM((2, 3, width, CW), BF),
            pltpu.VMEM((2, CW, width), BF),
            pltpu.VMEM((2, 3, rows, CW), BF),
            pltpu.VMEM((2, 8, rows), F32),
            pltpu.VMEM((rows, CW), BF),
            pltpu.VMEM((rows, rows), F32),
            pltpu.VMEM((2, 3, rows, CW), BF),
            sem((5,)), sem((2, 4)), sem((2, 2)), sem((2, 6)), sem((2, 3)), sem((7,)), sem((4,)), sem((4,)),
        ],
        chain,
        deps,
        "layer_backward",
        2 * rows * width * (4 * total + 6 * units) + 10 * rows * rows * total,
        70 << 20,
        turn,
        bool(sent),
    )


MESH = pl.DeviceIdType.MESH
CORE_LAG = 3
CROSS_LAG = 3
CHAIN_LAG = 2


def neighbours():
    t = lax.axis_index("tensor")
    d = lax.axis_index("dp")
    last = lax.axis_size("dp") // 2 - 1
    c = lax.rem(d, 2)
    z = d // 2
    return t, c, z, last, {"dp": d + 1 - 2 * c}, {"tensor": 1 - t}, {"dp": d + 2}, {"dp": d - 2}


def greet(c, z, chips, core, cross):
    barrier = pltpu.get_barrier_semaphore()
    pl.semaphore_signal(barrier, inc=1, device_id=core, device_id_type=MESH)
    pl.semaphore_signal(barrier, inc=1, device_id=cross, device_id_type=MESH)
    for shift in range(1, chips):
        chip = lax.rem(z + shift, chips)
        pl.semaphore_signal(barrier, inc=1, device_id={"dp": chip * 2 + c}, device_id_type=MESH)
    pl.semaphore_wait(barrier, 1 + chips)


def fetch_and_forward(weights, biases, inputs, cotangent, slopes, norms, lengths, chips, slots):
    seqs = inputs.shape[0] // 2
    shard_rows, width = inputs.shape[1:]
    rows = 2 * shard_rows
    groups = 2 * chips
    qkv, out, up, down = weights
    local, units = qkv.shape[2], up.shape[2]
    step = Forward(rows, width, local, units)
    ft, tiles = step.ft, step.tiles
    bias_widths = [b.shape[1] for b in biases]
    QKV, OUT, UP, DOWN, ROWS, BIAS = range(6)

    plan = [(UP, 0, groups), (ROWS, 0, 0), (BIAS, 0, 0), (BIAS, 1, 0)]
    for part in range(1, tiles):
        plan.append((UP, part, groups))
        if part <= 3:
            plan.append((QKV, part - 1, 2))
    plan += [(DOWN, 0, groups), (OUT, 0, 2)]
    plan += [(DOWN, part, groups) for part in range(1, tiles - 1)]
    plan += [(DOWN, tiles - 1, 2)]
    plan += [(ROWS, part, 0) for part in range(1, seqs)]
    n = len(plan)
    number = {item[:2]: index for index, item in enumerate(plan)}

    def size(index):
        kind, part, pieces = plan[index]
        whole = {QKV: width * local, OUT: local * width, UP: 2 * width * ft, DOWN: width * ft, ROWS: shard_rows * width, BIAS: 64}
        return whole[kind] / max(1, pieces)

    events, clock, busy = [], 0.0, 0.0
    for index, (kind, part, pieces) in enumerate(plan):
        clock += size(index)
        events.append((clock, index, 0))
        if pieces == groups:
            start = max(clock, busy)
            busy = start + size(index) * (chips - 1)
            events += [(start + size(index) * hop * 1.001, index, hop) for hop in range(1, chips)]
    events.sort()
    when = {event[1:]: event[0] for event in events}

    def ready(*keys):
        return max(when[key] for k in keys for key in when if key[0] == number[k])

    needs = [[(ROWS, 0), (BIAS, 0)], []] + [[(QKV, part) for part in range(3)], []] + [[(OUT, 0), (BIAS, 1)]]
    needs += [[] for _ in range(tiles - 1)]
    needs += [[(UP, part), (DOWN, part)] for part in range(tiles)] + [[]]
    assert step.heads_steps == 2
    rounds, taken = [], 0
    for need in needs:
        mine = []
        if need:
            limit = ready(*need)
            while taken < len(events) and events[taken][0] <= limit:
                mine.append(events[taken][1:])
                taken += 1
        rounds.append((mine, need))
    rest = [event[1:] for event in events[taken:]]
    n_rounds = len(rounds)
    n_kept = len(step.kept(slots))

    def kernel(*refs):
        lengths_ref, slope_ref, norm_refs = refs[0], refs[1], refs[2:6]
        refs = refs[6:]
        ins, bias_ins, held_refs = refs[:4], refs[4:6], refs[6:8]
        outs, bias_outs, row_refs = refs[8:12], refs[12:14], refs[14 : 14 + seqs]
        kept_refs = refs[14 + seqs : 14 + seqs + n_kept]
        y_ref = refs[14 + seqs + n_kept]
        stage, qv_bias, ub_bias, x_send, x_recv, c_send, c_recv, u_send, u_recv, d_send, d_recv, l_sem, b_sem = refs[
            15 + seqs + n_kept : 28 + seqs + n_kept
        ]
        t, c, z, last, core, cross, above, below = neighbours()
        section = lax.axis_index("section")
        greet(c, z, chips, core, cross)
        paired = [item for pair in zip(ins, outs) for item in pair]
        step.bind(
            row_refs[0], paired, qv_bias, ub_bias, slope_ref, norm_refs, 0, kept_refs, refs[28 + seqs + n_kept :]
        )

        def span(part):
            return block(part, shard_rows)

        def bias_part(m, side):
            return bias_outs[m].at[:, pl.ds(side * bias_widths[m], bias_widths[m])]

        def piece(side, index, chip, on):
            kind, part, pieces = plan[index]
            place = chip * 2 + on if pieces == groups else on
            ref = (ins, outs)[side][kind]
            if kind == QKV:
                return ref.at[part, block(place, width // pieces)]
            if kind == OUT:
                return ref.at[block(place, local // pieces)]
            cols = pl.ds(part * ft, ft)
            if kind == DOWN:
                return ref.at[block(place, width // pieces), cols]
            per = pieces // 2
            return ref.at[place // per, block(lax.rem(place, per), width // per), cols]

        def cross_copy(index, held_ref=None):
            kind, m, pieces = plan[index]
            if kind == ROWS:
                src = (held_refs[0] if held_ref is None else held_ref).at[(1 - t) * seqs + m]
                dst = row_refs[m].at[span(t)]
            elif kind == BIAS:
                src, dst = bias_ins[m], bias_part(m, 1)
            else:
                src, dst = piece(0, index, z, c), piece(1, index, z, c)
            return pltpu.make_async_remote_copy(
                src_ref=src, dst_ref=dst, send_sem=x_send.at[index], recv_sem=x_recv.at[index],
                device_id=cross, device_id_type=MESH,
            )

        def pass_on(index, chip, send, recv, device):
            place = piece(1, index, chip, c)
            return pltpu.make_async_remote_copy(
                src_ref=place, dst_ref=place, send_sem=send.at[index, chip], recv_sem=recv.at[index, chip],
                device_id=device, device_id_type=MESH,
            )

        def got(index, chip, on, sem):
            arrived(piece(1, index, chip, on), sem)

        for m in range(2):
            copy(bias_ins[m], bias_part(m, 0), b_sem.at[m]).start()
        for index in range(n):
            if plan[index][0] == ROWS:
                for turn in range(2):
                    @pl.when(section == turn)
                    def _(index=index, turn=turn):
                        cross_copy(index, held_refs[turn]).start()
            else:
                cross_copy(index).start()
        for turn in range(2):
            @pl.when(section == turn)
            def _(turn=turn):
                copy(held_refs[turn].at[pl.ds(t * seqs, seqs)], stage, l_sem.at[0]).start()

        @pl.when(section == 0)
        def _():
            for k in range(2):
                step.start_w(jnp.int32(k))
            step.start_o(0)
            for k in range(2):
                step.start_f(jnp.int32(k))
            fill_distance(step.dist, lengths_ref[t * seqs])

        arrived(stage, l_sem.at[0])
        for m in range(seqs):
            copy(stage.at[m], row_refs[m].at[span(t)], l_sem.at[m]).start()
        for m in range(seqs):
            arrived(stage.at[m], l_sem.at[m])
        for m in range(2):
            copy(bias_ins[m], bias_part(m, 0), b_sem.at[m]).wait()

        def handle(index, hop):
            kind, m, pieces = plan[index]
            if kind == ROWS:
                arrived(row_refs[m].at[span(1 - t)], x_recv.at[index])
            elif kind == BIAS:
                arrived(bias_part(m, 1), x_recv.at[index])
            elif hop == 0:
                got(index, z, c, x_recv.at[index])
                if pieces == groups:
                    @pl.when(z < last)
                    def _():
                        pass_on(index, z, u_send, u_recv, above).start()

                    @pl.when(z > 0)
                    def _():
                        pass_on(index, z, d_send, d_recv, below).start()

                pass_on(index, z, c_send, c_recv, core).start()
            else:
                @pl.when(z - hop >= 0)
                def _():
                    got(index, z - hop, c, u_recv.at[index, z - hop])

                    @pl.when(z < last)
                    def _():
                        pass_on(index, z - hop, u_send, u_recv, above).start()

                    pass_on(index, z - hop, c_send, c_recv, core).start()

                @pl.when(z + hop <= last)
                def _():
                    got(index, z + hop, c, d_recv.at[index, z + hop])

                    @pl.when(z > 0)
                    def _():
                        pass_on(index, z + hop, d_send, d_recv, below).start()

                    pass_on(index, z + hop, c_send, c_recv, core).start()

        def from_core(key):
            index = number[key]
            kind, m, pieces = plan[index]
            if pieces == groups:
                for chip in range(chips):
                    got(index, chip, 1 - c, c_recv.at[index, chip])
            elif pieces:
                got(index, z, 1 - c, c_recv.at[index, z])

        @pl.loop(0, n_rounds)
        def _(tau):
            for number_, (mine, need) in enumerate(rounds):
                if not (mine or need):
                    continue

                @pl.when(tau == number_)
                def _(number_=number_, mine=mine, need=need):
                    for index, hop in mine:
                        handle(index, hop)
                    for key in need:
                        from_core(key)
                    for key in need:
                        if key == (BIAS, 0):
                            @pl.when(section == 0)
                            def _():
                                step.start_x()
                                copy(bias_outs[0], qv_bias, b_sem.at[0]).start()
                                copy(bias_outs[0], qv_bias, b_sem.at[0]).wait()
                                arrived(step.x, step.x_sem)
                        elif key == (QKV, 2):
                            @pl.when(section == 0)
                            def _():
                                for k in range(2, 4):
                                    step.start_w(jnp.int32(k))
                        elif key == (OUT, 0):
                            @pl.when(section == 0)
                            def _():
                                step.start_o(1)
                        elif key == (BIAS, 1):
                            @pl.when(section == 0)
                            def _():
                                copy(bias_outs[1], ub_bias, b_sem.at[1]).start()
                                copy(bias_outs[1], ub_bias, b_sem.at[1]).wait()
                        elif key[0] == DOWN:
                            @pl.when(section == 0)
                            def _(key=key):
                                step.start_f(jnp.int32(tiles + key[1]))

            @pl.when(section == 0)
            def _():
                @pl.when(tau < 4)
                def _():
                    step.attention_step(tau, 2)

                @pl.when(tau == 4)
                def _():
                    step.middle()

                @pl.when(tau > 4)
                def _():
                    step.ffn_step(tau - 5, tiles)

        @pl.when(section == 0)
        def _():
            step.finish(y_ref)

        for index, hop in rest:
            handle(index, hop)
        for index in range(n):
            kind, part, pieces = plan[index]
            cross_copy(index).wait_send()
            if pieces == 2:
                pass_on(index, z, c_send, c_recv, core).wait_send()
            if pieces != groups:
                continue
            for chip in range(chips):
                pass_on(index, chip, c_send, c_recv, core).wait_send()

                @pl.when((chip <= z) & (z < last))
                def _(chip=chip):
                    pass_on(index, chip, u_send, u_recv, above).wait_send()

                @pl.when((chip >= z) & (z > 0))
                def _(chip=chip):
                    pass_on(index, chip, d_send, d_recv, below).wait_send()

    sem = pltpu.SemaphoreType.DMA
    return pl.pallas_call(
        kernel,
        in_specs=[SMEM, SMEM] + NORM_SPECS + [ANY] * 8,
        out_specs=[ANY] * (7 + seqs + n_kept),
        out_shape=[jax.ShapeDtypeStruct(w.shape, BF) for w in weights]
        + [jax.ShapeDtypeStruct((2, 2 * size_), BF) for size_ in bias_widths]
        + [jax.ShapeDtypeStruct((rows, width), BF)] * seqs
        + [jax.ShapeDtypeStruct(*shape) for shape in step.kept(slots)]
        + [jax.ShapeDtypeStruct((rows, width), BF)],
        scratch_shapes=[pltpu.VMEM((seqs, shard_rows, width), BF)]
        + [pltpu.VMEM((2, 2 * size_), BF) for size_ in bias_widths]
        + [sem((n,)), sem((n,))]
        + [sem((n, chips))] * 6
        + [sem((seqs,)), sem((2,))]
        + step.scratch(),
        compiler_params=pltpu.CompilerParams(collective_id=1, has_side_effects=True, vmem_limit_bytes=VMEM_LIMIT),
        cost_estimate=pl.CostEstimate(flops=step.flops(), bytes_accessed=90 << 20, transcendentals=0),
        name="fetch_and_forward",
    )(lengths, slopes, *norms, *weights, *biases, inputs, cotangent)


def norm_back(grad_z, u, rstd, gain):
    t = grad_z * gain
    return rstd * (t - jnp.mean(t, axis=1, keepdims=True) - u * jnp.mean(t * u, axis=1, keepdims=True))


def row_sum(values):
    return jnp.sum(values, axis=0, keepdims=True)


def backward_and_reduce(grad, kept, back, x_all, weights, slopes, norms, lengths, sums, low_grad, second, chips):
    q, k_, v, mixed_all, lse, act, slope, hidden_all, normed_all, u1, u2, r1, r2 = kept
    gg0, gg1, gl, ga, gq, gk, gv = back
    rows, width = grad.shape
    local, units = weights[0].shape[2], weights[4].shape[2]
    ft = CW
    tiles = units // ft
    heads_steps = local // CW
    seqs = 2
    bt = 128
    lefts = [gl, normed_all, x_all, ga]
    rights = [hidden_all, gg0, gg1, gq, gk, gv, mixed_all]
    group_of = [0, 1, 1, 2, 2, 2, 3]
    member_of = [0, 0, 1, 0, 1, 2, 0]
    half = width // 2
    quarter = half // 2
    per_pair = 2 * ft // bt
    pairs = tiles // 2
    ffn_blocks = 3 * per_pair * pairs
    head_blocks = local // bt
    total = ffn_blocks + 4 * head_blocks
    ring, mines, gives = 4, CORE_LAG + 1, 4
    ahead_of = 4
    drain = CORE_LAG + CROSS_LAG + 2 * (chips - 1) * CHAIN_LAG + 1
    shard_rows = rows // 2
    norm_at = 2 * tiles
    head_at = norm_at + 1
    end_at = head_at + 5 * 2 * heads_steps
    x_flip, ga_flip = ffn_blocks - per_pair, ffn_blocks + per_pair
    up_rows = units // width
    vec_shape = (6 + 4 * up_rows + 2, width)
    assert ahead_of + ffn_blocks - ring > end_at

    def kernel(*refs):
        lengths_ref, slope_ref, norm_refs, sum_refs = refs[0], refs[1], refs[2:6], refs[6:15]
        refs = refs[12:]
        g_hbm, q_hbm, k_hbm, v_hbm, lse_hbm, a_hbm, b_hbm, u1_hbm, u2_hbm, r1_hbm, r2_hbm = refs[3:14]
        (qkv_own_ref, qkv_oth_ref, o_own_ref, o_oth_ref, up_own_ref, up_oth_ref, down_own_ref, down_oth_ref) = refs[14:22]
        left_refs, right_refs = refs[22:26], refs[26:33]
        low_grad_ref, second_ref = refs[33:35]
        outs, sums_out, rows_out = refs[35:39], refs[39], refs[40]
        fresh = refs[41:46]
        gx_out, gxl_out = refs[46:48]
        (
            acc, from_x, from_z, flip, stage, tile, mine, give, vec, vec_in, vec_all,
            g_ref, u_ref, r_ref, low_ref, gacc_ref, w_ref, o_ref, qkv_ref, gqkv_ref, lse_ref, gm_ref, gs_ref, dist_ref,
            part_sums, ub_sums, qv_sums,
            tile_sem, stage_sem, give_send, core_recv, x_send, x_recv, z_send, z_recv, f_send, f_recv,
            store_sem, out_send, out_recv, v_send, v_recv, r_send, r_recv,
            g_sem, w_sem, t_sem, e_sem,
        ) = refs[48:]
        final = from_x
        t, c, z, last, core, cross, above, below = neighbours()
        section = lax.axis_index("section")
        first = section == 0
        greet(c, z, chips, core, cross)
        fresh_of = {1: fresh[0].at[0], 2: fresh[1].at[0], 3: fresh[2], 4: fresh[3], 5: fresh[4]}
        vec_w = norm_rows(norm_refs)

        def remote(src, dst, send, recv, device):
            return pltpu.make_async_remote_copy(
                src_ref=src, dst_ref=dst, send_sem=send, recv_sem=recv, device_id=device, device_id_type=MESH
            )

        def valid(k):
            return (k >= 0) & (k < total)

        def member(k, visit):
            for m in range(3):
                @pl.when((k < ffn_blocks) & (lax.rem(k, 3 * per_pair) // per_pair == m))
                def _(m=m):
                    visit(m, k // (3 * per_pair) * per_pair + lax.rem(k, per_pair))

            for m in range(3, 7):
                base = ffn_blocks + (m - 3) * head_blocks

                @pl.when((k >= base) & (k < base + head_blocks))
                def _(m=m, base=base):
                    visit(m, k - base)

        def load_tile(k):
            at = lax.rem(k, ring)

            def visit(m, j):
                count = right_refs[m].shape[2] // (2 * bt)
                for side in range(2):
                    cols = block(side * count + j, bt)
                    where = pl.ds(side * bt, bt)
                    copy(right_refs[m].at[0, :, cols], tile.at[at, 0, :, where], tile_sem.at[at]).start()
                    if m not in fresh_of:
                        copy(right_refs[m].at[1, :, cols], tile.at[at, 1, :, where], tile_sem.at[at]).start()
                        continue

                    @pl.when(first)
                    def _(cols=cols, where=where):
                        copy(fresh_of[m].at[:, cols], tile.at[at, 1, :, where], tile_sem.at[at]).start()

                    @pl.when(section == 1)
                    def _(cols=cols, where=where):
                        copy(right_refs[m].at[1, :, cols], tile.at[at, 1, :, where], tile_sem.at[at]).start()

            member(k, visit)

        def take_left(g, at, mine_low):
            copy(left_refs[g].at[0], stage.at[0], stage_sem.at[0]).start()
            if mine_low is None:
                copy(left_refs[g].at[1], stage.at[1], stage_sem.at[1]).start()
                arrived(stage.at[1], stage_sem.at[1])
            else:
                @pl.when(first)
                def _():
                    stage[1] = low_ref[mine_low]

                @pl.when(section == 1)
                def _():
                    copy(left_refs[g].at[1], stage.at[1], stage_sem.at[1]).start()
                    arrived(stage.at[1], stage_sem.at[1])

            arrived(stage.at[0], stage_sem.at[0])
            for m in range(seqs):
                flip[at, :, m * rows : (m + 1) * rows] = stage[m].T

        def place_of(u):
            within = lax.rem(u, 4)
            side = within // 2
            return side, u // 4 * 2 + lax.rem(within, 2)

        def start_f(u):
            at = lax.rem(u, 2)
            side, j = place_of(u)
            pick(side * tiles + j, tiles, (up_own_ref, down_own_ref), (up_oth_ref, down_oth_ref),
                 lambda ref, jj: [(ref[0].at[:, :, block(jj, ft)], w_ref.at[at, pl.ds(0, 2)], w_sem.at[at, 0]),
                                  (ref[1].at[:, block(jj, ft)], w_ref.at[at, 2], w_sem.at[at, 1])])
            for n, ref in enumerate((a_hbm, b_hbm)):
                copy(ref.at[1, :, block(side * tiles + j, ft)], qkv_ref.at[at, n], w_sem.at[at, 2 + n]).start()

        def write_tile(u):
            at = lax.rem(u, 2)
            side, j = place_of(u)
            return [copy(gqkv_ref.at[at, n], fresh[n].at[0, :, block(side * tiles + j, ft)], t_sem.at[at, n]) for n in range(2)]

        def start_w(i):
            at = lax.rem(i, 2)
            pick(i, heads_steps, (qkv_own_ref, o_own_ref), (qkv_oth_ref, o_oth_ref),
                 lambda ref, j: [(ref[0].at[:, :, block(j, CW)], w_ref.at[at], w_sem.at[at, 0]),
                                 (ref[1].at[block(j, CW)], o_ref.at[at], w_sem.at[at, 1])])
            for n, ref in enumerate((q_hbm, k_hbm, v_hbm)):
                copy(ref.at[1, :, block(i, CW)], qkv_ref.at[at, n], w_sem.at[at, 2 + n]).start()
            copy(lse_hbm.at[1, i], lse_ref.at[at], w_sem.at[at, 5]).start()

        def write_heads(i):
            at = lax.rem(i, 2)
            return [copy(gqkv_ref.at[at, n], fresh[2 + n].at[:, block(i, CW)], t_sem.at[at, n]) for n in range(3)]

        def norm_load(index, u_hbm, r_hbm):
            return [copy(u_hbm.at[1], u_ref, g_sem.at[index]), copy(r_hbm.at[1], r_ref, g_sem.at[index + 1])]

        def begin():
            copy(g_hbm, g_ref, g_sem.at[0]).start()
            for item in norm_load(1, u2_hbm, r2_hbm):
                item.start()
            start_f(jnp.int32(0))
            start_f(jnp.int32(1))
            copy(g_hbm, g_ref, g_sem.at[0]).wait()
            for item in norm_load(1, u2_hbm, r2_hbm):
                item.wait()
            totals = [jnp.zeros((1, width), F32)] * 3
            for rs in halves(rows):
                grad_y = g_ref[rs, :].astype(F32)
                u = u_ref[rs, :].astype(F32)
                grad_c = norm_back(grad_y, u, r_ref[rs, 0:1], vec_w[4])
                gacc_ref[rs, :] = grad_c
                low_ref[0, rs, :] = grad_c.astype(BF)
                for index, values in enumerate((grad_y * u, grad_y, grad_c)):
                    totals[index] += row_sum(values)
            for index in range(3):
                part_sums[index : index + 1, :] = totals[index]
            for item in norm_load(1, u1_hbm, r1_hbm):
                item.start()

        def ffn_unit(u):
            at = lax.rem(u, 2)

            @pl.when(u >= 1)
            def _():
                for item in write_tile(u - 1):
                    item.wait()

            arrived(w_ref.at[at, pl.ds(0, 2)], w_sem.at[at, 0])
            arrived(w_ref.at[at, 2], w_sem.at[at, 1])
            for n in range(2):
                arrived(qkv_ref.at[at, n], w_sem.at[at, 2 + n])
            gh = dot(low_ref[0], w_ref[at, 2])
            g0 = (gh * qkv_ref[at, 1].astype(F32)).astype(BF)
            g1 = (gh * qkv_ref[at, 0].astype(F32)).astype(BF)
            gqkv_ref[at, 0] = g0
            gqkv_ref[at, 1] = g1
            side, j = place_of(u)
            cols = block(side * tiles + j, ft)
            ub_sums[0:1, cols] = row_sum(g0.astype(F32))
            ub_sums[1:2, cols] = row_sum(g1.astype(F32))
            gacc_ref[...] += dot(g0, w_ref[at, 0], NT) + dot(g1, w_ref[at, 1], NT)

            @pl.when(u + 2 < 2 * tiles)
            def _():
                start_f(u + 2)

            for item in write_tile(u):
                item.start()

        def norm_unit():
            for item in write_tile(jnp.int32(2 * tiles - 1)):
                item.wait()
            for i in range(2):
                start_w(jnp.int32(i))
            fill_distance(dist_ref, lengths_ref[t * seqs + 1])
            for item in norm_load(1, u1_hbm, r1_hbm):
                item.wait()
            totals = [jnp.zeros((1, width), F32)] * 3
            for rs in halves(rows):
                grad_n = gacc_ref[rs, :]
                u = u_ref[rs, :].astype(F32)
                grad_a = norm_back(grad_n, u, r_ref[rs, 0:1], vec_w[1])
                low_ref[1, rs, :] = grad_a.astype(BF)
                gacc_ref[rs, :] = grad_a
                for index, values in enumerate((grad_n * u, grad_n, grad_a)):
                    totals[index] += row_sum(values)
            for index in range(3):
                part_sums[3 + index : 4 + index, :] = totals[index]

        def head_unit(a):
            i = a // 5
            phase = lax.rem(a, 5)
            pair = phase // 2
            at = lax.rem(i, 2)
            scale = BF(1.0 / math.sqrt(HD))
            cols = block(lax.rem(pair, 2), 2 * HD)

            @pl.when(phase == 0)
            def _():
                for index, ref in enumerate(
                    (w_ref.at[at], o_ref.at[at], qkv_ref.at[at, 0], qkv_ref.at[at, 1], qkv_ref.at[at, 2], lse_ref.at[at])
                ):
                    arrived(ref, w_sem.at[at, index])

                @pl.when(i >= 2)
                def _():
                    for item in write_heads(i - 2):
                        item.wait()

                gm_ref[...] = dot(low_ref[1], o_ref[at], NT).astype(BF)

            @pl.when((phase == 0) | (phase == 2))
            def _():
                query2 = qkv_ref[at, 0, :, cols] * scale
                key2 = qkv_ref[at, 1, :, cols]
                value2 = qkv_ref[at, 2, :, cols]
                gm2 = gm_ref[:, cols]
                parts = []
                for head in range(2):
                    here = slice(head * HD, (head + 1) * HD)
                    gm = gm2[:, here]
                    scores = dot(key2[:, here], query2[:, here], NT)
                    scores = scores - dist_ref[...] * slope_of(slope_ref, i * PER + pair * 2 + head)
                    likely = jnp.exp(scores - lse_ref[at, pl.ds(pair * 2 + head, 1), :])
                    parts.append(dot(likely.astype(BF), gm).astype(BF))
                    tt = likely * dot(value2[:, here], gm, NT)
                    inner = jnp.sum(tt, axis=0, keepdims=True)
                    gs_ref[head] = (tt - likely * inner).astype(BF)
                gqkv_ref[at, 2, :, cols] = jnp.concatenate(parts, axis=1)

            @pl.when((phase == 1) | (phase == 3))
            def _():
                query2 = qkv_ref[at, 0, :, cols] * scale
                key2 = qkv_ref[at, 1, :, cols] * scale
                parts = [[], []]
                for head in range(2):
                    here = slice(head * HD, (head + 1) * HD)
                    gs = gs_ref[head]
                    parts[1].append(dot(gs, query2[:, here]).astype(BF))
                    parts[0].append(dot(gs, key2[:, here], TN).astype(BF))
                for n in range(2):
                    gqkv_ref[at, n, :, cols] = jnp.concatenate(parts[n], axis=1)

            @pl.when(phase == 4)
            def _():
                for index, n in enumerate((0, 2)):
                    qv_sums[index : index + 1, block(i, CW)] = row_sum(gqkv_ref[at, n].astype(F32))
                gacc_ref[...] += (
                    dot(gqkv_ref[at, 0], w_ref[at, 0], NT)
                    + dot(gqkv_ref[at, 1], w_ref[at, 1], NT)
                    + dot(gqkv_ref[at, 2], w_ref[at, 2], NT)
                )

                @pl.when(i + 2 < 2 * heads_steps)
                def _():
                    start_w(i + 2)

                for item in write_heads(i):
                    item.start()

        def add_sums(norm_part, ub_part, qv_part):
            vec[0, 0:6] += norm_part[0:6]
            for own in range(2):
                @pl.when(t == own)
                def _(own=own):
                    for n in range(2):
                        for side in range(2):
                            place = own if side == 0 else 1 - own
                            for j in range(up_rows):
                                at = 6 + (2 * n + place) * up_rows + j
                                start = side * units + j * width
                                vec[0, at : at + 1] += ub_part[n : n + 1, start : start + width]
                            at = 6 + 4 * up_rows + n
                            cols = slice(place * local, (place + 1) * local)
                            vec[0, at : at + 1, cols] += qv_part[n : n + 1, side * local : (side + 1) * local]

        ends = [(g_ref, gxl_out), (gacc_ref, gx_out)]

        def end_unit():
            for i in (2 * heads_steps - 2, 2 * heads_steps - 1):
                for item in write_heads(jnp.int32(i)):
                    item.wait()
            g_ref[...] = gacc_ref[...].astype(BF)
            for index, item in enumerate(ends):
                copy(*item, e_sem.at[index]).start()
            add_sums(part_sums, ub_sums, qv_sums)
            for index, item in enumerate(ends):
                copy(*item, e_sem.at[index]).wait()

        vec[0] = jnp.zeros(vec_shape, F32)

        @pl.when(first)
        def _():
            begin()
            add_sums(*sum_refs[:3])

        @pl.when(section == 1)
        def _():
            add_sums(*sum_refs[3:6])
            add_sums(*sum_refs[6:9])

        take_left(0, 0, 0)
        vec_core = remote(vec.at[0], vec_in.at[0], v_send.at[0], v_recv.at[0], core)
        vec_cross = remote(vec.at[1], vec_in.at[1], v_send.at[1], v_recv.at[1], cross)

        def row_copy(m, source):
            return remote(
                source.at[block(1 - t, shard_rows)], rows_out.at[m], r_send.at[m], r_recv.at[m], cross
            )

        row_plan = [(0, 0, low_grad_ref, True), (0, 1, gxl_out, False), (1, 1, second_ref, True)]
        for number, m, source, early in row_plan:
            if early:
                @pl.when(section == number)
                def _(m=m, source=source):
                    row_copy(m, source).start()

        up = pl.ds(0, quarter)
        down = pl.ds(quarter, quarter)
        sides = ((up, 0, z, above, below), (down, 1, last - z, below, above))

        @pl.loop(0, ahead_of + total + drain)
        def _(turn):
            s = turn - ahead_of

            @pl.when(first)
            def _():
                @pl.when(turn < norm_at)
                def _():
                    ffn_unit(turn)

                @pl.when(turn == norm_at)
                def _():
                    norm_unit()

                @pl.when((turn >= head_at) & (turn < end_at))
                def _():
                    head_unit(turn - head_at)

                @pl.when(turn == end_at)
                def _():
                    end_unit()

            @pl.when(s == 0)
            def _():
                for k in range(ring - 1):
                    load_tile(jnp.int32(k))

            @pl.when(valid(s))
            def _():
                @pl.when(s == per_pair - 2)
                def _():
                    take_left(1, 1, None)

                @pl.when(s == x_flip)
                def _():
                    take_left(2, 0, None)

                @pl.when(s == ga_flip)
                def _():
                    take_left(3, 1, 1)

                at = lax.rem(s, ring)
                arrived(tile.at[at], tile_sem.at[at])
                give_at = lax.rem(s, gives)

                @pl.when(s >= gives)
                def _():
                    arrived(give.at[give_at], give_send.at[give_at])

                ffn_flip = jnp.where(lax.rem(s, 3 * per_pair) // per_pair == 0, 0, 1)
                which = jnp.where(s < ffn_blocks, ffn_flip, jnp.where(s < ffn_blocks + 3 * head_blocks, 0, 1))
                for place, store, spot in ((1 - c, give, give_at), (c, mine, lax.rem(s, mines))):
                    here = block(place, half)
                    product = dot(flip[which, here, :rows], tile[at, 0])
                    for m in range(1, seqs):
                        product += dot(flip[which, here, m * rows : (m + 1) * rows], tile[at, m])
                    store[spot, 1] = product[:, :bt].astype(BF)
                    store[spot, 0] = product[:, bt:].astype(BF)

            @pl.when((s >= 0) & (s + ring - 1 < total))
            def _():
                load_tile(s + ring - 1)

            k1 = s - CORE_LAG

            @pl.when(valid(k1))
            def _():
                arrived(acc.at[k1], core_recv.at[k1])
                at = lax.rem(k1, mines)
                for side in range(2):
                    acc[k1, side] = (acc[k1, side].astype(F32) + mine[at, side].astype(F32)).astype(BF)

            k2 = k1 - CROSS_LAG

            @pl.when(valid(k2))
            def _():
                arrived(from_x.at[k2], x_recv.at[k2])
                acc[k2, 1] = (acc[k2, 1].astype(F32) + from_x[k2].astype(F32)).astype(BF)

            for rows_, way, place, ahead, behind in sides:
                k3 = k2 - CHAIN_LAG * place

                @pl.when(valid(k3) & (place > 0))
                def _(rows_=rows_, way=way, k3=k3):
                    arrived(from_z.at[k3, rows_], z_recv.at[way, k3])
                    acc[k3, 1, rows_] = (acc[k3, 1, rows_].astype(F32) + from_z[k3, rows_].astype(F32)).astype(BF)

                k4 = k2 - CHAIN_LAG * (2 * last - place)

                @pl.when(valid(k4) & (place == last))
                def _(rows_=rows_, k4=k4):
                    final[k4, rows_] = acc[k4, 1, rows_]

                @pl.when(valid(k4) & (place < last))
                def _(rows_=rows_, way=way, k4=k4):
                    arrived(final.at[k4, rows_], f_recv.at[way, k4])

            @pl.when(valid(s))
            def _():
                at = lax.rem(s, gives)
                remote(give.at[at], acc.at[s], give_send.at[at], core_recv.at[s], core).start()

            @pl.when(valid(k1))
            def _():
                remote(acc.at[k1, 0], from_x.at[k1], x_send, x_recv.at[k1], cross).start()

            for number, m, source, early in row_plan:
                if not early:
                    @pl.when((k1 == total - 1) & (section == number))
                    def _(m=m, source=source):
                        row_copy(m, source).start()

            for rows_, way, place, ahead, behind in sides:
                k3 = k2 - CHAIN_LAG * place

                @pl.when(valid(k3) & (place < last))
                def _(rows_=rows_, way=way, k3=k3, ahead=ahead):
                    remote(acc.at[k3, 1, rows_], from_z.at[k3, rows_], z_send.at[way], z_recv.at[way, k3], ahead).start()

                k4 = k2 - CHAIN_LAG * (2 * last - place)

                @pl.when(valid(k4) & (place > 0))
                def _(rows_=rows_, way=way, k4=k4, behind=behind):
                    remote(final.at[k4, rows_], final.at[k4, rows_], f_send.at[way], f_recv.at[way, k4], behind).start()

            k5 = k2 - CHAIN_LAG * 2 * last

            @pl.when(valid(k5))
            def _():
                def visit(m, j):
                    dst = outs[group_of[m]].at[member_of[m], block(c, half), block(j, bt)]
                    copy(final.at[k5], dst, store_sem).start()
                    remote(final.at[k5], dst, out_send, out_recv, core).start()

                member(k5, visit)

            @pl.when(turn == end_at + 1)
            def _():
                vec_core.start()

            @pl.when(turn == end_at + 6)
            def _():
                vec_core.wait_recv()
                vec[1] = vec[0] + vec_in[0]

            @pl.when(turn == end_at + 7)
            def _():
                vec_cross.start()

            @pl.when(turn == end_at + 13)
            def _():
                vec_cross.wait_recv()
                vec_all[z] = vec[1] + vec_in[1]

            @pl.when(turn == end_at + 14)
            def _():
                for shift in range(1, chips):
                    to = lax.rem(z + shift, chips)
                    remote(
                        vec_all.at[z], vec_all.at[z], v_send.at[1 + shift], v_recv.at[1 + shift], {"dp": to * 2 + c}
                    ).start()

        for number, m, source, early in row_plan:
            @pl.when(section == number)
            def _(m=m, source=source):
                row_copy(m, source).wait()

        vec_core.wait_send()
        vec_cross.wait_send()
        for shift in range(1, chips):
            origin = lax.rem(z + chips - shift, chips)
            arrived(vec_all.at[origin], v_recv.at[1 + shift])
            arrived(vec_all.at[z], v_send.at[1 + shift])
        whole = vec_all[0]
        for chip in range(1, chips):
            whole += vec_all[chip]
        sums_out[...] = whole
        for at in range(gives):
            arrived(give.at[at], give_send.at[at])
        arrived(acc.at[:, 0], x_send)
        for rows_, way, place, ahead, behind in sides:
            @pl.when(place < last)
            def _(rows_=rows_, way=way):
                arrived(from_z.at[:, rows_], z_send.at[way])

            @pl.when(place > 0)
            def _(rows_=rows_, way=way):
                arrived(final.at[:, rows_], f_send.at[way])

        arrived(final, out_send)
        arrived(final, store_sem)
        arrived(final, out_recv)

    sem = pltpu.SemaphoreType.DMA
    flops = 2 * seqs * rows * width * 2 * bt * total
    members = [member_of[index] for index in range(7)]
    shapes = [(sum(g == index for g in group_of), width, rights[group_of.index(index)].shape[2] // 2) for index in range(4)]
    return pl.pallas_call(
        kernel,
        in_specs=[SMEM, SMEM] + NORM_SPECS + [WHOLE] * 9 + [ANY] * 32,
        out_specs=[ANY] * 4 + [WHOLE] + [ANY] * 8,
        out_shape=[jax.ShapeDtypeStruct(s, BF) for s in shapes]
        + [jax.ShapeDtypeStruct(vec_shape, F32), jax.ShapeDtypeStruct((seqs, shard_rows, width), BF)]
        + [jax.ShapeDtypeStruct(act.shape, BF)] * 2
        + [jax.ShapeDtypeStruct((rows, 2 * local), BF)] * 3
        + [jax.ShapeDtypeStruct((rows, width), F32), jax.ShapeDtypeStruct((rows, width), BF)],
        scratch_shapes=[
            pltpu.VMEM((total, 2, half, bt), BF),
            pltpu.VMEM((total, half, bt), BF),
            pltpu.VMEM((total, half, bt), BF),
            pltpu.VMEM((2, width, seqs * rows), BF),
            pltpu.VMEM((seqs, rows, width), BF),
            pltpu.VMEM((ring, seqs, rows, 2 * bt), BF),
            pltpu.VMEM((mines, 2, half, bt), BF),
            pltpu.VMEM((gives, 2, half, bt), BF),
            pltpu.VMEM((2,) + vec_shape, F32),
            pltpu.VMEM((2,) + vec_shape, F32),
            pltpu.VMEM((chips,) + vec_shape, F32),
            pltpu.VMEM((rows, width), BF),
            pltpu.VMEM((rows, width), BF),
            pltpu.VMEM((rows, 128), F32),
            pltpu.VMEM((2, rows, width), BF),
            pltpu.VMEM((rows, width), F32),
            pltpu.VMEM((2, 3, width, CW), BF),
            pltpu.VMEM((2, CW, width), BF),
            pltpu.VMEM((2, 3, rows, CW), BF),
            pltpu.VMEM((2, 3, rows, CW), BF),
            pltpu.VMEM((2, 8, rows), F32),
            pltpu.VMEM((rows, CW), BF),
            pltpu.VMEM((2, rows, rows), BF),
            pltpu.VMEM((rows, rows), F32),
            pltpu.VMEM((8, width), F32),
            pltpu.VMEM((2, 2 * units), F32),
            pltpu.VMEM((2, 2 * local), F32),
            sem((ring,)), sem((2,)), sem((gives,)), sem((total,)), sem, sem((total,)),
            sem((2,)), sem((2, total)), sem((2,)), sem((2, total)),
            sem, sem, sem, sem((chips + 1,)), sem((chips + 1,)), sem((seqs,)), sem((seqs,)),
            sem((3,)), sem((2, 6)), sem((2, 3)), sem((2,)),
        ],
        input_output_aliases={20: 6, 21: 7},
        compiler_params=pltpu.CompilerParams(
            collective_id=0, has_side_effects=True, vmem_limit_bytes=67_000_000
        ),
        cost_estimate=pl.CostEstimate(flops=flops, bytes_accessed=100 << 20, transcendentals=0),
        name="backward_and_reduce",
    )(
        lengths, slopes, *norms, *sums, grad, q, k_, v, lse, act, slope, u1, u2, r1, r2, *weights, *lefts, *rights,
        low_grad, second
    )


def exchange_rows(outputs, deps):
    seqs = len(outputs)
    rows, width = outputs[0].shape
    shard_rows = rows // 2
    n_in = seqs + len(deps)

    def kernel(*refs):
        y_refs, out_ref = refs[:seqs], refs[n_in]
        stage, send, recv, l_sem = refs[n_in + 1 :]
        t = lax.axis_index("tensor")
        cross = {"tensor": 1 - t}
        barrier = pltpu.get_barrier_semaphore()
        pl.semaphore_signal(barrier, inc=1, device_id=cross, device_id_type=MESH)
        pl.semaphore_wait(barrier, 1)

        @pl.when(lax.axis_index("section") == 0)
        def _():
            for m in range(seqs):
                pltpu.make_async_remote_copy(
                    src_ref=y_refs[m].at[block(1 - t, shard_rows)], dst_ref=out_ref.at[t * seqs + m],
                    send_sem=send.at[m], recv_sem=recv.at[m], device_id=cross, device_id_type=MESH,
                ).start()
            for m in range(seqs):
                copy(y_refs[m].at[block(t, shard_rows)], stage.at[m], l_sem.at[m]).start()
            for m in range(seqs):
                arrived(stage.at[m], l_sem.at[m])
                copy(stage.at[m], out_ref.at[t * seqs + m], l_sem.at[m]).start()
            for m in range(seqs):
                arrived(stage.at[m], l_sem.at[m])
            for m in range(seqs):
                arrived(out_ref.at[(1 - t) * seqs + m], recv.at[m])
                arrived(stage.at[m], send.at[m])

    sem = pltpu.SemaphoreType.DMA
    return pl.pallas_call(
        kernel,
        in_specs=[ANY] * n_in,
        out_specs=ANY,
        out_shape=jax.ShapeDtypeStruct((2 * seqs, shard_rows, width), BF),
        scratch_shapes=[pltpu.VMEM((seqs, shard_rows, width), BF), sem((seqs,)), sem((seqs,)), sem((seqs,))],
        compiler_params=pltpu.CompilerParams(collective_id=2, has_side_effects=True),
        cost_estimate=pl.CostEstimate(flops=0, bytes_accessed=0, transcendentals=0),
        name="exchange_rows",
    )(*outputs, *deps)


def widen(reduced, row_grads, got, got_second, produced, outputs, sums, units, local):
    shard_rows, width = got.shape[1:]
    seqs = got.shape[0]
    n = len(reduced)
    jobs = []
    for index, array in enumerate(reduced):
        lead, depth, columns = array.shape
        step = 512 * 1024 // columns
        if index == n - 1:
            jobs += [(index, 0, at, depth // 2, columns) for at in range(0, depth, depth // 2)]
        else:
            jobs += [(index, part, at, step, columns) for part in range(lead) for at in range(0, depth, step)]
    jobs += [(n, m, 0, shard_rows, width) for m in range(seqs)] + [(n + 1, m, 0, shard_rows, width) for m in range(seqs)]
    jobs += [(n + 2, m, 0, shard_rows, width) for m in range(2 * seqs)]
    ring = 5
    n_in = n + 3 * seqs + 4
    parts = units // width

    def kernel(*refs):
        ins = refs[:n]
        grad_refs = refs[n : n + 2 * seqs]
        got_ref, got_second_ref, produced_ref = refs[n + 2 * seqs : n + 2 * seqs + 3]
        y_refs, sums_ref = refs[n + 2 * seqs + 3 : n_in - 1], refs[n_in - 1]
        outs = refs[n_in : n_in + n + 2]
        qv_ref, out_bias_ref, gain_ref, shift_ref, ub_ref, down_bias_ref = refs[n_in + n + 2 : n_in + n + 8]
        shapes = sorted({(j[3], j[4]) for j in jobs if j[0] != n})
        buffers = refs[n_in + n + 8 :]
        wide_rows, in_sem, out_sem = buffers[0], buffers[1], buffers[2]
        low = {s: buffers[3 + 2 * i] for i, s in enumerate(shapes)}
        wide = {s: buffers[4 + 2 * i] for i, s in enumerate(shapes)}
        t = lax.axis_index("tensor")
        section = lax.axis_index("section")

        def load(number):
            index, part, at, rows, columns = jobs[number]
            s = number % ring
            if index < n:
                copy(ins[index].at[part, pl.ds(at, rows)], low[rows, columns].at[s], in_sem.at[s]).start()
            elif index == n:
                for turn in range(2):
                    @pl.when(section == turn)
                    def _(turn=turn):
                        source = grad_refs[turn * seqs + part].at[block(t, shard_rows)]
                        copy(source, wide_rows.at[part], in_sem.at[s]).start()
            elif index == n + 1:
                for number_ in range(2):
                    @pl.when(section == number_)
                    def _(number_=number_):
                        source = got_second_ref.at[seqs] if number_ == 1 and part == 0 else got_ref.at[part]
                        copy(source, low[rows, columns].at[s], in_sem.at[s]).start()
            else:
                @pl.when(section == 0)
                def _():
                    copy(produced_ref.at[part], low[rows, columns].at[s], in_sem.at[s]).start()

                @pl.when(section == 1)
                def _():
                    source = y_refs[part].at[block(t, shard_rows)] if part < seqs else got_second_ref.at[part - seqs]
                    copy(source, low[rows, columns].at[s], in_sem.at[s]).start()

        def store(number):
            index, part, at, rows, columns = jobs[number]
            s = number % ring
            if index < n - 1:
                return copy(wide[rows, columns].at[s], outs[index].at[part, pl.ds(at, rows)], out_sem.at[s])
            if index == n - 1:
                return copy(wide[rows, columns].at[s], outs[index].at[:, pl.ds(at, rows)], out_sem.at[s])
            if index == n:
                return copy(wide_rows.at[part], outs[n].at[t * seqs + part], out_sem.at[s])
            if index == n + 1:
                return copy(wide[rows, columns].at[s], outs[n].at[(1 - t) * seqs + part], out_sem.at[s])
            side, m = divmod(part, seqs)
            spread = (t + side - 2 * t * side) * seqs + m
            return copy(low[rows, columns].at[s], outs[n + 1].at[jnp.where(section == 0, part, spread)], out_sem.at[s])

        for number in range(ring):
            load(number)
        gain_ref[0:1] = sums_ref[3:4]
        gain_ref[1:2] = sums_ref[0:1]
        shift_ref[0:1] = sums_ref[4:5]
        shift_ref[1:2] = sums_ref[1:2]
        out_bias_ref[...] = sums_ref[5:6]
        down_bias_ref[...] = sums_ref[2:3]
        for half in range(2):
            @pl.when(t == half)
            def _(half=half):
                for g in range(2):
                    for j in range(parts):
                        at = 6 + (2 * g + half) * parts + j
                        ub_ref[g : g + 1, j * width : (j + 1) * width] = sums_ref[at : at + 1]
                    at = 6 + 4 * parts + g
                    qv_ref[g : g + 1] = sums_ref[at : at + 1, half * local : (half + 1) * local]

        for number, (index, part, at, rows, columns) in enumerate(jobs):
            s = number % ring
            if index == n:
                arrived(wide_rows.at[part], in_sem.at[s])
            else:
                arrived(low[rows, columns].at[s], in_sem.at[s])
            if number >= ring:
                store(number - ring).wait()
            if index == n - 1:
                wide[rows, columns][s] = low[rows, columns][s].astype(F32).T
            elif index not in (n, n + 2):
                wide[rows, columns][s] = low[rows, columns][s].astype(F32)
            store(number).start()
            if number + ring < len(jobs):
                load(number + ring)
        for number in range(len(jobs) - ring, len(jobs)):
            store(number).wait()

    shapes = sorted({(j[3], j[4]) for j in jobs if j[0] != n})
    square = (reduced[-1].shape[1] // 2, reduced[-1].shape[2])
    last = reduced[-1].shape
    sem = pltpu.SemaphoreType.DMA
    buffers = []
    for s in shapes:
        buffers += [pltpu.VMEM((ring,) + s, BF), pltpu.VMEM((ring,) + ((s[1], s[0]) if s == square else s), F32)]
    return pl.pallas_call(
        kernel,
        in_specs=[ANY] * (n_in - 1) + [WHOLE],
        out_specs=[ANY] * (n + 2) + [WHOLE] * 6,
        out_shape=[jax.ShapeDtypeStruct(r.shape, F32) for r in reduced[:-1]]
        + [jax.ShapeDtypeStruct((last[2], last[1]), F32), jax.ShapeDtypeStruct((2 * seqs, shard_rows, width), F32)]
        + [jax.ShapeDtypeStruct((2 * seqs, shard_rows, width), BF)]
        + [
            jax.ShapeDtypeStruct(shape, F32)
            for shape in ((2, local), (1, width), (2, width), (2, width), (2, units), (1, width))
        ],
        scratch_shapes=[pltpu.VMEM((seqs, shard_rows, width), F32), sem((ring,)), sem((ring,))] + buffers,
        compiler_params=pltpu.CompilerParams(vmem_limit_bytes=VMEM_LIMIT),
        cost_estimate=pl.CostEstimate(flops=0, bytes_accessed=56 << 20, transcendentals=0),
        name="widen",
    )(*reduced, *row_grads, got, got_second, produced, *outputs, sums)


MASKED = -1000000000.0


def shifted(value, axis, steps):
    count = lax.axis_size(axis)
    first, last = (max(0, -steps), min(count, count - steps))
    return lax.ppermute(value, axis, [(source, source + steps) for source in range(first, last)])


def layer_norm(values, gain, shift):
    mean = jnp.mean(values, axis=-1, keepdims=True)
    centred = values - mean
    spread = jnp.mean(centred * centred, axis=-1, keepdims=True)
    return centred * lax.rsqrt(spread + EPS) * gain + shift


def alibi_slopes(first, count, heads):
    index = (first + jnp.arange(count)).astype(jnp.float32)
    return jnp.exp2(-8.0 * (index + 1.0) / heads)


def attention_core(projected, qv_bias, slopes, key_ok):
    rows = projected.shape[0]
    width = projected.shape[2]
    count = slopes.shape[0]
    size = width // count
    query = (projected[:, 0] + qv_bias[0]).astype(jnp.bfloat16).reshape(rows, count, size)
    key = projected[:, 1].astype(jnp.bfloat16).reshape(rows, count, size)
    value = (projected[:, 2] + qv_bias[1]).astype(jnp.bfloat16).reshape(rows, count, size)
    place = jnp.arange(rows).astype(jnp.float32)
    distance = jnp.abs(place[:, None] - place[None, :])
    scale = 1.0 / math.sqrt(size)
    scores = (
        jnp.einsum("qhd,khd->hqk", query, key, preferred_element_type=jnp.float32) * scale
        - slopes[:, None, None] * distance[None]
    )
    scores = jnp.where(key_ok[None, None, :], scores, MASKED)
    weights = jax.nn.softmax(scores, axis=-1)
    weights_low = weights.astype(jnp.bfloat16)
    mixed = jnp.einsum("hqk,khd->qhd", weights_low, value, preferred_element_type=jnp.float32)
    mixed = mixed.reshape(rows, width).astype(jnp.bfloat16)
    return (query, key, value, weights, weights_low, mixed)


def attention_back(parts, grad_mixed, key_ok):
    query, key, value, weights, weights_low, mixed = parts
    rows, count, size = query.shape
    scale = 1.0 / math.sqrt(size)
    grad_low = grad_mixed.astype(jnp.bfloat16).reshape(rows, count, size)
    grad_weights = jnp.einsum("qhd,khd->hqk", grad_low, value, preferred_element_type=jnp.float32)
    grad_value = jnp.einsum(
        "hqk,qhd->khd", weights_low, grad_low, preferred_element_type=jnp.float32
    )
    inner = jnp.sum(weights * grad_weights, axis=-1, keepdims=True)
    grad_scores = weights * (grad_weights - inner)
    grad_scores = jnp.where(key_ok[None, None, :], grad_scores, 0.0).astype(jnp.bfloat16)
    grad_query = (
        jnp.einsum("hqk,khd->qhd", grad_scores, key, preferred_element_type=jnp.float32) * scale
    ).astype(jnp.bfloat16)
    grad_key = (
        jnp.einsum("hqk,qhd->khd", grad_scores, query, preferred_element_type=jnp.float32) * scale
    ).astype(jnp.bfloat16)
    grad_value = grad_value.astype(jnp.bfloat16)
    width = count * size
    grad_query = grad_query.reshape(rows, width)
    grad_key = grad_key.reshape(rows, width)
    grad_value = grad_value.reshape(rows, width)
    grad_projected = jnp.stack([grad_query, grad_key, grad_value], axis=1).reshape(rows, 3 * width)
    qv_grad = jnp.stack(
        [
            jnp.sum(grad_query.astype(jnp.float32), axis=0),
            jnp.sum(grad_value.astype(jnp.float32), axis=0),
        ]
    )
    return (grad_projected, qv_grad)


def gelu_product(both):
    return jax.nn.gelu(both[:, 0], approximate=False) * both[:, 1]


def geglu(lifted, up_bias):
    return gelu_product(lifted + up_bias[None])


def ffn_grads(rows_low, grad_low, up_weight, up_bias, down_weight):
    lifted = jnp.einsum("sd,gdf->sgf", rows_low, up_weight, preferred_element_type=jnp.float32)
    hidden, geglu_back = jax.vjp(gelu_product, lifted + up_bias[None])
    grad_hidden = jnp.einsum("sd,df->sf", grad_low, down_weight, preferred_element_type=jnp.float32)
    (grad_both,) = geglu_back(grad_hidden)
    grad_lifted = grad_both.astype(jnp.bfloat16)
    grad_bias = jnp.sum(grad_lifted.astype(jnp.float32), axis=0)
    up_grad = jnp.einsum("sd,sgf->gdf", rows_low, grad_lifted, preferred_element_type=jnp.float32)
    down_grad = jnp.einsum(
        "sd,sf->df", grad_low, hidden.astype(jnp.bfloat16), preferred_element_type=jnp.float32
    )
    return (grad_lifted, grad_bias, up_grad, down_grad)


def on_device(
    inputs,
    cotangent,
    lengths,
    w_qkv,
    b_qv,
    w_out,
    b_out,
    ln_gain,
    ln_bias,
    w_up,
    b_up,
    w_down,
    b_down,
):
    batches, shard_rows, width = inputs.shape
    parts = lax.axis_size("tensor")
    place = lax.axis_index("tensor")
    section = lax.axis_index("section")
    last_section = lax.axis_size("section") - 1
    full_rows = shard_rows * parts
    local_width = w_qkv.shape[3]
    local_heads = local_width // HD
    qkv_flat = w_qkv[0].reshape(width, 3 * local_width)
    out_weight = w_out[0]
    qv_bias = b_qv[0].astype(jnp.float32)
    out_bias = b_out[0].astype(jnp.float32)
    gains = ln_gain[0].astype(jnp.float32)
    shifts = ln_bias[0].astype(jnp.float32)
    down_bias = b_down[0].astype(jnp.float32)
    slopes = alibi_slopes(place * local_heads, local_heads, H)
    row_place = place * shard_rows + jnp.arange(shard_rows)
    kept_rows = 0

    def key_mask(length):
        return jnp.arange(full_rows) < length

    def after_attention(values, attended, bias, gain_rows, shift_rows):
        return layer_norm(values + attended + bias, gain_rows[0], shift_rows[0])

    def after_ffn(normed, lowered, bias, gain_rows, shift_rows):
        return layer_norm(normed + lowered + bias, gain_rows[1], shift_rows[1])

    def gather_inputs(values):
        return lax.all_gather(values.astype(jnp.bfloat16), "tensor", axis=0, tiled=True)

    def project(gathered):
        return jnp.dot(gathered, qkv_flat, preferred_element_type=jnp.float32).reshape(
            full_rows, 3, local_width
        )

    def attention_forward(values, length):
        gathered = gather_inputs(values)
        projected = project(gathered)
        mixed = attention_core(projected, qv_bias, slopes, key_mask(length))[5]

        def term(start, count):
            return jnp.dot(mixed, out_weight, preferred_element_type=jnp.float32)

        return (
            lax.psum_scatter(
                term(jnp.int32(0), shard_rows * lax.axis_size("tensor")).astype(jnp.bfloat16),
                "tensor",
                scatter_dimension=0,
                tiled=True,
            ).astype(jnp.float32),
            gathered,
            projected,
        )

    up_local = w_up[0]
    up_bias_local = b_up[0].astype(jnp.float32)
    down_local = w_down[0]

    def gather_normed(normed):
        return lax.all_gather(normed.astype(jnp.bfloat16), "tensor", axis=0, tiled=True)

    def ffn_forward(normed):
        lifted = jnp.einsum(
            "sd,gdf->sgf", gather_normed(normed), up_local, preferred_element_type=jnp.float32
        )
        hidden = geglu(lifted, up_bias_local).astype(jnp.bfloat16)

        def term(start, count):
            return jnp.einsum("sf,df->sd", hidden, down_local, preferred_element_type=jnp.float32)

        return lax.psum_scatter(
            term(jnp.int32(0), shard_rows * lax.axis_size("tensor")).astype(jnp.bfloat16),
            "tensor",
            scatter_dimension=0,
            tiled=True,
        ).astype(jnp.float32)

    def ffn_backward(normed, grad_lowered):
        gathered = gather_normed(normed)
        grad_whole = lax.all_gather(grad_lowered.astype(jnp.bfloat16), "tensor", axis=0, tiled=True)
        grad_lifted, grad_bias, up_grad, down_grad = ffn_grads(
            gathered, grad_whole, up_local, up_bias_local, down_local
        )

        def term(start, count):
            return jnp.einsum(
                "sgf,gdf->sd", grad_lifted, up_local, preferred_element_type=jnp.float32
            )

        grad_normed = lax.psum_scatter(
            term(jnp.int32(0), shard_rows * lax.axis_size("tensor")).astype(jnp.bfloat16),
            "tensor",
            scatter_dimension=0,
            tiled=True,
        ).astype(jnp.float32)
        return (grad_normed, (up_grad, grad_bias, down_grad))

    ffn_shapes = (up_local.shape, up_bias_local.shape, down_local.shape)

    def layer_forward(values, length):
        attended, gathered, projected = attention_forward(values, length)
        normed = after_attention(values, attended, out_bias, gains, shifts)
        lowered = ffn_forward(normed)
        return (
            after_ffn(normed, lowered, down_bias, gains, shifts),
            attended,
            lowered,
            gathered,
            projected,
        )

    def layer_backward(values, attended, lowered, length, grad_output):
        normed, attention_norm_back = jax.vjp(
            after_attention, values, attended, out_bias, gains, shifts
        )
        outcome, ffn_norm_back = jax.vjp(after_ffn, normed, lowered, down_bias, gains, shifts)
        grad_normed, grad_lowered, grad_down_bias, gain_late, shift_late = ffn_norm_back(
            grad_output
        )
        grad_from_ffn, ffn_terms = ffn_backward(normed, grad_lowered)
        grad_values, grad_attended, grad_out_bias, gain_early, shift_early = attention_norm_back(
            grad_normed + grad_from_ffn
        )
        gathered = gather_inputs(values)
        projected = project(gathered)
        grad_whole = lax.all_gather(
            grad_attended.astype(jnp.bfloat16), "tensor", axis=0, tiled=True
        )
        mask = key_mask(length)
        pieces = attention_core(projected, qv_bias, slopes, mask)
        mixed_low = pieces[5]
        out_grad = jnp.einsum(
            "se,sd->ed", mixed_low, grad_whole, preferred_element_type=jnp.float32
        )
        grad_mixed = jnp.einsum(
            "sd,ed->se", grad_whole, out_weight, preferred_element_type=jnp.float32
        )
        grad_projected, qv_grad = attention_back(pieces, grad_mixed, mask)
        qkv_grad = jnp.einsum(
            "sd,sx->dx", gathered, grad_projected, preferred_element_type=jnp.float32
        )

        def term(start, count):
            return jnp.einsum(
                "sx,dx->sd", grad_projected, qkv_flat, preferred_element_type=jnp.float32
            )

        grad_inputs = grad_values + lax.psum_scatter(
            term(jnp.int32(0), shard_rows * lax.axis_size("tensor")).astype(jnp.bfloat16),
            "tensor",
            scatter_dimension=0,
            tiled=True,
        ).astype(jnp.float32)
        terms = (
            qkv_grad,
            qv_grad,
            out_grad,
            grad_out_bias,
            gain_early + gain_late,
            shift_early + shift_late,
            ffn_terms[0],
            ffn_terms[1],
            ffn_terms[2],
            grad_down_bias,
        )
        return (grad_inputs, terms)

    def keep(store, item, batch, valid):
        old = lax.dynamic_index_in_dim(store, batch, 0, keepdims=False)
        return lax.dynamic_update_index_in_dim(store, jnp.where(valid, item, old), batch, 0)

    def forward_step(step, carry):
        (
            received,
            kept_values,
            kept_attended,
            kept_lowered,
            produced,
            kept_gathered,
            kept_projected,
        ) = carry
        index = step - section
        valid = (index >= 0) & (index < batches)
        batch = jnp.clip(index, 0, batches - 1)
        fresh = lax.dynamic_index_in_dim(
            inputs, jnp.minimum(step, batches - 1), 0, keepdims=False
        ).astype(jnp.float32)
        values = jnp.where(section == 0, fresh, received.astype(jnp.float32))
        output, attended, lowered, gathered, projected = layer_forward(values, lengths[batch])
        sent = output.astype(jnp.bfloat16)
        kept_values = keep(kept_values, values, batch, valid)
        kept_attended = keep(kept_attended, attended, batch, valid)
        kept_lowered = keep(kept_lowered, lowered, batch, valid)
        produced = keep(produced, sent, batch, valid)
        kept_gathered = keep(kept_gathered, gathered[:kept_rows], batch, valid)
        kept_projected = keep(kept_projected, projected[:kept_rows], batch, valid)
        received = shifted(sent, "section", 1)
        return (
            received,
            kept_values,
            kept_attended,
            kept_lowered,
            produced,
            kept_gathered,
            kept_projected,
        )

    store_zeros = jnp.zeros((batches, shard_rows, width), jnp.float32)
    gathered_zeros = jnp.zeros((batches, kept_rows, width), jnp.bfloat16)
    projected_zeros = jnp.zeros((batches, kept_rows, 3, local_width), jnp.float32)
    start_forward = (
        jnp.zeros((shard_rows, width), jnp.bfloat16),
        store_zeros,
        store_zeros,
        store_zeros,
        jnp.zeros((batches, shard_rows, width), jnp.bfloat16),
        gathered_zeros,
        projected_zeros,
    )
    received, kept_values, kept_attended, kept_lowered, produced, kept_gathered, kept_projected = (
        lax.fori_loop(0, batches + last_section, forward_step, start_forward)
    )

    def backward_step(step, carry):
        received, totals, grads_in = carry
        index = step - (last_section - section)
        valid = (index >= 0) & (index < batches)
        batch = jnp.clip(index, 0, batches - 1)
        length = lengths[batch]
        outer = lax.dynamic_index_in_dim(cotangent, batch, 0, keepdims=False).astype(jnp.float32)
        outer = outer * (row_place < length).astype(jnp.float32)[:, None]
        grad_output = jnp.where(section == last_section, outer, received.astype(jnp.float32))
        grad_output = jnp.where(valid, grad_output, 0.0)
        values = lax.dynamic_index_in_dim(kept_values, batch, 0, keepdims=False)
        attended = lax.dynamic_index_in_dim(kept_attended, batch, 0, keepdims=False)
        lowered = lax.dynamic_index_in_dim(kept_lowered, batch, 0, keepdims=False)
        grad_inputs, terms = layer_backward(values, attended, lowered, length, grad_output)
        totals = jax.tree.map(jnp.add, totals, terms)
        grads_in = keep(grads_in, grad_inputs, batch, valid)
        received = shifted(grad_inputs.astype(jnp.bfloat16), "section", -1)
        return (received, totals, grads_in)

    start_totals = (
        jnp.zeros((width, 3 * local_width), jnp.float32),
        jnp.zeros((2, local_width), jnp.float32),
        jnp.zeros((local_width, width), jnp.float32),
        jnp.zeros((width,), jnp.float32),
        jnp.zeros((2, width), jnp.float32),
        jnp.zeros((2, width), jnp.float32),
        jnp.zeros(ffn_shapes[0], jnp.float32),
        jnp.zeros(ffn_shapes[1], jnp.float32),
        jnp.zeros(ffn_shapes[2], jnp.float32),
        jnp.zeros((width,), jnp.float32),
    )
    start_backward = (jnp.zeros((shard_rows, width), jnp.bfloat16), start_totals, store_zeros)
    received, totals, grads_in = lax.fori_loop(
        0, batches + last_section, backward_step, start_backward
    )
    (
        qkv_total,
        qv_total,
        out_total,
        out_bias_total,
        gain_total,
        shift_total,
        up_total,
        up_bias_total,
        down_total,
        down_bias_total,
    ) = totals
    qkv_sum, qv_sum, out_sum, up_sum, up_bias_sum, down_sum = (
        lax.psum(qkv_total.astype(jnp.bfloat16), "dp").astype(jnp.float32),
        lax.psum(qv_total.astype(jnp.bfloat16), "dp").astype(jnp.float32),
        lax.psum(out_total.astype(jnp.bfloat16), "dp").astype(jnp.float32),
        lax.psum(up_total.astype(jnp.bfloat16), "dp").astype(jnp.float32),
        lax.psum(up_bias_total.astype(jnp.bfloat16), "dp").astype(jnp.float32),
        lax.psum(down_total.astype(jnp.bfloat16), "dp").astype(jnp.float32),
    )
    out_bias_sum, gain_sum, shift_sum, down_bias_sum = lax.psum(
        (out_bias_total, gain_total, shift_total, down_bias_total), ("tensor", "dp")
    )
    return (
        produced[None],
        grads_in[None],
        qkv_sum.reshape(1, width, 3, local_width),
        qv_sum[None],
        out_sum[None],
        out_bias_sum[None],
        gain_sum[None],
        shift_sum[None],
        up_sum[None],
        up_bias_sum[None],
        down_sum[None],
        down_bias_sum[None],
    )


def by_sequence(
    inputs,
    cotangent,
    lengths,
    w_qkv,
    b_qv,
    w_out,
    b_out,
    ln_gain,
    ln_bias,
    w_up,
    b_up,
    w_down,
    b_down,
):
    batches, shard_rows, width = inputs.shape
    place = lax.axis_index("tensor")
    section = lax.axis_index("section")
    groups = lax.axis_size("dp")
    rows = 2 * shard_rows
    seqs = batches // 2
    local = w_qkv.shape[3]
    units = w_up.shape[3]
    heads = local // HD
    chips = groups // 2

    qkv_own = jnp.transpose(w_qkv[0], (1, 0, 2))
    out_own = w_out[0]
    up_own = w_up[0]
    down_own = w_down[0]
    first = section == 0
    norms = (b_out, ln_gain[0], ln_bias[0], b_down)
    table = np.exp2(-8.0 * (np.arange(2 * heads, dtype=np.float32) + 1.0) / H).astype(np.float32)
    slopes = jnp.asarray(np.concatenate([table, np.roll(table, heads)]))

    qkv_oth, out_oth, up_oth, down_oth, *rest = fetch_and_forward(
        (qkv_own, out_own, up_own, down_own),
        (b_qv[0], b_up[0]),
        inputs,
        cotangent,
        slopes,
        norms,
        lengths,
        chips,
        seqs,
    )
    weights = (qkv_own, qkv_oth, out_own, out_oth, up_own, up_oth, down_own, down_oth)
    biases, rest = rest[:2], rest[2:]
    x_first = outer = rest[:seqs]
    *kept, y = rest[seqs:]
    deps = [y]

    def forward(x, m, turn):
        nonlocal kept, deps
        *kept, y = layer_forward(x, weights, biases, slopes, norms, lengths, m, turn, kept, deps, seqs)
        deps = [y]
        return y

    y_first = [y] + [forward(x_first[m], m, 0) for m in range(1, seqs)]
    x_second = [lax.ppermute(y, "section", [(0, 1)]) for y in y_first]
    y_second = [forward(x_second[0], 0, 1)]
    produced = exchange_rows(y_first, deps)
    deps = [produced]
    y_second += [forward(x_second[m], m, 1) for m in range(1, seqs)]

    back = None
    sums = [[None] * seqs, [None] * seqs]

    got_second = None

    def backward(grad, m, turn, *extra):
        nonlocal back, deps, got_second
        results = layer_backward(grad, kept, weights, slopes, norms, lengths, m, turn, back, deps, seqs, *extra)
        back, (gx, gx_low, norm_sums, up_sums, qv_sums) = results[:7], results[7:12]
        if extra:
            got_second = results[12]
        deps = [norm_sums]
        sums[turn][m] = (norm_sums, up_sums, qv_sums)
        return gx, gx_low

    gx_second = [backward(outer[0], 0, 1)]
    gx_second.append(backward(outer[1], 1, 1, [*y_second, gx_second[0][1]]))
    grad_middle = [lax.ppermute(gx_second[m][1], "section", [(1, 0)]) for m in range(seqs)]
    x_all = jnp.stack([jnp.where(first, x_first[m], x_second[m]) for m in range(seqs)])
    deps = deps + [x_all]
    gx_first = [backward(grad_middle[0], 0, 0)]

    *reduced, packed, got, _, _, _, _, _, gx, _ = backward_and_reduce(
        grad_middle[1], kept, back, x_all, weights, slopes, norms, lengths, [*sums[0][0], *sums[1][0], *sums[1][1]], gx_first[0][1],
        gx_second[1][1], chips,
    )
    gx_all = [gx_first[0][0], gx] + [g[0] for g in gx_second]
    (
        down_sum, up_sum, qkv_sum, out_sum, grads_in, produced,
        qv_sum, out_bias_sum, gain_sum, shift_sum, up_bias_sum, down_bias_sum,
    ) = widen(reduced, gx_all, got, got_second, produced, y_second, packed, units, local)
    return (
        produced[None],
        grads_in[None],
        jnp.transpose(qkv_sum, (1, 0, 2))[None],
        qv_sum[None],
        out_sum[None],
        out_bias_sum,
        gain_sum[None],
        shift_sum[None],
        up_sum[None],
        up_bias_sum[None],
        down_sum,
        down_bias_sum,
    )


def solution(mesh):
    sections, parts, groups = (mesh.shape[name] for name in ("section", "tensor", "dp"))

    def run(*args):
        paired = sections == 2 and parts == 2 and groups % 2 == 0 and args[0].shape[0] == 4
        return (by_sequence if paired else on_device)(*args)

    return jax.shard_map(
        run,
        mesh=mesh,
        in_specs=(
            P("dp", "tensor", None),
            P("dp", "tensor", None),
            P("dp"),
            P("section", None, None, "tensor"),
            P("section", None, "tensor"),
            P("section", "tensor", None),
            P("section", None),
            P("section", None, None),
            P("section", None, None),
            P("section", None, None, "tensor"),
            P("section", None, "tensor"),
            P("section", None, "tensor"),
            P("section", None),
        ),
        out_specs=(
            P("section", "dp", "tensor", None),
            P("section", "dp", "tensor", None),
            P("section", None, None, "tensor"),
            P("section", None, "tensor"),
            P("section", "tensor", None),
            P("section", None),
            P("section", None, None),
            P("section", None, None),
            P("section", None, None, "tensor"),
            P("section", None, "tensor"),
            P("section", None, "tensor"),
            P("section", None),
        ),
        check_vma=False,
    )
```

```python
import math

import jax
import jax.numpy as jnp
import numpy as np
from jax import lax
from jax.experimental import pallas as pl
from jax.experimental.pallas import tpu as pltpu
from jax.sharding import PartitionSpec as P

H = 16
HD = 64
EPS = 1e-05
BF = jnp.bfloat16
F32 = jnp.float32
VMEM_LIMIT = 62 * 1024 * 1024
ANY = pl.BlockSpec(memory_space=pl.ANY)
SMEM = pl.BlockSpec(memory_space=pltpu.SMEM)
WHOLE = pl.BlockSpec(memory_space=pltpu.VMEM)
NN = (((1,), (0,)), ((), ()))
NT = (((1,), (1,)), ((), ()))
TN = (((0,), (0,)), ((), ()))
CW = 256
PER = CW // HD


def dot(a, b, dims=NN):
    return lax.dot_general(a, b, dims, preferred_element_type=F32)


def arrived(ref, sem):
    pltpu.make_async_copy(ref, ref, sem).wait()


def call(kernel, inputs, outputs, scratch, chain, deps, name, flops, nbytes, turn, remote=False):
    pairs = [item if isinstance(item, tuple) else (item, ANY) for item in inputs]
    args = [p[0] for p in pairs]
    specs = [p[1] for p in pairs]
    n_in = len(args)
    aliases = {}
    if chain is not None:
        for buffer, index in zip(chain, [index for index, item in enumerate(outputs) if item[2]]):
            aliases[len(args)] = index
            args.append(buffer)
            specs.append(ANY)
    args += deps
    specs += [ANY] * len(deps)
    n_args, n_out = len(args), len(outputs)
    params = {"collective_id": 3, "has_side_effects": True} if remote else {}

    def body(*refs):
        @pl.when(lax.axis_index("section") == turn)
        def _():
            kernel(refs[:n_in], refs[n_args : n_args + n_out], refs[n_args + n_out :])

    return pl.pallas_call(
        body,
        in_specs=specs,
        out_specs=[ANY] * n_out,
        out_shape=[jax.ShapeDtypeStruct(o[0], o[1]) for o in outputs],
        scratch_shapes=scratch,
        input_output_aliases=aliases,
        compiler_params=pltpu.CompilerParams(vmem_limit_bytes=VMEM_LIMIT, **params),
        cost_estimate=pl.CostEstimate(flops=flops, bytes_accessed=nbytes, transcendentals=0),
        name=name,
    )(*args)


NORM_SPECS = [WHOLE] * 4


def norm_rows(refs):
    out_bias, gain, shift, down_bias = refs
    rows = [out_bias[...], gain[0:1], shift[0:1], down_bias[...], gain[1:2], shift[1:2]]
    return [row.astype(F32) for row in rows]


def slope_of(table_ref, head):
    return table_ref[lax.axis_index("tensor") * (table_ref.shape[0] // 2) + head]


def pick(k, count, own, oth, make):
    @pl.when(k < count)
    def _():
        for src, dst, sem in make(own, k):
            pltpu.make_async_copy(src, dst, sem).start()

    @pl.when(k >= count)
    def _():
        for src, dst, sem in make(oth, k - count):
            pltpu.make_async_copy(src, dst, sem).start()


def block(index, size):
    return pl.ds(pl.multiple_of(index * size, size), size)


def copy(src, dst, sem):
    return pltpu.make_async_copy(src, dst, sem)


def fill_distance(dist_ref, length):
    rows = dist_ref.shape[0]
    keys = lax.broadcasted_iota(jnp.int32, (rows, rows), 0)
    places = lax.broadcasted_iota(jnp.int32, (rows, rows), 1)
    distance = jnp.abs(keys - places).astype(F32)
    dist_ref[...] = jnp.where(keys < length, distance, 1e12)


def normalize(v):
    mean = jnp.mean(v, axis=1, keepdims=True)
    centred = v - mean
    rstd = lax.rsqrt(jnp.mean(centred * centred, axis=1, keepdims=True) + EPS)
    return centred * rstd, rstd


def halves(rows):
    return [slice(0, rows // 2), slice(rows // 2, rows)]


class Forward:
    def __init__(self, rows, width, local, units):
        self.rows, self.width, self.local, self.units = rows, width, local, units
        self.ft = min(512, units)
        self.tiles = units // self.ft
        self.heads_steps = local // CW
        self.total = 2 * local

    def kept(self, slots):
        rows, width = self.rows, self.width
        shapes = [((slots, rows, self.total), BF)] * 4
        shapes += [((slots, 2 * self.heads_steps, 8, rows), F32)]
        shapes += [((slots, rows, 2 * self.units), BF)] * 3
        return shapes + [((slots, rows, width), BF)] * 3 + [((slots, rows, 128), F32)] * 2

    def scratch(self):
        rows, width, ft, total = self.rows, self.width, self.ft, self.total
        sem = pltpu.SemaphoreType.DMA
        return [
            pltpu.VMEM((rows, width), BF),
            pltpu.VMEM((2, 3, width, CW), BF),
            pltpu.VMEM((total, width), BF),
            pltpu.VMEM((2, 2, width, ft), BF),
            pltpu.VMEM((2, width, ft), BF),
            pltpu.VMEM((2, 3, rows, CW), BF),
            pltpu.VMEM((2, 8, rows), F32),
            pltpu.VMEM((rows, total), BF),
            pltpu.VMEM((rows, rows), F32),
            pltpu.VMEM((rows, width), F32),
            pltpu.VMEM((rows, width), F32),
            pltpu.VMEM((rows, width), BF),
            pltpu.VMEM((2, 3, rows, ft), BF),
            pltpu.VMEM((3, rows, width), BF),
            pltpu.VMEM((2, rows, 128), F32),
            sem, sem((2,)), sem((2,)), sem((2, 2)), sem((2, 4)), sem, sem((2, 3)), sem((6,)),
        ]

    def bind(self, x, weights, bias, up_bias, slopes, norms, slot, outs, scratch):
        self.x_hbm, self.weights, self.bias, self.up_bias, self.slopes, self.norms = x, weights, bias, up_bias, slopes, norms
        self.slot, self.outs = slot, outs
        (self.x, self.w, self.o, self.up, self.down, self.qkv, self.lse, self.mixed, self.dist, self.normed, self.acc,
         self.low, self.tile, self.row, self.stat, self.x_sem, self.w_sem, self.o_sem, self.f_sem, self.q_sem, self.m_sem,
         self.t_sem, self.r_sem) = scratch

    def start_x(self):
        copy(self.x_hbm, self.x, self.x_sem).start()

    def start_w(self, k):
        s = lax.rem(k, 2)
        pick(k, self.heads_steps, self.weights[0], self.weights[1],
             lambda ref, j: [(ref.at[:, :, block(j, CW)], self.w.at[s], self.w_sem.at[s])])

    def start_o(self, side):
        copy(self.weights[2 + side], self.o.at[pl.ds(side * self.local, self.local)], self.o_sem.at[side]).start()

    def start_f(self, k):
        s = lax.rem(k, 2)
        ft = self.ft
        pick(k, self.tiles, (self.weights[4], self.weights[6]), (self.weights[5], self.weights[7]),
             lambda ref, j: [(ref[0].at[:, :, block(j, ft)], self.up.at[s], self.f_sem.at[s, 0]),
                             (ref[1].at[:, block(j, ft)], self.down.at[s], self.f_sem.at[s, 1])])

    def write_qkv(self, i, s):
        cols = block(i, CW)
        return [copy(self.qkv.at[s, c], out.at[self.slot, :, cols], self.q_sem.at[s, c])
                for c, out in enumerate(self.outs[:3])] + [
            copy(self.lse.at[s], self.outs[4].at[self.slot, i], self.q_sem.at[s, 3])]

    def attention_step(self, i, ahead):
        s = lax.rem(i, 2)
        qkv = self.qkv
        arrived(self.w.at[s], self.w_sem.at[s])

        @pl.when(i >= 2)
        def _():
            for item in self.write_qkv(i - 2, s):
                item.wait()

        values = self.x[...]
        b = self.bias[:, block(i, CW)].astype(F32)
        qkv[s, 0] = (dot(values, self.w[s, 0]) + b[0:1]).astype(BF)
        qkv[s, 1] = dot(values, self.w[s, 1]).astype(BF)
        qkv[s, 2] = (dot(values, self.w[s, 2]) + b[1:2]).astype(BF)

        @pl.when(i + 2 < ahead)
        def _():
            self.start_w(i + 2)

        parts = []
        for head in range(PER):
            cols = slice(head * HD, (head + 1) * HD)
            query = qkv[s, 0, :, cols] * BF(1.0 / math.sqrt(HD))
            scores = dot(qkv[s, 1, :, cols], query, NT)
            scores = scores - self.dist[...] * slope_of(self.slopes, i * PER + head)
            top = jnp.max(scores, axis=0, keepdims=True)
            likely = jnp.exp(scores - top)
            mass = jnp.sum(likely, axis=0, keepdims=True)
            low = (likely * (1.0 / mass)).astype(BF)
            parts.append(dot(low, qkv[s, 2, :, cols], TN).astype(BF))
            self.lse[s, head : head + 1, :] = top + jnp.log(mass)
        self.mixed[:, block(i, CW)] = jnp.concatenate(parts, axis=1)
        for item in self.write_qkv(i, s):
            item.start()

    def middle(self):
        rows, width = self.rows, self.width
        copy(self.mixed, self.outs[3].at[self.slot], self.m_sem).start()
        for side in range(2):
            arrived(self.o.at[pl.ds(side * self.local, self.local)], self.o_sem.at[side])
        vec = norm_rows(self.norms)
        for rs in halves(rows):
            attended = dot(self.mixed[rs, :], self.o[...])
            u, rstd = normalize(self.x[rs, :].astype(F32) + attended + vec[0])
            normed = u * vec[1] + vec[2]
            self.normed[rs, :] = normed
            self.low[rs, :] = normed.astype(BF)
            self.row[0, rs, :] = u.astype(BF)
            self.stat[0, rs, :] = jnp.broadcast_to(rstd, (rows // 2, 128))
            self.acc[rs, :] = jnp.zeros((rows // 2, width), F32)
        for index, item in enumerate(self.first_rows()):
            copy(*item, self.r_sem.at[index]).start()

    def first_rows(self):
        return [(self.low, self.outs[8].at[self.slot]), (self.row.at[0], self.outs[9].at[self.slot]),
                (self.stat.at[0], self.outs[11].at[self.slot])]

    def write_tiles(self, i, s):
        return [copy(self.tile.at[s, c], out.at[self.slot, :, block(i, self.ft)], self.t_sem.at[s, c])
                for c, out in enumerate(self.outs[5:8])]

    def ffn_step(self, i, ahead):
        s = lax.rem(i, 2)
        arrived(self.up.at[s], self.f_sem.at[s, 0])
        arrived(self.down.at[s], self.f_sem.at[s, 1])

        @pl.when(i >= 2)
        def _():
            for item in self.write_tiles(i - 2, s):
                item.wait()

        b = self.up_bias[:, block(i, self.ft)].astype(F32)
        low = self.low[...]
        gate = dot(low, self.up[s, 0]) + b[0:1]
        lift = dot(low, self.up[s, 1]) + b[1:2]
        cdf = 0.5 * lax.erf(gate * (1.0 / math.sqrt(2.0))) + 0.5
        act = gate * cdf
        slope = cdf + gate * (jnp.exp(gate * gate * -0.5) * (1.0 / math.sqrt(2.0 * math.pi)))
        self.tile[s, 0] = act.astype(BF)
        self.tile[s, 1] = (lift * slope).astype(BF)
        hidden = (act * lift).astype(BF)
        self.tile[s, 2] = hidden
        self.acc[...] += dot(hidden, self.down[s], NT)

        @pl.when(i + 2 < ahead)
        def _():
            self.start_f(i + 2)

        for item in self.write_tiles(i, s):
            item.start()

    def finish(self, y_out):
        rows = self.rows
        vec = norm_rows(self.norms)
        for rs in halves(rows):
            u, rstd = normalize(self.normed[rs, :] + self.acc[rs, :] + vec[3])
            self.row[1, rs, :] = u.astype(BF)
            self.stat[1, rs, :] = jnp.broadcast_to(rstd, (rows // 2, 128))
            self.row[2, rs, :] = (u * vec[4] + vec[5]).astype(BF)
        ends = [(self.row.at[1], self.outs[10].at[self.slot]), (self.stat.at[1], self.outs[12].at[self.slot]),
                (self.row.at[2], y_out)]
        for index, item in enumerate(ends):
            copy(*item, self.r_sem.at[3 + index]).start()
        for index, item in enumerate(self.first_rows() + ends):
            copy(*item, self.r_sem.at[index]).wait()
        copy(self.mixed, self.outs[3].at[self.slot], self.m_sem).wait()
        for i in (2 * self.heads_steps - 2, 2 * self.heads_steps - 1):
            for item in self.write_qkv(jnp.int32(i), i % 2):
                item.wait()
        for i in (2 * self.tiles - 2, 2 * self.tiles - 1):
            for item in self.write_tiles(jnp.int32(i), i % 2):
                item.wait()

    def flops(self):
        rows, width, total = self.rows, self.width, self.total
        return 2 * rows * width * (4 * total + 6 * self.units) + 4 * rows * rows * total


def layer_forward(x, weights, biases, slopes, norms, lengths, m, turn, chain, deps, slots):
    rows, width = x.shape
    step = Forward(rows, width, weights[0].shape[2], weights[4].shape[2])

    def kernel(ins, outs, scratch):
        lengths_ref = ins[0]
        step.bind(ins[1], ins[2:10], ins[10], ins[11], ins[12], ins[13:17], m, outs[:13], scratch)
        step.start_x()
        for k in range(2):
            step.start_w(jnp.int32(k))
        for side in range(2):
            step.start_o(side)
        for k in range(2):
            step.start_f(jnp.int32(k))
        fill_distance(step.dist, lengths_ref[lax.axis_index("tensor") * slots + m])
        arrived(step.x, step.x_sem)

        @pl.loop(0, 2 * step.heads_steps)
        def _(i):
            step.attention_step(i, 2 * step.heads_steps)

        step.middle()

        @pl.loop(0, 2 * step.tiles)
        def _(i):
            step.ffn_step(i, 2 * step.tiles)

        step.finish(outs[13])

    return call(
        kernel,
        [(lengths, SMEM), x, *weights, *zip(biases, [WHOLE] * 2), (slopes, SMEM), *zip(norms, NORM_SPECS)],
        [shape + (True,) for shape in step.kept(slots)] + [((rows, width), BF, False)],
        step.scratch(),
        chain,
        deps,
        "layer_forward",
        step.flops(),
        54 << 20,
        turn,
    )


def layer_backward(grad, kept, weights, slopes, norms, lengths, m, turn, chain, deps, slots, sent=()):
    qkv_own, qkv_oth, o_own, o_oth, up_own, up_oth, down_own, down_oth = weights
    q, k, v, _, lse, act, slope, _, _, u1, u2, r1, r2 = kept
    rows, width = grad.shape
    local = qkv_own.shape[2]
    units = up_own.shape[2]
    heads_steps = local // CW
    ft = min(512, units)
    tiles = units // ft
    total = 2 * local

    def norm_back(grad_z, u, rstd, gain):
        t = grad_z * gain
        return rstd * (t - jnp.mean(t, axis=1, keepdims=True) - u * jnp.mean(t * u, axis=1, keepdims=True))

    def row_sum(values):
        return jnp.sum(values, axis=0, keepdims=True)

    def kernel(ins, outs, scratch):
        (lengths_ref, g_hbm, q_hbm, k_hbm, v_hbm, lse_hbm, a_hbm, b_hbm, u1_hbm, u2_hbm, r1_hbm, r2_hbm,
         qkv_own_ref, qkv_oth_ref, o_own_ref, o_oth_ref, up_own_ref, up_oth_ref, down_own_ref, down_oth_ref,
         slope_ref) = ins[:21]
        gg0_out, gg1_out, gl_out, ga_out, gq_out, gk_out, gv_out, gx_out, gxl_out, sums_out, ub_out, qv_out = outs[:12]
        (g_ref, u_ref, r_ref, up_ref, down_ref, ab_ref, gg_ref, low_ref, acc_ref, sums_ref, ub_ref, qv_ref,
         w_ref, o_ref, qkv_ref, lse_ref, gm_ref, dist_ref, gqkv_ref,
         g_sem, f_sem, t_sem, w_sem, q_sem, r_sem, x_send, x_recv) = scratch
        slot = m
        t = lax.axis_index("tensor")
        length = lengths_ref[t * slots + m]
        travelling = []
        if sent:
            cross = {"tensor": 1 - t}
            barrier = pltpu.get_barrier_semaphore()
            pl.semaphore_signal(barrier, inc=1, device_id=cross, device_id_type=pl.DeviceIdType.MESH)
            pl.semaphore_wait(barrier, 1)
            for index in range(len(sent)):
                travelling.append(
                    pltpu.make_async_remote_copy(
                        src_ref=ins[25 + index].at[block(1 - t, rows // 2)], dst_ref=outs[12].at[index],
                        send_sem=x_send.at[index], recv_sem=x_recv.at[index],
                        device_id=cross, device_id_type=pl.DeviceIdType.MESH,
                    )
                )
                travelling[-1].start()

        def start_f(i):
            s = lax.rem(i, 2)
            pick(i, tiles, (up_own_ref, down_own_ref), (up_oth_ref, down_oth_ref),
                 lambda ref, j: [(ref[0].at[:, :, block(j, ft)], up_ref.at[s], f_sem.at[s, 0]),
                                 (ref[1].at[:, block(j, ft)], down_ref.at[s], f_sem.at[s, 1])])
            for c, ref in enumerate((a_hbm, b_hbm)):
                copy(ref.at[slot, :, block(i, ft)], ab_ref.at[s, c], f_sem.at[s, 2 + c]).start()

        def start_w(i):
            s = lax.rem(i, 2)
            pick(i, heads_steps, (qkv_own_ref, o_own_ref), (qkv_oth_ref, o_oth_ref),
                 lambda ref, j: [(ref[0].at[:, :, block(j, CW)], w_ref.at[s], w_sem.at[s, 0]),
                                 (ref[1].at[block(j, CW)], o_ref.at[s], w_sem.at[s, 1])])
            for c, ref in enumerate((q_hbm, k_hbm, v_hbm)):
                copy(ref.at[slot, :, block(i, CW)], qkv_ref.at[s, c], w_sem.at[s, 2 + c]).start()
            copy(lse_hbm.at[slot, i], lse_ref.at[s], w_sem.at[s, 5]).start()

        firsts = [(g_hbm, g_ref), (u2_hbm.at[slot], u_ref.at[1]), (r2_hbm.at[slot], r_ref.at[1]),
                  (u1_hbm.at[slot], u_ref.at[0]), (r1_hbm.at[slot], r_ref.at[0])]
        for index, (src, dst) in enumerate(firsts):
            copy(src, dst, g_sem.at[index]).start()
            if index == 2:
                start_f(jnp.int32(0))
                start_f(jnp.int32(1))
        start_w(jnp.int32(0))
        start_w(jnp.int32(1))
        vec = norm_rows(ins[21:25])
        fill_distance(dist_ref, length)
        for index, (src, dst) in enumerate(firsts[:3]):
            copy(src, dst, g_sem.at[index]).wait()
        sums = [jnp.zeros((1, width), F32)] * 3
        for rs in halves(rows):
            grad_y = g_ref[rs, :].astype(F32)
            if turn == 1:
                places = lax.broadcasted_iota(jnp.int32, (rows // 2, width), 0) + rs.start
                grad_y = jnp.where(places < length, grad_y, 0.0)
            u = u_ref[1, rs, :].astype(F32)
            grad_c = norm_back(grad_y, u, r_ref[1, rs, 0:1], vec[4])
            acc_ref[rs, :] = grad_c
            low_ref[0, rs, :] = grad_c.astype(BF)
            for index, values in enumerate((grad_y * u, grad_y, grad_c)):
                sums[index] += row_sum(values)
        for index in range(3):
            sums_ref[index : index + 1, :] = sums[index]
        copy(low_ref.at[0], gl_out.at[slot], r_sem.at[0]).start()

        def write_tiles(i, s):
            return [copy(gg_ref.at[s, c], out.at[slot, :, block(i, ft)], t_sem.at[s, c])
                    for c, out in enumerate((gg0_out, gg1_out))]

        @pl.loop(0, 2 * tiles)
        def _(i):
            s = lax.rem(i, 2)
            arrived(up_ref.at[s], f_sem.at[s, 0])
            arrived(down_ref.at[s], f_sem.at[s, 1])
            for c in range(2):
                arrived(ab_ref.at[s, c], f_sem.at[s, 2 + c])

            @pl.when(i >= 2)
            def _():
                for item in write_tiles(i - 2, s):
                    item.wait()

            gh = dot(low_ref[0], down_ref[s])
            g0 = (gh * ab_ref[s, 1].astype(F32)).astype(BF)
            g1 = (gh * ab_ref[s, 0].astype(F32)).astype(BF)
            gg_ref[s, 0] = g0
            gg_ref[s, 1] = g1
            ub_ref[0:1, block(i, ft)] = row_sum(g0.astype(F32))
            ub_ref[1:2, block(i, ft)] = row_sum(g1.astype(F32))
            acc_ref[...] += dot(g0, up_ref[s, 0], NT) + dot(g1, up_ref[s, 1], NT)

            @pl.when(i + 2 < 2 * tiles)
            def _():
                start_f(i + 2)

            for item in write_tiles(i, s):
                item.start()

        for index, (src, dst) in enumerate(firsts[3:]):
            copy(src, dst, g_sem.at[3 + index]).wait()
        sums = [jnp.zeros((1, width), F32)] * 3
        for rs in halves(rows):
            grad_n = acc_ref[rs, :]
            u = u_ref[0, rs, :].astype(F32)
            grad_a = norm_back(grad_n, u, r_ref[0, rs, 0:1], vec[1])
            low_ref[1, rs, :] = grad_a.astype(BF)
            acc_ref[rs, :] = grad_a
            for index, values in enumerate((grad_n * u, grad_n, grad_a)):
                sums[index] += row_sum(values)
        for index in range(3):
            sums_ref[3 + index : 4 + index, :] = sums[index]
        sums_ref[6:8, :] = jnp.zeros((2, width), F32)
        copy(low_ref.at[1], ga_out.at[slot], r_sem.at[1]).start()
        scale = BF(1.0 / math.sqrt(HD))

        def write_heads(i, s):
            return [copy(gqkv_ref.at[s, c], out.at[slot, :, block(i, CW)], q_sem.at[s, c])
                    for c, out in enumerate((gq_out, gk_out, gv_out))]

        @pl.loop(0, 2 * heads_steps)
        def _(i):
            s = lax.rem(i, 2)
            for index, ref in enumerate((w_ref.at[s], o_ref.at[s], qkv_ref.at[s, 0], qkv_ref.at[s, 1], qkv_ref.at[s, 2], lse_ref.at[s])):
                arrived(ref, w_sem.at[s, index])

            @pl.when(i >= 2)
            def _():
                for item in write_heads(i - 2, s):
                    item.wait()

            gm_ref[...] = dot(low_ref[1], o_ref[s], NT).astype(BF)
            parts = [[], [], []]
            for head in range(PER):
                cols = slice(head * HD, (head + 1) * HD)
                query = qkv_ref[s, 0, :, cols] * scale
                key = qkv_ref[s, 1, :, cols]
                gm = gm_ref[:, cols]
                scores = dot(key, query, NT)
                scores = scores - dist_ref[...] * slope_of(slope_ref, i * PER + head)
                likely = jnp.exp(scores - lse_ref[s, head : head + 1, :])
                parts[2].append(dot(likely.astype(BF), gm).astype(BF))
                t = likely * dot(qkv_ref[s, 2, :, cols], gm, NT)
                inner = jnp.sum(t, axis=0, keepdims=True)
                gs = (t - likely * inner).astype(BF)
                parts[1].append(dot(gs, query).astype(BF))
                parts[0].append(dot(gs, key * scale, TN).astype(BF))
            for c in range(3):
                gqkv_ref[s, c] = jnp.concatenate(parts[c], axis=1)
            for index, c in enumerate((0, 2)):
                qv_ref[index : index + 1, block(i, CW)] = row_sum(gqkv_ref[s, c].astype(F32))
            acc_ref[...] += (
                dot(gqkv_ref[s, 0], w_ref[s, 0], NT)
                + dot(gqkv_ref[s, 1], w_ref[s, 1], NT)
                + dot(gqkv_ref[s, 2], w_ref[s, 2], NT)
            )

            @pl.when(i + 2 < 2 * heads_steps)
            def _():
                start_w(i + 2)

            for item in write_heads(i, s):
                item.start()

        g_ref[...] = acc_ref[...].astype(BF)
        ends = [(g_ref, gxl_out), (acc_ref, gx_out), (sums_ref, sums_out), (ub_ref, ub_out), (qv_ref, qv_out)]
        for index, (src, dst) in enumerate(ends):
            copy(src, dst, r_sem.at[2 + index]).start()
        for index, (src, dst) in enumerate([(low_ref.at[0], gl_out.at[slot]), (low_ref.at[1], ga_out.at[slot])] + ends):
            copy(src, dst, r_sem.at[index]).wait()
        for i in (2 * tiles - 2, 2 * tiles - 1):
            for item in write_tiles(jnp.int32(i), i % 2):
                item.wait()
        for i in (2 * heads_steps - 2, 2 * heads_steps - 1):
            for item in write_heads(jnp.int32(i), i % 2):
                item.wait()
        for item in travelling:
            item.wait()

    sem = pltpu.SemaphoreType.DMA
    return call(
        kernel,
        [(lengths, SMEM), grad, q, k, v, lse, act, slope, u1, u2, r1, r2, *weights, (slopes, SMEM), *zip(norms, NORM_SPECS), *sent],
        [((slots, rows, 2 * units), BF, True)] * 2
        + [((slots, rows, width), BF, True)] * 2
        + [((slots, rows, total), BF, True)] * 3
        + [
            ((rows, width), F32, False),
            ((rows, width), BF, False),
            ((8, width), F32, False),
            ((2, 2 * units), F32, False),
            ((2, total), F32, False),
        ]
        + ([((len(sent), rows // 2, width), BF, False)] if sent else []),
        [
            pltpu.VMEM((rows, width), BF),
            pltpu.VMEM((2, rows, width), BF),
            pltpu.VMEM((2, rows, 128), F32),
            pltpu.VMEM((2, 2, width, ft), BF),
            pltpu.VMEM((2, width, ft), BF),
            pltpu.VMEM((2, 2, rows, ft), BF),
            pltpu.VMEM((2, 2, rows, ft), BF),
            pltpu.VMEM((2, rows, width), BF),
            pltpu.VMEM((rows, width), F32),
            pltpu.VMEM((8, width), F32),
            pltpu.VMEM((2, 2 * units), F32),
            pltpu.VMEM((2, total), F32),
            pltpu.VMEM((2, 3, width, CW), BF),
            pltpu.VMEM((2, CW, width), BF),
            pltpu.VMEM((2, 3, rows, CW), BF),
            pltpu.VMEM((2, 8, rows), F32),
            pltpu.VMEM((rows, CW), BF),
            pltpu.VMEM((rows, rows), F32),
            pltpu.VMEM((2, 3, rows, CW), BF),
            sem((5,)), sem((2, 4)), sem((2, 2)), sem((2, 6)), sem((2, 3)), sem((7,)), sem((4,)), sem((4,)),
        ],
        chain,
        deps,
        "layer_backward",
        2 * rows * width * (4 * total + 6 * units) + 10 * rows * rows * total,
        70 << 20,
        turn,
        bool(sent),
    )


MESH = pl.DeviceIdType.MESH
CORE_LAG = 3
CROSS_LAG = 3
CHAIN_LAG = 2


def neighbours():
    t = lax.axis_index("tensor")
    d = lax.axis_index("dp")
    last = lax.axis_size("dp") // 2 - 1
    c = lax.rem(d, 2)
    z = d // 2
    return t, c, z, last, {"dp": d + 1 - 2 * c}, {"tensor": 1 - t}, {"dp": d + 2}, {"dp": d - 2}


def greet(c, z, chips, core, cross):
    barrier = pltpu.get_barrier_semaphore()
    pl.semaphore_signal(barrier, inc=1, device_id=core, device_id_type=MESH)
    pl.semaphore_signal(barrier, inc=1, device_id=cross, device_id_type=MESH)
    for shift in range(1, chips):
        chip = lax.rem(z + shift, chips)
        pl.semaphore_signal(barrier, inc=1, device_id={"dp": chip * 2 + c}, device_id_type=MESH)
    pl.semaphore_wait(barrier, 1 + chips)


def fetch_and_forward(weights, biases, inputs, cotangent, slopes, norms, lengths, chips, slots):
    seqs = inputs.shape[0] // 2
    shard_rows, width = inputs.shape[1:]
    rows = 2 * shard_rows
    groups = 2 * chips
    qkv, out, up, down = weights
    local, units = qkv.shape[2], up.shape[2]
    step = Forward(rows, width, local, units)
    ft, tiles = step.ft, step.tiles
    bias_widths = [b.shape[1] for b in biases]
    QKV, OUT, UP, DOWN, ROWS, BIAS = range(6)

    plan = [(UP, 0, groups), (ROWS, 0, 0), (BIAS, 0, 0), (BIAS, 1, 0)]
    plan += [(UP, part, groups) for part in range(1, tiles)]
    plan += [(DOWN, part, groups) for part in range(tiles - 2)]
    plan += [(QKV, part, 2) for part in range(3)] + [(OUT, 0, 2)]
    plan += [(DOWN, part, 2) for part in range(tiles - 2, tiles)]
    plan += [(ROWS, part, 0) for part in range(1, seqs)]
    n = len(plan)
    number = {item[:2]: index for index, item in enumerate(plan)}

    def size(index):
        kind, part, pieces = plan[index]
        whole = {QKV: width * local, OUT: local * width, UP: 2 * width * ft, DOWN: width * ft, ROWS: shard_rows * width, BIAS: 64}
        return whole[kind] / max(1, pieces)

    events, clock, busy = [], 0.0, 0.0
    for index, (kind, part, pieces) in enumerate(plan):
        clock += size(index)
        events.append((clock + 66000, index, 0))
        if pieces == groups:
            start = max(clock, busy)
            busy = start + size(index) * (chips - 1) * 1.0
            events += [(start + (size(index) * 1.0 + 66000) * hop, index, hop) for hop in range(1, chips)]
    events.sort()
    when = {event[1:]: event[0] for event in events}

    def ready(*keys):
        return max(when[key] for k in keys for key in when if key[0] == number[k])

    needs = [[(ROWS, 0), (BIAS, 0)], []] + [[(QKV, part) for part in range(3)], []] + [[(OUT, 0), (BIAS, 1)]]
    needs += [[] for _ in range(tiles - 1)]
    needs += [[(UP, part), (DOWN, part)] for part in range(tiles)] + [[]]
    assert step.heads_steps == 2
    rounds, taken = [], 0
    for need in needs:
        mine = []
        if need:
            limit = ready(*need)
            while taken < len(events) and events[taken][0] <= limit:
                mine.append(events[taken][1:])
                taken += 1
        rounds.append((mine, need))
    rest = [event[1:] for event in events[taken:]]
    n_rounds = len(rounds)
    n_kept = len(step.kept(slots))

    def kernel(*refs):
        lengths_ref, slope_ref, norm_refs = refs[0], refs[1], refs[2:6]
        refs = refs[6:]
        ins, bias_ins, held_refs = refs[:4], refs[4:6], refs[6:8]
        outs, bias_outs, row_refs = refs[8:12], refs[12:14], refs[14 : 14 + seqs]
        kept_refs = refs[14 + seqs : 14 + seqs + n_kept]
        y_ref = refs[14 + seqs + n_kept]
        stage, qv_bias, ub_bias, x_send, x_recv, c_send, c_recv, u_send, u_recv, d_send, d_recv, l_sem, b_sem = refs[
            15 + seqs + n_kept : 28 + seqs + n_kept
        ]
        t, c, z, last, core, cross, above, below = neighbours()
        section = lax.axis_index("section")
        greet(c, z, chips, core, cross)
        paired = [item for pair in zip(ins, outs) for item in pair]
        step.bind(
            row_refs[0], paired, qv_bias, ub_bias, slope_ref, norm_refs, 0, kept_refs, refs[28 + seqs + n_kept :]
        )

        def span(part):
            return block(part, shard_rows)

        def bias_part(m, side):
            return bias_outs[m].at[:, pl.ds(side * bias_widths[m], bias_widths[m])]

        def piece(side, index, chip, on):
            kind, part, pieces = plan[index]
            place = chip * 2 + on if pieces == groups else on
            ref = (ins, outs)[side][kind]
            if kind == QKV:
                return ref.at[part, block(place, width // pieces)]
            if kind == OUT:
                return ref.at[block(place, local // pieces)]
            cols = pl.ds(part * ft, ft)
            if kind == DOWN:
                return ref.at[block(place, width // pieces), cols]
            per = pieces // 2
            return ref.at[place // per, block(lax.rem(place, per), width // per), cols]

        def cross_copy(index, held_ref=None):
            kind, m, pieces = plan[index]
            if kind == ROWS:
                src = (held_refs[0] if held_ref is None else held_ref).at[(1 - t) * seqs + m]
                dst = row_refs[m].at[span(t)]
            elif kind == BIAS:
                src, dst = bias_ins[m], bias_part(m, 1)
            else:
                src, dst = piece(0, index, z, c), piece(1, index, z, c)
            return pltpu.make_async_remote_copy(
                src_ref=src, dst_ref=dst, send_sem=x_send.at[index], recv_sem=x_recv.at[index],
                device_id=cross, device_id_type=MESH,
            )

        def pass_on(index, chip, send, recv, device):
            place = piece(1, index, chip, c)
            return pltpu.make_async_remote_copy(
                src_ref=place, dst_ref=place, send_sem=send.at[index, chip], recv_sem=recv.at[index, chip],
                device_id=device, device_id_type=MESH,
            )

        def got(index, chip, on, sem):
            arrived(piece(1, index, chip, on), sem)

        for m in range(2):
            copy(bias_ins[m], bias_part(m, 0), b_sem.at[m]).start()
        for index in range(n):
            if plan[index][0] == ROWS:
                for turn in range(2):
                    @pl.when(section == turn)
                    def _(index=index, turn=turn):
                        cross_copy(index, held_refs[turn]).start()
            else:
                cross_copy(index).start()
        for turn in range(2):
            @pl.when(section == turn)
            def _(turn=turn):
                copy(held_refs[turn].at[pl.ds(t * seqs, seqs)], stage, l_sem.at[0]).start()

        @pl.when(section == 0)
        def _():
            for k in range(2):
                step.start_w(jnp.int32(k))
            step.start_o(0)
            for k in range(2):
                step.start_f(jnp.int32(k))
            fill_distance(step.dist, lengths_ref[t * seqs])

        arrived(stage, l_sem.at[0])
        for m in range(seqs):
            copy(stage.at[m], row_refs[m].at[span(t)], l_sem.at[m]).start()
        for m in range(seqs):
            arrived(stage.at[m], l_sem.at[m])
        for m in range(2):
            copy(bias_ins[m], bias_part(m, 0), b_sem.at[m]).wait()

        def handle(index, hop):
            kind, m, pieces = plan[index]
            if kind == ROWS:
                arrived(row_refs[m].at[span(1 - t)], x_recv.at[index])
            elif kind == BIAS:
                arrived(bias_part(m, 1), x_recv.at[index])
            elif hop == 0:
                got(index, z, c, x_recv.at[index])
                if pieces == groups:
                    @pl.when(z < last)
                    def _():
                        pass_on(index, z, u_send, u_recv, above).start()

                    @pl.when(z > 0)
                    def _():
                        pass_on(index, z, d_send, d_recv, below).start()

                pass_on(index, z, c_send, c_recv, core).start()
            else:
                @pl.when(z - hop >= 0)
                def _():
                    got(index, z - hop, c, u_recv.at[index, z - hop])

                    @pl.when(z < last)
                    def _():
                        pass_on(index, z - hop, u_send, u_recv, above).start()

                    pass_on(index, z - hop, c_send, c_recv, core).start()

                @pl.when(z + hop <= last)
                def _():
                    got(index, z + hop, c, d_recv.at[index, z + hop])

                    @pl.when(z > 0)
                    def _():
                        pass_on(index, z + hop, d_send, d_recv, below).start()

                    pass_on(index, z + hop, c_send, c_recv, core).start()

        def from_core(key):
            index = number[key]
            kind, m, pieces = plan[index]
            if pieces == groups:
                for chip in range(chips):
                    got(index, chip, 1 - c, c_recv.at[index, chip])
            elif pieces:
                got(index, z, 1 - c, c_recv.at[index, z])

        @pl.loop(0, n_rounds)
        def _(tau):
            for number_, (mine, need) in enumerate(rounds):
                if not (mine or need):
                    continue

                @pl.when(tau == number_)
                def _(number_=number_, mine=mine, need=need):
                    for index, hop in mine:
                        handle(index, hop)
                    for key in need:
                        from_core(key)
                    for key in need:
                        if key == (BIAS, 0):
                            @pl.when(section == 0)
                            def _():
                                step.start_x()
                                copy(bias_outs[0], qv_bias, b_sem.at[0]).start()
                                copy(bias_outs[0], qv_bias, b_sem.at[0]).wait()
                                arrived(step.x, step.x_sem)
                        elif key == (QKV, 2):
                            @pl.when(section == 0)
                            def _():
                                for k in range(2, 4):
                                    step.start_w(jnp.int32(k))
                        elif key == (OUT, 0):
                            @pl.when(section == 0)
                            def _():
                                step.start_o(1)
                        elif key == (BIAS, 1):
                            @pl.when(section == 0)
                            def _():
                                copy(bias_outs[1], ub_bias, b_sem.at[1]).start()
                                copy(bias_outs[1], ub_bias, b_sem.at[1]).wait()
                        elif key[0] == DOWN:
                            @pl.when(section == 0)
                            def _(key=key):
                                step.start_f(jnp.int32(tiles + key[1]))

            @pl.when(section == 0)
            def _():
                @pl.when(tau < 4)
                def _():
                    step.attention_step(tau, 2)

                @pl.when(tau == 4)
                def _():
                    step.middle()

                @pl.when(tau > 4)
                def _():
                    step.ffn_step(tau - 5, tiles)

        @pl.when(section == 0)
        def _():
            step.finish(y_ref)

        for index, hop in rest:
            handle(index, hop)
        for index in range(n):
            kind, part, pieces = plan[index]
            cross_copy(index).wait_send()
            if pieces == 2:
                pass_on(index, z, c_send, c_recv, core).wait_send()
            if pieces != groups:
                continue
            for chip in range(chips):
                pass_on(index, chip, c_send, c_recv, core).wait_send()

                @pl.when((chip <= z) & (z < last))
                def _(chip=chip):
                    pass_on(index, chip, u_send, u_recv, above).wait_send()

                @pl.when((chip >= z) & (z > 0))
                def _(chip=chip):
                    pass_on(index, chip, d_send, d_recv, below).wait_send()

    sem = pltpu.SemaphoreType.DMA
    return pl.pallas_call(
        kernel,
        in_specs=[SMEM, SMEM] + NORM_SPECS + [ANY] * 8,
        out_specs=[ANY] * (7 + seqs + n_kept),
        out_shape=[jax.ShapeDtypeStruct(w.shape, BF) for w in weights]
        + [jax.ShapeDtypeStruct((2, 2 * size_), BF) for size_ in bias_widths]
        + [jax.ShapeDtypeStruct((rows, width), BF)] * seqs
        + [jax.ShapeDtypeStruct(*shape) for shape in step.kept(slots)]
        + [jax.ShapeDtypeStruct((rows, width), BF)],
        scratch_shapes=[pltpu.VMEM((seqs, shard_rows, width), BF)]
        + [pltpu.VMEM((2, 2 * size_), BF) for size_ in bias_widths]
        + [sem((n,)), sem((n,))]
        + [sem((n, chips))] * 6
        + [sem((seqs,)), sem((2,))]
        + step.scratch(),
        compiler_params=pltpu.CompilerParams(collective_id=1, has_side_effects=True, vmem_limit_bytes=VMEM_LIMIT),
        cost_estimate=pl.CostEstimate(flops=step.flops(), bytes_accessed=90 << 20, transcendentals=0),
        name="fetch_and_forward",
    )(lengths, slopes, *norms, *weights, *biases, inputs, cotangent)


def norm_back(grad_z, u, rstd, gain):
    t = grad_z * gain
    return rstd * (t - jnp.mean(t, axis=1, keepdims=True) - u * jnp.mean(t * u, axis=1, keepdims=True))


def row_sum(values):
    return jnp.sum(values, axis=0, keepdims=True)


def backward_and_reduce(grad, kept, back, x_all, weights, slopes, norms, lengths, sums, low_grad, second, chips):
    q, k_, v, mixed_all, lse, act, slope, hidden_all, normed_all, u1, u2, r1, r2 = kept
    gg0, gg1, gl, ga, gq, gk, gv = back
    rows, width = grad.shape
    local, units = weights[0].shape[2], weights[4].shape[2]
    ft = CW
    tiles = units // ft
    heads_steps = local // CW
    seqs = 2
    bt = 128
    lefts = [gl, normed_all, x_all, ga]
    rights = [hidden_all, gg0, gg1, gq, gk, gv, mixed_all]
    group_of = [0, 1, 1, 2, 2, 2, 3]
    member_of = [0, 0, 1, 0, 1, 2, 0]
    half = width // 2
    quarter = half // 2
    per_pair = 2 * ft // bt
    pairs = tiles // 2
    ffn_blocks = 3 * per_pair * pairs
    head_blocks = local // bt
    total = ffn_blocks + 4 * head_blocks
    ring, mines, gives = 4, CORE_LAG + 1, 4
    ahead_of = 4
    drain = CORE_LAG + CROSS_LAG + 2 * (chips - 1) * CHAIN_LAG + 1
    shard_rows = rows // 2
    norm_at = 2 * tiles
    head_at = norm_at + 1
    end_at = head_at + 5 * 2 * heads_steps
    x_flip, ga_flip = ffn_blocks - per_pair, ffn_blocks + per_pair
    up_rows = units // width
    vec_shape = (6 + 4 * up_rows + 2, width)
    spread = 41
    last_turn = ahead_of - (ahead_of - end_at) * spread // (end_at + 1 - ahead_of) + 1
    assert spread >= end_at + 1 - ahead_of and last_turn < ahead_of + ffn_blocks - ring

    def kernel(*refs):
        lengths_ref, slope_ref, norm_refs, sum_refs = refs[0], refs[1], refs[2:6], refs[6:15]
        refs = refs[12:]
        g_hbm, q_hbm, k_hbm, v_hbm, lse_hbm, a_hbm, b_hbm, u1_hbm, u2_hbm, r1_hbm, r2_hbm = refs[3:14]
        (qkv_own_ref, qkv_oth_ref, o_own_ref, o_oth_ref, up_own_ref, up_oth_ref, down_own_ref, down_oth_ref) = refs[14:22]
        left_refs, right_refs = refs[22:26], refs[26:33]
        low_grad_ref, second_ref = refs[33:35]
        outs, sums_out, rows_out = refs[35:39], refs[39], refs[40]
        fresh = refs[41:46]
        gx_out, gxl_out = refs[46:48]
        (
            acc, from_x, from_z, flip, stage, tile, mine, give, vec, vec_in, vec_all,
            g_ref, u_ref, r_ref, low_ref, gacc_ref, w_ref, o_ref, qkv_ref, gqkv_ref, lse_ref, gm_ref, gs_ref, dist_ref,
            part_sums, ub_sums, qv_sums,
            tile_sem, stage_sem, give_send, core_recv, x_send, x_recv, z_send, z_recv, f_send, f_recv,
            store_sem, out_send, out_recv, v_send, v_recv, r_send, r_recv,
            g_sem, w_sem, t_sem, e_sem,
        ) = refs[48:]
        final = from_x
        t, c, z, last, core, cross, above, below = neighbours()
        section = lax.axis_index("section")
        first = section == 0
        greet(c, z, chips, core, cross)
        fresh_of = {1: fresh[0].at[0], 2: fresh[1].at[0], 3: fresh[2], 4: fresh[3], 5: fresh[4]}
        vec_w = norm_rows(norm_refs)

        def remote(src, dst, send, recv, device):
            return pltpu.make_async_remote_copy(
                src_ref=src, dst_ref=dst, send_sem=send, recv_sem=recv, device_id=device, device_id_type=MESH
            )

        def valid(k):
            return (k >= 0) & (k < total)

        def member(k, visit):
            for m in range(3):
                @pl.when((k < ffn_blocks) & (lax.rem(k, 3 * per_pair) // per_pair == m))
                def _(m=m):
                    visit(m, k // (3 * per_pair) * per_pair + lax.rem(k, per_pair))

            for m in range(3, 7):
                base = ffn_blocks + (m - 3) * head_blocks

                @pl.when((k >= base) & (k < base + head_blocks))
                def _(m=m, base=base):
                    visit(m, k - base)

        def load_tile(k):
            at = lax.rem(k, ring)

            def visit(m, j):
                count = right_refs[m].shape[2] // (2 * bt)
                for side in range(2):
                    cols = block(side * count + j, bt)
                    where = pl.ds(side * bt, bt)
                    copy(right_refs[m].at[0, :, cols], tile.at[at, 0, :, where], tile_sem.at[at]).start()
                    if m not in fresh_of:
                        copy(right_refs[m].at[1, :, cols], tile.at[at, 1, :, where], tile_sem.at[at]).start()
                        continue

                    @pl.when(first)
                    def _(cols=cols, where=where):
                        copy(fresh_of[m].at[:, cols], tile.at[at, 1, :, where], tile_sem.at[at]).start()

                    @pl.when(section == 1)
                    def _(cols=cols, where=where):
                        copy(right_refs[m].at[1, :, cols], tile.at[at, 1, :, where], tile_sem.at[at]).start()

            member(k, visit)

        def take_left(g, at, mine_low):
            copy(left_refs[g].at[0], stage.at[0], stage_sem.at[0]).start()
            if mine_low is None:
                copy(left_refs[g].at[1], stage.at[1], stage_sem.at[1]).start()
                arrived(stage.at[1], stage_sem.at[1])
            else:
                @pl.when(first)
                def _():
                    stage[1] = low_ref[mine_low]

                @pl.when(section == 1)
                def _():
                    copy(left_refs[g].at[1], stage.at[1], stage_sem.at[1]).start()
                    arrived(stage.at[1], stage_sem.at[1])

            arrived(stage.at[0], stage_sem.at[0])
            for m in range(seqs):
                flip[at, :, m * rows : (m + 1) * rows] = stage[m].T

        def place_of(u):
            within = lax.rem(u, 4)
            side = within // 2
            return side, u // 4 * 2 + lax.rem(within, 2)

        def start_f(u):
            at = lax.rem(u, 2)
            side, j = place_of(u)
            pick(side * tiles + j, tiles, (up_own_ref, down_own_ref), (up_oth_ref, down_oth_ref),
                 lambda ref, jj: [(ref[0].at[:, :, block(jj, ft)], w_ref.at[at, pl.ds(0, 2)], w_sem.at[at, 0]),
                                  (ref[1].at[:, block(jj, ft)], w_ref.at[at, 2], w_sem.at[at, 1])])
            for n, ref in enumerate((a_hbm, b_hbm)):
                copy(ref.at[1, :, block(side * tiles + j, ft)], qkv_ref.at[at, n], w_sem.at[at, 2 + n]).start()

        def write_tile(u):
            at = lax.rem(u, 2)
            side, j = place_of(u)
            return [copy(gqkv_ref.at[at, n], fresh[n].at[0, :, block(side * tiles + j, ft)], t_sem.at[at, n]) for n in range(2)]

        def start_w(i):
            at = lax.rem(i, 2)
            pick(i, heads_steps, (qkv_own_ref, o_own_ref), (qkv_oth_ref, o_oth_ref),
                 lambda ref, j: [(ref[0].at[:, :, block(j, CW)], w_ref.at[at], w_sem.at[at, 0]),
                                 (ref[1].at[block(j, CW)], o_ref.at[at], w_sem.at[at, 1])])
            for n, ref in enumerate((q_hbm, k_hbm, v_hbm)):
                copy(ref.at[1, :, block(i, CW)], qkv_ref.at[at, n], w_sem.at[at, 2 + n]).start()
            copy(lse_hbm.at[1, i], lse_ref.at[at], w_sem.at[at, 5]).start()

        def write_heads(i):
            at = lax.rem(i, 2)
            return [copy(gqkv_ref.at[at, n], fresh[2 + n].at[:, block(i, CW)], t_sem.at[at, n]) for n in range(3)]

        def norm_load(index, u_hbm, r_hbm):
            return [copy(u_hbm.at[1], u_ref, g_sem.at[index]), copy(r_hbm.at[1], r_ref, g_sem.at[index + 1])]

        def begin():
            copy(g_hbm, g_ref, g_sem.at[0]).start()
            for item in norm_load(1, u2_hbm, r2_hbm):
                item.start()
            start_f(jnp.int32(0))
            start_f(jnp.int32(1))
            copy(g_hbm, g_ref, g_sem.at[0]).wait()
            for item in norm_load(1, u2_hbm, r2_hbm):
                item.wait()
            totals = [jnp.zeros((1, width), F32)] * 3
            for rs in halves(rows):
                grad_y = g_ref[rs, :].astype(F32)
                u = u_ref[rs, :].astype(F32)
                grad_c = norm_back(grad_y, u, r_ref[rs, 0:1], vec_w[4])
                gacc_ref[rs, :] = grad_c
                low_ref[0, rs, :] = grad_c.astype(BF)
                for index, values in enumerate((grad_y * u, grad_y, grad_c)):
                    totals[index] += row_sum(values)
            for index in range(3):
                part_sums[index : index + 1, :] = totals[index]
            for item in norm_load(1, u1_hbm, r1_hbm):
                item.start()

        def ffn_unit(u):
            at = lax.rem(u, 2)

            @pl.when(u >= 1)
            def _():
                for item in write_tile(u - 1):
                    item.wait()

            arrived(w_ref.at[at, pl.ds(0, 2)], w_sem.at[at, 0])
            arrived(w_ref.at[at, 2], w_sem.at[at, 1])
            for n in range(2):
                arrived(qkv_ref.at[at, n], w_sem.at[at, 2 + n])
            gh = dot(low_ref[0], w_ref[at, 2])
            g0 = (gh * qkv_ref[at, 1].astype(F32)).astype(BF)
            g1 = (gh * qkv_ref[at, 0].astype(F32)).astype(BF)
            gqkv_ref[at, 0] = g0
            gqkv_ref[at, 1] = g1
            side, j = place_of(u)
            cols = block(side * tiles + j, ft)
            ub_sums[0:1, cols] = row_sum(g0.astype(F32))
            ub_sums[1:2, cols] = row_sum(g1.astype(F32))
            gacc_ref[...] += dot(g0, w_ref[at, 0], NT) + dot(g1, w_ref[at, 1], NT)

            @pl.when(u + 2 < 2 * tiles)
            def _():
                start_f(u + 2)

            for item in write_tile(u):
                item.start()

        def norm_unit():
            for item in write_tile(jnp.int32(2 * tiles - 1)):
                item.wait()
            for i in range(2):
                start_w(jnp.int32(i))
            fill_distance(dist_ref, lengths_ref[t * seqs + 1])
            for item in norm_load(1, u1_hbm, r1_hbm):
                item.wait()
            totals = [jnp.zeros((1, width), F32)] * 3
            for rs in halves(rows):
                grad_n = gacc_ref[rs, :]
                u = u_ref[rs, :].astype(F32)
                grad_a = norm_back(grad_n, u, r_ref[rs, 0:1], vec_w[1])
                low_ref[1, rs, :] = grad_a.astype(BF)
                gacc_ref[rs, :] = grad_a
                for index, values in enumerate((grad_n * u, grad_n, grad_a)):
                    totals[index] += row_sum(values)
            for index in range(3):
                part_sums[3 + index : 4 + index, :] = totals[index]

        def head_unit(a):
            i = a // 5
            phase = lax.rem(a, 5)
            pair = phase // 2
            at = lax.rem(i, 2)
            scale = BF(1.0 / math.sqrt(HD))
            cols = block(lax.rem(pair, 2), 2 * HD)

            @pl.when(phase == 0)
            def _():
                for index, ref in enumerate(
                    (w_ref.at[at], o_ref.at[at], qkv_ref.at[at, 0], qkv_ref.at[at, 1], qkv_ref.at[at, 2], lse_ref.at[at])
                ):
                    arrived(ref, w_sem.at[at, index])

                @pl.when(i >= 2)
                def _():
                    for item in write_heads(i - 2):
                        item.wait()

                gm_ref[...] = dot(low_ref[1], o_ref[at], NT).astype(BF)

            @pl.when((phase == 0) | (phase == 2))
            def _():
                query2 = qkv_ref[at, 0, :, cols] * scale
                key2 = qkv_ref[at, 1, :, cols]
                value2 = qkv_ref[at, 2, :, cols]
                gm2 = gm_ref[:, cols]
                parts = []
                for head in range(2):
                    here = slice(head * HD, (head + 1) * HD)
                    gm = gm2[:, here]
                    scores = dot(key2[:, here], query2[:, here], NT)
                    scores = scores - dist_ref[...] * slope_of(slope_ref, i * PER + pair * 2 + head)
                    likely = jnp.exp(scores - lse_ref[at, pl.ds(pair * 2 + head, 1), :])
                    parts.append(dot(likely.astype(BF), gm).astype(BF))
                    tt = likely * dot(value2[:, here], gm, NT)
                    inner = jnp.sum(tt, axis=0, keepdims=True)
                    gs_ref[head] = (tt - likely * inner).astype(BF)
                gqkv_ref[at, 2, :, cols] = jnp.concatenate(parts, axis=1)

            @pl.when((phase == 1) | (phase == 3))
            def _():
                query2 = qkv_ref[at, 0, :, cols] * scale
                key2 = qkv_ref[at, 1, :, cols] * scale
                parts = [[], []]
                for head in range(2):
                    here = slice(head * HD, (head + 1) * HD)
                    gs = gs_ref[head]
                    parts[1].append(dot(gs, query2[:, here]).astype(BF))
                    parts[0].append(dot(gs, key2[:, here], TN).astype(BF))
                for n in range(2):
                    gqkv_ref[at, n, :, cols] = jnp.concatenate(parts[n], axis=1)

            @pl.when(phase == 4)
            def _():
                for index, n in enumerate((0, 2)):
                    qv_sums[index : index + 1, block(i, CW)] = row_sum(gqkv_ref[at, n].astype(F32))
                gacc_ref[...] += (
                    dot(gqkv_ref[at, 0], w_ref[at, 0], NT)
                    + dot(gqkv_ref[at, 1], w_ref[at, 1], NT)
                    + dot(gqkv_ref[at, 2], w_ref[at, 2], NT)
                )

                @pl.when(i + 2 < 2 * heads_steps)
                def _():
                    start_w(i + 2)

                for item in write_heads(i):
                    item.start()

        def add_sums(norm_part, ub_part, qv_part):
            vec[0, 0:6] += norm_part[0:6]
            for own in range(2):
                @pl.when(t == own)
                def _(own=own):
                    for n in range(2):
                        for side in range(2):
                            place = own if side == 0 else 1 - own
                            for j in range(up_rows):
                                at = 6 + (2 * n + place) * up_rows + j
                                start = side * units + j * width
                                vec[0, at : at + 1] += ub_part[n : n + 1, start : start + width]
                            at = 6 + 4 * up_rows + n
                            cols = slice(place * local, (place + 1) * local)
                            vec[0, at : at + 1, cols] += qv_part[n : n + 1, side * local : (side + 1) * local]

        ends = [(g_ref, gxl_out), (gacc_ref, gx_out)]

        def end_unit():
            for i in (2 * heads_steps - 2, 2 * heads_steps - 1):
                for item in write_heads(jnp.int32(i)):
                    item.wait()
            g_ref[...] = gacc_ref[...].astype(BF)
            for index, item in enumerate(ends):
                copy(*item, e_sem.at[index]).start()
            add_sums(part_sums, ub_sums, qv_sums)
            for index, item in enumerate(ends):
                copy(*item, e_sem.at[index]).wait()

        vec[0] = jnp.zeros(vec_shape, F32)

        @pl.when(first)
        def _():
            begin()
            add_sums(*sum_refs[:3])

        @pl.when(section == 1)
        def _():
            add_sums(*sum_refs[3:6])
            add_sums(*sum_refs[6:9])

        take_left(0, 0, 0)
        vec_core = remote(vec.at[0], vec_in.at[0], v_send.at[0], v_recv.at[0], core)
        vec_cross = remote(vec.at[1], vec_in.at[1], v_send.at[1], v_recv.at[1], cross)

        def row_copy(m, source):
            return remote(
                source.at[block(1 - t, shard_rows)], rows_out.at[m], r_send.at[m], r_recv.at[m], cross
            )

        row_plan = [(0, 0, low_grad_ref, True), (0, 1, gxl_out, False), (1, 1, second_ref, True)]
        for number, m, source, early in row_plan:
            if early:
                @pl.when(section == number)
                def _(m=m, source=source):
                    row_copy(m, source).start()

        def unit_at(turn):
            later = ahead_of + (turn - ahead_of) * (end_at + 1 - ahead_of) // spread
            return jnp.where(turn < ahead_of, turn, later)

        up = pl.ds(0, quarter)
        down = pl.ds(quarter, quarter)
        sides = ((up, 0, z, above, below), (down, 1, last - z, below, above))

        @pl.loop(0, ahead_of + total + drain)
        def _(turn):
            s = turn - ahead_of

            unit = unit_at(turn)

            @pl.when(first & (unit != unit_at(turn - 1)))
            def _():
                @pl.when(unit < norm_at)
                def _():
                    ffn_unit(unit)

                @pl.when(unit == norm_at)
                def _():
                    norm_unit()

                @pl.when((unit >= head_at) & (unit < end_at))
                def _():
                    head_unit(unit - head_at)

                @pl.when(unit == end_at)
                def _():
                    end_unit()

            @pl.when(s == 0)
            def _():
                for k in range(ring - 1):
                    load_tile(jnp.int32(k))

            @pl.when(valid(s))
            def _():
                @pl.when(s == per_pair - 2)
                def _():
                    take_left(1, 1, None)

                @pl.when(s == x_flip)
                def _():
                    take_left(2, 0, None)

                @pl.when(s == ga_flip)
                def _():
                    take_left(3, 1, 1)

                at = lax.rem(s, ring)
                arrived(tile.at[at], tile_sem.at[at])
                give_at = lax.rem(s, gives)

                @pl.when(s >= gives)
                def _():
                    arrived(give.at[give_at], give_send.at[give_at])

                ffn_flip = jnp.where(lax.rem(s, 3 * per_pair) // per_pair == 0, 0, 1)
                which = jnp.where(s < ffn_blocks, ffn_flip, jnp.where(s < ffn_blocks + 3 * head_blocks, 0, 1))
                for place, store, spot in ((1 - c, give, give_at), (c, mine, lax.rem(s, mines))):
                    here = block(place, half)
                    product = dot(flip[which, here, :rows], tile[at, 0])
                    for m in range(1, seqs):
                        product += dot(flip[which, here, m * rows : (m + 1) * rows], tile[at, m])
                    store[spot, 1] = product[:, :bt].astype(BF)
                    store[spot, 0] = product[:, bt:].astype(BF)

            @pl.when((s >= 0) & (s + ring - 1 < total))
            def _():
                load_tile(s + ring - 1)

            k1 = s - CORE_LAG

            @pl.when(valid(k1))
            def _():
                arrived(acc.at[k1], core_recv.at[k1])
                at = lax.rem(k1, mines)
                for side in range(2):
                    acc[k1, side] = acc[k1, side] + mine[at, side]

            k2 = k1 - CROSS_LAG

            @pl.when(valid(k2))
            def _():
                arrived(from_x.at[k2], x_recv.at[k2])
                acc[k2, 1] = acc[k2, 1] + from_x[k2]

            for rows_, way, place, ahead, behind in sides:
                k3 = k2 - CHAIN_LAG * place

                @pl.when(valid(k3) & (place > 0))
                def _(rows_=rows_, way=way, k3=k3):
                    arrived(from_z.at[k3, rows_], z_recv.at[way, k3])
                    acc[k3, 1, rows_] = acc[k3, 1, rows_] + from_z[k3, rows_]

                k4 = k2 - CHAIN_LAG * (2 * last - place)

                @pl.when(valid(k4) & (place == last))
                def _(rows_=rows_, k4=k4):
                    final[k4, rows_] = acc[k4, 1, rows_]

                @pl.when(valid(k4) & (place < last))
                def _(rows_=rows_, way=way, k4=k4):
                    arrived(final.at[k4, rows_], f_recv.at[way, k4])

            @pl.when(valid(s))
            def _():
                at = lax.rem(s, gives)
                remote(give.at[at], acc.at[s], give_send.at[at], core_recv.at[s], core).start()

            @pl.when(valid(k1))
            def _():
                remote(acc.at[k1, 0], from_x.at[k1], x_send, x_recv.at[k1], cross).start()

            for number, m, source, early in row_plan:
                if not early:
                    @pl.when((k1 == total - 1) & (section == number))
                    def _(m=m, source=source):
                        row_copy(m, source).start()

            for rows_, way, place, ahead, behind in sides:
                k3 = k2 - CHAIN_LAG * place

                @pl.when(valid(k3) & (place < last))
                def _(rows_=rows_, way=way, k3=k3, ahead=ahead):
                    remote(acc.at[k3, 1, rows_], from_z.at[k3, rows_], z_send.at[way], z_recv.at[way, k3], ahead).start()

                k4 = k2 - CHAIN_LAG * (2 * last - place)

                @pl.when(valid(k4) & (place > 0))
                def _(rows_=rows_, way=way, k4=k4, behind=behind):
                    remote(final.at[k4, rows_], final.at[k4, rows_], f_send.at[way], f_recv.at[way, k4], behind).start()

            k5 = k2 - CHAIN_LAG * 2 * last

            @pl.when(valid(k5))
            def _():
                def visit(m, j):
                    dst = outs[group_of[m]].at[member_of[m], block(c, half), block(j, bt)]
                    copy(final.at[k5], dst, store_sem).start()
                    remote(final.at[k5], dst, out_send, out_recv, core).start()

                member(k5, visit)

            @pl.when(turn == last_turn + 1)
            def _():
                vec_core.start()

            @pl.when(turn == last_turn + 6)
            def _():
                vec_core.wait_recv()
                vec[1] = vec[0] + vec_in[0]

            @pl.when(turn == last_turn + 7)
            def _():
                vec_cross.start()

            @pl.when(turn == last_turn + 13)
            def _():
                vec_cross.wait_recv()
                vec_all[z] = vec[1] + vec_in[1]

            @pl.when(turn == last_turn + 14)
            def _():
                for shift in range(1, chips):
                    to = lax.rem(z + shift, chips)
                    remote(
                        vec_all.at[z], vec_all.at[z], v_send.at[1 + shift], v_recv.at[1 + shift], {"dp": to * 2 + c}
                    ).start()

        for number, m, source, early in row_plan:
            @pl.when(section == number)
            def _(m=m, source=source):
                row_copy(m, source).wait()

        vec_core.wait_send()
        vec_cross.wait_send()
        for shift in range(1, chips):
            origin = lax.rem(z + chips - shift, chips)
            arrived(vec_all.at[origin], v_recv.at[1 + shift])
            arrived(vec_all.at[z], v_send.at[1 + shift])
        whole = vec_all[0]
        for chip in range(1, chips):
            whole += vec_all[chip]
        sums_out[...] = whole
        for at in range(gives):
            arrived(give.at[at], give_send.at[at])
        arrived(acc.at[:, 0], x_send)
        for rows_, way, place, ahead, behind in sides:
            @pl.when(place < last)
            def _(rows_=rows_, way=way):
                arrived(from_z.at[:, rows_], z_send.at[way])

            @pl.when(place > 0)
            def _(rows_=rows_, way=way):
                arrived(final.at[:, rows_], f_send.at[way])

        arrived(final, out_send)
        arrived(final, store_sem)
        arrived(final, out_recv)

    sem = pltpu.SemaphoreType.DMA
    flops = 2 * seqs * rows * width * 2 * bt * total
    members = [member_of[index] for index in range(7)]
    shapes = [(sum(g == index for g in group_of), width, rights[group_of.index(index)].shape[2] // 2) for index in range(4)]
    return pl.pallas_call(
        kernel,
        in_specs=[SMEM, SMEM] + NORM_SPECS + [WHOLE] * 9 + [ANY] * 32,
        out_specs=[ANY] * 4 + [WHOLE] + [ANY] * 8,
        out_shape=[jax.ShapeDtypeStruct(s, BF) for s in shapes]
        + [jax.ShapeDtypeStruct(vec_shape, F32), jax.ShapeDtypeStruct((seqs, shard_rows, width), BF)]
        + [jax.ShapeDtypeStruct(act.shape, BF)] * 2
        + [jax.ShapeDtypeStruct((rows, 2 * local), BF)] * 3
        + [jax.ShapeDtypeStruct((rows, width), F32), jax.ShapeDtypeStruct((rows, width), BF)],
        scratch_shapes=[
            pltpu.VMEM((total, 2, half, bt), BF),
            pltpu.VMEM((total, half, bt), BF),
            pltpu.VMEM((total, half, bt), BF),
            pltpu.VMEM((2, width, seqs * rows), BF),
            pltpu.VMEM((seqs, rows, width), BF),
            pltpu.VMEM((ring, seqs, rows, 2 * bt), BF),
            pltpu.VMEM((mines, 2, half, bt), BF),
            pltpu.VMEM((gives, 2, half, bt), BF),
            pltpu.VMEM((2,) + vec_shape, F32),
            pltpu.VMEM((2,) + vec_shape, F32),
            pltpu.VMEM((chips,) + vec_shape, F32),
            pltpu.VMEM((rows, width), BF),
            pltpu.VMEM((rows, width), BF),
            pltpu.VMEM((rows, 128), F32),
            pltpu.VMEM((2, rows, width), BF),
            pltpu.VMEM((rows, width), F32),
            pltpu.VMEM((2, 3, width, CW), BF),
            pltpu.VMEM((2, CW, width), BF),
            pltpu.VMEM((2, 3, rows, CW), BF),
            pltpu.VMEM((2, 3, rows, CW), BF),
            pltpu.VMEM((2, 8, rows), F32),
            pltpu.VMEM((rows, CW), BF),
            pltpu.VMEM((2, rows, rows), BF),
            pltpu.VMEM((rows, rows), F32),
            pltpu.VMEM((8, width), F32),
            pltpu.VMEM((2, 2 * units), F32),
            pltpu.VMEM((2, 2 * local), F32),
            sem((ring,)), sem((2,)), sem((gives,)), sem((total,)), sem, sem((total,)),
            sem((2,)), sem((2, total)), sem((2,)), sem((2, total)),
            sem, sem, sem, sem((chips + 1,)), sem((chips + 1,)), sem((seqs,)), sem((seqs,)),
            sem((3,)), sem((2, 6)), sem((2, 3)), sem((2,)),
        ],
        input_output_aliases={20: 6, 21: 7},
        compiler_params=pltpu.CompilerParams(
            collective_id=0, has_side_effects=True, vmem_limit_bytes=67_000_000
        ),
        cost_estimate=pl.CostEstimate(flops=flops, bytes_accessed=100 << 20, transcendentals=0),
        name="backward_and_reduce",
    )(
        lengths, slopes, *norms, *sums, grad, q, k_, v, lse, act, slope, u1, u2, r1, r2, *weights, *lefts, *rights,
        low_grad, second
    )


def exchange_rows(outputs, deps):
    seqs = len(outputs)
    rows, width = outputs[0].shape
    shard_rows = rows // 2
    n_in = seqs + len(deps)

    def kernel(*refs):
        y_refs, out_ref = refs[:seqs], refs[n_in]
        stage, send, recv, l_sem = refs[n_in + 1 :]
        t = lax.axis_index("tensor")
        cross = {"tensor": 1 - t}
        barrier = pltpu.get_barrier_semaphore()
        pl.semaphore_signal(barrier, inc=1, device_id=cross, device_id_type=MESH)
        pl.semaphore_wait(barrier, 1)

        @pl.when(lax.axis_index("section") == 0)
        def _():
            for m in range(seqs):
                pltpu.make_async_remote_copy(
                    src_ref=y_refs[m].at[block(1 - t, shard_rows)], dst_ref=out_ref.at[t * seqs + m],
                    send_sem=send.at[m], recv_sem=recv.at[m], device_id=cross, device_id_type=MESH,
                ).start()
            for m in range(seqs):
                copy(y_refs[m].at[block(t, shard_rows)], stage.at[m], l_sem.at[m]).start()
            for m in range(seqs):
                arrived(stage.at[m], l_sem.at[m])
                copy(stage.at[m], out_ref.at[t * seqs + m], l_sem.at[m]).start()
            for m in range(seqs):
                arrived(stage.at[m], l_sem.at[m])
            for m in range(seqs):
                arrived(out_ref.at[(1 - t) * seqs + m], recv.at[m])
                arrived(stage.at[m], send.at[m])

    sem = pltpu.SemaphoreType.DMA
    return pl.pallas_call(
        kernel,
        in_specs=[ANY] * n_in,
        out_specs=ANY,
        out_shape=jax.ShapeDtypeStruct((2 * seqs, shard_rows, width), BF),
        scratch_shapes=[pltpu.VMEM((seqs, shard_rows, width), BF), sem((seqs,)), sem((seqs,)), sem((seqs,))],
        compiler_params=pltpu.CompilerParams(collective_id=2, has_side_effects=True),
        cost_estimate=pl.CostEstimate(flops=0, bytes_accessed=0, transcendentals=0),
        name="exchange_rows",
    )(*outputs, *deps)


def widen(reduced, row_grads, got, got_second, produced, outputs, sums, units, local):
    shard_rows, width = got.shape[1:]
    seqs = got.shape[0]
    n = len(reduced)
    jobs = []
    for index, array in enumerate(reduced):
        lead, depth, columns = array.shape
        step = 512 * 1024 // columns
        if index == n - 1:
            jobs += [(index, 0, at, depth // 2, columns) for at in range(0, depth, depth // 2)]
        else:
            jobs += [(index, part, at, step, columns) for part in range(lead) for at in range(0, depth, step)]
    jobs += [(n, m, 0, shard_rows, width) for m in range(seqs)] + [(n + 1, m, 0, shard_rows, width) for m in range(seqs)]
    jobs += [(n + 2, m, 0, shard_rows, width) for m in range(2 * seqs)]
    ring = 5
    n_in = n + 3 * seqs + 4
    parts = units // width

    def kernel(*refs):
        ins = refs[:n]
        grad_refs = refs[n : n + 2 * seqs]
        got_ref, got_second_ref, produced_ref = refs[n + 2 * seqs : n + 2 * seqs + 3]
        y_refs, sums_ref = refs[n + 2 * seqs + 3 : n_in - 1], refs[n_in - 1]
        outs = refs[n_in : n_in + n + 2]
        qv_ref, out_bias_ref, gain_ref, shift_ref, ub_ref, down_bias_ref = refs[n_in + n + 2 : n_in + n + 8]
        shapes = sorted({(j[3], j[4]) for j in jobs if j[0] != n})
        buffers = refs[n_in + n + 8 :]
        wide_rows, in_sem, out_sem = buffers[0], buffers[1], buffers[2]
        low = {s: buffers[3 + 2 * i] for i, s in enumerate(shapes)}
        wide = {s: buffers[4 + 2 * i] for i, s in enumerate(shapes)}
        t = lax.axis_index("tensor")
        section = lax.axis_index("section")

        def load(number):
            index, part, at, rows, columns = jobs[number]
            s = number % ring
            if index < n:
                copy(ins[index].at[part, pl.ds(at, rows)], low[rows, columns].at[s], in_sem.at[s]).start()
            elif index == n:
                for turn in range(2):
                    @pl.when(section == turn)
                    def _(turn=turn):
                        source = grad_refs[turn * seqs + part].at[block(t, shard_rows)]
                        copy(source, wide_rows.at[part], in_sem.at[s]).start()
            elif index == n + 1:
                for number_ in range(2):
                    @pl.when(section == number_)
                    def _(number_=number_):
                        source = got_second_ref.at[seqs] if number_ == 1 and part == 0 else got_ref.at[part]
                        copy(source, low[rows, columns].at[s], in_sem.at[s]).start()
            else:
                @pl.when(section == 0)
                def _():
                    copy(produced_ref.at[part], low[rows, columns].at[s], in_sem.at[s]).start()

                @pl.when(section == 1)
                def _():
                    source = y_refs[part].at[block(t, shard_rows)] if part < seqs else got_second_ref.at[part - seqs]
                    copy(source, low[rows, columns].at[s], in_sem.at[s]).start()

        def store(number):
            index, part, at, rows, columns = jobs[number]
            s = number % ring
            if index < n - 1:
                return copy(wide[rows, columns].at[s], outs[index].at[part, pl.ds(at, rows)], out_sem.at[s])
            if index == n - 1:
                return copy(wide[rows, columns].at[s], outs[index].at[:, pl.ds(at, rows)], out_sem.at[s])
            if index == n:
                return copy(wide_rows.at[part], outs[n].at[t * seqs + part], out_sem.at[s])
            if index == n + 1:
                return copy(wide[rows, columns].at[s], outs[n].at[(1 - t) * seqs + part], out_sem.at[s])
            side, m = divmod(part, seqs)
            spread = (t + side - 2 * t * side) * seqs + m
            return copy(low[rows, columns].at[s], outs[n + 1].at[jnp.where(section == 0, part, spread)], out_sem.at[s])

        for number in range(ring):
            load(number)
        gain_ref[0:1] = sums_ref[3:4]
        gain_ref[1:2] = sums_ref[0:1]
        shift_ref[0:1] = sums_ref[4:5]
        shift_ref[1:2] = sums_ref[1:2]
        out_bias_ref[...] = sums_ref[5:6]
        down_bias_ref[...] = sums_ref[2:3]
        for half in range(2):
            @pl.when(t == half)
            def _(half=half):
                for g in range(2):
                    for j in range(parts):
                        at = 6 + (2 * g + half) * parts + j
                        ub_ref[g : g + 1, j * width : (j + 1) * width] = sums_ref[at : at + 1]
                    at = 6 + 4 * parts + g
                    qv_ref[g : g + 1] = sums_ref[at : at + 1, half * local : (half + 1) * local]

        for number, (index, part, at, rows, columns) in enumerate(jobs):
            s = number % ring
            if index == n:
                arrived(wide_rows.at[part], in_sem.at[s])
            else:
                arrived(low[rows, columns].at[s], in_sem.at[s])
            if number >= ring:
                store(number - ring).wait()
            if index == n - 1:
                wide[rows, columns][s] = low[rows, columns][s].astype(F32).T
            elif index not in (n, n + 2):
                wide[rows, columns][s] = low[rows, columns][s].astype(F32)
            store(number).start()
            if number + ring < len(jobs):
                load(number + ring)
        for number in range(len(jobs) - ring, len(jobs)):
            store(number).wait()

    shapes = sorted({(j[3], j[4]) for j in jobs if j[0] != n})
    square = (reduced[-1].shape[1] // 2, reduced[-1].shape[2])
    last = reduced[-1].shape
    sem = pltpu.SemaphoreType.DMA
    buffers = []
    for s in shapes:
        buffers += [pltpu.VMEM((ring,) + s, BF), pltpu.VMEM((ring,) + ((s[1], s[0]) if s == square else s), F32)]
    return pl.pallas_call(
        kernel,
        in_specs=[ANY] * (n_in - 1) + [WHOLE],
        out_specs=[ANY] * (n + 2) + [WHOLE] * 6,
        out_shape=[jax.ShapeDtypeStruct(r.shape, F32) for r in reduced[:-1]]
        + [jax.ShapeDtypeStruct((last[2], last[1]), F32), jax.ShapeDtypeStruct((2 * seqs, shard_rows, width), F32)]
        + [jax.ShapeDtypeStruct((2 * seqs, shard_rows, width), BF)]
        + [
            jax.ShapeDtypeStruct(shape, F32)
            for shape in ((2, local), (1, width), (2, width), (2, width), (2, units), (1, width))
        ],
        scratch_shapes=[pltpu.VMEM((seqs, shard_rows, width), F32), sem((ring,)), sem((ring,))] + buffers,
        compiler_params=pltpu.CompilerParams(vmem_limit_bytes=VMEM_LIMIT),
        cost_estimate=pl.CostEstimate(flops=0, bytes_accessed=56 << 20, transcendentals=0),
        name="widen",
    )(*reduced, *row_grads, got, got_second, produced, *outputs, sums)


MASKED = -1000000000.0


def shifted(value, axis, steps):
    count = lax.axis_size(axis)
    first, last = (max(0, -steps), min(count, count - steps))
    return lax.ppermute(value, axis, [(source, source + steps) for source in range(first, last)])


def layer_norm(values, gain, shift):
    mean = jnp.mean(values, axis=-1, keepdims=True)
    centred = values - mean
    spread = jnp.mean(centred * centred, axis=-1, keepdims=True)
    return centred * lax.rsqrt(spread + EPS) * gain + shift


def alibi_slopes(first, count, heads):
    index = (first + jnp.arange(count)).astype(jnp.float32)
    return jnp.exp2(-8.0 * (index + 1.0) / heads)


def attention_core(projected, qv_bias, slopes, key_ok):
    rows = projected.shape[0]
    width = projected.shape[2]
    count = slopes.shape[0]
    size = width // count
    query = (projected[:, 0] + qv_bias[0]).astype(jnp.bfloat16).reshape(rows, count, size)
    key = projected[:, 1].astype(jnp.bfloat16).reshape(rows, count, size)
    value = (projected[:, 2] + qv_bias[1]).astype(jnp.bfloat16).reshape(rows, count, size)
    place = jnp.arange(rows).astype(jnp.float32)
    distance = jnp.abs(place[:, None] - place[None, :])
    scale = 1.0 / math.sqrt(size)
    scores = (
        jnp.einsum("qhd,khd->hqk", query, key, preferred_element_type=jnp.float32) * scale
        - slopes[:, None, None] * distance[None]
    )
    scores = jnp.where(key_ok[None, None, :], scores, MASKED)
    weights = jax.nn.softmax(scores, axis=-1)
    weights_low = weights.astype(jnp.bfloat16)
    mixed = jnp.einsum("hqk,khd->qhd", weights_low, value, preferred_element_type=jnp.float32)
    mixed = mixed.reshape(rows, width).astype(jnp.bfloat16)
    return (query, key, value, weights, weights_low, mixed)


def attention_back(parts, grad_mixed, key_ok):
    query, key, value, weights, weights_low, mixed = parts
    rows, count, size = query.shape
    scale = 1.0 / math.sqrt(size)
    grad_low = grad_mixed.astype(jnp.bfloat16).reshape(rows, count, size)
    grad_weights = jnp.einsum("qhd,khd->hqk", grad_low, value, preferred_element_type=jnp.float32)
    grad_value = jnp.einsum(
        "hqk,qhd->khd", weights_low, grad_low, preferred_element_type=jnp.float32
    )
    inner = jnp.sum(weights * grad_weights, axis=-1, keepdims=True)
    grad_scores = weights * (grad_weights - inner)
    grad_scores = jnp.where(key_ok[None, None, :], grad_scores, 0.0).astype(jnp.bfloat16)
    grad_query = (
        jnp.einsum("hqk,khd->qhd", grad_scores, key, preferred_element_type=jnp.float32) * scale
    ).astype(jnp.bfloat16)
    grad_key = (
        jnp.einsum("hqk,qhd->khd", grad_scores, query, preferred_element_type=jnp.float32) * scale
    ).astype(jnp.bfloat16)
    grad_value = grad_value.astype(jnp.bfloat16)
    width = count * size
    grad_query = grad_query.reshape(rows, width)
    grad_key = grad_key.reshape(rows, width)
    grad_value = grad_value.reshape(rows, width)
    grad_projected = jnp.stack([grad_query, grad_key, grad_value], axis=1).reshape(rows, 3 * width)
    qv_grad = jnp.stack(
        [
            jnp.sum(grad_query.astype(jnp.float32), axis=0),
            jnp.sum(grad_value.astype(jnp.float32), axis=0),
        ]
    )
    return (grad_projected, qv_grad)


def gelu_product(both):
    return jax.nn.gelu(both[:, 0], approximate=False) * both[:, 1]


def geglu(lifted, up_bias):
    return gelu_product(lifted + up_bias[None])


def ffn_grads(rows_low, grad_low, up_weight, up_bias, down_weight):
    lifted = jnp.einsum("sd,gdf->sgf", rows_low, up_weight, preferred_element_type=jnp.float32)
    hidden, geglu_back = jax.vjp(gelu_product, lifted + up_bias[None])
    grad_hidden = jnp.einsum("sd,df->sf", grad_low, down_weight, preferred_element_type=jnp.float32)
    (grad_both,) = geglu_back(grad_hidden)
    grad_lifted = grad_both.astype(jnp.bfloat16)
    grad_bias = jnp.sum(grad_lifted.astype(jnp.float32), axis=0)
    up_grad = jnp.einsum("sd,sgf->gdf", rows_low, grad_lifted, preferred_element_type=jnp.float32)
    down_grad = jnp.einsum(
        "sd,sf->df", grad_low, hidden.astype(jnp.bfloat16), preferred_element_type=jnp.float32
    )
    return (grad_lifted, grad_bias, up_grad, down_grad)


def on_device(
    inputs,
    cotangent,
    lengths,
    w_qkv,
    b_qv,
    w_out,
    b_out,
    ln_gain,
    ln_bias,
    w_up,
    b_up,
    w_down,
    b_down,
):
    batches, shard_rows, width = inputs.shape
    parts = lax.axis_size("tensor")
    place = lax.axis_index("tensor")
    section = lax.axis_index("section")
    last_section = lax.axis_size("section") - 1
    full_rows = shard_rows * parts
    local_width = w_qkv.shape[3]
    local_heads = local_width // HD
    qkv_flat = w_qkv[0].reshape(width, 3 * local_width)
    out_weight = w_out[0]
    qv_bias = b_qv[0].astype(jnp.float32)
    out_bias = b_out[0].astype(jnp.float32)
    gains = ln_gain[0].astype(jnp.float32)
    shifts = ln_bias[0].astype(jnp.float32)
    down_bias = b_down[0].astype(jnp.float32)
    slopes = alibi_slopes(place * local_heads, local_heads, H)
    row_place = place * shard_rows + jnp.arange(shard_rows)
    kept_rows = 0

    def key_mask(length):
        return jnp.arange(full_rows) < length

    def after_attention(values, attended, bias, gain_rows, shift_rows):
        return layer_norm(values + attended + bias, gain_rows[0], shift_rows[0])

    def after_ffn(normed, lowered, bias, gain_rows, shift_rows):
        return layer_norm(normed + lowered + bias, gain_rows[1], shift_rows[1])

    def gather_inputs(values):
        return lax.all_gather(values.astype(jnp.bfloat16), "tensor", axis=0, tiled=True)

    def project(gathered):
        return jnp.dot(gathered, qkv_flat, preferred_element_type=jnp.float32).reshape(
            full_rows, 3, local_width
        )

    def attention_forward(values, length):
        gathered = gather_inputs(values)
        projected = project(gathered)
        mixed = attention_core(projected, qv_bias, slopes, key_mask(length))[5]

        def term(start, count):
            return jnp.dot(mixed, out_weight, preferred_element_type=jnp.float32)

        return (
            lax.psum_scatter(
                term(jnp.int32(0), shard_rows * lax.axis_size("tensor")).astype(jnp.bfloat16),
                "tensor",
                scatter_dimension=0,
                tiled=True,
            ).astype(jnp.float32),
            gathered,
            projected,
        )

    up_local = w_up[0]
    up_bias_local = b_up[0].astype(jnp.float32)
    down_local = w_down[0]

    def gather_normed(normed):
        return lax.all_gather(normed.astype(jnp.bfloat16), "tensor", axis=0, tiled=True)

    def ffn_forward(normed):
        lifted = jnp.einsum(
            "sd,gdf->sgf", gather_normed(normed), up_local, preferred_element_type=jnp.float32
        )
        hidden = geglu(lifted, up_bias_local).astype(jnp.bfloat16)

        def term(start, count):
            return jnp.einsum("sf,df->sd", hidden, down_local, preferred_element_type=jnp.float32)

        return lax.psum_scatter(
            term(jnp.int32(0), shard_rows * lax.axis_size("tensor")).astype(jnp.bfloat16),
            "tensor",
            scatter_dimension=0,
            tiled=True,
        ).astype(jnp.float32)

    def ffn_backward(normed, grad_lowered):
        gathered = gather_normed(normed)
        grad_whole = lax.all_gather(grad_lowered.astype(jnp.bfloat16), "tensor", axis=0, tiled=True)
        grad_lifted, grad_bias, up_grad, down_grad = ffn_grads(
            gathered, grad_whole, up_local, up_bias_local, down_local
        )

        def term(start, count):
            return jnp.einsum(
                "sgf,gdf->sd", grad_lifted, up_local, preferred_element_type=jnp.float32
            )

        grad_normed = lax.psum_scatter(
            term(jnp.int32(0), shard_rows * lax.axis_size("tensor")).astype(jnp.bfloat16),
            "tensor",
            scatter_dimension=0,
            tiled=True,
        ).astype(jnp.float32)
        return (grad_normed, (up_grad, grad_bias, down_grad))

    ffn_shapes = (up_local.shape, up_bias_local.shape, down_local.shape)

    def layer_forward(values, length):
        attended, gathered, projected = attention_forward(values, length)
        normed = after_attention(values, attended, out_bias, gains, shifts)
        lowered = ffn_forward(normed)
        return (
            after_ffn(normed, lowered, down_bias, gains, shifts),
            attended,
            lowered,
            gathered,
            projected,
        )

    def layer_backward(values, attended, lowered, length, grad_output):
        normed, attention_norm_back = jax.vjp(
            after_attention, values, attended, out_bias, gains, shifts
        )
        outcome, ffn_norm_back = jax.vjp(after_ffn, normed, lowered, down_bias, gains, shifts)
        grad_normed, grad_lowered, grad_down_bias, gain_late, shift_late = ffn_norm_back(
            grad_output
        )
        grad_from_ffn, ffn_terms = ffn_backward(normed, grad_lowered)
        grad_values, grad_attended, grad_out_bias, gain_early, shift_early = attention_norm_back(
            grad_normed + grad_from_ffn
        )
        gathered = gather_inputs(values)
        projected = project(gathered)
        grad_whole = lax.all_gather(
            grad_attended.astype(jnp.bfloat16), "tensor", axis=0, tiled=True
        )
        mask = key_mask(length)
        pieces = attention_core(projected, qv_bias, slopes, mask)
        mixed_low = pieces[5]
        out_grad = jnp.einsum(
            "se,sd->ed", mixed_low, grad_whole, preferred_element_type=jnp.float32
        )
        grad_mixed = jnp.einsum(
            "sd,ed->se", grad_whole, out_weight, preferred_element_type=jnp.float32
        )
        grad_projected, qv_grad = attention_back(pieces, grad_mixed, mask)
        qkv_grad = jnp.einsum(
            "sd,sx->dx", gathered, grad_projected, preferred_element_type=jnp.float32
        )

        def term(start, count):
            return jnp.einsum(
                "sx,dx->sd", grad_projected, qkv_flat, preferred_element_type=jnp.float32
            )

        grad_inputs = grad_values + lax.psum_scatter(
            term(jnp.int32(0), shard_rows * lax.axis_size("tensor")).astype(jnp.bfloat16),
            "tensor",
            scatter_dimension=0,
            tiled=True,
        ).astype(jnp.float32)
        terms = (
            qkv_grad,
            qv_grad,
            out_grad,
            grad_out_bias,
            gain_early + gain_late,
            shift_early + shift_late,
            ffn_terms[0],
            ffn_terms[1],
            ffn_terms[2],
            grad_down_bias,
        )
        return (grad_inputs, terms)

    def keep(store, item, batch, valid):
        old = lax.dynamic_index_in_dim(store, batch, 0, keepdims=False)
        return lax.dynamic_update_index_in_dim(store, jnp.where(valid, item, old), batch, 0)

    def forward_step(step, carry):
        (
            received,
            kept_values,
            kept_attended,
            kept_lowered,
            produced,
            kept_gathered,
            kept_projected,
        ) = carry
        index = step - section
        valid = (index >= 0) & (index < batches)
        batch = jnp.clip(index, 0, batches - 1)
        fresh = lax.dynamic_index_in_dim(
            inputs, jnp.minimum(step, batches - 1), 0, keepdims=False
        ).astype(jnp.float32)
        values = jnp.where(section == 0, fresh, received.astype(jnp.float32))
        output, attended, lowered, gathered, projected = layer_forward(values, lengths[batch])
        sent = output.astype(jnp.bfloat16)
        kept_values = keep(kept_values, values, batch, valid)
        kept_attended = keep(kept_attended, attended, batch, valid)
        kept_lowered = keep(kept_lowered, lowered, batch, valid)
        produced = keep(produced, sent, batch, valid)
        kept_gathered = keep(kept_gathered, gathered[:kept_rows], batch, valid)
        kept_projected = keep(kept_projected, projected[:kept_rows], batch, valid)
        received = shifted(sent, "section", 1)
        return (
            received,
            kept_values,
            kept_attended,
            kept_lowered,
            produced,
            kept_gathered,
            kept_projected,
        )

    store_zeros = jnp.zeros((batches, shard_rows, width), jnp.float32)
    gathered_zeros = jnp.zeros((batches, kept_rows, width), jnp.bfloat16)
    projected_zeros = jnp.zeros((batches, kept_rows, 3, local_width), jnp.float32)
    start_forward = (
        jnp.zeros((shard_rows, width), jnp.bfloat16),
        store_zeros,
        store_zeros,
        store_zeros,
        jnp.zeros((batches, shard_rows, width), jnp.bfloat16),
        gathered_zeros,
        projected_zeros,
    )
    received, kept_values, kept_attended, kept_lowered, produced, kept_gathered, kept_projected = (
        lax.fori_loop(0, batches + last_section, forward_step, start_forward)
    )

    def backward_step(step, carry):
        received, totals, grads_in = carry
        index = step - (last_section - section)
        valid = (index >= 0) & (index < batches)
        batch = jnp.clip(index, 0, batches - 1)
        length = lengths[batch]
        outer = lax.dynamic_index_in_dim(cotangent, batch, 0, keepdims=False).astype(jnp.float32)
        outer = outer * (row_place < length).astype(jnp.float32)[:, None]
        grad_output = jnp.where(section == last_section, outer, received.astype(jnp.float32))
        grad_output = jnp.where(valid, grad_output, 0.0)
        values = lax.dynamic_index_in_dim(kept_values, batch, 0, keepdims=False)
        attended = lax.dynamic_index_in_dim(kept_attended, batch, 0, keepdims=False)
        lowered = lax.dynamic_index_in_dim(kept_lowered, batch, 0, keepdims=False)
        grad_inputs, terms = layer_backward(values, attended, lowered, length, grad_output)
        totals = jax.tree.map(jnp.add, totals, terms)
        grads_in = keep(grads_in, grad_inputs, batch, valid)
        received = shifted(grad_inputs.astype(jnp.bfloat16), "section", -1)
        return (received, totals, grads_in)

    start_totals = (
        jnp.zeros((width, 3 * local_width), jnp.float32),
        jnp.zeros((2, local_width), jnp.float32),
        jnp.zeros((local_width, width), jnp.float32),
        jnp.zeros((width,), jnp.float32),
        jnp.zeros((2, width), jnp.float32),
        jnp.zeros((2, width), jnp.float32),
        jnp.zeros(ffn_shapes[0], jnp.float32),
        jnp.zeros(ffn_shapes[1], jnp.float32),
        jnp.zeros(ffn_shapes[2], jnp.float32),
        jnp.zeros((width,), jnp.float32),
    )
    start_backward = (jnp.zeros((shard_rows, width), jnp.bfloat16), start_totals, store_zeros)
    received, totals, grads_in = lax.fori_loop(
        0, batches + last_section, backward_step, start_backward
    )
    (
        qkv_total,
        qv_total,
        out_total,
        out_bias_total,
        gain_total,
        shift_total,
        up_total,
        up_bias_total,
        down_total,
        down_bias_total,
    ) = totals
    qkv_sum, qv_sum, out_sum, up_sum, up_bias_sum, down_sum = (
        lax.psum(qkv_total.astype(jnp.bfloat16), "dp").astype(jnp.float32),
        lax.psum(qv_total.astype(jnp.bfloat16), "dp").astype(jnp.float32),
        lax.psum(out_total.astype(jnp.bfloat16), "dp").astype(jnp.float32),
        lax.psum(up_total.astype(jnp.bfloat16), "dp").astype(jnp.float32),
        lax.psum(up_bias_total.astype(jnp.bfloat16), "dp").astype(jnp.float32),
        lax.psum(down_total.astype(jnp.bfloat16), "dp").astype(jnp.float32),
    )
    out_bias_sum, gain_sum, shift_sum, down_bias_sum = lax.psum(
        (out_bias_total, gain_total, shift_total, down_bias_total), ("tensor", "dp")
    )
    return (
        produced[None],
        grads_in[None],
        qkv_sum.reshape(1, width, 3, local_width),
        qv_sum[None],
        out_sum[None],
        out_bias_sum[None],
        gain_sum[None],
        shift_sum[None],
        up_sum[None],
        up_bias_sum[None],
        down_sum[None],
        down_bias_sum[None],
    )


def by_sequence(
    inputs,
    cotangent,
    lengths,
    w_qkv,
    b_qv,
    w_out,
    b_out,
    ln_gain,
    ln_bias,
    w_up,
    b_up,
    w_down,
    b_down,
):
    batches, shard_rows, width = inputs.shape
    place = lax.axis_index("tensor")
    section = lax.axis_index("section")
    groups = lax.axis_size("dp")
    rows = 2 * shard_rows
    seqs = batches // 2
    local = w_qkv.shape[3]
    units = w_up.shape[3]
    heads = local // HD
    chips = groups // 2

    qkv_own = jnp.transpose(w_qkv[0], (1, 0, 2))
    out_own = w_out[0]
    up_own = w_up[0]
    down_own = w_down[0]
    first = section == 0
    norms = (b_out, ln_gain[0], ln_bias[0], b_down)
    table = np.exp2(-8.0 * (np.arange(2 * heads, dtype=np.float32) + 1.0) / H).astype(np.float32)
    slopes = jnp.asarray(np.concatenate([table, np.roll(table, heads)]))

    qkv_oth, out_oth, up_oth, down_oth, *rest = fetch_and_forward(
        (qkv_own, out_own, up_own, down_own),
        (b_qv[0], b_up[0]),
        inputs,
        cotangent,
        slopes,
        norms,
        lengths,
        chips,
        seqs,
    )
    weights = (qkv_own, qkv_oth, out_own, out_oth, up_own, up_oth, down_own, down_oth)
    biases, rest = rest[:2], rest[2:]
    x_first = outer = rest[:seqs]
    *kept, y = rest[seqs:]
    deps = [y]

    def forward(x, m, turn):
        nonlocal kept, deps
        *kept, y = layer_forward(x, weights, biases, slopes, norms, lengths, m, turn, kept, deps, seqs)
        deps = [y]
        return y

    y_first = [y] + [forward(x_first[m], m, 0) for m in range(1, seqs)]
    x_second = [lax.ppermute(y, "section", [(0, 1)]) for y in y_first]
    y_second = [forward(x_second[0], 0, 1)]
    produced = exchange_rows(y_first, deps)
    deps = [produced]
    y_second += [forward(x_second[m], m, 1) for m in range(1, seqs)]

    back = None
    sums = [[None] * seqs, [None] * seqs]

    got_second = None

    def backward(grad, m, turn, *extra):
        nonlocal back, deps, got_second
        results = layer_backward(grad, kept, weights, slopes, norms, lengths, m, turn, back, deps, seqs, *extra)
        back, (gx, gx_low, norm_sums, up_sums, qv_sums) = results[:7], results[7:12]
        if extra:
            got_second = results[12]
        deps = [norm_sums]
        sums[turn][m] = (norm_sums, up_sums, qv_sums)
        return gx, gx_low

    gx_second = [backward(outer[0], 0, 1)]
    gx_second.append(backward(outer[1], 1, 1, [*y_second, gx_second[0][1]]))
    grad_middle = [lax.ppermute(gx_second[m][1], "section", [(1, 0)]) for m in range(seqs)]
    x_all = jnp.stack([jnp.where(first, x_first[m], x_second[m]) for m in range(seqs)])
    deps = deps + [x_all]
    gx_first = [backward(grad_middle[0], 0, 0)]

    *reduced, packed, got, _, _, _, _, _, gx, _ = backward_and_reduce(
        grad_middle[1], kept, back, x_all, weights, slopes, norms, lengths, [*sums[0][0], *sums[1][0], *sums[1][1]], gx_first[0][1],
        gx_second[1][1], chips,
    )
    gx_all = [gx_first[0][0], gx] + [g[0] for g in gx_second]
    (
        down_sum, up_sum, qkv_sum, out_sum, grads_in, produced,
        qv_sum, out_bias_sum, gain_sum, shift_sum, up_bias_sum, down_bias_sum,
    ) = widen(reduced, gx_all, got, got_second, produced, y_second, packed, units, local)
    return (
        produced[None],
        grads_in[None],
        jnp.transpose(qkv_sum, (1, 0, 2))[None],
        qv_sum[None],
        out_sum[None],
        out_bias_sum,
        gain_sum[None],
        shift_sum[None],
        up_sum[None],
        up_bias_sum[None],
        down_sum,
        down_bias_sum,
    )


def solution(mesh):
    sections, parts, groups = (mesh.shape[name] for name in ("section", "tensor", "dp"))

    def run(*args):
        paired = sections == 2 and parts == 2 and groups % 2 == 0 and args[0].shape[0] == 4
        return (by_sequence if paired else on_device)(*args)

    return jax.shard_map(
        run,
        mesh=mesh,
        in_specs=(
            P("dp", "tensor", None),
            P("dp", "tensor", None),
            P("dp"),
            P("section", None, None, "tensor"),
            P("section", None, "tensor"),
            P("section", "tensor", None),
            P("section", None),
            P("section", None, None),
            P("section", None, None),
            P("section", None, None, "tensor"),
            P("section", None, "tensor"),
            P("section", None, "tensor"),
            P("section", None),
        ),
        out_specs=(
            P("section", "dp", "tensor", None),
            P("section", "dp", "tensor", None),
            P("section", None, None, "tensor"),
            P("section", None, "tensor"),
            P("section", "tensor", None),
            P("section", None),
            P("section", None, None),
            P("section", None, None),
            P("section", None, None, "tensor"),
            P("section", None, "tensor"),
            P("section", None, "tensor"),
            P("section", None),
        ),
        check_vma=False,
    )
```

```python
import math

import jax
import jax.numpy as jnp
import numpy as np
from jax import lax
from jax.experimental import pallas as pl
from jax.experimental.pallas import tpu as pltpu
from jax.sharding import PartitionSpec as P

H = 16
HD = 64
EPS = 1e-05
BF = jnp.bfloat16
F32 = jnp.float32
VMEM_LIMIT = 62 * 1024 * 1024
ANY = pl.BlockSpec(memory_space=pl.ANY)
SMEM = pl.BlockSpec(memory_space=pltpu.SMEM)
WHOLE = pl.BlockSpec(memory_space=pltpu.VMEM)
NN = (((1,), (0,)), ((), ()))
NT = (((1,), (1,)), ((), ()))
TN = (((0,), (0,)), ((), ()))
CW = 256
PER = CW // HD


def dot(a, b, dims=NN):
    return lax.dot_general(a, b, dims, preferred_element_type=F32)


def arrived(ref, sem):
    pltpu.make_async_copy(ref, ref, sem).wait()


def call(kernel, inputs, outputs, scratch, chain, deps, name, flops, nbytes, turn, remote=False):
    pairs = [item if isinstance(item, tuple) else (item, ANY) for item in inputs]
    args = [p[0] for p in pairs]
    specs = [p[1] for p in pairs]
    n_in = len(args)
    aliases = {}
    if chain is not None:
        for buffer, index in zip(chain, [index for index, item in enumerate(outputs) if item[2]]):
            aliases[len(args)] = index
            args.append(buffer)
            specs.append(ANY)
    args += deps
    specs += [ANY] * len(deps)
    n_args, n_out = len(args), len(outputs)
    params = {"collective_id": 3, "has_side_effects": True} if remote else {}

    def body(*refs):
        @pl.when(lax.axis_index("section") == turn)
        def _():
            kernel(refs[:n_in], refs[n_args : n_args + n_out], refs[n_args + n_out :])

    return pl.pallas_call(
        body,
        in_specs=specs,
        out_specs=[ANY] * n_out,
        out_shape=[jax.ShapeDtypeStruct(o[0], o[1]) for o in outputs],
        scratch_shapes=scratch,
        input_output_aliases=aliases,
        compiler_params=pltpu.CompilerParams(vmem_limit_bytes=VMEM_LIMIT, **params),
        cost_estimate=pl.CostEstimate(flops=flops, bytes_accessed=nbytes, transcendentals=0),
        name=name,
    )(*args)


NORM_SPECS = [WHOLE] * 4


def norm_rows(refs):
    out_bias, gain, shift, down_bias = refs
    rows = [out_bias[...], gain[0:1], shift[0:1], down_bias[...], gain[1:2], shift[1:2]]
    return [row.astype(F32) for row in rows]


def slope_of(table_ref, head):
    return table_ref[lax.axis_index("tensor") * (table_ref.shape[0] // 2) + head]


def pick(k, count, own, oth, make):
    @pl.when(k < count)
    def _():
        for src, dst, sem in make(own, k):
            pltpu.make_async_copy(src, dst, sem).start()

    @pl.when(k >= count)
    def _():
        for src, dst, sem in make(oth, k - count):
            pltpu.make_async_copy(src, dst, sem).start()


def block(index, size):
    return pl.ds(pl.multiple_of(index * size, size), size)


def copy(src, dst, sem):
    return pltpu.make_async_copy(src, dst, sem)


def fill_distance(dist_ref, length):
    rows = dist_ref.shape[0]
    keys = lax.broadcasted_iota(jnp.int32, (rows, rows), 0)
    places = lax.broadcasted_iota(jnp.int32, (rows, rows), 1)
    distance = jnp.abs(keys - places).astype(F32)
    dist_ref[...] = jnp.where(keys < length, distance, 1e12)


def normalize(v):
    mean = jnp.mean(v, axis=1, keepdims=True)
    centred = v - mean
    rstd = lax.rsqrt(jnp.mean(centred * centred, axis=1, keepdims=True) + EPS)
    return centred * rstd, rstd


def halves(rows):
    return [slice(0, rows // 2), slice(rows // 2, rows)]


class Forward:
    def __init__(self, rows, width, local, units):
        self.rows, self.width, self.local, self.units = rows, width, local, units
        self.ft = min(512, units)
        self.tiles = units // self.ft
        self.heads_steps = local // CW
        self.total = 2 * local

    def kept(self, slots):
        rows, width = self.rows, self.width
        shapes = [((slots, rows, self.total), BF)] * 4
        shapes += [((slots, 2 * self.heads_steps, 8, rows), F32)]
        shapes += [((slots, rows, 2 * self.units), BF)] * 3
        return shapes + [((slots, rows, width), BF)] * 3 + [((slots, rows, 128), F32)] * 2

    def scratch(self):
        rows, width, ft, total = self.rows, self.width, self.ft, self.total
        sem = pltpu.SemaphoreType.DMA
        return [
            pltpu.VMEM((rows, width), BF),
            pltpu.VMEM((2, 3, width, CW), BF),
            pltpu.VMEM((total, width), BF),
            pltpu.VMEM((2, 2, width, ft), BF),
            pltpu.VMEM((2, width, ft), BF),
            pltpu.VMEM((2, 3, rows, CW), BF),
            pltpu.VMEM((2, 8, rows), F32),
            pltpu.VMEM((rows, total), BF),
            pltpu.VMEM((rows, rows), F32),
            pltpu.VMEM((rows, width), F32),
            pltpu.VMEM((rows, width), F32),
            pltpu.VMEM((rows, width), BF),
            pltpu.VMEM((2, 3, rows, ft), BF),
            pltpu.VMEM((3, rows, width), BF),
            pltpu.VMEM((2, rows, 128), F32),
            sem, sem((2,)), sem((2,)), sem((2, 2)), sem((2, 4)), sem, sem((2, 3)), sem((6,)),
        ]

    def bind(self, x, weights, bias, up_bias, slopes, norms, slot, outs, scratch):
        self.x_hbm, self.weights, self.bias, self.up_bias, self.slopes, self.norms = x, weights, bias, up_bias, slopes, norms
        self.slot, self.outs = slot, outs
        (self.x, self.w, self.o, self.up, self.down, self.qkv, self.lse, self.mixed, self.dist, self.normed, self.acc,
         self.low, self.tile, self.row, self.stat, self.x_sem, self.w_sem, self.o_sem, self.f_sem, self.q_sem, self.m_sem,
         self.t_sem, self.r_sem) = scratch

    def start_x(self):
        copy(self.x_hbm, self.x, self.x_sem).start()

    def start_w(self, k):
        s = lax.rem(k, 2)
        pick(k, self.heads_steps, self.weights[0], self.weights[1],
             lambda ref, j: [(ref.at[:, :, block(j, CW)], self.w.at[s], self.w_sem.at[s])])

    def start_o(self, side):
        copy(self.weights[2 + side], self.o.at[pl.ds(side * self.local, self.local)], self.o_sem.at[side]).start()

    def start_f(self, k):
        s = lax.rem(k, 2)
        ft = self.ft
        pick(k, self.tiles, (self.weights[4], self.weights[6]), (self.weights[5], self.weights[7]),
             lambda ref, j: [(ref[0].at[:, :, block(j, ft)], self.up.at[s], self.f_sem.at[s, 0]),
                             (ref[1].at[:, block(j, ft)], self.down.at[s], self.f_sem.at[s, 1])])

    def write_qkv(self, i, s):
        cols = block(i, CW)
        return [copy(self.qkv.at[s, c], out.at[self.slot, :, cols], self.q_sem.at[s, c])
                for c, out in enumerate(self.outs[:3])] + [
            copy(self.lse.at[s], self.outs[4].at[self.slot, i], self.q_sem.at[s, 3])]

    def attention_step(self, i, ahead):
        s = lax.rem(i, 2)
        qkv = self.qkv
        arrived(self.w.at[s], self.w_sem.at[s])

        @pl.when(i >= 2)
        def _():
            for item in self.write_qkv(i - 2, s):
                item.wait()

        values = self.x[...]
        b = self.bias[:, block(i, CW)].astype(F32)
        qkv[s, 0] = (dot(values, self.w[s, 0]) + b[0:1]).astype(BF)
        qkv[s, 1] = dot(values, self.w[s, 1]).astype(BF)
        qkv[s, 2] = (dot(values, self.w[s, 2]) + b[1:2]).astype(BF)

        @pl.when(i + 2 < ahead)
        def _():
            self.start_w(i + 2)

        parts = []
        scores_of = []
        for head in range(PER):
            cols = slice(head * HD, (head + 1) * HD)
            query = qkv[s, 0, :, cols] * BF(1.0 / math.sqrt(HD))
            scores_of.append(dot(qkv[s, 1, :, cols], query, NT))
        lows = []
        for head in range(PER):
            scores = scores_of[head] - self.dist[...] * slope_of(self.slopes, i * PER + head)
            top = jnp.max(scores, axis=0, keepdims=True)
            likely = jnp.exp(scores - top)
            mass = jnp.sum(likely, axis=0, keepdims=True)
            lows.append((likely * (1.0 / mass)).astype(BF))
            self.lse[s, head : head + 1, :] = top + jnp.log(mass)
        for head in range(PER):
            cols = slice(head * HD, (head + 1) * HD)
            parts.append(dot(lows[head], qkv[s, 2, :, cols], TN).astype(BF))
        self.mixed[:, block(i, CW)] = jnp.concatenate(parts, axis=1)
        for item in self.write_qkv(i, s):
            item.start()

    def middle(self):
        rows, width = self.rows, self.width
        copy(self.mixed, self.outs[3].at[self.slot], self.m_sem).start()
        for side in range(2):
            arrived(self.o.at[pl.ds(side * self.local, self.local)], self.o_sem.at[side])
        vec = norm_rows(self.norms)
        for rs in halves(rows):
            attended = dot(self.mixed[rs, :], self.o[...])
            u, rstd = normalize(self.x[rs, :].astype(F32) + attended + vec[0])
            normed = u * vec[1] + vec[2]
            self.normed[rs, :] = normed
            self.low[rs, :] = normed.astype(BF)
            self.row[0, rs, :] = u.astype(BF)
            self.stat[0, rs, :] = jnp.broadcast_to(rstd, (rows // 2, 128))
            self.acc[rs, :] = jnp.zeros((rows // 2, width), F32)
        for index, item in enumerate(self.first_rows()):
            copy(*item, self.r_sem.at[index]).start()

    def first_rows(self):
        return [(self.low, self.outs[8].at[self.slot]), (self.row.at[0], self.outs[9].at[self.slot]),
                (self.stat.at[0], self.outs[11].at[self.slot])]

    def write_tiles(self, i, s):
        return [copy(self.tile.at[s, c], out.at[self.slot, :, block(i, self.ft)], self.t_sem.at[s, c])
                for c, out in enumerate(self.outs[5:8])]

    def ffn_step(self, i, ahead):
        s = lax.rem(i, 2)
        arrived(self.up.at[s], self.f_sem.at[s, 0])
        arrived(self.down.at[s], self.f_sem.at[s, 1])

        @pl.when(i >= 2)
        def _():
            for item in self.write_tiles(i - 2, s):
                item.wait()

        b = self.up_bias[:, block(i, self.ft)].astype(F32)
        low = self.low[...]
        gate = dot(low, self.up[s, 0]) + b[0:1]
        lift = dot(low, self.up[s, 1]) + b[1:2]
        cdf = 0.5 * lax.erf(gate * (1.0 / math.sqrt(2.0))) + 0.5
        act = gate * cdf
        slope = cdf + gate * (jnp.exp(gate * gate * -0.5) * (1.0 / math.sqrt(2.0 * math.pi)))
        self.tile[s, 0] = act.astype(BF)
        self.tile[s, 1] = (lift * slope).astype(BF)
        hidden = (act * lift).astype(BF)
        self.tile[s, 2] = hidden
        self.acc[...] += dot(hidden, self.down[s], NT)

        @pl.when(i + 2 < ahead)
        def _():
            self.start_f(i + 2)

        for item in self.write_tiles(i, s):
            item.start()

    def finish(self, y_out):
        rows = self.rows
        vec = norm_rows(self.norms)
        for rs in halves(rows):
            u, rstd = normalize(self.normed[rs, :] + self.acc[rs, :] + vec[3])
            self.row[1, rs, :] = u.astype(BF)
            self.stat[1, rs, :] = jnp.broadcast_to(rstd, (rows // 2, 128))
            self.row[2, rs, :] = (u * vec[4] + vec[5]).astype(BF)
        ends = [(self.row.at[1], self.outs[10].at[self.slot]), (self.stat.at[1], self.outs[12].at[self.slot]),
                (self.row.at[2], y_out)]
        for index, item in enumerate(ends):
            copy(*item, self.r_sem.at[3 + index]).start()
        for index, item in enumerate(self.first_rows() + ends):
            copy(*item, self.r_sem.at[index]).wait()
        copy(self.mixed, self.outs[3].at[self.slot], self.m_sem).wait()
        for i in (2 * self.heads_steps - 2, 2 * self.heads_steps - 1):
            for item in self.write_qkv(jnp.int32(i), i % 2):
                item.wait()
        for i in (2 * self.tiles - 2, 2 * self.tiles - 1):
            for item in self.write_tiles(jnp.int32(i), i % 2):
                item.wait()

    def flops(self):
        rows, width, total = self.rows, self.width, self.total
        return 2 * rows * width * (4 * total + 6 * self.units) + 4 * rows * rows * total


def layer_forward(x, weights, biases, slopes, norms, lengths, m, turn, chain, deps, slots):
    rows, width = x.shape
    step = Forward(rows, width, weights[0].shape[2], weights[4].shape[2])

    def kernel(ins, outs, scratch):
        lengths_ref = ins[0]
        step.bind(ins[1], ins[2:10], ins[10], ins[11], ins[12], ins[13:17], m, outs[:13], scratch)
        step.start_x()
        for k in range(2):
            step.start_w(jnp.int32(k))
        for side in range(2):
            step.start_o(side)
        for k in range(2):
            step.start_f(jnp.int32(k))
        fill_distance(step.dist, lengths_ref[lax.axis_index("tensor") * slots + m])
        arrived(step.x, step.x_sem)

        @pl.loop(0, 2 * step.heads_steps)
        def _(i):
            step.attention_step(i, 2 * step.heads_steps)

        step.middle()

        @pl.loop(0, 2 * step.tiles)
        def _(i):
            step.ffn_step(i, 2 * step.tiles)

        step.finish(outs[13])

    return call(
        kernel,
        [(lengths, SMEM), x, *weights, *zip(biases, [WHOLE] * 2), (slopes, SMEM), *zip(norms, NORM_SPECS)],
        [shape + (True,) for shape in step.kept(slots)] + [((rows, width), BF, False)],
        step.scratch(),
        chain,
        deps,
        "layer_forward",
        step.flops(),
        54 << 20,
        turn,
    )


def layer_backward(grad, kept, weights, slopes, norms, lengths, m, turn, chain, deps, slots, sent=()):
    qkv_own, qkv_oth, o_own, o_oth, up_own, up_oth, down_own, down_oth = weights
    q, k, v, _, lse, act, slope, _, _, u1, u2, r1, r2 = kept
    rows, width = grad.shape
    local = qkv_own.shape[2]
    units = up_own.shape[2]
    heads_steps = local // CW
    ft = min(512, units)
    tiles = units // ft
    total = 2 * local

    def norm_back(grad_z, u, rstd, gain):
        t = grad_z * gain
        return rstd * (t - jnp.mean(t, axis=1, keepdims=True) - u * jnp.mean(t * u, axis=1, keepdims=True))

    def row_sum(values):
        return jnp.sum(values, axis=0, keepdims=True)

    def kernel(ins, outs, scratch):
        (lengths_ref, g_hbm, q_hbm, k_hbm, v_hbm, lse_hbm, a_hbm, b_hbm, u1_hbm, u2_hbm, r1_hbm, r2_hbm,
         qkv_own_ref, qkv_oth_ref, o_own_ref, o_oth_ref, up_own_ref, up_oth_ref, down_own_ref, down_oth_ref,
         slope_ref) = ins[:21]
        gg0_out, gg1_out, gl_out, ga_out, gq_out, gk_out, gv_out, gx_out, gxl_out, sums_out, ub_out, qv_out = outs[:12]
        (g_ref, u_ref, r_ref, up_ref, down_ref, ab_ref, gg_ref, low_ref, acc_ref, sums_ref, ub_ref, qv_ref,
         w_ref, o_ref, qkv_ref, lse_ref, gm_ref, dist_ref, gqkv_ref,
         g_sem, f_sem, t_sem, w_sem, q_sem, r_sem, x_send, x_recv) = scratch
        slot = m
        t = lax.axis_index("tensor")
        length = lengths_ref[t * slots + m]
        travelling = []
        if sent:
            cross = {"tensor": 1 - t}
            barrier = pltpu.get_barrier_semaphore()
            pl.semaphore_signal(barrier, inc=1, device_id=cross, device_id_type=pl.DeviceIdType.MESH)
            pl.semaphore_wait(barrier, 1)
            for index in range(len(sent)):
                travelling.append(
                    pltpu.make_async_remote_copy(
                        src_ref=ins[25 + index].at[block(1 - t, rows // 2)], dst_ref=outs[12].at[index],
                        send_sem=x_send.at[index], recv_sem=x_recv.at[index],
                        device_id=cross, device_id_type=pl.DeviceIdType.MESH,
                    )
                )
                travelling[-1].start()

        def start_f(i):
            s = lax.rem(i, 2)
            pick(i, tiles, (up_own_ref, down_own_ref), (up_oth_ref, down_oth_ref),
                 lambda ref, j: [(ref[0].at[:, :, block(j, ft)], up_ref.at[s], f_sem.at[s, 0]),
                                 (ref[1].at[:, block(j, ft)], down_ref.at[s], f_sem.at[s, 1])])
            for c, ref in enumerate((a_hbm, b_hbm)):
                copy(ref.at[slot, :, block(i, ft)], ab_ref.at[s, c], f_sem.at[s, 2 + c]).start()

        def start_w(i):
            s = lax.rem(i, 2)
            pick(i, heads_steps, (qkv_own_ref, o_own_ref), (qkv_oth_ref, o_oth_ref),
                 lambda ref, j: [(ref[0].at[:, :, block(j, CW)], w_ref.at[s], w_sem.at[s, 0]),
                                 (ref[1].at[block(j, CW)], o_ref.at[s], w_sem.at[s, 1])])
            for c, ref in enumerate((q_hbm, k_hbm, v_hbm)):
                copy(ref.at[slot, :, block(i, CW)], qkv_ref.at[s, c], w_sem.at[s, 2 + c]).start()
            copy(lse_hbm.at[slot, i], lse_ref.at[s], w_sem.at[s, 5]).start()

        firsts = [(g_hbm, g_ref), (u2_hbm.at[slot], u_ref.at[1]), (r2_hbm.at[slot], r_ref.at[1]),
                  (u1_hbm.at[slot], u_ref.at[0]), (r1_hbm.at[slot], r_ref.at[0])]
        for index, (src, dst) in enumerate(firsts):
            copy(src, dst, g_sem.at[index]).start()
            if index == 2:
                start_f(jnp.int32(0))
                start_f(jnp.int32(1))
        start_w(jnp.int32(0))
        start_w(jnp.int32(1))
        vec = norm_rows(ins[21:25])
        fill_distance(dist_ref, length)
        for index, (src, dst) in enumerate(firsts[:3]):
            copy(src, dst, g_sem.at[index]).wait()
        sums = [jnp.zeros((1, width), F32)] * 3
        for rs in halves(rows):
            grad_y = g_ref[rs, :].astype(F32)
            if turn == 1:
                places = lax.broadcasted_iota(jnp.int32, (rows // 2, width), 0) + rs.start
                grad_y = jnp.where(places < length, grad_y, 0.0)
            u = u_ref[1, rs, :].astype(F32)
            grad_c = norm_back(grad_y, u, r_ref[1, rs, 0:1], vec[4])
            acc_ref[rs, :] = grad_c
            low_ref[0, rs, :] = grad_c.astype(BF)
            for index, values in enumerate((grad_y * u, grad_y, grad_c)):
                sums[index] += row_sum(values)
        for index in range(3):
            sums_ref[index : index + 1, :] = sums[index]
        copy(low_ref.at[0], gl_out.at[slot], r_sem.at[0]).start()

        def write_tiles(i, s):
            return [copy(gg_ref.at[s, c], out.at[slot, :, block(i, ft)], t_sem.at[s, c])
                    for c, out in enumerate((gg0_out, gg1_out))]

        @pl.loop(0, 2 * tiles)
        def _(i):
            s = lax.rem(i, 2)
            arrived(up_ref.at[s], f_sem.at[s, 0])
            arrived(down_ref.at[s], f_sem.at[s, 1])
            for c in range(2):
                arrived(ab_ref.at[s, c], f_sem.at[s, 2 + c])

            @pl.when(i >= 2)
            def _():
                for item in write_tiles(i - 2, s):
                    item.wait()

            gh = dot(low_ref[0], down_ref[s])
            g0 = (gh * ab_ref[s, 1].astype(F32)).astype(BF)
            g1 = (gh * ab_ref[s, 0].astype(F32)).astype(BF)
            gg_ref[s, 0] = g0
            gg_ref[s, 1] = g1
            ub_ref[0:1, block(i, ft)] = row_sum(g0.astype(F32))
            ub_ref[1:2, block(i, ft)] = row_sum(g1.astype(F32))
            acc_ref[...] += dot(g0, up_ref[s, 0], NT) + dot(g1, up_ref[s, 1], NT)

            @pl.when(i + 2 < 2 * tiles)
            def _():
                start_f(i + 2)

            for item in write_tiles(i, s):
                item.start()

        for index, (src, dst) in enumerate(firsts[3:]):
            copy(src, dst, g_sem.at[3 + index]).wait()
        sums = [jnp.zeros((1, width), F32)] * 3
        for rs in halves(rows):
            grad_n = acc_ref[rs, :]
            u = u_ref[0, rs, :].astype(F32)
            grad_a = norm_back(grad_n, u, r_ref[0, rs, 0:1], vec[1])
            low_ref[1, rs, :] = grad_a.astype(BF)
            acc_ref[rs, :] = grad_a
            for index, values in enumerate((grad_n * u, grad_n, grad_a)):
                sums[index] += row_sum(values)
        for index in range(3):
            sums_ref[3 + index : 4 + index, :] = sums[index]
        sums_ref[6:8, :] = jnp.zeros((2, width), F32)
        copy(low_ref.at[1], ga_out.at[slot], r_sem.at[1]).start()
        scale = BF(1.0 / math.sqrt(HD))

        def write_heads(i, s):
            return [copy(gqkv_ref.at[s, c], out.at[slot, :, block(i, CW)], q_sem.at[s, c])
                    for c, out in enumerate((gq_out, gk_out, gv_out))]

        @pl.loop(0, 2 * heads_steps)
        def _(i):
            s = lax.rem(i, 2)
            for index, ref in enumerate((w_ref.at[s], o_ref.at[s], qkv_ref.at[s, 0], qkv_ref.at[s, 1], qkv_ref.at[s, 2], lse_ref.at[s])):
                arrived(ref, w_sem.at[s, index])

            @pl.when(i >= 2)
            def _():
                for item in write_heads(i - 2, s):
                    item.wait()

            gm_ref[...] = dot(low_ref[1], o_ref[s], NT).astype(BF)
            parts = [[], [], []]
            scores_of = []
            for head in range(PER):
                cols = slice(head * HD, (head + 1) * HD)
                query = qkv_ref[s, 0, :, cols] * scale
                scores_of.append(dot(qkv_ref[s, 1, :, cols], query, NT))
            for head in range(PER):
                cols = slice(head * HD, (head + 1) * HD)
                query = qkv_ref[s, 0, :, cols] * scale
                key = qkv_ref[s, 1, :, cols]
                gm = gm_ref[:, cols]
                gw = dot(qkv_ref[s, 2, :, cols], gm, NT)
                scores = scores_of[head] - dist_ref[...] * slope_of(slope_ref, i * PER + head)
                likely = jnp.exp(scores - lse_ref[s, head : head + 1, :])
                parts[2].append(dot(likely.astype(BF), gm).astype(BF))
                t = likely * gw
                inner = jnp.sum(t, axis=0, keepdims=True)
                gs = (t - likely * inner).astype(BF)
                parts[1].append(dot(gs, query).astype(BF))
                parts[0].append(dot(key * scale, gs, TN).astype(BF).T)
            for c in range(3):
                gqkv_ref[s, c] = jnp.concatenate(parts[c], axis=1)
            for index, c in enumerate((0, 2)):
                qv_ref[index : index + 1, block(i, CW)] = row_sum(gqkv_ref[s, c].astype(F32))
            acc_ref[...] += (
                dot(gqkv_ref[s, 0], w_ref[s, 0], NT)
                + dot(gqkv_ref[s, 1], w_ref[s, 1], NT)
                + dot(gqkv_ref[s, 2], w_ref[s, 2], NT)
            )

            @pl.when(i + 2 < 2 * heads_steps)
            def _():
                start_w(i + 2)

            for item in write_heads(i, s):
                item.start()

        g_ref[...] = acc_ref[...].astype(BF)
        ends = [(g_ref, gxl_out), (acc_ref, gx_out), (sums_ref, sums_out), (ub_ref, ub_out), (qv_ref, qv_out)]
        for index, (src, dst) in enumerate(ends):
            copy(src, dst, r_sem.at[2 + index]).start()
        for index, (src, dst) in enumerate([(low_ref.at[0], gl_out.at[slot]), (low_ref.at[1], ga_out.at[slot])] + ends):
            copy(src, dst, r_sem.at[index]).wait()
        for i in (2 * tiles - 2, 2 * tiles - 1):
            for item in write_tiles(jnp.int32(i), i % 2):
                item.wait()
        for i in (2 * heads_steps - 2, 2 * heads_steps - 1):
            for item in write_heads(jnp.int32(i), i % 2):
                item.wait()
        for item in travelling:
            item.wait()

    sem = pltpu.SemaphoreType.DMA
    return call(
        kernel,
        [(lengths, SMEM), grad, q, k, v, lse, act, slope, u1, u2, r1, r2, *weights, (slopes, SMEM), *zip(norms, NORM_SPECS), *sent],
        [((slots, rows, 2 * units), BF, True)] * 2
        + [((slots, rows, width), BF, True)] * 2
        + [((slots, rows, total), BF, True)] * 3
        + [
            ((rows, width), F32, False),
            ((rows, width), BF, False),
            ((8, width), F32, False),
            ((2, 2 * units), F32, False),
            ((2, total), F32, False),
        ]
        + ([((len(sent), rows // 2, width), BF, False)] if sent else []),
        [
            pltpu.VMEM((rows, width), BF),
            pltpu.VMEM((2, rows, width), BF),
            pltpu.VMEM((2, rows, 128), F32),
            pltpu.VMEM((2, 2, width, ft), BF),
            pltpu.VMEM((2, width, ft), BF),
            pltpu.VMEM((2, 2, rows, ft), BF),
            pltpu.VMEM((2, 2, rows, ft), BF),
            pltpu.VMEM((2, rows, width), BF),
            pltpu.VMEM((rows, width), F32),
            pltpu.VMEM((8, width), F32),
            pltpu.VMEM((2, 2 * units), F32),
            pltpu.VMEM((2, total), F32),
            pltpu.VMEM((2, 3, width, CW), BF),
            pltpu.VMEM((2, CW, width), BF),
            pltpu.VMEM((2, 3, rows, CW), BF),
            pltpu.VMEM((2, 8, rows), F32),
            pltpu.VMEM((rows, CW), BF),
            pltpu.VMEM((rows, rows), F32),
            pltpu.VMEM((2, 3, rows, CW), BF),
            sem((5,)), sem((2, 4)), sem((2, 2)), sem((2, 6)), sem((2, 3)), sem((7,)), sem((4,)), sem((4,)),
        ],
        chain,
        deps,
        "layer_backward",
        2 * rows * width * (4 * total + 6 * units) + 10 * rows * rows * total,
        70 << 20,
        turn,
        bool(sent),
    )


MESH = pl.DeviceIdType.MESH
CORE_LAG = 3
CROSS_LAG = 3
CHAIN_LAG = 2


def neighbours():
    t = lax.axis_index("tensor")
    d = lax.axis_index("dp")
    last = lax.axis_size("dp") // 2 - 1
    c = lax.rem(d, 2)
    z = d // 2
    return t, c, z, last, {"dp": d + 1 - 2 * c}, {"tensor": 1 - t}, {"dp": d + 2}, {"dp": d - 2}


def greet(c, z, chips, core, cross):
    barrier = pltpu.get_barrier_semaphore()
    pl.semaphore_signal(barrier, inc=1, device_id=core, device_id_type=MESH)
    pl.semaphore_signal(barrier, inc=1, device_id=cross, device_id_type=MESH)
    for shift in range(1, chips):
        chip = lax.rem(z + shift, chips)
        pl.semaphore_signal(barrier, inc=1, device_id={"dp": chip * 2 + c}, device_id_type=MESH)
    pl.semaphore_wait(barrier, 1 + chips)


def fetch_and_forward(weights, biases, inputs, cotangent, slopes, norms, lengths, chips, slots):
    seqs = inputs.shape[0] // 2
    shard_rows, width = inputs.shape[1:]
    rows = 2 * shard_rows
    groups = 2 * chips
    qkv, out, up, down = weights
    local, units = qkv.shape[2], up.shape[2]
    step = Forward(rows, width, local, units)
    ft, tiles = step.ft, step.tiles
    bias_widths = [b.shape[1] for b in biases]
    QKV, OUT, UP, DOWN, ROWS, BIAS = range(6)

    plan = [(UP, 0, groups), (ROWS, 0, 0), (BIAS, 0, 0), (BIAS, 1, 0)]
    plan += [(UP, part, groups) for part in range(1, tiles)]
    plan += [(DOWN, part, groups) for part in range(tiles - 2)]
    plan += [(QKV, part, 2) for part in range(3)] + [(OUT, 0, 2)]
    plan += [(DOWN, part, 2) for part in range(tiles - 2, tiles)]
    plan += [(ROWS, part, 0) for part in range(1, seqs)]
    n = len(plan)
    number = {item[:2]: index for index, item in enumerate(plan)}

    def size(index):
        kind, part, pieces = plan[index]
        whole = {QKV: width * local, OUT: local * width, UP: 2 * width * ft, DOWN: width * ft, ROWS: shard_rows * width, BIAS: 64}
        return whole[kind] / max(1, pieces)

    events, clock, busy = [], 0.0, 0.0
    for index, (kind, part, pieces) in enumerate(plan):
        clock += size(index)
        events.append((clock + 66000, index, 0))
        if pieces == groups:
            start = max(clock, busy)
            busy = start + size(index) * (chips - 1) * 1.0
            events += [(start + (size(index) * 1.0 + 66000) * hop, index, hop) for hop in range(1, chips)]
    events.sort()
    when = {event[1:]: event[0] for event in events}

    def ready(*keys):
        return max(when[key] for k in keys for key in when if key[0] == number[k])

    needs = [[(ROWS, 0), (BIAS, 0)], []] + [[(QKV, part) for part in range(3)], []] + [[(OUT, 0), (BIAS, 1)]]
    needs += [[] for _ in range(tiles - 1)]
    needs += [[(UP, part), (DOWN, part)] for part in range(tiles)] + [[]]
    assert step.heads_steps == 2
    rounds, taken = [], 0
    for need in needs:
        mine = []
        if need:
            limit = ready(*need)
            while taken < len(events) and events[taken][0] <= limit:
                mine.append(events[taken][1:])
                taken += 1
        rounds.append((mine, need))
    rest = [event[1:] for event in events[taken:]]
    n_rounds = len(rounds)
    n_kept = len(step.kept(slots))

    def kernel(*refs):
        lengths_ref, slope_ref, norm_refs = refs[0], refs[1], refs[2:6]
        refs = refs[6:]
        ins, bias_ins, held_refs = refs[:4], refs[4:6], refs[6:8]
        outs, bias_outs, row_refs = refs[8:12], refs[12:14], refs[14 : 14 + seqs]
        kept_refs = refs[14 + seqs : 14 + seqs + n_kept]
        y_ref = refs[14 + seqs + n_kept]
        stage, qv_bias, ub_bias, x_send, x_recv, c_send, c_recv, u_send, u_recv, d_send, d_recv, l_sem, b_sem = refs[
            15 + seqs + n_kept : 28 + seqs + n_kept
        ]
        t, c, z, last, core, cross, above, below = neighbours()
        section = lax.axis_index("section")
        greet(c, z, chips, core, cross)
        paired = [item for pair in zip(ins, outs) for item in pair]
        step.bind(
            row_refs[0], paired, qv_bias, ub_bias, slope_ref, norm_refs, 0, kept_refs, refs[28 + seqs + n_kept :]
        )

        def span(part):
            return block(part, shard_rows)

        def bias_part(m, side):
            return bias_outs[m].at[:, pl.ds(side * bias_widths[m], bias_widths[m])]

        def piece(side, index, chip, on):
            kind, part, pieces = plan[index]
            place = chip * 2 + on if pieces == groups else on
            ref = (ins, outs)[side][kind]
            if kind == QKV:
                return ref.at[part, block(place, width // pieces)]
            if kind == OUT:
                return ref.at[block(place, local // pieces)]
            cols = pl.ds(part * ft, ft)
            if kind == DOWN:
                return ref.at[block(place, width // pieces), cols]
            per = pieces // 2
            return ref.at[place // per, block(lax.rem(place, per), width // per), cols]

        def cross_copy(index, held_ref=None):
            kind, m, pieces = plan[index]
            if kind == ROWS:
                src = (held_refs[0] if held_ref is None else held_ref).at[(1 - t) * seqs + m]
                dst = row_refs[m].at[span(t)]
            elif kind == BIAS:
                src, dst = bias_ins[m], bias_part(m, 1)
            else:
                src, dst = piece(0, index, z, c), piece(1, index, z, c)
            return pltpu.make_async_remote_copy(
                src_ref=src, dst_ref=dst, send_sem=x_send.at[index], recv_sem=x_recv.at[index],
                device_id=cross, device_id_type=MESH,
            )

        def pass_on(index, chip, send, recv, device):
            place = piece(1, index, chip, c)
            return pltpu.make_async_remote_copy(
                src_ref=place, dst_ref=place, send_sem=send.at[index, chip], recv_sem=recv.at[index, chip],
                device_id=device, device_id_type=MESH,
            )

        def got(index, chip, on, sem):
            arrived(piece(1, index, chip, on), sem)

        for m in range(2):
            copy(bias_ins[m], bias_part(m, 0), b_sem.at[m]).start()
        for index in range(n):
            if plan[index][0] == ROWS:
                for turn in range(2):
                    @pl.when(section == turn)
                    def _(index=index, turn=turn):
                        cross_copy(index, held_refs[turn]).start()
            else:
                cross_copy(index).start()
        for turn in range(2):
            @pl.when(section == turn)
            def _(turn=turn):
                copy(held_refs[turn].at[pl.ds(t * seqs, seqs)], stage, l_sem.at[0]).start()

        @pl.when(section == 0)
        def _():
            for k in range(2):
                step.start_w(jnp.int32(k))
            step.start_o(0)
            for k in range(2):
                step.start_f(jnp.int32(k))
            fill_distance(step.dist, lengths_ref[t * seqs])

        arrived(stage, l_sem.at[0])
        for m in range(seqs):
            copy(stage.at[m], row_refs[m].at[span(t)], l_sem.at[m]).start()
        for m in range(seqs):
            arrived(stage.at[m], l_sem.at[m])
        for m in range(2):
            copy(bias_ins[m], bias_part(m, 0), b_sem.at[m]).wait()

        def handle(index, hop):
            kind, m, pieces = plan[index]
            if kind == ROWS:
                arrived(row_refs[m].at[span(1 - t)], x_recv.at[index])
            elif kind == BIAS:
                arrived(bias_part(m, 1), x_recv.at[index])
            elif hop == 0:
                got(index, z, c, x_recv.at[index])
                if pieces == groups:
                    @pl.when(z < last)
                    def _():
                        pass_on(index, z, u_send, u_recv, above).start()

                    @pl.when(z > 0)
                    def _():
                        pass_on(index, z, d_send, d_recv, below).start()

                pass_on(index, z, c_send, c_recv, core).start()
            else:
                @pl.when(z - hop >= 0)
                def _():
                    got(index, z - hop, c, u_recv.at[index, z - hop])

                    @pl.when(z < last)
                    def _():
                        pass_on(index, z - hop, u_send, u_recv, above).start()

                    pass_on(index, z - hop, c_send, c_recv, core).start()

                @pl.when(z + hop <= last)
                def _():
                    got(index, z + hop, c, d_recv.at[index, z + hop])

                    @pl.when(z > 0)
                    def _():
                        pass_on(index, z + hop, d_send, d_recv, below).start()

                    pass_on(index, z + hop, c_send, c_recv, core).start()

        def from_core(key):
            index = number[key]
            kind, m, pieces = plan[index]
            if pieces == groups:
                for chip in range(chips):
                    got(index, chip, 1 - c, c_recv.at[index, chip])
            elif pieces:
                got(index, z, 1 - c, c_recv.at[index, z])

        @pl.loop(0, n_rounds)
        def _(tau):
            for number_, (mine, need) in enumerate(rounds):
                if not (mine or need):
                    continue

                @pl.when(tau == number_)
                def _(number_=number_, mine=mine, need=need):
                    for index, hop in mine:
                        handle(index, hop)
                    for key in need:
                        from_core(key)
                    for key in need:
                        if key == (BIAS, 0):
                            @pl.when(section == 0)
                            def _():
                                step.start_x()
                                copy(bias_outs[0], qv_bias, b_sem.at[0]).start()
                                copy(bias_outs[0], qv_bias, b_sem.at[0]).wait()
                                arrived(step.x, step.x_sem)
                        elif key == (QKV, 2):
                            @pl.when(section == 0)
                            def _():
                                for k in range(2, 4):
                                    step.start_w(jnp.int32(k))
                        elif key == (OUT, 0):
                            @pl.when(section == 0)
                            def _():
                                step.start_o(1)
                        elif key == (BIAS, 1):
                            @pl.when(section == 0)
                            def _():
                                copy(bias_outs[1], ub_bias, b_sem.at[1]).start()
                                copy(bias_outs[1], ub_bias, b_sem.at[1]).wait()
                        elif key[0] == DOWN:
                            @pl.when(section == 0)
                            def _(key=key):
                                step.start_f(jnp.int32(tiles + key[1]))

            @pl.when(section == 0)
            def _():
                @pl.when(tau < 4)
                def _():
                    step.attention_step(tau, 2)

                @pl.when(tau == 4)
                def _():
                    step.middle()

                @pl.when(tau > 4)
                def _():
                    step.ffn_step(tau - 5, tiles)

        @pl.when(section == 0)
        def _():
            step.finish(y_ref)

        for index, hop in rest:
            handle(index, hop)
        for index in range(n):
            kind, part, pieces = plan[index]
            cross_copy(index).wait_send()
            if pieces == 2:
                pass_on(index, z, c_send, c_recv, core).wait_send()
            if pieces != groups:
                continue
            for chip in range(chips):
                pass_on(index, chip, c_send, c_recv, core).wait_send()

                @pl.when((chip <= z) & (z < last))
                def _(chip=chip):
                    pass_on(index, chip, u_send, u_recv, above).wait_send()

                @pl.when((chip >= z) & (z > 0))
                def _(chip=chip):
                    pass_on(index, chip, d_send, d_recv, below).wait_send()

    sem = pltpu.SemaphoreType.DMA
    return pl.pallas_call(
        kernel,
        in_specs=[SMEM, SMEM] + NORM_SPECS + [ANY] * 8,
        out_specs=[ANY] * (7 + seqs + n_kept),
        out_shape=[jax.ShapeDtypeStruct(w.shape, BF) for w in weights]
        + [jax.ShapeDtypeStruct((2, 2 * size_), BF) for size_ in bias_widths]
        + [jax.ShapeDtypeStruct((rows, width), BF)] * seqs
        + [jax.ShapeDtypeStruct(*shape) for shape in step.kept(slots)]
        + [jax.ShapeDtypeStruct((rows, width), BF)],
        scratch_shapes=[pltpu.VMEM((seqs, shard_rows, width), BF)]
        + [pltpu.VMEM((2, 2 * size_), BF) for size_ in bias_widths]
        + [sem((n,)), sem((n,))]
        + [sem((n, chips))] * 6
        + [sem((seqs,)), sem((2,))]
        + step.scratch(),
        compiler_params=pltpu.CompilerParams(collective_id=1, has_side_effects=True, vmem_limit_bytes=VMEM_LIMIT),
        cost_estimate=pl.CostEstimate(flops=step.flops(), bytes_accessed=90 << 20, transcendentals=0),
        name="fetch_and_forward",
    )(lengths, slopes, *norms, *weights, *biases, inputs, cotangent)


def norm_back(grad_z, u, rstd, gain):
    t = grad_z * gain
    return rstd * (t - jnp.mean(t, axis=1, keepdims=True) - u * jnp.mean(t * u, axis=1, keepdims=True))


def row_sum(values):
    return jnp.sum(values, axis=0, keepdims=True)


def backward_and_reduce(grad, kept, back, x_all, weights, slopes, norms, lengths, sums, low_grad, second, chips):
    q, k_, v, mixed_all, lse, act, slope, hidden_all, normed_all, u1, u2, r1, r2 = kept
    gg0, gg1, gl, ga, gq, gk, gv = back
    rows, width = grad.shape
    local, units = weights[0].shape[2], weights[4].shape[2]
    ft = CW
    tiles = units // ft
    heads_steps = local // CW
    seqs = 2
    bt = 128
    lefts = [gl, normed_all, x_all, ga]
    rights = [hidden_all, gg0, gg1, gq, gk, gv, mixed_all]
    group_of = [0, 1, 1, 2, 2, 2, 3]
    member_of = [0, 0, 1, 0, 1, 2, 0]
    half = width // 2
    quarter = half // 2
    per_pair = ft // bt
    pairs = tiles
    ffn_blocks = 3 * per_pair * pairs
    head_blocks = local // bt
    total = ffn_blocks + 4 * head_blocks
    ring, mines, gives = 4, CORE_LAG + 1, 4
    ahead_of = 2
    drain = CORE_LAG + CROSS_LAG + 2 * (chips - 1) * CHAIN_LAG + 1
    shard_rows = rows // 2
    norm_at = 2 * tiles
    head_at = norm_at + 1
    end_at = head_at + 5 * 2 * heads_steps
    x_flip, ga_flip = ffn_blocks - per_pair, ffn_blocks + per_pair
    up_rows = units // width
    vec_shape = (6 + 4 * up_rows + 2, width)
    spread = 42
    last_turn = ahead_of - (ahead_of - end_at) * spread // (end_at + 1 - ahead_of) + 1
    assert spread >= end_at + 1 - ahead_of and last_turn < ahead_of + ffn_blocks - ring

    def kernel(*refs):
        lengths_ref, slope_ref, norm_refs, sum_refs = refs[0], refs[1], refs[2:6], refs[6:15]
        refs = refs[12:]
        g_hbm, q_hbm, k_hbm, v_hbm, lse_hbm, a_hbm, b_hbm, u1_hbm, u2_hbm, r1_hbm, r2_hbm = refs[3:14]
        (qkv_own_ref, qkv_oth_ref, o_own_ref, o_oth_ref, up_own_ref, up_oth_ref, down_own_ref, down_oth_ref) = refs[14:22]
        left_refs, right_refs = refs[22:26], refs[26:33]
        low_grad_ref, second_ref = refs[33:35]
        outs, sums_out, rows_out = refs[35:39], refs[39], refs[40]
        fresh = refs[41:46]
        gx_out, gxl_out = refs[46:48]
        (
            acc, from_x, from_z, flip, stage, tile, mine, give, vec, vec_in, vec_all,
            g_ref, u_ref, r_ref, low_ref, gacc_ref, w_ref, o_ref, qkv_ref, gqkv_ref, lse_ref, gm_ref, gs_ref, dist_ref,
            part_sums, ub_sums, qv_sums,
            tile_sem, stage_sem, give_send, core_recv, x_send, x_recv, z_send, z_recv, f_send, f_recv,
            store_sem, out_send, out_recv, v_send, v_recv, r_send, r_recv,
            g_sem, w_sem, t_sem, e_sem,
        ) = refs[48:]
        final = from_x
        t, c, z, last, core, cross, above, below = neighbours()
        section = lax.axis_index("section")
        first = section == 0
        greet(c, z, chips, core, cross)
        fresh_of = {1: fresh[0].at[0], 2: fresh[1].at[0], 3: fresh[2], 4: fresh[3], 5: fresh[4]}
        vec_w = norm_rows(norm_refs)

        def remote(src, dst, send, recv, device):
            return pltpu.make_async_remote_copy(
                src_ref=src, dst_ref=dst, send_sem=send, recv_sem=recv, device_id=device, device_id_type=MESH
            )

        def valid(k):
            return (k >= 0) & (k < total)

        def member(k, visit):
            for m in range(3):
                @pl.when((k < ffn_blocks) & (lax.rem(k, 3 * per_pair) // per_pair == m))
                def _(m=m):
                    visit(m, k // (3 * per_pair) * per_pair + lax.rem(k, per_pair))

            for m in range(3, 7):
                base = ffn_blocks + (m - 3) * head_blocks

                @pl.when((k >= base) & (k < base + head_blocks))
                def _(m=m, base=base):
                    visit(m, k - base)

        def load_tile(k):
            at = lax.rem(k, ring)

            def visit(m, j):
                count = right_refs[m].shape[2] // (2 * bt)
                for side in range(2):
                    cols = block(side * count + j, bt)
                    where = pl.ds(side * bt, bt)
                    copy(right_refs[m].at[0, :, cols], tile.at[at, 0, :, where], tile_sem.at[at]).start()
                    if m not in fresh_of:
                        copy(right_refs[m].at[1, :, cols], tile.at[at, 1, :, where], tile_sem.at[at]).start()
                        continue

                    @pl.when(first)
                    def _(cols=cols, where=where):
                        copy(fresh_of[m].at[:, cols], tile.at[at, 1, :, where], tile_sem.at[at]).start()

                    @pl.when(section == 1)
                    def _(cols=cols, where=where):
                        copy(right_refs[m].at[1, :, cols], tile.at[at, 1, :, where], tile_sem.at[at]).start()

            member(k, visit)

        def take_left(g, at, mine_low):
            copy(left_refs[g].at[0], stage.at[0], stage_sem.at[0]).start()
            if mine_low is None:
                copy(left_refs[g].at[1], stage.at[1], stage_sem.at[1]).start()
                arrived(stage.at[1], stage_sem.at[1])
            else:
                @pl.when(first)
                def _():
                    stage[1] = low_ref[mine_low]

                @pl.when(section == 1)
                def _():
                    copy(left_refs[g].at[1], stage.at[1], stage_sem.at[1]).start()
                    arrived(stage.at[1], stage_sem.at[1])

            arrived(stage.at[0], stage_sem.at[0])
            for m in range(seqs):
                flip[at, :, m * rows : (m + 1) * rows] = stage[m].T

        def place_of(u):
            return lax.rem(u, 2), u // 2

        def start_f(u):
            at = lax.rem(u, 2)
            side, j = place_of(u)
            pick(side * tiles + j, tiles, (up_own_ref, down_own_ref), (up_oth_ref, down_oth_ref),
                 lambda ref, jj: [(ref[0].at[:, :, block(jj, ft)], w_ref.at[at, pl.ds(0, 2)], w_sem.at[at, 0]),
                                  (ref[1].at[:, block(jj, ft)], w_ref.at[at, 2], w_sem.at[at, 1])])
            for n, ref in enumerate((a_hbm, b_hbm)):
                copy(ref.at[1, :, block(side * tiles + j, ft)], qkv_ref.at[at, n], w_sem.at[at, 2 + n]).start()

        def write_tile(u):
            at = lax.rem(u, 2)
            side, j = place_of(u)
            return [copy(gqkv_ref.at[at, n], fresh[n].at[0, :, block(side * tiles + j, ft)], t_sem.at[at, n]) for n in range(2)]

        def start_w(i):
            at = lax.rem(i, 2)
            pick(i, heads_steps, (qkv_own_ref, o_own_ref), (qkv_oth_ref, o_oth_ref),
                 lambda ref, j: [(ref[0].at[:, :, block(j, CW)], w_ref.at[at], w_sem.at[at, 0]),
                                 (ref[1].at[block(j, CW)], o_ref.at[at], w_sem.at[at, 1])])
            for n, ref in enumerate((q_hbm, k_hbm, v_hbm)):
                copy(ref.at[1, :, block(i, CW)], qkv_ref.at[at, n], w_sem.at[at, 2 + n]).start()
            copy(lse_hbm.at[1, i], lse_ref.at[at], w_sem.at[at, 5]).start()

        def write_heads(i):
            at = lax.rem(i, 2)
            return [copy(gqkv_ref.at[at, n], fresh[2 + n].at[:, block(i, CW)], t_sem.at[at, n]) for n in range(3)]

        def norm_load(index, u_hbm, r_hbm):
            return [copy(u_hbm.at[1], u_ref, g_sem.at[index]), copy(r_hbm.at[1], r_ref, g_sem.at[index + 1])]

        def begin():
            copy(g_hbm, g_ref, g_sem.at[0]).start()
            for item in norm_load(1, u2_hbm, r2_hbm):
                item.start()
            start_f(jnp.int32(0))
            start_f(jnp.int32(1))
            copy(g_hbm, g_ref, g_sem.at[0]).wait()
            for item in norm_load(1, u2_hbm, r2_hbm):
                item.wait()
            totals = [jnp.zeros((1, width), F32)] * 3
            for rs in halves(rows):
                grad_y = g_ref[rs, :].astype(F32)
                u = u_ref[rs, :].astype(F32)
                grad_c = norm_back(grad_y, u, r_ref[rs, 0:1], vec_w[4])
                gacc_ref[rs, :] = grad_c
                low_ref[0, rs, :] = grad_c.astype(BF)
                for index, values in enumerate((grad_y * u, grad_y, grad_c)):
                    totals[index] += row_sum(values)
            for index in range(3):
                part_sums[index : index + 1, :] = totals[index]
            for item in norm_load(1, u1_hbm, r1_hbm):
                item.start()

        def ffn_unit(u):
            at = lax.rem(u, 2)

            @pl.when(u >= 1)
            def _():
                for item in write_tile(u - 1):
                    item.wait()

            arrived(w_ref.at[at, pl.ds(0, 2)], w_sem.at[at, 0])
            arrived(w_ref.at[at, 2], w_sem.at[at, 1])
            for n in range(2):
                arrived(qkv_ref.at[at, n], w_sem.at[at, 2 + n])
            gh = dot(low_ref[0], w_ref[at, 2])
            g0 = (gh * qkv_ref[at, 1].astype(F32)).astype(BF)
            g1 = (gh * qkv_ref[at, 0].astype(F32)).astype(BF)
            gqkv_ref[at, 0] = g0
            gqkv_ref[at, 1] = g1
            side, j = place_of(u)
            cols = block(side * tiles + j, ft)
            ub_sums[0:1, cols] = row_sum(g0.astype(F32))
            ub_sums[1:2, cols] = row_sum(g1.astype(F32))
            gacc_ref[...] += dot(g0, w_ref[at, 0], NT) + dot(g1, w_ref[at, 1], NT)

            @pl.when(u + 2 < 2 * tiles)
            def _():
                start_f(u + 2)

            for item in write_tile(u):
                item.start()

        def norm_unit():
            for item in write_tile(jnp.int32(2 * tiles - 1)):
                item.wait()
            for i in range(2):
                start_w(jnp.int32(i))
            fill_distance(dist_ref, lengths_ref[t * seqs + 1])
            for item in norm_load(1, u1_hbm, r1_hbm):
                item.wait()
            totals = [jnp.zeros((1, width), F32)] * 3
            for rs in halves(rows):
                grad_n = gacc_ref[rs, :]
                u = u_ref[rs, :].astype(F32)
                grad_a = norm_back(grad_n, u, r_ref[rs, 0:1], vec_w[1])
                low_ref[1, rs, :] = grad_a.astype(BF)
                gacc_ref[rs, :] = grad_a
                for index, values in enumerate((grad_n * u, grad_n, grad_a)):
                    totals[index] += row_sum(values)
            for index in range(3):
                part_sums[3 + index : 4 + index, :] = totals[index]

        def head_unit(a):
            i = a // 5
            phase = lax.rem(a, 5)
            pair = phase // 2
            at = lax.rem(i, 2)
            scale = BF(1.0 / math.sqrt(HD))
            cols = block(lax.rem(pair, 2), 2 * HD)

            @pl.when(phase == 0)
            def _():
                for index, ref in enumerate(
                    (w_ref.at[at], o_ref.at[at], qkv_ref.at[at, 0], qkv_ref.at[at, 1], qkv_ref.at[at, 2], lse_ref.at[at])
                ):
                    arrived(ref, w_sem.at[at, index])

                @pl.when(i >= 2)
                def _():
                    for item in write_heads(i - 2):
                        item.wait()

                gm_ref[...] = dot(low_ref[1], o_ref[at], NT).astype(BF)

            @pl.when((phase == 0) | (phase == 2))
            def _():
                query2 = qkv_ref[at, 0, :, cols] * scale
                key2 = qkv_ref[at, 1, :, cols]
                value2 = qkv_ref[at, 2, :, cols]
                gm2 = gm_ref[:, cols]
                parts = []
                pairs_here = [slice(head * HD, (head + 1) * HD) for head in range(2)]
                scores_of = [dot(key2[:, here], query2[:, here], NT) for here in pairs_here]
                for head, here in enumerate(pairs_here):
                    gm = gm2[:, here]
                    scores = scores_of[head] - dist_ref[...] * slope_of(slope_ref, i * PER + pair * 2 + head)
                    likely = jnp.exp(scores - lse_ref[at, pl.ds(pair * 2 + head, 1), :])
                    parts.append(dot(likely.astype(BF), gm).astype(BF))
                    tt = likely * dot(value2[:, here], gm, NT)
                    inner = jnp.sum(tt, axis=0, keepdims=True)
                    gs_ref[head] = (tt - likely * inner).astype(BF)
                gqkv_ref[at, 2, :, cols] = jnp.concatenate(parts, axis=1)

            @pl.when((phase == 1) | (phase == 3))
            def _():
                query2 = qkv_ref[at, 0, :, cols] * scale
                key2 = qkv_ref[at, 1, :, cols] * scale
                parts = [[], []]
                for head in range(2):
                    here = slice(head * HD, (head + 1) * HD)
                    gs = gs_ref[head]
                    parts[1].append(dot(gs, query2[:, here]).astype(BF))
                    parts[0].append(dot(key2[:, here], gs, TN).astype(BF).T)
                for n in range(2):
                    gqkv_ref[at, n, :, cols] = jnp.concatenate(parts[n], axis=1)

            @pl.when(phase == 4)
            def _():
                for index, n in enumerate((0, 2)):
                    qv_sums[index : index + 1, block(i, CW)] = row_sum(gqkv_ref[at, n].astype(F32))
                gacc_ref[...] += (
                    dot(gqkv_ref[at, 0], w_ref[at, 0], NT)
                    + dot(gqkv_ref[at, 1], w_ref[at, 1], NT)
                    + dot(gqkv_ref[at, 2], w_ref[at, 2], NT)
                )

                @pl.when(i + 2 < 2 * heads_steps)
                def _():
                    start_w(i + 2)

                for item in write_heads(i):
                    item.start()

        def add_sums(norm_part, ub_part, qv_part):
            vec[0, 0:6] += norm_part[0:6]
            for own in range(2):
                @pl.when(t == own)
                def _(own=own):
                    for n in range(2):
                        for side in range(2):
                            place = own if side == 0 else 1 - own
                            for j in range(up_rows):
                                at = 6 + (2 * n + place) * up_rows + j
                                start = side * units + j * width
                                vec[0, at : at + 1] += ub_part[n : n + 1, start : start + width]
                            at = 6 + 4 * up_rows + n
                            cols = slice(place * local, (place + 1) * local)
                            vec[0, at : at + 1, cols] += qv_part[n : n + 1, side * local : (side + 1) * local]

        ends = [(g_ref, gxl_out), (gacc_ref, gx_out)]

        def end_unit():
            for i in (2 * heads_steps - 2, 2 * heads_steps - 1):
                for item in write_heads(jnp.int32(i)):
                    item.wait()
            g_ref[...] = gacc_ref[...].astype(BF)
            for index, item in enumerate(ends):
                copy(*item, e_sem.at[index]).start()
            add_sums(part_sums, ub_sums, qv_sums)
            for index, item in enumerate(ends):
                copy(*item, e_sem.at[index]).wait()

        vec[0] = jnp.zeros(vec_shape, F32)

        @pl.when(first)
        def _():
            begin()
            add_sums(*sum_refs[:3])

        @pl.when(section == 1)
        def _():
            add_sums(*sum_refs[3:6])
            add_sums(*sum_refs[6:9])

        take_left(0, 0, 0)
        vec_core = remote(vec.at[0], vec_in.at[0], v_send.at[0], v_recv.at[0], core)
        vec_cross = remote(vec.at[1], vec_in.at[1], v_send.at[1], v_recv.at[1], cross)

        def row_copy(m, source):
            return remote(
                source.at[block(1 - t, shard_rows)], rows_out.at[m], r_send.at[m], r_recv.at[m], cross
            )

        row_plan = [(0, 0, low_grad_ref, True), (0, 1, gxl_out, False), (1, 1, second_ref, True)]
        for number, m, source, early in row_plan:
            if early:
                @pl.when(section == number)
                def _(m=m, source=source):
                    row_copy(m, source).start()

        def unit_at(turn):
            later = ahead_of + (turn - ahead_of) * (end_at + 1 - ahead_of) // spread
            return jnp.where(turn < ahead_of, turn, later)

        up = pl.ds(0, quarter)
        down = pl.ds(quarter, quarter)
        sides = ((up, 0, z, above, below), (down, 1, last - z, below, above))

        @pl.loop(0, ahead_of + total + drain)
        def _(turn):
            s = turn - ahead_of

            unit = unit_at(turn)

            @pl.when(first & (unit != unit_at(turn - 1)))
            def _():
                @pl.when(unit < norm_at)
                def _():
                    ffn_unit(unit)

                @pl.when(unit == norm_at)
                def _():
                    norm_unit()

                @pl.when((unit >= head_at) & (unit < end_at))
                def _():
                    head_unit(unit - head_at)

                @pl.when(unit == end_at)
                def _():
                    end_unit()

            @pl.when(s == 0)
            def _():
                for k in range(ring - 1):
                    load_tile(jnp.int32(k))

            @pl.when(valid(s))
            def _():
                @pl.when(s == per_pair - 1)
                def _():
                    take_left(1, 1, None)

                @pl.when(s == x_flip)
                def _():
                    take_left(2, 0, None)

                @pl.when(s == ga_flip)
                def _():
                    take_left(3, 1, 1)

                at = lax.rem(s, ring)
                arrived(tile.at[at], tile_sem.at[at])
                give_at = lax.rem(s, gives)

                @pl.when(s >= gives)
                def _():
                    arrived(give.at[give_at], give_send.at[give_at])

                ffn_flip = jnp.where(lax.rem(s, 3 * per_pair) // per_pair == 0, 0, 1)
                which = jnp.where(s < ffn_blocks, ffn_flip, jnp.where(s < ffn_blocks + 3 * head_blocks, 0, 1))
                for place, store, spot in ((1 - c, give, give_at), (c, mine, lax.rem(s, mines))):
                    here = block(place, half)
                    product = dot(flip[which, here, :rows], tile[at, 0])
                    for m in range(1, seqs):
                        product += dot(flip[which, here, m * rows : (m + 1) * rows], tile[at, m])
                    store[spot, 1] = product[:, :bt].astype(BF)
                    store[spot, 0] = product[:, bt:].astype(BF)

            @pl.when((s >= 0) & (s + ring - 1 < total))
            def _():
                load_tile(s + ring - 1)

            k1 = s - CORE_LAG

            @pl.when(valid(k1))
            def _():
                arrived(acc.at[k1], core_recv.at[k1])
                at = lax.rem(k1, mines)
                for side in range(2):
                    acc[k1, side] = acc[k1, side] + mine[at, side]

            k2 = k1 - CROSS_LAG

            @pl.when(valid(k2))
            def _():
                arrived(from_x.at[k2], x_recv.at[k2])
                acc[k2, 1] = acc[k2, 1] + from_x[k2]

            for rows_, way, place, ahead, behind in sides:
                k3 = k2 - CHAIN_LAG * place

                @pl.when(valid(k3) & (place > 0))
                def _(rows_=rows_, way=way, k3=k3):
                    arrived(from_z.at[k3, rows_], z_recv.at[way, k3])
                    acc[k3, 1, rows_] = acc[k3, 1, rows_] + from_z[k3, rows_]

                k4 = k2 - CHAIN_LAG * (2 * last - place)

                @pl.when(valid(k4) & (place == last))
                def _(rows_=rows_, k4=k4):
                    final[k4, rows_] = acc[k4, 1, rows_]

                @pl.when(valid(k4) & (place < last))
                def _(rows_=rows_, way=way, k4=k4):
                    arrived(final.at[k4, rows_], f_recv.at[way, k4])

            @pl.when(valid(s))
            def _():
                at = lax.rem(s, gives)
                remote(give.at[at], acc.at[s], give_send.at[at], core_recv.at[s], core).start()

            @pl.when(valid(k1))
            def _():
                remote(acc.at[k1, 0], from_x.at[k1], x_send, x_recv.at[k1], cross).start()

            for number, m, source, early in row_plan:
                if not early:
                    @pl.when((k1 == total - 1) & (section == number))
                    def _(m=m, source=source):
                        row_copy(m, source).start()

            for rows_, way, place, ahead, behind in sides:
                k3 = k2 - CHAIN_LAG * place

                @pl.when(valid(k3) & (place < last))
                def _(rows_=rows_, way=way, k3=k3, ahead=ahead):
                    remote(acc.at[k3, 1, rows_], from_z.at[k3, rows_], z_send.at[way], z_recv.at[way, k3], ahead).start()

                k4 = k2 - CHAIN_LAG * (2 * last - place)

                @pl.when(valid(k4) & (place > 0))
                def _(rows_=rows_, way=way, k4=k4, behind=behind):
                    remote(final.at[k4, rows_], final.at[k4, rows_], f_send.at[way], f_recv.at[way, k4], behind).start()

            k5 = k2 - CHAIN_LAG * 2 * last

            @pl.when(valid(k5))
            def _():
                def visit(m, j):
                    dst = outs[group_of[m]].at[member_of[m], block(c, half), block(j, bt)]
                    copy(final.at[k5], dst, store_sem).start()
                    remote(final.at[k5], dst, out_send, out_recv, core).start()

                member(k5, visit)

            @pl.when(turn == last_turn + 1)
            def _():
                vec_core.start()

            @pl.when(turn == last_turn + 6)
            def _():
                vec_core.wait_recv()
                vec[1] = vec[0] + vec_in[0]

            @pl.when(turn == last_turn + 7)
            def _():
                vec_cross.start()

            @pl.when(turn == last_turn + 13)
            def _():
                vec_cross.wait_recv()
                vec_all[z] = vec[1] + vec_in[1]

            @pl.when(turn == last_turn + 14)
            def _():
                for shift in range(1, chips):
                    to = lax.rem(z + shift, chips)
                    remote(
                        vec_all.at[z], vec_all.at[z], v_send.at[1 + shift], v_recv.at[1 + shift], {"dp": to * 2 + c}
                    ).start()

        for number, m, source, early in row_plan:
            @pl.when(section == number)
            def _(m=m, source=source):
                row_copy(m, source).wait()

        vec_core.wait_send()
        vec_cross.wait_send()
        for shift in range(1, chips):
            origin = lax.rem(z + chips - shift, chips)
            arrived(vec_all.at[origin], v_recv.at[1 + shift])
            arrived(vec_all.at[z], v_send.at[1 + shift])
        whole = vec_all[0]
        for chip in range(1, chips):
            whole += vec_all[chip]
        sums_out[...] = whole
        for at in range(gives):
            arrived(give.at[at], give_send.at[at])
        arrived(acc.at[:, 0], x_send)
        for rows_, way, place, ahead, behind in sides:
            @pl.when(place < last)
            def _(rows_=rows_, way=way):
                arrived(from_z.at[:, rows_], z_send.at[way])

            @pl.when(place > 0)
            def _(rows_=rows_, way=way):
                arrived(final.at[:, rows_], f_send.at[way])

        arrived(final, out_send)
        arrived(final, store_sem)
        arrived(final, out_recv)

    sem = pltpu.SemaphoreType.DMA
    flops = 2 * seqs * rows * width * 2 * bt * total
    members = [member_of[index] for index in range(7)]
    shapes = [(sum(g == index for g in group_of), width, rights[group_of.index(index)].shape[2] // 2) for index in range(4)]
    return pl.pallas_call(
        kernel,
        in_specs=[SMEM, SMEM] + NORM_SPECS + [WHOLE] * 9 + [ANY] * 32,
        out_specs=[ANY] * 4 + [WHOLE] + [ANY] * 8,
        out_shape=[jax.ShapeDtypeStruct(s, BF) for s in shapes]
        + [jax.ShapeDtypeStruct(vec_shape, F32), jax.ShapeDtypeStruct((seqs, shard_rows, width), BF)]
        + [jax.ShapeDtypeStruct(act.shape, BF)] * 2
        + [jax.ShapeDtypeStruct((rows, 2 * local), BF)] * 3
        + [jax.ShapeDtypeStruct((rows, width), F32), jax.ShapeDtypeStruct((rows, width), BF)],
        scratch_shapes=[
            pltpu.VMEM((total, 2, half, bt), BF),
            pltpu.VMEM((total, half, bt), BF),
            pltpu.VMEM((total, half, bt), BF),
            pltpu.VMEM((2, width, seqs * rows), BF),
            pltpu.VMEM((seqs, rows, width), BF),
            pltpu.VMEM((ring, seqs, rows, 2 * bt), BF),
            pltpu.VMEM((mines, 2, half, bt), BF),
            pltpu.VMEM((gives, 2, half, bt), BF),
            pltpu.VMEM((2,) + vec_shape, F32),
            pltpu.VMEM((2,) + vec_shape, F32),
            pltpu.VMEM((chips,) + vec_shape, F32),
            pltpu.VMEM((rows, width), BF),
            pltpu.VMEM((rows, width), BF),
            pltpu.VMEM((rows, 128), F32),
            pltpu.VMEM((2, rows, width), BF),
            pltpu.VMEM((rows, width), F32),
            pltpu.VMEM((2, 3, width, CW), BF),
            pltpu.VMEM((2, CW, width), BF),
            pltpu.VMEM((2, 3, rows, CW), BF),
            pltpu.VMEM((2, 3, rows, CW), BF),
            pltpu.VMEM((2, 8, rows), F32),
            pltpu.VMEM((rows, CW), BF),
            pltpu.VMEM((2, rows, rows), BF),
            pltpu.VMEM((rows, rows), F32),
            pltpu.VMEM((8, width), F32),
            pltpu.VMEM((2, 2 * units), F32),
            pltpu.VMEM((2, 2 * local), F32),
            sem((ring,)), sem((2,)), sem((gives,)), sem((total,)), sem, sem((total,)),
            sem((2,)), sem((2, total)), sem((2,)), sem((2, total)),
            sem, sem, sem, sem((chips + 1,)), sem((chips + 1,)), sem((seqs,)), sem((seqs,)),
            sem((3,)), sem((2, 6)), sem((2, 3)), sem((2,)),
        ],
        input_output_aliases={20: 6, 21: 7},
        compiler_params=pltpu.CompilerParams(
            collective_id=0, has_side_effects=True, vmem_limit_bytes=67_000_000
        ),
        cost_estimate=pl.CostEstimate(flops=flops, bytes_accessed=100 << 20, transcendentals=0),
        name="backward_and_reduce",
    )(
        lengths, slopes, *norms, *sums, grad, q, k_, v, lse, act, slope, u1, u2, r1, r2, *weights, *lefts, *rights,
        low_grad, second
    )


def exchange_rows(outputs, deps):
    seqs = len(outputs)
    rows, width = outputs[0].shape
    shard_rows = rows // 2
    n_in = seqs + len(deps)

    def kernel(*refs):
        y_refs, out_ref = refs[:seqs], refs[n_in]
        stage, send, recv, l_sem = refs[n_in + 1 :]
        t = lax.axis_index("tensor")
        cross = {"tensor": 1 - t}
        barrier = pltpu.get_barrier_semaphore()
        pl.semaphore_signal(barrier, inc=1, device_id=cross, device_id_type=MESH)
        pl.semaphore_wait(barrier, 1)

        @pl.when(lax.axis_index("section") == 0)
        def _():
            for m in range(seqs):
                pltpu.make_async_remote_copy(
                    src_ref=y_refs[m].at[block(1 - t, shard_rows)], dst_ref=out_ref.at[t * seqs + m],
                    send_sem=send.at[m], recv_sem=recv.at[m], device_id=cross, device_id_type=MESH,
                ).start()
            for m in range(seqs):
                copy(y_refs[m].at[block(t, shard_rows)], stage.at[m], l_sem.at[m]).start()
            for m in range(seqs):
                arrived(stage.at[m], l_sem.at[m])
                copy(stage.at[m], out_ref.at[t * seqs + m], l_sem.at[m]).start()
            for m in range(seqs):
                arrived(stage.at[m], l_sem.at[m])
            for m in range(seqs):
                arrived(out_ref.at[(1 - t) * seqs + m], recv.at[m])
                arrived(stage.at[m], send.at[m])

    sem = pltpu.SemaphoreType.DMA
    return pl.pallas_call(
        kernel,
        in_specs=[ANY] * n_in,
        out_specs=ANY,
        out_shape=jax.ShapeDtypeStruct((2 * seqs, shard_rows, width), BF),
        scratch_shapes=[pltpu.VMEM((seqs, shard_rows, width), BF), sem((seqs,)), sem((seqs,)), sem((seqs,))],
        compiler_params=pltpu.CompilerParams(collective_id=2, has_side_effects=True),
        cost_estimate=pl.CostEstimate(flops=0, bytes_accessed=0, transcendentals=0),
        name="exchange_rows",
    )(*outputs, *deps)


def widen(reduced, row_grads, got, got_second, produced, outputs, sums, units, local):
    shard_rows, width = got.shape[1:]
    seqs = got.shape[0]
    n = len(reduced)
    jobs = []
    for index, array in enumerate(reduced):
        lead, depth, columns = array.shape
        step = 512 * 1024 // columns
        if index == n - 1:
            jobs += [(index, 0, at, depth // 2, columns) for at in range(0, depth, depth // 2)]
        else:
            jobs += [(index, part, at, step, columns) for part in range(lead) for at in range(0, depth, step)]
    jobs += [(n, m, 0, shard_rows, width) for m in range(seqs)] + [(n + 1, m, 0, shard_rows, width) for m in range(seqs)]
    jobs += [(n + 2, m, 0, shard_rows, width) for m in range(2 * seqs)]
    ring = 5
    n_in = n + 3 * seqs + 4
    parts = units // width

    def kernel(*refs):
        ins = refs[:n]
        grad_refs = refs[n : n + 2 * seqs]
        got_ref, got_second_ref, produced_ref = refs[n + 2 * seqs : n + 2 * seqs + 3]
        y_refs, sums_ref = refs[n + 2 * seqs + 3 : n_in - 1], refs[n_in - 1]
        outs = refs[n_in : n_in + n + 2]
        qv_ref, out_bias_ref, gain_ref, shift_ref, ub_ref, down_bias_ref = refs[n_in + n + 2 : n_in + n + 8]
        shapes = sorted({(j[3], j[4]) for j in jobs if j[0] != n})
        buffers = refs[n_in + n + 8 :]
        wide_rows, in_sem, out_sem = buffers[0], buffers[1], buffers[2]
        low = {s: buffers[3 + 2 * i] for i, s in enumerate(shapes)}
        wide = {s: buffers[4 + 2 * i] for i, s in enumerate(shapes)}
        t = lax.axis_index("tensor")
        section = lax.axis_index("section")

        def load(number):
            index, part, at, rows, columns = jobs[number]
            s = number % ring
            if index < n:
                copy(ins[index].at[part, pl.ds(at, rows)], low[rows, columns].at[s], in_sem.at[s]).start()
            elif index == n:
                for turn in range(2):
                    @pl.when(section == turn)
                    def _(turn=turn):
                        source = grad_refs[turn * seqs + part].at[block(t, shard_rows)]
                        copy(source, wide_rows.at[part], in_sem.at[s]).start()
            elif index == n + 1:
                for number_ in range(2):
                    @pl.when(section == number_)
                    def _(number_=number_):
                        source = got_second_ref.at[seqs] if number_ == 1 and part == 0 else got_ref.at[part]
                        copy(source, low[rows, columns].at[s], in_sem.at[s]).start()
            else:
                @pl.when(section == 0)
                def _():
                    copy(produced_ref.at[part], low[rows, columns].at[s], in_sem.at[s]).start()

                @pl.when(section == 1)
                def _():
                    source = y_refs[part].at[block(t, shard_rows)] if part < seqs else got_second_ref.at[part - seqs]
                    copy(source, low[rows, columns].at[s], in_sem.at[s]).start()

        def store(number):
            index, part, at, rows, columns = jobs[number]
            s = number % ring
            if index < n - 1:
                return copy(wide[rows, columns].at[s], outs[index].at[part, pl.ds(at, rows)], out_sem.at[s])
            if index == n - 1:
                return copy(wide[rows, columns].at[s], outs[index].at[:, pl.ds(at, rows)], out_sem.at[s])
            if index == n:
                return copy(wide_rows.at[part], outs[n].at[t * seqs + part], out_sem.at[s])
            if index == n + 1:
                return copy(wide[rows, columns].at[s], outs[n].at[(1 - t) * seqs + part], out_sem.at[s])
            side, m = divmod(part, seqs)
            spread = (t + side - 2 * t * side) * seqs + m
            return copy(low[rows, columns].at[s], outs[n + 1].at[jnp.where(section == 0, part, spread)], out_sem.at[s])

        for number in range(ring):
            load(number)
        gain_ref[0:1] = sums_ref[3:4]
        gain_ref[1:2] = sums_ref[0:1]
        shift_ref[0:1] = sums_ref[4:5]
        shift_ref[1:2] = sums_ref[1:2]
        out_bias_ref[...] = sums_ref[5:6]
        down_bias_ref[...] = sums_ref[2:3]
        for half in range(2):
            @pl.when(t == half)
            def _(half=half):
                for g in range(2):
                    for j in range(parts):
                        at = 6 + (2 * g + half) * parts + j
                        ub_ref[g : g + 1, j * width : (j + 1) * width] = sums_ref[at : at + 1]
                    at = 6 + 4 * parts + g
                    qv_ref[g : g + 1] = sums_ref[at : at + 1, half * local : (half + 1) * local]

        for number, (index, part, at, rows, columns) in enumerate(jobs):
            s = number % ring
            if index == n:
                arrived(wide_rows.at[part], in_sem.at[s])
            else:
                arrived(low[rows, columns].at[s], in_sem.at[s])
            if number >= ring:
                store(number - ring).wait()
            if index == n - 1:
                wide[rows, columns][s] = low[rows, columns][s].astype(F32).T
            elif index not in (n, n + 2):
                wide[rows, columns][s] = low[rows, columns][s].astype(F32)
            store(number).start()
            if number + ring < len(jobs):
                load(number + ring)
        for number in range(len(jobs) - ring, len(jobs)):
            store(number).wait()

    shapes = sorted({(j[3], j[4]) for j in jobs if j[0] != n})
    square = (reduced[-1].shape[1] // 2, reduced[-1].shape[2])
    last = reduced[-1].shape
    sem = pltpu.SemaphoreType.DMA
    buffers = []
    for s in shapes:
        buffers += [pltpu.VMEM((ring,) + s, BF), pltpu.VMEM((ring,) + ((s[1], s[0]) if s == square else s), F32)]
    return pl.pallas_call(
        kernel,
        in_specs=[ANY] * (n_in - 1) + [WHOLE],
        out_specs=[ANY] * (n + 2) + [WHOLE] * 6,
        out_shape=[jax.ShapeDtypeStruct(r.shape, F32) for r in reduced[:-1]]
        + [jax.ShapeDtypeStruct((last[2], last[1]), F32), jax.ShapeDtypeStruct((2 * seqs, shard_rows, width), F32)]
        + [jax.ShapeDtypeStruct((2 * seqs, shard_rows, width), BF)]
        + [
            jax.ShapeDtypeStruct(shape, F32)
            for shape in ((2, local), (1, width), (2, width), (2, width), (2, units), (1, width))
        ],
        scratch_shapes=[pltpu.VMEM((seqs, shard_rows, width), F32), sem((ring,)), sem((ring,))] + buffers,
        compiler_params=pltpu.CompilerParams(vmem_limit_bytes=VMEM_LIMIT),
        cost_estimate=pl.CostEstimate(flops=0, bytes_accessed=56 << 20, transcendentals=0),
        name="widen",
    )(*reduced, *row_grads, got, got_second, produced, *outputs, sums)


MASKED = -1000000000.0


def shifted(value, axis, steps):
    count = lax.axis_size(axis)
    first, last = (max(0, -steps), min(count, count - steps))
    return lax.ppermute(value, axis, [(source, source + steps) for source in range(first, last)])


def layer_norm(values, gain, shift):
    mean = jnp.mean(values, axis=-1, keepdims=True)
    centred = values - mean
    spread = jnp.mean(centred * centred, axis=-1, keepdims=True)
    return centred * lax.rsqrt(spread + EPS) * gain + shift


def alibi_slopes(first, count, heads):
    index = (first + jnp.arange(count)).astype(jnp.float32)
    return jnp.exp2(-8.0 * (index + 1.0) / heads)


def attention_core(projected, qv_bias, slopes, key_ok):
    rows = projected.shape[0]
    width = projected.shape[2]
    count = slopes.shape[0]
    size = width // count
    query = (projected[:, 0] + qv_bias[0]).astype(jnp.bfloat16).reshape(rows, count, size)
    key = projected[:, 1].astype(jnp.bfloat16).reshape(rows, count, size)
    value = (projected[:, 2] + qv_bias[1]).astype(jnp.bfloat16).reshape(rows, count, size)
    place = jnp.arange(rows).astype(jnp.float32)
    distance = jnp.abs(place[:, None] - place[None, :])
    scale = 1.0 / math.sqrt(size)
    scores = (
        jnp.einsum("qhd,khd->hqk", query, key, preferred_element_type=jnp.float32) * scale
        - slopes[:, None, None] * distance[None]
    )
    scores = jnp.where(key_ok[None, None, :], scores, MASKED)
    weights = jax.nn.softmax(scores, axis=-1)
    weights_low = weights.astype(jnp.bfloat16)
    mixed = jnp.einsum("hqk,khd->qhd", weights_low, value, preferred_element_type=jnp.float32)
    mixed = mixed.reshape(rows, width).astype(jnp.bfloat16)
    return (query, key, value, weights, weights_low, mixed)


def attention_back(parts, grad_mixed, key_ok):
    query, key, value, weights, weights_low, mixed = parts
    rows, count, size = query.shape
    scale = 1.0 / math.sqrt(size)
    grad_low = grad_mixed.astype(jnp.bfloat16).reshape(rows, count, size)
    grad_weights = jnp.einsum("qhd,khd->hqk", grad_low, value, preferred_element_type=jnp.float32)
    grad_value = jnp.einsum(
        "hqk,qhd->khd", weights_low, grad_low, preferred_element_type=jnp.float32
    )
    inner = jnp.sum(weights * grad_weights, axis=-1, keepdims=True)
    grad_scores = weights * (grad_weights - inner)
    grad_scores = jnp.where(key_ok[None, None, :], grad_scores, 0.0).astype(jnp.bfloat16)
    grad_query = (
        jnp.einsum("hqk,khd->qhd", grad_scores, key, preferred_element_type=jnp.float32) * scale
    ).astype(jnp.bfloat16)
    grad_key = (
        jnp.einsum("hqk,qhd->khd", grad_scores, query, preferred_element_type=jnp.float32) * scale
    ).astype(jnp.bfloat16)
    grad_value = grad_value.astype(jnp.bfloat16)
    width = count * size
    grad_query = grad_query.reshape(rows, width)
    grad_key = grad_key.reshape(rows, width)
    grad_value = grad_value.reshape(rows, width)
    grad_projected = jnp.stack([grad_query, grad_key, grad_value], axis=1).reshape(rows, 3 * width)
    qv_grad = jnp.stack(
        [
            jnp.sum(grad_query.astype(jnp.float32), axis=0),
            jnp.sum(grad_value.astype(jnp.float32), axis=0),
        ]
    )
    return (grad_projected, qv_grad)


def gelu_product(both):
    return jax.nn.gelu(both[:, 0], approximate=False) * both[:, 1]


def geglu(lifted, up_bias):
    return gelu_product(lifted + up_bias[None])


def ffn_grads(rows_low, grad_low, up_weight, up_bias, down_weight):
    lifted = jnp.einsum("sd,gdf->sgf", rows_low, up_weight, preferred_element_type=jnp.float32)
    hidden, geglu_back = jax.vjp(gelu_product, lifted + up_bias[None])
    grad_hidden = jnp.einsum("sd,df->sf", grad_low, down_weight, preferred_element_type=jnp.float32)
    (grad_both,) = geglu_back(grad_hidden)
    grad_lifted = grad_both.astype(jnp.bfloat16)
    grad_bias = jnp.sum(grad_lifted.astype(jnp.float32), axis=0)
    up_grad = jnp.einsum("sd,sgf->gdf", rows_low, grad_lifted, preferred_element_type=jnp.float32)
    down_grad = jnp.einsum(
        "sd,sf->df", grad_low, hidden.astype(jnp.bfloat16), preferred_element_type=jnp.float32
    )
    return (grad_lifted, grad_bias, up_grad, down_grad)


def on_device(
    inputs,
    cotangent,
    lengths,
    w_qkv,
    b_qv,
    w_out,
    b_out,
    ln_gain,
    ln_bias,
    w_up,
    b_up,
    w_down,
    b_down,
):
    batches, shard_rows, width = inputs.shape
    parts = lax.axis_size("tensor")
    place = lax.axis_index("tensor")
    section = lax.axis_index("section")
    last_section = lax.axis_size("section") - 1
    full_rows = shard_rows * parts
    local_width = w_qkv.shape[3]
    local_heads = local_width // HD
    qkv_flat = w_qkv[0].reshape(width, 3 * local_width)
    out_weight = w_out[0]
    qv_bias = b_qv[0].astype(jnp.float32)
    out_bias = b_out[0].astype(jnp.float32)
    gains = ln_gain[0].astype(jnp.float32)
    shifts = ln_bias[0].astype(jnp.float32)
    down_bias = b_down[0].astype(jnp.float32)
    slopes = alibi_slopes(place * local_heads, local_heads, H)
    row_place = place * shard_rows + jnp.arange(shard_rows)
    kept_rows = 0

    def key_mask(length):
        return jnp.arange(full_rows) < length

    def after_attention(values, attended, bias, gain_rows, shift_rows):
        return layer_norm(values + attended + bias, gain_rows[0], shift_rows[0])

    def after_ffn(normed, lowered, bias, gain_rows, shift_rows):
        return layer_norm(normed + lowered + bias, gain_rows[1], shift_rows[1])

    def gather_inputs(values):
        return lax.all_gather(values.astype(jnp.bfloat16), "tensor", axis=0, tiled=True)

    def project(gathered):
        return jnp.dot(gathered, qkv_flat, preferred_element_type=jnp.float32).reshape(
            full_rows, 3, local_width
        )

    def attention_forward(values, length):
        gathered = gather_inputs(values)
        projected = project(gathered)
        mixed = attention_core(projected, qv_bias, slopes, key_mask(length))[5]

        def term(start, count):
            return jnp.dot(mixed, out_weight, preferred_element_type=jnp.float32)

        return (
            lax.psum_scatter(
                term(jnp.int32(0), shard_rows * lax.axis_size("tensor")).astype(jnp.bfloat16),
                "tensor",
                scatter_dimension=0,
                tiled=True,
            ).astype(jnp.float32),
            gathered,
            projected,
        )

    up_local = w_up[0]
    up_bias_local = b_up[0].astype(jnp.float32)
    down_local = w_down[0]

    def gather_normed(normed):
        return lax.all_gather(normed.astype(jnp.bfloat16), "tensor", axis=0, tiled=True)

    def ffn_forward(normed):
        lifted = jnp.einsum(
            "sd,gdf->sgf", gather_normed(normed), up_local, preferred_element_type=jnp.float32
        )
        hidden = geglu(lifted, up_bias_local).astype(jnp.bfloat16)

        def term(start, count):
            return jnp.einsum("sf,df->sd", hidden, down_local, preferred_element_type=jnp.float32)

        return lax.psum_scatter(
            term(jnp.int32(0), shard_rows * lax.axis_size("tensor")).astype(jnp.bfloat16),
            "tensor",
            scatter_dimension=0,
            tiled=True,
        ).astype(jnp.float32)

    def ffn_backward(normed, grad_lowered):
        gathered = gather_normed(normed)
        grad_whole = lax.all_gather(grad_lowered.astype(jnp.bfloat16), "tensor", axis=0, tiled=True)
        grad_lifted, grad_bias, up_grad, down_grad = ffn_grads(
            gathered, grad_whole, up_local, up_bias_local, down_local
        )

        def term(start, count):
            return jnp.einsum(
                "sgf,gdf->sd", grad_lifted, up_local, preferred_element_type=jnp.float32
            )

        grad_normed = lax.psum_scatter(
            term(jnp.int32(0), shard_rows * lax.axis_size("tensor")).astype(jnp.bfloat16),
            "tensor",
            scatter_dimension=0,
            tiled=True,
        ).astype(jnp.float32)
        return (grad_normed, (up_grad, grad_bias, down_grad))

    ffn_shapes = (up_local.shape, up_bias_local.shape, down_local.shape)

    def layer_forward(values, length):
        attended, gathered, projected = attention_forward(values, length)
        normed = after_attention(values, attended, out_bias, gains, shifts)
        lowered = ffn_forward(normed)
        return (
            after_ffn(normed, lowered, down_bias, gains, shifts),
            attended,
            lowered,
            gathered,
            projected,
        )

    def layer_backward(values, attended, lowered, length, grad_output):
        normed, attention_norm_back = jax.vjp(
            after_attention, values, attended, out_bias, gains, shifts
        )
        outcome, ffn_norm_back = jax.vjp(after_ffn, normed, lowered, down_bias, gains, shifts)
        grad_normed, grad_lowered, grad_down_bias, gain_late, shift_late = ffn_norm_back(
            grad_output
        )
        grad_from_ffn, ffn_terms = ffn_backward(normed, grad_lowered)
        grad_values, grad_attended, grad_out_bias, gain_early, shift_early = attention_norm_back(
            grad_normed + grad_from_ffn
        )
        gathered = gather_inputs(values)
        projected = project(gathered)
        grad_whole = lax.all_gather(
            grad_attended.astype(jnp.bfloat16), "tensor", axis=0, tiled=True
        )
        mask = key_mask(length)
        pieces = attention_core(projected, qv_bias, slopes, mask)
        mixed_low = pieces[5]
        out_grad = jnp.einsum(
            "se,sd->ed", mixed_low, grad_whole, preferred_element_type=jnp.float32
        )
        grad_mixed = jnp.einsum(
            "sd,ed->se", grad_whole, out_weight, preferred_element_type=jnp.float32
        )
        grad_projected, qv_grad = attention_back(pieces, grad_mixed, mask)
        qkv_grad = jnp.einsum(
            "sd,sx->dx", gathered, grad_projected, preferred_element_type=jnp.float32
        )

        def term(start, count):
            return jnp.einsum(
                "sx,dx->sd", grad_projected, qkv_flat, preferred_element_type=jnp.float32
            )

        grad_inputs = grad_values + lax.psum_scatter(
            term(jnp.int32(0), shard_rows * lax.axis_size("tensor")).astype(jnp.bfloat16),
            "tensor",
            scatter_dimension=0,
            tiled=True,
        ).astype(jnp.float32)
        terms = (
            qkv_grad,
            qv_grad,
            out_grad,
            grad_out_bias,
            gain_early + gain_late,
            shift_early + shift_late,
            ffn_terms[0],
            ffn_terms[1],
            ffn_terms[2],
            grad_down_bias,
        )
        return (grad_inputs, terms)

    def keep(store, item, batch, valid):
        old = lax.dynamic_index_in_dim(store, batch, 0, keepdims=False)
        return lax.dynamic_update_index_in_dim(store, jnp.where(valid, item, old), batch, 0)

    def forward_step(step, carry):
        (
            received,
            kept_values,
            kept_attended,
            kept_lowered,
            produced,
            kept_gathered,
            kept_projected,
        ) = carry
        index = step - section
        valid = (index >= 0) & (index < batches)
        batch = jnp.clip(index, 0, batches - 1)
        fresh = lax.dynamic_index_in_dim(
            inputs, jnp.minimum(step, batches - 1), 0, keepdims=False
        ).astype(jnp.float32)
        values = jnp.where(section == 0, fresh, received.astype(jnp.float32))
        output, attended, lowered, gathered, projected = layer_forward(values, lengths[batch])
        sent = output.astype(jnp.bfloat16)
        kept_values = keep(kept_values, values, batch, valid)
        kept_attended = keep(kept_attended, attended, batch, valid)
        kept_lowered = keep(kept_lowered, lowered, batch, valid)
        produced = keep(produced, sent, batch, valid)
        kept_gathered = keep(kept_gathered, gathered[:kept_rows], batch, valid)
        kept_projected = keep(kept_projected, projected[:kept_rows], batch, valid)
        received = shifted(sent, "section", 1)
        return (
            received,
            kept_values,
            kept_attended,
            kept_lowered,
            produced,
            kept_gathered,
            kept_projected,
        )

    store_zeros = jnp.zeros((batches, shard_rows, width), jnp.float32)
    gathered_zeros = jnp.zeros((batches, kept_rows, width), jnp.bfloat16)
    projected_zeros = jnp.zeros((batches, kept_rows, 3, local_width), jnp.float32)
    start_forward = (
        jnp.zeros((shard_rows, width), jnp.bfloat16),
        store_zeros,
        store_zeros,
        store_zeros,
        jnp.zeros((batches, shard_rows, width), jnp.bfloat16),
        gathered_zeros,
        projected_zeros,
    )
    received, kept_values, kept_attended, kept_lowered, produced, kept_gathered, kept_projected = (
        lax.fori_loop(0, batches + last_section, forward_step, start_forward)
    )

    def backward_step(step, carry):
        received, totals, grads_in = carry
        index = step - (last_section - section)
        valid = (index >= 0) & (index < batches)
        batch = jnp.clip(index, 0, batches - 1)
        length = lengths[batch]
        outer = lax.dynamic_index_in_dim(cotangent, batch, 0, keepdims=False).astype(jnp.float32)
        outer = outer * (row_place < length).astype(jnp.float32)[:, None]
        grad_output = jnp.where(section == last_section, outer, received.astype(jnp.float32))
        grad_output = jnp.where(valid, grad_output, 0.0)
        values = lax.dynamic_index_in_dim(kept_values, batch, 0, keepdims=False)
        attended = lax.dynamic_index_in_dim(kept_attended, batch, 0, keepdims=False)
        lowered = lax.dynamic_index_in_dim(kept_lowered, batch, 0, keepdims=False)
        grad_inputs, terms = layer_backward(values, attended, lowered, length, grad_output)
        totals = jax.tree.map(jnp.add, totals, terms)
        grads_in = keep(grads_in, grad_inputs, batch, valid)
        received = shifted(grad_inputs.astype(jnp.bfloat16), "section", -1)
        return (received, totals, grads_in)

    start_totals = (
        jnp.zeros((width, 3 * local_width), jnp.float32),
        jnp.zeros((2, local_width), jnp.float32),
        jnp.zeros((local_width, width), jnp.float32),
        jnp.zeros((width,), jnp.float32),
        jnp.zeros((2, width), jnp.float32),
        jnp.zeros((2, width), jnp.float32),
        jnp.zeros(ffn_shapes[0], jnp.float32),
        jnp.zeros(ffn_shapes[1], jnp.float32),
        jnp.zeros(ffn_shapes[2], jnp.float32),
        jnp.zeros((width,), jnp.float32),
    )
    start_backward = (jnp.zeros((shard_rows, width), jnp.bfloat16), start_totals, store_zeros)
    received, totals, grads_in = lax.fori_loop(
        0, batches + last_section, backward_step, start_backward
    )
    (
        qkv_total,
        qv_total,
        out_total,
        out_bias_total,
        gain_total,
        shift_total,
        up_total,
        up_bias_total,
        down_total,
        down_bias_total,
    ) = totals
    qkv_sum, qv_sum, out_sum, up_sum, up_bias_sum, down_sum = (
        lax.psum(qkv_total.astype(jnp.bfloat16), "dp").astype(jnp.float32),
        lax.psum(qv_total.astype(jnp.bfloat16), "dp").astype(jnp.float32),
        lax.psum(out_total.astype(jnp.bfloat16), "dp").astype(jnp.float32),
        lax.psum(up_total.astype(jnp.bfloat16), "dp").astype(jnp.float32),
        lax.psum(up_bias_total.astype(jnp.bfloat16), "dp").astype(jnp.float32),
        lax.psum(down_total.astype(jnp.bfloat16), "dp").astype(jnp.float32),
    )
    out_bias_sum, gain_sum, shift_sum, down_bias_sum = lax.psum(
        (out_bias_total, gain_total, shift_total, down_bias_total), ("tensor", "dp")
    )
    return (
        produced[None],
        grads_in[None],
        qkv_sum.reshape(1, width, 3, local_width),
        qv_sum[None],
        out_sum[None],
        out_bias_sum[None],
        gain_sum[None],
        shift_sum[None],
        up_sum[None],
        up_bias_sum[None],
        down_sum[None],
        down_bias_sum[None],
    )


def by_sequence(
    inputs,
    cotangent,
    lengths,
    w_qkv,
    b_qv,
    w_out,
    b_out,
    ln_gain,
    ln_bias,
    w_up,
    b_up,
    w_down,
    b_down,
):
    batches, shard_rows, width = inputs.shape
    place = lax.axis_index("tensor")
    section = lax.axis_index("section")
    groups = lax.axis_size("dp")
    rows = 2 * shard_rows
    seqs = batches // 2
    local = w_qkv.shape[3]
    units = w_up.shape[3]
    heads = local // HD
    chips = groups // 2

    qkv_own = jnp.transpose(w_qkv[0], (1, 0, 2))
    out_own = w_out[0]
    up_own = w_up[0]
    down_own = w_down[0]
    first = section == 0
    norms = (b_out, ln_gain[0], ln_bias[0], b_down)
    table = np.exp2(-8.0 * (np.arange(2 * heads, dtype=np.float32) + 1.0) / H).astype(np.float32)
    slopes = jnp.asarray(np.concatenate([table, np.roll(table, heads)]))

    qkv_oth, out_oth, up_oth, down_oth, *rest = fetch_and_forward(
        (qkv_own, out_own, up_own, down_own),
        (b_qv[0], b_up[0]),
        inputs,
        cotangent,
        slopes,
        norms,
        lengths,
        chips,
        seqs,
    )
    weights = (qkv_own, qkv_oth, out_own, out_oth, up_own, up_oth, down_own, down_oth)
    biases, rest = rest[:2], rest[2:]
    x_first = outer = rest[:seqs]
    *kept, y = rest[seqs:]
    deps = [y]

    def forward(x, m, turn):
        nonlocal kept, deps
        *kept, y = layer_forward(x, weights, biases, slopes, norms, lengths, m, turn, kept, deps, seqs)
        deps = [y]
        return y

    y_first = [y] + [forward(x_first[m], m, 0) for m in range(1, seqs)]
    x_second = [lax.ppermute(y, "section", [(0, 1)]) for y in y_first]
    y_second = [forward(x_second[0], 0, 1)]
    produced = exchange_rows(y_first, deps)
    deps = [produced]
    y_second += [forward(x_second[m], m, 1) for m in range(1, seqs)]

    back = None
    sums = [[None] * seqs, [None] * seqs]

    got_second = None

    def backward(grad, m, turn, *extra):
        nonlocal back, deps, got_second
        results = layer_backward(grad, kept, weights, slopes, norms, lengths, m, turn, back, deps, seqs, *extra)
        back, (gx, gx_low, norm_sums, up_sums, qv_sums) = results[:7], results[7:12]
        if extra:
            got_second = results[12]
        deps = [norm_sums]
        sums[turn][m] = (norm_sums, up_sums, qv_sums)
        return gx, gx_low

    gx_second = [backward(outer[0], 0, 1)]
    gx_second.append(backward(outer[1], 1, 1, [*y_second, gx_second[0][1]]))
    grad_middle = [lax.ppermute(gx_second[m][1], "section", [(1, 0)]) for m in range(seqs)]
    x_all = jnp.stack([jnp.where(first, x_first[m], x_second[m]) for m in range(seqs)])
    deps = deps + [x_all]
    gx_first = [backward(grad_middle[0], 0, 0)]

    *reduced, packed, got, _, _, _, _, _, gx, _ = backward_and_reduce(
        grad_middle[1], kept, back, x_all, weights, slopes, norms, lengths, [*sums[0][0], *sums[1][0], *sums[1][1]], gx_first[0][1],
        gx_second[1][1], chips,
    )
    gx_all = [gx_first[0][0], gx] + [g[0] for g in gx_second]
    (
        down_sum, up_sum, qkv_sum, out_sum, grads_in, produced,
        qv_sum, out_bias_sum, gain_sum, shift_sum, up_bias_sum, down_bias_sum,
    ) = widen(reduced, gx_all, got, got_second, produced, y_second, packed, units, local)
    return (
        produced[None],
        grads_in[None],
        jnp.transpose(qkv_sum, (1, 0, 2))[None],
        qv_sum[None],
        out_sum[None],
        out_bias_sum,
        gain_sum[None],
        shift_sum[None],
        up_sum[None],
        up_bias_sum[None],
        down_sum,
        down_bias_sum,
    )


def solution(mesh):
    sections, parts, groups = (mesh.shape[name] for name in ("section", "tensor", "dp"))

    def run(*args):
        paired = sections == 2 and parts == 2 and groups % 2 == 0 and args[0].shape[0] == 4
        return (by_sequence if paired else on_device)(*args)

    return jax.shard_map(
        run,
        mesh=mesh,
        in_specs=(
            P("dp", "tensor", None),
            P("dp", "tensor", None),
            P("dp"),
            P("section", None, None, "tensor"),
            P("section", None, "tensor"),
            P("section", "tensor", None),
            P("section", None),
            P("section", None, None),
            P("section", None, None),
            P("section", None, None, "tensor"),
            P("section", None, "tensor"),
            P("section", None, "tensor"),
            P("section", None),
        ),
        out_specs=(
            P("section", "dp", "tensor", None),
            P("section", "dp", "tensor", None),
            P("section", None, None, "tensor"),
            P("section", None, "tensor"),
            P("section", "tensor", None),
            P("section", None),
            P("section", None, None),
            P("section", None, None),
            P("section", None, None, "tensor"),
            P("section", None, "tensor"),
            P("section", None, "tensor"),
            P("section", None),
        ),
        check_vma=False,
    )
```

```python
import math

import jax
import jax.numpy as jnp
import numpy as np
from jax import lax
from jax.experimental import pallas as pl
from jax.experimental.pallas import tpu as pltpu
from jax.sharding import PartitionSpec as P

H = 16
HD = 64
EPS = 1e-05
BF = jnp.bfloat16
F32 = jnp.float32
VMEM_LIMIT = 62 * 1024 * 1024
ANY = pl.BlockSpec(memory_space=pl.ANY)
SMEM = pl.BlockSpec(memory_space=pltpu.SMEM)
WHOLE = pl.BlockSpec(memory_space=pltpu.VMEM)
NN = (((1,), (0,)), ((), ()))
NT = (((1,), (1,)), ((), ()))
TN = (((0,), (0,)), ((), ()))
CW = 256
PER = CW // HD


def dot(a, b, dims=NN):
    return lax.dot_general(a, b, dims, preferred_element_type=F32)


def arrived(ref, sem):
    pltpu.make_async_copy(ref, ref, sem).wait()


def call(kernel, inputs, outputs, scratch, chain, deps, name, flops, nbytes, turn, remote=False):
    pairs = [item if isinstance(item, tuple) else (item, ANY) for item in inputs]
    args = [p[0] for p in pairs]
    specs = [p[1] for p in pairs]
    n_in = len(args)
    aliases = {}
    if chain is not None:
        for buffer, index in zip(chain, [index for index, item in enumerate(outputs) if item[2]]):
            aliases[len(args)] = index
            args.append(buffer)
            specs.append(ANY)
    args += deps
    specs += [ANY] * len(deps)
    n_args, n_out = len(args), len(outputs)
    params = {"collective_id": 3, "has_side_effects": True} if remote else {}

    def body(*refs):
        @pl.when(lax.axis_index("section") == turn)
        def _():
            kernel(refs[:n_in], refs[n_args : n_args + n_out], refs[n_args + n_out :])

    return pl.pallas_call(
        body,
        in_specs=specs,
        out_specs=[ANY] * n_out,
        out_shape=[jax.ShapeDtypeStruct(o[0], o[1]) for o in outputs],
        scratch_shapes=scratch,
        input_output_aliases=aliases,
        compiler_params=pltpu.CompilerParams(vmem_limit_bytes=VMEM_LIMIT, **params),
        cost_estimate=pl.CostEstimate(flops=flops, bytes_accessed=nbytes, transcendentals=0),
        name=name,
    )(*args)


NORM_SPECS = [WHOLE] * 4


def norm_rows(refs):
    out_bias, gain, shift, down_bias = refs
    rows = [out_bias[...], gain[0:1], shift[0:1], down_bias[...], gain[1:2], shift[1:2]]
    return [row.astype(F32) for row in rows]


def slope_of(table_ref, head):
    return table_ref[lax.axis_index("tensor") * (table_ref.shape[0] // 2) + head]


def pick(k, count, own, oth, make):
    @pl.when(k < count)
    def _():
        for src, dst, sem in make(own, k):
            pltpu.make_async_copy(src, dst, sem).start()

    @pl.when(k >= count)
    def _():
        for src, dst, sem in make(oth, k - count):
            pltpu.make_async_copy(src, dst, sem).start()


def block(index, size):
    return pl.ds(pl.multiple_of(index * size, size), size)


def copy(src, dst, sem):
    return pltpu.make_async_copy(src, dst, sem)


def fill_distance(dist_ref, length):
    rows = dist_ref.shape[0]
    keys = lax.broadcasted_iota(jnp.int32, (rows, rows), 0)
    places = lax.broadcasted_iota(jnp.int32, (rows, rows), 1)
    distance = jnp.abs(keys - places).astype(F32)
    dist_ref[...] = jnp.where(keys < length, distance, 1e12)


def normalize(v):
    mean = jnp.mean(v, axis=1, keepdims=True)
    centred = v - mean
    rstd = lax.rsqrt(jnp.mean(centred * centred, axis=1, keepdims=True) + EPS)
    return centred * rstd, rstd


def halves(rows):
    return [slice(0, rows // 2), slice(rows // 2, rows)]


class Forward:
    def __init__(self, rows, width, local, units):
        self.rows, self.width, self.local, self.units = rows, width, local, units
        self.ft = min(512, units)
        self.tiles = units // self.ft
        self.heads_steps = local // CW
        self.total = 2 * local

    def kept(self, slots):
        rows, width = self.rows, self.width
        shapes = [((slots, rows, self.total), BF)] * 4
        shapes += [((slots, 2 * self.heads_steps, 8, rows), F32)]
        shapes += [((slots, rows, 2 * self.units), BF)] * 3
        return shapes + [((slots, rows, width), BF)] * 3 + [((slots, rows, 128), F32)] * 2

    def scratch(self):
        rows, width, ft, total = self.rows, self.width, self.ft, self.total
        sem = pltpu.SemaphoreType.DMA
        return [
            pltpu.VMEM((rows, width), BF),
            pltpu.VMEM((2, 3, width, CW), BF),
            pltpu.VMEM((total, width), BF),
            pltpu.VMEM((2, 2, width, ft), BF),
            pltpu.VMEM((2, width, ft), BF),
            pltpu.VMEM((2, 3, rows, CW), BF),
            pltpu.VMEM((2, 8, rows), F32),
            pltpu.VMEM((rows, total), BF),
            pltpu.VMEM((rows, rows), F32),
            pltpu.VMEM((rows, width), F32),
            pltpu.VMEM((rows, width), F32),
            pltpu.VMEM((rows, width), BF),
            pltpu.VMEM((2, 3, rows, ft), BF),
            pltpu.VMEM((3, rows, width), BF),
            pltpu.VMEM((2, rows, 128), F32),
            sem, sem((2,)), sem((2,)), sem((2, 2)), sem((2, 4)), sem, sem((2, 3)), sem((6,)),
        ]

    def bind(self, x, weights, bias, up_bias, slopes, norms, slot, outs, scratch):
        self.x_hbm, self.weights, self.bias, self.up_bias, self.slopes, self.norms = x, weights, bias, up_bias, slopes, norms
        self.slot, self.outs = slot, outs
        (self.x, self.w, self.o, self.up, self.down, self.qkv, self.lse, self.mixed, self.dist, self.normed, self.acc,
         self.low, self.tile, self.row, self.stat, self.x_sem, self.w_sem, self.o_sem, self.f_sem, self.q_sem, self.m_sem,
         self.t_sem, self.r_sem) = scratch

    def start_x(self):
        copy(self.x_hbm, self.x, self.x_sem).start()

    def start_w(self, k):
        s = lax.rem(k, 2)
        pick(k, self.heads_steps, self.weights[0], self.weights[1],
             lambda ref, j: [(ref.at[:, :, block(j, CW)], self.w.at[s], self.w_sem.at[s])])

    def start_o(self, side):
        copy(self.weights[2 + side], self.o.at[pl.ds(side * self.local, self.local)], self.o_sem.at[side]).start()

    def start_f(self, k):
        s = lax.rem(k, 2)
        ft = self.ft
        pick(k, self.tiles, (self.weights[4], self.weights[6]), (self.weights[5], self.weights[7]),
             lambda ref, j: [(ref[0].at[:, :, block(j, ft)], self.up.at[s], self.f_sem.at[s, 0]),
                             (ref[1].at[:, block(j, ft)], self.down.at[s], self.f_sem.at[s, 1])])

    def write_qkv(self, i, s):
        cols = block(i, CW)
        return [copy(self.qkv.at[s, c], out.at[self.slot, :, cols], self.q_sem.at[s, c])
                for c, out in enumerate(self.outs[:3])] + [
            copy(self.lse.at[s], self.outs[4].at[self.slot, i], self.q_sem.at[s, 3])]

    def attention_step(self, i, ahead):
        s = lax.rem(i, 2)
        qkv = self.qkv
        arrived(self.w.at[s], self.w_sem.at[s])

        @pl.when(i >= 2)
        def _():
            for item in self.write_qkv(i - 2, s):
                item.wait()

        values = self.x[...]
        b = self.bias[:, block(i, CW)].astype(F32)
        qkv[s, 0] = (dot(values, self.w[s, 0]) + b[0:1]).astype(BF)
        qkv[s, 1] = dot(values, self.w[s, 1]).astype(BF)
        qkv[s, 2] = (dot(values, self.w[s, 2]) + b[1:2]).astype(BF)

        @pl.when(i + 2 < ahead)
        def _():
            self.start_w(i + 2)

        parts = []
        scores_of = []
        for head in range(PER):
            cols = slice(head * HD, (head + 1) * HD)
            query = qkv[s, 0, :, cols] * BF(1.0 / math.sqrt(HD))
            scores_of.append(dot(qkv[s, 1, :, cols], query, NT))
        lows = []
        for head in range(PER):
            scores = scores_of[head] - self.dist[...] * slope_of(self.slopes, i * PER + head)
            top = jnp.max(scores, axis=0, keepdims=True)
            likely = jnp.exp(scores - top)
            mass = jnp.sum(likely, axis=0, keepdims=True)
            lows.append((likely * (1.0 / mass)).astype(BF))
            self.lse[s, head : head + 1, :] = top + jnp.log(mass)
        for head in range(PER):
            cols = slice(head * HD, (head + 1) * HD)
            parts.append(dot(lows[head], qkv[s, 2, :, cols], TN).astype(BF))
        self.mixed[:, block(i, CW)] = jnp.concatenate(parts, axis=1)
        for item in self.write_qkv(i, s):
            item.start()

    def middle(self):
        rows, width = self.rows, self.width
        copy(self.mixed, self.outs[3].at[self.slot], self.m_sem).start()
        for side in range(2):
            arrived(self.o.at[pl.ds(side * self.local, self.local)], self.o_sem.at[side])
        vec = norm_rows(self.norms)
        for rs in halves(rows):
            attended = dot(self.mixed[rs, :], self.o[...])
            u, rstd = normalize(self.x[rs, :].astype(F32) + attended + vec[0])
            normed = u * vec[1] + vec[2]
            self.normed[rs, :] = normed
            self.low[rs, :] = normed.astype(BF)
            self.row[0, rs, :] = u.astype(BF)
            self.stat[0, rs, :] = jnp.broadcast_to(rstd, (rows // 2, 128))
            self.acc[rs, :] = jnp.zeros((rows // 2, width), F32)
        for index, item in enumerate(self.first_rows()):
            copy(*item, self.r_sem.at[index]).start()

    def first_rows(self):
        return [(self.low, self.outs[8].at[self.slot]), (self.row.at[0], self.outs[9].at[self.slot]),
                (self.stat.at[0], self.outs[11].at[self.slot])]

    def write_tiles(self, i, s):
        return [copy(self.tile.at[s, c], out.at[self.slot, :, block(i, self.ft)], self.t_sem.at[s, c])
                for c, out in enumerate(self.outs[5:8])]

    def ffn_step(self, i, ahead):
        s = lax.rem(i, 2)
        arrived(self.up.at[s], self.f_sem.at[s, 0])
        arrived(self.down.at[s], self.f_sem.at[s, 1])

        @pl.when(i >= 2)
        def _():
            for item in self.write_tiles(i - 2, s):
                item.wait()

        b = self.up_bias[:, block(i, self.ft)].astype(F32)
        low = self.low[...]
        gate = dot(low, self.up[s, 0]) + b[0:1]
        lift = dot(low, self.up[s, 1]) + b[1:2]
        cdf = 0.5 * lax.erf(gate * (1.0 / math.sqrt(2.0))) + 0.5
        act = gate * cdf
        slope = cdf + gate * (jnp.exp(gate * gate * -0.5) * (1.0 / math.sqrt(2.0 * math.pi)))
        self.tile[s, 0] = act.astype(BF)
        self.tile[s, 1] = (lift * slope).astype(BF)
        hidden = (act * lift).astype(BF)
        self.tile[s, 2] = hidden
        self.acc[...] += dot(hidden, self.down[s], NT)

        @pl.when(i + 2 < ahead)
        def _():
            self.start_f(i + 2)

        for item in self.write_tiles(i, s):
            item.start()

    def finish(self, y_out):
        rows = self.rows
        vec = norm_rows(self.norms)
        for rs in halves(rows):
            u, rstd = normalize(self.normed[rs, :] + self.acc[rs, :] + vec[3])
            self.row[1, rs, :] = u.astype(BF)
            self.stat[1, rs, :] = jnp.broadcast_to(rstd, (rows // 2, 128))
            self.row[2, rs, :] = (u * vec[4] + vec[5]).astype(BF)
        ends = [(self.row.at[1], self.outs[10].at[self.slot]), (self.stat.at[1], self.outs[12].at[self.slot]),
                (self.row.at[2], y_out)]
        for index, item in enumerate(ends):
            copy(*item, self.r_sem.at[3 + index]).start()
        for index, item in enumerate(self.first_rows() + ends):
            copy(*item, self.r_sem.at[index]).wait()
        copy(self.mixed, self.outs[3].at[self.slot], self.m_sem).wait()
        for i in (2 * self.heads_steps - 2, 2 * self.heads_steps - 1):
            for item in self.write_qkv(jnp.int32(i), i % 2):
                item.wait()
        for i in (2 * self.tiles - 2, 2 * self.tiles - 1):
            for item in self.write_tiles(jnp.int32(i), i % 2):
                item.wait()

    def flops(self):
        rows, width, total = self.rows, self.width, self.total
        return 2 * rows * width * (4 * total + 6 * self.units) + 4 * rows * rows * total


def layer_forward(x, weights, biases, slopes, norms, lengths, m, turn, chain, deps, slots):
    rows, width = x.shape
    step = Forward(rows, width, weights[0].shape[2], weights[4].shape[2])

    def kernel(ins, outs, scratch):
        lengths_ref = ins[0]
        step.bind(ins[1], ins[2:10], ins[10], ins[11], ins[12], ins[13:17], m, outs[:13], scratch)
        step.start_x()
        for k in range(2):
            step.start_w(jnp.int32(k))
        for side in range(2):
            step.start_o(side)
        for k in range(2):
            step.start_f(jnp.int32(k))
        fill_distance(step.dist, lengths_ref[lax.axis_index("tensor") * slots + m])
        arrived(step.x, step.x_sem)

        @pl.loop(0, 2 * step.heads_steps)
        def _(i):
            step.attention_step(i, 2 * step.heads_steps)

        step.middle()

        @pl.loop(0, 2 * step.tiles)
        def _(i):
            step.ffn_step(i, 2 * step.tiles)

        step.finish(outs[13])

    return call(
        kernel,
        [(lengths, SMEM), x, *weights, *zip(biases, [WHOLE] * 2), (slopes, SMEM), *zip(norms, NORM_SPECS)],
        [shape + (True,) for shape in step.kept(slots)] + [((rows, width), BF, False)],
        step.scratch(),
        chain,
        deps,
        "layer_forward",
        step.flops(),
        54 << 20,
        turn,
    )


def layer_backward(grad, kept, weights, slopes, norms, lengths, m, turn, chain, deps, slots, sent=()):
    qkv_own, qkv_oth, o_own, o_oth, up_own, up_oth, down_own, down_oth = weights
    q, k, v, _, lse, act, slope, _, _, u1, u2, r1, r2 = kept
    rows, width = grad.shape
    local = qkv_own.shape[2]
    units = up_own.shape[2]
    heads_steps = local // CW
    ft = min(512, units)
    tiles = units // ft
    total = 2 * local

    def norm_back(grad_z, u, rstd, gain):
        t = grad_z * gain
        return rstd * (t - jnp.mean(t, axis=1, keepdims=True) - u * jnp.mean(t * u, axis=1, keepdims=True))

    def row_sum(values):
        return jnp.sum(values, axis=0, keepdims=True)

    def kernel(ins, outs, scratch):
        (lengths_ref, g_hbm, q_hbm, k_hbm, v_hbm, lse_hbm, a_hbm, b_hbm, u1_hbm, u2_hbm, r1_hbm, r2_hbm,
         qkv_own_ref, qkv_oth_ref, o_own_ref, o_oth_ref, up_own_ref, up_oth_ref, down_own_ref, down_oth_ref,
         slope_ref) = ins[:21]
        gg0_out, gg1_out, gl_out, ga_out, gq_out, gk_out, gv_out, gx_out, gxl_out, sums_out, ub_out, qv_out = outs[:12]
        (g_ref, u_ref, r_ref, up_ref, down_ref, ab_ref, gg_ref, low_ref, acc_ref, sums_ref, ub_ref, qv_ref,
         w_ref, o_ref, qkv_ref, lse_ref, gm_ref, dist_ref, gqkv_ref,
         g_sem, f_sem, t_sem, w_sem, q_sem, r_sem, x_send, x_recv) = scratch
        slot = m
        t = lax.axis_index("tensor")
        length = lengths_ref[t * slots + m]
        travelling = []
        if sent:
            cross = {"tensor": 1 - t}
            barrier = pltpu.get_barrier_semaphore()
            pl.semaphore_signal(barrier, inc=1, device_id=cross, device_id_type=pl.DeviceIdType.MESH)
            pl.semaphore_wait(barrier, 1)
            for index in range(len(sent)):
                travelling.append(
                    pltpu.make_async_remote_copy(
                        src_ref=ins[25 + index].at[block(1 - t, rows // 2)], dst_ref=outs[12].at[index],
                        send_sem=x_send.at[index], recv_sem=x_recv.at[index],
                        device_id=cross, device_id_type=pl.DeviceIdType.MESH,
                    )
                )
                travelling[-1].start()

        def start_f(i):
            s = lax.rem(i, 2)
            pick(i, tiles, (up_own_ref, down_own_ref), (up_oth_ref, down_oth_ref),
                 lambda ref, j: [(ref[0].at[:, :, block(j, ft)], up_ref.at[s], f_sem.at[s, 0]),
                                 (ref[1].at[:, block(j, ft)], down_ref.at[s], f_sem.at[s, 1])])
            for c, ref in enumerate((a_hbm, b_hbm)):
                copy(ref.at[slot, :, block(i, ft)], ab_ref.at[s, c], f_sem.at[s, 2 + c]).start()

        def start_w(i):
            s = lax.rem(i, 2)
            pick(i, heads_steps, (qkv_own_ref, o_own_ref), (qkv_oth_ref, o_oth_ref),
                 lambda ref, j: [(ref[0].at[:, :, block(j, CW)], w_ref.at[s], w_sem.at[s, 0]),
                                 (ref[1].at[block(j, CW)], o_ref.at[s], w_sem.at[s, 1])])
            for c, ref in enumerate((q_hbm, k_hbm, v_hbm)):
                copy(ref.at[slot, :, block(i, CW)], qkv_ref.at[s, c], w_sem.at[s, 2 + c]).start()
            copy(lse_hbm.at[slot, i], lse_ref.at[s], w_sem.at[s, 5]).start()

        firsts = [(g_hbm, g_ref), (u2_hbm.at[slot], u_ref.at[1]), (r2_hbm.at[slot], r_ref.at[1]),
                  (u1_hbm.at[slot], u_ref.at[0]), (r1_hbm.at[slot], r_ref.at[0])]
        for index, (src, dst) in enumerate(firsts):
            copy(src, dst, g_sem.at[index]).start()
            if index == 2:
                start_f(jnp.int32(0))
                start_f(jnp.int32(1))
        start_w(jnp.int32(0))
        start_w(jnp.int32(1))
        vec = norm_rows(ins[21:25])
        fill_distance(dist_ref, length)
        for index, (src, dst) in enumerate(firsts[:3]):
            copy(src, dst, g_sem.at[index]).wait()
        sums = [jnp.zeros((1, width), F32)] * 3
        for rs in halves(rows):
            grad_y = g_ref[rs, :].astype(F32)
            if turn == 1:
                places = lax.broadcasted_iota(jnp.int32, (rows // 2, width), 0) + rs.start
                grad_y = jnp.where(places < length, grad_y, 0.0)
            u = u_ref[1, rs, :].astype(F32)
            grad_c = norm_back(grad_y, u, r_ref[1, rs, 0:1], vec[4])
            acc_ref[rs, :] = grad_c
            low_ref[0, rs, :] = grad_c.astype(BF)
            for index, values in enumerate((grad_y * u, grad_y, grad_c)):
                sums[index] += row_sum(values)
        for index in range(3):
            sums_ref[index : index + 1, :] = sums[index]
        copy(low_ref.at[0], gl_out.at[slot], r_sem.at[0]).start()

        def write_tiles(i, s):
            return [copy(gg_ref.at[s, c], out.at[slot, :, block(i, ft)], t_sem.at[s, c])
                    for c, out in enumerate((gg0_out, gg1_out))]

        @pl.loop(0, 2 * tiles)
        def _(i):
            s = lax.rem(i, 2)
            arrived(up_ref.at[s], f_sem.at[s, 0])
            arrived(down_ref.at[s], f_sem.at[s, 1])
            for c in range(2):
                arrived(ab_ref.at[s, c], f_sem.at[s, 2 + c])

            @pl.when(i >= 2)
            def _():
                for item in write_tiles(i - 2, s):
                    item.wait()

            gh = dot(low_ref[0], down_ref[s])
            g0 = (gh * ab_ref[s, 1].astype(F32)).astype(BF)
            g1 = (gh * ab_ref[s, 0].astype(F32)).astype(BF)
            gg_ref[s, 0] = g0
            gg_ref[s, 1] = g1
            ub_ref[0:1, block(i, ft)] = row_sum(g0.astype(F32))
            ub_ref[1:2, block(i, ft)] = row_sum(g1.astype(F32))
            acc_ref[...] += dot(g0, up_ref[s, 0], NT) + dot(g1, up_ref[s, 1], NT)

            @pl.when(i + 2 < 2 * tiles)
            def _():
                start_f(i + 2)

            for item in write_tiles(i, s):
                item.start()

        for index, (src, dst) in enumerate(firsts[3:]):
            copy(src, dst, g_sem.at[3 + index]).wait()
        sums = [jnp.zeros((1, width), F32)] * 3
        for rs in halves(rows):
            grad_n = acc_ref[rs, :]
            u = u_ref[0, rs, :].astype(F32)
            grad_a = norm_back(grad_n, u, r_ref[0, rs, 0:1], vec[1])
            low_ref[1, rs, :] = grad_a.astype(BF)
            acc_ref[rs, :] = grad_a
            for index, values in enumerate((grad_n * u, grad_n, grad_a)):
                sums[index] += row_sum(values)
        for index in range(3):
            sums_ref[3 + index : 4 + index, :] = sums[index]
        sums_ref[6:8, :] = jnp.zeros((2, width), F32)
        copy(low_ref.at[1], ga_out.at[slot], r_sem.at[1]).start()
        scale = BF(1.0 / math.sqrt(HD))

        def write_heads(i, s):
            return [copy(gqkv_ref.at[s, c], out.at[slot, :, block(i, CW)], q_sem.at[s, c])
                    for c, out in enumerate((gq_out, gk_out, gv_out))]

        @pl.loop(0, 2 * heads_steps)
        def _(i):
            s = lax.rem(i, 2)
            for index, ref in enumerate((w_ref.at[s], o_ref.at[s], qkv_ref.at[s, 0], qkv_ref.at[s, 1], qkv_ref.at[s, 2], lse_ref.at[s])):
                arrived(ref, w_sem.at[s, index])

            @pl.when(i >= 2)
            def _():
                for item in write_heads(i - 2, s):
                    item.wait()

            gm_ref[...] = dot(low_ref[1], o_ref[s], NT).astype(BF)
            parts = [[], [], []]
            scores_of = []
            for head in range(PER):
                cols = slice(head * HD, (head + 1) * HD)
                query = qkv_ref[s, 0, :, cols] * scale
                scores_of.append(dot(qkv_ref[s, 1, :, cols], query, NT))
            for head in range(PER):
                cols = slice(head * HD, (head + 1) * HD)
                query = qkv_ref[s, 0, :, cols] * scale
                key = qkv_ref[s, 1, :, cols]
                gm = gm_ref[:, cols]
                gw = dot(qkv_ref[s, 2, :, cols], gm, NT)
                scores = scores_of[head] - dist_ref[...] * slope_of(slope_ref, i * PER + head)
                likely = jnp.exp(scores - lse_ref[s, head : head + 1, :])
                parts[2].append(dot(likely.astype(BF), gm).astype(BF))
                t = likely * gw
                inner = jnp.sum(t, axis=0, keepdims=True)
                gs = (t - likely * inner).astype(BF)
                parts[1].append(dot(gs, query).astype(BF))
                parts[0].append(dot(key * scale, gs, TN).astype(BF).T)
            for c in range(3):
                gqkv_ref[s, c] = jnp.concatenate(parts[c], axis=1)
            for index, c in enumerate((0, 2)):
                qv_ref[index : index + 1, block(i, CW)] = row_sum(gqkv_ref[s, c].astype(F32))
            acc_ref[...] += (
                dot(gqkv_ref[s, 0], w_ref[s, 0], NT)
                + dot(gqkv_ref[s, 1], w_ref[s, 1], NT)
                + dot(gqkv_ref[s, 2], w_ref[s, 2], NT)
            )

            @pl.when(i + 2 < 2 * heads_steps)
            def _():
                start_w(i + 2)

            for item in write_heads(i, s):
                item.start()

        g_ref[...] = acc_ref[...].astype(BF)
        ends = [(g_ref, gxl_out), (acc_ref, gx_out), (sums_ref, sums_out), (ub_ref, ub_out), (qv_ref, qv_out)]
        for index, (src, dst) in enumerate(ends):
            copy(src, dst, r_sem.at[2 + index]).start()
        for index, (src, dst) in enumerate([(low_ref.at[0], gl_out.at[slot]), (low_ref.at[1], ga_out.at[slot])] + ends):
            copy(src, dst, r_sem.at[index]).wait()
        for i in (2 * tiles - 2, 2 * tiles - 1):
            for item in write_tiles(jnp.int32(i), i % 2):
                item.wait()
        for i in (2 * heads_steps - 2, 2 * heads_steps - 1):
            for item in write_heads(jnp.int32(i), i % 2):
                item.wait()
        for item in travelling:
            item.wait()

    sem = pltpu.SemaphoreType.DMA
    return call(
        kernel,
        [(lengths, SMEM), grad, q, k, v, lse, act, slope, u1, u2, r1, r2, *weights, (slopes, SMEM), *zip(norms, NORM_SPECS), *sent],
        [((slots, rows, 2 * units), BF, True)] * 2
        + [((slots, rows, width), BF, True)] * 2
        + [((slots, rows, total), BF, True)] * 3
        + [
            ((rows, width), F32, False),
            ((rows, width), BF, False),
            ((8, width), F32, False),
            ((2, 2 * units), F32, False),
            ((2, total), F32, False),
        ]
        + ([((len(sent), rows // 2, width), BF, False)] if sent else []),
        [
            pltpu.VMEM((rows, width), BF),
            pltpu.VMEM((2, rows, width), BF),
            pltpu.VMEM((2, rows, 128), F32),
            pltpu.VMEM((2, 2, width, ft), BF),
            pltpu.VMEM((2, width, ft), BF),
            pltpu.VMEM((2, 2, rows, ft), BF),
            pltpu.VMEM((2, 2, rows, ft), BF),
            pltpu.VMEM((2, rows, width), BF),
            pltpu.VMEM((rows, width), F32),
            pltpu.VMEM((8, width), F32),
            pltpu.VMEM((2, 2 * units), F32),
            pltpu.VMEM((2, total), F32),
            pltpu.VMEM((2, 3, width, CW), BF),
            pltpu.VMEM((2, CW, width), BF),
            pltpu.VMEM((2, 3, rows, CW), BF),
            pltpu.VMEM((2, 8, rows), F32),
            pltpu.VMEM((rows, CW), BF),
            pltpu.VMEM((rows, rows), F32),
            pltpu.VMEM((2, 3, rows, CW), BF),
            sem((5,)), sem((2, 4)), sem((2, 2)), sem((2, 6)), sem((2, 3)), sem((7,)), sem((4,)), sem((4,)),
        ],
        chain,
        deps,
        "layer_backward",
        2 * rows * width * (4 * total + 6 * units) + 10 * rows * rows * total,
        70 << 20,
        turn,
        bool(sent),
    )


MESH = pl.DeviceIdType.MESH
CORE_LAG = 2
CROSS_LAG = 2
CHAIN_LAG = 2


def neighbours():
    t = lax.axis_index("tensor")
    d = lax.axis_index("dp")
    last = lax.axis_size("dp") // 2 - 1
    c = lax.rem(d, 2)
    z = d // 2
    return t, c, z, last, {"dp": d + 1 - 2 * c}, {"tensor": 1 - t}, {"dp": d + 2}, {"dp": d - 2}


def greet(c, z, chips, core, cross):
    barrier = pltpu.get_barrier_semaphore()
    pl.semaphore_signal(barrier, inc=1, device_id=core, device_id_type=MESH)
    pl.semaphore_signal(barrier, inc=1, device_id=cross, device_id_type=MESH)
    for shift in range(1, chips):
        chip = lax.rem(z + shift, chips)
        pl.semaphore_signal(barrier, inc=1, device_id={"dp": chip * 2 + c}, device_id_type=MESH)
    pl.semaphore_wait(barrier, 1 + chips)


def fetch_and_forward(weights, biases, inputs, cotangent, slopes, norms, lengths, chips, slots):
    seqs = inputs.shape[0] // 2
    shard_rows, width = inputs.shape[1:]
    rows = 2 * shard_rows
    groups = 2 * chips
    qkv, out, up, down = weights
    local, units = qkv.shape[2], up.shape[2]
    step = Forward(rows, width, local, units)
    ft, tiles = step.ft, step.tiles
    bias_widths = [b.shape[1] for b in biases]
    QKV, OUT, UP, DOWN, ROWS, BIAS = range(6)

    plan = [(UP, 0, groups), (ROWS, 0, 0), (BIAS, 0, 0), (BIAS, 1, 0)]
    plan += [(UP, part, groups) for part in range(1, tiles)]
    plan += [(DOWN, part, groups) for part in range(tiles - 2)]
    plan += [(QKV, part, 2) for part in range(3)] + [(OUT, 0, 2)]
    plan += [(DOWN, part, 2) for part in range(tiles - 2, tiles)]
    plan += [(ROWS, part, 0) for part in range(1, seqs)]
    n = len(plan)
    number = {item[:2]: index for index, item in enumerate(plan)}

    def size(index):
        kind, part, pieces = plan[index]
        whole = {QKV: width * local, OUT: local * width, UP: 2 * width * ft, DOWN: width * ft, ROWS: shard_rows * width, BIAS: 64}
        return whole[kind] / max(1, pieces)

    events, clock, busy = [], 0.0, 0.0
    for index, (kind, part, pieces) in enumerate(plan):
        clock += size(index)
        events.append((clock + 132000, index, 0))
        if pieces == groups:
            start = max(clock, busy)
            busy = start + size(index) * (chips - 1) * 1.0
            events += [(start + (size(index) * 1.0 + 132000) * hop, index, hop) for hop in range(1, chips)]
    events.sort()
    when = {event[1:]: event[0] for event in events}

    def ready(*keys):
        return max(when[key] for k in keys for key in when if key[0] == number[k])

    needs = [[(ROWS, 0), (BIAS, 0)], []] + [[(QKV, part) for part in range(3)], []] + [[(OUT, 0), (BIAS, 1)]]
    needs += [[] for _ in range(tiles - 1)]
    needs += [[(UP, part), (DOWN, part)] for part in range(tiles)] + [[]]
    assert step.heads_steps == 2
    rounds, taken = [], 0
    for need in needs:
        mine = []
        if need:
            limit = ready(*need)
            while taken < len(events) and events[taken][0] <= limit:
                mine.append(events[taken][1:])
                taken += 1
        rounds.append((mine, need))
    rest = [event[1:] for event in events[taken:]]
    n_rounds = len(rounds)
    n_kept = len(step.kept(slots))

    def kernel(*refs):
        lengths_ref, slope_ref, norm_refs = refs[0], refs[1], refs[2:6]
        refs = refs[6:]
        ins, bias_ins, held_refs = refs[:4], refs[4:6], refs[6:8]
        outs, bias_outs, row_refs = refs[8:12], refs[12:14], refs[14 : 14 + seqs]
        kept_refs = refs[14 + seqs : 14 + seqs + n_kept]
        y_ref = refs[14 + seqs + n_kept]
        stage, qv_bias, ub_bias, x_send, x_recv, c_send, c_recv, u_send, u_recv, d_send, d_recv, l_sem, b_sem = refs[
            15 + seqs + n_kept : 28 + seqs + n_kept
        ]
        t, c, z, last, core, cross, above, below = neighbours()
        section = lax.axis_index("section")
        greet(c, z, chips, core, cross)
        paired = [item for pair in zip(ins, outs) for item in pair]
        step.bind(
            row_refs[0], paired, qv_bias, ub_bias, slope_ref, norm_refs, 0, kept_refs, refs[28 + seqs + n_kept :]
        )

        def span(part):
            return block(part, shard_rows)

        def bias_part(m, side):
            return bias_outs[m].at[:, pl.ds(side * bias_widths[m], bias_widths[m])]

        def piece(side, index, chip, on):
            kind, part, pieces = plan[index]
            place = chip * 2 + on if pieces == groups else on
            ref = (ins, outs)[side][kind]
            if kind == QKV:
                return ref.at[part, block(place, width // pieces)]
            if kind == OUT:
                return ref.at[block(place, local // pieces)]
            cols = pl.ds(part * ft, ft)
            if kind == DOWN:
                return ref.at[block(place, width // pieces), cols]
            per = pieces // 2
            return ref.at[place // per, block(lax.rem(place, per), width // per), cols]

        def cross_copy(index, held_ref=None):
            kind, m, pieces = plan[index]
            if kind == ROWS:
                src = (held_refs[0] if held_ref is None else held_ref).at[(1 - t) * seqs + m]
                dst = row_refs[m].at[span(t)]
            elif kind == BIAS:
                src, dst = bias_ins[m], bias_part(m, 1)
            else:
                src, dst = piece(0, index, z, c), piece(1, index, z, c)
            return pltpu.make_async_remote_copy(
                src_ref=src, dst_ref=dst, send_sem=x_send.at[index], recv_sem=x_recv.at[index],
                device_id=cross, device_id_type=MESH,
            )

        def pass_on(index, chip, send, recv, device):
            place = piece(1, index, chip, c)
            return pltpu.make_async_remote_copy(
                src_ref=place, dst_ref=place, send_sem=send.at[index, chip], recv_sem=recv.at[index, chip],
                device_id=device, device_id_type=MESH,
            )

        def got(index, chip, on, sem):
            arrived(piece(1, index, chip, on), sem)

        for m in range(2):
            copy(bias_ins[m], bias_part(m, 0), b_sem.at[m]).start()
        for index in range(n):
            if plan[index][0] == ROWS:
                for turn in range(2):
                    @pl.when(section == turn)
                    def _(index=index, turn=turn):
                        cross_copy(index, held_refs[turn]).start()
            else:
                cross_copy(index).start()
        for turn in range(2):
            @pl.when(section == turn)
            def _(turn=turn):
                copy(held_refs[turn].at[pl.ds(t * seqs, seqs)], stage, l_sem.at[0]).start()

        @pl.when(section == 0)
        def _():
            for k in range(2):
                step.start_w(jnp.int32(k))
            step.start_o(0)
            for k in range(2):
                step.start_f(jnp.int32(k))
            fill_distance(step.dist, lengths_ref[t * seqs])

        arrived(stage, l_sem.at[0])
        for m in range(seqs):
            copy(stage.at[m], row_refs[m].at[span(t)], l_sem.at[m]).start()
        for m in range(seqs):
            arrived(stage.at[m], l_sem.at[m])
        for m in range(2):
            copy(bias_ins[m], bias_part(m, 0), b_sem.at[m]).wait()

        def handle(index, hop):
            kind, m, pieces = plan[index]
            if kind == ROWS:
                arrived(row_refs[m].at[span(1 - t)], x_recv.at[index])
            elif kind == BIAS:
                arrived(bias_part(m, 1), x_recv.at[index])
            elif hop == 0:
                got(index, z, c, x_recv.at[index])
                if pieces == groups:
                    @pl.when(z < last)
                    def _():
                        pass_on(index, z, u_send, u_recv, above).start()

                    @pl.when(z > 0)
                    def _():
                        pass_on(index, z, d_send, d_recv, below).start()

                pass_on(index, z, c_send, c_recv, core).start()
            else:
                @pl.when(z - hop >= 0)
                def _():
                    got(index, z - hop, c, u_recv.at[index, z - hop])

                    @pl.when(z < last)
                    def _():
                        pass_on(index, z - hop, u_send, u_recv, above).start()

                    pass_on(index, z - hop, c_send, c_recv, core).start()

                @pl.when(z + hop <= last)
                def _():
                    got(index, z + hop, c, d_recv.at[index, z + hop])

                    @pl.when(z > 0)
                    def _():
                        pass_on(index, z + hop, d_send, d_recv, below).start()

                    pass_on(index, z + hop, c_send, c_recv, core).start()

        def from_core(key):
            index = number[key]
            kind, m, pieces = plan[index]
            if pieces == groups:
                for chip in range(chips):
                    got(index, chip, 1 - c, c_recv.at[index, chip])
            elif pieces:
                got(index, z, 1 - c, c_recv.at[index, z])

        @pl.loop(0, n_rounds)
        def _(tau):
            for number_, (mine, need) in enumerate(rounds):
                if not (mine or need):
                    continue

                @pl.when(tau == number_)
                def _(number_=number_, mine=mine, need=need):
                    for index, hop in mine:
                        handle(index, hop)
                    for key in need:
                        from_core(key)
                    for key in need:
                        if key == (BIAS, 0):
                            @pl.when(section == 0)
                            def _():
                                step.start_x()
                                copy(bias_outs[0], qv_bias, b_sem.at[0]).start()
                                copy(bias_outs[0], qv_bias, b_sem.at[0]).wait()
                                arrived(step.x, step.x_sem)
                        elif key == (QKV, 2):
                            @pl.when(section == 0)
                            def _():
                                for k in range(2, 4):
                                    step.start_w(jnp.int32(k))
                        elif key == (OUT, 0):
                            @pl.when(section == 0)
                            def _():
                                step.start_o(1)
                        elif key == (BIAS, 1):
                            @pl.when(section == 0)
                            def _():
                                copy(bias_outs[1], ub_bias, b_sem.at[1]).start()
                                copy(bias_outs[1], ub_bias, b_sem.at[1]).wait()
                        elif key[0] == DOWN:
                            @pl.when(section == 0)
                            def _(key=key):
                                step.start_f(jnp.int32(tiles + key[1]))

            @pl.when(section == 0)
            def _():
                @pl.when(tau < 4)
                def _():
                    step.attention_step(tau, 2)

                @pl.when(tau == 4)
                def _():
                    step.middle()

                @pl.when(tau > 4)
                def _():
                    step.ffn_step(tau - 5, tiles)

        @pl.when(section == 0)
        def _():
            step.finish(y_ref)

        for index, hop in rest:
            handle(index, hop)
        for index in range(n):
            kind, part, pieces = plan[index]
            cross_copy(index).wait_send()
            if pieces == 2:
                pass_on(index, z, c_send, c_recv, core).wait_send()
            if pieces != groups:
                continue
            for chip in range(chips):
                pass_on(index, chip, c_send, c_recv, core).wait_send()

                @pl.when((chip <= z) & (z < last))
                def _(chip=chip):
                    pass_on(index, chip, u_send, u_recv, above).wait_send()

                @pl.when((chip >= z) & (z > 0))
                def _(chip=chip):
                    pass_on(index, chip, d_send, d_recv, below).wait_send()

    sem = pltpu.SemaphoreType.DMA
    return pl.pallas_call(
        kernel,
        in_specs=[SMEM, SMEM] + NORM_SPECS + [ANY] * 8,
        out_specs=[ANY] * (7 + seqs + n_kept),
        out_shape=[jax.ShapeDtypeStruct(w.shape, BF) for w in weights]
        + [jax.ShapeDtypeStruct((2, 2 * size_), BF) for size_ in bias_widths]
        + [jax.ShapeDtypeStruct((rows, width), BF)] * seqs
        + [jax.ShapeDtypeStruct(*shape) for shape in step.kept(slots)]
        + [jax.ShapeDtypeStruct((rows, width), BF)],
        scratch_shapes=[pltpu.VMEM((seqs, shard_rows, width), BF)]
        + [pltpu.VMEM((2, 2 * size_), BF) for size_ in bias_widths]
        + [sem((n,)), sem((n,))]
        + [sem((n, chips))] * 6
        + [sem((seqs,)), sem((2,))]
        + step.scratch(),
        compiler_params=pltpu.CompilerParams(collective_id=1, has_side_effects=True, vmem_limit_bytes=VMEM_LIMIT),
        cost_estimate=pl.CostEstimate(flops=step.flops(), bytes_accessed=90 << 20, transcendentals=0),
        name="fetch_and_forward",
    )(lengths, slopes, *norms, *weights, *biases, inputs, cotangent)


def norm_back(grad_z, u, rstd, gain):
    t = grad_z * gain
    return rstd * (t - jnp.mean(t, axis=1, keepdims=True) - u * jnp.mean(t * u, axis=1, keepdims=True))


def row_sum(values):
    return jnp.sum(values, axis=0, keepdims=True)


def backward_and_reduce(grad, kept, back, x_all, weights, slopes, norms, lengths, sums, low_grad, second, chips):
    q, k_, v, mixed_all, lse, act, slope, hidden_all, normed_all, u1, u2, r1, r2 = kept
    gg0, gg1, gl, ga, gq, gk, gv = back
    rows, width = grad.shape
    local, units = weights[0].shape[2], weights[4].shape[2]
    ft = CW
    tiles = units // ft
    heads_steps = local // CW
    seqs = 2
    bt = 128
    lefts = [gl, normed_all, x_all, ga]
    rights = [hidden_all, gg0, gg1, gq, gk, gv, mixed_all]
    group_of = [0, 1, 1, 2, 2, 2, 3]
    member_of = [0, 0, 1, 0, 1, 2, 0]
    half = width // 2
    quarter = half // 2
    per_pair = ft // bt
    pairs = tiles
    ffn_blocks = 3 * per_pair * pairs
    head_blocks = local // bt
    total = ffn_blocks + 4 * head_blocks
    ring, mines, gives = 4, CORE_LAG + 1, 4
    ahead_of = 2
    drain = CORE_LAG + CROSS_LAG + 2 * (chips - 1) * CHAIN_LAG + 1
    shard_rows = rows // 2
    norm_at = 2 * tiles
    head_at = norm_at + 1
    end_at = head_at + 5 * 2 * heads_steps
    x_flip, ga_flip = ffn_blocks - per_pair, ffn_blocks + per_pair
    up_rows = units // width
    vec_shape = (6 + 4 * up_rows + 2, width)
    spread = 42
    last_turn = ahead_of - (ahead_of - end_at) * spread // (end_at + 1 - ahead_of) + 1
    assert spread >= end_at + 1 - ahead_of and last_turn < ahead_of + ffn_blocks - ring

    def kernel(*refs):
        lengths_ref, slope_ref, norm_refs, sum_refs = refs[0], refs[1], refs[2:6], refs[6:15]
        refs = refs[12:]
        g_hbm, q_hbm, k_hbm, v_hbm, lse_hbm, a_hbm, b_hbm, u1_hbm, u2_hbm, r1_hbm, r2_hbm = refs[3:14]
        (qkv_own_ref, qkv_oth_ref, o_own_ref, o_oth_ref, up_own_ref, up_oth_ref, down_own_ref, down_oth_ref) = refs[14:22]
        left_refs, right_refs = refs[22:26], refs[26:33]
        low_grad_ref, second_ref = refs[33:35]
        outs, sums_out, rows_out = refs[35:39], refs[39], refs[40]
        fresh = refs[41:46]
        gx_out, gxl_out = refs[46:48]
        (
            acc, from_x, from_z, flip, stage, tile, mine, give, vec, vec_in, vec_all,
            g_ref, u_ref, r_ref, low_ref, gacc_ref, w_ref, o_ref, qkv_ref, gqkv_ref, lse_ref, gm_ref, gs_ref, dist_ref,
            part_sums, ub_sums, qv_sums,
            tile_sem, stage_sem, give_send, core_recv, x_send, x_recv, z_send, z_recv, f_send, f_recv,
            store_sem, out_send, out_recv, v_send, v_recv, r_send, r_recv,
            g_sem, w_sem, t_sem, e_sem,
        ) = refs[48:]
        final = from_x
        t, c, z, last, core, cross, above, below = neighbours()
        section = lax.axis_index("section")
        first = section == 0
        greet(c, z, chips, core, cross)
        fresh_of = {1: fresh[0].at[0], 2: fresh[1].at[0], 3: fresh[2], 4: fresh[3], 5: fresh[4]}
        vec_w = norm_rows(norm_refs)

        def remote(src, dst, send, recv, device):
            return pltpu.make_async_remote_copy(
                src_ref=src, dst_ref=dst, send_sem=send, recv_sem=recv, device_id=device, device_id_type=MESH
            )

        def valid(k):
            return (k >= 0) & (k < total)

        def member(k, visit):
            for m in range(3):
                @pl.when((k < ffn_blocks) & (lax.rem(k, 3 * per_pair) // per_pair == m))
                def _(m=m):
                    visit(m, k // (3 * per_pair) * per_pair + lax.rem(k, per_pair))

            for m in range(3, 7):
                base = ffn_blocks + (m - 3) * head_blocks

                @pl.when((k >= base) & (k < base + head_blocks))
                def _(m=m, base=base):
                    visit(m, k - base)

        def load_tile(k):
            at = lax.rem(k, ring)

            def visit(m, j):
                count = right_refs[m].shape[2] // (2 * bt)
                for side in range(2):
                    cols = block(side * count + j, bt)
                    where = pl.ds(side * bt, bt)
                    copy(right_refs[m].at[0, :, cols], tile.at[at, 0, :, where], tile_sem.at[at]).start()
                    if m not in fresh_of:
                        copy(right_refs[m].at[1, :, cols], tile.at[at, 1, :, where], tile_sem.at[at]).start()
                        continue

                    @pl.when(first)
                    def _(cols=cols, where=where):
                        copy(fresh_of[m].at[:, cols], tile.at[at, 1, :, where], tile_sem.at[at]).start()

                    @pl.when(section == 1)
                    def _(cols=cols, where=where):
                        copy(right_refs[m].at[1, :, cols], tile.at[at, 1, :, where], tile_sem.at[at]).start()

            member(k, visit)

        def take_left(g, at, mine_low):
            copy(left_refs[g].at[0], stage.at[0], stage_sem.at[0]).start()
            if mine_low is None:
                copy(left_refs[g].at[1], stage.at[1], stage_sem.at[1]).start()
                arrived(stage.at[1], stage_sem.at[1])
            else:
                @pl.when(first)
                def _():
                    stage[1] = low_ref[mine_low]

                @pl.when(section == 1)
                def _():
                    copy(left_refs[g].at[1], stage.at[1], stage_sem.at[1]).start()
                    arrived(stage.at[1], stage_sem.at[1])

            arrived(stage.at[0], stage_sem.at[0])
            for m in range(seqs):
                flip[at, :, m * rows : (m + 1) * rows] = stage[m].T

        def place_of(u):
            return lax.rem(u, 2), u // 2

        def start_f(u):
            at = lax.rem(u, 2)
            side, j = place_of(u)
            pick(side * tiles + j, tiles, (up_own_ref, down_own_ref), (up_oth_ref, down_oth_ref),
                 lambda ref, jj: [(ref[0].at[:, :, block(jj, ft)], w_ref.at[at, pl.ds(0, 2)], w_sem.at[at, 0]),
                                  (ref[1].at[:, block(jj, ft)], w_ref.at[at, 2], w_sem.at[at, 1])])
            for n, ref in enumerate((a_hbm, b_hbm)):
                copy(ref.at[1, :, block(side * tiles + j, ft)], qkv_ref.at[at, n], w_sem.at[at, 2 + n]).start()

        def write_tile(u):
            at = lax.rem(u, 2)
            side, j = place_of(u)
            return [copy(gqkv_ref.at[at, n], fresh[n].at[0, :, block(side * tiles + j, ft)], t_sem.at[at, n]) for n in range(2)]

        def start_w(i):
            at = lax.rem(i, 2)
            pick(i, heads_steps, (qkv_own_ref, o_own_ref), (qkv_oth_ref, o_oth_ref),
                 lambda ref, j: [(ref[0].at[:, :, block(j, CW)], w_ref.at[at], w_sem.at[at, 0]),
                                 (ref[1].at[block(j, CW)], o_ref.at[at], w_sem.at[at, 1])])
            for n, ref in enumerate((q_hbm, k_hbm, v_hbm)):
                copy(ref.at[1, :, block(i, CW)], qkv_ref.at[at, n], w_sem.at[at, 2 + n]).start()
            copy(lse_hbm.at[1, i], lse_ref.at[at], w_sem.at[at, 5]).start()

        def write_heads(i):
            at = lax.rem(i, 2)
            return [copy(gqkv_ref.at[at, n], fresh[2 + n].at[:, block(i, CW)], t_sem.at[at, n]) for n in range(3)]

        def norm_load(index, u_hbm, r_hbm):
            return [copy(u_hbm.at[1], u_ref, g_sem.at[index]), copy(r_hbm.at[1], r_ref, g_sem.at[index + 1])]

        def begin():
            copy(g_hbm, g_ref, g_sem.at[0]).start()
            for item in norm_load(1, u2_hbm, r2_hbm):
                item.start()
            start_f(jnp.int32(0))
            start_f(jnp.int32(1))
            copy(g_hbm, g_ref, g_sem.at[0]).wait()
            for item in norm_load(1, u2_hbm, r2_hbm):
                item.wait()
            totals = [jnp.zeros((1, width), F32)] * 3
            for rs in halves(rows):
                grad_y = g_ref[rs, :].astype(F32)
                u = u_ref[rs, :].astype(F32)
                grad_c = norm_back(grad_y, u, r_ref[rs, 0:1], vec_w[4])
                gacc_ref[rs, :] = grad_c
                low_ref[0, rs, :] = grad_c.astype(BF)
                for index, values in enumerate((grad_y * u, grad_y, grad_c)):
                    totals[index] += row_sum(values)
            for index in range(3):
                part_sums[index : index + 1, :] = totals[index]
            for item in norm_load(1, u1_hbm, r1_hbm):
                item.start()

        def ffn_unit(u):
            at = lax.rem(u, 2)

            @pl.when(u >= 1)
            def _():
                for item in write_tile(u - 1):
                    item.wait()

            arrived(w_ref.at[at, pl.ds(0, 2)], w_sem.at[at, 0])
            arrived(w_ref.at[at, 2], w_sem.at[at, 1])
            for n in range(2):
                arrived(qkv_ref.at[at, n], w_sem.at[at, 2 + n])
            gh = dot(low_ref[0], w_ref[at, 2])
            g0 = (gh * qkv_ref[at, 1].astype(F32)).astype(BF)
            g1 = (gh * qkv_ref[at, 0].astype(F32)).astype(BF)
            gqkv_ref[at, 0] = g0
            gqkv_ref[at, 1] = g1
            side, j = place_of(u)
            cols = block(side * tiles + j, ft)
            ub_sums[0:1, cols] = row_sum(g0.astype(F32))
            ub_sums[1:2, cols] = row_sum(g1.astype(F32))
            gacc_ref[...] += dot(g0, w_ref[at, 0], NT) + dot(g1, w_ref[at, 1], NT)

            @pl.when(u + 2 < 2 * tiles)
            def _():
                start_f(u + 2)

            for item in write_tile(u):
                item.start()

        def norm_unit():
            for item in write_tile(jnp.int32(2 * tiles - 1)):
                item.wait()
            for i in range(2):
                start_w(jnp.int32(i))
            fill_distance(dist_ref, lengths_ref[t * seqs + 1])
            for item in norm_load(1, u1_hbm, r1_hbm):
                item.wait()
            totals = [jnp.zeros((1, width), F32)] * 3
            for rs in halves(rows):
                grad_n = gacc_ref[rs, :]
                u = u_ref[rs, :].astype(F32)
                grad_a = norm_back(grad_n, u, r_ref[rs, 0:1], vec_w[1])
                low_ref[1, rs, :] = grad_a.astype(BF)
                gacc_ref[rs, :] = grad_a
                for index, values in enumerate((grad_n * u, grad_n, grad_a)):
                    totals[index] += row_sum(values)
            for index in range(3):
                part_sums[3 + index : 4 + index, :] = totals[index]

        def head_unit(a):
            i = a // 5
            phase = lax.rem(a, 5)
            pair = phase // 2
            at = lax.rem(i, 2)
            scale = BF(1.0 / math.sqrt(HD))
            cols = block(lax.rem(pair, 2), 2 * HD)

            @pl.when(phase == 0)
            def _():
                for index, ref in enumerate(
                    (w_ref.at[at], o_ref.at[at], qkv_ref.at[at, 0], qkv_ref.at[at, 1], qkv_ref.at[at, 2], lse_ref.at[at])
                ):
                    arrived(ref, w_sem.at[at, index])

                @pl.when(i >= 2)
                def _():
                    for item in write_heads(i - 2):
                        item.wait()

                gm_ref[...] = dot(low_ref[1], o_ref[at], NT).astype(BF)

            @pl.when((phase == 0) | (phase == 2))
            def _():
                query2 = qkv_ref[at, 0, :, cols] * scale
                key2 = qkv_ref[at, 1, :, cols]
                value2 = qkv_ref[at, 2, :, cols]
                gm2 = gm_ref[:, cols]
                parts = []
                pairs_here = [slice(head * HD, (head + 1) * HD) for head in range(2)]
                scores_of = [dot(key2[:, here], query2[:, here], NT) for here in pairs_here]
                for head, here in enumerate(pairs_here):
                    gm = gm2[:, here]
                    scores = scores_of[head] - dist_ref[...] * slope_of(slope_ref, i * PER + pair * 2 + head)
                    likely = jnp.exp(scores - lse_ref[at, pl.ds(pair * 2 + head, 1), :])
                    parts.append(dot(likely.astype(BF), gm).astype(BF))
                    tt = likely * dot(value2[:, here], gm, NT)
                    inner = jnp.sum(tt, axis=0, keepdims=True)
                    gs_ref[head] = (tt - likely * inner).astype(BF)
                gqkv_ref[at, 2, :, cols] = jnp.concatenate(parts, axis=1)

            @pl.when((phase == 1) | (phase == 3))
            def _():
                query2 = qkv_ref[at, 0, :, cols] * scale
                key2 = qkv_ref[at, 1, :, cols] * scale
                parts = [[], []]
                for head in range(2):
                    here = slice(head * HD, (head + 1) * HD)
                    gs = gs_ref[head]
                    parts[1].append(dot(gs, query2[:, here]).astype(BF))
                    parts[0].append(dot(key2[:, here], gs, TN).astype(BF).T)
                for n in range(2):
                    gqkv_ref[at, n, :, cols] = jnp.concatenate(parts[n], axis=1)

            @pl.when(phase == 4)
            def _():
                for index, n in enumerate((0, 2)):
                    qv_sums[index : index + 1, block(i, CW)] = row_sum(gqkv_ref[at, n].astype(F32))
                gacc_ref[...] += (
                    dot(gqkv_ref[at, 0], w_ref[at, 0], NT)
                    + dot(gqkv_ref[at, 1], w_ref[at, 1], NT)
                    + dot(gqkv_ref[at, 2], w_ref[at, 2], NT)
                )

                @pl.when(i + 2 < 2 * heads_steps)
                def _():
                    start_w(i + 2)

                for item in write_heads(i):
                    item.start()

        def add_sums(norm_part, ub_part, qv_part):
            vec[0, 0:6] += norm_part[0:6]
            for own in range(2):
                @pl.when(t == own)
                def _(own=own):
                    for n in range(2):
                        for side in range(2):
                            place = own if side == 0 else 1 - own
                            for j in range(up_rows):
                                at = 6 + (2 * n + place) * up_rows + j
                                start = side * units + j * width
                                vec[0, at : at + 1] += ub_part[n : n + 1, start : start + width]
                            at = 6 + 4 * up_rows + n
                            cols = slice(place * local, (place + 1) * local)
                            vec[0, at : at + 1, cols] += qv_part[n : n + 1, side * local : (side + 1) * local]

        ends = [(g_ref, gxl_out), (gacc_ref, gx_out)]

        def end_unit():
            for i in (2 * heads_steps - 2, 2 * heads_steps - 1):
                for item in write_heads(jnp.int32(i)):
                    item.wait()
            g_ref[...] = gacc_ref[...].astype(BF)
            for index, item in enumerate(ends):
                copy(*item, e_sem.at[index]).start()
            add_sums(part_sums, ub_sums, qv_sums)
            for index, item in enumerate(ends):
                copy(*item, e_sem.at[index]).wait()

        vec[0] = jnp.zeros(vec_shape, F32)

        @pl.when(first)
        def _():
            begin()
            add_sums(*sum_refs[:3])

        @pl.when(section == 1)
        def _():
            add_sums(*sum_refs[3:6])
            add_sums(*sum_refs[6:9])

        take_left(0, 0, 0)
        vec_core = remote(vec.at[0], vec_in.at[0], v_send.at[0], v_recv.at[0], core)
        vec_cross = remote(vec.at[1], vec_in.at[1], v_send.at[1], v_recv.at[1], cross)

        def row_copy(m, source):
            return remote(
                source.at[block(1 - t, shard_rows)], rows_out.at[m], r_send.at[m], r_recv.at[m], cross
            )

        row_plan = [(0, 0, low_grad_ref, True), (0, 1, gxl_out, False), (1, 1, second_ref, False)]
        for number, m, source, early in row_plan:
            if early:
                @pl.when(section == number)
                def _(m=m, source=source):
                    row_copy(m, source).start()

        def unit_at(turn):
            later = ahead_of + (turn - ahead_of) * (end_at + 1 - ahead_of) // spread
            return jnp.where(turn < ahead_of, turn, later)

        up = pl.ds(0, quarter)
        down = pl.ds(quarter, quarter)
        sides = ((up, 0, z, above, below), (down, 1, last - z, below, above))

        @pl.loop(0, ahead_of + total + drain)
        def _(turn):
            s = turn - ahead_of

            unit = unit_at(turn)

            @pl.when(first & (unit != unit_at(turn - 1)))
            def _():
                @pl.when(unit < norm_at)
                def _():
                    ffn_unit(unit)

                @pl.when(unit == norm_at)
                def _():
                    norm_unit()

                @pl.when((unit >= head_at) & (unit < end_at))
                def _():
                    head_unit(unit - head_at)

                @pl.when(unit == end_at)
                def _():
                    end_unit()

            @pl.when(s == 0)
            def _():
                for k in range(ring - 1):
                    load_tile(jnp.int32(k))

            @pl.when(valid(s))
            def _():
                @pl.when(s == per_pair - 1)
                def _():
                    take_left(1, 1, None)

                @pl.when(s == x_flip)
                def _():
                    take_left(2, 0, None)

                @pl.when(s == ga_flip)
                def _():
                    take_left(3, 1, 1)

                at = lax.rem(s, ring)
                arrived(tile.at[at], tile_sem.at[at])
                give_at = lax.rem(s, gives)

                @pl.when(s >= gives)
                def _():
                    arrived(give.at[give_at], give_send.at[give_at])

                ffn_flip = jnp.where(lax.rem(s, 3 * per_pair) // per_pair == 0, 0, 1)
                which = jnp.where(s < ffn_blocks, ffn_flip, jnp.where(s < ffn_blocks + 3 * head_blocks, 0, 1))
                for place, store, spot in ((1 - c, give, give_at), (c, mine, lax.rem(s, mines))):
                    here = block(place, half)
                    product = dot(flip[which, here, :rows], tile[at, 0])
                    for m in range(1, seqs):
                        product += dot(flip[which, here, m * rows : (m + 1) * rows], tile[at, m])
                    store[spot, 1] = product[:, :bt].astype(BF)
                    store[spot, 0] = product[:, bt:].astype(BF)

            @pl.when((s >= 0) & (s + ring - 1 < total))
            def _():
                load_tile(s + ring - 1)

            k1 = s - CORE_LAG

            @pl.when(valid(k1))
            def _():
                arrived(acc.at[k1], core_recv.at[k1])
                at = lax.rem(k1, mines)
                for side in range(2):
                    acc[k1, side] = acc[k1, side] + mine[at, side]

            k2 = k1 - CROSS_LAG

            @pl.when(valid(k2))
            def _():
                arrived(from_x.at[k2], x_recv.at[k2])
                acc[k2, 1] = acc[k2, 1] + from_x[k2]

            for rows_, way, place, ahead, behind in sides:
                k3 = k2 - CHAIN_LAG * place

                @pl.when(valid(k3) & (place > 0))
                def _(rows_=rows_, way=way, k3=k3):
                    arrived(from_z.at[k3, rows_], z_recv.at[way, k3])
                    acc[k3, 1, rows_] = acc[k3, 1, rows_] + from_z[k3, rows_]

                k4 = k2 - CHAIN_LAG * (2 * last - place)

                @pl.when(valid(k4) & (place == last))
                def _(rows_=rows_, k4=k4):
                    final[k4, rows_] = acc[k4, 1, rows_]

                @pl.when(valid(k4) & (place < last))
                def _(rows_=rows_, way=way, k4=k4):
                    arrived(final.at[k4, rows_], f_recv.at[way, k4])

            @pl.when(valid(s))
            def _():
                at = lax.rem(s, gives)
                remote(give.at[at], acc.at[s], give_send.at[at], core_recv.at[s], core).start()

            @pl.when(valid(k1))
            def _():
                remote(acc.at[k1, 0], from_x.at[k1], x_send, x_recv.at[k1], cross).start()

            for number, m, source, early in row_plan:
                if not early:
                    @pl.when((k1 == total - 1) & (section == number))
                    def _(m=m, source=source):
                        row_copy(m, source).start()

            for rows_, way, place, ahead, behind in sides:
                k3 = k2 - CHAIN_LAG * place

                @pl.when(valid(k3) & (place < last))
                def _(rows_=rows_, way=way, k3=k3, ahead=ahead):
                    remote(acc.at[k3, 1, rows_], from_z.at[k3, rows_], z_send.at[way], z_recv.at[way, k3], ahead).start()

                k4 = k2 - CHAIN_LAG * (2 * last - place)

                @pl.when(valid(k4) & (place > 0))
                def _(rows_=rows_, way=way, k4=k4, behind=behind):
                    remote(final.at[k4, rows_], final.at[k4, rows_], f_send.at[way], f_recv.at[way, k4], behind).start()

            k5 = k2 - CHAIN_LAG * 2 * last

            @pl.when(valid(k5))
            def _():
                def visit(m, j):
                    dst = outs[group_of[m]].at[member_of[m], block(c, half), block(j, bt)]
                    copy(final.at[k5], dst, store_sem).start()
                    remote(final.at[k5], dst, out_send, out_recv, core).start()

                member(k5, visit)

            @pl.when(turn == last_turn + 1)
            def _():
                vec_core.start()

            @pl.when(turn == last_turn + 6)
            def _():
                vec_core.wait_recv()
                vec[1] = vec[0] + vec_in[0]

            @pl.when(turn == last_turn + 7)
            def _():
                vec_cross.start()

            @pl.when(turn == last_turn + 13)
            def _():
                vec_cross.wait_recv()
                vec_all[z] = vec[1] + vec_in[1]

            @pl.when(turn == last_turn + 14)
            def _():
                for shift in range(1, chips):
                    to = lax.rem(z + shift, chips)
                    remote(
                        vec_all.at[z], vec_all.at[z], v_send.at[1 + shift], v_recv.at[1 + shift], {"dp": to * 2 + c}
                    ).start()

        for number, m, source, early in row_plan:
            @pl.when(section == number)
            def _(m=m, source=source):
                row_copy(m, source).wait()

        vec_core.wait_send()
        vec_cross.wait_send()
        for shift in range(1, chips):
            origin = lax.rem(z + chips - shift, chips)
            arrived(vec_all.at[origin], v_recv.at[1 + shift])
            arrived(vec_all.at[z], v_send.at[1 + shift])
        whole = vec_all[0]
        for chip in range(1, chips):
            whole += vec_all[chip]
        sums_out[...] = whole
        for at in range(gives):
            arrived(give.at[at], give_send.at[at])
        arrived(acc.at[:, 0], x_send)
        for rows_, way, place, ahead, behind in sides:
            @pl.when(place < last)
            def _(rows_=rows_, way=way):
                arrived(from_z.at[:, rows_], z_send.at[way])

            @pl.when(place > 0)
            def _(rows_=rows_, way=way):
                arrived(final.at[:, rows_], f_send.at[way])

        arrived(final, out_send)
        arrived(final, store_sem)
        arrived(final, out_recv)

    sem = pltpu.SemaphoreType.DMA
    flops = 2 * seqs * rows * width * 2 * bt * total
    members = [member_of[index] for index in range(7)]
    shapes = [(sum(g == index for g in group_of), width, rights[group_of.index(index)].shape[2] // 2) for index in range(4)]
    return pl.pallas_call(
        kernel,
        in_specs=[SMEM, SMEM] + NORM_SPECS + [WHOLE] * 9 + [ANY] * 32,
        out_specs=[ANY] * 4 + [WHOLE] + [ANY] * 8,
        out_shape=[jax.ShapeDtypeStruct(s, BF) for s in shapes]
        + [jax.ShapeDtypeStruct(vec_shape, F32), jax.ShapeDtypeStruct((seqs, shard_rows, width), BF)]
        + [jax.ShapeDtypeStruct(act.shape, BF)] * 2
        + [jax.ShapeDtypeStruct((rows, 2 * local), BF)] * 3
        + [jax.ShapeDtypeStruct((rows, width), F32), jax.ShapeDtypeStruct((rows, width), BF)],
        scratch_shapes=[
            pltpu.VMEM((total, 2, half, bt), BF),
            pltpu.VMEM((total, half, bt), BF),
            pltpu.VMEM((total, half, bt), BF),
            pltpu.VMEM((2, width, seqs * rows), BF),
            pltpu.VMEM((seqs, rows, width), BF),
            pltpu.VMEM((ring, seqs, rows, 2 * bt), BF),
            pltpu.VMEM((mines, 2, half, bt), BF),
            pltpu.VMEM((gives, 2, half, bt), BF),
            pltpu.VMEM((2,) + vec_shape, F32),
            pltpu.VMEM((2,) + vec_shape, F32),
            pltpu.VMEM((chips,) + vec_shape, F32),
            pltpu.VMEM((rows, width), BF),
            pltpu.VMEM((rows, width), BF),
            pltpu.VMEM((rows, 128), F32),
            pltpu.VMEM((2, rows, width), BF),
            pltpu.VMEM((rows, width), F32),
            pltpu.VMEM((2, 3, width, CW), BF),
            pltpu.VMEM((2, CW, width), BF),
            pltpu.VMEM((2, 3, rows, CW), BF),
            pltpu.VMEM((2, 3, rows, CW), BF),
            pltpu.VMEM((2, 8, rows), F32),
            pltpu.VMEM((rows, CW), BF),
            pltpu.VMEM((2, rows, rows), BF),
            pltpu.VMEM((rows, rows), F32),
            pltpu.VMEM((8, width), F32),
            pltpu.VMEM((2, 2 * units), F32),
            pltpu.VMEM((2, 2 * local), F32),
            sem((ring,)), sem((2,)), sem((gives,)), sem((total,)), sem, sem((total,)),
            sem((2,)), sem((2, total)), sem((2,)), sem((2, total)),
            sem, sem, sem, sem((chips + 1,)), sem((chips + 1,)), sem((seqs,)), sem((seqs,)),
            sem((3,)), sem((2, 6)), sem((2, 3)), sem((2,)),
        ],
        input_output_aliases={20: 6, 21: 7},
        compiler_params=pltpu.CompilerParams(
            collective_id=0, has_side_effects=True, vmem_limit_bytes=67_000_000
        ),
        cost_estimate=pl.CostEstimate(flops=flops, bytes_accessed=100 << 20, transcendentals=0),
        name="backward_and_reduce",
    )(
        lengths, slopes, *norms, *sums, grad, q, k_, v, lse, act, slope, u1, u2, r1, r2, *weights, *lefts, *rights,
        low_grad, second
    )


def exchange_rows(outputs, deps):
    seqs = len(outputs)
    rows, width = outputs[0].shape
    shard_rows = rows // 2
    n_in = seqs + len(deps)

    def kernel(*refs):
        y_refs, out_ref = refs[:seqs], refs[n_in]
        stage, send, recv, l_sem = refs[n_in + 1 :]
        t = lax.axis_index("tensor")
        cross = {"tensor": 1 - t}
        barrier = pltpu.get_barrier_semaphore()
        pl.semaphore_signal(barrier, inc=1, device_id=cross, device_id_type=MESH)
        pl.semaphore_wait(barrier, 1)

        @pl.when(lax.axis_index("section") == 0)
        def _():
            for m in range(seqs):
                pltpu.make_async_remote_copy(
                    src_ref=y_refs[m].at[block(1 - t, shard_rows)], dst_ref=out_ref.at[t * seqs + m],
                    send_sem=send.at[m], recv_sem=recv.at[m], device_id=cross, device_id_type=MESH,
                ).start()
            for m in range(seqs):
                copy(y_refs[m].at[block(t, shard_rows)], stage.at[m], l_sem.at[m]).start()
            for m in range(seqs):
                arrived(stage.at[m], l_sem.at[m])
                copy(stage.at[m], out_ref.at[t * seqs + m], l_sem.at[m]).start()
            for m in range(seqs):
                arrived(stage.at[m], l_sem.at[m])
            for m in range(seqs):
                arrived(out_ref.at[(1 - t) * seqs + m], recv.at[m])
                arrived(stage.at[m], send.at[m])

    sem = pltpu.SemaphoreType.DMA
    return pl.pallas_call(
        kernel,
        in_specs=[ANY] * n_in,
        out_specs=ANY,
        out_shape=jax.ShapeDtypeStruct((2 * seqs, shard_rows, width), BF),
        scratch_shapes=[pltpu.VMEM((seqs, shard_rows, width), BF), sem((seqs,)), sem((seqs,)), sem((seqs,))],
        compiler_params=pltpu.CompilerParams(collective_id=2, has_side_effects=True),
        cost_estimate=pl.CostEstimate(flops=0, bytes_accessed=0, transcendentals=0),
        name="exchange_rows",
    )(*outputs, *deps)


def widen(reduced, row_grads, got, got_second, produced, outputs, sums, units, local):
    shard_rows, width = got.shape[1:]
    seqs = got.shape[0]
    n = len(reduced)
    jobs = []
    for index, array in enumerate(reduced):
        lead, depth, columns = array.shape
        step = 512 * 1024 // columns
        if index == n - 1:
            jobs += [(index, 0, at, depth // 2, columns) for at in range(0, depth, depth // 2)]
        else:
            jobs += [(index, part, at, step, columns) for part in range(lead) for at in range(0, depth, step)]
    jobs += [(n, m, 0, shard_rows, width) for m in range(seqs)] + [(n + 1, m, 0, shard_rows, width) for m in range(seqs)]
    jobs += [(n + 2, m, 0, shard_rows, width) for m in range(2 * seqs)]
    ring = 6
    n_in = n + 3 * seqs + 4
    parts = units // width

    def kernel(*refs):
        ins = refs[:n]
        grad_refs = refs[n : n + 2 * seqs]
        got_ref, got_second_ref, produced_ref = refs[n + 2 * seqs : n + 2 * seqs + 3]
        y_refs, sums_ref = refs[n + 2 * seqs + 3 : n_in - 1], refs[n_in - 1]
        outs = refs[n_in : n_in + n + 2]
        qv_ref, out_bias_ref, gain_ref, shift_ref, ub_ref, down_bias_ref = refs[n_in + n + 2 : n_in + n + 8]
        shapes = sorted({(j[3], j[4]) for j in jobs if j[0] != n})
        buffers = refs[n_in + n + 8 :]
        wide_rows, in_sem, out_sem = buffers[0], buffers[1], buffers[2]
        low = {s: buffers[3 + 2 * i] for i, s in enumerate(shapes)}
        wide = {s: buffers[4 + 2 * i] for i, s in enumerate(shapes)}
        t = lax.axis_index("tensor")
        section = lax.axis_index("section")

        def load(number):
            index, part, at, rows, columns = jobs[number]
            s = number % ring
            if index < n:
                copy(ins[index].at[part, pl.ds(at, rows)], low[rows, columns].at[s], in_sem.at[s]).start()
            elif index == n:
                for turn in range(2):
                    @pl.when(section == turn)
                    def _(turn=turn):
                        source = grad_refs[turn * seqs + part].at[block(t, shard_rows)]
                        copy(source, wide_rows.at[part], in_sem.at[s]).start()
            elif index == n + 1:
                for number_ in range(2):
                    @pl.when(section == number_)
                    def _(number_=number_):
                        source = got_second_ref.at[seqs] if number_ == 1 and part == 0 else got_ref.at[part]
                        copy(source, low[rows, columns].at[s], in_sem.at[s]).start()
            else:
                @pl.when(section == 0)
                def _():
                    copy(produced_ref.at[part], low[rows, columns].at[s], in_sem.at[s]).start()

                @pl.when(section == 1)
                def _():
                    source = y_refs[part].at[block(t, shard_rows)] if part < seqs else got_second_ref.at[part - seqs]
                    copy(source, low[rows, columns].at[s], in_sem.at[s]).start()

        def store(number):
            index, part, at, rows, columns = jobs[number]
            s = number % ring
            if index < n - 1:
                return copy(wide[rows, columns].at[s], outs[index].at[part, pl.ds(at, rows)], out_sem.at[s])
            if index == n - 1:
                return copy(wide[rows, columns].at[s], outs[index].at[:, pl.ds(at, rows)], out_sem.at[s])
            if index == n:
                return copy(wide_rows.at[part], outs[n].at[t * seqs + part], out_sem.at[s])
            if index == n + 1:
                return copy(wide[rows, columns].at[s], outs[n].at[(1 - t) * seqs + part], out_sem.at[s])
            side, m = divmod(part, seqs)
            spread = (t + side - 2 * t * side) * seqs + m
            return copy(low[rows, columns].at[s], outs[n + 1].at[jnp.where(section == 0, part, spread)], out_sem.at[s])

        for number in range(ring):
            load(number)
        gain_ref[0:1] = sums_ref[3:4]
        gain_ref[1:2] = sums_ref[0:1]
        shift_ref[0:1] = sums_ref[4:5]
        shift_ref[1:2] = sums_ref[1:2]
        out_bias_ref[...] = sums_ref[5:6]
        down_bias_ref[...] = sums_ref[2:3]
        for half in range(2):
            @pl.when(t == half)
            def _(half=half):
                for g in range(2):
                    for j in range(parts):
                        at = 6 + (2 * g + half) * parts + j
                        ub_ref[g : g + 1, j * width : (j + 1) * width] = sums_ref[at : at + 1]
                    at = 6 + 4 * parts + g
                    qv_ref[g : g + 1] = sums_ref[at : at + 1, half * local : (half + 1) * local]

        for number, (index, part, at, rows, columns) in enumerate(jobs):
            s = number % ring
            if index == n:
                arrived(wide_rows.at[part], in_sem.at[s])
            else:
                arrived(low[rows, columns].at[s], in_sem.at[s])
            if number >= ring:
                store(number - ring).wait()
            if index == n - 1:
                wide[rows, columns][s] = low[rows, columns][s].astype(F32).T
            elif index not in (n, n + 2):
                wide[rows, columns][s] = low[rows, columns][s].astype(F32)
            store(number).start()
            if number + ring < len(jobs):
                load(number + ring)
        for number in range(len(jobs) - ring, len(jobs)):
            store(number).wait()

    shapes = sorted({(j[3], j[4]) for j in jobs if j[0] != n})
    square = (reduced[-1].shape[1] // 2, reduced[-1].shape[2])
    last = reduced[-1].shape
    sem = pltpu.SemaphoreType.DMA
    buffers = []
    for s in shapes:
        buffers += [pltpu.VMEM((ring,) + s, BF), pltpu.VMEM((ring,) + ((s[1], s[0]) if s == square else s), F32)]
    return pl.pallas_call(
        kernel,
        in_specs=[ANY] * (n_in - 1) + [WHOLE],
        out_specs=[ANY] * (n + 2) + [WHOLE] * 6,
        out_shape=[jax.ShapeDtypeStruct(r.shape, F32) for r in reduced[:-1]]
        + [jax.ShapeDtypeStruct((last[2], last[1]), F32), jax.ShapeDtypeStruct((2 * seqs, shard_rows, width), F32)]
        + [jax.ShapeDtypeStruct((2 * seqs, shard_rows, width), BF)]
        + [
            jax.ShapeDtypeStruct(shape, F32)
            for shape in ((2, local), (1, width), (2, width), (2, width), (2, units), (1, width))
        ],
        scratch_shapes=[pltpu.VMEM((seqs, shard_rows, width), F32), sem((ring,)), sem((ring,))] + buffers,
        compiler_params=pltpu.CompilerParams(vmem_limit_bytes=VMEM_LIMIT),
        cost_estimate=pl.CostEstimate(flops=0, bytes_accessed=56 << 20, transcendentals=0),
        name="widen",
    )(*reduced, *row_grads, got, got_second, produced, *outputs, sums)


MASKED = -1000000000.0


def shifted(value, axis, steps):
    count = lax.axis_size(axis)
    first, last = (max(0, -steps), min(count, count - steps))
    return lax.ppermute(value, axis, [(source, source + steps) for source in range(first, last)])


def layer_norm(values, gain, shift):
    mean = jnp.mean(values, axis=-1, keepdims=True)
    centred = values - mean
    spread = jnp.mean(centred * centred, axis=-1, keepdims=True)
    return centred * lax.rsqrt(spread + EPS) * gain + shift


def alibi_slopes(first, count, heads):
    index = (first + jnp.arange(count)).astype(jnp.float32)
    return jnp.exp2(-8.0 * (index + 1.0) / heads)


def attention_core(projected, qv_bias, slopes, key_ok):
    rows = projected.shape[0]
    width = projected.shape[2]
    count = slopes.shape[0]
    size = width // count
    query = (projected[:, 0] + qv_bias[0]).astype(jnp.bfloat16).reshape(rows, count, size)
    key = projected[:, 1].astype(jnp.bfloat16).reshape(rows, count, size)
    value = (projected[:, 2] + qv_bias[1]).astype(jnp.bfloat16).reshape(rows, count, size)
    place = jnp.arange(rows).astype(jnp.float32)
    distance = jnp.abs(place[:, None] - place[None, :])
    scale = 1.0 / math.sqrt(size)
    scores = (
        jnp.einsum("qhd,khd->hqk", query, key, preferred_element_type=jnp.float32) * scale
        - slopes[:, None, None] * distance[None]
    )
    scores = jnp.where(key_ok[None, None, :], scores, MASKED)
    weights = jax.nn.softmax(scores, axis=-1)
    weights_low = weights.astype(jnp.bfloat16)
    mixed = jnp.einsum("hqk,khd->qhd", weights_low, value, preferred_element_type=jnp.float32)
    mixed = mixed.reshape(rows, width).astype(jnp.bfloat16)
    return (query, key, value, weights, weights_low, mixed)


def attention_back(parts, grad_mixed, key_ok):
    query, key, value, weights, weights_low, mixed = parts
    rows, count, size = query.shape
    scale = 1.0 / math.sqrt(size)
    grad_low = grad_mixed.astype(jnp.bfloat16).reshape(rows, count, size)
    grad_weights = jnp.einsum("qhd,khd->hqk", grad_low, value, preferred_element_type=jnp.float32)
    grad_value = jnp.einsum(
        "hqk,qhd->khd", weights_low, grad_low, preferred_element_type=jnp.float32
    )
    inner = jnp.sum(weights * grad_weights, axis=-1, keepdims=True)
    grad_scores = weights * (grad_weights - inner)
    grad_scores = jnp.where(key_ok[None, None, :], grad_scores, 0.0).astype(jnp.bfloat16)
    grad_query = (
        jnp.einsum("hqk,khd->qhd", grad_scores, key, preferred_element_type=jnp.float32) * scale
    ).astype(jnp.bfloat16)
    grad_key = (
        jnp.einsum("hqk,qhd->khd", grad_scores, query, preferred_element_type=jnp.float32) * scale
    ).astype(jnp.bfloat16)
    grad_value = grad_value.astype(jnp.bfloat16)
    width = count * size
    grad_query = grad_query.reshape(rows, width)
    grad_key = grad_key.reshape(rows, width)
    grad_value = grad_value.reshape(rows, width)
    grad_projected = jnp.stack([grad_query, grad_key, grad_value], axis=1).reshape(rows, 3 * width)
    qv_grad = jnp.stack(
        [
            jnp.sum(grad_query.astype(jnp.float32), axis=0),
            jnp.sum(grad_value.astype(jnp.float32), axis=0),
        ]
    )
    return (grad_projected, qv_grad)


def gelu_product(both):
    return jax.nn.gelu(both[:, 0], approximate=False) * both[:, 1]


def geglu(lifted, up_bias):
    return gelu_product(lifted + up_bias[None])


def ffn_grads(rows_low, grad_low, up_weight, up_bias, down_weight):
    lifted = jnp.einsum("sd,gdf->sgf", rows_low, up_weight, preferred_element_type=jnp.float32)
    hidden, geglu_back = jax.vjp(gelu_product, lifted + up_bias[None])
    grad_hidden = jnp.einsum("sd,df->sf", grad_low, down_weight, preferred_element_type=jnp.float32)
    (grad_both,) = geglu_back(grad_hidden)
    grad_lifted = grad_both.astype(jnp.bfloat16)
    grad_bias = jnp.sum(grad_lifted.astype(jnp.float32), axis=0)
    up_grad = jnp.einsum("sd,sgf->gdf", rows_low, grad_lifted, preferred_element_type=jnp.float32)
    down_grad = jnp.einsum(
        "sd,sf->df", grad_low, hidden.astype(jnp.bfloat16), preferred_element_type=jnp.float32
    )
    return (grad_lifted, grad_bias, up_grad, down_grad)


def on_device(
    inputs,
    cotangent,
    lengths,
    w_qkv,
    b_qv,
    w_out,
    b_out,
    ln_gain,
    ln_bias,
    w_up,
    b_up,
    w_down,
    b_down,
):
    batches, shard_rows, width = inputs.shape
    parts = lax.axis_size("tensor")
    place = lax.axis_index("tensor")
    section = lax.axis_index("section")
    last_section = lax.axis_size("section") - 1
    full_rows = shard_rows * parts
    local_width = w_qkv.shape[3]
    local_heads = local_width // HD
    qkv_flat = w_qkv[0].reshape(width, 3 * local_width)
    out_weight = w_out[0]
    qv_bias = b_qv[0].astype(jnp.float32)
    out_bias = b_out[0].astype(jnp.float32)
    gains = ln_gain[0].astype(jnp.float32)
    shifts = ln_bias[0].astype(jnp.float32)
    down_bias = b_down[0].astype(jnp.float32)
    slopes = alibi_slopes(place * local_heads, local_heads, H)
    row_place = place * shard_rows + jnp.arange(shard_rows)
    kept_rows = 0

    def key_mask(length):
        return jnp.arange(full_rows) < length

    def after_attention(values, attended, bias, gain_rows, shift_rows):
        return layer_norm(values + attended + bias, gain_rows[0], shift_rows[0])

    def after_ffn(normed, lowered, bias, gain_rows, shift_rows):
        return layer_norm(normed + lowered + bias, gain_rows[1], shift_rows[1])

    def gather_inputs(values):
        return lax.all_gather(values.astype(jnp.bfloat16), "tensor", axis=0, tiled=True)

    def project(gathered):
        return jnp.dot(gathered, qkv_flat, preferred_element_type=jnp.float32).reshape(
            full_rows, 3, local_width
        )

    def attention_forward(values, length):
        gathered = gather_inputs(values)
        projected = project(gathered)
        mixed = attention_core(projected, qv_bias, slopes, key_mask(length))[5]

        def term(start, count):
            return jnp.dot(mixed, out_weight, preferred_element_type=jnp.float32)

        return (
            lax.psum_scatter(
                term(jnp.int32(0), shard_rows * lax.axis_size("tensor")).astype(jnp.bfloat16),
                "tensor",
                scatter_dimension=0,
                tiled=True,
            ).astype(jnp.float32),
            gathered,
            projected,
        )

    up_local = w_up[0]
    up_bias_local = b_up[0].astype(jnp.float32)
    down_local = w_down[0]

    def gather_normed(normed):
        return lax.all_gather(normed.astype(jnp.bfloat16), "tensor", axis=0, tiled=True)

    def ffn_forward(normed):
        lifted = jnp.einsum(
            "sd,gdf->sgf", gather_normed(normed), up_local, preferred_element_type=jnp.float32
        )
        hidden = geglu(lifted, up_bias_local).astype(jnp.bfloat16)

        def term(start, count):
            return jnp.einsum("sf,df->sd", hidden, down_local, preferred_element_type=jnp.float32)

        return lax.psum_scatter(
            term(jnp.int32(0), shard_rows * lax.axis_size("tensor")).astype(jnp.bfloat16),
            "tensor",
            scatter_dimension=0,
            tiled=True,
        ).astype(jnp.float32)

    def ffn_backward(normed, grad_lowered):
        gathered = gather_normed(normed)
        grad_whole = lax.all_gather(grad_lowered.astype(jnp.bfloat16), "tensor", axis=0, tiled=True)
        grad_lifted, grad_bias, up_grad, down_grad = ffn_grads(
            gathered, grad_whole, up_local, up_bias_local, down_local
        )

        def term(start, count):
            return jnp.einsum(
                "sgf,gdf->sd", grad_lifted, up_local, preferred_element_type=jnp.float32
            )

        grad_normed = lax.psum_scatter(
            term(jnp.int32(0), shard_rows * lax.axis_size("tensor")).astype(jnp.bfloat16),
            "tensor",
            scatter_dimension=0,
            tiled=True,
        ).astype(jnp.float32)
        return (grad_normed, (up_grad, grad_bias, down_grad))

    ffn_shapes = (up_local.shape, up_bias_local.shape, down_local.shape)

    def layer_forward(values, length):
        attended, gathered, projected = attention_forward(values, length)
        normed = after_attention(values, attended, out_bias, gains, shifts)
        lowered = ffn_forward(normed)
        return (
            after_ffn(normed, lowered, down_bias, gains, shifts),
            attended,
            lowered,
            gathered,
            projected,
        )

    def layer_backward(values, attended, lowered, length, grad_output):
        normed, attention_norm_back = jax.vjp(
            after_attention, values, attended, out_bias, gains, shifts
        )
        outcome, ffn_norm_back = jax.vjp(after_ffn, normed, lowered, down_bias, gains, shifts)
        grad_normed, grad_lowered, grad_down_bias, gain_late, shift_late = ffn_norm_back(
            grad_output
        )
        grad_from_ffn, ffn_terms = ffn_backward(normed, grad_lowered)
        grad_values, grad_attended, grad_out_bias, gain_early, shift_early = attention_norm_back(
            grad_normed + grad_from_ffn
        )
        gathered = gather_inputs(values)
        projected = project(gathered)
        grad_whole = lax.all_gather(
            grad_attended.astype(jnp.bfloat16), "tensor", axis=0, tiled=True
        )
        mask = key_mask(length)
        pieces = attention_core(projected, qv_bias, slopes, mask)
        mixed_low = pieces[5]
        out_grad = jnp.einsum(
            "se,sd->ed", mixed_low, grad_whole, preferred_element_type=jnp.float32
        )
        grad_mixed = jnp.einsum(
            "sd,ed->se", grad_whole, out_weight, preferred_element_type=jnp.float32
        )
        grad_projected, qv_grad = attention_back(pieces, grad_mixed, mask)
        qkv_grad = jnp.einsum(
            "sd,sx->dx", gathered, grad_projected, preferred_element_type=jnp.float32
        )

        def term(start, count):
            return jnp.einsum(
                "sx,dx->sd", grad_projected, qkv_flat, preferred_element_type=jnp.float32
            )

        grad_inputs = grad_values + lax.psum_scatter(
            term(jnp.int32(0), shard_rows * lax.axis_size("tensor")).astype(jnp.bfloat16),
            "tensor",
            scatter_dimension=0,
            tiled=True,
        ).astype(jnp.float32)
        terms = (
            qkv_grad,
            qv_grad,
            out_grad,
            grad_out_bias,
            gain_early + gain_late,
            shift_early + shift_late,
            ffn_terms[0],
            ffn_terms[1],
            ffn_terms[2],
            grad_down_bias,
        )
        return (grad_inputs, terms)

    def keep(store, item, batch, valid):
        old = lax.dynamic_index_in_dim(store, batch, 0, keepdims=False)
        return lax.dynamic_update_index_in_dim(store, jnp.where(valid, item, old), batch, 0)

    def forward_step(step, carry):
        (
            received,
            kept_values,
            kept_attended,
            kept_lowered,
            produced,
            kept_gathered,
            kept_projected,
        ) = carry
        index = step - section
        valid = (index >= 0) & (index < batches)
        batch = jnp.clip(index, 0, batches - 1)
        fresh = lax.dynamic_index_in_dim(
            inputs, jnp.minimum(step, batches - 1), 0, keepdims=False
        ).astype(jnp.float32)
        values = jnp.where(section == 0, fresh, received.astype(jnp.float32))
        output, attended, lowered, gathered, projected = layer_forward(values, lengths[batch])
        sent = output.astype(jnp.bfloat16)
        kept_values = keep(kept_values, values, batch, valid)
        kept_attended = keep(kept_attended, attended, batch, valid)
        kept_lowered = keep(kept_lowered, lowered, batch, valid)
        produced = keep(produced, sent, batch, valid)
        kept_gathered = keep(kept_gathered, gathered[:kept_rows], batch, valid)
        kept_projected = keep(kept_projected, projected[:kept_rows], batch, valid)
        received = shifted(sent, "section", 1)
        return (
            received,
            kept_values,
            kept_attended,
            kept_lowered,
            produced,
            kept_gathered,
            kept_projected,
        )

    store_zeros = jnp.zeros((batches, shard_rows, width), jnp.float32)
    gathered_zeros = jnp.zeros((batches, kept_rows, width), jnp.bfloat16)
    projected_zeros = jnp.zeros((batches, kept_rows, 3, local_width), jnp.float32)
    start_forward = (
        jnp.zeros((shard_rows, width), jnp.bfloat16),
        store_zeros,
        store_zeros,
        store_zeros,
        jnp.zeros((batches, shard_rows, width), jnp.bfloat16),
        gathered_zeros,
        projected_zeros,
    )
    received, kept_values, kept_attended, kept_lowered, produced, kept_gathered, kept_projected = (
        lax.fori_loop(0, batches + last_section, forward_step, start_forward)
    )

    def backward_step(step, carry):
        received, totals, grads_in = carry
        index = step - (last_section - section)
        valid = (index >= 0) & (index < batches)
        batch = jnp.clip(index, 0, batches - 1)
        length = lengths[batch]
        outer = lax.dynamic_index_in_dim(cotangent, batch, 0, keepdims=False).astype(jnp.float32)
        outer = outer * (row_place < length).astype(jnp.float32)[:, None]
        grad_output = jnp.where(section == last_section, outer, received.astype(jnp.float32))
        grad_output = jnp.where(valid, grad_output, 0.0)
        values = lax.dynamic_index_in_dim(kept_values, batch, 0, keepdims=False)
        attended = lax.dynamic_index_in_dim(kept_attended, batch, 0, keepdims=False)
        lowered = lax.dynamic_index_in_dim(kept_lowered, batch, 0, keepdims=False)
        grad_inputs, terms = layer_backward(values, attended, lowered, length, grad_output)
        totals = jax.tree.map(jnp.add, totals, terms)
        grads_in = keep(grads_in, grad_inputs, batch, valid)
        received = shifted(grad_inputs.astype(jnp.bfloat16), "section", -1)
        return (received, totals, grads_in)

    start_totals = (
        jnp.zeros((width, 3 * local_width), jnp.float32),
        jnp.zeros((2, local_width), jnp.float32),
        jnp.zeros((local_width, width), jnp.float32),
        jnp.zeros((width,), jnp.float32),
        jnp.zeros((2, width), jnp.float32),
        jnp.zeros((2, width), jnp.float32),
        jnp.zeros(ffn_shapes[0], jnp.float32),
        jnp.zeros(ffn_shapes[1], jnp.float32),
        jnp.zeros(ffn_shapes[2], jnp.float32),
        jnp.zeros((width,), jnp.float32),
    )
    start_backward = (jnp.zeros((shard_rows, width), jnp.bfloat16), start_totals, store_zeros)
    received, totals, grads_in = lax.fori_loop(
        0, batches + last_section, backward_step, start_backward
    )
    (
        qkv_total,
        qv_total,
        out_total,
        out_bias_total,
        gain_total,
        shift_total,
        up_total,
        up_bias_total,
        down_total,
        down_bias_total,
    ) = totals
    qkv_sum, qv_sum, out_sum, up_sum, up_bias_sum, down_sum = (
        lax.psum(qkv_total.astype(jnp.bfloat16), "dp").astype(jnp.float32),
        lax.psum(qv_total.astype(jnp.bfloat16), "dp").astype(jnp.float32),
        lax.psum(out_total.astype(jnp.bfloat16), "dp").astype(jnp.float32),
        lax.psum(up_total.astype(jnp.bfloat16), "dp").astype(jnp.float32),
        lax.psum(up_bias_total.astype(jnp.bfloat16), "dp").astype(jnp.float32),
        lax.psum(down_total.astype(jnp.bfloat16), "dp").astype(jnp.float32),
    )
    out_bias_sum, gain_sum, shift_sum, down_bias_sum = lax.psum(
        (out_bias_total, gain_total, shift_total, down_bias_total), ("tensor", "dp")
    )
    return (
        produced[None],
        grads_in[None],
        qkv_sum.reshape(1, width, 3, local_width),
        qv_sum[None],
        out_sum[None],
        out_bias_sum[None],
        gain_sum[None],
        shift_sum[None],
        up_sum[None],
        up_bias_sum[None],
        down_sum[None],
        down_bias_sum[None],
    )


def by_sequence(
    inputs,
    cotangent,
    lengths,
    w_qkv,
    b_qv,
    w_out,
    b_out,
    ln_gain,
    ln_bias,
    w_up,
    b_up,
    w_down,
    b_down,
):
    batches, shard_rows, width = inputs.shape
    place = lax.axis_index("tensor")
    section = lax.axis_index("section")
    groups = lax.axis_size("dp")
    rows = 2 * shard_rows
    seqs = batches // 2
    local = w_qkv.shape[3]
    units = w_up.shape[3]
    heads = local // HD
    chips = groups // 2

    qkv_own = jnp.transpose(w_qkv[0], (1, 0, 2))
    out_own = w_out[0]
    up_own = w_up[0]
    down_own = w_down[0]
    first = section == 0
    norms = (b_out, ln_gain[0], ln_bias[0], b_down)
    table = np.exp2(-8.0 * (np.arange(2 * heads, dtype=np.float32) + 1.0) / H).astype(np.float32)
    slopes = jnp.asarray(np.concatenate([table, np.roll(table, heads)]))

    qkv_oth, out_oth, up_oth, down_oth, *rest = fetch_and_forward(
        (qkv_own, out_own, up_own, down_own),
        (b_qv[0], b_up[0]),
        inputs,
        cotangent,
        slopes,
        norms,
        lengths,
        chips,
        seqs,
    )
    weights = (qkv_own, qkv_oth, out_own, out_oth, up_own, up_oth, down_own, down_oth)
    biases, rest = rest[:2], rest[2:]
    x_first = outer = rest[:seqs]
    *kept, y = rest[seqs:]
    deps = [y]

    def forward(x, m, turn):
        nonlocal kept, deps
        *kept, y = layer_forward(x, weights, biases, slopes, norms, lengths, m, turn, kept, deps, seqs)
        deps = [y]
        return y

    y_first = [y] + [forward(x_first[m], m, 0) for m in range(1, seqs)]
    x_second = [lax.ppermute(y, "section", [(0, 1)]) for y in y_first]
    y_second = [forward(x_second[0], 0, 1)]
    produced = exchange_rows(y_first, deps)
    deps = [produced]
    y_second += [forward(x_second[m], m, 1) for m in range(1, seqs)]

    back = None
    sums = [[None] * seqs, [None] * seqs]

    got_second = None

    def backward(grad, m, turn, *extra):
        nonlocal back, deps, got_second
        results = layer_backward(grad, kept, weights, slopes, norms, lengths, m, turn, back, deps, seqs, *extra)
        back, (gx, gx_low, norm_sums, up_sums, qv_sums) = results[:7], results[7:12]
        if extra:
            got_second = results[12]
        deps = [norm_sums]
        sums[turn][m] = (norm_sums, up_sums, qv_sums)
        return gx, gx_low

    gx_second = [backward(outer[0], 0, 1)]
    gx_second.append(backward(outer[1], 1, 1, [*y_second, gx_second[0][1]]))
    grad_middle = [lax.ppermute(gx_second[m][1], "section", [(1, 0)]) for m in range(seqs)]
    x_all = jnp.stack([jnp.where(first, x_first[m], x_second[m]) for m in range(seqs)])
    deps = deps + [x_all]
    gx_first = [backward(grad_middle[0], 0, 0)]

    *reduced, packed, got, _, _, _, _, _, gx, _ = backward_and_reduce(
        grad_middle[1], kept, back, x_all, weights, slopes, norms, lengths, [*sums[0][0], *sums[1][0], *sums[1][1]], gx_first[0][1],
        gx_second[1][1], chips,
    )
    gx_all = [gx_first[0][0], gx] + [g[0] for g in gx_second]
    (
        down_sum, up_sum, qkv_sum, out_sum, grads_in, produced,
        qv_sum, out_bias_sum, gain_sum, shift_sum, up_bias_sum, down_bias_sum,
    ) = widen(reduced, gx_all, got, got_second, produced, y_second, packed, units, local)
    return (
        produced[None],
        grads_in[None],
        jnp.transpose(qkv_sum, (1, 0, 2))[None],
        qv_sum[None],
        out_sum[None],
        out_bias_sum,
        gain_sum[None],
        shift_sum[None],
        up_sum[None],
        up_bias_sum[None],
        down_sum,
        down_bias_sum,
    )


def solution(mesh):
    sections, parts, groups = (mesh.shape[name] for name in ("section", "tensor", "dp"))

    def run(*args):
        paired = sections == 2 and parts == 2 and groups % 2 == 0 and args[0].shape[0] == 4
        return (by_sequence if paired else on_device)(*args)

    return jax.shard_map(
        run,
        mesh=mesh,
        in_specs=(
            P("dp", "tensor", None),
            P("dp", "tensor", None),
            P("dp"),
            P("section", None, None, "tensor"),
            P("section", None, "tensor"),
            P("section", "tensor", None),
            P("section", None),
            P("section", None, None),
            P("section", None, None),
            P("section", None, None, "tensor"),
            P("section", None, "tensor"),
            P("section", None, "tensor"),
            P("section", None),
        ),
        out_specs=(
            P("section", "dp", "tensor", None),
            P("section", "dp", "tensor", None),
            P("section", None, None, "tensor"),
            P("section", None, "tensor"),
            P("section", "tensor", None),
            P("section", None),
            P("section", None, None),
            P("section", None, None),
            P("section", None, None, "tensor"),
            P("section", None, "tensor"),
            P("section", None, "tensor"),
            P("section", None),
        ),
        check_vma=False,
    )
```

```python
import math

import jax
import jax.numpy as jnp
import numpy as np
from jax import lax
from jax.experimental import pallas as pl
from jax.experimental.pallas import tpu as pltpu
from jax.sharding import PartitionSpec as P

H = 16
HD = 64
EPS = 1e-05
BF = jnp.bfloat16
F32 = jnp.float32
VMEM_LIMIT = 62 * 1024 * 1024
ANY = pl.BlockSpec(memory_space=pl.ANY)
SMEM = pl.BlockSpec(memory_space=pltpu.SMEM)
WHOLE = pl.BlockSpec(memory_space=pltpu.VMEM)
NN = (((1,), (0,)), ((), ()))
NT = (((1,), (1,)), ((), ()))
TN = (((0,), (0,)), ((), ()))
CW = 256
PER = CW // HD


def dot(a, b, dims=NN):
    return lax.dot_general(a, b, dims, preferred_element_type=F32)


def arrived(ref, sem):
    pltpu.make_async_copy(ref, ref, sem).wait()


def call(kernel, inputs, outputs, scratch, chain, deps, name, flops, nbytes, turn, remote=False):
    pairs = [item if isinstance(item, tuple) else (item, ANY) for item in inputs]
    args = [p[0] for p in pairs]
    specs = [p[1] for p in pairs]
    n_in = len(args)
    aliases = {}
    if chain is not None:
        for buffer, index in zip(chain, [index for index, item in enumerate(outputs) if item[2]]):
            aliases[len(args)] = index
            args.append(buffer)
            specs.append(ANY)
    args += deps
    specs += [ANY] * len(deps)
    n_args, n_out = len(args), len(outputs)
    params = {"collective_id": 3, "has_side_effects": True} if remote else {}

    def body(*refs):
        @pl.when(lax.axis_index("section") == turn)
        def _():
            kernel(refs[:n_in], refs[n_args : n_args + n_out], refs[n_args + n_out :])

    return pl.pallas_call(
        body,
        in_specs=specs,
        out_specs=[ANY] * n_out,
        out_shape=[jax.ShapeDtypeStruct(o[0], o[1]) for o in outputs],
        scratch_shapes=scratch,
        input_output_aliases=aliases,
        compiler_params=pltpu.CompilerParams(vmem_limit_bytes=VMEM_LIMIT, **params),
        cost_estimate=pl.CostEstimate(flops=flops, bytes_accessed=nbytes, transcendentals=0),
        name=name,
    )(*args)


NORM_SPECS = [WHOLE] * 4


def norm_rows(refs):
    out_bias, gain, shift, down_bias = refs
    rows = [out_bias[...], gain[0:1], shift[0:1], down_bias[...], gain[1:2], shift[1:2]]
    return [row.astype(F32) for row in rows]


def slope_of(table_ref, head):
    return table_ref[lax.axis_index("tensor") * (table_ref.shape[0] // 2) + head]


def pick(k, count, own, oth, make):
    @pl.when(k < count)
    def _():
        for src, dst, sem in make(own, k):
            pltpu.make_async_copy(src, dst, sem).start()

    @pl.when(k >= count)
    def _():
        for src, dst, sem in make(oth, k - count):
            pltpu.make_async_copy(src, dst, sem).start()


def block(index, size):
    return pl.ds(pl.multiple_of(index * size, size), size)


def copy(src, dst, sem):
    return pltpu.make_async_copy(src, dst, sem)


def fill_distance(dist_ref, length):
    rows = dist_ref.shape[0]
    keys = lax.broadcasted_iota(jnp.int32, (rows, rows), 0)
    places = lax.broadcasted_iota(jnp.int32, (rows, rows), 1)
    distance = jnp.abs(keys - places).astype(F32)
    dist_ref[...] = jnp.where(keys < length, distance, 1e12)


def normalize(v):
    mean = jnp.mean(v, axis=1, keepdims=True)
    centred = v - mean
    rstd = lax.rsqrt(jnp.mean(centred * centred, axis=1, keepdims=True) + EPS)
    return centred * rstd, rstd


def halves(rows):
    return [slice(0, rows // 2), slice(rows // 2, rows)]


class Forward:
    def __init__(self, rows, width, local, units):
        self.rows, self.width, self.local, self.units = rows, width, local, units
        self.ft = min(512, units)
        self.tiles = units // self.ft
        self.heads_steps = local // CW
        self.total = 2 * local

    def kept(self, slots):
        rows, width = self.rows, self.width
        shapes = [((slots, rows, self.total), BF)] * 4
        shapes += [((slots, 2 * self.heads_steps, 8, rows), F32)]
        shapes += [((slots, rows, 2 * self.units), BF)] * 3
        return shapes + [((slots, rows, width), BF)] * 3 + [((slots, rows, 128), F32)] * 2

    def scratch(self):
        rows, width, ft, total = self.rows, self.width, self.ft, self.total
        sem = pltpu.SemaphoreType.DMA
        return [
            pltpu.VMEM((rows, width), BF),
            pltpu.VMEM((2, 3, width, CW), BF),
            pltpu.VMEM((total, width), BF),
            pltpu.VMEM((2, 2, width, ft), BF),
            pltpu.VMEM((2, width, ft), BF),
            pltpu.VMEM((2, 3, rows, CW), BF),
            pltpu.VMEM((2, 8, rows), F32),
            pltpu.VMEM((rows, total), BF),
            pltpu.VMEM((rows, rows), F32),
            pltpu.VMEM((rows, width), F32),
            pltpu.VMEM((rows, width), F32),
            pltpu.VMEM((rows, width), BF),
            pltpu.VMEM((2, 3, rows, ft), BF),
            pltpu.VMEM((3, rows, width), BF),
            pltpu.VMEM((2, rows, 128), F32),
            sem, sem((2,)), sem((2,)), sem((2, 2)), sem((2, 4)), sem, sem((2, 3)), sem((6,)),
        ]

    def bind(self, x, weights, bias, up_bias, slopes, norms, slot, outs, scratch):
        self.x_hbm, self.weights, self.bias, self.up_bias, self.slopes, self.norms = x, weights, bias, up_bias, slopes, norms
        self.slot, self.outs = slot, outs
        (self.x, self.w, self.o, self.up, self.down, self.qkv, self.lse, self.mixed, self.dist, self.normed, self.acc,
         self.low, self.tile, self.row, self.stat, self.x_sem, self.w_sem, self.o_sem, self.f_sem, self.q_sem, self.m_sem,
         self.t_sem, self.r_sem) = scratch

    def start_x(self):
        copy(self.x_hbm, self.x, self.x_sem).start()

    def start_w(self, k):
        s = lax.rem(k, 2)
        pick(k, self.heads_steps, self.weights[0], self.weights[1],
             lambda ref, j: [(ref.at[:, :, block(j, CW)], self.w.at[s], self.w_sem.at[s])])

    def start_o(self, side):
        copy(self.weights[2 + side], self.o.at[pl.ds(side * self.local, self.local)], self.o_sem.at[side]).start()

    def start_f(self, k):
        s = lax.rem(k, 2)
        ft = self.ft
        pick(k, self.tiles, (self.weights[4], self.weights[6]), (self.weights[5], self.weights[7]),
             lambda ref, j: [(ref[0].at[:, :, block(j, ft)], self.up.at[s], self.f_sem.at[s, 0]),
                             (ref[1].at[:, block(j, ft)], self.down.at[s], self.f_sem.at[s, 1])])

    def write_qkv(self, i, s):
        cols = block(i, CW)
        return [copy(self.qkv.at[s, c], out.at[self.slot, :, cols], self.q_sem.at[s, c])
                for c, out in enumerate(self.outs[:3])] + [
            copy(self.lse.at[s], self.outs[4].at[self.slot, i], self.q_sem.at[s, 3])]

    def attention_step(self, i, ahead):
        s = lax.rem(i, 2)
        qkv = self.qkv
        arrived(self.w.at[s], self.w_sem.at[s])

        @pl.when(i >= 2)
        def _():
            for item in self.write_qkv(i - 2, s):
                item.wait()

        values = self.x[...]
        b = self.bias[:, block(i, CW)].astype(F32)
        qkv[s, 0] = (dot(values, self.w[s, 0]) + b[0:1]).astype(BF)
        qkv[s, 1] = dot(values, self.w[s, 1]).astype(BF)
        qkv[s, 2] = (dot(values, self.w[s, 2]) + b[1:2]).astype(BF)

        @pl.when(i + 2 < ahead)
        def _():
            self.start_w(i + 2)

        parts = []
        scores_of = []
        for head in range(PER):
            cols = slice(head * HD, (head + 1) * HD)
            query = qkv[s, 0, :, cols] * BF(1.0 / math.sqrt(HD))
            scores_of.append(dot(qkv[s, 1, :, cols], query, NT))
        lows = []
        for head in range(PER):
            scores = scores_of[head] - self.dist[...] * slope_of(self.slopes, i * PER + head)
            top = jnp.max(scores, axis=0, keepdims=True)
            likely = jnp.exp(scores - top)
            mass = jnp.sum(likely, axis=0, keepdims=True)
            lows.append((likely * (1.0 / mass)).astype(BF))
            self.lse[s, head : head + 1, :] = top + jnp.log(mass)
        for head in range(PER):
            cols = slice(head * HD, (head + 1) * HD)
            parts.append(dot(lows[head], qkv[s, 2, :, cols], TN).astype(BF))
        self.mixed[:, block(i, CW)] = jnp.concatenate(parts, axis=1)
        for item in self.write_qkv(i, s):
            item.start()

    def middle(self):
        rows, width = self.rows, self.width
        copy(self.mixed, self.outs[3].at[self.slot], self.m_sem).start()
        for side in range(2):
            arrived(self.o.at[pl.ds(side * self.local, self.local)], self.o_sem.at[side])
        vec = norm_rows(self.norms)
        for rs in halves(rows):
            attended = dot(self.mixed[rs, :], self.o[...])
            u, rstd = normalize(self.x[rs, :].astype(F32) + attended + vec[0])
            normed = u * vec[1] + vec[2]
            self.normed[rs, :] = normed
            self.low[rs, :] = normed.astype(BF)
            self.row[0, rs, :] = u.astype(BF)
            self.stat[0, rs, :] = jnp.broadcast_to(rstd, (rows // 2, 128))
            self.acc[rs, :] = jnp.zeros((rows // 2, width), F32)
        for index, item in enumerate(self.first_rows()):
            copy(*item, self.r_sem.at[index]).start()

    def first_rows(self):
        return [(self.low, self.outs[8].at[self.slot]), (self.row.at[0], self.outs[9].at[self.slot]),
                (self.stat.at[0], self.outs[11].at[self.slot])]

    def write_tiles(self, i, s):
        return [copy(self.tile.at[s, c], out.at[self.slot, :, block(i, self.ft)], self.t_sem.at[s, c])
                for c, out in enumerate(self.outs[5:8])]

    def ffn_step(self, i, ahead):
        s = lax.rem(i, 2)
        arrived(self.up.at[s], self.f_sem.at[s, 0])
        arrived(self.down.at[s], self.f_sem.at[s, 1])

        @pl.when(i >= 2)
        def _():
            for item in self.write_tiles(i - 2, s):
                item.wait()

        b = self.up_bias[:, block(i, self.ft)].astype(F32)
        low = self.low[...]
        gate = dot(low, self.up[s, 0]) + b[0:1]
        lift = dot(low, self.up[s, 1]) + b[1:2]
        cdf = 0.5 * lax.erf(gate * (1.0 / math.sqrt(2.0))) + 0.5
        act = gate * cdf
        slope = cdf + gate * (jnp.exp(gate * gate * -0.5) * (1.0 / math.sqrt(2.0 * math.pi)))
        self.tile[s, 0] = act.astype(BF)
        self.tile[s, 1] = (lift * slope).astype(BF)
        hidden = (act * lift).astype(BF)
        self.tile[s, 2] = hidden
        self.acc[...] += dot(hidden, self.down[s], NT)

        @pl.when(i + 2 < ahead)
        def _():
            self.start_f(i + 2)

        for item in self.write_tiles(i, s):
            item.start()

    def finish(self, y_out):
        rows = self.rows
        vec = norm_rows(self.norms)
        for rs in halves(rows):
            u, rstd = normalize(self.normed[rs, :] + self.acc[rs, :] + vec[3])
            self.row[1, rs, :] = u.astype(BF)
            self.stat[1, rs, :] = jnp.broadcast_to(rstd, (rows // 2, 128))
            self.row[2, rs, :] = (u * vec[4] + vec[5]).astype(BF)
        ends = [(self.row.at[1], self.outs[10].at[self.slot]), (self.stat.at[1], self.outs[12].at[self.slot]),
                (self.row.at[2], y_out)]
        for index, item in enumerate(ends):
            copy(*item, self.r_sem.at[3 + index]).start()
        for index, item in enumerate(self.first_rows() + ends):
            copy(*item, self.r_sem.at[index]).wait()
        copy(self.mixed, self.outs[3].at[self.slot], self.m_sem).wait()
        for i in (2 * self.heads_steps - 2, 2 * self.heads_steps - 1):
            for item in self.write_qkv(jnp.int32(i), i % 2):
                item.wait()
        for i in (2 * self.tiles - 2, 2 * self.tiles - 1):
            for item in self.write_tiles(jnp.int32(i), i % 2):
                item.wait()

    def flops(self):
        rows, width, total = self.rows, self.width, self.total
        return 2 * rows * width * (4 * total + 6 * self.units) + 4 * rows * rows * total


def layer_forward(x, weights, biases, slopes, norms, lengths, m, turn, chain, deps, slots):
    rows, width = x.shape
    step = Forward(rows, width, weights[0].shape[2], weights[4].shape[2])

    def kernel(ins, outs, scratch):
        lengths_ref = ins[0]
        step.bind(ins[1], ins[2:10], ins[10], ins[11], ins[12], ins[13:17], m, outs[:13], scratch)
        step.start_x()
        for k in range(2):
            step.start_w(jnp.int32(k))
        for side in range(2):
            step.start_o(side)
        for k in range(2):
            step.start_f(jnp.int32(k))
        fill_distance(step.dist, lengths_ref[lax.axis_index("tensor") * slots + m])
        arrived(step.x, step.x_sem)

        @pl.loop(0, 2 * step.heads_steps)
        def _(i):
            step.attention_step(i, 2 * step.heads_steps)

        step.middle()

        @pl.loop(0, 2 * step.tiles)
        def _(i):
            step.ffn_step(i, 2 * step.tiles)

        step.finish(outs[13])

    return call(
        kernel,
        [(lengths, SMEM), x, *weights, *zip(biases, [WHOLE] * 2), (slopes, SMEM), *zip(norms, NORM_SPECS)],
        [shape + (True,) for shape in step.kept(slots)] + [((rows, width), BF, False)],
        step.scratch(),
        chain,
        deps,
        "layer_forward",
        step.flops(),
        54 << 20,
        turn,
    )


def layer_backward(grad, kept, weights, slopes, norms, lengths, m, turn, chain, deps, slots, sent=()):
    qkv_own, qkv_oth, o_own, o_oth, up_own, up_oth, down_own, down_oth = weights
    q, k, v, _, lse, act, slope, _, _, u1, u2, r1, r2 = kept
    rows, width = grad.shape
    local = qkv_own.shape[2]
    units = up_own.shape[2]
    heads_steps = local // CW
    ft = min(512, units)
    tiles = units // ft
    total = 2 * local

    def norm_back(grad_z, u, rstd, gain):
        t = grad_z * gain
        return rstd * (t - jnp.mean(t, axis=1, keepdims=True) - u * jnp.mean(t * u, axis=1, keepdims=True))

    def row_sum(values):
        return jnp.sum(values, axis=0, keepdims=True)

    def kernel(ins, outs, scratch):
        (lengths_ref, g_hbm, q_hbm, k_hbm, v_hbm, lse_hbm, a_hbm, b_hbm, u1_hbm, u2_hbm, r1_hbm, r2_hbm,
         qkv_own_ref, qkv_oth_ref, o_own_ref, o_oth_ref, up_own_ref, up_oth_ref, down_own_ref, down_oth_ref,
         slope_ref) = ins[:21]
        gg0_out, gg1_out, gl_out, ga_out, gq_out, gk_out, gv_out, gx_out, gxl_out, sums_out, ub_out, qv_out = outs[:12]
        (g_ref, u_ref, r_ref, up_ref, down_ref, ab_ref, gg_ref, low_ref, acc_ref, sums_ref, ub_ref, qv_ref,
         w_ref, o_ref, qkv_ref, lse_ref, gm_ref, dist_ref, gqkv_ref,
         g_sem, f_sem, t_sem, w_sem, q_sem, r_sem, x_send, x_recv) = scratch
        slot = m
        t = lax.axis_index("tensor")
        length = lengths_ref[t * slots + m]
        travelling = []
        if sent:
            cross = {"tensor": 1 - t}
            barrier = pltpu.get_barrier_semaphore()
            pl.semaphore_signal(barrier, inc=1, device_id=cross, device_id_type=pl.DeviceIdType.MESH)
            pl.semaphore_wait(barrier, 1)
            for index in range(len(sent)):
                travelling.append(
                    pltpu.make_async_remote_copy(
                        src_ref=ins[25 + index].at[block(1 - t, rows // 2)], dst_ref=outs[12].at[index],
                        send_sem=x_send.at[index], recv_sem=x_recv.at[index],
                        device_id=cross, device_id_type=pl.DeviceIdType.MESH,
                    )
                )
                travelling[-1].start()

        def start_f(i):
            s = lax.rem(i, 2)
            pick(i, tiles, (up_own_ref, down_own_ref), (up_oth_ref, down_oth_ref),
                 lambda ref, j: [(ref[0].at[:, :, block(j, ft)], up_ref.at[s], f_sem.at[s, 0]),
                                 (ref[1].at[:, block(j, ft)], down_ref.at[s], f_sem.at[s, 1])])
            for c, ref in enumerate((a_hbm, b_hbm)):
                copy(ref.at[slot, :, block(i, ft)], ab_ref.at[s, c], f_sem.at[s, 2 + c]).start()

        def start_w(i):
            s = lax.rem(i, 2)
            pick(i, heads_steps, (qkv_own_ref, o_own_ref), (qkv_oth_ref, o_oth_ref),
                 lambda ref, j: [(ref[0].at[:, :, block(j, CW)], w_ref.at[s], w_sem.at[s, 0]),
                                 (ref[1].at[block(j, CW)], o_ref.at[s], w_sem.at[s, 1])])
            for c, ref in enumerate((q_hbm, k_hbm, v_hbm)):
                copy(ref.at[slot, :, block(i, CW)], qkv_ref.at[s, c], w_sem.at[s, 2 + c]).start()
            copy(lse_hbm.at[slot, i], lse_ref.at[s], w_sem.at[s, 5]).start()

        firsts = [(g_hbm, g_ref), (u2_hbm.at[slot], u_ref.at[1]), (r2_hbm.at[slot], r_ref.at[1]),
                  (u1_hbm.at[slot], u_ref.at[0]), (r1_hbm.at[slot], r_ref.at[0])]
        for index, (src, dst) in enumerate(firsts):
            copy(src, dst, g_sem.at[index]).start()
            if index == 2:
                start_f(jnp.int32(0))
                start_f(jnp.int32(1))
        start_w(jnp.int32(0))
        start_w(jnp.int32(1))
        vec = norm_rows(ins[21:25])
        fill_distance(dist_ref, length)
        for index, (src, dst) in enumerate(firsts[:3]):
            copy(src, dst, g_sem.at[index]).wait()
        sums = [jnp.zeros((1, width), F32)] * 3
        for rs in halves(rows):
            grad_y = g_ref[rs, :].astype(F32)
            if turn == 1:
                places = lax.broadcasted_iota(jnp.int32, (rows // 2, width), 0) + rs.start
                grad_y = jnp.where(places < length, grad_y, 0.0)
            u = u_ref[1, rs, :].astype(F32)
            grad_c = norm_back(grad_y, u, r_ref[1, rs, 0:1], vec[4])
            acc_ref[rs, :] = grad_c
            low_ref[0, rs, :] = grad_c.astype(BF)
            for index, values in enumerate((grad_y * u, grad_y, grad_c)):
                sums[index] += row_sum(values)
        for index in range(3):
            sums_ref[index : index + 1, :] = sums[index]
        copy(low_ref.at[0], gl_out.at[slot], r_sem.at[0]).start()

        def write_tiles(i, s):
            return [copy(gg_ref.at[s, c], out.at[slot, :, block(i, ft)], t_sem.at[s, c])
                    for c, out in enumerate((gg0_out, gg1_out))]

        @pl.loop(0, 2 * tiles)
        def _(i):
            s = lax.rem(i, 2)
            arrived(up_ref.at[s], f_sem.at[s, 0])
            arrived(down_ref.at[s], f_sem.at[s, 1])
            for c in range(2):
                arrived(ab_ref.at[s, c], f_sem.at[s, 2 + c])

            @pl.when(i >= 2)
            def _():
                for item in write_tiles(i - 2, s):
                    item.wait()

            gh = dot(low_ref[0], down_ref[s])
            g0 = (gh * ab_ref[s, 1].astype(F32)).astype(BF)
            g1 = (gh * ab_ref[s, 0].astype(F32)).astype(BF)
            gg_ref[s, 0] = g0
            gg_ref[s, 1] = g1
            ub_ref[0:1, block(i, ft)] = row_sum(g0.astype(F32))
            ub_ref[1:2, block(i, ft)] = row_sum(g1.astype(F32))
            acc_ref[...] += dot(g0, up_ref[s, 0], NT) + dot(g1, up_ref[s, 1], NT)

            @pl.when(i + 2 < 2 * tiles)
            def _():
                start_f(i + 2)

            for item in write_tiles(i, s):
                item.start()

        for index, (src, dst) in enumerate(firsts[3:]):
            copy(src, dst, g_sem.at[3 + index]).wait()
        sums = [jnp.zeros((1, width), F32)] * 3
        for rs in halves(rows):
            grad_n = acc_ref[rs, :]
            u = u_ref[0, rs, :].astype(F32)
            grad_a = norm_back(grad_n, u, r_ref[0, rs, 0:1], vec[1])
            low_ref[1, rs, :] = grad_a.astype(BF)
            acc_ref[rs, :] = grad_a
            for index, values in enumerate((grad_n * u, grad_n, grad_a)):
                sums[index] += row_sum(values)
        for index in range(3):
            sums_ref[3 + index : 4 + index, :] = sums[index]
        sums_ref[6:8, :] = jnp.zeros((2, width), F32)
        copy(low_ref.at[1], ga_out.at[slot], r_sem.at[1]).start()
        scale = BF(1.0 / math.sqrt(HD))

        def write_heads(i, s):
            return [copy(gqkv_ref.at[s, c], out.at[slot, :, block(i, CW)], q_sem.at[s, c])
                    for c, out in enumerate((gq_out, gk_out, gv_out))]

        @pl.loop(0, 2 * heads_steps)
        def _(i):
            s = lax.rem(i, 2)
            for index, ref in enumerate((w_ref.at[s], o_ref.at[s], qkv_ref.at[s, 0], qkv_ref.at[s, 1], qkv_ref.at[s, 2], lse_ref.at[s])):
                arrived(ref, w_sem.at[s, index])

            @pl.when(i >= 2)
            def _():
                for item in write_heads(i - 2, s):
                    item.wait()

            gm_ref[...] = dot(low_ref[1], o_ref[s], NT).astype(BF)
            parts = [[], [], []]
            scores_of = []
            for head in range(PER):
                cols = slice(head * HD, (head + 1) * HD)
                query = qkv_ref[s, 0, :, cols] * scale
                scores_of.append(dot(qkv_ref[s, 1, :, cols], query, NT))
            for head in range(PER):
                cols = slice(head * HD, (head + 1) * HD)
                query = qkv_ref[s, 0, :, cols] * scale
                key = qkv_ref[s, 1, :, cols]
                gm = gm_ref[:, cols]
                gw = dot(qkv_ref[s, 2, :, cols], gm, NT)
                scores = scores_of[head] - dist_ref[...] * slope_of(slope_ref, i * PER + head)
                likely = jnp.exp(scores - lse_ref[s, head : head + 1, :])
                parts[2].append(dot(likely.astype(BF), gm).astype(BF))
                t = likely * gw
                inner = jnp.sum(t, axis=0, keepdims=True)
                gs = (t - likely * inner).astype(BF)
                parts[1].append(dot(gs, query).astype(BF))
                parts[0].append(dot(key * scale, gs, TN).astype(BF).T)
            for c in range(3):
                gqkv_ref[s, c] = jnp.concatenate(parts[c], axis=1)
            for index, c in enumerate((0, 2)):
                qv_ref[index : index + 1, block(i, CW)] = row_sum(gqkv_ref[s, c].astype(F32))
            acc_ref[...] += (
                dot(gqkv_ref[s, 0], w_ref[s, 0], NT)
                + dot(gqkv_ref[s, 1], w_ref[s, 1], NT)
                + dot(gqkv_ref[s, 2], w_ref[s, 2], NT)
            )

            @pl.when(i + 2 < 2 * heads_steps)
            def _():
                start_w(i + 2)

            for item in write_heads(i, s):
                item.start()

        g_ref[...] = acc_ref[...].astype(BF)
        ends = [(g_ref, gxl_out), (acc_ref, gx_out), (sums_ref, sums_out), (ub_ref, ub_out), (qv_ref, qv_out)]
        for index, (src, dst) in enumerate(ends):
            copy(src, dst, r_sem.at[2 + index]).start()
        for index, (src, dst) in enumerate([(low_ref.at[0], gl_out.at[slot]), (low_ref.at[1], ga_out.at[slot])] + ends):
            copy(src, dst, r_sem.at[index]).wait()
        for i in (2 * tiles - 2, 2 * tiles - 1):
            for item in write_tiles(jnp.int32(i), i % 2):
                item.wait()
        for i in (2 * heads_steps - 2, 2 * heads_steps - 1):
            for item in write_heads(jnp.int32(i), i % 2):
                item.wait()
        for item in travelling:
            item.wait()

    sem = pltpu.SemaphoreType.DMA
    return call(
        kernel,
        [(lengths, SMEM), grad, q, k, v, lse, act, slope, u1, u2, r1, r2, *weights, (slopes, SMEM), *zip(norms, NORM_SPECS), *sent],
        [((slots, rows, 2 * units), BF, True)] * 2
        + [((slots, rows, width), BF, True)] * 2
        + [((slots, rows, total), BF, True)] * 3
        + [
            ((rows, width), F32, False),
            ((rows, width), BF, False),
            ((8, width), F32, False),
            ((2, 2 * units), F32, False),
            ((2, total), F32, False),
        ]
        + ([((len(sent), rows // 2, width), BF, False)] if sent else []),
        [
            pltpu.VMEM((rows, width), BF),
            pltpu.VMEM((2, rows, width), BF),
            pltpu.VMEM((2, rows, 128), F32),
            pltpu.VMEM((2, 2, width, ft), BF),
            pltpu.VMEM((2, width, ft), BF),
            pltpu.VMEM((2, 2, rows, ft), BF),
            pltpu.VMEM((2, 2, rows, ft), BF),
            pltpu.VMEM((2, rows, width), BF),
            pltpu.VMEM((rows, width), F32),
            pltpu.VMEM((8, width), F32),
            pltpu.VMEM((2, 2 * units), F32),
            pltpu.VMEM((2, total), F32),
            pltpu.VMEM((2, 3, width, CW), BF),
            pltpu.VMEM((2, CW, width), BF),
            pltpu.VMEM((2, 3, rows, CW), BF),
            pltpu.VMEM((2, 8, rows), F32),
            pltpu.VMEM((rows, CW), BF),
            pltpu.VMEM((rows, rows), F32),
            pltpu.VMEM((2, 3, rows, CW), BF),
            sem((5,)), sem((2, 4)), sem((2, 2)), sem((2, 6)), sem((2, 3)), sem((7,)), sem((4,)), sem((4,)),
        ],
        chain,
        deps,
        "layer_backward",
        2 * rows * width * (4 * total + 6 * units) + 10 * rows * rows * total,
        70 << 20,
        turn,
        bool(sent),
    )


MESH = pl.DeviceIdType.MESH
CORE_LAG = 2
CROSS_LAG = 2
CHAIN_LAG = 1


def neighbours():
    t = lax.axis_index("tensor")
    d = lax.axis_index("dp")
    last = lax.axis_size("dp") // 2 - 1
    c = lax.rem(d, 2)
    z = d // 2
    return t, c, z, last, {"dp": d + 1 - 2 * c}, {"tensor": 1 - t}, {"dp": d + 2}, {"dp": d - 2}


def greet(c, z, chips, core, cross):
    barrier = pltpu.get_barrier_semaphore()
    pl.semaphore_signal(barrier, inc=1, device_id=core, device_id_type=MESH)
    pl.semaphore_signal(barrier, inc=1, device_id=cross, device_id_type=MESH)
    for shift in range(1, chips):
        chip = lax.rem(z + shift, chips)
        pl.semaphore_signal(barrier, inc=1, device_id={"dp": chip * 2 + c}, device_id_type=MESH)
    pl.semaphore_wait(barrier, 1 + chips)


def fetch_and_forward(weights, biases, inputs, cotangent, slopes, norms, lengths, chips, slots):
    seqs = inputs.shape[0] // 2
    shard_rows, width = inputs.shape[1:]
    rows = 2 * shard_rows
    groups = 2 * chips
    qkv, out, up, down = weights
    local, units = qkv.shape[2], up.shape[2]
    step = Forward(rows, width, local, units)
    ft, tiles = step.ft, step.tiles
    bias_widths = [b.shape[1] for b in biases]
    QKV, OUT, UP, DOWN, ROWS, BIAS = range(6)

    plan = [(UP, 0, groups), (ROWS, 0, 0), (BIAS, 0, 0), (BIAS, 1, 0)]
    plan += [(UP, part, groups) for part in range(1, tiles)]
    plan += [(DOWN, part, groups) for part in range(tiles - 2)]
    plan += [(QKV, part, 2) for part in range(3)] + [(OUT, 0, 2)]
    plan += [(DOWN, part, 2) for part in range(tiles - 2, tiles)]
    plan += [(ROWS, part, 0) for part in range(1, seqs)]
    n = len(plan)
    number = {item[:2]: index for index, item in enumerate(plan)}

    def size(index):
        kind, part, pieces = plan[index]
        whole = {QKV: width * local, OUT: local * width, UP: 2 * width * ft, DOWN: width * ft, ROWS: shard_rows * width, BIAS: 64}
        return whole[kind] / max(1, pieces)

    events, clock, busy = [], 0.0, 0.0
    for index, (kind, part, pieces) in enumerate(plan):
        clock += size(index)
        events.append((clock + 132000, index, 0))
        if pieces == groups:
            start = max(clock, busy)
            busy = start + size(index) * (chips - 1) * 1.0
            events += [(start + (size(index) * 1.0 + 132000) * hop, index, hop) for hop in range(1, chips)]
    events.sort()
    when = {event[1:]: event[0] for event in events}

    def ready(*keys):
        return max(when[key] for k in keys for key in when if key[0] == number[k])

    needs = [[(ROWS, 0), (BIAS, 0)], []] + [[(QKV, part) for part in range(3)], []] + [[(OUT, 0), (BIAS, 1)]]
    needs += [[] for _ in range(tiles - 1)]
    needs += [[(UP, part), (DOWN, part)] for part in range(tiles)] + [[]]
    assert step.heads_steps == 2
    rounds, taken = [], 0
    for need in needs:
        mine = []
        if need:
            limit = ready(*need)
            while taken < len(events) and events[taken][0] <= limit:
                mine.append(events[taken][1:])
                taken += 1
        rounds.append((mine, need))
    rest = [event[1:] for event in events[taken:]]
    n_rounds = len(rounds)
    n_kept = len(step.kept(slots))

    def kernel(*refs):
        lengths_ref, slope_ref, norm_refs = refs[0], refs[1], refs[2:6]
        refs = refs[6:]
        ins, bias_ins, held_refs = refs[:4], refs[4:6], refs[6:8]
        outs, bias_outs, row_refs = refs[8:12], refs[12:14], refs[14 : 14 + seqs]
        kept_refs = refs[14 + seqs : 14 + seqs + n_kept]
        y_ref = refs[14 + seqs + n_kept]
        stage, qv_bias, ub_bias, x_send, x_recv, c_send, c_recv, u_send, u_recv, d_send, d_recv, l_sem, b_sem = refs[
            15 + seqs + n_kept : 28 + seqs + n_kept
        ]
        t, c, z, last, core, cross, above, below = neighbours()
        section = lax.axis_index("section")
        greet(c, z, chips, core, cross)
        paired = [item for pair in zip(ins, outs) for item in pair]
        step.bind(
            row_refs[0], paired, qv_bias, ub_bias, slope_ref, norm_refs, 0, kept_refs, refs[28 + seqs + n_kept :]
        )

        def span(part):
            return block(part, shard_rows)

        def bias_part(m, side):
            return bias_outs[m].at[:, pl.ds(side * bias_widths[m], bias_widths[m])]

        def piece(side, index, chip, on):
            kind, part, pieces = plan[index]
            place = chip * 2 + on if pieces == groups else on
            ref = (ins, outs)[side][kind]
            if kind == QKV:
                return ref.at[part, block(place, width // pieces)]
            if kind == OUT:
                return ref.at[block(place, local // pieces)]
            cols = pl.ds(part * ft, ft)
            if kind == DOWN:
                return ref.at[block(place, width // pieces), cols]
            per = pieces // 2
            return ref.at[place // per, block(lax.rem(place, per), width // per), cols]

        def cross_copy(index, held_ref=None):
            kind, m, pieces = plan[index]
            if kind == ROWS:
                src = (held_refs[0] if held_ref is None else held_ref).at[(1 - t) * seqs + m]
                dst = row_refs[m].at[span(t)]
            elif kind == BIAS:
                src, dst = bias_ins[m], bias_part(m, 1)
            else:
                src, dst = piece(0, index, z, c), piece(1, index, z, c)
            return pltpu.make_async_remote_copy(
                src_ref=src, dst_ref=dst, send_sem=x_send.at[index], recv_sem=x_recv.at[index],
                device_id=cross, device_id_type=MESH,
            )

        def pass_on(index, chip, send, recv, device):
            place = piece(1, index, chip, c)
            return pltpu.make_async_remote_copy(
                src_ref=place, dst_ref=place, send_sem=send.at[index, chip], recv_sem=recv.at[index, chip],
                device_id=device, device_id_type=MESH,
            )

        def got(index, chip, on, sem):
            arrived(piece(1, index, chip, on), sem)

        for m in range(2):
            copy(bias_ins[m], bias_part(m, 0), b_sem.at[m]).start()
        for index in range(n):
            if plan[index][0] == ROWS:
                for turn in range(2):
                    @pl.when(section == turn)
                    def _(index=index, turn=turn):
                        cross_copy(index, held_refs[turn]).start()
            else:
                cross_copy(index).start()
        for turn in range(2):
            @pl.when(section == turn)
            def _(turn=turn):
                copy(held_refs[turn].at[pl.ds(t * seqs, seqs)], stage, l_sem.at[0]).start()

        @pl.when(section == 0)
        def _():
            for k in range(2):
                step.start_w(jnp.int32(k))
            step.start_o(0)
            for k in range(2):
                step.start_f(jnp.int32(k))
            fill_distance(step.dist, lengths_ref[t * seqs])

        arrived(stage, l_sem.at[0])
        for m in range(seqs):
            copy(stage.at[m], row_refs[m].at[span(t)], l_sem.at[m]).start()
        for m in range(seqs):
            arrived(stage.at[m], l_sem.at[m])
        for m in range(2):
            copy(bias_ins[m], bias_part(m, 0), b_sem.at[m]).wait()

        def handle(index, hop):
            kind, m, pieces = plan[index]
            if kind == ROWS:
                arrived(row_refs[m].at[span(1 - t)], x_recv.at[index])
            elif kind == BIAS:
                arrived(bias_part(m, 1), x_recv.at[index])
            elif hop == 0:
                got(index, z, c, x_recv.at[index])
                if pieces == groups:
                    @pl.when(z < last)
                    def _():
                        pass_on(index, z, u_send, u_recv, above).start()

                    @pl.when(z > 0)
                    def _():
                        pass_on(index, z, d_send, d_recv, below).start()

                pass_on(index, z, c_send, c_recv, core).start()
            else:
                @pl.when(z - hop >= 0)
                def _():
                    got(index, z - hop, c, u_recv.at[index, z - hop])

                    @pl.when(z < last)
                    def _():
                        pass_on(index, z - hop, u_send, u_recv, above).start()

                    pass_on(index, z - hop, c_send, c_recv, core).start()

                @pl.when(z + hop <= last)
                def _():
                    got(index, z + hop, c, d_recv.at[index, z + hop])

                    @pl.when(z > 0)
                    def _():
                        pass_on(index, z + hop, d_send, d_recv, below).start()

                    pass_on(index, z + hop, c_send, c_recv, core).start()

        def from_core(key):
            index = number[key]
            kind, m, pieces = plan[index]
            if pieces == groups:
                for chip in range(chips):
                    got(index, chip, 1 - c, c_recv.at[index, chip])
            elif pieces:
                got(index, z, 1 - c, c_recv.at[index, z])

        @pl.loop(0, n_rounds)
        def _(tau):
            for number_, (mine, need) in enumerate(rounds):
                if not (mine or need):
                    continue

                @pl.when(tau == number_)
                def _(number_=number_, mine=mine, need=need):
                    for index, hop in mine:
                        handle(index, hop)
                    for key in need:
                        from_core(key)
                    for key in need:
                        if key == (BIAS, 0):
                            @pl.when(section == 0)
                            def _():
                                step.start_x()
                                copy(bias_outs[0], qv_bias, b_sem.at[0]).start()
                                copy(bias_outs[0], qv_bias, b_sem.at[0]).wait()
                                arrived(step.x, step.x_sem)
                        elif key == (QKV, 2):
                            @pl.when(section == 0)
                            def _():
                                for k in range(2, 4):
                                    step.start_w(jnp.int32(k))
                        elif key == (OUT, 0):
                            @pl.when(section == 0)
                            def _():
                                step.start_o(1)
                        elif key == (BIAS, 1):
                            @pl.when(section == 0)
                            def _():
                                copy(bias_outs[1], ub_bias, b_sem.at[1]).start()
                                copy(bias_outs[1], ub_bias, b_sem.at[1]).wait()
                        elif key[0] == DOWN:
                            @pl.when(section == 0)
                            def _(key=key):
                                step.start_f(jnp.int32(tiles + key[1]))

            @pl.when(section == 0)
            def _():
                @pl.when(tau < 4)
                def _():
                    step.attention_step(tau, 2)

                @pl.when(tau == 4)
                def _():
                    step.middle()

                @pl.when(tau > 4)
                def _():
                    step.ffn_step(tau - 5, tiles)

        @pl.when(section == 0)
        def _():
            step.finish(y_ref)

        for index, hop in rest:
            handle(index, hop)
        for index in range(n):
            kind, part, pieces = plan[index]
            cross_copy(index).wait_send()
            if pieces == 2:
                pass_on(index, z, c_send, c_recv, core).wait_send()
            if pieces != groups:
                continue
            for chip in range(chips):
                pass_on(index, chip, c_send, c_recv, core).wait_send()

                @pl.when((chip <= z) & (z < last))
                def _(chip=chip):
                    pass_on(index, chip, u_send, u_recv, above).wait_send()

                @pl.when((chip >= z) & (z > 0))
                def _(chip=chip):
                    pass_on(index, chip, d_send, d_recv, below).wait_send()

    sem = pltpu.SemaphoreType.DMA
    return pl.pallas_call(
        kernel,
        in_specs=[SMEM, SMEM] + NORM_SPECS + [ANY] * 8,
        out_specs=[ANY] * (7 + seqs + n_kept),
        out_shape=[jax.ShapeDtypeStruct(w.shape, BF) for w in weights]
        + [jax.ShapeDtypeStruct((2, 2 * size_), BF) for size_ in bias_widths]
        + [jax.ShapeDtypeStruct((rows, width), BF)] * seqs
        + [jax.ShapeDtypeStruct(*shape) for shape in step.kept(slots)]
        + [jax.ShapeDtypeStruct((rows, width), BF)],
        scratch_shapes=[pltpu.VMEM((seqs, shard_rows, width), BF)]
        + [pltpu.VMEM((2, 2 * size_), BF) for size_ in bias_widths]
        + [sem((n,)), sem((n,))]
        + [sem((n, chips))] * 6
        + [sem((seqs,)), sem((2,))]
        + step.scratch(),
        compiler_params=pltpu.CompilerParams(collective_id=1, has_side_effects=True, vmem_limit_bytes=VMEM_LIMIT),
        cost_estimate=pl.CostEstimate(flops=step.flops(), bytes_accessed=90 << 20, transcendentals=0),
        name="fetch_and_forward",
    )(lengths, slopes, *norms, *weights, *biases, inputs, cotangent)


def norm_back(grad_z, u, rstd, gain):
    t = grad_z * gain
    return rstd * (t - jnp.mean(t, axis=1, keepdims=True) - u * jnp.mean(t * u, axis=1, keepdims=True))


def row_sum(values):
    return jnp.sum(values, axis=0, keepdims=True)


def backward_and_reduce(grad, kept, back, x_all, weights, slopes, norms, lengths, sums, low_grad, second, chips):
    q, k_, v, mixed_all, lse, act, slope, hidden_all, normed_all, u1, u2, r1, r2 = kept
    gg0, gg1, gl, ga, gq, gk, gv = back
    rows, width = grad.shape
    local, units = weights[0].shape[2], weights[4].shape[2]
    ft = CW
    tiles = units // ft
    heads_steps = local // CW
    seqs = 2
    bt = 128
    lefts = [gl, normed_all, x_all, ga]
    rights = [hidden_all, gg0, gg1, gq, gk, gv, mixed_all]
    group_of = [0, 1, 1, 2, 2, 2, 3]
    member_of = [0, 0, 1, 0, 1, 2, 0]
    half = width // 2
    quarter = half // 2
    per_pair = ft // bt
    pairs = tiles
    ffn_blocks = 3 * per_pair * pairs
    head_blocks = local // bt
    total = ffn_blocks + 4 * head_blocks
    ring, mines, gives = 4, CORE_LAG + 1, 4
    ahead_of = 2
    drain = CORE_LAG + CROSS_LAG + 2 * (chips - 1) * CHAIN_LAG + 1
    shard_rows = rows // 2
    norm_at = 2 * tiles
    head_at = norm_at + 1
    end_at = head_at + 5 * 2 * heads_steps
    x_flip, ga_flip = ffn_blocks - per_pair, ffn_blocks + per_pair
    up_rows = units // width
    vec_shape = (6 + 4 * up_rows + 2, width)
    spread = 42
    last_turn = ahead_of - (ahead_of - end_at) * spread // (end_at + 1 - ahead_of) + 1
    assert spread >= end_at + 1 - ahead_of and last_turn < ahead_of + ffn_blocks - ring

    def kernel(*refs):
        lengths_ref, slope_ref, norm_refs, sum_refs = refs[0], refs[1], refs[2:6], refs[6:15]
        refs = refs[12:]
        g_hbm, q_hbm, k_hbm, v_hbm, lse_hbm, a_hbm, b_hbm, u1_hbm, u2_hbm, r1_hbm, r2_hbm = refs[3:14]
        (qkv_own_ref, qkv_oth_ref, o_own_ref, o_oth_ref, up_own_ref, up_oth_ref, down_own_ref, down_oth_ref) = refs[14:22]
        left_refs, right_refs = refs[22:26], refs[26:33]
        low_grad_ref, second_ref = refs[33:35]
        outs, sums_out, rows_out = refs[35:39], refs[39], refs[40]
        fresh = refs[41:46]
        gx_out, gxl_out = refs[46:48]
        (
            acc, from_x, from_z, flip, stage, tile, mine, give, vec, vec_in, vec_all,
            g_ref, u_ref, r_ref, low_ref, gacc_ref, w_ref, o_ref, qkv_ref, gqkv_ref, lse_ref, gm_ref, gs_ref, dist_ref,
            part_sums, ub_sums, qv_sums,
            tile_sem, stage_sem, give_send, core_recv, x_send, x_recv, z_send, z_recv, f_send, f_recv,
            store_sem, out_send, out_recv, v_send, v_recv, r_send, r_recv,
            g_sem, w_sem, t_sem, e_sem,
        ) = refs[48:]
        final = from_x
        t, c, z, last, core, cross, above, below = neighbours()
        section = lax.axis_index("section")
        first = section == 0
        greet(c, z, chips, core, cross)
        fresh_of = {1: fresh[0].at[0], 2: fresh[1].at[0], 3: fresh[2], 4: fresh[3], 5: fresh[4]}
        vec_w = norm_rows(norm_refs)

        def remote(src, dst, send, recv, device):
            return pltpu.make_async_remote_copy(
                src_ref=src, dst_ref=dst, send_sem=send, recv_sem=recv, device_id=device, device_id_type=MESH
            )

        def valid(k):
            return (k >= 0) & (k < total)

        def member(k, visit):
            for m in range(3):
                @pl.when((k < ffn_blocks) & (lax.rem(k, 3 * per_pair) // per_pair == m))
                def _(m=m):
                    visit(m, k // (3 * per_pair) * per_pair + lax.rem(k, per_pair))

            for m in range(3, 7):
                base = ffn_blocks + (m - 3) * head_blocks

                @pl.when((k >= base) & (k < base + head_blocks))
                def _(m=m, base=base):
                    visit(m, k - base)

        def load_tile(k):
            at = lax.rem(k, ring)

            def visit(m, j):
                count = right_refs[m].shape[2] // (2 * bt)
                for side in range(2):
                    cols = block(side * count + j, bt)
                    where = pl.ds(side * bt, bt)
                    copy(right_refs[m].at[0, :, cols], tile.at[at, 0, :, where], tile_sem.at[at]).start()
                    if m not in fresh_of:
                        copy(right_refs[m].at[1, :, cols], tile.at[at, 1, :, where], tile_sem.at[at]).start()
                        continue

                    @pl.when(first)
                    def _(cols=cols, where=where):
                        copy(fresh_of[m].at[:, cols], tile.at[at, 1, :, where], tile_sem.at[at]).start()

                    @pl.when(section == 1)
                    def _(cols=cols, where=where):
                        copy(right_refs[m].at[1, :, cols], tile.at[at, 1, :, where], tile_sem.at[at]).start()

            member(k, visit)

        def take_left(g, at, mine_low):
            copy(left_refs[g].at[0], stage.at[0], stage_sem.at[0]).start()
            if mine_low is None:
                copy(left_refs[g].at[1], stage.at[1], stage_sem.at[1]).start()
                arrived(stage.at[1], stage_sem.at[1])
            else:
                @pl.when(first)
                def _():
                    stage[1] = low_ref[mine_low]

                @pl.when(section == 1)
                def _():
                    copy(left_refs[g].at[1], stage.at[1], stage_sem.at[1]).start()
                    arrived(stage.at[1], stage_sem.at[1])

            arrived(stage.at[0], stage_sem.at[0])
            for m in range(seqs):
                flip[at, :, m * rows : (m + 1) * rows] = stage[m].T

        def place_of(u):
            return lax.rem(u, 2), u // 2

        def start_f(u):
            at = lax.rem(u, 2)
            side, j = place_of(u)
            pick(side * tiles + j, tiles, (up_own_ref, down_own_ref), (up_oth_ref, down_oth_ref),
                 lambda ref, jj: [(ref[0].at[:, :, block(jj, ft)], w_ref.at[at, pl.ds(0, 2)], w_sem.at[at, 0]),
                                  (ref[1].at[:, block(jj, ft)], w_ref.at[at, 2], w_sem.at[at, 1])])
            for n, ref in enumerate((a_hbm, b_hbm)):
                copy(ref.at[1, :, block(side * tiles + j, ft)], qkv_ref.at[at, n], w_sem.at[at, 2 + n]).start()

        def write_tile(u):
            at = lax.rem(u, 2)
            side, j = place_of(u)
            return [copy(gqkv_ref.at[at, n], fresh[n].at[0, :, block(side * tiles + j, ft)], t_sem.at[at, n]) for n in range(2)]

        def start_w(i):
            at = lax.rem(i, 2)
            pick(i, heads_steps, (qkv_own_ref, o_own_ref), (qkv_oth_ref, o_oth_ref),
                 lambda ref, j: [(ref[0].at[:, :, block(j, CW)], w_ref.at[at], w_sem.at[at, 0]),
                                 (ref[1].at[block(j, CW)], o_ref.at[at], w_sem.at[at, 1])])
            for n, ref in enumerate((q_hbm, k_hbm, v_hbm)):
                copy(ref.at[1, :, block(i, CW)], qkv_ref.at[at, n], w_sem.at[at, 2 + n]).start()
            copy(lse_hbm.at[1, i], lse_ref.at[at], w_sem.at[at, 5]).start()

        def write_heads(i):
            at = lax.rem(i, 2)
            return [copy(gqkv_ref.at[at, n], fresh[2 + n].at[:, block(i, CW)], t_sem.at[at, n]) for n in range(3)]

        def norm_load(index, u_hbm, r_hbm):
            return [copy(u_hbm.at[1], u_ref, g_sem.at[index]), copy(r_hbm.at[1], r_ref, g_sem.at[index + 1])]

        def begin():
            copy(g_hbm, g_ref, g_sem.at[0]).start()
            for item in norm_load(1, u2_hbm, r2_hbm):
                item.start()
            start_f(jnp.int32(0))
            start_f(jnp.int32(1))
            copy(g_hbm, g_ref, g_sem.at[0]).wait()
            for item in norm_load(1, u2_hbm, r2_hbm):
                item.wait()
            totals = [jnp.zeros((1, width), F32)] * 3
            for rs in halves(rows):
                grad_y = g_ref[rs, :].astype(F32)
                u = u_ref[rs, :].astype(F32)
                grad_c = norm_back(grad_y, u, r_ref[rs, 0:1], vec_w[4])
                gacc_ref[rs, :] = grad_c
                low_ref[0, rs, :] = grad_c.astype(BF)
                for index, values in enumerate((grad_y * u, grad_y, grad_c)):
                    totals[index] += row_sum(values)
            for index in range(3):
                part_sums[index : index + 1, :] = totals[index]
            for item in norm_load(1, u1_hbm, r1_hbm):
                item.start()

        def ffn_unit(u):
            at = lax.rem(u, 2)

            @pl.when(u >= 1)
            def _():
                for item in write_tile(u - 1):
                    item.wait()

            arrived(w_ref.at[at, pl.ds(0, 2)], w_sem.at[at, 0])
            arrived(w_ref.at[at, 2], w_sem.at[at, 1])
            for n in range(2):
                arrived(qkv_ref.at[at, n], w_sem.at[at, 2 + n])
            gh = dot(low_ref[0], w_ref[at, 2])
            g0 = (gh * qkv_ref[at, 1].astype(F32)).astype(BF)
            g1 = (gh * qkv_ref[at, 0].astype(F32)).astype(BF)
            gqkv_ref[at, 0] = g0
            gqkv_ref[at, 1] = g1
            side, j = place_of(u)
            cols = block(side * tiles + j, ft)
            ub_sums[0:1, cols] = row_sum(g0.astype(F32))
            ub_sums[1:2, cols] = row_sum(g1.astype(F32))
            gacc_ref[...] += dot(g0, w_ref[at, 0], NT) + dot(g1, w_ref[at, 1], NT)

            @pl.when(u + 2 < 2 * tiles)
            def _():
                start_f(u + 2)

            for item in write_tile(u):
                item.start()

        def norm_unit():
            for item in write_tile(jnp.int32(2 * tiles - 1)):
                item.wait()
            for i in range(2):
                start_w(jnp.int32(i))
            fill_distance(dist_ref, lengths_ref[t * seqs + 1])
            for item in norm_load(1, u1_hbm, r1_hbm):
                item.wait()
            totals = [jnp.zeros((1, width), F32)] * 3
            for rs in halves(rows):
                grad_n = gacc_ref[rs, :]
                u = u_ref[rs, :].astype(F32)
                grad_a = norm_back(grad_n, u, r_ref[rs, 0:1], vec_w[1])
                low_ref[1, rs, :] = grad_a.astype(BF)
                gacc_ref[rs, :] = grad_a
                for index, values in enumerate((grad_n * u, grad_n, grad_a)):
                    totals[index] += row_sum(values)
            for index in range(3):
                part_sums[3 + index : 4 + index, :] = totals[index]

        def head_unit(a):
            i = a // 5
            phase = lax.rem(a, 5)
            pair = phase // 2
            at = lax.rem(i, 2)
            scale = BF(1.0 / math.sqrt(HD))
            cols = block(lax.rem(pair, 2), 2 * HD)

            @pl.when(phase == 0)
            def _():
                for index, ref in enumerate(
                    (w_ref.at[at], o_ref.at[at], qkv_ref.at[at, 0], qkv_ref.at[at, 1], qkv_ref.at[at, 2], lse_ref.at[at])
                ):
                    arrived(ref, w_sem.at[at, index])

                @pl.when(i >= 2)
                def _():
                    for item in write_heads(i - 2):
                        item.wait()

                gm_ref[...] = dot(low_ref[1], o_ref[at], NT).astype(BF)

            @pl.when((phase == 0) | (phase == 2))
            def _():
                query2 = qkv_ref[at, 0, :, cols] * scale
                key2 = qkv_ref[at, 1, :, cols]
                value2 = qkv_ref[at, 2, :, cols]
                gm2 = gm_ref[:, cols]
                parts = []
                pairs_here = [slice(head * HD, (head + 1) * HD) for head in range(2)]
                scores_of = [dot(key2[:, here], query2[:, here], NT) for here in pairs_here]
                for head, here in enumerate(pairs_here):
                    gm = gm2[:, here]
                    scores = scores_of[head] - dist_ref[...] * slope_of(slope_ref, i * PER + pair * 2 + head)
                    likely = jnp.exp(scores - lse_ref[at, pl.ds(pair * 2 + head, 1), :])
                    parts.append(dot(likely.astype(BF), gm).astype(BF))
                    tt = likely * dot(value2[:, here], gm, NT)
                    inner = jnp.sum(tt, axis=0, keepdims=True)
                    gs_ref[head] = (tt - likely * inner).astype(BF)
                gqkv_ref[at, 2, :, cols] = jnp.concatenate(parts, axis=1)

            @pl.when((phase == 1) | (phase == 3))
            def _():
                query2 = qkv_ref[at, 0, :, cols] * scale
                key2 = qkv_ref[at, 1, :, cols] * scale
                parts = [[], []]
                for head in range(2):
                    here = slice(head * HD, (head + 1) * HD)
                    gs = gs_ref[head]
                    parts[1].append(dot(gs, query2[:, here]).astype(BF))
                    parts[0].append(dot(key2[:, here], gs, TN).astype(BF).T)
                for n in range(2):
                    gqkv_ref[at, n, :, cols] = jnp.concatenate(parts[n], axis=1)

            @pl.when(phase == 4)
            def _():
                for index, n in enumerate((0, 2)):
                    qv_sums[index : index + 1, block(i, CW)] = row_sum(gqkv_ref[at, n].astype(F32))
                gacc_ref[...] += (
                    dot(gqkv_ref[at, 0], w_ref[at, 0], NT)
                    + dot(gqkv_ref[at, 1], w_ref[at, 1], NT)
                    + dot(gqkv_ref[at, 2], w_ref[at, 2], NT)
                )

                @pl.when(i + 2 < 2 * heads_steps)
                def _():
                    start_w(i + 2)

                for item in write_heads(i):
                    item.start()

        def add_sums(norm_part, ub_part, qv_part):
            vec[0, 0:6] += norm_part[0:6]
            for own in range(2):
                @pl.when(t == own)
                def _(own=own):
                    for n in range(2):
                        for side in range(2):
                            place = own if side == 0 else 1 - own
                            for j in range(up_rows):
                                at = 6 + (2 * n + place) * up_rows + j
                                start = side * units + j * width
                                vec[0, at : at + 1] += ub_part[n : n + 1, start : start + width]
                            at = 6 + 4 * up_rows + n
                            cols = slice(place * local, (place + 1) * local)
                            vec[0, at : at + 1, cols] += qv_part[n : n + 1, side * local : (side + 1) * local]

        ends = [(g_ref, gxl_out), (gacc_ref, gx_out)]

        def end_unit():
            for i in (2 * heads_steps - 2, 2 * heads_steps - 1):
                for item in write_heads(jnp.int32(i)):
                    item.wait()
            g_ref[...] = gacc_ref[...].astype(BF)
            for index, item in enumerate(ends):
                copy(*item, e_sem.at[index]).start()
            add_sums(part_sums, ub_sums, qv_sums)
            for index, item in enumerate(ends):
                copy(*item, e_sem.at[index]).wait()

        vec[0] = jnp.zeros(vec_shape, F32)

        @pl.when(first)
        def _():
            begin()
            add_sums(*sum_refs[:3])

        @pl.when(section == 1)
        def _():
            add_sums(*sum_refs[3:6])
            add_sums(*sum_refs[6:9])

        take_left(0, 0, 0)
        vec_core = remote(vec.at[0], vec_in.at[0], v_send.at[0], v_recv.at[0], core)
        vec_cross = remote(vec.at[1], vec_in.at[1], v_send.at[1], v_recv.at[1], cross)

        def row_copy(m, source):
            return remote(
                source.at[block(1 - t, shard_rows)], rows_out.at[m], r_send.at[m], r_recv.at[m], cross
            )

        row_plan = [(0, 0, low_grad_ref, True), (0, 1, gxl_out, False), (1, 1, second_ref, False)]
        for number, m, source, early in row_plan:
            if early:
                @pl.when(section == number)
                def _(m=m, source=source):
                    row_copy(m, source).start()

        def unit_at(turn):
            later = ahead_of + (turn - ahead_of) * (end_at + 1 - ahead_of) // spread
            return jnp.where(turn < ahead_of, turn, later)

        up = pl.ds(0, quarter)
        down = pl.ds(quarter, quarter)
        sides = ((up, 0, z, above, below), (down, 1, last - z, below, above))

        @pl.loop(0, ahead_of + total + drain)
        def _(turn):
            s = turn - ahead_of

            unit = unit_at(turn)

            @pl.when(first & (unit != unit_at(turn - 1)))
            def _():
                @pl.when(unit < norm_at)
                def _():
                    ffn_unit(unit)

                @pl.when(unit == norm_at)
                def _():
                    norm_unit()

                @pl.when((unit >= head_at) & (unit < end_at))
                def _():
                    head_unit(unit - head_at)

                @pl.when(unit == end_at)
                def _():
                    end_unit()

            @pl.when(s == 0)
            def _():
                for k in range(ring - 1):
                    load_tile(jnp.int32(k))

            @pl.when(valid(s))
            def _():
                @pl.when(s == per_pair - 1)
                def _():
                    take_left(1, 1, None)

                @pl.when(s == x_flip)
                def _():
                    take_left(2, 0, None)

                @pl.when(s == ga_flip)
                def _():
                    take_left(3, 1, 1)

                at = lax.rem(s, ring)
                arrived(tile.at[at], tile_sem.at[at])
                give_at = lax.rem(s, gives)

                @pl.when(s >= gives)
                def _():
                    arrived(give.at[give_at], give_send.at[give_at])

                ffn_flip = jnp.where(lax.rem(s, 3 * per_pair) // per_pair == 0, 0, 1)
                which = jnp.where(s < ffn_blocks, ffn_flip, jnp.where(s < ffn_blocks + 3 * head_blocks, 0, 1))
                for place, store, spot in ((1 - c, give, give_at), (c, mine, lax.rem(s, mines))):
                    here = block(place, half)
                    product = dot(flip[which, here, :rows], tile[at, 0])
                    for m in range(1, seqs):
                        product += dot(flip[which, here, m * rows : (m + 1) * rows], tile[at, m])
                    store[spot, 1] = product[:, :bt].astype(BF)
                    store[spot, 0] = product[:, bt:].astype(BF)

            @pl.when((s >= 0) & (s + ring - 1 < total))
            def _():
                load_tile(s + ring - 1)

            k1 = s - CORE_LAG

            @pl.when(valid(k1))
            def _():
                arrived(acc.at[k1], core_recv.at[k1])
                at = lax.rem(k1, mines)
                for side in range(2):
                    acc[k1, side] = acc[k1, side] + mine[at, side]

            k2 = k1 - CROSS_LAG

            @pl.when(valid(k2))
            def _():
                arrived(from_x.at[k2], x_recv.at[k2])
                acc[k2, 1] = acc[k2, 1] + from_x[k2]

            for rows_, way, place, ahead, behind in sides:
                k3 = k2 - CHAIN_LAG * place

                @pl.when(valid(k3) & (place > 0))
                def _(rows_=rows_, way=way, k3=k3):
                    arrived(from_z.at[k3, rows_], z_recv.at[way, k3])
                    acc[k3, 1, rows_] = acc[k3, 1, rows_] + from_z[k3, rows_]

                k4 = k2 - CHAIN_LAG * (2 * last - place)

                @pl.when(valid(k4) & (place == last))
                def _(rows_=rows_, k4=k4):
                    final[k4, rows_] = acc[k4, 1, rows_]

                @pl.when(valid(k4) & (place < last))
                def _(rows_=rows_, way=way, k4=k4):
                    arrived(final.at[k4, rows_], f_recv.at[way, k4])

            @pl.when(valid(s))
            def _():
                at = lax.rem(s, gives)
                remote(give.at[at], acc.at[s], give_send.at[at], core_recv.at[s], core).start()

            @pl.when(valid(k1))
            def _():
                remote(acc.at[k1, 0], from_x.at[k1], x_send, x_recv.at[k1], cross).start()

            for number, m, source, early in row_plan:
                if not early:
                    @pl.when((k1 == total - 1) & (section == number))
                    def _(m=m, source=source):
                        row_copy(m, source).start()

            for rows_, way, place, ahead, behind in sides:
                k3 = k2 - CHAIN_LAG * place

                @pl.when(valid(k3) & (place < last))
                def _(rows_=rows_, way=way, k3=k3, ahead=ahead):
                    remote(acc.at[k3, 1, rows_], from_z.at[k3, rows_], z_send.at[way], z_recv.at[way, k3], ahead).start()

                k4 = k2 - CHAIN_LAG * (2 * last - place)

                @pl.when(valid(k4) & (place > 0))
                def _(rows_=rows_, way=way, k4=k4, behind=behind):
                    remote(final.at[k4, rows_], final.at[k4, rows_], f_send.at[way], f_recv.at[way, k4], behind).start()

            k5 = k2 - CHAIN_LAG * 2 * last

            @pl.when(valid(k5))
            def _():
                def visit(m, j):
                    dst = outs[group_of[m]].at[member_of[m], block(c, half), block(j, bt)]
                    copy(final.at[k5], dst, store_sem).start()
                    remote(final.at[k5], dst, out_send, out_recv, core).start()

                member(k5, visit)

            @pl.when(turn == last_turn + 1)
            def _():
                vec_core.start()

            @pl.when(turn == last_turn + 6)
            def _():
                vec_core.wait_recv()
                vec[1] = vec[0] + vec_in[0]

            @pl.when(turn == last_turn + 7)
            def _():
                vec_cross.start()

            @pl.when(turn == last_turn + 13)
            def _():
                vec_cross.wait_recv()
                vec_all[z] = vec[1] + vec_in[1]

            @pl.when(turn == last_turn + 14)
            def _():
                for shift in range(1, chips):
                    to = lax.rem(z + shift, chips)
                    remote(
                        vec_all.at[z], vec_all.at[z], v_send.at[1 + shift], v_recv.at[1 + shift], {"dp": to * 2 + c}
                    ).start()

        for number, m, source, early in row_plan:
            @pl.when(section == number)
            def _(m=m, source=source):
                row_copy(m, source).wait()

        vec_core.wait_send()
        vec_cross.wait_send()
        for shift in range(1, chips):
            origin = lax.rem(z + chips - shift, chips)
            arrived(vec_all.at[origin], v_recv.at[1 + shift])
            arrived(vec_all.at[z], v_send.at[1 + shift])
        whole = vec_all[0]
        for chip in range(1, chips):
            whole += vec_all[chip]
        sums_out[...] = whole
        for at in range(gives):
            arrived(give.at[at], give_send.at[at])
        arrived(acc.at[:, 0], x_send)
        for rows_, way, place, ahead, behind in sides:
            @pl.when(place < last)
            def _(rows_=rows_, way=way):
                arrived(from_z.at[:, rows_], z_send.at[way])

            @pl.when(place > 0)
            def _(rows_=rows_, way=way):
                arrived(final.at[:, rows_], f_send.at[way])

        arrived(final, out_send)
        arrived(final, store_sem)
        arrived(final, out_recv)

    sem = pltpu.SemaphoreType.DMA
    flops = 2 * seqs * rows * width * 2 * bt * total
    members = [member_of[index] for index in range(7)]
    shapes = [(sum(g == index for g in group_of), width, rights[group_of.index(index)].shape[2] // 2) for index in range(4)]
    return pl.pallas_call(
        kernel,
        in_specs=[SMEM, SMEM] + NORM_SPECS + [WHOLE] * 9 + [ANY] * 32,
        out_specs=[ANY] * 4 + [WHOLE] + [ANY] * 8,
        out_shape=[jax.ShapeDtypeStruct(s, BF) for s in shapes]
        + [jax.ShapeDtypeStruct(vec_shape, F32), jax.ShapeDtypeStruct((seqs, shard_rows, width), BF)]
        + [jax.ShapeDtypeStruct(act.shape, BF)] * 2
        + [jax.ShapeDtypeStruct((rows, 2 * local), BF)] * 3
        + [jax.ShapeDtypeStruct((rows, width), F32), jax.ShapeDtypeStruct((rows, width), BF)],
        scratch_shapes=[
            pltpu.VMEM((total, 2, half, bt), BF),
            pltpu.VMEM((total, half, bt), BF),
            pltpu.VMEM((total, half, bt), BF),
            pltpu.VMEM((2, width, seqs * rows), BF),
            pltpu.VMEM((seqs, rows, width), BF),
            pltpu.VMEM((ring, seqs, rows, 2 * bt), BF),
            pltpu.VMEM((mines, 2, half, bt), BF),
            pltpu.VMEM((gives, 2, half, bt), BF),
            pltpu.VMEM((2,) + vec_shape, F32),
            pltpu.VMEM((2,) + vec_shape, F32),
            pltpu.VMEM((chips,) + vec_shape, F32),
            pltpu.VMEM((rows, width), BF),
            pltpu.VMEM((rows, width), BF),
            pltpu.VMEM((rows, 128), F32),
            pltpu.VMEM((2, rows, width), BF),
            pltpu.VMEM((rows, width), F32),
            pltpu.VMEM((2, 3, width, CW), BF),
            pltpu.VMEM((2, CW, width), BF),
            pltpu.VMEM((2, 3, rows, CW), BF),
            pltpu.VMEM((2, 3, rows, CW), BF),
            pltpu.VMEM((2, 8, rows), F32),
            pltpu.VMEM((rows, CW), BF),
            pltpu.VMEM((2, rows, rows), BF),
            pltpu.VMEM((rows, rows), F32),
            pltpu.VMEM((8, width), F32),
            pltpu.VMEM((2, 2 * units), F32),
            pltpu.VMEM((2, 2 * local), F32),
            sem((ring,)), sem((2,)), sem((gives,)), sem((total,)), sem, sem((total,)),
            sem((2,)), sem((2, total)), sem((2,)), sem((2, total)),
            sem, sem, sem, sem((chips + 1,)), sem((chips + 1,)), sem((seqs,)), sem((seqs,)),
            sem((3,)), sem((2, 6)), sem((2, 3)), sem((2,)),
        ],
        input_output_aliases={20: 6, 21: 7},
        compiler_params=pltpu.CompilerParams(
            collective_id=0, has_side_effects=True, vmem_limit_bytes=67_000_000
        ),
        cost_estimate=pl.CostEstimate(flops=flops, bytes_accessed=100 << 20, transcendentals=0),
        name="backward_and_reduce",
    )(
        lengths, slopes, *norms, *sums, grad, q, k_, v, lse, act, slope, u1, u2, r1, r2, *weights, *lefts, *rights,
        low_grad, second
    )


def exchange_rows(outputs, deps):
    seqs = len(outputs)
    rows, width = outputs[0].shape
    shard_rows = rows // 2
    n_in = seqs + len(deps)

    def kernel(*refs):
        y_refs, out_ref = refs[:seqs], refs[n_in]
        stage, send, recv, l_sem = refs[n_in + 1 :]
        t = lax.axis_index("tensor")
        cross = {"tensor": 1 - t}
        barrier = pltpu.get_barrier_semaphore()
        pl.semaphore_signal(barrier, inc=1, device_id=cross, device_id_type=MESH)
        pl.semaphore_wait(barrier, 1)

        @pl.when(lax.axis_index("section") == 0)
        def _():
            for m in range(seqs):
                pltpu.make_async_remote_copy(
                    src_ref=y_refs[m].at[block(1 - t, shard_rows)], dst_ref=out_ref.at[t * seqs + m],
                    send_sem=send.at[m], recv_sem=recv.at[m], device_id=cross, device_id_type=MESH,
                ).start()
            for m in range(seqs):
                copy(y_refs[m].at[block(t, shard_rows)], stage.at[m], l_sem.at[m]).start()
            for m in range(seqs):
                arrived(stage.at[m], l_sem.at[m])
                copy(stage.at[m], out_ref.at[t * seqs + m], l_sem.at[m]).start()
            for m in range(seqs):
                arrived(stage.at[m], l_sem.at[m])
            for m in range(seqs):
                arrived(out_ref.at[(1 - t) * seqs + m], recv.at[m])
                arrived(stage.at[m], send.at[m])

    sem = pltpu.SemaphoreType.DMA
    return pl.pallas_call(
        kernel,
        in_specs=[ANY] * n_in,
        out_specs=ANY,
        out_shape=jax.ShapeDtypeStruct((2 * seqs, shard_rows, width), BF),
        scratch_shapes=[pltpu.VMEM((seqs, shard_rows, width), BF), sem((seqs,)), sem((seqs,)), sem((seqs,))],
        compiler_params=pltpu.CompilerParams(collective_id=2, has_side_effects=True),
        cost_estimate=pl.CostEstimate(flops=0, bytes_accessed=0, transcendentals=0),
        name="exchange_rows",
    )(*outputs, *deps)


def widen(reduced, row_grads, got, got_second, produced, outputs, sums, units, local):
    shard_rows, width = got.shape[1:]
    seqs = got.shape[0]
    n = len(reduced)
    jobs = []
    for index, array in enumerate(reduced):
        lead, depth, columns = array.shape
        step = 512 * 1024 // columns
        if index == n - 1:
            jobs += [(index, 0, at, depth // 2, columns) for at in range(0, depth, depth // 2)]
        else:
            jobs += [(index, part, at, step, columns) for part in range(lead) for at in range(0, depth, step)]
    jobs += [(n, m, 0, shard_rows, width) for m in range(seqs)] + [(n + 1, m, 0, shard_rows, width) for m in range(seqs)]
    jobs += [(n + 2, m, 0, shard_rows, width) for m in range(2 * seqs)]
    ring = 6
    n_in = n + 3 * seqs + 4
    parts = units // width

    def kernel(*refs):
        ins = refs[:n]
        grad_refs = refs[n : n + 2 * seqs]
        got_ref, got_second_ref, produced_ref = refs[n + 2 * seqs : n + 2 * seqs + 3]
        y_refs, sums_ref = refs[n + 2 * seqs + 3 : n_in - 1], refs[n_in - 1]
        outs = refs[n_in : n_in + n + 2]
        qv_ref, out_bias_ref, gain_ref, shift_ref, ub_ref, down_bias_ref = refs[n_in + n + 2 : n_in + n + 8]
        shapes = sorted({(j[3], j[4]) for j in jobs if j[0] != n})
        buffers = refs[n_in + n + 8 :]
        wide_rows, in_sem, out_sem = buffers[0], buffers[1], buffers[2]
        low = {s: buffers[3 + 2 * i] for i, s in enumerate(shapes)}
        wide = {s: buffers[4 + 2 * i] for i, s in enumerate(shapes)}
        t = lax.axis_index("tensor")
        section = lax.axis_index("section")

        def load(number):
            index, part, at, rows, columns = jobs[number]
            s = number % ring
            if index < n:
                copy(ins[index].at[part, pl.ds(at, rows)], low[rows, columns].at[s], in_sem.at[s]).start()
            elif index == n:
                for turn in range(2):
                    @pl.when(section == turn)
                    def _(turn=turn):
                        source = grad_refs[turn * seqs + part].at[block(t, shard_rows)]
                        copy(source, wide_rows.at[part], in_sem.at[s]).start()
            elif index == n + 1:
                for number_ in range(2):
                    @pl.when(section == number_)
                    def _(number_=number_):
                        source = got_second_ref.at[seqs] if number_ == 1 and part == 0 else got_ref.at[part]
                        copy(source, low[rows, columns].at[s], in_sem.at[s]).start()
            else:
                @pl.when(section == 0)
                def _():
                    copy(produced_ref.at[part], low[rows, columns].at[s], in_sem.at[s]).start()

                @pl.when(section == 1)
                def _():
                    source = y_refs[part].at[block(t, shard_rows)] if part < seqs else got_second_ref.at[part - seqs]
                    copy(source, low[rows, columns].at[s], in_sem.at[s]).start()

        def store(number):
            index, part, at, rows, columns = jobs[number]
            s = number % ring
            if index < n - 1:
                return copy(wide[rows, columns].at[s], outs[index].at[part, pl.ds(at, rows)], out_sem.at[s])
            if index == n - 1:
                return copy(wide[rows, columns].at[s], outs[index].at[:, pl.ds(at, rows)], out_sem.at[s])
            if index == n:
                return copy(wide_rows.at[part], outs[n].at[t * seqs + part], out_sem.at[s])
            if index == n + 1:
                return copy(wide[rows, columns].at[s], outs[n].at[(1 - t) * seqs + part], out_sem.at[s])
            side, m = divmod(part, seqs)
            spread = (t + side - 2 * t * side) * seqs + m
            return copy(low[rows, columns].at[s], outs[n + 1].at[jnp.where(section == 0, part, spread)], out_sem.at[s])

        for number in range(ring):
            load(number)
        gain_ref[0:1] = sums_ref[3:4]
        gain_ref[1:2] = sums_ref[0:1]
        shift_ref[0:1] = sums_ref[4:5]
        shift_ref[1:2] = sums_ref[1:2]
        out_bias_ref[...] = sums_ref[5:6]
        down_bias_ref[...] = sums_ref[2:3]
        for half in range(2):
            @pl.when(t == half)
            def _(half=half):
                for g in range(2):
                    for j in range(parts):
                        at = 6 + (2 * g + half) * parts + j
                        ub_ref[g : g + 1, j * width : (j + 1) * width] = sums_ref[at : at + 1]
                    at = 6 + 4 * parts + g
                    qv_ref[g : g + 1] = sums_ref[at : at + 1, half * local : (half + 1) * local]

        for number, (index, part, at, rows, columns) in enumerate(jobs):
            s = number % ring
            if index == n:
                arrived(wide_rows.at[part], in_sem.at[s])
            else:
                arrived(low[rows, columns].at[s], in_sem.at[s])
            if number >= ring:
                store(number - ring).wait()
            if index == n - 1:
                wide[rows, columns][s] = low[rows, columns][s].astype(F32).T
            elif index not in (n, n + 2):
                wide[rows, columns][s] = low[rows, columns][s].astype(F32)
            store(number).start()
            if number + ring < len(jobs):
                load(number + ring)
        for number in range(len(jobs) - ring, len(jobs)):
            store(number).wait()

    shapes = sorted({(j[3], j[4]) for j in jobs if j[0] != n})
    square = (reduced[-1].shape[1] // 2, reduced[-1].shape[2])
    last = reduced[-1].shape
    sem = pltpu.SemaphoreType.DMA
    buffers = []
    for s in shapes:
        buffers += [pltpu.VMEM((ring,) + s, BF), pltpu.VMEM((ring,) + ((s[1], s[0]) if s == square else s), F32)]
    return pl.pallas_call(
        kernel,
        in_specs=[ANY] * (n_in - 1) + [WHOLE],
        out_specs=[ANY] * (n + 2) + [WHOLE] * 6,
        out_shape=[jax.ShapeDtypeStruct(r.shape, F32) for r in reduced[:-1]]
        + [jax.ShapeDtypeStruct((last[2], last[1]), F32), jax.ShapeDtypeStruct((2 * seqs, shard_rows, width), F32)]
        + [jax.ShapeDtypeStruct((2 * seqs, shard_rows, width), BF)]
        + [
            jax.ShapeDtypeStruct(shape, F32)
            for shape in ((2, local), (1, width), (2, width), (2, width), (2, units), (1, width))
        ],
        scratch_shapes=[pltpu.VMEM((seqs, shard_rows, width), F32), sem((ring,)), sem((ring,))] + buffers,
        compiler_params=pltpu.CompilerParams(vmem_limit_bytes=VMEM_LIMIT),
        cost_estimate=pl.CostEstimate(flops=0, bytes_accessed=56 << 20, transcendentals=0),
        name="widen",
    )(*reduced, *row_grads, got, got_second, produced, *outputs, sums)


MASKED = -1000000000.0


def shifted(value, axis, steps):
    count = lax.axis_size(axis)
    first, last = (max(0, -steps), min(count, count - steps))
    return lax.ppermute(value, axis, [(source, source + steps) for source in range(first, last)])


def layer_norm(values, gain, shift):
    mean = jnp.mean(values, axis=-1, keepdims=True)
    centred = values - mean
    spread = jnp.mean(centred * centred, axis=-1, keepdims=True)
    return centred * lax.rsqrt(spread + EPS) * gain + shift


def alibi_slopes(first, count, heads):
    index = (first + jnp.arange(count)).astype(jnp.float32)
    return jnp.exp2(-8.0 * (index + 1.0) / heads)


def attention_core(projected, qv_bias, slopes, key_ok):
    rows = projected.shape[0]
    width = projected.shape[2]
    count = slopes.shape[0]
    size = width // count
    query = (projected[:, 0] + qv_bias[0]).astype(jnp.bfloat16).reshape(rows, count, size)
    key = projected[:, 1].astype(jnp.bfloat16).reshape(rows, count, size)
    value = (projected[:, 2] + qv_bias[1]).astype(jnp.bfloat16).reshape(rows, count, size)
    place = jnp.arange(rows).astype(jnp.float32)
    distance = jnp.abs(place[:, None] - place[None, :])
    scale = 1.0 / math.sqrt(size)
    scores = (
        jnp.einsum("qhd,khd->hqk", query, key, preferred_element_type=jnp.float32) * scale
        - slopes[:, None, None] * distance[None]
    )
    scores = jnp.where(key_ok[None, None, :], scores, MASKED)
    weights = jax.nn.softmax(scores, axis=-1)
    weights_low = weights.astype(jnp.bfloat16)
    mixed = jnp.einsum("hqk,khd->qhd", weights_low, value, preferred_element_type=jnp.float32)
    mixed = mixed.reshape(rows, width).astype(jnp.bfloat16)
    return (query, key, value, weights, weights_low, mixed)


def attention_back(parts, grad_mixed, key_ok):
    query, key, value, weights, weights_low, mixed = parts
    rows, count, size = query.shape
    scale = 1.0 / math.sqrt(size)
    grad_low = grad_mixed.astype(jnp.bfloat16).reshape(rows, count, size)
    grad_weights = jnp.einsum("qhd,khd->hqk", grad_low, value, preferred_element_type=jnp.float32)
    grad_value = jnp.einsum(
        "hqk,qhd->khd", weights_low, grad_low, preferred_element_type=jnp.float32
    )
    inner = jnp.sum(weights * grad_weights, axis=-1, keepdims=True)
    grad_scores = weights * (grad_weights - inner)
    grad_scores = jnp.where(key_ok[None, None, :], grad_scores, 0.0).astype(jnp.bfloat16)
    grad_query = (
        jnp.einsum("hqk,khd->qhd", grad_scores, key, preferred_element_type=jnp.float32) * scale
    ).astype(jnp.bfloat16)
    grad_key = (
        jnp.einsum("hqk,qhd->khd", grad_scores, query, preferred_element_type=jnp.float32) * scale
    ).astype(jnp.bfloat16)
    grad_value = grad_value.astype(jnp.bfloat16)
    width = count * size
    grad_query = grad_query.reshape(rows, width)
    grad_key = grad_key.reshape(rows, width)
    grad_value = grad_value.reshape(rows, width)
    grad_projected = jnp.stack([grad_query, grad_key, grad_value], axis=1).reshape(rows, 3 * width)
    qv_grad = jnp.stack(
        [
            jnp.sum(grad_query.astype(jnp.float32), axis=0),
            jnp.sum(grad_value.astype(jnp.float32), axis=0),
        ]
    )
    return (grad_projected, qv_grad)


def gelu_product(both):
    return jax.nn.gelu(both[:, 0], approximate=False) * both[:, 1]


def geglu(lifted, up_bias):
    return gelu_product(lifted + up_bias[None])


def ffn_grads(rows_low, grad_low, up_weight, up_bias, down_weight):
    lifted = jnp.einsum("sd,gdf->sgf", rows_low, up_weight, preferred_element_type=jnp.float32)
    hidden, geglu_back = jax.vjp(gelu_product, lifted + up_bias[None])
    grad_hidden = jnp.einsum("sd,df->sf", grad_low, down_weight, preferred_element_type=jnp.float32)
    (grad_both,) = geglu_back(grad_hidden)
    grad_lifted = grad_both.astype(jnp.bfloat16)
    grad_bias = jnp.sum(grad_lifted.astype(jnp.float32), axis=0)
    up_grad = jnp.einsum("sd,sgf->gdf", rows_low, grad_lifted, preferred_element_type=jnp.float32)
    down_grad = jnp.einsum(
        "sd,sf->df", grad_low, hidden.astype(jnp.bfloat16), preferred_element_type=jnp.float32
    )
    return (grad_lifted, grad_bias, up_grad, down_grad)


def on_device(
    inputs,
    cotangent,
    lengths,
    w_qkv,
    b_qv,
    w_out,
    b_out,
    ln_gain,
    ln_bias,
    w_up,
    b_up,
    w_down,
    b_down,
):
    batches, shard_rows, width = inputs.shape
    parts = lax.axis_size("tensor")
    place = lax.axis_index("tensor")
    section = lax.axis_index("section")
    last_section = lax.axis_size("section") - 1
    full_rows = shard_rows * parts
    local_width = w_qkv.shape[3]
    local_heads = local_width // HD
    qkv_flat = w_qkv[0].reshape(width, 3 * local_width)
    out_weight = w_out[0]
    qv_bias = b_qv[0].astype(jnp.float32)
    out_bias = b_out[0].astype(jnp.float32)
    gains = ln_gain[0].astype(jnp.float32)
    shifts = ln_bias[0].astype(jnp.float32)
    down_bias = b_down[0].astype(jnp.float32)
    slopes = alibi_slopes(place * local_heads, local_heads, H)
    row_place = place * shard_rows + jnp.arange(shard_rows)
    kept_rows = 0

    def key_mask(length):
        return jnp.arange(full_rows) < length

    def after_attention(values, attended, bias, gain_rows, shift_rows):
        return layer_norm(values + attended + bias, gain_rows[0], shift_rows[0])

    def after_ffn(normed, lowered, bias, gain_rows, shift_rows):
        return layer_norm(normed + lowered + bias, gain_rows[1], shift_rows[1])

    def gather_inputs(values):
        return lax.all_gather(values.astype(jnp.bfloat16), "tensor", axis=0, tiled=True)

    def project(gathered):
        return jnp.dot(gathered, qkv_flat, preferred_element_type=jnp.float32).reshape(
            full_rows, 3, local_width
        )

    def attention_forward(values, length):
        gathered = gather_inputs(values)
        projected = project(gathered)
        mixed = attention_core(projected, qv_bias, slopes, key_mask(length))[5]

        def term(start, count):
            return jnp.dot(mixed, out_weight, preferred_element_type=jnp.float32)

        return (
            lax.psum_scatter(
                term(jnp.int32(0), shard_rows * lax.axis_size("tensor")).astype(jnp.bfloat16),
                "tensor",
                scatter_dimension=0,
                tiled=True,
            ).astype(jnp.float32),
            gathered,
            projected,
        )

    up_local = w_up[0]
    up_bias_local = b_up[0].astype(jnp.float32)
    down_local = w_down[0]

    def gather_normed(normed):
        return lax.all_gather(normed.astype(jnp.bfloat16), "tensor", axis=0, tiled=True)

    def ffn_forward(normed):
        lifted = jnp.einsum(
            "sd,gdf->sgf", gather_normed(normed), up_local, preferred_element_type=jnp.float32
        )
        hidden = geglu(lifted, up_bias_local).astype(jnp.bfloat16)

        def term(start, count):
            return jnp.einsum("sf,df->sd", hidden, down_local, preferred_element_type=jnp.float32)

        return lax.psum_scatter(
            term(jnp.int32(0), shard_rows * lax.axis_size("tensor")).astype(jnp.bfloat16),
            "tensor",
            scatter_dimension=0,
            tiled=True,
        ).astype(jnp.float32)

    def ffn_backward(normed, grad_lowered):
        gathered = gather_normed(normed)
        grad_whole = lax.all_gather(grad_lowered.astype(jnp.bfloat16), "tensor", axis=0, tiled=True)
        grad_lifted, grad_bias, up_grad, down_grad = ffn_grads(
            gathered, grad_whole, up_local, up_bias_local, down_local
        )

        def term(start, count):
            return jnp.einsum(
                "sgf,gdf->sd", grad_lifted, up_local, preferred_element_type=jnp.float32
            )

        grad_normed = lax.psum_scatter(
            term(jnp.int32(0), shard_rows * lax.axis_size("tensor")).astype(jnp.bfloat16),
            "tensor",
            scatter_dimension=0,
            tiled=True,
        ).astype(jnp.float32)
        return (grad_normed, (up_grad, grad_bias, down_grad))

    ffn_shapes = (up_local.shape, up_bias_local.shape, down_local.shape)

    def layer_forward(values, length):
        attended, gathered, projected = attention_forward(values, length)
        normed = after_attention(values, attended, out_bias, gains, shifts)
        lowered = ffn_forward(normed)
        return (
            after_ffn(normed, lowered, down_bias, gains, shifts),
            attended,
            lowered,
            gathered,
            projected,
        )

    def layer_backward(values, attended, lowered, length, grad_output):
        normed, attention_norm_back = jax.vjp(
            after_attention, values, attended, out_bias, gains, shifts
        )
        outcome, ffn_norm_back = jax.vjp(after_ffn, normed, lowered, down_bias, gains, shifts)
        grad_normed, grad_lowered, grad_down_bias, gain_late, shift_late = ffn_norm_back(
            grad_output
        )
        grad_from_ffn, ffn_terms = ffn_backward(normed, grad_lowered)
        grad_values, grad_attended, grad_out_bias, gain_early, shift_early = attention_norm_back(
            grad_normed + grad_from_ffn
        )
        gathered = gather_inputs(values)
        projected = project(gathered)
        grad_whole = lax.all_gather(
            grad_attended.astype(jnp.bfloat16), "tensor", axis=0, tiled=True
        )
        mask = key_mask(length)
        pieces = attention_core(projected, qv_bias, slopes, mask)
        mixed_low = pieces[5]
        out_grad = jnp.einsum(
            "se,sd->ed", mixed_low, grad_whole, preferred_element_type=jnp.float32
        )
        grad_mixed = jnp.einsum(
            "sd,ed->se", grad_whole, out_weight, preferred_element_type=jnp.float32
        )
        grad_projected, qv_grad = attention_back(pieces, grad_mixed, mask)
        qkv_grad = jnp.einsum(
            "sd,sx->dx", gathered, grad_projected, preferred_element_type=jnp.float32
        )

        def term(start, count):
            return jnp.einsum(
                "sx,dx->sd", grad_projected, qkv_flat, preferred_element_type=jnp.float32
            )

        grad_inputs = grad_values + lax.psum_scatter(
            term(jnp.int32(0), shard_rows * lax.axis_size("tensor")).astype(jnp.bfloat16),
            "tensor",
            scatter_dimension=0,
            tiled=True,
        ).astype(jnp.float32)
        terms = (
            qkv_grad,
            qv_grad,
            out_grad,
            grad_out_bias,
            gain_early + gain_late,
            shift_early + shift_late,
            ffn_terms[0],
            ffn_terms[1],
            ffn_terms[2],
            grad_down_bias,
        )
        return (grad_inputs, terms)

    def keep(store, item, batch, valid):
        old = lax.dynamic_index_in_dim(store, batch, 0, keepdims=False)
        return lax.dynamic_update_index_in_dim(store, jnp.where(valid, item, old), batch, 0)

    def forward_step(step, carry):
        (
            received,
            kept_values,
            kept_attended,
            kept_lowered,
            produced,
            kept_gathered,
            kept_projected,
        ) = carry
        index = step - section
        valid = (index >= 0) & (index < batches)
        batch = jnp.clip(index, 0, batches - 1)
        fresh = lax.dynamic_index_in_dim(
            inputs, jnp.minimum(step, batches - 1), 0, keepdims=False
        ).astype(jnp.float32)
        values = jnp.where(section == 0, fresh, received.astype(jnp.float32))
        output, attended, lowered, gathered, projected = layer_forward(values, lengths[batch])
        sent = output.astype(jnp.bfloat16)
        kept_values = keep(kept_values, values, batch, valid)
        kept_attended = keep(kept_attended, attended, batch, valid)
        kept_lowered = keep(kept_lowered, lowered, batch, valid)
        produced = keep(produced, sent, batch, valid)
        kept_gathered = keep(kept_gathered, gathered[:kept_rows], batch, valid)
        kept_projected = keep(kept_projected, projected[:kept_rows], batch, valid)
        received = shifted(sent, "section", 1)
        return (
            received,
            kept_values,
            kept_attended,
            kept_lowered,
            produced,
            kept_gathered,
            kept_projected,
        )

    store_zeros = jnp.zeros((batches, shard_rows, width), jnp.float32)
    gathered_zeros = jnp.zeros((batches, kept_rows, width), jnp.bfloat16)
    projected_zeros = jnp.zeros((batches, kept_rows, 3, local_width), jnp.float32)
    start_forward = (
        jnp.zeros((shard_rows, width), jnp.bfloat16),
        store_zeros,
        store_zeros,
        store_zeros,
        jnp.zeros((batches, shard_rows, width), jnp.bfloat16),
        gathered_zeros,
        projected_zeros,
    )
    received, kept_values, kept_attended, kept_lowered, produced, kept_gathered, kept_projected = (
        lax.fori_loop(0, batches + last_section, forward_step, start_forward)
    )

    def backward_step(step, carry):
        received, totals, grads_in = carry
        index = step - (last_section - section)
        valid = (index >= 0) & (index < batches)
        batch = jnp.clip(index, 0, batches - 1)
        length = lengths[batch]
        outer = lax.dynamic_index_in_dim(cotangent, batch, 0, keepdims=False).astype(jnp.float32)
        outer = outer * (row_place < length).astype(jnp.float32)[:, None]
        grad_output = jnp.where(section == last_section, outer, received.astype(jnp.float32))
        grad_output = jnp.where(valid, grad_output, 0.0)
        values = lax.dynamic_index_in_dim(kept_values, batch, 0, keepdims=False)
        attended = lax.dynamic_index_in_dim(kept_attended, batch, 0, keepdims=False)
        lowered = lax.dynamic_index_in_dim(kept_lowered, batch, 0, keepdims=False)
        grad_inputs, terms = layer_backward(values, attended, lowered, length, grad_output)
        totals = jax.tree.map(jnp.add, totals, terms)
        grads_in = keep(grads_in, grad_inputs, batch, valid)
        received = shifted(grad_inputs.astype(jnp.bfloat16), "section", -1)
        return (received, totals, grads_in)

    start_totals = (
        jnp.zeros((width, 3 * local_width), jnp.float32),
        jnp.zeros((2, local_width), jnp.float32),
        jnp.zeros((local_width, width), jnp.float32),
        jnp.zeros((width,), jnp.float32),
        jnp.zeros((2, width), jnp.float32),
        jnp.zeros((2, width), jnp.float32),
        jnp.zeros(ffn_shapes[0], jnp.float32),
        jnp.zeros(ffn_shapes[1], jnp.float32),
        jnp.zeros(ffn_shapes[2], jnp.float32),
        jnp.zeros((width,), jnp.float32),
    )
    start_backward = (jnp.zeros((shard_rows, width), jnp.bfloat16), start_totals, store_zeros)
    received, totals, grads_in = lax.fori_loop(
        0, batches + last_section, backward_step, start_backward
    )
    (
        qkv_total,
        qv_total,
        out_total,
        out_bias_total,
        gain_total,
        shift_total,
        up_total,
        up_bias_total,
        down_total,
        down_bias_total,
    ) = totals
    qkv_sum, qv_sum, out_sum, up_sum, up_bias_sum, down_sum = (
        lax.psum(qkv_total.astype(jnp.bfloat16), "dp").astype(jnp.float32),
        lax.psum(qv_total.astype(jnp.bfloat16), "dp").astype(jnp.float32),
        lax.psum(out_total.astype(jnp.bfloat16), "dp").astype(jnp.float32),
        lax.psum(up_total.astype(jnp.bfloat16), "dp").astype(jnp.float32),
        lax.psum(up_bias_total.astype(jnp.bfloat16), "dp").astype(jnp.float32),
        lax.psum(down_total.astype(jnp.bfloat16), "dp").astype(jnp.float32),
    )
    out_bias_sum, gain_sum, shift_sum, down_bias_sum = lax.psum(
        (out_bias_total, gain_total, shift_total, down_bias_total), ("tensor", "dp")
    )
    return (
        produced[None],
        grads_in[None],
        qkv_sum.reshape(1, width, 3, local_width),
        qv_sum[None],
        out_sum[None],
        out_bias_sum[None],
        gain_sum[None],
        shift_sum[None],
        up_sum[None],
        up_bias_sum[None],
        down_sum[None],
        down_bias_sum[None],
    )


def by_sequence(
    inputs,
    cotangent,
    lengths,
    w_qkv,
    b_qv,
    w_out,
    b_out,
    ln_gain,
    ln_bias,
    w_up,
    b_up,
    w_down,
    b_down,
):
    batches, shard_rows, width = inputs.shape
    place = lax.axis_index("tensor")
    section = lax.axis_index("section")
    groups = lax.axis_size("dp")
    rows = 2 * shard_rows
    seqs = batches // 2
    local = w_qkv.shape[3]
    units = w_up.shape[3]
    heads = local // HD
    chips = groups // 2

    qkv_own = jnp.transpose(w_qkv[0], (1, 0, 2))
    out_own = w_out[0]
    up_own = w_up[0]
    down_own = w_down[0]
    first = section == 0
    norms = (b_out, ln_gain[0], ln_bias[0], b_down)
    table = np.exp2(-8.0 * (np.arange(2 * heads, dtype=np.float32) + 1.0) / H).astype(np.float32)
    slopes = jnp.asarray(np.concatenate([table, np.roll(table, heads)]))

    qkv_oth, out_oth, up_oth, down_oth, *rest = fetch_and_forward(
        (qkv_own, out_own, up_own, down_own),
        (b_qv[0], b_up[0]),
        inputs,
        cotangent,
        slopes,
        norms,
        lengths,
        chips,
        seqs,
    )
    weights = (qkv_own, qkv_oth, out_own, out_oth, up_own, up_oth, down_own, down_oth)
    biases, rest = rest[:2], rest[2:]
    x_first = outer = rest[:seqs]
    *kept, y = rest[seqs:]
    deps = [y]

    def forward(x, m, turn):
        nonlocal kept, deps
        *kept, y = layer_forward(x, weights, biases, slopes, norms, lengths, m, turn, kept, deps, seqs)
        deps = [y]
        return y

    y_first = [y] + [forward(x_first[m], m, 0) for m in range(1, seqs)]
    x_second = [lax.ppermute(y, "section", [(0, 1)]) for y in y_first]
    y_second = [forward(x_second[0], 0, 1)]
    produced = exchange_rows(y_first, deps)
    deps = [produced]
    y_second += [forward(x_second[m], m, 1) for m in range(1, seqs)]

    back = None
    sums = [[None] * seqs, [None] * seqs]

    got_second = None

    def backward(grad, m, turn, *extra):
        nonlocal back, deps, got_second
        results = layer_backward(grad, kept, weights, slopes, norms, lengths, m, turn, back, deps, seqs, *extra)
        back, (gx, gx_low, norm_sums, up_sums, qv_sums) = results[:7], results[7:12]
        if extra:
            got_second = results[12]
        deps = [norm_sums]
        sums[turn][m] = (norm_sums, up_sums, qv_sums)
        return gx, gx_low

    gx_second = [backward(outer[0], 0, 1)]
    gx_second.append(backward(outer[1], 1, 1, [*y_second, gx_second[0][1]]))
    grad_middle = [lax.ppermute(gx_second[m][1], "section", [(1, 0)]) for m in range(seqs)]
    x_all = jnp.stack([jnp.where(first, x_first[m], x_second[m]) for m in range(seqs)])
    deps = deps + [x_all]
    gx_first = [backward(grad_middle[0], 0, 0)]

    *reduced, packed, got, _, _, _, _, _, gx, _ = backward_and_reduce(
        grad_middle[1], kept, back, x_all, weights, slopes, norms, lengths, [*sums[0][0], *sums[1][0], *sums[1][1]], gx_first[0][1],
        gx_second[1][1], chips,
    )
    gx_all = [gx_first[0][0], gx] + [g[0] for g in gx_second]
    (
        down_sum, up_sum, qkv_sum, out_sum, grads_in, produced,
        qv_sum, out_bias_sum, gain_sum, shift_sum, up_bias_sum, down_bias_sum,
    ) = widen(reduced, gx_all, got, got_second, produced, y_second, packed, units, local)
    return (
        produced[None],
        grads_in[None],
        jnp.transpose(qkv_sum, (1, 0, 2))[None],
        qv_sum[None],
        out_sum[None],
        out_bias_sum,
        gain_sum[None],
        shift_sum[None],
        up_sum[None],
        up_bias_sum[None],
        down_sum,
        down_bias_sum,
    )


def solution(mesh):
    sections, parts, groups = (mesh.shape[name] for name in ("section", "tensor", "dp"))

    def run(*args):
        paired = sections == 2 and parts == 2 and groups % 2 == 0 and args[0].shape[0] == 4
        return (by_sequence if paired else on_device)(*args)

    return jax.shard_map(
        run,
        mesh=mesh,
        in_specs=(
            P("dp", "tensor", None),
            P("dp", "tensor", None),
            P("dp"),
            P("section", None, None, "tensor"),
            P("section", None, "tensor"),
            P("section", "tensor", None),
            P("section", None),
            P("section", None, None),
            P("section", None, None),
            P("section", None, None, "tensor"),
            P("section", None, "tensor"),
            P("section", None, "tensor"),
            P("section", None),
        ),
        out_specs=(
            P("section", "dp", "tensor", None),
            P("section", "dp", "tensor", None),
            P("section", None, None, "tensor"),
            P("section", None, "tensor"),
            P("section", "tensor", None),
            P("section", None),
            P("section", None, None),
            P("section", None, None),
            P("section", None, None, "tensor"),
            P("section", None, "tensor"),
            P("section", None, "tensor"),
            P("section", None),
        ),
        check_vma=False,
    )
```
